32 devices in a mesh: ctx: 16 (over z, y, core), fsdp: 2 (over x).
Axes of the slice: x: 2, y: 2, z: 4, core: 2. Of those that a mesh axis runs over, the one named last changes fastest.
Arguments:
- tokens: bfloat16 [8192, 768], P(('ctx', 'fsdp')), may hold values from -6 to 6
- cotangent: bfloat16 [8192, 768], P(('ctx', 'fsdp')), may hold values from -6 to 6
- doc_lengths: int32 [4], replicated, may hold values from 1 to 4096, 8192 in all
- deal: int32 [64], replicated, may hold values from 0 to 63, each once
- first_gain: bfloat16 [768], P('fsdp'), may hold values from 0.5 to 1.5
- first_shift: bfloat16 [768], P('fsdp'), may hold values from -4 to 4
- query_weight: bfloat16 [768, 768], P('fsdp'), may hold values from -0.21875 to 0.21875
- query_bias: bfloat16 [768], P('fsdp'), may hold values from -6 to 6
- key_weight: bfloat16 [768, 768], P('fsdp'), may hold values from -0.21875 to 0.21875
- value_weight: bfloat16 [768, 768], P('fsdp'), may hold values from -0.21875 to 0.21875
- value_bias: bfloat16 [768], P('fsdp'), may hold values from -0.75 to 0.75
- output_weight: bfloat16 [768, 768], P('fsdp'), may hold values from -3.5 to 3.5
- output_bias: bfloat16 [768], P('fsdp'), may hold values from -4 to 4
- second_gain: bfloat16 [768], P('fsdp'), may hold values from 0.5 to 1.5
- second_shift: bfloat16 [768], P('fsdp'), may hold values from -4 to 4
- up_weight: bfloat16 [768, 3072], P('fsdp'), may hold values from -0.21875 to 0.21875
- up_bias: bfloat16 [3072], P('fsdp'), may hold values from -4 to 4
- down_weight: bfloat16 [3072, 768], P('fsdp'), may hold values from -0.109375 to 0.109375
- down_bias: bfloat16 [768], P('fsdp'), may hold values from -4 to 4
Outputs:
- result: bfloat16 [8192, 768], P(('ctx', 'fsdp'))
- grad_tokens: float32 [8192, 768], P(('ctx', 'fsdp'))
- grad_first_gain: float32 [768], P('fsdp')
- grad_first_shift: float32 [768], P('fsdp')
- grad_query_weight: float32 [768, 768], P('fsdp')
- grad_query_bias: float32 [768], P('fsdp')
- grad_key_weight: float32 [768, 768], P('fsdp')
- grad_value_weight: float32 [768, 768], P('fsdp')
- grad_value_bias: float32 [768], P('fsdp')
- grad_output_weight: float32 [768, 768], P('fsdp')
- grad_output_bias: float32 [768], P('fsdp')
- grad_second_gain: float32 [768], P('fsdp')
- grad_second_shift: float32 [768], P('fsdp')
- grad_up_weight: float32 [768, 3072], P('fsdp')
- grad_up_bias: float32 [3072], P('fsdp')
- grad_down_weight: float32 [3072, 768], P('fsdp')
- grad_down_bias: float32 [768], P('fsdp')
The draws below stay inside these ranges and needn't reach their ends.
Inputs may be any that keep to these rules, and one draw needn't show every extreme that they name: Slot j of the 64 slots holds text block deal[j]; every block stands in exactly one slot. `doc_lengths`: the documents in text order; their lengths sum to 8192.
All inputs are finite; a program needn't handle non-finite values.
Results may differ from the reference program's by a relative error of at most 0.014.
Values may be sent and summed in bfloat16 or wider, within the bound.
A program may use at most 384 MiB of HBM per device.

```python
import math
import jax
import jax.numpy as jnp
import numpy as np
from jax import lax

D = 768
HEADS = 12
DH = 64
FF = 3072
NSUM = 50
SEG = 2048
DOC_MAX = 4096
BLK = 128
TOKENS = 8192
NBLK = 64
NDOC = 4


def level_of(stream_key, dims, cuts, low, largest):
    def one(dim, shards_of):
        heights = jax.random.uniform(jax.random.fold_in(jax.random.fold_in(stream_key, 6), dim), (shards_of,), jnp.float32, low / len(cuts), largest / len(cuts))
        return jnp.repeat(jnp.exp(heights), dims[dim] // shards_of).reshape((-1,) + (1,) * (len(dims) - dim - 1))

    factor_of = one(*cuts[0])
    for cut in cuts[1:]:
        factor_of = factor_of * one(*cut)
    return factor_of


def length_profile(number_of, total, most, skew):
    loads = [(1 << 20) // math.isqrt(rank ** skew) + 1 for rank in range(2, number_of + 1)]
    rest, counts = total - most - (number_of - 1), [1] * (number_of - 1)
    while rest > 0:
        free = [i for i in range(number_of - 1) if counts[i] < most]
        whole, remaining = sum([loads[i] for i in free]), rest
        for i in free:
            extra = min(most - counts[i], max(1, remaining * loads[i] // whole), rest)
            counts[i] = counts[i] + extra
            rest = rest - extra
    return np.array([most] + counts)


def ragged_sizes(own_key, number_of, total, most, skew):
    if number_of == 2:
        one = jax.random.randint(own_key, (), max(1, total - most), min(most, total - 1) + 1)
        return jnp.stack([one, total - one])
    sizes = jnp.asarray(length_profile(number_of, total, most, skew), jnp.int32)
    couples = (number_of - 1) // 2
    giver, sink = sizes[1:1 + 2 * couples:2], sizes[2:2 + 2 * couples:2]
    margin = jnp.minimum(giver - 1, most - sink)
    passed = jax.random.randint(jax.random.fold_in(own_key, 1), (couples,), 0, 1 << 20) % (margin + 1)
    sizes = sizes.at[1:1 + 2 * couples:2].set(giver - passed).at[2:2 + 2 * couples:2].set(sink + passed)
    return sizes[jax.random.permutation(jax.random.fold_in(own_key, 2), number_of)]


def scatter_about(own_key, extent, scale, most, cuts=(), kind=jnp.bfloat16):
    drawn = jax.random.normal(own_key, extent, jnp.float32) * scale
    if len(cuts) > 0:
        drawn = level_of(own_key, extent, cuts, -0.22, 0.18) * drawn
    return jnp.clip(drawn, min=-most, max=most).astype(kind)


def setup_inputs(seed: int = 0) -> dict:
    splits = jax.random.split(jax.random.key(seed), 20)
    tokens = scatter_about(splits[0], (TOKENS, D), 1.0, 6.0, ((0, 32),))
    cotangent = scatter_about(splits[1], (TOKENS, D), 1.0, 6.0, ((0, 32),))
    doc_lengths = ragged_sizes(splits[2], NDOC, TOKENS, DOC_MAX, 2).astype(jnp.int32)
    deal = jax.random.permutation(splits[3], NBLK).astype(jnp.int32)
    first_gain = jnp.clip(1.0 + 0.1 * jax.random.normal(splits[4], (D,), jnp.float32), 0.5, 1.5).astype(jnp.bfloat16)
    first_shift = scatter_about(splits[5], (D,), 0.3, 4.0, ((0, 2),))
    query_weight = scatter_about(splits[6], (D, D), D ** -0.5, 0.21875, ((0, 2),))
    query_bias = scatter_about(splits[7], (D,), 0.5, 6.0, ((0, 2),))
    key_weight = scatter_about(splits[8], (D, D), D ** -0.5, 0.21875, ((0, 2),))
    value_weight = scatter_about(splits[9], (D, D), D ** -0.5, 0.21875, ((0, 2),))
    value_bias = scatter_about(splits[10], (D,), 0.05, 0.75, ((0, 2),))
    output_weight = scatter_about(splits[11], (D, D), (max(1, D // 256)) ** -0.5, 3.5, ((0, 2),))
    output_bias = scatter_about(splits[12], (D,), 0.3, 4.0, ((0, 2),))
    second_gain = jnp.clip(1.0 + 0.1 * jax.random.normal(splits[13], (D,), jnp.float32), 0.5, 1.5).astype(jnp.bfloat16)
    second_shift = scatter_about(splits[14], (D,), 0.3, 4.0, ((0, 2),))
    up_weight = scatter_about(splits[15], (D, FF), D ** -0.5, 0.21875, ((0, 2),))
    up_bias = scatter_about(splits[16], (FF,), 0.3, 4.0, ((0, 2),))
    down_weight = scatter_about(splits[17], (FF, D), FF ** -0.5, 0.109375, ((0, 2),))
    down_bias = scatter_about(splits[18], (D,), 0.3, 4.0, ((0, 2),))
    return dict(tokens=tokens, cotangent=cotangent, doc_lengths=doc_lengths, deal=deal, first_gain=first_gain, first_shift=first_shift, query_weight=query_weight, query_bias=query_bias, key_weight=key_weight, value_weight=value_weight, value_bias=value_bias, output_weight=output_weight, output_bias=output_bias, second_gain=second_gain, second_shift=second_shift, up_weight=up_weight, up_bias=up_bias, down_weight=down_weight, down_bias=down_bias)


@jax.custom_vjp
def low(v):
    return lax.optimization_barrier(v.astype(jnp.bfloat16)).astype(jnp.float32)

@jax.custom_vjp
def low_back(v):
    return v

def low_keep(v):
    return (low(v), None)

def low_pass(kept, grad):
    return (grad,)

def back_keep(v):
    return (v, None)

def back_low(kept, grad):
    return (low(grad),)
low.defvjp(low_keep, low_pass)
low_back.defvjp(back_keep, back_low)
EPS = 1e-05
SCALE = 0.125
MASKED = -1e+30
HIGH = lax.Precision.HIGHEST
ROOT_HALF = 0.7071067811865476

def smooth_unit(values):
    return 0.5 * values * (1.0 + jax.scipy.special.erf(values * ROOT_HALF))

def layer_norm(values, gain, shift):
    mean = lax.optimization_barrier(jnp.mean(values, axis=-1, keepdims=True))
    centred = values - mean
    spread = lax.optimization_barrier(jnp.mean(centred * centred, axis=-1, keepdims=True))
    return centred * lax.rsqrt(spread + EPS) * gain + shift

def describe(positions, doc_lengths):
    positions = positions.astype(jnp.int32)
    lengths = doc_lengths.astype(jnp.int32)
    starts = (jnp.cumsum(lengths) - lengths).astype(jnp.int32)
    before = starts <= positions[..., None]
    begin = lax.optimization_barrier(jnp.max(jnp.where(before, starts, jnp.int32(0)), axis=-1)).astype(jnp.int32)
    within = (positions - begin).astype(jnp.int32)
    period = jnp.int32(SEG + NSUM)
    return (positions, begin, (within // period).astype(jnp.int32), within % period >= SEG)

def permitted(query, key):
    same_doc = query[1][:, None] == key[1][None, :]
    causal = (key[0][None, :] <= query[0][:, None]) & (key[0][None, :] >= 0)
    visible = (key[2][None, :] == query[2][:, None]) | key[3][None, :]
    return same_doc & causal & visible

def attention(queries, keys, values, info):
    rows_block = min(512, TOKENS)
    window = min(TOKENS, DOC_MAX + rows_block)

    def one_block(index):
        first = (index * rows_block).astype(jnp.int32)
        lead = jnp.clip(first + rows_block - window, 0, TOKENS - window).astype(jnp.int32)
        part_q = lax.dynamic_slice_in_dim(queries, first, rows_block).reshape(rows_block, HEADS, DH)
        part_k = lax.dynamic_slice_in_dim(keys, lead, window).reshape(window, HEADS, DH)
        part_v = lax.dynamic_slice_in_dim(values, lead, window).reshape(window, HEADS, DH)
        query_info = tuple((lax.dynamic_slice_in_dim(item, first, rows_block) for item in info))
        key_info = tuple((lax.dynamic_slice_in_dim(item, lead, window) for item in info))
        permit = permitted(query_info, key_info)
        scores = low_back(jnp.einsum('qhd,khd->hqk', part_q, part_k, precision=HIGH))
        scores = jnp.where(permit[None], scores, MASKED)
        probs = low(jax.nn.softmax(scores, axis=-1))
        return jnp.einsum('hqk,khd->qhd', probs, part_v, precision=HIGH).reshape(rows_block, D)
    pieces = lax.map(jax.checkpoint(one_block), jnp.arange(TOKENS // rows_block, dtype=jnp.int32))
    return pieces.reshape(TOKENS, D)

def reference(tokens, cotangent, doc_lengths, deal, first_gain, first_shift, query_weight, query_bias, key_weight, value_weight, value_bias, output_weight, output_bias, second_gain, second_shift, up_weight, up_bias, down_weight, down_bias):
    rows = jnp.arange(TOKENS, dtype=jnp.int32)
    positions = (deal[rows // BLK] * BLK + rows % BLK).astype(jnp.int32)
    inverse = jnp.zeros((TOKENS,), jnp.int32).at[positions].set(rows)
    ordered_x = tokens.astype(jnp.float32)[inverse]
    ordered_g = cotangent.astype(jnp.float32)[inverse]
    info = describe(rows, doc_lengths)
    weights = tuple((item.astype(jnp.float32) for item in (first_gain, first_shift, query_weight, query_bias, key_weight, value_weight, value_bias, output_weight, output_bias, second_gain, second_shift, up_weight, up_bias, down_weight, down_bias)))

    def forward(values, lower_gain, lower_shift, query_mat, query_add, key_mat, value_mat, value_add, output_mat, output_add, upper_gain, upper_shift, expand_mat, expand_add, reduce_mat, reduce_add):
        normed = low(layer_norm(values, lower_gain, lower_shift))
        queries = low(low_back((jnp.dot(normed, query_mat, precision=HIGH) + query_add) * SCALE))
        keys = low(low_back(jnp.dot(normed, key_mat, precision=HIGH)))
        vals = low(low_back(jnp.dot(normed, value_mat, precision=HIGH) + value_add))
        mixed = low(low_back(attention(queries, keys, vals, info)))
        middle = values + low_back(jnp.dot(mixed, output_mat, precision=HIGH) + output_add)
        second = low(layer_norm(middle, upper_gain, upper_shift))
        expanded = low_back(jnp.dot(second, expand_mat, precision=HIGH) + expand_add)
        hidden = low(low_back(smooth_unit(expanded)))
        return middle + jnp.dot(hidden, reduce_mat, precision=HIGH) + reduce_add
    output, pull = jax.vjp(forward, ordered_x, *weights)
    grads = pull(ordered_g)
    return (output[positions].astype(jnp.bfloat16), grads[0][positions], grads[1], grads[2], grads[3], grads[4], grads[5], grads[6], grads[7], grads[8], grads[9], grads[10], grads[11], grads[12], grads[13], grads[14], grads[15])
```

```python
import functools

import jax
import jax.numpy as jnp
from jax import lax
from jax.experimental import pallas as pl
from jax.experimental.pallas import tpu as pltpu
from jax.sharding import Mesh
from jax.sharding import PartitionSpec as P

HEADS = 12
DH = 64
NSUM = 50
SEG = 2048
BLK = 128
GROUPS = 4
PER = HEADS // GROUPS
HW = PER * DH
WIDE = PER * BLK
CHUNK = 2 * BLK
EPS = 1e-05
SCALE = 0.125
MASKED = -1e30
ROOT_HALF = 0.7071067811865476
VMEM_LIMIT = 56 << 20
bf16 = jnp.bfloat16
f32 = jnp.float32


def smooth_unit(values):
    return 0.5 * values * (1.0 + jax.scipy.special.erf(values * ROOT_HALF))


def layer_norm(values, gain, shift):
    mean = jnp.mean(values, axis=-1, keepdims=True)
    centred = values - mean
    spread = jnp.mean(centred * centred, axis=-1, keepdims=True)
    return centred * lax.rsqrt(spread + EPS) * gain + shift


def outer(left, right):
    return lax.dot_general(left, right, (((0,), (0,)), ((), ())), preferred_element_type=f32)


def inner(left, right):
    return lax.dot_general(left, right, (((1,), (1,)), ((), ())), preferred_element_type=f32)


def dot(left, right):
    return jnp.dot(left, right, preferred_element_type=f32)


def first_visible(positions, doc_lengths):
    count = doc_lengths.shape[0]
    order = jnp.arange(count)
    starts = jnp.sum(jnp.where(order[None, :] < order[:, None], doc_lengths[None, :], 0), axis=1)
    before = starts <= positions[..., None]
    begin = jnp.max(jnp.where(before, starts, 0), axis=-1)
    return jnp.where(positions - begin >= SEG + NSUM, begin + SEG, begin)


def spread_heads_t(part_t, order):
    rows = []
    zero = jnp.zeros((DH, BLK), part_t.dtype)
    for head in order:
        if head is None:
            rows.append(jnp.zeros((DH, WIDE), part_t.dtype))
        else:
            piece = part_t[DH * head : DH * head + DH]
            rows.append(
                jnp.concatenate([piece if h == head else zero for h in range(PER)], axis=1)
            )
    return jnp.concatenate(rows, axis=0)


K_ORDER = (0, 1, 2, None)
V_ORDER = (None, 2, 0, 1)


def visible(chunk, first, own):
    at = chunk * CHUNK + lax.broadcasted_iota(jnp.int32, (CHUNK, BLK), 0)
    allowed = (at >= first) & (at <= own)
    return jnp.concatenate([allowed] * PER, axis=1)


def load_chunk(kv_ref, where_ref, chunk):
    return jnp.concatenate(
        [kv_ref[where_ref[2 * chunk]], kv_ref[where_ref[2 * chunk + 1]]], axis=0
    )


def forward_kernel(
    where_ref, text_ref, low_ref, high_ref, q_ref, kv_ref, first_ref,
    out_ref, wide_ref, lse_ref, vt_ref, acc_ref,
):
    chunks = kv_ref.shape[0] // 2

    def turn(chunk, _):
        vt_ref[chunk] = load_chunk(kv_ref, where_ref, chunk)[:, BLK : 3 * BLK].T[DH:]
        return _

    lax.fori_loop(0, chunks, turn, 0)

    def one_slot(slot, _):
        wide_q = spread_heads_t(q_ref[slot].T[:HW], K_ORDER)
        first = first_ref[slot]
        own = text_ref[slot] * BLK + lax.broadcasted_iota(jnp.int32, (1, BLK), 1)
        acc_ref[...] = jnp.zeros_like(acc_ref)

        def step(chunk, carry):
            top, total = carry
            part = load_chunk(kv_ref, where_ref, chunk)
            scores = dot(part[:, : 2 * BLK], wide_q)
            scores = jnp.where(visible(chunk, first, own), scores, MASKED)
            fresh = jnp.maximum(top, jnp.max(scores, axis=0, keepdims=True))
            expo = jnp.exp(scores - fresh)
            shrink = jnp.exp(top - fresh)
            total = total * shrink + jnp.sum(expo, axis=0, keepdims=True)
            acc_ref[...] = acc_ref[...] * shrink + dot(vt_ref[chunk], expo.astype(bf16))
            return fresh, total

        top, total = lax.fori_loop(
            low_ref[slot],
            high_ref[slot] + 1,
            step,
            (jnp.full((1, WIDE), MASKED, f32), jnp.zeros((1, WIDE), f32)),
        )
        lse_ref[slot] = top + jnp.log(total)
        scaled = acc_ref[...] / total
        pieces = []
        for head in range(PER):
            row = DH * V_ORDER.index(head) - DH
            pieces.append(scaled[row : row + DH, BLK * head : BLK * head + BLK])
        kept = jnp.concatenate(pieces, axis=0)
        wide_ref[slot] = kept
        out_ref[slot] = kept.astype(bf16)
        return _

    lax.fori_loop(0, q_ref.shape[0], one_slot, 0)


def whole_vmem():
    return pl.BlockSpec(memory_space=pltpu.VMEM)


def whole_smem():
    return pl.BlockSpec(memory_space=pltpu.SMEM)


def attend_forward(where, text, low, high, q, kv, first):
    slots = q.shape[0]
    blocks = kv.shape[0]
    return pl.pallas_call(
        forward_kernel,
        out_shape=(
            jax.ShapeDtypeStruct((slots, HW, BLK), bf16),
            jax.ShapeDtypeStruct((slots, HW, BLK), f32),
            jax.ShapeDtypeStruct((slots, 1, WIDE), f32),
        ),
        in_specs=[whole_smem()] * 4 + [whole_vmem()] * 3,
        out_specs=(whole_vmem(),) * 3,
        scratch_shapes=[
            pltpu.VMEM((blocks // 2, HW, CHUNK), bf16),
            pltpu.VMEM((HW, WIDE), f32),
        ],
        compiler_params=pltpu.CompilerParams(vmem_limit_bytes=VMEM_LIMIT),
        name="attend_forward",
    )(where, text, low, high, q, kv, first)


def backward_kernel(
    where_ref, text_ref, low_ref, high_ref, q_ref, kv_ref, first_ref, lse_ref, do_ref, wide_ref,
    dq_ref, dkv_ref, qt_ref, qm_ref, dot_ref, dom_ref, delta_ref, acc_ref, dk_acc, dv_acc,
):
    slots = q_ref.shape[0]
    chunks = kv_ref.shape[0] // 2

    def ready(slot, _):
        q = q_ref[slot]
        qt_ref[slot] = spread_heads_t(q.T[:HW], K_ORDER)
        lane = lax.broadcasted_iota(jnp.int32, (BLK, 2 * BLK), 1) // DH
        zero = jnp.zeros_like(q)
        qm_ref[slot] = jnp.concatenate(
            [jnp.where(lane == K_ORDER.index(h), q, zero) for h in range(PER)], axis=0
        )
        grad_t = do_ref[slot]
        dot_ref[slot] = spread_heads_t(grad_t, V_ORDER)
        ordered = jnp.concatenate(
            [
                jnp.zeros((DH, BLK), bf16) if h is None else grad_t[DH * h : DH * h + DH]
                for h in V_ORDER
            ],
            axis=0,
        ).T
        dom_ref[slot] = jnp.concatenate(
            [jnp.where(lane == V_ORDER.index(h), ordered, zero) for h in range(PER)], axis=0
        )
        both = grad_t.astype(f32) * wide_ref[slot]
        delta_ref[slot] = jnp.concatenate(
            [jnp.sum(both[DH * h : DH * h + DH], axis=0, keepdims=True) for h in range(PER)],
            axis=1,
        )
        acc_ref[slot] = jnp.zeros((HW, WIDE), f32)
        return _

    lax.fori_loop(0, slots, ready, 0)

    def one_chunk(chunk, _):
        part = load_chunk(kv_ref, where_ref, chunk)
        keys = part[:, : 2 * BLK]
        vals = part[:, BLK:]
        keys_t = keys.T[:HW]
        dk_acc[...] = jnp.zeros_like(dk_acc)
        dv_acc[...] = jnp.zeros_like(dv_acc)

        def one_slot(slot, kept):
            @pl.when((low_ref[slot] <= chunk) & (chunk <= high_ref[slot]))
            def _():
                own = text_ref[slot] * BLK + lax.broadcasted_iota(jnp.int32, (1, BLK), 1)
                scores = dot(keys, qt_ref[slot])
                probs = jnp.where(
                    visible(chunk, first_ref[slot], own), jnp.exp(scores - lse_ref[slot]), 0.0
                )
                dprobs = dot(vals, dot_ref[slot])
                dscores = (probs * (dprobs - delta_ref[slot])).astype(bf16)
                dv_acc[...] += dot(probs.astype(bf16), dom_ref[slot])
                dk_acc[...] += dot(dscores, qm_ref[slot])
                acc_ref[slot] += dot(keys_t, dscores)

            return kept

        lax.fori_loop(0, slots, one_slot, 0)
        packed = jnp.concatenate(
            [
                dk_acc[:, :BLK],
                dk_acc[:, BLK:] + dv_acc[:, :BLK],
                dv_acc[:, BLK:],
            ],
            axis=1,
        ).astype(bf16)
        dkv_ref[where_ref[2 * chunk]] = packed[:BLK]
        dkv_ref[where_ref[2 * chunk + 1]] = packed[BLK:]
        return _

    lax.fori_loop(0, chunks, one_chunk, 0)

    def finish(slot, _):
        total = acc_ref[slot]
        kept = jnp.concatenate(
            [total[DH * h : DH * h + DH, BLK * h : BLK * h + BLK] for h in range(PER)]
            + [jnp.zeros((DH, BLK), f32)],
            axis=0,
        )
        dq_ref[slot] = kept.T.astype(bf16)
        return _

    lax.fori_loop(0, slots, finish, 0)


def attend_backward(where, text, low, high, q, kv, first, lse, grad_t, wide):
    slots = q.shape[0]
    return pl.pallas_call(
        backward_kernel,
        out_shape=(
            jax.ShapeDtypeStruct((slots, BLK, 2 * BLK), bf16),
            jax.ShapeDtypeStruct(kv.shape, bf16),
        ),
        in_specs=[whole_smem()] * 4 + [whole_vmem()] * 6,
        out_specs=(whole_vmem(),) * 2,
        scratch_shapes=[
            pltpu.VMEM((slots, 2 * BLK, WIDE), bf16),
            pltpu.VMEM((slots, WIDE, 2 * BLK), bf16),
            pltpu.VMEM((slots, 2 * BLK, WIDE), bf16),
            pltpu.VMEM((slots, WIDE, 2 * BLK), bf16),
            pltpu.VMEM((slots, 1, WIDE), f32),
            pltpu.VMEM((slots, HW, WIDE), f32),
            pltpu.VMEM((CHUNK, 2 * BLK), f32),
            pltpu.VMEM((CHUNK, 2 * BLK), f32),
        ],
        compiler_params=pltpu.CompilerParams(vmem_limit_bytes=VMEM_LIMIT + (4 << 20)),
        name="attend_backward",
    )(where, text, low, high, q, kv, first, lse, grad_t, wide)


def pack_kv(key_part, value_part):
    return jnp.concatenate(
        [key_part, value_part[..., 2 * DH :], value_part[..., : 2 * DH]], axis=-1
    )


def unpack_kv(both):
    return both[..., :HW], jnp.concatenate([both[..., HW + DH :], both[..., HW : HW + DH]], axis=-1)


ROWS = ("r", "core", "x")
ALL = ("g", "r", "core", "x")


def shards(
    tokens, cotangent, doc_lengths, deal, first_gain, first_shift, query_weight, query_bias,
    key_weight, value_weight, value_bias, output_weight, output_bias, second_gain, second_shift,
    up_weight, up_bias, down_weight, down_bias,
):
    def whole(item):
        return lax.all_gather(item, "x", axis=0, tiled=True)

    rows, width = tokens.shape
    group = lax.axis_index("g")
    rest = lax.axis_index(ROWS)
    blocks = deal.shape[0]
    per_group = blocks // (2 * GROUPS)

    gathered = deal.reshape(GROUPS, per_group, 2).transpose(1, 0, 2).reshape(-1)
    order = jnp.arange(blocks, dtype=jnp.int32)
    where = jnp.sum(jnp.where(gathered[None, :] == order[:, None], order[None, :], 0), axis=1)
    text = lax.dynamic_slice_in_dim(gathered, rest * 2 * GROUPS, 2 * GROUPS)
    positions = text[:, None] * BLK + jnp.arange(BLK, dtype=jnp.int32)[None, :]
    first = first_visible(positions, doc_lengths)
    low = first[:, 0] // CHUNK
    high = text // 2

    def columns(item):
        return lax.dynamic_slice_in_dim(item, group * HW, HW, 1)

    narrow = jnp.concatenate(
        [columns(query_weight), columns(key_weight), columns(value_weight)], axis=1
    )
    narrow = whole(narrow)
    wq, wk, wv = narrow[:, :HW], narrow[:, HW : 2 * HW], narrow[:, 2 * HW :]
    small = whole(
        jnp.stack([first_gain, first_shift, query_bias, value_bias, output_bias, second_gain, second_shift, down_bias], axis=1)
    ).astype(f32)
    lower_gain, lower_shift, query_add, value_add, output_add, upper_gain, upper_shift, reduce_add = (
        small[:, i] for i in range(8)
    )
    query_part = lax.dynamic_slice_in_dim(query_add, group * HW, HW)
    value_part = lax.dynamic_slice_in_dim(value_add, group * HW, HW)
    expand_add = whole(up_bias).astype(f32)
    output_mat = whole(output_weight)
    expand_mat = whole(up_weight)
    reduce_mat = whole(down_weight)

    lined = lax.all_gather(tokens, "g", axis=0, tiled=True).astype(f32)
    normed = layer_norm(lined, lower_gain, lower_shift).astype(bf16)
    q = ((dot(normed, wq) + query_part) * SCALE).astype(bf16)
    k = dot(normed, wk).astype(bf16)
    v = (dot(normed, wv) + value_part).astype(bf16)
    kv = lax.all_gather(pack_kv(k, v), ROWS, axis=0, tiled=True)
    kv = kv.reshape(blocks, BLK, 2 * HW)
    q_pad = jnp.pad(q, ((0, 0), (0, 2 * BLK - HW))).reshape(2 * GROUPS, BLK, 2 * BLK)
    first = first.reshape(2 * GROUPS, 1, BLK)
    out_t, wide, lse = attend_forward(where, text, low, high, q_pad, kv, first)

    def swap(item):
        item = item.reshape(GROUPS, 2, HW, BLK)
        return lax.all_to_all(item, "g", 0, 0, tiled=True)

    attn_t = swap(out_t).transpose(0, 2, 1, 3).reshape(width, rows)

    inputs = tokens.astype(f32)
    middle = inputs + outer(attn_t, output_mat) + output_add
    second_normed = layer_norm(middle, upper_gain, upper_shift).astype(bf16)
    expanded = dot(second_normed, expand_mat) + expand_add
    hidden = smooth_unit(expanded).astype(bf16)
    result = (middle + dot(hidden, reduce_mat) + reduce_add).astype(bf16)
    grad_in = cotangent.astype(f32)
    term_reduce_mat = outer(hidden, cotangent)
    term_reduce_add = jnp.sum(grad_in, axis=0)
    grad_hidden = inner(cotangent, reduce_mat).astype(bf16)
    _, pull_unit = jax.vjp(smooth_unit, expanded)
    grad_expand = pull_unit(grad_hidden.astype(f32))[0].astype(bf16)
    term_expand_mat = outer(second_normed, grad_expand)
    term_expand_add = jnp.sum(grad_expand.astype(f32), axis=0)
    grad_second = inner(grad_expand, expand_mat)
    _, pull_second = jax.vjp(layer_norm, middle, upper_gain, upper_shift)
    grad_middle_part, term_upper_gain, term_upper_shift = pull_second(grad_second)
    grad_middle = grad_in + grad_middle_part
    grad_branch = grad_middle.astype(bf16)
    term_output_mat = dot(attn_t, grad_branch)
    term_output_add = jnp.sum(grad_branch.astype(f32), axis=0)
    grad_mixed_t = inner(output_mat, grad_branch).astype(bf16)

    grad_t = swap(grad_mixed_t.reshape(GROUPS, HW, 2, BLK).transpose(0, 2, 1, 3))
    grad_t = grad_t.reshape(2 * GROUPS, HW, BLK)
    dq, dkv = attend_backward(where, text, low, high, q_pad, kv, first, lse, grad_t, wide)
    dq = dq.reshape(-1, 2 * BLK)[:, :HW] * bf16(SCALE)
    dkv = lax.psum_scatter(dkv.reshape(-1, 2 * HW), ROWS, scatter_dimension=0, tiled=True)
    dk, dv = unpack_kv(dkv)
    grad_first = (inner(dq, wq) + inner(dk, wk) + inner(dv, wv)).astype(bf16)
    grad_first = lax.psum_scatter(grad_first, "g", scatter_dimension=0, tiled=True).astype(f32)
    term_narrow = outer(normed, jnp.concatenate([dq, dk, dv], axis=1)).astype(bf16)
    term_query_add = jnp.sum(dq.astype(f32), axis=0)
    term_value_add = jnp.sum(dv.astype(f32), axis=0)
    _, pull_first = jax.vjp(layer_norm, inputs, lower_gain, lower_shift)
    grad_input_part, term_lower_gain, term_lower_shift = pull_first(grad_first)
    grad_tokens = grad_middle + grad_input_part

    def owned(item, axes):
        mine = lax.psum_scatter(item.astype(bf16), "x", scatter_dimension=0, tiled=True)
        return lax.psum(mine, axes).astype(f32)

    ctx = ("g", "r", "core")
    narrow_own = owned(term_narrow, ("r", "core"))
    narrow_own = lax.all_gather(narrow_own.astype(bf16), "g").astype(f32)
    query_own, key_own, value_own = (
        narrow_own[:, :, i * HW : (i + 1) * HW].transpose(1, 0, 2).reshape(-1, width)
        for i in range(3)
    )
    half = lax.axis_index("x") * (width // 2)

    def own_half(item):
        return lax.dynamic_slice_in_dim(item, half, width // 2)

    vectors = jnp.stack(
        [
            term_lower_gain, term_lower_shift, term_output_add, term_upper_gain, term_upper_shift, term_reduce_add,
            lax.dynamic_update_slice_in_dim(jnp.zeros((width,), f32), term_query_add, group * HW, 0),
            lax.dynamic_update_slice_in_dim(jnp.zeros((width,), f32), term_value_add, group * HW, 0),
        ]
        + [term_expand_add[i * width : (i + 1) * width] for i in range(4)]
    )
    vectors = lax.psum(vectors, ALL)
    expand_own = lax.dynamic_slice_in_dim(
        vectors[8:].reshape(-1), lax.axis_index("x") * (2 * width), 2 * width
    )
    return (
        result,
        grad_tokens,
        own_half(vectors[0]),
        own_half(vectors[1]),
        query_own,
        own_half(vectors[6]),
        key_own,
        value_own,
        own_half(vectors[7]),
        owned(term_output_mat, ctx),
        own_half(vectors[2]),
        own_half(vectors[3]),
        own_half(vectors[4]),
        owned(term_expand_mat, ctx),
        expand_own,
        owned(term_reduce_mat, ctx),
        own_half(vectors[5]),
    )


def solution(mesh):
    devices = mesh.devices
    inner_mesh = Mesh(devices.reshape(GROUPS, devices.shape[0] // (2 * GROUPS), 2, 2), ALL)
    row = P(ALL, None)
    mat = P("x", None)
    vec = P("x")
    in_specs = (
        row, row, P(), P(), vec, vec, mat, vec, mat, mat, vec, mat, vec, vec, vec, mat, vec, mat, vec,
    )
    out_specs = (
        row, row, vec, vec, mat, vec, mat, mat, vec, mat, vec, vec, vec, mat, vec, mat, vec,
    )
    return jax.shard_map(
        shards, mesh=inner_mesh, in_specs=in_specs, out_specs=out_specs, check_vma=False
    )
```

```python
import functools

import jax
import jax.numpy as jnp
from jax import lax
from jax.experimental import pallas as pl
from jax.experimental.pallas import tpu as pltpu
from jax.sharding import Mesh
from jax.sharding import PartitionSpec as P

HEADS = 12
DH = 64
NSUM = 50
SEG = 2048
BLK = 128
GROUPS = 4
PER = HEADS // GROUPS
HW = PER * DH
WIDE = PER * BLK
CHUNK = 2 * BLK
EPS = 1e-05
SCALE = 0.125
MASKED = -1e30
ROOT_HALF = 0.7071067811865476
PDF_SCALE = 0.3989422804014327
VMEM_LIMIT = 56 << 20
bf16 = jnp.bfloat16
f32 = jnp.float32


def layer_norm(values, gain, shift):
    mean = jnp.mean(values, axis=-1, keepdims=True)
    centred = values - mean
    spread = jnp.mean(centred * centred, axis=-1, keepdims=True)
    return centred * lax.rsqrt(spread + EPS) * gain + shift


def outer(left, right):
    return lax.dot_general(left, right, (((0,), (0,)), ((), ())), preferred_element_type=f32)


def inner(left, right):
    return lax.dot_general(left, right, (((1,), (1,)), ((), ())), preferred_element_type=f32)


def dot(left, right):
    return jnp.dot(left, right, preferred_element_type=f32)


def first_visible(positions, doc_lengths):
    count = doc_lengths.shape[0]
    order = jnp.arange(count)
    starts = jnp.sum(jnp.where(order[None, :] < order[:, None], doc_lengths[None, :], 0), axis=1)
    before = starts <= positions[..., None]
    begin = jnp.max(jnp.where(before, starts, 0), axis=-1)
    return jnp.where(positions - begin >= SEG + NSUM, begin + SEG, begin)


def spread_heads_t(part_t, order):
    rows = []
    zero = jnp.zeros((DH, BLK), part_t.dtype)
    for head in order:
        if head is None:
            rows.append(jnp.zeros((DH, WIDE), part_t.dtype))
        else:
            piece = part_t[DH * head : DH * head + DH]
            rows.append(
                jnp.concatenate([piece if h == head else zero for h in range(PER)], axis=1)
            )
    return jnp.concatenate(rows, axis=0)


K_ORDER = (0, 1, 2, None)
V_ORDER = (None, 2, 0, 1)


def visible(chunk, first, own):
    at = chunk * CHUNK + lax.broadcasted_iota(jnp.int32, (CHUNK, BLK), 0)
    allowed = (at >= first) & (at <= own)
    return jnp.concatenate([allowed] * PER, axis=1)


def load_chunk(kv_ref, where_ref, chunk):
    return jnp.concatenate(
        [kv_ref[where_ref[2 * chunk]], kv_ref[where_ref[2 * chunk + 1]]], axis=0
    )


def forward_kernel(
    where_ref, text_ref, low_ref, high_ref, q_ref, kv_ref, first_ref,
    out_ref, wide_ref, lse_ref, vt_ref, acc_ref,
):
    chunks = kv_ref.shape[0] // 2

    def turn(chunk, _):
        vt_ref[chunk] = load_chunk(kv_ref, where_ref, chunk)[:, BLK : 3 * BLK].T[DH:]
        return _

    lax.fori_loop(0, chunks, turn, 0)

    def one_slot(slot, _):
        wide_q = spread_heads_t(q_ref[slot].T[:HW], K_ORDER)
        first = first_ref[slot]
        own = text_ref[slot] * BLK + lax.broadcasted_iota(jnp.int32, (1, BLK), 1)
        acc_ref[...] = jnp.zeros_like(acc_ref)

        def step(chunk, carry):
            top, total = carry
            part = load_chunk(kv_ref, where_ref, chunk)
            scores = dot(part[:, : 2 * BLK], wide_q)
            scores = jnp.where(visible(chunk, first, own), scores, MASKED)
            fresh = jnp.maximum(top, jnp.max(scores, axis=0, keepdims=True))
            expo = jnp.exp(scores - fresh)
            shrink = jnp.exp(top - fresh)
            total = total * shrink + jnp.sum(expo, axis=0, keepdims=True)
            acc_ref[...] = acc_ref[...] * shrink + dot(vt_ref[chunk], expo.astype(bf16))
            return fresh, total

        top, total = lax.fori_loop(
            low_ref[slot],
            high_ref[slot] + 1,
            step,
            (jnp.full((1, WIDE), MASKED, f32), jnp.zeros((1, WIDE), f32)),
        )
        lse_ref[slot] = top + jnp.log(total)
        scaled = acc_ref[...] / total
        pieces = []
        for head in range(PER):
            row = DH * V_ORDER.index(head) - DH
            pieces.append(scaled[row : row + DH, BLK * head : BLK * head + BLK])
        kept = jnp.concatenate(pieces, axis=0)
        wide_ref[slot] = kept
        out_ref[slot] = kept.astype(bf16)
        return _

    lax.fori_loop(0, q_ref.shape[0], one_slot, 0)


def whole_vmem():
    return pl.BlockSpec(memory_space=pltpu.VMEM)


def whole_smem():
    return pl.BlockSpec(memory_space=pltpu.SMEM)


def attend_forward(where, text, low, high, q, kv, first):
    slots = q.shape[0]
    blocks = kv.shape[0]
    return pl.pallas_call(
        forward_kernel,
        out_shape=(
            jax.ShapeDtypeStruct((slots, HW, BLK), bf16),
            jax.ShapeDtypeStruct((slots, HW, BLK), f32),
            jax.ShapeDtypeStruct((slots, 1, WIDE), f32),
        ),
        in_specs=[whole_smem()] * 4 + [whole_vmem()] * 3,
        out_specs=(whole_vmem(),) * 3,
        scratch_shapes=[
            pltpu.VMEM((blocks // 2, HW, CHUNK), bf16),
            pltpu.VMEM((HW, WIDE), f32),
        ],
        compiler_params=pltpu.CompilerParams(vmem_limit_bytes=VMEM_LIMIT),
        name="attend_forward",
    )(where, text, low, high, q, kv, first)


def backward_kernel(
    where_ref, text_ref, low_ref, high_ref, q_ref, kv_ref, first_ref, lse_ref, do_ref, wide_ref,
    dq_ref, dkv_ref, qt_ref, qm_ref, dot_ref, dom_ref, delta_ref, acc_ref, dk_acc, dv_acc,
):
    slots = q_ref.shape[0]
    chunks = kv_ref.shape[0] // 2

    def ready(slot, _):
        q = q_ref[slot]
        qt_ref[slot] = spread_heads_t(q.T[:HW], K_ORDER)
        lane = lax.broadcasted_iota(jnp.int32, (BLK, 2 * BLK), 1) // DH
        zero = jnp.zeros_like(q)
        qm_ref[slot] = jnp.concatenate(
            [jnp.where(lane == K_ORDER.index(h), q, zero) for h in range(PER)], axis=0
        )
        grad_t = do_ref[slot]
        dot_ref[slot] = spread_heads_t(grad_t, V_ORDER)
        ordered = jnp.concatenate(
            [
                jnp.zeros((DH, BLK), bf16) if h is None else grad_t[DH * h : DH * h + DH]
                for h in V_ORDER
            ],
            axis=0,
        ).T
        dom_ref[slot] = jnp.concatenate(
            [jnp.where(lane == V_ORDER.index(h), ordered, zero) for h in range(PER)], axis=0
        )
        both = grad_t.astype(f32) * wide_ref[slot]
        delta_ref[slot] = jnp.concatenate(
            [jnp.sum(both[DH * h : DH * h + DH], axis=0, keepdims=True) for h in range(PER)],
            axis=1,
        )
        acc_ref[slot] = jnp.zeros((HW, WIDE), f32)
        return _

    lax.fori_loop(0, slots, ready, 0)

    def one_chunk(chunk, _):
        part = load_chunk(kv_ref, where_ref, chunk)
        keys = part[:, : 2 * BLK]
        vals = part[:, BLK:]
        keys_t = keys.T[:HW]
        dk_acc[...] = jnp.zeros_like(dk_acc)
        dv_acc[...] = jnp.zeros_like(dv_acc)

        def one_slot(slot, kept):
            @pl.when((low_ref[slot] <= chunk) & (chunk <= high_ref[slot]))
            def _():
                own = text_ref[slot] * BLK + lax.broadcasted_iota(jnp.int32, (1, BLK), 1)
                scores = dot(keys, qt_ref[slot])
                probs = jnp.where(
                    visible(chunk, first_ref[slot], own), jnp.exp(scores - lse_ref[slot]), 0.0
                )
                dprobs = dot(vals, dot_ref[slot])
                dscores = (probs * (dprobs - delta_ref[slot])).astype(bf16)
                dv_acc[...] += dot(probs.astype(bf16), dom_ref[slot])
                dk_acc[...] += dot(dscores, qm_ref[slot])
                acc_ref[slot] += dot(keys_t, dscores)

            return kept

        lax.fori_loop(0, slots, one_slot, 0)
        packed = jnp.concatenate(
            [
                dk_acc[:, :BLK],
                dk_acc[:, BLK:] + dv_acc[:, :BLK],
                dv_acc[:, BLK:],
            ],
            axis=1,
        ).astype(bf16)
        dkv_ref[where_ref[2 * chunk]] = packed[:BLK]
        dkv_ref[where_ref[2 * chunk + 1]] = packed[BLK:]
        return _

    lax.fori_loop(0, chunks, one_chunk, 0)

    def finish(slot, _):
        total = acc_ref[slot]
        kept = jnp.concatenate(
            [total[DH * h : DH * h + DH, BLK * h : BLK * h + BLK] for h in range(PER)]
            + [jnp.zeros((DH, BLK), f32)],
            axis=0,
        )
        dq_ref[slot] = kept.T.astype(bf16)
        return _

    lax.fori_loop(0, slots, finish, 0)


def attend_backward(where, text, low, high, q, kv, first, lse, grad_t, wide):
    slots = q.shape[0]
    return pl.pallas_call(
        backward_kernel,
        out_shape=(
            jax.ShapeDtypeStruct((slots, BLK, 2 * BLK), bf16),
            jax.ShapeDtypeStruct(kv.shape, bf16),
        ),
        in_specs=[whole_smem()] * 4 + [whole_vmem()] * 6,
        out_specs=(whole_vmem(),) * 2,
        scratch_shapes=[
            pltpu.VMEM((slots, 2 * BLK, WIDE), bf16),
            pltpu.VMEM((slots, WIDE, 2 * BLK), bf16),
            pltpu.VMEM((slots, 2 * BLK, WIDE), bf16),
            pltpu.VMEM((slots, WIDE, 2 * BLK), bf16),
            pltpu.VMEM((slots, 1, WIDE), f32),
            pltpu.VMEM((slots, HW, WIDE), f32),
            pltpu.VMEM((CHUNK, 2 * BLK), f32),
            pltpu.VMEM((CHUNK, 2 * BLK), f32),
        ],
        compiler_params=pltpu.CompilerParams(vmem_limit_bytes=VMEM_LIMIT + (4 << 20)),
        name="attend_backward",
    )(where, text, low, high, q, kv, first, lse, grad_t, wide)


MESH = pl.DeviceIdType.MESH


def send(src, dst, out_sem, in_sem, **device):
    return pltpu.make_async_remote_copy(
        src_ref=src, dst_ref=dst, send_sem=out_sem, recv_sem=in_sem, device_id=device, device_id_type=MESH
    )


def place():
    return tuple(lax.axis_index(name) for name in ("g", "r", "core", "x"))


def seat(r, core, x):
    return (r * 2 + core) * 2 + x


def greet(g, r, core, x, line):
    barrier = pltpu.get_barrier_semaphore()

    def hello(**device):
        pl.semaphore_signal(barrier, inc=1, device_id=device, device_id_type=MESH)

    hello(core=1 - core)
    hello(x=1 - x)
    hello(r=1 - r)
    if line:
        for away in range(1, GROUPS):
            hello(g=lax.rem(g + away, GROUPS))
        pl.semaphore_wait(barrier, 3 + GROUPS - 1)
    else:
        pl.when(g > 0)(lambda: hello(g=g - 1))
        pl.when(g < GROUPS - 1)(lambda: hello(g=g + 1))
        pl.semaphore_wait(barrier, 5 - jnp.where(g == 0, 1, 0) - jnp.where(g == GROUPS - 1, 1, 0))


NEAREST = tuple(tuple(sorted(range(GROUPS), key=lambda s: (abs(s - z), s))) for z in range(GROUPS))


def nearest(g, step):
    picked = NEAREST[0][step]
    for z in range(1, GROUPS):
        picked = jnp.where(g == z, NEAREST[z][step], picked)
    return picked


def gather_kernel(
    tokens_ref, narrow_ref, small_ref, up_ref, down_ref, wo_ref,
    kv_ref, q_ref, normed_ref, small_out, up_out, down_out, wo_out,
    lined, wfull, small_in, kvs,
    z_own, z_send, z_recv, s_sem, n_send, n_recv, kv_send, kv_recv, kv_local, w_send, w_recv, w_local,
):
    g, r, core, x = place()
    other = 1 - x
    rows, width = tokens_ref.shape
    half = width // 2
    fourth = half // 2
    eighth = half // 4
    greet(g, r, core, x, False)

    def along(source, away, sem):
        return send(lined.at[source], lined.at[source], sem, z_recv.at[source], g=g + away)

    lined[g] = tokens_ref[...]
    pl.when(g > 0)(lambda: along(g, -1, z_own.at[0]).start())
    pl.when(g < GROUPS - 1)(lambda: along(g, 1, z_own.at[1]).start())

    small_move = send(small_ref, small_in, s_sem.at[0], s_sem.at[1], x=other)
    small_move.start()
    mine = pl.ds(x * half + core * fourth, fourth)
    narrow_x = send(narrow_ref.at[pl.ds(core * fourth, fourth)], wfull.at[mine], n_send.at[0], n_recv.at[0], x=other)
    narrow_x.start()

    def wo_rows(owner, part):
        return wo_out.at[pl.ds(owner * half + core * fourth + part * eighth, eighth)]

    def up_rows(owner, part):
        return up_out.at[part, pl.ds(owner * half, half)]

    def down_rows(owner, part):
        return down_out.at[owner, pl.ds(part * half, half)]

    wo_x = send(wo_ref.at[pl.ds(core * fourth + r * eighth, eighth)], wo_rows(x, r), w_send.at[0], w_recv.at[0], x=other)
    up_x = send(
        up_ref.at[:, pl.ds(pl.multiple_of((2 * r + core) * width, width), width)],
        up_rows(x, r), w_send.at[1], w_recv.at[1], x=other,
    )
    down_x = send(down_ref.at[pl.ds(core * width + r * half, half)], down_rows(x, r), w_send.at[2], w_recv.at[2], x=other)
    wo_y = send(wo_rows(other, r), wo_rows(other, r), w_send.at[3], w_recv.at[3], r=1 - r)
    up_y = send(up_rows(other, r), up_rows(other, r), w_send.at[4], w_recv.at[4], r=1 - r)
    down_y = send(down_rows(other, r), down_rows(other, r), w_send.at[5], w_recv.at[5], r=1 - r)
    wo_s = [
        send(wo_rows(other, part), wo_rows(other, part), w_send.at[6 + i], w_recv.at[6 + i], core=1 - core)
        for i, part in enumerate((r, 1 - r))
    ]
    wo_x.start()
    locals_ = [
        pltpu.make_async_copy(wo_ref, wo_out.at[pl.ds(x * half, half)], w_local.at[0]),
        pltpu.make_async_copy(down_ref.at[pl.ds(core * width, width)], down_out.at[x], w_local.at[1]),
    ] + [
        pltpu.make_async_copy(
            up_ref.at[:, pl.ds(pl.multiple_of((2 * h + core) * width, width), width)],
            up_out.at[h, pl.ds(x * half, half)], w_local.at[2 + h],
        )
        for h in range(2)
    ]
    for item in locals_:
        item.start()

    wfull[pl.ds(x * half, half)] = narrow_ref[...]
    narrow_x.wait_recv()
    theirs = wfull.at[pl.ds(other * half + core * fourth, fourth)]
    narrow_s = send(theirs, theirs, n_send.at[1], n_recv.at[1], core=1 - core)
    narrow_s.start()
    small_move.wait_recv()
    small_out[...] = small_ref[...] + small_in[...]
    narrow_s.wait_recv()

    own = seat(r, core, x)

    def block(owner, source):
        return kv_ref.at[owner, source]

    def push(step, kind, what, **device):
        copy = send(what[0], what[1], kv_send.at[kind, step], kv_recv.at[kind, step], **device)
        copy.start()

    def settle(step, kind, owner, source):
        send(block(owner, source), block(owner, source), kv_send.at[kind, step], kv_recv.at[kind, step], x=other).wait_recv()

    def forward(step):
        source = nearest(g, step)
        by_x = block(seat(r, core, other), source)
        settle(step, 0, seat(r, core, other), source)
        if step % 2 == 0:
            push(step, 3, (by_x, by_x), r=1 - r)
        push(step, 4, (by_x, by_x), core=1 - core)
        by_y = block(seat(1 - r, core, x), source)
        settle(step, 1, seat(1 - r, core, x), source)
        if step % 2 == 1:
            push(step, 3, (by_y, by_y), x=other)
        push(step, 5, (by_y, by_y), core=1 - core)

    def forward_far(step):
        source = nearest(g, step)
        far = block(seat(1 - r, core, other), source)
        settle(step, 3, seat(1 - r, core, other), source)
        push(step, 6, (far, far), core=1 - core)

    for step in range(GROUPS):
        source = nearest(g, step)
        if step > 0:
            send(lined.at[source], lined.at[source], z_send.at[source], z_recv.at[source], x=other).wait_recv()
            pl.when((source < g) & (g < GROUPS - 1))(lambda: along(source, 1, z_send.at[source]).start())
            pl.when((source > g) & (g > 0))(lambda: along(source, -1, z_send.at[source]).start())
        values = lined[source].astype(f32)
        normed = layer_norm(values, small_out[0:1], small_out[1:2]).astype(bf16)
        normed_ref[source] = normed
        both = dot(normed, wfull[...]) + small_out[12:13, : wfull.shape[1]]
        q_ref[source] = (both[:, : 2 * BLK] * SCALE).astype(bf16)
        kvs[step] = both[:, 2 * BLK :].astype(bf16)
        here = (kvs.at[step], block(own, source))
        push(step, 0, here, x=other)
        push(step, 1, here, r=1 - r)
        push(step, 2, here, core=1 - core)
        pltpu.make_async_copy(kvs.at[step], block(own, source), kv_local.at[step]).start()
        if step == 0:
            up_x.start()
        if step == GROUPS - 1:
            down_x.start()
        if step > 0:
            forward(step - 1)
        if step > 1:
            forward_far(step - 2)
    wo_x.wait_recv()
    wo_y.start()
    wo_s[0].start()
    forward(GROUPS - 1)
    forward_far(GROUPS - 2)
    up_x.wait_recv()
    up_y.start()
    send(wo_rows(other, 1 - r), wo_rows(other, 1 - r), w_send.at[3], w_recv.at[3], r=1 - r).wait_recv()
    wo_s[1].start()
    forward_far(GROUPS - 1)
    down_x.wait_recv()
    down_y.start()

    for step in range(GROUPS):
        source = nearest(g, step)
        pltpu.make_async_copy(kvs.at[step], block(own, source), kv_local.at[step]).wait()
        settle(step, 2, seat(r, 1 - core, x), source)
        settle(step, 4, seat(r, 1 - core, other), source)
        settle(step, 5, seat(1 - r, 1 - core, x), source)
        settle(step, 6, seat(1 - r, 1 - core, other), source)
        for kind in range(7):
            send(kvs.at[step], block(own, source), kv_send.at[kind, step], kv_recv.at[kind, step], x=other).wait_send()
    pl.when(g > 0)(lambda: along(g, -1, z_own.at[0]).wait_send())
    pl.when(g < GROUPS - 1)(lambda: along(g, 1, z_own.at[1]).wait_send())
    for step in range(1, GROUPS):
        source = nearest(g, step)
        passed = ((source < g) & (g < GROUPS - 1)) | ((source > g) & (g > 0))
        pl.when(passed)(lambda: send(lined.at[source], lined.at[source], z_send.at[source], z_recv.at[source], x=other).wait_send())
    small_move.wait_send()
    narrow_x.wait_send()
    narrow_s.wait_send()
    for item in locals_:
        item.wait()
    for item in (wo_x, up_x, down_x, wo_y, up_y, down_y, *wo_s):
        item.wait_send()
    send(up_rows(other, 1 - r), up_rows(other, 1 - r), w_send.at[4], w_recv.at[4], r=1 - r).wait_recv()
    send(down_rows(other, 1 - r), down_rows(other, 1 - r), w_send.at[5], w_recv.at[5], r=1 - r).wait_recv()
    for i, part in enumerate((r, 1 - r)):
        there = wo_out.at[pl.ds(other * half + (1 - core) * fourth + part * eighth, eighth)]
        send(there, there, w_send.at[6 + i], w_recv.at[6 + i], core=1 - core).wait_recv()


def anywhere():
    return pl.BlockSpec(memory_space=pl.ANY)


def gather(tokens, narrow, small, up, down, wo):
    rows, width = tokens.shape
    wide = narrow.shape[1]
    dma = pltpu.SemaphoreType.DMA
    return pl.pallas_call(
        gather_kernel,
        out_shape=(
            jax.ShapeDtypeStruct((8, GROUPS, rows, 2 * HW), bf16),
            jax.ShapeDtypeStruct((GROUPS, rows, 2 * BLK), bf16),
            jax.ShapeDtypeStruct((GROUPS, rows, width), bf16),
            jax.ShapeDtypeStruct(small.shape, f32),
            jax.ShapeDtypeStruct((2, width, width), bf16),
            jax.ShapeDtypeStruct((2, width, width), bf16),
            jax.ShapeDtypeStruct((width, width), bf16),
        ),
        in_specs=[whole_vmem()] * 3 + [anywhere()] * 3,
        out_specs=(anywhere(), whole_vmem(), whole_vmem(), whole_vmem(), anywhere(), anywhere(), anywhere()),
        scratch_shapes=[
            pltpu.VMEM((GROUPS, rows, width), bf16),
            pltpu.VMEM((width, wide), bf16),
            pltpu.VMEM(small.shape, f32),
            pltpu.VMEM((GROUPS, rows, 2 * HW), bf16),
            dma((2,)), dma((GROUPS,)), dma((GROUPS,)), dma((2,)), dma((2,)), dma((2,)),
            dma((7, GROUPS)), dma((7, GROUPS)), dma((GROUPS,)), dma((8,)), dma((8,)), dma((4,)),
        ],
        compiler_params=pltpu.CompilerParams(
            collective_id=0, has_side_effects=True, vmem_limit_bytes=32 << 20
        ),
        name="gather",
    )(tokens, narrow, small, up, down, wo)


def erf_parts(values):
    below = 0.5 * (1.0 + lax.erf(values * ROOT_HALF))
    return below, PDF_SCALE * jnp.exp(-0.5 * values * values)


def dense_kernel(
    out_t_ref, tokens_ref, cot_ref, small_ref, up_ref, down_ref, wo_ref,
    result_ref, middle_grad_ref, grad_t_ref, up_grad_ref, down_grad_ref, wo_grad_ref, sums_ref,
    attn_in, attn_t, cots, h2s, mid_ref, n2_ref, part_y, part_d, in_y, in_d, hids, dus, grad_out,
    a_send, a_recv, c_sem, h_sem, y_sem, d_sem, o_send, o_recv,
):
    g, r, core, x = place()
    rows, width = tokens_ref.shape
    greet(g, r, core, x, True)
    cots[0] = cot_ref[...]
    cot_move = send(cots.at[0], cots.at[1], c_sem.at[0], c_sem.at[1], core=1 - core)
    cot_move.start()

    def other_group(away):
        return lax.rem(g + away, GROUPS)

    attn_moves = []
    for away in range(1, GROUPS):
        to = other_group(away)
        attn_moves.append(
            send(out_t_ref.at[pl.ds(2 * to, 2)], attn_in.at[g], a_send.at[away], a_recv.at[g], g=to)
        )
        attn_moves[-1].start()
    attn_in[g] = out_t_ref[pl.ds(2 * g, 2)]
    sums_ref[...] = jnp.zeros_like(sums_ref)
    sums_ref[5:6] = jnp.sum(cot_ref[...].astype(f32), axis=0, keepdims=True)
    for away in range(1, GROUPS):
        source = other_group(away)
        send(attn_in.at[source], attn_in.at[source], a_send.at[away], a_recv.at[source], g=source).wait_recv()
    for source in range(GROUPS):
        attn_t[HW * source : HW * source + HW] = jnp.concatenate(
            [attn_in[source, 0], attn_in[source, 1]], axis=1
        )
    middle = tokens_ref[...].astype(f32) + outer(attn_t[...], wo_ref[...]) + small_ref[2:3]
    mid_ref[...] = middle
    mean = jnp.mean(middle, axis=-1, keepdims=True)
    centred = middle - mean
    spread = jnp.mean(centred * centred, axis=-1, keepdims=True)
    scale = lax.rsqrt(spread + EPS)
    n2_ref[...] = centred * scale
    h2s[0] = (n2_ref[...] * small_ref[3:4] + small_ref[4:5]).astype(bf16)
    h2_move = send(h2s.at[0], h2s.at[1], h_sem.at[0], h_sem.at[1], core=1 - core)
    h2_move.start()

    for part in range(2):
        if part == 1:
            cot_move.wait_recv()
            h2_move.wait_recv()
        for h in range(2):
            expanded = dot(h2s[part], up_ref[h]) + small_ref[pl.ds(8 + 2 * h + core, 1)]
            below, density = erf_parts(expanded)
            hidden = (expanded * below).astype(bf16)
            hids[part, h] = hidden
            slope = below + expanded * density
            grad_hidden = inner(cots[part], down_ref[h]).astype(bf16).astype(f32)
            grad_expand = (grad_hidden * slope).astype(bf16)
            dus[part, h] = grad_expand
            if h == 0:
                part_y[part] = dot(hidden, down_ref[h])
                part_d[part] = inner(grad_expand, up_ref[h])
            else:
                part_y[part] += dot(hidden, down_ref[h])
                part_d[part] += inner(grad_expand, up_ref[h])
            sums_ref[pl.ds(8 + 2 * h + core, 1)] += jnp.sum(
                grad_expand.astype(f32), axis=0, keepdims=True
            )
    d_move = send(part_d.at[1], in_d, d_sem.at[0], d_sem.at[1], core=1 - core)
    d_move.start()
    y_move = send(part_y.at[1], in_y, y_sem.at[0], y_sem.at[1], core=1 - core)
    y_move.start()
    d_move.wait_recv()
    grad_second = part_d[0] + in_d[...]
    n2 = n2_ref[...]
    sums_ref[3:4] = jnp.sum(grad_second * n2, axis=0, keepdims=True)
    sums_ref[4:5] = jnp.sum(grad_second, axis=0, keepdims=True)
    pulled = grad_second * small_ref[3:4]
    inward = pulled - jnp.mean(pulled, axis=-1, keepdims=True) - n2 * jnp.mean(pulled * n2, axis=-1, keepdims=True)
    grad_middle = cot_ref[...].astype(f32) + inward * scale
    middle_grad_ref[...] = grad_middle
    branch = grad_middle.astype(bf16)
    sums_ref[2:3] = jnp.sum(branch.astype(f32), axis=0, keepdims=True)
    grad_out_t = inner(wo_ref[...], branch).astype(bf16)
    for group in range(GROUPS):
        for b in range(2):
            grad_out[group, b] = grad_out_t[HW * group : HW * group + HW, BLK * b : BLK * b + BLK]
    grad_moves = []
    for away in range(1, GROUPS):
        to = other_group(away)
        grad_moves.append(
            send(grad_out.at[to], grad_t_ref.at[pl.ds(2 * g, 2)], o_send.at[away], o_recv.at[g], g=to)
        )
        grad_moves[-1].start()
    grad_t_ref[pl.ds(2 * g, 2)] = grad_out[g]
    y_move.wait_recv()
    result_ref[...] = (mid_ref[...] + part_y[0] + in_y[...] + small_ref[5:6]).astype(bf16)
    wo_grad_ref[...] = dot(attn_t[...], branch).astype(bf16)
    for h in range(2):
        down_grad_ref[h] = (outer(hids[0, h], cots[0]) + outer(hids[1, h], cots[1])).astype(bf16)
        up_grad_ref[:, h * width : h * width + width] = (
            outer(h2s[0], dus[0, h]) + outer(h2s[1], dus[1, h])
        ).astype(bf16)
    for away in range(1, GROUPS):
        source = other_group(away)
        send(
            grad_t_ref.at[pl.ds(2 * source, 2)], grad_t_ref.at[pl.ds(2 * source, 2)],
            o_send.at[away], o_recv.at[source], g=source,
        ).wait_recv()
    for item in (cot_move, h2_move, y_move, d_move, *attn_moves, *grad_moves):
        item.wait_send()


def dense(out_t, tokens, cot, small, up, down, wo):
    rows, width = tokens.shape
    dma = pltpu.SemaphoreType.DMA
    full = (rows, width)
    return pl.pallas_call(
        dense_kernel,
        out_shape=(
            jax.ShapeDtypeStruct(full, bf16),
            jax.ShapeDtypeStruct(full, f32),
            jax.ShapeDtypeStruct(out_t.shape, bf16),
            jax.ShapeDtypeStruct((width, 2 * width), bf16),
            jax.ShapeDtypeStruct((2, width, width), bf16),
            jax.ShapeDtypeStruct((width, width), bf16),
            jax.ShapeDtypeStruct(small.shape, f32),
        ),
        in_specs=[whole_vmem()] * 7,
        out_specs=(whole_vmem(),) * 7,
        scratch_shapes=[
            pltpu.VMEM((GROUPS, 2, HW, BLK), bf16),
            pltpu.VMEM((width, rows), bf16),
            pltpu.VMEM((2, *full), bf16),
            pltpu.VMEM((2, *full), bf16),
            pltpu.VMEM(full, f32),
            pltpu.VMEM(full, f32),
            pltpu.VMEM((2, *full), f32),
            pltpu.VMEM((2, *full), f32),
            pltpu.VMEM(full, f32),
            pltpu.VMEM(full, f32),
            pltpu.VMEM((2, 2, *full), bf16),
            pltpu.VMEM((2, 2, *full), bf16),
            pltpu.VMEM((GROUPS, 2, HW, BLK), bf16),
            dma((GROUPS,)), dma((GROUPS,)), dma((2,)), dma((2,)), dma((2,)), dma((2,)), dma((GROUPS,)), dma((GROUPS,)),
        ],
        compiler_params=pltpu.CompilerParams(
            collective_id=1, has_side_effects=True, vmem_limit_bytes=VMEM_LIMIT
        ),
        name="dense",
    )(out_t, tokens, cot, small, up, down, wo)


def pack_kv(key_part, value_part):
    return jnp.concatenate(
        [key_part, value_part[..., 2 * DH :], value_part[..., : 2 * DH]], axis=-1
    )


def unpack_kv(both):
    return both[..., :HW], jnp.concatenate([both[..., HW + DH :], both[..., HW : HW + DH]], axis=-1)


ROWS = ("s", "r", "core", "x")
ALL = ("g", "s", "r", "core", "x")


def shards(
    tokens, cotangent, doc_lengths, deal, first_gain, first_shift, query_weight, query_bias,
    key_weight, value_weight, value_bias, output_weight, output_bias, second_gain, second_shift,
    up_weight, up_bias, down_weight, down_bias,
):
    rows, width = tokens.shape
    half = width // 2
    group = lax.axis_index("g")
    rest = lax.axis_index(ROWS)
    x = lax.axis_index("x")
    blocks = deal.shape[0]
    per_group = blocks // (2 * GROUPS)

    gathered = deal.reshape(GROUPS, per_group, 2).transpose(1, 0, 2).reshape(-1)
    order = jnp.arange(blocks, dtype=jnp.int32)
    where = jnp.sum(jnp.where(gathered[None, :] == order[:, None], order[None, :], 0), axis=1)
    text = lax.dynamic_slice_in_dim(gathered, rest * 2 * GROUPS, 2 * GROUPS)
    positions = text[:, None] * BLK + jnp.arange(BLK, dtype=jnp.int32)[None, :]
    first = first_visible(positions, doc_lengths)
    low = first[:, 0] // CHUNK
    high = text // 2
    first = first.reshape(2 * GROUPS, 1, BLK)

    def columns(item):
        return lax.dynamic_slice_in_dim(item, group * HW, HW, 1)

    wq, wk, wv = columns(query_weight), columns(key_weight), columns(value_weight)
    gap = jnp.zeros((half, 2 * BLK - HW), bf16)
    narrow = jnp.concatenate([wq, gap, pack_kv(wk, wv)], axis=1)

    def bias_part(item):
        part = lax.dynamic_slice_in_dim(item, lax.rem(group, 2) * HW, HW)
        return jnp.where(group // 2 == x, part, jnp.zeros_like(part))

    query_part, value_part = bias_part(query_bias), bias_part(value_bias)
    bias_row = jnp.concatenate(
        [query_part, jnp.zeros((2 * BLK,), bf16), value_part[2 * DH :], value_part[: 2 * DH], jnp.zeros((BLK,), bf16)]
    )
    own_rows = jnp.stack(
        [first_gain, first_shift, output_bias, second_gain, second_shift, down_bias, down_bias, down_bias]
    )
    place_rows = lax.dynamic_update_slice(jnp.zeros((8, width), bf16), own_rows, (0, x * half))
    place_up = lax.dynamic_update_slice(
        jnp.zeros((4, width), bf16), up_bias.reshape(2, width), (2 * x, 0)
    )
    small = jnp.concatenate(
        [place_rows, place_up, bias_row[None], jnp.zeros((3, width), bf16)], axis=0
    ).astype(f32)

    kv, q, normed, small, up, down, wo = gather(
        tokens, narrow, small, up_weight, down_weight, output_weight
    )
    kv = lax.all_gather(kv, "s", axis=0, tiled=True) if kv.shape[0] * 2 * GROUPS < blocks else kv
    kv = kv.reshape(blocks, BLK, 2 * HW)
    q = q.reshape(2 * GROUPS, BLK, 2 * BLK)
    out_t, wide, lse = attend_forward(where, text, low, high, q, kv, first)
    result, grad_middle, grad_t, up_grad, down_grad, wo_grad, sums = dense(
        out_t, tokens, cotangent, small, up, down, wo
    )

    across = ("x", "g", "s", "r")
    count = 2 * blocks // 8
    up_own = lax.psum_scatter(
        up_grad.reshape(count, -1, 2 * width), across, scatter_dimension=0, tiled=True
    )
    down_own = lax.psum_scatter(
        down_grad.reshape(count, -1, width), across, scatter_dimension=0, tiled=True
    )
    wo_own = lax.psum_scatter(
        wo_grad.reshape(2 * count, -1, width), (*across, "core"), scatter_dimension=0, tiled=True
    )
    up_own = lax.all_gather(up_own, ("g", "s", "r", "core"), axis=0, tiled=True)
    up_own = (
        up_own.reshape(count // 2, 2, -1, 2, width).transpose(0, 2, 3, 1, 4).reshape(half, 4 * width)
    )
    down_own = lax.all_gather(down_own, ("core", "g", "s", "r"), axis=0, tiled=True).reshape(-1, width)
    wo_own = lax.all_gather(wo_own, ("g", "s", "r", "core"), axis=0, tiled=True).reshape(-1, width)

    dq, dkv = attend_backward(where, text, low, high, q, kv, first, lse, grad_t, wide)
    narrow_all = lax.all_gather(narrow, "x", axis=0, tiled=True)
    wq = narrow_all[:, :HW]
    wk, wv = unpack_kv(narrow_all[:, 2 * BLK :])
    normed = normed.reshape(GROUPS * rows, width)
    inputs = tokens.astype(f32)
    lower_gain, lower_shift = small[0], small[1]

    dq = dq.reshape(-1, 2 * BLK)[:, :HW] * bf16(SCALE)
    dkv = lax.psum_scatter(dkv.reshape(-1, 2 * HW), ROWS, scatter_dimension=0, tiled=True)
    dk, dv = unpack_kv(dkv)
    grad_first = (inner(dq, wq) + inner(dk, wk) + inner(dv, wv)).astype(bf16)
    grad_first = lax.psum_scatter(grad_first, "g", scatter_dimension=0, tiled=True).astype(f32)
    term_narrow = outer(normed, jnp.concatenate([dq, dk, dv], axis=1)).astype(bf16)
    term_query_add = jnp.sum(dq.astype(f32), axis=0)
    term_value_add = jnp.sum(dv.astype(f32), axis=0)
    _, pull_first = jax.vjp(layer_norm, inputs, lower_gain, lower_shift)
    grad_input_part, term_lower_gain, term_lower_shift = pull_first(grad_first)
    grad_tokens = grad_middle + grad_input_part

    narrow_own = lax.psum_scatter(term_narrow, "x", scatter_dimension=0, tiled=True)
    narrow_own = lax.psum(narrow_own, ("s", "r", "core"))
    narrow_own = lax.all_gather(narrow_own, "g").astype(f32)
    query_own, key_own, value_own = (
        narrow_own[:, :, i * HW : (i + 1) * HW].transpose(1, 0, 2).reshape(-1, width)
        for i in range(3)
    )

    def own_half(item):
        return lax.dynamic_slice_in_dim(item, x * half, half)

    spread = jnp.zeros((width,), f32)
    sums = lax.psum(
        jnp.concatenate(
            [
                sums,
                jnp.stack(
                    [
                        term_lower_gain,
                        term_lower_shift,
                        lax.dynamic_update_slice_in_dim(spread, term_query_add, group * HW, 0),
                        lax.dynamic_update_slice_in_dim(spread, term_value_add, group * HW, 0),
                    ]
                ),
            ]
        ),
        ALL,
    )
    expand_own = lax.dynamic_slice_in_dim(sums, 8 + 2 * x, 2).reshape(-1)
    return (
        result,
        grad_tokens,
        own_half(sums[16]),
        own_half(sums[17]),
        query_own,
        own_half(sums[18]),
        key_own,
        value_own,
        own_half(sums[19]),
        wo_own.astype(f32),
        own_half(sums[2]),
        own_half(sums[3]),
        own_half(sums[4]),
        up_own.astype(f32),
        expand_own,
        down_own.astype(f32),
        own_half(sums[5]),
    )


def solution(mesh):
    devices = mesh.devices
    inner_mesh = Mesh(devices.reshape(GROUPS, devices.shape[0] // (4 * GROUPS), 2, 2, 2), ALL)
    row = P(ALL, None)
    mat = P("x", None)
    vec = P("x")
    in_specs = (
        row, row, P(), P(), vec, vec, mat, vec, mat, mat, vec, mat, vec, vec, vec, mat, vec, mat, vec,
    )
    out_specs = (
        row, row, vec, vec, mat, vec, mat, mat, vec, mat, vec, vec, vec, mat, vec, mat, vec,
    )
    return jax.shard_map(
        shards, mesh=inner_mesh, in_specs=in_specs, out_specs=out_specs, check_vma=False
    )
```

```python
import jax
import jax.numpy as jnp
from jax import lax
from jax.experimental import pallas as pl
from jax.experimental.pallas import tpu as pltpu
from jax.sharding import Mesh
from jax.sharding import PartitionSpec as P

HEADS = 12
DH = 64
NSUM = 50
SEG = 2048
BLK = 128
GROUPS = 4
PER = HEADS // GROUPS
HW = PER * DH
WIDE = PER * BLK
CHUNK = 2 * BLK
EPS = 1e-05
SCALE = 0.125
MASKED = -1e30
ROOT_HALF = 0.7071067811865476
PDF_SCALE = 0.3989422804014327
VMEM_LIMIT = 56 << 20
bf16 = jnp.bfloat16
f32 = jnp.float32


def layer_norm(values, gain, shift):
    mean = jnp.mean(values, axis=-1, keepdims=True)
    centred = values - mean
    spread = jnp.mean(centred * centred, axis=-1, keepdims=True)
    return centred * lax.rsqrt(spread + EPS) * gain + shift


def outer(left, right):
    return lax.dot_general(left, right, (((0,), (0,)), ((), ())), preferred_element_type=f32)


def inner(left, right):
    return lax.dot_general(left, right, (((1,), (1,)), ((), ())), preferred_element_type=f32)


def dot(left, right):
    return jnp.dot(left, right, preferred_element_type=f32)


def first_visible(positions, doc_lengths):
    count = doc_lengths.shape[0]
    order = jnp.arange(count)
    starts = jnp.sum(jnp.where(order[None, :] < order[:, None], doc_lengths[None, :], 0), axis=1)
    before = starts <= positions[..., None]
    begin = jnp.max(jnp.where(before, starts, 0), axis=-1)
    return jnp.where(positions - begin >= SEG + NSUM, begin + SEG, begin)


def spread_heads_t(part_t, order):
    rows = []
    zero = jnp.zeros((DH, BLK), part_t.dtype)
    for head in order:
        if head is None:
            rows.append(jnp.zeros((DH, WIDE), part_t.dtype))
        else:
            piece = part_t[DH * head : DH * head + DH]
            rows.append(
                jnp.concatenate([piece if h == head else zero for h in range(PER)], axis=1)
            )
    return jnp.concatenate(rows, axis=0)


K_ORDER = (0, 1, 2, None)
V_ORDER = (None, 2, 0, 1)


def visible(chunk, first, own):
    at = chunk * CHUNK + lax.broadcasted_iota(jnp.int32, (CHUNK, BLK), 0)
    allowed = (at >= first) & (at <= own)
    return jnp.concatenate([allowed] * PER, axis=1)


def load_chunk(kv_ref, where_ref, chunk):
    return jnp.concatenate(
        [kv_ref[where_ref[2 * chunk]], kv_ref[where_ref[2 * chunk + 1]]], axis=0
    )


def forward_kernel(
    where_ref, text_ref, low_ref, high_ref, q_ref, kv_ref, first_ref,
    out_ref, wide_ref, lse_ref, vt_ref, acc_ref,
):
    chunks = kv_ref.shape[0] // 2

    def turn(chunk, _):
        vt_ref[chunk] = load_chunk(kv_ref, where_ref, chunk)[:, BLK : 3 * BLK].T[DH:]
        return _

    lax.fori_loop(0, chunks, turn, 0)

    def one_slot(slot, _):
        wide_q = spread_heads_t(q_ref[slot].T[:HW], K_ORDER)
        first = first_ref[slot]
        own = text_ref[slot] * BLK + lax.broadcasted_iota(jnp.int32, (1, BLK), 1)
        acc_ref[...] = jnp.zeros_like(acc_ref)

        def step(chunk, carry):
            top, total = carry
            part = load_chunk(kv_ref, where_ref, chunk)
            scores = dot(part[:, : 2 * BLK], wide_q)
            scores = jnp.where(visible(chunk, first, own), scores, MASKED)
            fresh = jnp.maximum(top, jnp.max(scores, axis=0, keepdims=True))
            expo = jnp.exp(scores - fresh)
            shrink = jnp.exp(top - fresh)
            total = total * shrink + jnp.sum(expo, axis=0, keepdims=True)
            acc_ref[...] = acc_ref[...] * shrink + dot(vt_ref[chunk], expo.astype(bf16))
            return fresh, total

        top, total = lax.fori_loop(
            low_ref[slot],
            high_ref[slot] + 1,
            step,
            (jnp.full((1, WIDE), MASKED, f32), jnp.zeros((1, WIDE), f32)),
        )
        lse_ref[slot] = top + jnp.log(total)
        scaled = acc_ref[...] / total
        pieces = []
        for head in range(PER):
            row = DH * V_ORDER.index(head) - DH
            pieces.append(scaled[row : row + DH, BLK * head : BLK * head + BLK])
        kept = jnp.concatenate(pieces, axis=0)
        wide_ref[slot] = kept
        out_ref[slot] = kept.astype(bf16)
        return _

    lax.fori_loop(0, q_ref.shape[0], one_slot, 0)


def whole_vmem():
    return pl.BlockSpec(memory_space=pltpu.VMEM)


def whole_smem():
    return pl.BlockSpec(memory_space=pltpu.SMEM)


def attend_forward(where, text, low, high, q, kv, first):
    slots = q.shape[0]
    blocks = kv.shape[0]
    return pl.pallas_call(
        forward_kernel,
        out_shape=(
            jax.ShapeDtypeStruct((slots, HW, BLK), bf16),
            jax.ShapeDtypeStruct((slots, HW, BLK), f32),
            jax.ShapeDtypeStruct((slots, 1, WIDE), f32),
        ),
        in_specs=[whole_smem()] * 4 + [whole_vmem()] * 3,
        out_specs=(whole_vmem(),) * 3,
        scratch_shapes=[
            pltpu.VMEM((blocks // 2, HW, CHUNK), bf16),
            pltpu.VMEM((HW, WIDE), f32),
        ],
        compiler_params=pltpu.CompilerParams(vmem_limit_bytes=VMEM_LIMIT),
        name="attend_forward",
    )(where, text, low, high, q, kv, first)


def backward_kernel(
    where_ref, text_ref, low_ref, high_ref, q_ref, kv_ref, first_ref, lse_ref, do_ref, wide_ref,
    dq_ref, dkv_ref, qt_ref, qm_ref, dot_ref, dom_ref, delta_ref, acc_ref, dk_acc, dv_acc,
):
    slots = q_ref.shape[0]
    chunks = kv_ref.shape[0] // 2

    def ready(slot, _):
        q = q_ref[slot]
        qt_ref[slot] = spread_heads_t(q.T[:HW], K_ORDER)
        lane = lax.broadcasted_iota(jnp.int32, (BLK, 2 * BLK), 1) // DH
        zero = jnp.zeros_like(q)
        qm_ref[slot] = jnp.concatenate(
            [jnp.where(lane == K_ORDER.index(h), q, zero) for h in range(PER)], axis=0
        )
        grad_t = do_ref[slot]
        dot_ref[slot] = spread_heads_t(grad_t, V_ORDER)
        ordered = jnp.concatenate(
            [
                jnp.zeros((DH, BLK), bf16) if h is None else grad_t[DH * h : DH * h + DH]
                for h in V_ORDER
            ],
            axis=0,
        ).T
        dom_ref[slot] = jnp.concatenate(
            [jnp.where(lane == V_ORDER.index(h), ordered, zero) for h in range(PER)], axis=0
        )
        both = grad_t.astype(f32) * wide_ref[slot]
        delta_ref[slot] = jnp.concatenate(
            [jnp.sum(both[DH * h : DH * h + DH], axis=0, keepdims=True) for h in range(PER)],
            axis=1,
        )
        acc_ref[slot] = jnp.zeros((HW, WIDE), f32)
        return _

    lax.fori_loop(0, slots, ready, 0)

    def one_chunk(chunk, _):
        part = load_chunk(kv_ref, where_ref, chunk)
        keys = part[:, : 2 * BLK]
        vals = part[:, BLK:]
        keys_t = keys.T[:HW]
        dk_acc[...] = jnp.zeros_like(dk_acc)
        dv_acc[...] = jnp.zeros_like(dv_acc)

        def one_slot(slot, kept):
            @pl.when((low_ref[slot] <= chunk) & (chunk <= high_ref[slot]))
            def _():
                own = text_ref[slot] * BLK + lax.broadcasted_iota(jnp.int32, (1, BLK), 1)
                scores = dot(keys, qt_ref[slot])
                probs = jnp.where(
                    visible(chunk, first_ref[slot], own), jnp.exp(scores - lse_ref[slot]), 0.0
                )
                dprobs = dot(vals, dot_ref[slot])
                dscores = (probs * (dprobs - delta_ref[slot])).astype(bf16)
                dv_acc[...] += dot(probs.astype(bf16), dom_ref[slot])
                dk_acc[...] += dot(dscores, qm_ref[slot])
                acc_ref[slot] += dot(keys_t, dscores)

            return kept

        lax.fori_loop(0, slots, one_slot, 0)
        packed = jnp.concatenate(
            [
                dk_acc[:, :BLK],
                dk_acc[:, BLK:] + dv_acc[:, :BLK],
                dv_acc[:, BLK:],
            ],
            axis=1,
        ).astype(bf16)
        dkv_ref[where_ref[2 * chunk]] = packed[:BLK]
        dkv_ref[where_ref[2 * chunk + 1]] = packed[BLK:]
        return _

    lax.fori_loop(0, chunks, one_chunk, 0)

    def finish(slot, _):
        total = acc_ref[slot]
        kept = jnp.concatenate(
            [total[DH * h : DH * h + DH, BLK * h : BLK * h + BLK] for h in range(PER)]
            + [jnp.zeros((DH, BLK), f32)],
            axis=0,
        )
        dq_ref[slot] = kept.T.astype(bf16)
        return _

    lax.fori_loop(0, slots, finish, 0)


def attend_backward(where, text, low, high, q, kv, first, lse, grad_t, wide):
    slots = q.shape[0]
    return pl.pallas_call(
        backward_kernel,
        out_shape=(
            jax.ShapeDtypeStruct((slots, BLK, 2 * BLK), bf16),
            jax.ShapeDtypeStruct(kv.shape, bf16),
        ),
        in_specs=[whole_smem()] * 4 + [whole_vmem()] * 6,
        out_specs=(whole_vmem(),) * 2,
        scratch_shapes=[
            pltpu.VMEM((slots, 2 * BLK, WIDE), bf16),
            pltpu.VMEM((slots, WIDE, 2 * BLK), bf16),
            pltpu.VMEM((slots, 2 * BLK, WIDE), bf16),
            pltpu.VMEM((slots, WIDE, 2 * BLK), bf16),
            pltpu.VMEM((slots, 1, WIDE), f32),
            pltpu.VMEM((slots, HW, WIDE), f32),
            pltpu.VMEM((CHUNK, 2 * BLK), f32),
            pltpu.VMEM((CHUNK, 2 * BLK), f32),
        ],
        compiler_params=pltpu.CompilerParams(vmem_limit_bytes=VMEM_LIMIT + (4 << 20)),
        name="attend_backward",
    )(where, text, low, high, q, kv, first, lse, grad_t, wide)


MESH = pl.DeviceIdType.MESH


def send(src, dst, out_sem, in_sem, **device):
    return pltpu.make_async_remote_copy(
        src_ref=src, dst_ref=dst, send_sem=out_sem, recv_sem=in_sem, device_id=device, device_id_type=MESH
    )


def place():
    return tuple(lax.axis_index(name) for name in ("g", "r", "core", "x"))


def seat(r, core, x):
    return (r * 2 + core) * 2 + x


def greet(g, r, core, x, line):
    barrier = pltpu.get_barrier_semaphore()

    def hello(**device):
        pl.semaphore_signal(barrier, inc=1, device_id=device, device_id_type=MESH)

    hello(core=1 - core)
    hello(x=1 - x)
    hello(r=1 - r)
    if line:
        for away in range(1, GROUPS):
            hello(g=lax.rem(g + away, GROUPS))
        pl.semaphore_wait(barrier, 3 + GROUPS - 1)
    else:
        pl.when(g > 0)(lambda: hello(g=g - 1))
        pl.when(g < GROUPS - 1)(lambda: hello(g=g + 1))
        pl.semaphore_wait(barrier, 5 - jnp.where(g == 0, 1, 0) - jnp.where(g == GROUPS - 1, 1, 0))


NEAREST = tuple(tuple(sorted(range(GROUPS), key=lambda s: (abs(s - z), s))) for z in range(GROUPS))


def nearest(g, step):
    picked = NEAREST[0][step]
    for z in range(1, GROUPS):
        picked = jnp.where(g == z, NEAREST[z][step], picked)
    return picked


def gather_kernel(
    tokens_ref, narrow_ref, small_ref, up_ref, wo_ref,
    kv_ref, q_ref, normed_ref, small_out, wfull, up_out, wo_out,
    lined, small_in, kvs,
    z_own, z_send, z_recv, s_sem, n_send, n_recv, kv_send, kv_recv, kv_local, w_send, w_recv, w_local,
):
    g, r, core, x = place()
    other = 1 - x
    rows, width = tokens_ref.shape
    half = width // 2
    fourth = half // 2
    eighth = half // 4
    greet(g, r, core, x, False)

    def along(source, away, sem):
        return send(lined.at[source], lined.at[source], sem, z_recv.at[source], g=g + away)

    lined[g] = tokens_ref[...]
    pl.when(g > 0)(lambda: along(g, -1, z_own.at[0]).start())
    pl.when(g < GROUPS - 1)(lambda: along(g, 1, z_own.at[1]).start())

    small_move = send(small_ref, small_in, s_sem.at[0], s_sem.at[1], x=other)
    small_move.start()
    mine = pl.ds(x * half + core * fourth, fourth)
    narrow_x = send(narrow_ref.at[pl.ds(core * fourth, fourth)], wfull.at[mine], n_send.at[0], n_recv.at[0], x=other)
    narrow_x.start()

    def wo_rows(owner, part):
        return wo_out.at[pl.ds(owner * half + core * fourth + part * eighth, eighth)]

    def up_rows(owner, part):
        return up_out.at[pl.ds(owner * half + part * fourth, fourth)]

    def up_columns(owner):
        return pl.ds(pl.multiple_of((2 * owner + core) * width, width), width)

    wo_x = send(wo_ref.at[pl.ds(core * fourth + r * eighth, eighth)], wo_rows(x, r), w_send.at[0], w_recv.at[0], x=other)
    up_x = send(
        up_ref.at[pl.ds(r * fourth, fourth), up_columns(other)], up_rows(x, r), w_send.at[1], w_recv.at[1], x=other
    )
    wo_y = send(wo_rows(other, r), wo_rows(other, r), w_send.at[3], w_recv.at[3], r=1 - r)
    up_y = send(up_rows(other, r), up_rows(other, r), w_send.at[4], w_recv.at[4], r=1 - r)
    wo_s = [
        send(wo_rows(other, part), wo_rows(other, part), w_send.at[6 + i], w_recv.at[6 + i], core=1 - core)
        for i, part in enumerate((r, 1 - r))
    ]
    wo_x.start()
    locals_ = [
        pltpu.make_async_copy(wo_ref, wo_out.at[pl.ds(x * half, half)], w_local.at[0]),
        pltpu.make_async_copy(up_ref.at[:, up_columns(x)], up_out.at[pl.ds(x * half, half)], w_local.at[1]),
    ]
    for item in locals_:
        item.start()

    wfull[pl.ds(x * half, half)] = narrow_ref[...]
    narrow_x.wait_recv()
    theirs = wfull.at[pl.ds(other * half + core * fourth, fourth)]
    narrow_s = send(theirs, theirs, n_send.at[1], n_recv.at[1], core=1 - core)
    narrow_s.start()
    small_move.wait_recv()
    small_out[...] = small_ref[...] + small_in[...]
    narrow_s.wait_recv()

    own = seat(r, core, x)

    def block(owner, source):
        return kv_ref.at[owner, source]

    def push(step, kind, what, **device):
        copy = send(what[0], what[1], kv_send.at[kind, step], kv_recv.at[kind, step], **device)
        copy.start()

    def settle(step, kind, owner, source):
        send(block(owner, source), block(owner, source), kv_send.at[kind, step], kv_recv.at[kind, step], x=other).wait_recv()

    def forward(step):
        source = nearest(g, step)
        by_x = block(seat(r, core, other), source)
        settle(step, 0, seat(r, core, other), source)
        if step % 2 == 0:
            push(step, 3, (by_x, by_x), r=1 - r)
        push(step, 4, (by_x, by_x), core=1 - core)
        by_y = block(seat(1 - r, core, x), source)
        settle(step, 1, seat(1 - r, core, x), source)
        if step % 2 == 1:
            push(step, 3, (by_y, by_y), x=other)
        push(step, 5, (by_y, by_y), core=1 - core)

    def forward_far(step):
        source = nearest(g, step)
        far = block(seat(1 - r, core, other), source)
        settle(step, 3, seat(1 - r, core, other), source)
        push(step, 6, (far, far), core=1 - core)

    for step in range(GROUPS):
        source = nearest(g, step)
        if step > 0:
            send(lined.at[source], lined.at[source], z_send.at[source], z_recv.at[source], x=other).wait_recv()
            pl.when((source < g) & (g < GROUPS - 1))(lambda: along(source, 1, z_send.at[source]).start())
            pl.when((source > g) & (g > 0))(lambda: along(source, -1, z_send.at[source]).start())
        values = lined[source].astype(f32)
        normed = layer_norm(values, small_out[0:1], small_out[1:2]).astype(bf16)
        normed_ref[source] = normed
        both = dot(normed, wfull[...]) + small_out[12:13, : wfull.shape[1]]
        q_ref[source] = (both[:, : 2 * BLK] * SCALE).astype(bf16)
        kvs[step] = both[:, 2 * BLK :].astype(bf16)
        here = (kvs.at[step], block(own, source))
        push(step, 0, here, x=other)
        push(step, 1, here, r=1 - r)
        push(step, 2, here, core=1 - core)
        pltpu.make_async_copy(kvs.at[step], block(own, source), kv_local.at[step]).start()
        if step == 0:
            up_x.start()
        if step > 0:
            forward(step - 1)
        if step > 1:
            forward_far(step - 2)
    wo_x.wait_recv()
    wo_y.start()
    wo_s[0].start()
    forward(GROUPS - 1)
    forward_far(GROUPS - 2)
    up_x.wait_recv()
    up_y.start()
    send(wo_rows(other, 1 - r), wo_rows(other, 1 - r), w_send.at[3], w_recv.at[3], r=1 - r).wait_recv()
    wo_s[1].start()
    forward_far(GROUPS - 1)

    for step in range(GROUPS):
        source = nearest(g, step)
        pltpu.make_async_copy(kvs.at[step], block(own, source), kv_local.at[step]).wait()
        settle(step, 2, seat(r, 1 - core, x), source)
        settle(step, 4, seat(r, 1 - core, other), source)
        settle(step, 5, seat(1 - r, 1 - core, x), source)
        settle(step, 6, seat(1 - r, 1 - core, other), source)
        for kind in range(7):
            send(kvs.at[step], block(own, source), kv_send.at[kind, step], kv_recv.at[kind, step], x=other).wait_send()
    pl.when(g > 0)(lambda: along(g, -1, z_own.at[0]).wait_send())
    pl.when(g < GROUPS - 1)(lambda: along(g, 1, z_own.at[1]).wait_send())
    for step in range(1, GROUPS):
        source = nearest(g, step)
        passed = ((source < g) & (g < GROUPS - 1)) | ((source > g) & (g > 0))
        pl.when(passed)(lambda: send(lined.at[source], lined.at[source], z_send.at[source], z_recv.at[source], x=other).wait_send())
    small_move.wait_send()
    narrow_x.wait_send()
    narrow_s.wait_send()
    for item in locals_:
        item.wait()
    for item in (wo_x, up_x, wo_y, up_y, *wo_s):
        item.wait_send()
    send(up_rows(other, 1 - r), up_rows(other, 1 - r), w_send.at[4], w_recv.at[4], r=1 - r).wait_recv()
    for i, part in enumerate((r, 1 - r)):
        there = wo_out.at[pl.ds(other * half + (1 - core) * fourth + part * eighth, eighth)]
        send(there, there, w_send.at[6 + i], w_recv.at[6 + i], core=1 - core).wait_recv()


def anywhere():
    return pl.BlockSpec(memory_space=pl.ANY)


def gather(tokens, narrow, small, up, wo):
    rows, width = tokens.shape
    wide = narrow.shape[1]
    dma = pltpu.SemaphoreType.DMA
    return pl.pallas_call(
        gather_kernel,
        out_shape=(
            jax.ShapeDtypeStruct((8, GROUPS, rows, 2 * HW), bf16),
            jax.ShapeDtypeStruct((GROUPS, rows, 2 * BLK), bf16),
            jax.ShapeDtypeStruct((GROUPS, rows, width), bf16),
            jax.ShapeDtypeStruct(small.shape, f32),
            jax.ShapeDtypeStruct((width, wide), bf16),
            jax.ShapeDtypeStruct((width, width), bf16),
            jax.ShapeDtypeStruct((width, width), bf16),
        ),
        in_specs=[whole_vmem()] * 3 + [anywhere()] * 2,
        out_specs=(anywhere(), *(whole_vmem(),) * 4, anywhere(), anywhere()),
        scratch_shapes=[
            pltpu.VMEM((GROUPS, rows, width), bf16),
            pltpu.VMEM(small.shape, f32),
            pltpu.VMEM((GROUPS, rows, 2 * HW), bf16),
            dma((2,)), dma((GROUPS,)), dma((GROUPS,)), dma((2,)), dma((2,)), dma((2,)),
            dma((7, GROUPS)), dma((7, GROUPS)), dma((GROUPS,)), dma((8,)), dma((8,)), dma((2,)),
        ],
        compiler_params=pltpu.CompilerParams(
            collective_id=0, has_side_effects=True, vmem_limit_bytes=32 << 20
        ),
        name="gather",
    )(tokens, narrow, small, up, wo)


def erf_parts(values):
    below = 0.5 * (1.0 + lax.erf(values * ROOT_HALF))
    return below, PDF_SCALE * jnp.exp(-0.5 * values * values)


PARTS = 8
UNIT = 216


def dense_kernel(
    out_t_ref, tokens_ref, cot_ref, small_ref, up_ref, wo_ref, down_any,
    result_ref, middle_grad_ref, grad_t_ref, bundle_ref, sums_ref,
    down_ref, attn_in, attn_t, cots, h2s, mid_ref, n2_ref, part_y, part_d, in_y, in_d, pass_y, pass_d, x_y, x_d,
    hids, dus, grad_out, wo_keep, wo_give, wo_in, wo_pass, wo_x,
    down_sem, a_send, a_recv, c_send, c_recv, h_send, h_recv, y_send, y_recv, d_send, d_recv, o_send, o_recv,
    w_send, w_recv,
):
    g, r, core, x = place()
    other = 1 - x
    rows, width = tokens_ref.shape
    half = width // 2
    fourth = half // 2
    load = pltpu.make_async_copy(
        down_any.at[pl.ds(pl.multiple_of(core * width, width), width)], down_ref, down_sem
    )
    load.start()
    greet(g, r, core, x, True)
    cots[0] = cot_ref[...]

    def share(rows_ref, out_sem, in_sem):
        moves = (
            send(rows_ref.at[0], rows_ref.at[2], out_sem.at[1], in_sem.at[1], x=other),
            send(rows_ref.at[0], rows_ref.at[1], out_sem.at[0], in_sem.at[0], core=1 - core),
        )
        for move in moves:
            move.start()
        return moves

    def pass_on(rows_ref, moves, out_sem, in_sem):
        moves[0].wait_recv()
        move = send(rows_ref.at[2], rows_ref.at[3], out_sem.at[2], in_sem.at[2], core=1 - core)
        move.start()
        return move

    def other_group(away):
        return lax.rem(g + away, GROUPS)

    attn_moves = []
    for away in range(1, GROUPS):
        to = other_group(away)
        attn_moves.append(
            send(out_t_ref.at[pl.ds(2 * to, 2)], attn_in.at[g], a_send.at[away], a_recv.at[g], g=to)
        )
        attn_moves[-1].start()
    cot_moves = share(cots, c_send, c_recv)
    attn_in[g] = out_t_ref[pl.ds(2 * g, 2)]
    sums_ref[...] = jnp.zeros_like(sums_ref)
    sums_ref[5:6] = jnp.sum(cot_ref[...].astype(f32), axis=0, keepdims=True)
    for away in range(1, GROUPS):
        source = other_group(away)
        send(attn_in.at[source], attn_in.at[source], a_send.at[away], a_recv.at[source], g=source).wait_recv()
    for source in range(GROUPS):
        attn_t[HW * source : HW * source + HW] = jnp.concatenate(
            [attn_in[source, 0], attn_in[source, 1]], axis=1
        )
    middle = tokens_ref[...].astype(f32) + outer(attn_t[...], wo_ref[...]) + small_ref[2:3]
    mid_ref[...] = middle
    mean = jnp.mean(middle, axis=-1, keepdims=True)
    centred = middle - mean
    spread = jnp.mean(centred * centred, axis=-1, keepdims=True)
    scale = lax.rsqrt(spread + EPS)
    n2_ref[...] = centred * scale
    h2s[0] = (n2_ref[...] * small_ref[3:4] + small_ref[4:5]).astype(bf16)
    h2_moves = share(h2s, h_send, h_recv)
    cot_pass = pass_on(cots, cot_moves, c_send, c_recv)
    load.wait()
    bias_row = 8 + 2 * x + core
    bias = small_ref[pl.ds(bias_row, 1)]
    sums_ref[pl.ds(bias_row, 1)] = jnp.zeros((1, width), f32)

    def one_part(part):
        expanded = dot(h2s[part], up_ref[...]) + bias
        below, density = erf_parts(expanded)
        hidden = (expanded * below).astype(bf16)
        hids[part] = hidden
        slope = below + expanded * density
        grad_hidden = inner(cots[part], down_ref[...]).astype(bf16).astype(f32)
        grad_expand = (grad_hidden * slope).astype(bf16)
        dus[part] = grad_expand
        part_d[part] = inner(grad_expand, up_ref[...])
        part_y[part] = dot(hidden, down_ref[...])
        sums_ref[pl.ds(bias_row, 1)] += jnp.sum(grad_expand.astype(f32), axis=0, keepdims=True)

    one_part(0)
    cot_moves[1].wait_recv()
    h2_moves[1].wait_recv()
    h2_pass = pass_on(h2s, h2_moves, h_send, h_recv)
    one_part(1)
    d_sib = send(part_d.at[1], in_d, d_send.at[0], d_recv.at[0], core=1 - core)
    d_sib.start()
    cot_pass.wait_recv()
    h2_pass.wait_recv()
    one_part(3)
    x_d[0] = part_d[3].astype(bf16)
    x_y[0] = part_y[3].astype(bf16)
    d_pass = send(x_d.at[0], pass_d, d_send.at[1], d_recv.at[1], core=1 - core)
    y_pass = send(x_y.at[0], pass_y, y_send.at[1], y_recv.at[1], core=1 - core)
    d_pass.start()
    y_pass.start()
    one_part(2)
    d_pass.wait_recv()
    x_d[1] = (part_d[2] + pass_d[...].astype(f32)).astype(bf16)
    d_x = send(x_d.at[1], x_d.at[2], d_send.at[2], d_recv.at[2], x=other)
    d_x.start()
    y_pass.wait_recv()
    x_y[1] = (part_y[2] + pass_y[...].astype(f32)).astype(bf16)
    y_x = send(x_y.at[1], x_y.at[2], y_send.at[2], y_recv.at[2], x=other)
    y_x.start()
    y_sib = send(part_y.at[1], in_y, y_send.at[0], y_recv.at[0], core=1 - core)
    y_sib.start()

    def over_rows(left, right):
        total = outer(left[0], right[0])
        for part in range(1, 4):
            total += outer(left[part], right[part])
        return total.astype(bf16)

    down_grad = over_rows(hids, cots)
    up_grad = over_rows(h2s, dus)
    for p in range(PARTS):
        bundle_ref[p // GROUPS, p % GROUPS, 0:96] = down_grad[96 * p : 96 * p + 96]
        bundle_ref[p // GROUPS, p % GROUPS, 96:144] = up_grad[48 * p : 48 * p + 48]
        bundle_ref[p // GROUPS, p % GROUPS, 144:192] = up_grad[half + 48 * p : half + 48 * p + 48]

    d_sib.wait_recv()
    d_x.wait_recv()
    grad_second = part_d[0] + in_d[...] + x_d[2].astype(f32)
    n2 = n2_ref[...]
    sums_ref[3:4] = jnp.sum(grad_second * n2, axis=0, keepdims=True)
    sums_ref[4:5] = jnp.sum(grad_second, axis=0, keepdims=True)
    pulled = grad_second * small_ref[3:4]
    inward = pulled - jnp.mean(pulled, axis=-1, keepdims=True) - n2 * jnp.mean(pulled * n2, axis=-1, keepdims=True)
    grad_middle = cot_ref[...].astype(f32) + inward * scale
    middle_grad_ref[...] = grad_middle
    branch = grad_middle.astype(bf16)
    sums_ref[2:3] = jnp.sum(branch.astype(f32), axis=0, keepdims=True)
    grad_out_t = inner(wo_ref[...], branch).astype(bf16)
    for group in range(GROUPS):
        for b in range(2):
            grad_out[group, b] = grad_out_t[HW * group : HW * group + HW, BLK * b : BLK * b + BLK]
    grad_moves = []
    for away in range(1, GROUPS):
        to = other_group(away)
        grad_moves.append(
            send(grad_out.at[to], grad_t_ref.at[pl.ds(2 * g, 2)], o_send.at[away], o_recv.at[g], g=to)
        )
        grad_moves[-1].start()
    grad_t_ref[pl.ds(2 * g, 2)] = grad_out[g]

    for owner in range(2):
        for c in range(2):
            piece = dot(attn_t[half * owner + fourth * c : half * owner + fourth * c + fourth], branch)

            @pl.when(core == c)
            def _():
                wo_keep[owner] = piece

            @pl.when(core != c)
            def _():
                wo_give[owner] = piece.astype(bf16)

    w_sib = send(wo_give, wo_in, w_send.at[0], w_recv.at[0], core=1 - core)
    w_sib.start()
    y_x.wait_recv()
    y_sib.wait_recv()
    result_ref[...] = (
        mid_ref[...] + part_y[0] + in_y[...] + x_y[2].astype(f32) + small_ref[5:6]
    ).astype(bf16)
    w_sib.wait_recv()
    wo_pass[...] = (wo_keep[other] + wo_in[other].astype(f32)).astype(bf16)
    w_x = send(wo_pass, wo_x, w_send.at[1], w_recv.at[1], x=other)
    w_x.start()
    mine = wo_keep[x] + wo_in[x].astype(f32)
    w_x.wait_recv()
    wo_sum = (mine + wo_x[...].astype(f32)).astype(bf16)
    for p in range(PARTS):
        bundle_ref[p // GROUPS, p % GROUPS, 192:UNIT] = wo_sum[24 * p : 24 * p + 24]
    for away in range(1, GROUPS):
        source = other_group(away)
        send(
            grad_t_ref.at[pl.ds(2 * source, 2)], grad_t_ref.at[pl.ds(2 * source, 2)],
            o_send.at[away], o_recv.at[source], g=source,
        ).wait_recv()
    for item in (
        *cot_moves, cot_pass, *h2_moves, h2_pass, d_sib, d_pass, d_x, y_sib, y_pass, y_x, w_sib, w_x, *attn_moves, *grad_moves,
    ):
        item.wait_send()


def dense(out_t, tokens, cot, small, up, wo, down):
    rows, width = tokens.shape
    dma = pltpu.SemaphoreType.DMA
    full = (rows, width)
    fourth = (width // 4, width)
    return pl.pallas_call(
        dense_kernel,
        out_shape=(
            jax.ShapeDtypeStruct(full, bf16),
            jax.ShapeDtypeStruct(full, f32),
            jax.ShapeDtypeStruct(out_t.shape, bf16),
            jax.ShapeDtypeStruct((2, GROUPS, UNIT, width), bf16),
            jax.ShapeDtypeStruct(small.shape, f32),
        ),
        in_specs=[whole_vmem()] * 6 + [anywhere()],
        out_specs=(whole_vmem(),) * 5,
        scratch_shapes=[
            pltpu.VMEM((width, width), bf16),
            pltpu.VMEM((GROUPS, 2, HW, BLK), bf16),
            pltpu.VMEM((width, rows), bf16),
            pltpu.VMEM((4, *full), bf16),
            pltpu.VMEM((4, *full), bf16),
            pltpu.VMEM(full, f32),
            pltpu.VMEM(full, f32),
            pltpu.VMEM((4, *full), f32),
            pltpu.VMEM((4, *full), f32),
            pltpu.VMEM(full, f32),
            pltpu.VMEM(full, f32),
            pltpu.VMEM(full, bf16),
            pltpu.VMEM(full, bf16),
            pltpu.VMEM((3, *full), bf16),
            pltpu.VMEM((3, *full), bf16),
            pltpu.VMEM((4, *full), bf16),
            pltpu.VMEM((4, *full), bf16),
            pltpu.VMEM((GROUPS, 2, HW, BLK), bf16),
            pltpu.VMEM((2, *fourth), f32),
            pltpu.VMEM((2, *fourth), bf16),
            pltpu.VMEM((2, *fourth), bf16),
            pltpu.VMEM(fourth, bf16),
            pltpu.VMEM(fourth, bf16),
            dma(()), dma((GROUPS,)), dma((GROUPS,)), dma((3,)), dma((3,)), dma((3,)), dma((3,)),
            dma((3,)), dma((3,)), dma((3,)), dma((3,)), dma((GROUPS,)), dma((GROUPS,)), dma((2,)), dma((2,)),
        ],
        compiler_params=pltpu.CompilerParams(
            collective_id=1, has_side_effects=True, vmem_limit_bytes=VMEM_LIMIT
        ),
        name="dense",
    )(out_t, tokens, cot, small, up, wo, down)


FARTHEST = ((3, 2, 1, 0), (3, 0, 2, 1), (0, 3, 1, 2), (0, 1, 2, 3))


def farthest(g, step):
    picked = FARTHEST[0][step]
    for z in range(1, GROUPS):
        picked = jnp.where(g == z, FARTHEST[z][step], picked)
    return picked


class Chain:
    def __init__(self, g, x, total, parts, inward, outward, out_sem, in_sem):
        self.g, self.x, self.total, self.parts = g, x, total, parts
        self.inward, self.outward, self.out_sem, self.in_sem = inward, outward, out_sem, in_sem

    def move(self, to, way):
        return send(
            self.outward.at[to], self.inward.at[way, to], self.out_sem.at[to], self.in_sem.at[way, to],
            g=jnp.clip(self.g + (1 if way == 0 else -1), 0, GROUPS - 1),
        )

    def step(self, to):
        g = self.g
        self.total[...] = self.parts[to].astype(f32)

        def take(way):
            arrived(self.inward.at[way, to], self.out_sem.at[to], self.in_sem.at[way, to], self.x)
            self.total[...] += self.inward[way, to].astype(f32)

        pl.when((to >= g) & (g > 0))(lambda: take(0))
        pl.when((to <= g) & (g < GROUPS - 1))(lambda: take(1))

        @pl.when(to != g)
        def _():
            self.outward[to] = self.total[...].astype(bf16)

        pl.when(to > g)(lambda: self.move(to, 0).start())
        pl.when(to < g)(lambda: self.move(to, 1).start())

    def finish(self):
        for step in range(GROUPS - 1):
            to = farthest(self.g, step)
            left(self.outward.at[to], self.out_sem.at[to], self.in_sem.at[0, to], self.x)


class Ring:
    def __init__(self, g, x, slot, own_sem, out_sem, in_sem):
        self.g, self.x, self.slot = g, x, slot
        self.own_sem, self.out_sem, self.in_sem = own_sem, out_sem, in_sem

    def move(self, source, way, sem):
        return send(
            self.slot(source), self.slot(source), sem, self.in_sem.at[source],
            g=jnp.clip(self.g + way, 0, GROUPS - 1),
        )

    def start(self):
        g = self.g
        pl.when(g > 0)(lambda: self.move(g, -1, self.own_sem.at[0]).start())
        pl.when(g < GROUPS - 1)(lambda: self.move(g, 1, self.own_sem.at[1]).start())

    def step(self, step):
        g, source = self.g, nearest(self.g, step)
        arrived(self.slot(source), self.out_sem.at[source], self.in_sem.at[source], self.x)
        pl.when((source < g) & (g < GROUPS - 1))(lambda: self.move(source, 1, self.out_sem.at[source]).start())
        pl.when((source > g) & (g > 0))(lambda: self.move(source, -1, self.out_sem.at[source]).start())
        return source

    def finish(self):
        g = self.g
        for i, there in enumerate((g > 0, g < GROUPS - 1)):
            pl.when(there)(lambda: left(self.slot(g), self.own_sem.at[i], self.in_sem.at[g], self.x))
        for step in range(1, GROUPS):
            source = nearest(g, step)
            passed = ((source < g) & (g < GROUPS - 1)) | ((source > g) & (g > 0))
            pl.when(passed)(
                lambda: left(self.slot(source), self.out_sem.at[source], self.in_sem.at[source], self.x)
            )


def arrived(what, out_sem, in_sem, x):
    send(what, what, out_sem, in_sem, x=1 - x).wait_recv()


def left(what, out_sem, in_sem, x):
    send(what, what, out_sem, in_sem, x=1 - x).wait_send()


def scatter_kernel(
    dkv_ref, dq_ref, normed_ref, wfull_ref, tokens_ref, mgrad_ref, small_ref, bundle_ref, sums_in,
    tokens_grad_ref, big_ref, qout_ref, kvout_ref, sums_ref,
    own_kv, sib_kv, keep_x, give_x, in_x, give_y, in_y, part_a, total_a, inward_a, outward_a, wg_kv,
    by_in, by_sum, total_b, inward_b, outward_b, unit,
    q_keep, q_give, q_in, q_pass, q_x, q_y, q_sum, v_keep, v_give, v_in, v_pass, v_x, v_y, v_sum,
    sums_got,
    own_sem, k_send, k_recv, x_send, x_recv, y_send, y_recv, ca_send, ca_recv,
    b_send, b_recv, cb_send, cb_recv, u_send, u_recv, rb_own, rb_send, rb_recv,
    fy_send, fy_recv, fs_send, fs_recv,
    q_send, q_recv, rq_own, rq_send, rq_recv, qs_send, qs_recv,
    v_send, v_recv, rv_own, rv_send, rv_recv, vs_send, vs_recv,
    s_send, s_recv, l_sem,
):
    g, r, core, x = place()
    other, sib, far_r = 1 - x, 1 - core, 1 - r
    rows, width = tokens_ref.shape
    half = width // 2
    fourth = half // 2
    wide_q = 2 * BLK
    greet(g, r, core, x, True)
    pending = []

    def begin(src, dst, out_sem, in_sem, **device):
        move = send(src, dst, out_sem, in_sem, **device)
        move.start()
        pending.append(move)
        return move

    def settled(move):
        move.wait_recv()
        move.wait_send()
        pending[:] = [item for item in pending if item is not move]

    kv_moves = []
    for i in range(GROUPS):
        c = farthest(g, i)
        for spot in range(4):
            own = pltpu.make_async_copy(dkv_ref.at[seat(spot // 2, core, spot % 2), c], own_kv.at[i, spot], own_sem.at[i, spot])
            own.start()
            across = begin(
                dkv_ref.at[seat(spot // 2, sib, spot % 2), c], sib_kv.at[i, spot],
                k_send.at[i, spot], k_recv.at[i, spot], core=sib,
            )
            kv_moves.append((own, across))

    def piece(i):
        z = farthest(g, i)
        begin(bundle_ref.at[far_r, z], by_in.at[z], b_send.at[i], b_recv.at[i], r=far_r)

    piece(0)
    piece(1)

    def split(total, keep, give, wide):
        for owner in range(2):
            for c in range(2):
                low = half * owner + fourth * c
                chunk = total[low : low + fourth]

                @pl.when(core == c)
                def _():
                    keep[owner] = chunk

                @pl.when(core != c)
                def _():
                    give[owner] = chunk.astype(bf16)

    def scaled(c):
        return dq_ref[c] * bf16(SCALE)

    query_total = outer(normed_ref[0], scaled(0))
    for c in range(1, GROUPS):
        query_total += outer(normed_ref[c], scaled(c))
    split(query_total, q_keep, q_give, wide_q)
    q_move = begin(q_give, q_in, q_send.at[0], q_recv.at[0], core=sib)
    sums_ref[...] = jnp.zeros_like(sums_ref)
    sums_ref[0:16] = sums_in[...]
    line_q = scaled(0).astype(f32)
    for c in range(1, GROUPS):
        line_q += scaled(c).astype(f32)
    sums_ref[pl.ds(16 + g, 1), 0:wide_q] = jnp.sum(line_q, axis=0, keepdims=True)
    wg_kv[...] = jnp.zeros_like(wg_kv)

    for i in range(GROUPS):
        for own, across in kv_moves[4 * i : 4 * i + 4]:
            own.wait()
            across.wait_recv()
        for row in range(2):
            give_x[i, row] = (
                own_kv[i, 2 * row + other].astype(f32) + sib_kv[i, 2 * row + other].astype(f32)
            ).astype(bf16)
        begin(give_x.at[i], in_x.at[i], x_send.at[i], x_recv.at[i], x=other)
        for row in range(2):
            keep_x[i, row] = own_kv[i, 2 * row + x].astype(f32) + sib_kv[i, 2 * row + x].astype(f32)
        if i == 1:
            q_move.wait_recv()
            q_pass[...] = (q_keep[other] + q_in[other].astype(f32)).astype(bf16)
    q_across = begin(q_pass, q_x, q_send.at[1], q_recv.at[1], x=other)

    chain_a = Chain(g, x, total_a, part_a, inward_a, outward_a, ca_send, ca_recv)
    chain_b = Chain(g, x, total_b, by_sum, inward_b, outward_b, cb_send, cb_recv)

    def on_x(i):
        arrived(in_x.at[i], x_send.at[i], x_recv.at[i], x)
        give_y[i] = (keep_x[i, far_r] + in_x[i, far_r].astype(f32)).astype(bf16)
        begin(give_y.at[i], in_y.at[i], y_send.at[i], y_recv.at[i], r=far_r)
        keep_x[i, r] += in_x[i, r].astype(f32)

    def on_y(i):
        c = farthest(g, i)
        arrived(in_y.at[i], y_send.at[i], y_recv.at[i], x)
        both = (keep_x[i, r] + in_y[i].astype(f32)).astype(bf16)
        part_a[c] = inner(scaled(c), wfull_ref[:, :wide_q]) + inner(both, wfull_ref[:, wide_q:])
        wg_kv[...] += outer(normed_ref[c], both)
        sums_ref[pl.ds(16 + g, 1), wide_q : wide_q + 2 * HW] += jnp.sum(both.astype(f32), axis=0, keepdims=True)

    def on_piece(i):
        z = farthest(g, i)
        arrived(by_in.at[z], b_send.at[i], b_recv.at[i], x)
        by_sum[z] = bundle_ref[r, z].astype(f32) + by_in[z].astype(f32)

    for i in range(GROUPS):
        on_x(i)
        if i < 2:
            piece(2 + i)
        on_piece(i)
        if i >= 1:
            on_y(i - 1)
        if i >= 2:
            chain_a.step(farthest(g, i - 2))
    on_y(GROUPS - 1)
    split(wg_kv, v_keep, v_give, 2 * HW)
    v_move = begin(v_give, v_in, v_send.at[0], v_recv.at[0], core=sib)
    chain_a.step(farthest(g, GROUPS - 2))
    q_across.wait_recv()
    q_sum[...] = (q_keep[x] + q_in[x].astype(f32) + q_x[...].astype(f32)).astype(bf16)
    q_over = begin(q_sum, q_y, q_send.at[2], q_recv.at[2], r=far_r)
    v_move.wait_recv()
    v_pass[...] = (v_keep[other] + v_in[other].astype(f32)).astype(bf16)
    v_across = begin(v_pass, v_x, v_send.at[1], v_recv.at[1], x=other)
    chain_b.step(farthest(g, 0))
    chain_b.step(farthest(g, 1))
    chain_a.step(g)

    grad_first = total_a[...]
    values = tokens_ref[...].astype(f32)
    mean = jnp.mean(values, axis=-1, keepdims=True)
    centred = values - mean
    scale = lax.rsqrt(jnp.mean(centred * centred, axis=-1, keepdims=True) + EPS)
    n1 = centred * scale
    pulled = grad_first * small_ref[0:1]
    inward = pulled - jnp.mean(pulled, axis=-1, keepdims=True) - n1 * jnp.mean(pulled * n1, axis=-1, keepdims=True)
    tokens_grad_ref[...] = mgrad_ref[...] + inward * scale
    sums_ref[0:1] = jnp.sum(grad_first * n1, axis=0, keepdims=True)
    sums_ref[1:2] = jnp.sum(grad_first, axis=0, keepdims=True)
    s_sib = begin(sums_ref, sums_got.at[0], s_send.at[0], s_recv.at[0], core=sib)

    def q_slot(z):
        return qout_ref.at[core, z]

    def v_slot(z):
        return kvout_ref.at[core, z]

    def b_slot(z):
        return big_ref.at[core, r, z]

    ring_q = Ring(g, x, q_slot, rq_own, rq_send, rq_recv)
    ring_v = Ring(g, x, v_slot, rv_own, rv_send, rv_recv)
    ring_b = Ring(g, x, b_slot, rb_own, rb_send, rb_recv)

    def store(value_ref, slot, sem):
        copy = pltpu.make_async_copy(value_ref, slot, sem)
        copy.start()
        copy.wait()

    settled(q_over)
    q_sum[...] = (q_sum[...].astype(f32) + q_y[...].astype(f32)).astype(bf16)
    store(q_sum, q_slot(g), l_sem.at[0])
    ring_q.start()
    begin(q_slot(g), q_slot(g), qs_send.at[0], qs_recv.at[0], core=sib)

    chain_b.step(farthest(g, 2))
    v_across.wait_recv()
    v_sum[...] = (v_keep[x] + v_in[x].astype(f32) + v_x[...].astype(f32)).astype(bf16)
    v_over = begin(v_sum, v_y, v_send.at[2], v_recv.at[2], r=far_r)
    chain_b.step(g)
    unit[...] = total_b[...].astype(bf16)
    up_rows = 96 + 48 * other
    u_move = begin(
        unit.at[pl.ds(up_rows, 48)], big_ref.at[core, r, g, pl.ds(96 + 48 * x, 48)], u_send.at[0], u_recv.at[0], x=other
    )
    copies = [
        pltpu.make_async_copy(unit.at[pl.ds(0, 96)], big_ref.at[core, r, g, pl.ds(0, 96)], l_sem.at[1]),
        pltpu.make_async_copy(
            unit.at[pl.ds(96 + 48 * x, 48)], big_ref.at[core, r, g, pl.ds(96 + 48 * x, 48)], l_sem.at[2]
        ),
        pltpu.make_async_copy(unit.at[pl.ds(192, 24)], big_ref.at[core, r, g, pl.ds(192, 24)], l_sem.at[3]),
    ]
    for copy in copies:
        copy.start()
    settled(s_sib)
    sums_ref[...] += sums_got[0]
    s_x = begin(sums_ref, sums_got.at[1], s_send.at[1], s_recv.at[1], x=other)
    for copy in copies:
        copy.wait()
    there = big_ref.at[core, r, g, pl.ds(up_rows, 48)]
    arrived(there, u_send.at[0], u_recv.at[0], x)
    ring_b.start()

    def spread_b(z, step):
        begin(b_slot(z), b_slot(z), fy_send.at[step], fy_recv.at[step], r=far_r)
        begin(b_slot(z), b_slot(z), fs_send.at[0, step], fs_recv.at[0, step], core=sib)

    def spread_far(z, step):
        what = big_ref.at[core, far_r, z]
        arrived(what, fy_send.at[step], fy_recv.at[step], x)
        begin(what, what, fs_send.at[1, step], fs_recv.at[1, step], core=sib)

    spread_b(g, 0)
    settled(v_over)
    v_sum[...] = (v_sum[...].astype(f32) + v_y[...].astype(f32)).astype(bf16)
    store(v_sum, v_slot(g), l_sem.at[0])
    ring_v.start()
    begin(v_slot(g), v_slot(g), vs_send.at[0], vs_recv.at[0], core=sib)
    settled(s_x)
    sums_ref[...] += sums_got[1]
    s_y = begin(sums_ref, sums_got.at[2], s_send.at[2], s_recv.at[2], r=far_r)
    for step in range(1, GROUPS):
        z = ring_q.step(step)
        begin(q_slot(z), q_slot(z), qs_send.at[step], qs_recv.at[step], core=sib)
        if step == 1:
            settled(s_y)
            sums_ref[...] += sums_got[2]
            for away in range(1, GROUPS):
                begin(
                    sums_ref, sums_got.at[2 + away], s_send.at[2 + away], s_recv.at[2 + away],
                    g=lax.rem(g + away, GROUPS),
                )
        z = ring_b.step(step)
        spread_b(z, step)
        spread_far(nearest(g, step - 1), step - 1)
        z = ring_v.step(step)
        begin(v_slot(z), v_slot(z), vs_send.at[step], vs_recv.at[step], core=sib)
    spread_far(nearest(g, GROUPS - 1), GROUPS - 1)

    for away in range(1, GROUPS):
        arrived(sums_got.at[2 + away], s_send.at[2 + away], s_recv.at[2 + away], x)
    for step in range(GROUPS):
        z = nearest(g, step)
        arrived(qout_ref.at[sib, z], qs_send.at[step], qs_recv.at[step], x)
        arrived(kvout_ref.at[sib, z], vs_send.at[step], vs_recv.at[step], x)
        arrived(big_ref.at[sib, r, z], fs_send.at[0, step], fs_recv.at[0, step], x)
        arrived(big_ref.at[sib, far_r, z], fs_send.at[1, step], fs_recv.at[1, step], x)
    for move in pending:
        move.wait_send()
    for item in (chain_a, chain_b, ring_q, ring_v, ring_b):
        item.finish()
    sums_ref[...] += sums_got[3] + sums_got[4] + sums_got[5]


def scatter(dkv, dq, normed, wfull, tokens, mgrad, small, bundle, sums):
    rows, width = tokens.shape
    fourth = width // 4
    dma = pltpu.SemaphoreType.DMA
    wide_q, wide_v = 2 * BLK, 2 * HW
    kv_block = (rows, wide_v)
    full = (rows, width)
    unit = (UNIT, width)

    def weight_scratch(wide):
        return [
            pltpu.VMEM((2, fourth, wide), f32),
            pltpu.VMEM((2, fourth, wide), bf16),
            pltpu.VMEM((2, fourth, wide), bf16),
            *[pltpu.VMEM((fourth, wide), bf16)] * 4,
        ]

    return pl.pallas_call(
        scatter_kernel,
        out_shape=(
            jax.ShapeDtypeStruct(full, f32),
            jax.ShapeDtypeStruct((2, 2, GROUPS, *unit), bf16),
            jax.ShapeDtypeStruct((2, GROUPS, fourth, wide_q), bf16),
            jax.ShapeDtypeStruct((2, GROUPS, fourth, wide_v), bf16),
            jax.ShapeDtypeStruct((24, width), f32),
        ),
        in_specs=[anywhere()] + [whole_vmem()] * 8,
        out_specs=(whole_vmem(), anywhere(), anywhere(), anywhere(), whole_vmem()),
        scratch_shapes=[
            pltpu.VMEM((GROUPS, 4, *kv_block), bf16),
            pltpu.VMEM((GROUPS, 4, *kv_block), bf16),
            pltpu.VMEM((GROUPS, 2, *kv_block), f32),
            pltpu.VMEM((GROUPS, 2, *kv_block), bf16),
            pltpu.VMEM((GROUPS, 2, *kv_block), bf16),
            pltpu.VMEM((GROUPS, *kv_block), bf16),
            pltpu.VMEM((GROUPS, *kv_block), bf16),
            pltpu.VMEM((GROUPS, *full), f32),
            pltpu.VMEM(full, f32),
            pltpu.VMEM((2, GROUPS, *full), bf16),
            pltpu.VMEM((GROUPS, *full), bf16),
            pltpu.VMEM((width, wide_v), f32),
            pltpu.VMEM((GROUPS, *unit), bf16),
            pltpu.VMEM((GROUPS, *unit), f32),
            pltpu.VMEM(unit, f32),
            pltpu.VMEM((2, GROUPS, *unit), bf16),
            pltpu.VMEM((GROUPS, *unit), bf16),
            pltpu.VMEM(unit, bf16),
            *weight_scratch(wide_q),
            *weight_scratch(wide_v),
            pltpu.VMEM((6, 24, width), f32),
            dma((GROUPS, 4)), dma((GROUPS, 4)), dma((GROUPS, 4)), dma((GROUPS,)), dma((GROUPS,)), dma((GROUPS,)), dma((GROUPS,)),
            dma((GROUPS,)), dma((2, GROUPS)),
            dma((GROUPS,)), dma((GROUPS,)), dma((GROUPS,)), dma((2, GROUPS)), dma((1,)), dma((1,)), dma((2,)), dma((GROUPS,)), dma((GROUPS,)),
            dma((GROUPS,)), dma((GROUPS,)), dma((2, GROUPS)), dma((2, GROUPS)),
            dma((3,)), dma((3,)), dma((2,)), dma((GROUPS,)), dma((GROUPS,)), dma((GROUPS,)), dma((GROUPS,)),
            dma((3,)), dma((3,)), dma((2,)), dma((GROUPS,)), dma((GROUPS,)), dma((GROUPS,)), dma((GROUPS,)),
            dma((6,)), dma((6,)), dma((4,)),
        ],
        compiler_params=pltpu.CompilerParams(
            collective_id=2, has_side_effects=True, vmem_limit_bytes=VMEM_LIMIT + (4 << 20)
        ),
        name="scatter",
    )(dkv, dq, normed, wfull, tokens, mgrad, small, bundle, sums)


def pack_kv(key_part, value_part):
    return jnp.concatenate(
        [key_part, value_part[..., 2 * DH :], value_part[..., : 2 * DH]], axis=-1
    )


def unpack_kv(both):
    return both[..., :HW], jnp.concatenate([both[..., HW + DH :], both[..., HW : HW + DH]], axis=-1)


ROWS = ("s", "r", "core", "x")
ALL = ("g", "s", "r", "core", "x")


def shards(
    tokens, cotangent, doc_lengths, deal, first_gain, first_shift, query_weight, query_bias,
    key_weight, value_weight, value_bias, output_weight, output_bias, second_gain, second_shift,
    up_weight, up_bias, down_weight, down_bias,
):
    rows, width = tokens.shape
    half = width // 2
    group = lax.axis_index("g")
    rest = lax.axis_index(ROWS)
    x = lax.axis_index("x")
    blocks = deal.shape[0]
    per_group = blocks // (2 * GROUPS)

    gathered = deal.reshape(GROUPS, per_group, 2).transpose(1, 0, 2).reshape(-1)
    order = jnp.arange(blocks, dtype=jnp.int32)
    where = jnp.sum(jnp.where(gathered[None, :] == order[:, None], order[None, :], 0), axis=1)
    text = lax.dynamic_slice_in_dim(gathered, rest * 2 * GROUPS, 2 * GROUPS)
    positions = text[:, None] * BLK + jnp.arange(BLK, dtype=jnp.int32)[None, :]
    first = first_visible(positions, doc_lengths)
    low = first[:, 0] // CHUNK
    high = text // 2
    first = first.reshape(2 * GROUPS, 1, BLK)

    def columns(item):
        return lax.dynamic_slice_in_dim(item, group * HW, HW, 1)

    wq, wk, wv = columns(query_weight), columns(key_weight), columns(value_weight)
    gap = jnp.zeros((half, 2 * BLK - HW), bf16)
    narrow = jnp.concatenate([wq, gap, pack_kv(wk, wv)], axis=1)

    def bias_part(item):
        part = lax.dynamic_slice_in_dim(item, lax.rem(group, 2) * HW, HW)
        return jnp.where(group // 2 == x, part, jnp.zeros_like(part))

    query_part, value_part = bias_part(query_bias), bias_part(value_bias)
    bias_row = jnp.concatenate(
        [query_part, jnp.zeros((2 * BLK,), bf16), value_part[2 * DH :], value_part[: 2 * DH], jnp.zeros((BLK,), bf16)]
    )
    own_rows = jnp.stack(
        [first_gain, first_shift, output_bias, second_gain, second_shift, down_bias, down_bias, down_bias]
    )
    place_rows = lax.dynamic_update_slice(jnp.zeros((8, width), bf16), own_rows, (0, x * half))
    place_up = lax.dynamic_update_slice(
        jnp.zeros((4, width), bf16), up_bias.reshape(2, width), (2 * x, 0)
    )
    small = jnp.concatenate(
        [place_rows, place_up, bias_row[None], jnp.zeros((3, width), bf16)], axis=0
    ).astype(f32)

    kv, q, normed, small, wfull, up, wo = gather(tokens, narrow, small, up_weight, output_weight)
    wide = blocks > 8 * 2 * GROUPS
    if wide:
        kv = lax.all_gather(kv, "s", axis=0, tiled=True)
    kv = kv.reshape(blocks, BLK, 2 * HW)
    q = q.reshape(2 * GROUPS, BLK, 2 * BLK)
    out_t, kept, lse = attend_forward(where, text, low, high, q, kv, first)
    result, grad_middle, grad_t, bundle, sums = dense(
        out_t, tokens, cotangent, small, up, wo, down_weight
    )
    dq, dkv = attend_backward(where, text, low, high, q, kv, first, lse, grad_t, kept)
    dkv = dkv.reshape(-1, GROUPS, rows, 2 * HW)
    if wide:
        dkv = lax.psum_scatter(dkv, "s", scatter_dimension=0, tiled=True)
    dq = dq.reshape(GROUPS, rows, 2 * BLK)
    grad_tokens, big, query_own, kv_own, sums = scatter(
        dkv, dq, normed, wfull, tokens, grad_middle, small, bundle, sums
    )
    if wide:
        big, query_own, kv_own, sums = (
            lax.psum(item, "s") for item in (big, query_own, kv_own, sums)
        )

    big = big.reshape(2, PARTS, UNIT, width)
    down_own = big[:, :, :96].reshape(-1, width)
    up_own = big[:, :, 96:192].reshape(2, PARTS, 2, 48, width).transpose(1, 3, 2, 0, 4).reshape(half, 4 * width)
    wo_own = big[:, :, 192:].reshape(half, width)

    def flat(item):
        return item.transpose(0, 2, 1, 3).reshape(half, width)

    key_own, value_own = unpack_kv(kv_own)

    def own_half(item):
        return lax.dynamic_slice_in_dim(item, x * half, half)

    query_sum = sums[16 : 16 + GROUPS, :HW].reshape(width)
    value_sum = unpack_kv(sums[16 : 16 + GROUPS, 2 * BLK : 2 * BLK + 2 * HW])[1].reshape(width)
    expand_own = lax.dynamic_slice_in_dim(sums, 8 + 2 * x, 2).reshape(-1)
    return (
        result,
        grad_tokens,
        own_half(sums[0]),
        own_half(sums[1]),
        flat(query_own[..., :HW]).astype(f32),
        own_half(query_sum),
        flat(key_own).astype(f32),
        flat(value_own).astype(f32),
        own_half(value_sum),
        wo_own.astype(f32),
        own_half(sums[2]),
        own_half(sums[3]),
        own_half(sums[4]),
        up_own.astype(f32),
        expand_own,
        down_own.astype(f32),
        own_half(sums[5]),
    )


def solution(mesh):
    devices = mesh.devices
    inner_mesh = Mesh(devices.reshape(GROUPS, devices.shape[0] // (4 * GROUPS), 2, 2, 2), ALL)
    row = P(ALL, None)
    mat = P("x", None)
    vec = P("x")
    in_specs = (
        row, row, P(), P(), vec, vec, mat, vec, mat, mat, vec, mat, vec, vec, vec, mat, vec, mat, vec,
    )
    out_specs = (
        row, row, vec, vec, mat, vec, mat, mat, vec, mat, vec, vec, vec, mat, vec, mat, vec,
    )
    return jax.shard_map(
        shards, mesh=inner_mesh, in_specs=in_specs, out_specs=out_specs, check_vma=False
    )
```

```python
import jax
import jax.numpy as jnp
from jax import lax
from jax.experimental import pallas as pl
from jax.experimental.pallas import tpu as pltpu
from jax.sharding import Mesh
from jax.sharding import PartitionSpec as P

HEADS = 12
DH = 64
NSUM = 50
SEG = 2048
BLK = 128
GROUPS = 4
PER = HEADS // GROUPS
HW = PER * DH
WIDE = PER * BLK
CHUNK = 2 * BLK
EPS = 1e-05
SCALE = 0.125
MASKED = -1e30
ROOT_HALF = 0.7071067811865476
PDF_SCALE = 0.3989422804014327
VMEM_LIMIT = 56 << 20
bf16 = jnp.bfloat16
f32 = jnp.float32


def layer_norm(values, gain, shift):
    mean = jnp.mean(values, axis=-1, keepdims=True)
    centred = values - mean
    spread = jnp.mean(centred * centred, axis=-1, keepdims=True)
    return centred * lax.rsqrt(spread + EPS) * gain + shift


def outer(left, right):
    return lax.dot_general(left, right, (((0,), (0,)), ((), ())), preferred_element_type=f32)


def inner(left, right):
    return lax.dot_general(left, right, (((1,), (1,)), ((), ())), preferred_element_type=f32)


def dot(left, right):
    return jnp.dot(left, right, preferred_element_type=f32)


def survey(deal_ref, lengths_ref, where_ref, text_ref, low_ref, high_ref, first_ref):
    blocks = deal_ref.shape[0]
    per_group = blocks // (2 * GROUPS)
    rest = lax.axis_index(ROWS)

    def note(j, kept):
        pair = j // 2
        group = pair // per_group
        where_ref[deal_ref[j]] = ((pair - group * per_group) * GROUPS + group) * 2 + j % 2
        return kept

    lax.fori_loop(0, blocks, note, 0)
    starts = [jnp.int32(0)]
    for doc in range(lengths_ref.shape[0] - 1):
        starts.append(starts[-1] + lengths_ref[doc])

    def first_of(at):
        begin = jnp.zeros_like(at)
        for start in starts:
            begin = jnp.where(start <= at, jnp.maximum(begin, start), begin)
        return jnp.where(at - begin >= SEG + NSUM, begin + SEG, begin)

    for slot in range(2 * GROUPS):
        text = deal_ref[2 * ((slot // 2) * per_group + rest) + slot % 2]
        text_ref[slot] = text
        low_ref[slot] = first_of(text * BLK) // CHUNK
        high_ref[slot] = text // 2
        first_ref[slot] = first_of(text * BLK + lax.broadcasted_iota(jnp.int32, (1, BLK), 1))


def survey_scratch(blocks):
    slots = 2 * GROUPS
    return [
        pltpu.SMEM((blocks,), jnp.int32),
        pltpu.SMEM((slots,), jnp.int32),
        pltpu.SMEM((slots,), jnp.int32),
        pltpu.SMEM((slots,), jnp.int32),
        pltpu.VMEM((slots, 1, BLK), jnp.int32),
    ]


def spread_heads_t(part_t, order):
    rows = []
    zero = jnp.zeros((DH, BLK), part_t.dtype)
    for head in order:
        if head is None:
            rows.append(jnp.zeros((DH, WIDE), part_t.dtype))
        else:
            piece = part_t[DH * head : DH * head + DH]
            rows.append(
                jnp.concatenate([piece if h == head else zero for h in range(PER)], axis=1)
            )
    return jnp.concatenate(rows, axis=0)


K_ORDER = (0, 1, 2, None)
V_ORDER = (None, 2, 0, 1)


def visible(chunk, first, own):
    at = chunk * CHUNK + lax.broadcasted_iota(jnp.int32, (CHUNK, BLK), 0)
    allowed = (at >= first) & (at <= own)
    return jnp.concatenate([allowed] * PER, axis=1)


def load_chunk(kv_ref, where_ref, chunk):
    return jnp.concatenate(
        [kv_ref[where_ref[2 * chunk]], kv_ref[where_ref[2 * chunk + 1]]], axis=0
    )


def forward_kernel(
    deal_ref, lengths_ref, q_ref, kv_ref,
    out_ref, wide_ref, lse_ref,
    where_ref, text_ref, low_ref, high_ref, first_ref, vt_ref, acc_ref,
):
    survey(deal_ref, lengths_ref, where_ref, text_ref, low_ref, high_ref, first_ref)
    chunks = kv_ref.shape[0] // 2

    def turn(chunk, _):
        vt_ref[chunk] = load_chunk(kv_ref, where_ref, chunk)[:, BLK : 3 * BLK].T[DH:]
        return _

    lax.fori_loop(0, chunks, turn, 0)

    def one_slot(slot, _):
        wide_q = spread_heads_t(q_ref[slot].T[:HW], K_ORDER)
        first = first_ref[slot]
        own = text_ref[slot] * BLK + lax.broadcasted_iota(jnp.int32, (1, BLK), 1)
        acc_ref[...] = jnp.zeros_like(acc_ref)

        def step(chunk, carry):
            top, total = carry
            part = load_chunk(kv_ref, where_ref, chunk)
            scores = dot(part[:, : 2 * BLK], wide_q)
            scores = jnp.where(visible(chunk, first, own), scores, MASKED)
            fresh = jnp.maximum(top, jnp.max(scores, axis=0, keepdims=True))
            expo = jnp.exp(scores - fresh)
            shrink = jnp.exp(top - fresh)
            total = total * shrink + jnp.sum(expo, axis=0, keepdims=True)
            acc_ref[...] = acc_ref[...] * shrink + dot(vt_ref[chunk], expo.astype(bf16))
            return fresh, total

        top, total = lax.fori_loop(
            low_ref[slot],
            high_ref[slot] + 1,
            step,
            (jnp.full((1, WIDE), MASKED, f32), jnp.zeros((1, WIDE), f32)),
        )
        lse_ref[slot] = top + jnp.log(total)
        scaled = acc_ref[...] / total
        pieces = []
        for head in range(PER):
            row = DH * V_ORDER.index(head) - DH
            pieces.append(scaled[row : row + DH, BLK * head : BLK * head + BLK])
        kept = jnp.concatenate(pieces, axis=0)
        wide_ref[slot] = kept
        out_ref[slot] = kept.astype(bf16)
        return _

    lax.fori_loop(0, q_ref.shape[0], one_slot, 0)


def whole_vmem():
    return pl.BlockSpec(memory_space=pltpu.VMEM)


def whole_smem():
    return pl.BlockSpec(memory_space=pltpu.SMEM)


def attend_forward(deal, lengths, q, kv):
    slots = q.shape[0]
    blocks = kv.shape[0]
    return pl.pallas_call(
        forward_kernel,
        out_shape=(
            jax.ShapeDtypeStruct((slots, HW, BLK), bf16),
            jax.ShapeDtypeStruct((slots, HW, BLK), f32),
            jax.ShapeDtypeStruct((slots, 1, WIDE), f32),
        ),
        in_specs=[whole_smem()] * 2 + [whole_vmem()] * 2,
        out_specs=(whole_vmem(),) * 3,
        scratch_shapes=[
            *survey_scratch(blocks),
            pltpu.VMEM((blocks // 2, HW, CHUNK), bf16),
            pltpu.VMEM((HW, WIDE), f32),
        ],
        compiler_params=pltpu.CompilerParams(vmem_limit_bytes=(6 << 20) + kv.size // 5 * 16),
        name="attend_forward",
    )(deal, lengths, q, kv)


def backward_kernel(
    deal_ref, lengths_ref, q_ref, kv_ref, lse_ref, do_ref, wide_ref,
    dq_ref, dkv_ref, where_ref, text_ref, low_ref, high_ref, first_ref, qt_ref, qm_ref, dot_ref, dom_ref, delta_ref, acc_ref, dk_acc, dv_acc,
):
    survey(deal_ref, lengths_ref, where_ref, text_ref, low_ref, high_ref, first_ref)
    slots = q_ref.shape[0]
    chunks = kv_ref.shape[0] // 2

    def ready(slot, _):
        q = q_ref[slot]
        qt_ref[slot] = spread_heads_t(q.T[:HW], K_ORDER)
        lane = lax.broadcasted_iota(jnp.int32, (BLK, 2 * BLK), 1) // DH
        zero = jnp.zeros_like(q)
        qm_ref[slot] = jnp.concatenate(
            [jnp.where(lane == K_ORDER.index(h), q, zero) for h in range(PER)], axis=0
        )
        grad_t = do_ref[slot]
        dot_ref[slot] = spread_heads_t(grad_t, V_ORDER)
        ordered = jnp.concatenate(
            [
                jnp.zeros((DH, BLK), bf16) if h is None else grad_t[DH * h : DH * h + DH]
                for h in V_ORDER
            ],
            axis=0,
        ).T
        dom_ref[slot] = jnp.concatenate(
            [jnp.where(lane == V_ORDER.index(h), ordered, zero) for h in range(PER)], axis=0
        )
        both = grad_t.astype(f32) * wide_ref[slot]
        delta_ref[slot] = jnp.concatenate(
            [jnp.sum(both[DH * h : DH * h + DH], axis=0, keepdims=True) for h in range(PER)],
            axis=1,
        )
        acc_ref[slot] = jnp.zeros((HW, WIDE), f32)
        return _

    lax.fori_loop(0, slots, ready, 0)

    def one_chunk(chunk, _):
        part = load_chunk(kv_ref, where_ref, chunk)
        keys = part[:, : 2 * BLK]
        vals = part[:, BLK:]
        keys_t = keys.T[:HW]
        dk_acc[...] = jnp.zeros_like(dk_acc)
        dv_acc[...] = jnp.zeros_like(dv_acc)

        def one_slot(slot, kept):
            @pl.when((low_ref[slot] <= chunk) & (chunk <= high_ref[slot]))
            def _():
                own = text_ref[slot] * BLK + lax.broadcasted_iota(jnp.int32, (1, BLK), 1)
                scores = dot(keys, qt_ref[slot])
                probs = jnp.where(
                    visible(chunk, first_ref[slot], own), jnp.exp(scores - lse_ref[slot]), 0.0
                )
                dprobs = dot(vals, dot_ref[slot])
                dscores = (probs * (dprobs - delta_ref[slot])).astype(bf16)
                dv_acc[...] += dot(probs.astype(bf16), dom_ref[slot])
                dk_acc[...] += dot(dscores, qm_ref[slot])
                acc_ref[slot] += dot(keys_t, dscores)

            return kept

        lax.fori_loop(0, slots, one_slot, 0)
        packed = jnp.concatenate(
            [
                dk_acc[:, :BLK],
                dk_acc[:, BLK:] + dv_acc[:, :BLK],
                dv_acc[:, BLK:],
            ],
            axis=1,
        ).astype(bf16)
        dkv_ref[where_ref[2 * chunk]] = packed[:BLK]
        dkv_ref[where_ref[2 * chunk + 1]] = packed[BLK:]
        return _

    lax.fori_loop(0, chunks, one_chunk, 0)

    def finish(slot, _):
        total = acc_ref[slot]
        kept = jnp.concatenate(
            [total[DH * h : DH * h + DH, BLK * h : BLK * h + BLK] for h in range(PER)]
            + [jnp.zeros((DH, BLK), f32)],
            axis=0,
        )
        dq_ref[slot] = kept.T.astype(bf16)
        return _

    lax.fori_loop(0, slots, finish, 0)


def attend_backward(deal, lengths, q, kv, lse, grad_t, wide):
    slots = q.shape[0]
    return pl.pallas_call(
        backward_kernel,
        out_shape=(
            jax.ShapeDtypeStruct((slots, BLK, 2 * BLK), bf16),
            jax.ShapeDtypeStruct(kv.shape, bf16),
        ),
        in_specs=[whole_smem()] * 2 + [whole_vmem()] * 5,
        out_specs=(whole_vmem(),) * 2,
        scratch_shapes=[
            *survey_scratch(kv.shape[0]),
            pltpu.VMEM((slots, 2 * BLK, WIDE), bf16),
            pltpu.VMEM((slots, WIDE, 2 * BLK), bf16),
            pltpu.VMEM((slots, 2 * BLK, WIDE), bf16),
            pltpu.VMEM((slots, WIDE, 2 * BLK), bf16),
            pltpu.VMEM((slots, 1, WIDE), f32),
            pltpu.VMEM((slots, HW, WIDE), f32),
            pltpu.VMEM((CHUNK, 2 * BLK), f32),
            pltpu.VMEM((CHUNK, 2 * BLK), f32),
        ],
        compiler_params=pltpu.CompilerParams(
            vmem_limit_bytes=min((17 << 20) + kv.size // 5 * 21, VMEM_LIMIT + (4 << 20))
        ),
        name="attend_backward",
    )(deal, lengths, q, kv, lse, grad_t, wide)


MESH = pl.DeviceIdType.MESH


def send(src, dst, out_sem, in_sem, **device):
    return pltpu.make_async_remote_copy(
        src_ref=src, dst_ref=dst, send_sem=out_sem, recv_sem=in_sem, device_id=device, device_id_type=MESH
    )


def place():
    return tuple(lax.axis_index(name) for name in ("g", "r", "core", "x"))


def seat(r, core, x):
    return (r * 2 + core) * 2 + x


def greet(g, r, core, x, line):
    barrier = pltpu.get_barrier_semaphore()

    def hello(**device):
        pl.semaphore_signal(barrier, inc=1, device_id=device, device_id_type=MESH)

    hello(core=1 - core)
    hello(x=1 - x)
    hello(r=1 - r)
    if line:
        for away in range(1, GROUPS):
            hello(g=lax.rem(g + away, GROUPS))
        pl.semaphore_wait(barrier, 3 + GROUPS - 1)
    else:
        pl.when(g > 0)(lambda: hello(g=g - 1))
        pl.when(g < GROUPS - 1)(lambda: hello(g=g + 1))
        pl.semaphore_wait(barrier, 5 - jnp.where(g == 0, 1, 0) - jnp.where(g == GROUPS - 1, 1, 0))


NEAREST = tuple(tuple(sorted(range(GROUPS), key=lambda s: (abs(s - z), s))) for z in range(GROUPS))


def nearest(g, step):
    picked = NEAREST[0][step]
    for z in range(1, GROUPS):
        picked = jnp.where(g == z, NEAREST[z][step], picked)
    return picked


def prepare(g, x, query_ref, key_ref, value_ref, lines_ref, narrow_ref, small_ref):
    half = lines_ref.shape[1]
    odd = lax.rem(g, 2) == 1

    def columns(ref):
        low = pl.multiple_of(3 * g // 2 * BLK, BLK)
        window = ref[:, pl.ds(low, 2 * BLK)]
        moved = jnp.concatenate([window[:, DH:], window[:, :DH]], axis=1)
        return jnp.where(odd, moved, window)

    lane = lax.broadcasted_iota(jnp.int32, (half, 2 * BLK), 1)
    query = columns(query_ref)
    narrow_ref[:, : 2 * BLK] = jnp.where(lane < HW, query, jnp.zeros_like(query))
    narrow_ref[:, 2 * BLK :] = pack_kv(columns(key_ref)[:, :HW], columns(value_ref)[:, :HW])

    lines = lines_ref[...].astype(f32)
    zero = jnp.zeros((1, half), f32)
    small_ref[...] = jnp.zeros_like(small_ref)
    for row in range(6):
        line = lines[row : row + 1]
        small_ref[row : row + 1] = jnp.where(
            x == 0, jnp.concatenate([line, zero], axis=1), jnp.concatenate([zero, line], axis=1)
        )
    for i in range(2):
        small_ref[pl.ds(8 + 2 * x + i, 1)] = jnp.concatenate(
            [lines[8 + 2 * i : 9 + 2 * i], lines[9 + 2 * i : 10 + 2 * i]], axis=1
        )

    def part(row):
        line = lines[row : row + 1]
        mine = jnp.where(odd, line[:, HW:], line[:, :HW])
        return jnp.where(g // 2 == x, mine, jnp.zeros_like(mine))

    value = part(7)
    small_ref[12:13] = jnp.concatenate(
        [part(6), jnp.zeros((1, 2 * BLK), f32), value[:, 2 * DH :], value[:, : 2 * DH], jnp.zeros((1, BLK), f32)], axis=1
    )


def gather_kernel(
    tokens_ref, query_ref, key_ref, value_ref, lines_ref, up_ref, wo_ref,
    kv_ref, q_ref, normed_ref, small_out, wfull, up_out, wo_out,
    lined, narrow_ref, small_ref, small_in, kvs,
    z_own, z_send, z_recv, s_sem, n_send, n_recv, kv_send, kv_recv, kv_local, w_send, w_recv, w_local,
):
    g, r, core, x = place()
    other = 1 - x
    rows, width = tokens_ref.shape
    half = width // 2
    fourth = half // 2
    eighth = half // 4
    greet(g, r, core, x, False)

    def along(source, away, sem):
        return send(lined.at[source], lined.at[source], sem, z_recv.at[source], g=g + away)

    lined[g] = tokens_ref[...]
    pl.when(g > 0)(lambda: along(g, -1, z_own.at[0]).start())
    pl.when(g < GROUPS - 1)(lambda: along(g, 1, z_own.at[1]).start())

    prepare(g, x, query_ref, key_ref, value_ref, lines_ref, narrow_ref, small_ref)
    small_move = send(small_ref, small_in, s_sem.at[0], s_sem.at[1], x=other)
    small_move.start()
    mine = pl.ds(x * half + core * fourth, fourth)
    narrow_x = send(narrow_ref.at[pl.ds(core * fourth, fourth)], wfull.at[mine], n_send.at[0], n_recv.at[0], x=other)
    narrow_x.start()

    def wo_rows(owner, part):
        return wo_out.at[pl.ds(owner * half + core * fourth + part * eighth, eighth)]

    def up_rows(owner, part):
        return up_out.at[pl.ds(owner * half + part * fourth, fourth)]

    def up_columns(owner):
        return pl.ds(pl.multiple_of((2 * owner + core) * width, width), width)

    wo_x = send(wo_ref.at[pl.ds(core * fourth + r * eighth, eighth)], wo_rows(x, r), w_send.at[0], w_recv.at[0], x=other)
    up_x = send(
        up_ref.at[pl.ds(r * fourth, fourth), up_columns(other)], up_rows(x, r), w_send.at[1], w_recv.at[1], x=other
    )
    wo_y = send(wo_rows(other, r), wo_rows(other, r), w_send.at[3], w_recv.at[3], r=1 - r)
    up_y = send(up_rows(other, r), up_rows(other, r), w_send.at[4], w_recv.at[4], r=1 - r)
    wo_s = [
        send(wo_rows(other, part), wo_rows(other, part), w_send.at[6 + i], w_recv.at[6 + i], core=1 - core)
        for i, part in enumerate((r, 1 - r))
    ]
    wo_x.start()
    locals_ = [
        pltpu.make_async_copy(wo_ref, wo_out.at[pl.ds(x * half, half)], w_local.at[0]),
        pltpu.make_async_copy(up_ref.at[:, up_columns(x)], up_out.at[pl.ds(x * half, half)], w_local.at[1]),
    ]
    for item in locals_:
        item.start()

    wfull[pl.ds(x * half, half)] = narrow_ref[...]
    narrow_x.wait_recv()
    theirs = wfull.at[pl.ds(other * half + core * fourth, fourth)]
    narrow_s = send(theirs, theirs, n_send.at[1], n_recv.at[1], core=1 - core)
    narrow_s.start()
    small_move.wait_recv()
    small_out[...] = small_ref[...] + small_in[...]
    narrow_s.wait_recv()

    own = seat(r, core, x)

    def block(owner, source):
        return kv_ref.at[owner, source]

    def push(step, kind, what, **device):
        copy = send(what[0], what[1], kv_send.at[kind, step], kv_recv.at[kind, step], **device)
        copy.start()

    def settle(step, kind, owner, source):
        send(block(owner, source), block(owner, source), kv_send.at[kind, step], kv_recv.at[kind, step], x=other).wait_recv()

    def forward(step):
        source = nearest(g, step)
        by_x = block(seat(r, core, other), source)
        settle(step, 0, seat(r, core, other), source)
        if step % 2 == 0:
            push(step, 3, (by_x, by_x), r=1 - r)
        push(step, 4, (by_x, by_x), core=1 - core)
        by_y = block(seat(1 - r, core, x), source)
        settle(step, 1, seat(1 - r, core, x), source)
        if step % 2 == 1:
            push(step, 3, (by_y, by_y), x=other)
        push(step, 5, (by_y, by_y), core=1 - core)

    def forward_far(step):
        source = nearest(g, step)
        far = block(seat(1 - r, core, other), source)
        settle(step, 3, seat(1 - r, core, other), source)
        push(step, 6, (far, far), core=1 - core)

    for step in range(GROUPS):
        source = nearest(g, step)
        if step > 0:
            send(lined.at[source], lined.at[source], z_send.at[source], z_recv.at[source], x=other).wait_recv()
            pl.when((source < g) & (g < GROUPS - 1))(lambda: along(source, 1, z_send.at[source]).start())
            pl.when((source > g) & (g > 0))(lambda: along(source, -1, z_send.at[source]).start())
        values = lined[source].astype(f32)
        normed = layer_norm(values, small_out[0:1], small_out[1:2]).astype(bf16)
        normed_ref[source] = normed
        both = dot(normed, wfull[...]) + small_out[12:13, : wfull.shape[1]]
        q_ref[source] = (both[:, : 2 * BLK] * SCALE).astype(bf16)
        kvs[step] = both[:, 2 * BLK :].astype(bf16)
        here = (kvs.at[step], block(own, source))
        push(step, 0, here, x=other)
        push(step, 1, here, r=1 - r)
        push(step, 2, here, core=1 - core)
        pltpu.make_async_copy(kvs.at[step], block(own, source), kv_local.at[step]).start()
        if step == 0:
            up_x.start()
        if step > 0:
            forward(step - 1)
        if step > 1:
            forward_far(step - 2)
    wo_x.wait_recv()
    wo_y.start()
    wo_s[0].start()
    forward(GROUPS - 1)
    forward_far(GROUPS - 2)
    up_x.wait_recv()
    up_y.start()
    send(wo_rows(other, 1 - r), wo_rows(other, 1 - r), w_send.at[3], w_recv.at[3], r=1 - r).wait_recv()
    wo_s[1].start()
    forward_far(GROUPS - 1)

    for step in range(GROUPS):
        source = nearest(g, step)
        pltpu.make_async_copy(kvs.at[step], block(own, source), kv_local.at[step]).wait()
        settle(step, 2, seat(r, 1 - core, x), source)
        settle(step, 4, seat(r, 1 - core, other), source)
        settle(step, 5, seat(1 - r, 1 - core, x), source)
        settle(step, 6, seat(1 - r, 1 - core, other), source)
        for kind in range(7):
            send(kvs.at[step], block(own, source), kv_send.at[kind, step], kv_recv.at[kind, step], x=other).wait_send()
    pl.when(g > 0)(lambda: along(g, -1, z_own.at[0]).wait_send())
    pl.when(g < GROUPS - 1)(lambda: along(g, 1, z_own.at[1]).wait_send())
    for step in range(1, GROUPS):
        source = nearest(g, step)
        passed = ((source < g) & (g < GROUPS - 1)) | ((source > g) & (g > 0))
        pl.when(passed)(lambda: send(lined.at[source], lined.at[source], z_send.at[source], z_recv.at[source], x=other).wait_send())
    small_move.wait_send()
    narrow_x.wait_send()
    narrow_s.wait_send()
    for item in locals_:
        item.wait()
    for item in (wo_x, up_x, wo_y, up_y, *wo_s):
        item.wait_send()
    send(up_rows(other, 1 - r), up_rows(other, 1 - r), w_send.at[4], w_recv.at[4], r=1 - r).wait_recv()
    for i, part in enumerate((r, 1 - r)):
        there = wo_out.at[pl.ds(other * half + (1 - core) * fourth + part * eighth, eighth)]
        send(there, there, w_send.at[6 + i], w_recv.at[6 + i], core=1 - core).wait_recv()


def anywhere():
    return pl.BlockSpec(memory_space=pl.ANY)


def gather(tokens, query, key, value, lines, up, wo):
    rows, width = tokens.shape
    wide = 2 * BLK + 2 * HW
    small = (16, width)
    dma = pltpu.SemaphoreType.DMA
    return pl.pallas_call(
        gather_kernel,
        out_shape=(
            jax.ShapeDtypeStruct((8, GROUPS, rows, 2 * HW), bf16),
            jax.ShapeDtypeStruct((GROUPS, rows, 2 * BLK), bf16),
            jax.ShapeDtypeStruct((GROUPS, rows, width), bf16),
            jax.ShapeDtypeStruct(small, f32),
            jax.ShapeDtypeStruct((width, wide), bf16),
            jax.ShapeDtypeStruct((width, width), bf16),
            jax.ShapeDtypeStruct((width, width), bf16),
        ),
        in_specs=[whole_vmem()] * 5 + [anywhere()] * 2,
        out_specs=(anywhere(), *(whole_vmem(),) * 4, anywhere(), anywhere()),
        scratch_shapes=[
            pltpu.VMEM((GROUPS, rows, width), bf16),
            pltpu.VMEM((width // 2, wide), bf16),
            pltpu.VMEM(small, f32),
            pltpu.VMEM(small, f32),
            pltpu.VMEM((GROUPS, rows, 2 * HW), bf16),
            dma((2,)), dma((GROUPS,)), dma((GROUPS,)), dma((2,)), dma((2,)), dma((2,)),
            dma((7, GROUPS)), dma((7, GROUPS)), dma((GROUPS,)), dma((8,)), dma((8,)), dma((2,)),
        ],
        compiler_params=pltpu.CompilerParams(
            collective_id=0, has_side_effects=True, vmem_limit_bytes=14 << 20
        ),
        name="gather",
    )(tokens, query, key, value, lines, up, wo)


def erf_parts(values):
    below = 0.5 * (1.0 + lax.erf(values * ROOT_HALF))
    return below, PDF_SCALE * jnp.exp(-0.5 * values * values)


PARTS = 8
UNIT = 216


def dense_kernel(
    out_t_ref, tokens_ref, cot_ref, small_ref, up_ref, wo_ref, down_any,
    result_ref, middle_grad_ref, grad_t_ref, bundle_ref, sums_ref,
    down_ref, attn_in, attn_t, cots, h2s, mid_ref, n2_ref, part_y, part_d, in_y, in_d, pass_y, pass_d, x_y, x_d,
    hids, dus, grad_out, wo_keep, wo_give, wo_in, wo_pass, wo_x,
    down_sem, a_send, a_recv, c_send, c_recv, h_send, h_recv, y_send, y_recv, d_send, d_recv, o_send, o_recv,
    w_send, w_recv,
):
    g, r, core, x = place()
    other = 1 - x
    rows, width = tokens_ref.shape
    half = width // 2
    fourth = half // 2
    load = pltpu.make_async_copy(
        down_any.at[pl.ds(pl.multiple_of(core * width, width), width)], down_ref, down_sem
    )
    load.start()
    greet(g, r, core, x, True)
    cots[0] = cot_ref[...]

    def share(rows_ref, out_sem, in_sem):
        moves = (
            send(rows_ref.at[0], rows_ref.at[2], out_sem.at[1], in_sem.at[1], x=other),
            send(rows_ref.at[0], rows_ref.at[1], out_sem.at[0], in_sem.at[0], core=1 - core),
        )
        for move in moves:
            move.start()
        return moves

    def pass_on(rows_ref, moves, out_sem, in_sem):
        moves[0].wait_recv()
        move = send(rows_ref.at[2], rows_ref.at[3], out_sem.at[2], in_sem.at[2], core=1 - core)
        move.start()
        return move

    def other_group(away):
        return lax.rem(g + away, GROUPS)

    attn_moves = []
    for away in range(1, GROUPS):
        to = other_group(away)
        attn_moves.append(
            send(out_t_ref.at[pl.ds(2 * to, 2)], attn_in.at[g], a_send.at[away], a_recv.at[g], g=to)
        )
        attn_moves[-1].start()
    cot_moves = share(cots, c_send, c_recv)
    attn_in[g] = out_t_ref[pl.ds(2 * g, 2)]
    sums_ref[...] = jnp.zeros_like(sums_ref)
    sums_ref[5:6] = jnp.sum(cot_ref[...].astype(f32), axis=0, keepdims=True)
    for away in range(1, GROUPS):
        source = other_group(away)
        send(attn_in.at[source], attn_in.at[source], a_send.at[away], a_recv.at[source], g=source).wait_recv()
    for source in range(GROUPS):
        attn_t[HW * source : HW * source + HW] = jnp.concatenate(
            [attn_in[source, 0], attn_in[source, 1]], axis=1
        )
    middle = tokens_ref[...].astype(f32) + outer(attn_t[...], wo_ref[...]) + small_ref[2:3]
    mid_ref[...] = middle
    mean = jnp.mean(middle, axis=-1, keepdims=True)
    centred = middle - mean
    spread = jnp.mean(centred * centred, axis=-1, keepdims=True)
    scale = lax.rsqrt(spread + EPS)
    n2_ref[...] = centred * scale
    h2s[0] = (n2_ref[...] * small_ref[3:4] + small_ref[4:5]).astype(bf16)
    h2_moves = share(h2s, h_send, h_recv)
    cot_pass = pass_on(cots, cot_moves, c_send, c_recv)
    load.wait()
    bias_row = 8 + 2 * x + core
    bias = small_ref[pl.ds(bias_row, 1)]
    sums_ref[pl.ds(bias_row, 1)] = jnp.zeros((1, width), f32)

    def one_part(part):
        expanded = dot(h2s[part], up_ref[...]) + bias
        below, density = erf_parts(expanded)
        hidden = (expanded * below).astype(bf16)
        hids[part] = hidden
        slope = below + expanded * density
        grad_hidden = inner(cots[part], down_ref[...]).astype(bf16).astype(f32)
        grad_expand = (grad_hidden * slope).astype(bf16)
        dus[part] = grad_expand
        part_d[part] = inner(grad_expand, up_ref[...])
        part_y[part] = dot(hidden, down_ref[...])
        sums_ref[pl.ds(bias_row, 1)] += jnp.sum(grad_expand.astype(f32), axis=0, keepdims=True)

    one_part(0)
    cot_moves[1].wait_recv()
    h2_moves[1].wait_recv()
    h2_pass = pass_on(h2s, h2_moves, h_send, h_recv)
    one_part(1)
    d_sib = send(part_d.at[1], in_d, d_send.at[0], d_recv.at[0], core=1 - core)
    d_sib.start()
    cot_pass.wait_recv()
    h2_pass.wait_recv()
    one_part(3)
    x_d[0] = part_d[3].astype(bf16)
    x_y[0] = part_y[3].astype(bf16)
    d_pass = send(x_d.at[0], pass_d, d_send.at[1], d_recv.at[1], core=1 - core)
    y_pass = send(x_y.at[0], pass_y, y_send.at[1], y_recv.at[1], core=1 - core)
    d_pass.start()
    y_pass.start()
    one_part(2)
    d_pass.wait_recv()
    x_d[1] = (part_d[2] + pass_d[...].astype(f32)).astype(bf16)
    d_x = send(x_d.at[1], x_d.at[2], d_send.at[2], d_recv.at[2], x=other)
    d_x.start()
    y_pass.wait_recv()
    x_y[1] = (part_y[2] + pass_y[...].astype(f32)).astype(bf16)
    y_x = send(x_y.at[1], x_y.at[2], y_send.at[2], y_recv.at[2], x=other)
    y_x.start()
    y_sib = send(part_y.at[1], in_y, y_send.at[0], y_recv.at[0], core=1 - core)
    y_sib.start()

    def over_rows(left, right):
        total = outer(left[0], right[0])
        for part in range(1, 4):
            total += outer(left[part], right[part])
        return total.astype(bf16)

    down_grad = over_rows(hids, cots)
    up_grad = over_rows(h2s, dus)
    for p in range(PARTS):
        bundle_ref[p // GROUPS, p % GROUPS, 0:96] = down_grad[96 * p : 96 * p + 96]
        bundle_ref[p // GROUPS, p % GROUPS, 96:144] = up_grad[48 * p : 48 * p + 48]
        bundle_ref[p // GROUPS, p % GROUPS, 144:192] = up_grad[half + 48 * p : half + 48 * p + 48]

    d_sib.wait_recv()
    d_x.wait_recv()
    grad_second = part_d[0] + in_d[...] + x_d[2].astype(f32)
    n2 = n2_ref[...]
    sums_ref[3:4] = jnp.sum(grad_second * n2, axis=0, keepdims=True)
    sums_ref[4:5] = jnp.sum(grad_second, axis=0, keepdims=True)
    pulled = grad_second * small_ref[3:4]
    inward = pulled - jnp.mean(pulled, axis=-1, keepdims=True) - n2 * jnp.mean(pulled * n2, axis=-1, keepdims=True)
    grad_middle = cot_ref[...].astype(f32) + inward * scale
    middle_grad_ref[...] = grad_middle
    branch = grad_middle.astype(bf16)
    sums_ref[2:3] = jnp.sum(branch.astype(f32), axis=0, keepdims=True)
    grad_out_t = inner(wo_ref[...], branch).astype(bf16)
    for group in range(GROUPS):
        for b in range(2):
            grad_out[group, b] = grad_out_t[HW * group : HW * group + HW, BLK * b : BLK * b + BLK]
    grad_moves = []
    for away in range(1, GROUPS):
        to = other_group(away)
        grad_moves.append(
            send(grad_out.at[to], grad_t_ref.at[pl.ds(2 * g, 2)], o_send.at[away], o_recv.at[g], g=to)
        )
        grad_moves[-1].start()
    grad_t_ref[pl.ds(2 * g, 2)] = grad_out[g]

    for owner in range(2):
        for c in range(2):
            piece = dot(attn_t[half * owner + fourth * c : half * owner + fourth * c + fourth], branch)

            @pl.when(core == c)
            def _():
                wo_keep[owner] = piece

            @pl.when(core != c)
            def _():
                wo_give[owner] = piece.astype(bf16)

    w_sib = send(wo_give, wo_in, w_send.at[0], w_recv.at[0], core=1 - core)
    w_sib.start()
    y_x.wait_recv()
    y_sib.wait_recv()
    result_ref[...] = (
        mid_ref[...] + part_y[0] + in_y[...] + x_y[2].astype(f32) + small_ref[5:6]
    ).astype(bf16)
    w_sib.wait_recv()
    wo_pass[...] = (wo_keep[other] + wo_in[other].astype(f32)).astype(bf16)
    w_x = send(wo_pass, wo_x, w_send.at[1], w_recv.at[1], x=other)
    w_x.start()
    mine = wo_keep[x] + wo_in[x].astype(f32)
    w_x.wait_recv()
    wo_sum = (mine + wo_x[...].astype(f32)).astype(bf16)
    for p in range(PARTS):
        bundle_ref[p // GROUPS, p % GROUPS, 192:UNIT] = wo_sum[24 * p : 24 * p + 24]
    for away in range(1, GROUPS):
        source = other_group(away)
        send(
            grad_t_ref.at[pl.ds(2 * source, 2)], grad_t_ref.at[pl.ds(2 * source, 2)],
            o_send.at[away], o_recv.at[source], g=source,
        ).wait_recv()
    for item in (
        *cot_moves, cot_pass, *h2_moves, h2_pass, d_sib, d_pass, d_x, y_sib, y_pass, y_x, w_sib, w_x, *attn_moves, *grad_moves,
    ):
        item.wait_send()


def dense(out_t, tokens, cot, small, up, wo, down):
    rows, width = tokens.shape
    dma = pltpu.SemaphoreType.DMA
    full = (rows, width)
    fourth = (width // 4, width)
    return pl.pallas_call(
        dense_kernel,
        out_shape=(
            jax.ShapeDtypeStruct(full, bf16),
            jax.ShapeDtypeStruct(full, f32),
            jax.ShapeDtypeStruct(out_t.shape, bf16),
            jax.ShapeDtypeStruct((2, GROUPS, UNIT, width), bf16),
            jax.ShapeDtypeStruct(small.shape, f32),
        ),
        in_specs=[whole_vmem()] * 6 + [anywhere()],
        out_specs=(whole_vmem(),) * 5,
        scratch_shapes=[
            pltpu.VMEM((width, width), bf16),
            pltpu.VMEM((GROUPS, 2, HW, BLK), bf16),
            pltpu.VMEM((width, rows), bf16),
            pltpu.VMEM((4, *full), bf16),
            pltpu.VMEM((4, *full), bf16),
            pltpu.VMEM(full, f32),
            pltpu.VMEM(full, f32),
            pltpu.VMEM((4, *full), f32),
            pltpu.VMEM((4, *full), f32),
            pltpu.VMEM(full, f32),
            pltpu.VMEM(full, f32),
            pltpu.VMEM(full, bf16),
            pltpu.VMEM(full, bf16),
            pltpu.VMEM((3, *full), bf16),
            pltpu.VMEM((3, *full), bf16),
            pltpu.VMEM((4, *full), bf16),
            pltpu.VMEM((4, *full), bf16),
            pltpu.VMEM((GROUPS, 2, HW, BLK), bf16),
            pltpu.VMEM((2, *fourth), f32),
            pltpu.VMEM((2, *fourth), bf16),
            pltpu.VMEM((2, *fourth), bf16),
            pltpu.VMEM(fourth, bf16),
            pltpu.VMEM(fourth, bf16),
            dma(()), dma((GROUPS,)), dma((GROUPS,)), dma((3,)), dma((3,)), dma((3,)), dma((3,)),
            dma((3,)), dma((3,)), dma((3,)), dma((3,)), dma((GROUPS,)), dma((GROUPS,)), dma((2,)), dma((2,)),
        ],
        compiler_params=pltpu.CompilerParams(
            collective_id=1, has_side_effects=True, vmem_limit_bytes=40 << 20
        ),
        name="dense",
    )(out_t, tokens, cot, small, up, wo, down)


FARTHEST = ((3, 2, 1, 0), (3, 0, 2, 1), (0, 3, 1, 2), (0, 1, 2, 3))


def farthest(g, step):
    picked = FARTHEST[0][step]
    for z in range(1, GROUPS):
        picked = jnp.where(g == z, FARTHEST[z][step], picked)
    return picked


class Chain:
    def __init__(self, g, x, total, parts, inward, outward, out_sem, in_sem):
        self.g, self.x, self.total, self.parts = g, x, total, parts
        self.inward, self.outward, self.out_sem, self.in_sem = inward, outward, out_sem, in_sem

    def move(self, to, way):
        return send(
            self.outward.at[to], self.inward.at[way, to], self.out_sem.at[to], self.in_sem.at[way, to],
            g=jnp.clip(self.g + (1 if way == 0 else -1), 0, GROUPS - 1),
        )

    def step(self, to):
        g = self.g
        self.total[...] = self.parts[to].astype(f32)

        def take(way):
            arrived(self.inward.at[way, to], self.out_sem.at[to], self.in_sem.at[way, to], self.x)
            self.total[...] += self.inward[way, to].astype(f32)

        pl.when((to >= g) & (g > 0))(lambda: take(0))
        pl.when((to <= g) & (g < GROUPS - 1))(lambda: take(1))

        @pl.when(to != g)
        def _():
            self.outward[to] = self.total[...].astype(bf16)

        pl.when(to > g)(lambda: self.move(to, 0).start())
        pl.when(to < g)(lambda: self.move(to, 1).start())

    def finish(self):
        for step in range(GROUPS - 1):
            to = farthest(self.g, step)
            left(self.outward.at[to], self.out_sem.at[to], self.in_sem.at[0, to], self.x)


class Ring:
    def __init__(self, g, x, slot, own_sem, out_sem, in_sem):
        self.g, self.x, self.slot = g, x, slot
        self.own_sem, self.out_sem, self.in_sem = own_sem, out_sem, in_sem

    def move(self, source, way, sem):
        return send(
            self.slot(source), self.slot(source), sem, self.in_sem.at[source],
            g=jnp.clip(self.g + way, 0, GROUPS - 1),
        )

    def start(self):
        g = self.g
        pl.when(g > 0)(lambda: self.move(g, -1, self.own_sem.at[0]).start())
        pl.when(g < GROUPS - 1)(lambda: self.move(g, 1, self.own_sem.at[1]).start())

    def step(self, step):
        g, source = self.g, nearest(self.g, step)
        arrived(self.slot(source), self.out_sem.at[source], self.in_sem.at[source], self.x)
        pl.when((source < g) & (g < GROUPS - 1))(lambda: self.move(source, 1, self.out_sem.at[source]).start())
        pl.when((source > g) & (g > 0))(lambda: self.move(source, -1, self.out_sem.at[source]).start())
        return source

    def finish(self):
        g = self.g
        for i, there in enumerate((g > 0, g < GROUPS - 1)):
            pl.when(there)(lambda: left(self.slot(g), self.own_sem.at[i], self.in_sem.at[g], self.x))
        for step in range(1, GROUPS):
            source = nearest(g, step)
            passed = ((source < g) & (g < GROUPS - 1)) | ((source > g) & (g > 0))
            pl.when(passed)(
                lambda: left(self.slot(source), self.out_sem.at[source], self.in_sem.at[source], self.x)
            )


def arrived(what, out_sem, in_sem, x):
    send(what, what, out_sem, in_sem, x=1 - x).wait_recv()


def left(what, out_sem, in_sem, x):
    send(what, what, out_sem, in_sem, x=1 - x).wait_send()


def scatter_kernel(
    dkv_ref, dq_ref, normed_ref, wfull_ref, tokens_ref, mgrad_ref, small_ref, bundle_ref, sums_in,
    tokens_grad_ref, big_ref, qout_ref, kvout_ref, sums_ref,
    own_kv, sib_kv, keep_x, give_x, in_x, give_y, in_y, part_a, total_a, inward_a, outward_a, wg_kv,
    by_in, by_sum, total_b, inward_b, outward_b, unit,
    q_keep, q_give, q_in, q_pass, q_x, q_y, q_sum, v_keep, v_give, v_in, v_pass, v_x, v_y, v_sum,
    sums_got,
    own_sem, k_send, k_recv, x_send, x_recv, y_send, y_recv, ca_send, ca_recv,
    b_send, b_recv, cb_send, cb_recv, u_send, u_recv, rb_own, rb_send, rb_recv,
    fy_send, fy_recv, fs_send, fs_recv,
    q_send, q_recv, rq_own, rq_send, rq_recv, qs_send, qs_recv,
    v_send, v_recv, rv_own, rv_send, rv_recv, vs_send, vs_recv,
    s_send, s_recv, l_sem,
):
    g, r, core, x = place()
    other, sib, far_r = 1 - x, 1 - core, 1 - r
    rows, width = tokens_ref.shape
    half = width // 2
    fourth = half // 2
    wide_q = 2 * BLK
    greet(g, r, core, x, True)
    pending = []

    def begin(src, dst, out_sem, in_sem, **device):
        move = send(src, dst, out_sem, in_sem, **device)
        move.start()
        pending.append(move)
        return move

    def settled(move):
        move.wait_recv()
        move.wait_send()
        pending[:] = [item for item in pending if item is not move]

    kv_moves = []
    for i in range(GROUPS):
        c = farthest(g, i)
        for spot in range(4):
            own = pltpu.make_async_copy(dkv_ref.at[seat(spot // 2, core, spot % 2), c], own_kv.at[i, spot], own_sem.at[i, spot])
            own.start()
            across = begin(
                dkv_ref.at[seat(spot // 2, sib, spot % 2), c], sib_kv.at[i, spot],
                k_send.at[i, spot], k_recv.at[i, spot], core=sib,
            )
            kv_moves.append((own, across))

    def piece(i):
        z = farthest(g, i)
        begin(bundle_ref.at[far_r, z], by_in.at[z], b_send.at[i], b_recv.at[i], r=far_r)

    piece(0)
    piece(1)

    def split(total, keep, give, wide):
        for owner in range(2):
            for c in range(2):
                low = half * owner + fourth * c
                chunk = total[low : low + fourth]

                @pl.when(core == c)
                def _():
                    keep[owner] = chunk

                @pl.when(core != c)
                def _():
                    give[owner] = chunk.astype(bf16)

    def scaled(c):
        return dq_ref[c] * bf16(SCALE)

    query_total = outer(normed_ref[0], scaled(0))
    for c in range(1, GROUPS):
        query_total += outer(normed_ref[c], scaled(c))
    split(query_total, q_keep, q_give, wide_q)
    q_move = begin(q_give, q_in, q_send.at[0], q_recv.at[0], core=sib)
    sums_ref[...] = jnp.zeros_like(sums_ref)
    sums_ref[0:16] = sums_in[...]
    line_q = scaled(0).astype(f32)
    for c in range(1, GROUPS):
        line_q += scaled(c).astype(f32)
    sums_ref[pl.ds(16 + g, 1), 0:wide_q] = jnp.sum(line_q, axis=0, keepdims=True)
    wg_kv[...] = jnp.zeros_like(wg_kv)

    for i in range(GROUPS):
        for own, across in kv_moves[4 * i : 4 * i + 4]:
            own.wait()
            across.wait_recv()
        for row in range(2):
            give_x[i, row] = (
                own_kv[i, 2 * row + other].astype(f32) + sib_kv[i, 2 * row + other].astype(f32)
            ).astype(bf16)
        begin(give_x.at[i], in_x.at[i], x_send.at[i], x_recv.at[i], x=other)
        for row in range(2):
            keep_x[i, row] = own_kv[i, 2 * row + x].astype(f32) + sib_kv[i, 2 * row + x].astype(f32)
        if i == 1:
            q_move.wait_recv()
            q_pass[...] = (q_keep[other] + q_in[other].astype(f32)).astype(bf16)
    q_across = begin(q_pass, q_x, q_send.at[1], q_recv.at[1], x=other)

    chain_a = Chain(g, x, total_a, part_a, inward_a, outward_a, ca_send, ca_recv)
    chain_b = Chain(g, x, total_b, by_sum, inward_b, outward_b, cb_send, cb_recv)

    def on_x(i):
        arrived(in_x.at[i], x_send.at[i], x_recv.at[i], x)
        give_y[i] = (keep_x[i, far_r] + in_x[i, far_r].astype(f32)).astype(bf16)
        begin(give_y.at[i], in_y.at[i], y_send.at[i], y_recv.at[i], r=far_r)
        keep_x[i, r] += in_x[i, r].astype(f32)

    def on_y(i):
        c = farthest(g, i)
        arrived(in_y.at[i], y_send.at[i], y_recv.at[i], x)
        both = (keep_x[i, r] + in_y[i].astype(f32)).astype(bf16)
        part_a[c] = inner(scaled(c), wfull_ref[:, :wide_q]) + inner(both, wfull_ref[:, wide_q:])
        wg_kv[...] += outer(normed_ref[c], both)
        sums_ref[pl.ds(16 + g, 1), wide_q : wide_q + 2 * HW] += jnp.sum(both.astype(f32), axis=0, keepdims=True)

    def on_piece(i):
        z = farthest(g, i)
        arrived(by_in.at[z], b_send.at[i], b_recv.at[i], x)
        by_sum[z] = bundle_ref[r, z].astype(f32) + by_in[z].astype(f32)

    for i in range(GROUPS):
        on_x(i)
        if i < 2:
            piece(2 + i)
        on_piece(i)
        if i >= 1:
            on_y(i - 1)
        if i >= 2:
            chain_a.step(farthest(g, i - 2))
    on_y(GROUPS - 1)
    split(wg_kv, v_keep, v_give, 2 * HW)
    v_move = begin(v_give, v_in, v_send.at[0], v_recv.at[0], core=sib)
    chain_a.step(farthest(g, GROUPS - 2))
    q_across.wait_recv()
    q_sum[...] = (q_keep[x] + q_in[x].astype(f32) + q_x[...].astype(f32)).astype(bf16)
    q_over = begin(q_sum, q_y, q_send.at[2], q_recv.at[2], r=far_r)
    v_move.wait_recv()
    v_pass[...] = (v_keep[other] + v_in[other].astype(f32)).astype(bf16)
    v_across = begin(v_pass, v_x, v_send.at[1], v_recv.at[1], x=other)
    chain_b.step(farthest(g, 0))
    chain_b.step(farthest(g, 1))
    chain_a.step(g)

    grad_first = total_a[...]
    values = tokens_ref[...].astype(f32)
    mean = jnp.mean(values, axis=-1, keepdims=True)
    centred = values - mean
    scale = lax.rsqrt(jnp.mean(centred * centred, axis=-1, keepdims=True) + EPS)
    n1 = centred * scale
    pulled = grad_first * small_ref[0:1]
    inward = pulled - jnp.mean(pulled, axis=-1, keepdims=True) - n1 * jnp.mean(pulled * n1, axis=-1, keepdims=True)
    tokens_grad_ref[...] = mgrad_ref[...] + inward * scale
    sums_ref[0:1] = jnp.sum(grad_first * n1, axis=0, keepdims=True)
    sums_ref[1:2] = jnp.sum(grad_first, axis=0, keepdims=True)
    s_sib = begin(sums_ref, sums_got.at[0], s_send.at[0], s_recv.at[0], core=sib)

    def q_slot(z):
        return qout_ref.at[core, z]

    def v_slot(z):
        return kvout_ref.at[core, z]

    def b_slot(z):
        return big_ref.at[core, r, z]

    ring_q = Ring(g, x, q_slot, rq_own, rq_send, rq_recv)
    ring_v = Ring(g, x, v_slot, rv_own, rv_send, rv_recv)
    ring_b = Ring(g, x, b_slot, rb_own, rb_send, rb_recv)

    def store(value_ref, slot, sem):
        copy = pltpu.make_async_copy(value_ref, slot, sem)
        copy.start()
        copy.wait()

    settled(q_over)
    q_sum[...] = (q_sum[...].astype(f32) + q_y[...].astype(f32)).astype(bf16)
    store(q_sum, q_slot(g), l_sem.at[0])
    ring_q.start()
    begin(q_slot(g), q_slot(g), qs_send.at[0], qs_recv.at[0], core=sib)

    chain_b.step(farthest(g, 2))
    v_across.wait_recv()
    v_sum[...] = (v_keep[x] + v_in[x].astype(f32) + v_x[...].astype(f32)).astype(bf16)
    v_over = begin(v_sum, v_y, v_send.at[2], v_recv.at[2], r=far_r)
    chain_b.step(g)
    unit[...] = total_b[...].astype(bf16)
    up_rows = 96 + 48 * other
    u_move = begin(
        unit.at[pl.ds(up_rows, 48)], big_ref.at[core, r, g, pl.ds(96 + 48 * x, 48)], u_send.at[0], u_recv.at[0], x=other
    )
    copies = [
        pltpu.make_async_copy(unit.at[pl.ds(0, 96)], big_ref.at[core, r, g, pl.ds(0, 96)], l_sem.at[1]),
        pltpu.make_async_copy(
            unit.at[pl.ds(96 + 48 * x, 48)], big_ref.at[core, r, g, pl.ds(96 + 48 * x, 48)], l_sem.at[2]
        ),
        pltpu.make_async_copy(unit.at[pl.ds(192, 24)], big_ref.at[core, r, g, pl.ds(192, 24)], l_sem.at[3]),
    ]
    for copy in copies:
        copy.start()
    settled(s_sib)
    sums_ref[...] += sums_got[0]
    s_x = begin(sums_ref, sums_got.at[1], s_send.at[1], s_recv.at[1], x=other)
    for copy in copies:
        copy.wait()
    there = big_ref.at[core, r, g, pl.ds(up_rows, 48)]
    arrived(there, u_send.at[0], u_recv.at[0], x)
    ring_b.start()

    def spread_b(z, step):
        begin(b_slot(z), b_slot(z), fy_send.at[step], fy_recv.at[step], r=far_r)
        begin(b_slot(z), b_slot(z), fs_send.at[0, step], fs_recv.at[0, step], core=sib)

    def spread_far(z, step):
        what = big_ref.at[core, far_r, z]
        arrived(what, fy_send.at[step], fy_recv.at[step], x)
        begin(what, what, fs_send.at[1, step], fs_recv.at[1, step], core=sib)

    spread_b(g, 0)
    settled(v_over)
    v_sum[...] = (v_sum[...].astype(f32) + v_y[...].astype(f32)).astype(bf16)
    store(v_sum, v_slot(g), l_sem.at[0])
    ring_v.start()
    begin(v_slot(g), v_slot(g), vs_send.at[0], vs_recv.at[0], core=sib)
    settled(s_x)
    sums_ref[...] += sums_got[1]
    s_y = begin(sums_ref, sums_got.at[2], s_send.at[2], s_recv.at[2], r=far_r)
    for step in range(1, GROUPS):
        z = ring_q.step(step)
        begin(q_slot(z), q_slot(z), qs_send.at[step], qs_recv.at[step], core=sib)
        if step == 1:
            settled(s_y)
            sums_ref[...] += sums_got[2]
            for away in range(1, GROUPS):
                begin(
                    sums_ref, sums_got.at[2 + away], s_send.at[2 + away], s_recv.at[2 + away],
                    g=lax.rem(g + away, GROUPS),
                )
        z = ring_b.step(step)
        spread_b(z, step)
        spread_far(nearest(g, step - 1), step - 1)
        z = ring_v.step(step)
        begin(v_slot(z), v_slot(z), vs_send.at[step], vs_recv.at[step], core=sib)
    spread_far(nearest(g, GROUPS - 1), GROUPS - 1)

    for away in range(1, GROUPS):
        arrived(sums_got.at[2 + away], s_send.at[2 + away], s_recv.at[2 + away], x)
    for step in range(GROUPS):
        z = nearest(g, step)
        arrived(qout_ref.at[sib, z], qs_send.at[step], qs_recv.at[step], x)
        arrived(kvout_ref.at[sib, z], vs_send.at[step], vs_recv.at[step], x)
        arrived(big_ref.at[sib, r, z], fs_send.at[0, step], fs_recv.at[0, step], x)
        arrived(big_ref.at[sib, far_r, z], fs_send.at[1, step], fs_recv.at[1, step], x)
    for move in pending:
        move.wait_send()
    for item in (chain_a, chain_b, ring_q, ring_v, ring_b):
        item.finish()
    sums_ref[...] += sums_got[3] + sums_got[4] + sums_got[5]


def scatter(dkv, dq, normed, wfull, tokens, mgrad, small, bundle, sums):
    rows, width = tokens.shape
    fourth = width // 4
    dma = pltpu.SemaphoreType.DMA
    wide_q, wide_v = 2 * BLK, 2 * HW
    kv_block = (rows, wide_v)
    full = (rows, width)
    unit = (UNIT, width)

    def weight_scratch(wide):
        return [
            pltpu.VMEM((2, fourth, wide), f32),
            pltpu.VMEM((2, fourth, wide), bf16),
            pltpu.VMEM((2, fourth, wide), bf16),
            *[pltpu.VMEM((fourth, wide), bf16)] * 4,
        ]

    return pl.pallas_call(
        scatter_kernel,
        out_shape=(
            jax.ShapeDtypeStruct(full, f32),
            jax.ShapeDtypeStruct((2, 2, GROUPS, *unit), bf16),
            jax.ShapeDtypeStruct((2, GROUPS, fourth, wide_q), bf16),
            jax.ShapeDtypeStruct((2, GROUPS, fourth, wide_v), bf16),
            jax.ShapeDtypeStruct((24, width), f32),
        ),
        in_specs=[anywhere()] + [whole_vmem()] * 8,
        out_specs=(whole_vmem(), anywhere(), anywhere(), anywhere(), whole_vmem()),
        scratch_shapes=[
            pltpu.VMEM((GROUPS, 4, *kv_block), bf16),
            pltpu.VMEM((GROUPS, 4, *kv_block), bf16),
            pltpu.VMEM((GROUPS, 2, *kv_block), f32),
            pltpu.VMEM((GROUPS, 2, *kv_block), bf16),
            pltpu.VMEM((GROUPS, 2, *kv_block), bf16),
            pltpu.VMEM((GROUPS, *kv_block), bf16),
            pltpu.VMEM((GROUPS, *kv_block), bf16),
            pltpu.VMEM((GROUPS, *full), f32),
            pltpu.VMEM(full, f32),
            pltpu.VMEM((2, GROUPS, *full), bf16),
            pltpu.VMEM((GROUPS, *full), bf16),
            pltpu.VMEM((width, wide_v), f32),
            pltpu.VMEM((GROUPS, *unit), bf16),
            pltpu.VMEM((GROUPS, *unit), f32),
            pltpu.VMEM(unit, f32),
            pltpu.VMEM((2, GROUPS, *unit), bf16),
            pltpu.VMEM((GROUPS, *unit), bf16),
            pltpu.VMEM(unit, bf16),
            *weight_scratch(wide_q),
            *weight_scratch(wide_v),
            pltpu.VMEM((6, 24, width), f32),
            dma((GROUPS, 4)), dma((GROUPS, 4)), dma((GROUPS, 4)), dma((GROUPS,)), dma((GROUPS,)), dma((GROUPS,)), dma((GROUPS,)),
            dma((GROUPS,)), dma((2, GROUPS)),
            dma((GROUPS,)), dma((GROUPS,)), dma((GROUPS,)), dma((2, GROUPS)), dma((1,)), dma((1,)), dma((2,)), dma((GROUPS,)), dma((GROUPS,)),
            dma((GROUPS,)), dma((GROUPS,)), dma((2, GROUPS)), dma((2, GROUPS)),
            dma((3,)), dma((3,)), dma((2,)), dma((GROUPS,)), dma((GROUPS,)), dma((GROUPS,)), dma((GROUPS,)),
            dma((3,)), dma((3,)), dma((2,)), dma((GROUPS,)), dma((GROUPS,)), dma((GROUPS,)), dma((GROUPS,)),
            dma((6,)), dma((6,)), dma((4,)),
        ],
        compiler_params=pltpu.CompilerParams(
            collective_id=2, has_side_effects=True, vmem_limit_bytes=51 << 20
        ),
        name="scatter",
    )(dkv, dq, normed, wfull, tokens, mgrad, small, bundle, sums)


def pack_kv(key_part, value_part):
    return jnp.concatenate(
        [key_part, value_part[..., 2 * DH :], value_part[..., : 2 * DH]], axis=-1
    )


def unpack_kv(both):
    return both[..., :HW], jnp.concatenate([both[..., HW + DH :], both[..., HW : HW + DH]], axis=-1)


def layout_kernel(
    big_ref, query_ref, kv_ref, sums_ref,
    up_out, down_out, wo_out, query_out, key_out, value_out,
    low_gain, low_shift, query_bias, value_bias, out_bias, high_gain, high_shift, up_bias, down_bias,
):
    x = lax.axis_index("x")
    width = big_ref.shape[-1]
    half = width // 2
    for core in range(2):
        down_out[core] = big_ref[core, 0, 0:96].astype(f32)
        wo_out[core] = big_ref[core, 0, 192:UNIT].astype(f32)
        for owner in range(2):
            lane = (2 * owner + core) * width
            up_out[:, lane : lane + width] = big_ref[core, 0, 96 + 48 * owner : 144 + 48 * owner].astype(f32)
        query_out[core] = jnp.concatenate(
            [query_ref[core, z].astype(f32)[:, :HW] for z in range(GROUPS)], axis=1
        )
        both = [unpack_kv(kv_ref[core, z].astype(f32)) for z in range(GROUPS)]
        key_out[core] = jnp.concatenate([item[0] for item in both], axis=1)
        value_out[core] = jnp.concatenate([item[1] for item in both], axis=1)

    @pl.when(pl.program_id(0) == 0)
    def _():
        def own_half(row):
            whole = sums_ref[row : row + 1]
            return jnp.where(x == 0, whole[:, :half], whole[:, half:])

        for ref, row in (
            (low_gain, 0), (low_shift, 1), (out_bias, 2), (high_gain, 3), (high_shift, 4), (down_bias, 5),
        ):
            ref[...] = own_half(row)
        pair = [sums_ref[pl.ds(16 + 2 * x + i, 1)] for i in range(2)]
        query_bias[...] = jnp.concatenate([item[:, :HW] for item in pair], axis=1)
        value_bias[...] = jnp.concatenate(
            [unpack_kv(item[:, 2 * BLK : 2 * BLK + 2 * HW])[1] for item in pair], axis=1
        )
        up_bias[...] = jnp.concatenate([sums_ref[pl.ds(8 + 2 * x + i, 1)] for i in range(2)], axis=1)


def lay_out(big, query, kv, sums):
    width = big.shape[-1]
    half, fourth = width // 2, width // 4
    rows = fourth // PARTS

    def spec(shape, index):
        return pl.BlockSpec(shape, index)

    def fixed(wide):
        return pl.BlockSpec((1, wide), lambda p: (0, 0))

    narrow = spec((2, rows, width), lambda p: (0, p, 0))
    vector = jax.ShapeDtypeStruct((1, half), f32)
    return pl.pallas_call(
        layout_kernel,
        grid=(PARTS,),
        out_shape=(
            jax.ShapeDtypeStruct((half, 4 * width), f32),
            jax.ShapeDtypeStruct((2, width, width), f32),
            *[jax.ShapeDtypeStruct((2, fourth, width), f32)] * 4,
            *[vector] * 7,
            jax.ShapeDtypeStruct((1, 2 * width), f32),
            vector,
        ),
        in_specs=[
            spec((2, 1, UNIT, width), lambda p: (0, p, 0, 0)),
            spec((2, GROUPS, rows, query.shape[-1]), lambda p: (0, 0, p, 0)),
            spec((2, GROUPS, rows, kv.shape[-1]), lambda p: (0, 0, p, 0)),
            spec(sums.shape, lambda p: (0, 0)),
        ],
        out_specs=(
            spec((48, 4 * width), lambda p: (p, 0)),
            spec((2, 96, width), lambda p: (0, p, 0)),
            *[narrow] * 4,
            *[fixed(half)] * 7,
            fixed(2 * width),
            fixed(half),
        ),
        compiler_params=pltpu.CompilerParams(
            vmem_limit_bytes=12 << 20, dimension_semantics=("arbitrary",)
        ),
        name="lay_out",
    )(big, query, kv, sums)


ROWS = ("s", "r", "core", "x")
ALL = ("g", "s", "r", "core", "x")


def shards(
    tokens, cotangent, doc_lengths, deal, first_gain, first_shift, query_weight, query_bias,
    key_weight, value_weight, value_bias, output_weight, output_bias, second_gain, second_shift,
    up_weight, up_bias, down_weight, down_bias,
):
    rows, width = tokens.shape
    half = width // 2
    blocks = deal.shape[0]
    lines = jnp.concatenate(
        [
            first_gain, first_shift, output_bias, second_gain, second_shift, down_bias, query_bias, value_bias, up_bias,
        ]
    ).reshape(-1, half)
    kv, q, normed, small, wfull, up, wo = gather(
        tokens, query_weight, key_weight, value_weight, lines, up_weight, output_weight
    )
    wide = blocks > 8 * 2 * GROUPS
    if wide:
        kv = lax.all_gather(kv, "s", axis=0, tiled=True)
    kv = kv.reshape(blocks, BLK, 2 * HW)
    q = q.reshape(2 * GROUPS, BLK, 2 * BLK)
    out_t, kept, lse = attend_forward(deal, doc_lengths, q, kv)
    result, grad_middle, grad_t, bundle, sums = dense(
        out_t, tokens, cotangent, small, up, wo, down_weight
    )
    dq, dkv = attend_backward(deal, doc_lengths, q, kv, lse, grad_t, kept)
    dkv = dkv.reshape(-1, GROUPS, rows, 2 * HW)
    if wide:
        dkv = lax.psum_scatter(dkv, "s", scatter_dimension=0, tiled=True)
    dq = dq.reshape(GROUPS, rows, 2 * BLK)
    grad_tokens, big, query_own, kv_own, sums = scatter(
        dkv, dq, normed, wfull, tokens, grad_middle, small, bundle, sums
    )
    if wide:
        big, query_own, kv_own, sums = (
            lax.psum(item, "s") for item in (big, query_own, kv_own, sums)
        )

    (
        up_own, down_own, wo_own, query_own, key_own, value_own,
        low_gain, low_shift, query_sum, value_sum, out_sum, high_gain, high_shift, up_sum, down_sum,
    ) = lay_out(big.reshape(2, PARTS, UNIT, width), query_own, kv_own, sums)

    def flat(item):
        return item.reshape(-1, width)

    def line(item):
        return item.reshape(-1)

    return (
        result,
        grad_tokens,
        line(low_gain),
        line(low_shift),
        flat(query_own),
        line(query_sum),
        flat(key_own),
        flat(value_own),
        line(value_sum),
        flat(wo_own),
        line(out_sum),
        line(high_gain),
        line(high_shift),
        up_own,
        line(up_sum),
        flat(down_own),
        line(down_sum),
    )


def solution(mesh):
    devices = mesh.devices
    inner_mesh = Mesh(devices.reshape(GROUPS, devices.shape[0] // (4 * GROUPS), 2, 2, 2), ALL)
    row = P(ALL, None)
    mat = P("x", None)
    vec = P("x")
    in_specs = (
        row, row, P(), P(), vec, vec, mat, vec, mat, mat, vec, mat, vec, vec, vec, mat, vec, mat, vec,
    )
    out_specs = (
        row, row, vec, vec, mat, vec, mat, mat, vec, mat, vec, vec, vec, mat, vec, mat, vec,
    )
    return jax.shard_map(
        shards, mesh=inner_mesh, in_specs=in_specs, out_specs=out_specs, check_vma=False
    )
```

```python
import jax
import jax.numpy as jnp
from jax import lax
from jax.experimental import pallas as pl
from jax.experimental.pallas import tpu as pltpu
from jax.sharding import Mesh
from jax.sharding import PartitionSpec as P

HEADS = 12
DH = 64
NSUM = 50
SEG = 2048
BLK = 128
GROUPS = 4
PER = HEADS // GROUPS
HW = PER * DH
WIDE = PER * BLK
CHUNK = 2 * BLK
EPS = 1e-05
SCALE = 0.125
MASKED = -1e30
ROOT_HALF = 0.7071067811865476
PDF_SCALE = 0.3989422804014327
VMEM_LIMIT = 56 << 20
bf16 = jnp.bfloat16
f32 = jnp.float32


def layer_norm(values, gain, shift):
    mean = jnp.mean(values, axis=-1, keepdims=True)
    centred = values - mean
    spread = jnp.mean(centred * centred, axis=-1, keepdims=True)
    return centred * lax.rsqrt(spread + EPS) * gain + shift


def outer(left, right):
    return lax.dot_general(left, right, (((0,), (0,)), ((), ())), preferred_element_type=f32)


def inner(left, right):
    return lax.dot_general(left, right, (((1,), (1,)), ((), ())), preferred_element_type=f32)


def dot(left, right):
    return jnp.dot(left, right, preferred_element_type=f32)


def survey(deal_ref, lengths_ref, where_ref, text_ref, low_ref, high_ref, first_ref):
    blocks = deal_ref.shape[0]
    per_group = blocks // (2 * GROUPS)
    rest = lax.axis_index(ROWS)

    def note(j, kept):
        pair = j // 2
        group = pair // per_group
        where_ref[deal_ref[j]] = ((pair - group * per_group) * GROUPS + group) * 2 + j % 2
        return kept

    lax.fori_loop(0, blocks, note, 0)
    starts = [jnp.int32(0)]
    for doc in range(lengths_ref.shape[0] - 1):
        starts.append(starts[-1] + lengths_ref[doc])

    def first_of(at):
        begin = jnp.zeros_like(at)
        for start in starts:
            begin = jnp.where(start <= at, jnp.maximum(begin, start), begin)
        return jnp.where(at - begin >= SEG + NSUM, begin + SEG, begin)

    for slot in range(2 * GROUPS):
        text = deal_ref[2 * ((slot // 2) * per_group + rest) + slot % 2]
        text_ref[slot] = text
        low_ref[slot] = first_of(text * BLK) // CHUNK
        high_ref[slot] = text // 2
        first_ref[slot] = first_of(text * BLK + lax.broadcasted_iota(jnp.int32, (1, BLK), 1))


def survey_scratch(blocks):
    slots = 2 * GROUPS
    return [
        pltpu.SMEM((blocks,), jnp.int32),
        pltpu.SMEM((slots,), jnp.int32),
        pltpu.SMEM((slots,), jnp.int32),
        pltpu.SMEM((slots,), jnp.int32),
        pltpu.VMEM((slots, 1, BLK), jnp.int32),
    ]


def spread_heads_t(part_t, order):
    rows = []
    zero = jnp.zeros((DH, BLK), part_t.dtype)
    for head in order:
        if head is None:
            rows.append(jnp.zeros((DH, WIDE), part_t.dtype))
        else:
            piece = part_t[DH * head : DH * head + DH]
            rows.append(
                jnp.concatenate([piece if h == head else zero for h in range(PER)], axis=1)
            )
    return jnp.concatenate(rows, axis=0)


K_ORDER = (0, 1, 2, None)
V_ORDER = (None, 2, 0, 1)


def visible(chunk, first, own):
    at = chunk * CHUNK + lax.broadcasted_iota(jnp.int32, (CHUNK, BLK), 0)
    allowed = (at >= first) & (at <= own)
    return jnp.concatenate([allowed] * PER, axis=1)


def load_chunk(kv_ref, where_ref, chunk):
    return jnp.concatenate(
        [kv_ref[where_ref[2 * chunk]], kv_ref[where_ref[2 * chunk + 1]]], axis=0
    )


def forward_kernel(
    deal_ref, lengths_ref, q_ref, kv_ref,
    out_ref, wide_ref, lse_ref,
    where_ref, text_ref, low_ref, high_ref, first_ref, vt_ref, acc_ref,
):
    survey(deal_ref, lengths_ref, where_ref, text_ref, low_ref, high_ref, first_ref)
    chunks = kv_ref.shape[0] // 2

    def turn(chunk, _):
        vt_ref[chunk] = load_chunk(kv_ref, where_ref, chunk)[:, BLK : 3 * BLK].T[DH:]
        return _

    lax.fori_loop(0, chunks, turn, 0)

    def one_slot(slot, _):
        wide_q = spread_heads_t(q_ref[slot].T[:HW], K_ORDER)
        first = first_ref[slot]
        own = text_ref[slot] * BLK + lax.broadcasted_iota(jnp.int32, (1, BLK), 1)
        acc_ref[...] = jnp.zeros_like(acc_ref)

        def step(chunk, carry):
            top, total = carry
            part = load_chunk(kv_ref, where_ref, chunk)
            scores = dot(part[:, : 2 * BLK], wide_q)
            scores = jnp.where(visible(chunk, first, own), scores, MASKED)
            fresh = jnp.maximum(top, jnp.max(scores, axis=0, keepdims=True))
            expo = jnp.exp(scores - fresh)
            shrink = jnp.exp(top - fresh)
            total = total * shrink + jnp.sum(expo, axis=0, keepdims=True)
            acc_ref[...] = acc_ref[...] * shrink + dot(vt_ref[chunk], expo.astype(bf16))
            return fresh, total

        top, total = lax.fori_loop(
            low_ref[slot],
            high_ref[slot] + 1,
            step,
            (jnp.full((1, WIDE), MASKED, f32), jnp.zeros((1, WIDE), f32)),
        )
        lse_ref[slot] = top + jnp.log(total)
        scaled = acc_ref[...] / total
        pieces = []
        for head in range(PER):
            row = DH * V_ORDER.index(head) - DH
            pieces.append(scaled[row : row + DH, BLK * head : BLK * head + BLK])
        kept = jnp.concatenate(pieces, axis=0)
        wide_ref[slot] = kept
        out_ref[slot] = kept.astype(bf16)
        return _

    lax.fori_loop(0, q_ref.shape[0], one_slot, 0)


def whole_vmem():
    return pl.BlockSpec(memory_space=pltpu.VMEM)


def whole_smem():
    return pl.BlockSpec(memory_space=pltpu.SMEM)


def attend_forward(deal, lengths, q, kv):
    slots = q.shape[0]
    blocks = kv.shape[0]
    return pl.pallas_call(
        forward_kernel,
        out_shape=(
            jax.ShapeDtypeStruct((slots, HW, BLK), bf16),
            jax.ShapeDtypeStruct((slots, HW, BLK), f32),
            jax.ShapeDtypeStruct((slots, 1, WIDE), f32),
        ),
        in_specs=[whole_smem()] * 2 + [whole_vmem()] * 2,
        out_specs=(whole_vmem(),) * 3,
        scratch_shapes=[
            *survey_scratch(blocks),
            pltpu.VMEM((blocks // 2, HW, CHUNK), bf16),
            pltpu.VMEM((HW, WIDE), f32),
        ],
        compiler_params=pltpu.CompilerParams(vmem_limit_bytes=(6 << 20) + kv.size // 5 * 16),
        name="attend_forward",
    )(deal, lengths, q, kv)


def backward_kernel(
    deal_ref, lengths_ref, q_ref, kv_ref, lse_ref, do_ref, wide_ref,
    dq_ref, dkv_ref, where_ref, text_ref, low_ref, high_ref, first_ref, qt_ref, qm_ref, dot_ref, dom_ref, delta_ref, acc_ref, dk_acc, dv_acc,
    packed_ref, out_sem,
):
    survey(deal_ref, lengths_ref, where_ref, text_ref, low_ref, high_ref, first_ref)
    slots = q_ref.shape[0]
    chunks = kv_ref.shape[0] // 2

    def ready(slot, _):
        q = q_ref[slot]
        qt_ref[slot] = spread_heads_t(q.T[:HW], K_ORDER)
        lane = lax.broadcasted_iota(jnp.int32, (BLK, 2 * BLK), 1) // DH
        zero = jnp.zeros_like(q)
        qm_ref[slot] = jnp.concatenate(
            [jnp.where(lane == K_ORDER.index(h), q, zero) for h in range(PER)], axis=0
        )
        grad_t = do_ref[slot]
        dot_ref[slot] = spread_heads_t(grad_t, V_ORDER)
        ordered = jnp.concatenate(
            [
                jnp.zeros((DH, BLK), bf16) if h is None else grad_t[DH * h : DH * h + DH]
                for h in V_ORDER
            ],
            axis=0,
        ).T
        dom_ref[slot] = jnp.concatenate(
            [jnp.where(lane == V_ORDER.index(h), ordered, zero) for h in range(PER)], axis=0
        )
        both = grad_t.astype(f32) * wide_ref[slot]
        delta_ref[slot] = jnp.concatenate(
            [jnp.sum(both[DH * h : DH * h + DH], axis=0, keepdims=True) for h in range(PER)],
            axis=1,
        )
        acc_ref[slot] = jnp.zeros((HW, WIDE), f32)
        return _

    lax.fori_loop(0, slots, ready, 0)

    def written(chunk, i):
        return pltpu.make_async_copy(
            packed_ref.at[chunk % 2, i], dkv_ref.at[where_ref[2 * chunk + i]], out_sem.at[chunk % 2, i]
        )

    def one_chunk(chunk, kept):
        part = load_chunk(kv_ref, where_ref, chunk)
        keys = part[:, : 2 * BLK]
        vals = part[:, BLK:]
        keys_t = keys.T[:HW]
        dk_acc[...] = jnp.zeros_like(dk_acc)
        dv_acc[...] = jnp.zeros_like(dv_acc)

        def one_slot(slot, kept):
            @pl.when((low_ref[slot] <= chunk) & (chunk <= high_ref[slot]))
            def _():
                own = text_ref[slot] * BLK + lax.broadcasted_iota(jnp.int32, (1, BLK), 1)
                scores = dot(keys, qt_ref[slot])
                probs = jnp.where(
                    visible(chunk, first_ref[slot], own), jnp.exp(scores - lse_ref[slot]), 0.0
                )
                dprobs = dot(vals, dot_ref[slot])
                dscores = (probs * (dprobs - delta_ref[slot])).astype(bf16)
                dv_acc[...] += dot(probs.astype(bf16), dom_ref[slot])
                dk_acc[...] += dot(dscores, qm_ref[slot])
                acc_ref[slot] += dot(keys_t, dscores)

            return kept

        lax.fori_loop(0, slots, one_slot, 0)
        packed = jnp.concatenate(
            [
                dk_acc[:, :BLK],
                dk_acc[:, BLK:] + dv_acc[:, :BLK],
                dv_acc[:, BLK:],
            ],
            axis=1,
        ).astype(bf16)

        @pl.when(chunk >= 2)
        def _():
            for i in range(2):
                written(chunk - 2, i).wait()

        for i in range(2):
            packed_ref[chunk % 2, i] = packed[BLK * i : BLK * i + BLK]
            written(chunk, i).start()
        return kept

    lax.fori_loop(0, chunks, one_chunk, 0)
    for last in range(2):
        for i in range(2):
            written(chunks - 2 + last, i).wait()

    def finish(slot, _):
        total = acc_ref[slot]
        kept = jnp.concatenate(
            [total[DH * h : DH * h + DH, BLK * h : BLK * h + BLK] for h in range(PER)]
            + [jnp.zeros((DH, BLK), f32)],
            axis=0,
        )
        dq_ref[slot] = kept.T.astype(bf16)
        return _

    lax.fori_loop(0, slots, finish, 0)


def attend_backward(deal, lengths, q, kv, lse, grad_t, wide):
    slots = q.shape[0]
    return pl.pallas_call(
        backward_kernel,
        out_shape=(
            jax.ShapeDtypeStruct((slots, BLK, 2 * BLK), bf16),
            jax.ShapeDtypeStruct(kv.shape, bf16),
        ),
        in_specs=[whole_smem()] * 2 + [whole_vmem()] * 5,
        out_specs=(whole_vmem(), in_hbm()),
        scratch_shapes=[
            *survey_scratch(kv.shape[0]),
            pltpu.VMEM((slots, 2 * BLK, WIDE), bf16),
            pltpu.VMEM((slots, WIDE, 2 * BLK), bf16),
            pltpu.VMEM((slots, 2 * BLK, WIDE), bf16),
            pltpu.VMEM((slots, WIDE, 2 * BLK), bf16),
            pltpu.VMEM((slots, 1, WIDE), f32),
            pltpu.VMEM((slots, HW, WIDE), f32),
            pltpu.VMEM((CHUNK, 2 * BLK), f32),
            pltpu.VMEM((CHUNK, 2 * BLK), f32),
            pltpu.VMEM((2, 2, BLK, 2 * HW), bf16),
            pltpu.SemaphoreType.DMA((2, 2)),
        ],
        compiler_params=pltpu.CompilerParams(
            vmem_limit_bytes=max(48 << 20, (17 << 20) + kv.size * 2)
        ),
        name="attend_backward",
    )(deal, lengths, q, kv, lse, grad_t, wide)


MESH = pl.DeviceIdType.MESH


def send(src, dst, out_sem, in_sem, **device):
    return pltpu.make_async_remote_copy(
        src_ref=src, dst_ref=dst, send_sem=out_sem, recv_sem=in_sem, device_id=device, device_id_type=MESH
    )


def place():
    return tuple(lax.axis_index(name) for name in ("g", "r", "core", "x"))


def seat(r, core, x):
    return (r * 2 + core) * 2 + x


def greet(g, r, core, x, line):
    barrier = pltpu.get_barrier_semaphore()

    def hello(**device):
        pl.semaphore_signal(barrier, inc=1, device_id=device, device_id_type=MESH)

    hello(core=1 - core)
    hello(x=1 - x)
    hello(r=1 - r)
    if line:
        for away in range(1, GROUPS):
            hello(g=lax.rem(g + away, GROUPS))
        pl.semaphore_wait(barrier, 3 + GROUPS - 1)
    else:
        pl.when(g > 0)(lambda: hello(g=g - 1))
        pl.when(g < GROUPS - 1)(lambda: hello(g=g + 1))
        pl.semaphore_wait(barrier, 5 - jnp.where(g == 0, 1, 0) - jnp.where(g == GROUPS - 1, 1, 0))


NEAREST = tuple(tuple(sorted(range(GROUPS), key=lambda s: (abs(s - z), s))) for z in range(GROUPS))


def nearest(g, step):
    picked = NEAREST[0][step]
    for z in range(1, GROUPS):
        picked = jnp.where(g == z, NEAREST[z][step], picked)
    return picked


def prepare(g, x, weights, lines, narrow_ref, small_ref):
    half = weights.shape[1]
    odd = lax.rem(g, 2) == 1

    def columns(i):
        low = pl.multiple_of(3 * g // 2 * BLK, BLK)
        window = weights[i, :, pl.ds(low, 2 * BLK)]
        moved = jnp.concatenate([window[:, DH:], window[:, :DH]], axis=1)
        return jnp.where(odd, moved, window)

    lane = lax.broadcasted_iota(jnp.int32, (half, 2 * BLK), 1)
    query = columns(0)
    narrow_ref[:, : 2 * BLK] = jnp.where(lane < HW, query, jnp.zeros_like(query))
    narrow_ref[:, 2 * BLK :] = pack_kv(columns(1)[:, :HW], columns(2)[:, :HW])

    def line(i):
        return lines[i][...].astype(f32).reshape(1, -1)

    zero = jnp.zeros((1, half), f32)
    small_ref[...] = jnp.zeros_like(small_ref)
    for row in range(6):
        small_ref[row : row + 1] = jnp.where(
            x == 0, jnp.concatenate([line(row), zero], axis=1), jnp.concatenate([zero, line(row)], axis=1)
        )
    ups = line(8)
    for i in range(2):
        small_ref[pl.ds(8 + 2 * x + i, 1)] = ups[:, 2 * half * i : 2 * half * i + 2 * half]

    def part(i):
        mine = jnp.where(odd, line(i)[:, HW:], line(i)[:, :HW])
        return jnp.where(g // 2 == x, mine, jnp.zeros_like(mine))

    value = part(7)
    small_ref[12:13] = jnp.concatenate(
        [part(6), jnp.zeros((1, 2 * BLK), f32), value[:, 2 * DH :], value[:, : 2 * DH], jnp.zeros((1, BLK), f32)], axis=1
    )


def gather_kernel(
    tokens_ref, query_any, key_any, value_any, up_ref, wo_ref, l0, l1, l2, l3, l4, l5, l6, l7, l8,
    kv_ref, q_ref, normed_ref, small_out, wfull, up_out, wo_out,
    lined, attn_w, narrow_ref, small_ref, small_in, kvs,
    z_own, z_send, z_recv, s_sem, n_send, n_recv, kv_send, kv_recv, kv_local, w_send, w_recv, w_local, a_sem,
):
    g, r, core, x = place()
    other = 1 - x
    rows, width = tokens_ref.shape
    half = width // 2
    fourth = half // 2
    eighth = half // 4
    loads = [
        pltpu.make_async_copy(ref, attn_w.at[i], a_sem.at[i]) for i, ref in enumerate((query_any, key_any, value_any))
    ]
    for load in loads:
        load.start()
    greet(g, r, core, x, False)

    def along(source, away, sem):
        return send(lined.at[source], lined.at[source], sem, z_recv.at[source], g=g + away)

    lined[g] = tokens_ref[...]
    pl.when(g > 0)(lambda: along(g, -1, z_own.at[0]).start())
    pl.when(g < GROUPS - 1)(lambda: along(g, 1, z_own.at[1]).start())

    for load in loads:
        load.wait()
    prepare(g, x, attn_w, (l0, l1, l2, l3, l4, l5, l6, l7, l8), narrow_ref, small_ref)
    small_move = send(small_ref, small_in, s_sem.at[0], s_sem.at[1], x=other)
    small_move.start()
    mine = pl.ds(x * half + core * fourth, fourth)
    narrow_x = send(narrow_ref.at[pl.ds(core * fourth, fourth)], wfull.at[mine], n_send.at[0], n_recv.at[0], x=other)
    narrow_x.start()

    def wo_rows(owner, part):
        return wo_out.at[pl.ds(owner * half + core * fourth + part * eighth, eighth)]

    def up_rows(owner, part):
        return up_out.at[pl.ds(owner * half + part * fourth, fourth)]

    def up_columns(owner):
        return pl.ds(pl.multiple_of((2 * owner + core) * width, width), width)

    wo_x = send(wo_ref.at[pl.ds(core * fourth + r * eighth, eighth)], wo_rows(x, r), w_send.at[0], w_recv.at[0], x=other)
    up_x = send(
        up_ref.at[pl.ds(r * fourth, fourth), up_columns(other)], up_rows(x, r), w_send.at[1], w_recv.at[1], x=other
    )
    wo_y = send(wo_rows(other, r), wo_rows(other, r), w_send.at[3], w_recv.at[3], r=1 - r)
    up_y = send(up_rows(other, r), up_rows(other, r), w_send.at[4], w_recv.at[4], r=1 - r)
    wo_s = [
        send(wo_rows(other, part), wo_rows(other, part), w_send.at[6 + i], w_recv.at[6 + i], core=1 - core)
        for i, part in enumerate((r, 1 - r))
    ]
    wo_x.start()
    locals_ = [
        pltpu.make_async_copy(wo_ref, wo_out.at[pl.ds(x * half, half)], w_local.at[0]),
        pltpu.make_async_copy(up_ref.at[:, up_columns(x)], up_out.at[pl.ds(x * half, half)], w_local.at[1]),
    ]
    for item in locals_:
        item.start()

    wfull[pl.ds(x * half, half)] = narrow_ref[...]
    narrow_x.wait_recv()
    theirs = wfull.at[pl.ds(other * half + core * fourth, fourth)]
    narrow_s = send(theirs, theirs, n_send.at[1], n_recv.at[1], core=1 - core)
    narrow_s.start()
    small_move.wait_recv()
    small_out[...] = small_ref[...] + small_in[...]
    narrow_s.wait_recv()

    own = seat(r, core, x)

    def block(owner, source):
        return kv_ref.at[owner, source]

    def push(step, kind, what, **device):
        copy = send(what[0], what[1], kv_send.at[kind, step], kv_recv.at[kind, step], **device)
        copy.start()

    def settle(step, kind, owner, source):
        send(block(owner, source), block(owner, source), kv_send.at[kind, step], kv_recv.at[kind, step], x=other).wait_recv()

    def forward(step):
        source = nearest(g, step)
        by_x = block(seat(r, core, other), source)
        settle(step, 0, seat(r, core, other), source)
        if step % 2 == 0:
            push(step, 3, (by_x, by_x), r=1 - r)
        push(step, 4, (by_x, by_x), core=1 - core)
        by_y = block(seat(1 - r, core, x), source)
        settle(step, 1, seat(1 - r, core, x), source)
        if step % 2 == 1:
            push(step, 3, (by_y, by_y), x=other)
        push(step, 5, (by_y, by_y), core=1 - core)

    def forward_far(step):
        source = nearest(g, step)
        far = block(seat(1 - r, core, other), source)
        settle(step, 3, seat(1 - r, core, other), source)
        push(step, 6, (far, far), core=1 - core)

    for step in range(GROUPS):
        source = nearest(g, step)
        if step > 0:
            send(lined.at[source], lined.at[source], z_send.at[source], z_recv.at[source], x=other).wait_recv()
            pl.when((source < g) & (g < GROUPS - 1))(lambda: along(source, 1, z_send.at[source]).start())
            pl.when((source > g) & (g > 0))(lambda: along(source, -1, z_send.at[source]).start())
        values = lined[source].astype(f32)
        normed = layer_norm(values, small_out[0:1], small_out[1:2]).astype(bf16)
        normed_ref[source] = normed
        both = dot(normed, wfull[...]) + small_out[12:13, : wfull.shape[1]]
        q_ref[source] = (both[:, : 2 * BLK] * SCALE).astype(bf16)
        kvs[step] = both[:, 2 * BLK :].astype(bf16)
        here = (kvs.at[step], block(own, source))
        push(step, 0, here, x=other)
        push(step, 1, here, r=1 - r)
        push(step, 2, here, core=1 - core)
        pltpu.make_async_copy(kvs.at[step], block(own, source), kv_local.at[step]).start()
        if step == 0:
            up_x.start()
        if step > 0:
            forward(step - 1)
        if step > 1:
            forward_far(step - 2)
    wo_x.wait_recv()
    wo_y.start()
    wo_s[0].start()
    forward(GROUPS - 1)
    forward_far(GROUPS - 2)
    up_x.wait_recv()
    up_y.start()
    send(wo_rows(other, 1 - r), wo_rows(other, 1 - r), w_send.at[3], w_recv.at[3], r=1 - r).wait_recv()
    wo_s[1].start()
    forward_far(GROUPS - 1)

    for step in range(GROUPS):
        source = nearest(g, step)
        pltpu.make_async_copy(kvs.at[step], block(own, source), kv_local.at[step]).wait()
        settle(step, 2, seat(r, 1 - core, x), source)
        settle(step, 4, seat(r, 1 - core, other), source)
        settle(step, 5, seat(1 - r, 1 - core, x), source)
        settle(step, 6, seat(1 - r, 1 - core, other), source)
        for kind in range(7):
            send(kvs.at[step], block(own, source), kv_send.at[kind, step], kv_recv.at[kind, step], x=other).wait_send()
    pl.when(g > 0)(lambda: along(g, -1, z_own.at[0]).wait_send())
    pl.when(g < GROUPS - 1)(lambda: along(g, 1, z_own.at[1]).wait_send())
    for step in range(1, GROUPS):
        source = nearest(g, step)
        passed = ((source < g) & (g < GROUPS - 1)) | ((source > g) & (g > 0))
        pl.when(passed)(lambda: send(lined.at[source], lined.at[source], z_send.at[source], z_recv.at[source], x=other).wait_send())
    small_move.wait_send()
    narrow_x.wait_send()
    narrow_s.wait_send()
    for item in locals_:
        item.wait()
    for item in (wo_x, up_x, wo_y, up_y, *wo_s):
        item.wait_send()
    send(up_rows(other, 1 - r), up_rows(other, 1 - r), w_send.at[4], w_recv.at[4], r=1 - r).wait_recv()
    for i, part in enumerate((r, 1 - r)):
        there = wo_out.at[pl.ds(other * half + (1 - core) * fourth + part * eighth, eighth)]
        send(there, there, w_send.at[6 + i], w_recv.at[6 + i], core=1 - core).wait_recv()


def anywhere():
    return pl.BlockSpec(memory_space=pl.ANY)


def in_hbm():
    return pl.BlockSpec(memory_space=pltpu.HBM)


def gather(tokens, query, key, value, up, wo, *lines):
    rows, width = tokens.shape
    wide = 2 * BLK + 2 * HW
    small = (16, width)
    dma = pltpu.SemaphoreType.DMA
    return pl.pallas_call(
        gather_kernel,
        out_shape=(
            jax.ShapeDtypeStruct((8, GROUPS, rows, 2 * HW), bf16),
            jax.ShapeDtypeStruct((GROUPS, rows, 2 * BLK), bf16),
            jax.ShapeDtypeStruct((GROUPS, rows, width), bf16),
            jax.ShapeDtypeStruct(small, f32),
            jax.ShapeDtypeStruct((width, wide), bf16),
            jax.ShapeDtypeStruct((width, width), bf16),
            jax.ShapeDtypeStruct((width, width), bf16),
        ),
        in_specs=[whole_vmem(), *[in_hbm()] * 5, *[whole_vmem()] * len(lines)],
        out_specs=(anywhere(), *(whole_vmem(),) * 4, anywhere(), anywhere()),
        scratch_shapes=[
            pltpu.VMEM((GROUPS, rows, width), bf16),
            pltpu.VMEM((3, width // 2, width), bf16),
            pltpu.VMEM((width // 2, wide), bf16),
            pltpu.VMEM(small, f32),
            pltpu.VMEM(small, f32),
            pltpu.VMEM((GROUPS, rows, 2 * HW), bf16),
            dma((2,)), dma((GROUPS,)), dma((GROUPS,)), dma((2,)), dma((2,)), dma((2,)),
            dma((7, GROUPS)), dma((7, GROUPS)), dma((GROUPS,)), dma((8,)), dma((8,)), dma((2,)), dma((3,)),
        ],
        compiler_params=pltpu.CompilerParams(
            collective_id=0, has_side_effects=True, vmem_limit_bytes=60 << 20
        ),
        name="gather",
    )(tokens, query, key, value, up, wo, *lines)


def erf_parts(values):
    below = 0.5 * (1.0 + lax.erf(values * ROOT_HALF))
    return below, PDF_SCALE * jnp.exp(-0.5 * values * values)


PARTS = 8
UNIT = 216


def dense_kernel(
    out_t_ref, tokens_ref, cot_ref, small_ref, up_ref, wo_ref, down_any,
    result_ref, middle_grad_ref, grad_t_ref, keep_ref, give_ref, sums_ref,
    down_ref, attn_in, attn_t, cots, h2s, mid_ref, n2_ref, part_y, part_d, in_y, in_d, pass_y, pass_d, x_y, x_d,
    hids, dus, grad_out, wo_keep, wo_give, wo_in, wo_pass, wo_x,
    down_sem, a_send, a_recv, c_send, c_recv, h_send, h_recv, y_send, y_recv, d_send, d_recv, o_send, o_recv,
    w_send, w_recv,
):
    g, r, core, x = place()
    other = 1 - x
    rows, width = tokens_ref.shape
    half = width // 2
    fourth = half // 2
    load = pltpu.make_async_copy(
        down_any.at[pl.ds(pl.multiple_of(core * width, width), width)], down_ref, down_sem
    )
    load.start()
    greet(g, r, core, x, True)
    cots[0] = cot_ref[...]

    def share(rows_ref, out_sem, in_sem):
        moves = (
            send(rows_ref.at[0], rows_ref.at[2], out_sem.at[1], in_sem.at[1], x=other),
            send(rows_ref.at[0], rows_ref.at[1], out_sem.at[0], in_sem.at[0], core=1 - core),
        )
        for move in moves:
            move.start()
        return moves

    def pass_on(rows_ref, moves, out_sem, in_sem):
        moves[0].wait_recv()
        move = send(rows_ref.at[2], rows_ref.at[3], out_sem.at[2], in_sem.at[2], core=1 - core)
        move.start()
        return move

    def other_group(away):
        return lax.rem(g + away, GROUPS)

    attn_moves = []
    for away in range(1, GROUPS):
        to = other_group(away)
        attn_moves.append(
            send(out_t_ref.at[pl.ds(2 * to, 2)], attn_in.at[g], a_send.at[away], a_recv.at[g], g=to)
        )
        attn_moves[-1].start()
    cot_moves = share(cots, c_send, c_recv)
    attn_in[g] = out_t_ref[pl.ds(2 * g, 2)]
    sums_ref[...] = jnp.zeros_like(sums_ref)
    sums_ref[5:6] = jnp.sum(cot_ref[...].astype(f32), axis=0, keepdims=True)
    for away in range(1, GROUPS):
        source = other_group(away)
        send(attn_in.at[source], attn_in.at[source], a_send.at[away], a_recv.at[source], g=source).wait_recv()
    for source in range(GROUPS):
        attn_t[HW * source : HW * source + HW] = jnp.concatenate(
            [attn_in[source, 0], attn_in[source, 1]], axis=1
        )
    middle = tokens_ref[...].astype(f32) + outer(attn_t[...], wo_ref[...]) + small_ref[2:3]
    mid_ref[...] = middle
    mean = jnp.mean(middle, axis=-1, keepdims=True)
    centred = middle - mean
    spread = jnp.mean(centred * centred, axis=-1, keepdims=True)
    scale = lax.rsqrt(spread + EPS)
    n2_ref[...] = centred * scale
    h2s[0] = (n2_ref[...] * small_ref[3:4] + small_ref[4:5]).astype(bf16)
    h2_moves = share(h2s, h_send, h_recv)
    cot_pass = pass_on(cots, cot_moves, c_send, c_recv)
    load.wait()
    bias_row = 8 + 2 * x + core
    bias = small_ref[pl.ds(bias_row, 1)]
    sums_ref[pl.ds(bias_row, 1)] = jnp.zeros((1, width), f32)

    def one_part(part):
        expanded = dot(h2s[part], up_ref[...]) + bias
        below, density = erf_parts(expanded)
        hidden = (expanded * below).astype(bf16)
        hids[part] = hidden
        slope = below + expanded * density
        grad_hidden = inner(cots[part], down_ref[...]).astype(bf16).astype(f32)
        grad_expand = (grad_hidden * slope).astype(bf16)
        dus[part] = grad_expand
        part_d[part] = inner(grad_expand, up_ref[...])
        part_y[part] = dot(hidden, down_ref[...])
        sums_ref[pl.ds(bias_row, 1)] += jnp.sum(grad_expand.astype(f32), axis=0, keepdims=True)

    one_part(0)
    cot_moves[1].wait_recv()
    h2_moves[1].wait_recv()
    h2_pass = pass_on(h2s, h2_moves, h_send, h_recv)
    one_part(1)
    d_sib = send(part_d.at[1], in_d, d_send.at[0], d_recv.at[0], core=1 - core)
    d_sib.start()
    cot_pass.wait_recv()
    h2_pass.wait_recv()
    one_part(3)
    x_d[0] = part_d[3].astype(bf16)
    x_y[0] = part_y[3].astype(bf16)
    d_pass = send(x_d.at[0], pass_d, d_send.at[1], d_recv.at[1], core=1 - core)
    y_pass = send(x_y.at[0], pass_y, y_send.at[1], y_recv.at[1], core=1 - core)
    d_pass.start()
    y_pass.start()
    one_part(2)
    d_pass.wait_recv()
    x_d[1] = (part_d[2] + pass_d[...].astype(f32)).astype(bf16)
    d_x = send(x_d.at[1], x_d.at[2], d_send.at[2], d_recv.at[2], x=other)
    d_x.start()
    y_pass.wait_recv()
    x_y[1] = (part_y[2] + pass_y[...].astype(f32)).astype(bf16)
    y_x = send(x_y.at[1], x_y.at[2], y_send.at[2], y_recv.at[2], x=other)
    y_x.start()
    y_sib = send(part_y.at[1], in_y, y_send.at[0], y_recv.at[0], core=1 - core)
    y_sib.start()

    def over_rows(left, right):
        total = outer(left[0], right[0])
        for part in range(1, 4):
            total += outer(left[part], right[part])
        return total.astype(bf16)

    down_grad = over_rows(hids, cots)
    up_grad = over_rows(h2s, dus)

    def parts(write):
        for y in range(2):
            pl.when(r == y)(lambda: write(keep_ref, y))
            pl.when(r != y)(lambda: write(give_ref, y))

    def write_dense(ref, y):
        for z in range(GROUPS):
            p = y * GROUPS + z
            ref[z, 0:96] = down_grad[96 * p : 96 * p + 96]
            ref[z, 96:144] = up_grad[48 * p : 48 * p + 48]
            ref[z, 144:192] = up_grad[half + 48 * p : half + 48 * p + 48]

    parts(write_dense)

    d_sib.wait_recv()
    d_x.wait_recv()
    grad_second = part_d[0] + in_d[...] + x_d[2].astype(f32)
    n2 = n2_ref[...]
    sums_ref[3:4] = jnp.sum(grad_second * n2, axis=0, keepdims=True)
    sums_ref[4:5] = jnp.sum(grad_second, axis=0, keepdims=True)
    pulled = grad_second * small_ref[3:4]
    inward = pulled - jnp.mean(pulled, axis=-1, keepdims=True) - n2 * jnp.mean(pulled * n2, axis=-1, keepdims=True)
    grad_middle = cot_ref[...].astype(f32) + inward * scale
    middle_grad_ref[...] = grad_middle
    branch = grad_middle.astype(bf16)
    sums_ref[2:3] = jnp.sum(branch.astype(f32), axis=0, keepdims=True)
    grad_out_t = inner(wo_ref[...], branch).astype(bf16)
    for group in range(GROUPS):
        for b in range(2):
            grad_out[group, b] = grad_out_t[HW * group : HW * group + HW, BLK * b : BLK * b + BLK]
    grad_moves = []
    for away in range(1, GROUPS):
        to = other_group(away)
        grad_moves.append(
            send(grad_out.at[to], grad_t_ref.at[pl.ds(2 * g, 2)], o_send.at[away], o_recv.at[g], g=to)
        )
        grad_moves[-1].start()
    grad_t_ref[pl.ds(2 * g, 2)] = grad_out[g]

    for owner in range(2):
        for c in range(2):
            piece = dot(attn_t[half * owner + fourth * c : half * owner + fourth * c + fourth], branch)

            @pl.when(core == c)
            def _():
                wo_keep[owner] = piece

            @pl.when(core != c)
            def _():
                wo_give[owner] = piece.astype(bf16)

    w_sib = send(wo_give, wo_in, w_send.at[0], w_recv.at[0], core=1 - core)
    w_sib.start()
    y_x.wait_recv()
    y_sib.wait_recv()
    result_ref[...] = (
        mid_ref[...] + part_y[0] + in_y[...] + x_y[2].astype(f32) + small_ref[5:6]
    ).astype(bf16)
    w_sib.wait_recv()
    wo_pass[...] = (wo_keep[other] + wo_in[other].astype(f32)).astype(bf16)
    w_x = send(wo_pass, wo_x, w_send.at[1], w_recv.at[1], x=other)
    w_x.start()
    mine = wo_keep[x] + wo_in[x].astype(f32)
    w_x.wait_recv()
    wo_sum = (mine + wo_x[...].astype(f32)).astype(bf16)

    def write_wo(ref, y):
        for z in range(GROUPS):
            p = y * GROUPS + z
            ref[z, 192:UNIT] = wo_sum[24 * p : 24 * p + 24]

    parts(write_wo)
    for away in range(1, GROUPS):
        source = other_group(away)
        send(
            grad_t_ref.at[pl.ds(2 * source, 2)], grad_t_ref.at[pl.ds(2 * source, 2)],
            o_send.at[away], o_recv.at[source], g=source,
        ).wait_recv()
    for item in (
        *cot_moves, cot_pass, *h2_moves, h2_pass, d_sib, d_pass, d_x, y_sib, y_pass, y_x, w_sib, w_x, *attn_moves, *grad_moves,
    ):
        item.wait_send()


def dense(out_t, tokens, cot, small, up, wo, down):
    rows, width = tokens.shape
    dma = pltpu.SemaphoreType.DMA
    full = (rows, width)
    fourth = (width // 4, width)
    return pl.pallas_call(
        dense_kernel,
        out_shape=(
            jax.ShapeDtypeStruct(full, bf16),
            jax.ShapeDtypeStruct(full, f32),
            jax.ShapeDtypeStruct(out_t.shape, bf16),
            jax.ShapeDtypeStruct((GROUPS, UNIT, width), bf16),
            jax.ShapeDtypeStruct((GROUPS, UNIT, width), bf16),
            jax.ShapeDtypeStruct(small.shape, f32),
        ),
        in_specs=[whole_vmem()] * 6 + [in_hbm()],
        out_specs=(whole_vmem(),) * 6,
        scratch_shapes=[
            pltpu.VMEM((width, width), bf16),
            pltpu.VMEM((GROUPS, 2, HW, BLK), bf16),
            pltpu.VMEM((width, rows), bf16),
            pltpu.VMEM((4, *full), bf16),
            pltpu.VMEM((4, *full), bf16),
            pltpu.VMEM(full, f32),
            pltpu.VMEM(full, f32),
            pltpu.VMEM((4, *full), f32),
            pltpu.VMEM((4, *full), f32),
            pltpu.VMEM(full, f32),
            pltpu.VMEM(full, f32),
            pltpu.VMEM(full, bf16),
            pltpu.VMEM(full, bf16),
            pltpu.VMEM((3, *full), bf16),
            pltpu.VMEM((3, *full), bf16),
            pltpu.VMEM((4, *full), bf16),
            pltpu.VMEM((4, *full), bf16),
            pltpu.VMEM((GROUPS, 2, HW, BLK), bf16),
            pltpu.VMEM((2, *fourth), f32),
            pltpu.VMEM((2, *fourth), bf16),
            pltpu.VMEM((2, *fourth), bf16),
            pltpu.VMEM(fourth, bf16),
            pltpu.VMEM(fourth, bf16),
            dma(()), dma((GROUPS,)), dma((GROUPS,)), dma((3,)), dma((3,)), dma((3,)), dma((3,)),
            dma((3,)), dma((3,)), dma((3,)), dma((3,)), dma((GROUPS,)), dma((GROUPS,)), dma((2,)), dma((2,)),
        ],
        compiler_params=pltpu.CompilerParams(
            collective_id=1, has_side_effects=True, vmem_limit_bytes=40 << 20
        ),
        name="dense",
    )(out_t, tokens, cot, small, up, wo, down)


FARTHEST = ((3, 2, 1, 0), (3, 0, 2, 1), (0, 3, 1, 2), (0, 1, 2, 3))


def farthest(g, step):
    picked = FARTHEST[0][step]
    for z in range(1, GROUPS):
        picked = jnp.where(g == z, FARTHEST[z][step], picked)
    return picked


class Chain:
    def __init__(self, g, x, total, parts, inward, outward, out_sem, in_sem):
        self.g, self.x, self.total, self.parts = g, x, total, parts
        self.inward, self.outward, self.out_sem, self.in_sem = inward, outward, out_sem, in_sem

    def move(self, to, way):
        return send(
            self.outward.at[to], self.inward.at[way, to], self.out_sem.at[to], self.in_sem.at[way, to],
            g=jnp.clip(self.g + (1 if way == 0 else -1), 0, GROUPS - 1),
        )

    def step(self, to):
        g = self.g
        self.total[...] = self.parts[to].astype(f32)

        def take(way):
            arrived(self.inward.at[way, to], self.out_sem.at[to], self.in_sem.at[way, to], self.x)
            self.total[...] += self.inward[way, to].astype(f32)

        pl.when((to >= g) & (g > 0))(lambda: take(0))
        pl.when((to <= g) & (g < GROUPS - 1))(lambda: take(1))

        @pl.when(to != g)
        def _():
            self.outward[to] = self.total[...].astype(bf16)

        pl.when(to > g)(lambda: self.move(to, 0).start())
        pl.when(to < g)(lambda: self.move(to, 1).start())

    def finish(self):
        for step in range(GROUPS - 1):
            to = farthest(self.g, step)
            left(self.outward.at[to], self.out_sem.at[to], self.in_sem.at[0, to], self.x)


class Ring:
    def __init__(self, g, x, slot, own_sem, out_sem, in_sem):
        self.g, self.x, self.slot = g, x, slot
        self.own_sem, self.out_sem, self.in_sem = own_sem, out_sem, in_sem

    def move(self, source, way, sem):
        return send(
            self.slot(source), self.slot(source), sem, self.in_sem.at[source],
            g=jnp.clip(self.g + way, 0, GROUPS - 1),
        )

    def start(self):
        g = self.g
        pl.when(g > 0)(lambda: self.move(g, -1, self.own_sem.at[0]).start())
        pl.when(g < GROUPS - 1)(lambda: self.move(g, 1, self.own_sem.at[1]).start())

    def step(self, step):
        g, source = self.g, nearest(self.g, step)
        arrived(self.slot(source), self.out_sem.at[source], self.in_sem.at[source], self.x)
        pl.when((source < g) & (g < GROUPS - 1))(lambda: self.move(source, 1, self.out_sem.at[source]).start())
        pl.when((source > g) & (g > 0))(lambda: self.move(source, -1, self.out_sem.at[source]).start())
        return source

    def finish(self):
        g = self.g
        for i, there in enumerate((g > 0, g < GROUPS - 1)):
            pl.when(there)(lambda: left(self.slot(g), self.own_sem.at[i], self.in_sem.at[g], self.x))
        for step in range(1, GROUPS):
            source = nearest(g, step)
            passed = ((source < g) & (g < GROUPS - 1)) | ((source > g) & (g > 0))
            pl.when(passed)(
                lambda: left(self.slot(source), self.out_sem.at[source], self.in_sem.at[source], self.x)
            )


def arrived(what, out_sem, in_sem, x):
    send(what, what, out_sem, in_sem, x=1 - x).wait_recv()


def left(what, out_sem, in_sem, x):
    send(what, what, out_sem, in_sem, x=1 - x).wait_send()


def scatter_kernel(
    dkv_ref, dq_ref, normed_ref, wfull_ref, tokens_ref, mgrad_ref, small_ref, bundle_ref, by_in, sums_in,
    tokens_grad_ref, big_ref, qout_ref, kvout_ref, sums_ref,
    own_kv, sib_kv, keep_x, give_x, in_x, give_y, in_y, part_a, total_a, inward_a, outward_a, wg_kv,
    by_sum, total_b, inward_b, outward_b, unit,
    q_keep, q_give, q_in, q_pass, q_x, q_y, q_sum, v_keep, v_give, v_in, v_pass, v_x, v_y, v_sum,
    sums_got,
    own_sem, k_send, k_recv, x_send, x_recv, y_send, y_recv, ca_send, ca_recv,
    cb_send, cb_recv, u_send, u_recv, rb_own, rb_send, rb_recv,
    fy_send, fy_recv, fs_send, fs_recv,
    q_send, q_recv, rq_own, rq_send, rq_recv, qs_send, qs_recv,
    v_send, v_recv, rv_own, rv_send, rv_recv, vs_send, vs_recv,
    s_send, s_recv, l_sem,
):
    g, r, core, x = place()
    other, sib, far_r = 1 - x, 1 - core, 1 - r
    rows, width = tokens_ref.shape
    half = width // 2
    fourth = half // 2
    wide_q = 2 * BLK
    greet(g, r, core, x, True)
    pending = []

    def begin(src, dst, out_sem, in_sem, **device):
        move = send(src, dst, out_sem, in_sem, **device)
        move.start()
        pending.append(move)
        return move

    def settled(move):
        move.wait_recv()
        move.wait_send()
        pending[:] = [item for item in pending if item is not move]

    kv_moves = []
    for i in range(GROUPS):
        c = farthest(g, i)
        for spot in range(4):
            own = pltpu.make_async_copy(dkv_ref.at[seat(spot // 2, core, spot % 2), c], own_kv.at[i, spot], own_sem.at[i, spot])
            own.start()
            across = begin(
                dkv_ref.at[seat(spot // 2, sib, spot % 2), c], sib_kv.at[i, spot],
                k_send.at[i, spot], k_recv.at[i, spot], core=sib,
            )
            kv_moves.append((own, across))

    def split(total, keep, give, wide):
        for owner in range(2):
            for c in range(2):
                low = half * owner + fourth * c
                chunk = total[low : low + fourth]

                @pl.when(core == c)
                def _():
                    keep[owner] = chunk

                @pl.when(core != c)
                def _():
                    give[owner] = chunk.astype(bf16)

    def scaled(c):
        return dq_ref[c] * bf16(SCALE)

    def query_grad():
        query_total = outer(normed_ref[0], scaled(0))
        for c in range(1, GROUPS):
            query_total += outer(normed_ref[c], scaled(c))
        split(query_total, q_keep, q_give, wide_q)
        q_move.start()

    q_move = send(q_give, q_in, q_send.at[0], q_recv.at[0], core=sib)
    sums_ref[...] = jnp.zeros_like(sums_ref)
    sums_ref[0:16] = sums_in[...]
    line_q = scaled(0).astype(f32)
    for c in range(1, GROUPS):
        line_q += scaled(c).astype(f32)
    sums_ref[pl.ds(16 + g, 1), 0:wide_q] = jnp.sum(line_q, axis=0, keepdims=True)
    wg_kv[...] = jnp.zeros_like(wg_kv)

    def q_slot(z):
        return qout_ref.at[core, z]

    def v_slot(z):
        return kvout_ref.at[core, z]

    def b_slot(z):
        return big_ref.at[core, r, z]

    ring_q = Ring(g, x, q_slot, rq_own, rq_send, rq_recv)
    ring_v = Ring(g, x, v_slot, rv_own, rv_send, rv_recv)
    ring_b = Ring(g, x, b_slot, rb_own, rb_send, rb_recv)

    def store(value_ref, slot, sem):
        copy = pltpu.make_async_copy(value_ref, slot, sem)
        copy.start()
        copy.wait()

    def spread_b(z, step):
        begin(b_slot(z), b_slot(z), fy_send.at[step], fy_recv.at[step], r=far_r)
        begin(b_slot(z), b_slot(z), fs_send.at[0, step], fs_recv.at[0, step], core=sib)

    def spread_far(z, step):
        what = big_ref.at[core, far_r, z]
        arrived(what, fy_send.at[step], fy_recv.at[step], x)
        begin(what, what, fs_send.at[1, step], fs_recv.at[1, step], core=sib)

    chain_a = Chain(g, x, total_a, part_a, inward_a, outward_a, ca_send, ca_recv)
    chain_b = Chain(g, x, total_b, by_sum, inward_b, outward_b, cb_send, cb_recv)
    at_end = (g == 0) | (g == GROUPS - 1)
    between = jnp.logical_not(at_end)

    def steps(chain, *which):
        for i in which:
            chain.step(farthest(g, i))

    def on_sibling(i):
        for own, across in kv_moves[4 * i : 4 * i + 4]:
            own.wait()
            across.wait_recv()

        def total(row, column):
            spot = 2 * row + column
            return own_kv[i, spot].astype(f32) + sib_kv[i, spot].astype(f32)

        for k in range(2):
            give_x[i, k] = (total(k, other) if i % 2 == 0 else total(far_r, k)).astype(bf16)
            keep_x[i, k] = total(k, x) if i % 2 == 0 else total(r, k)

    def go_first(i):
        along = {"x": other} if i % 2 == 0 else {"r": far_r}
        begin(give_x.at[i], in_x.at[i], x_send.at[i], x_recv.at[i], **along)

    def on_first(i):
        arrived(in_x.at[i], x_send.at[i], x_recv.at[i], x)
        away, stay, along = (far_r, r, {"r": far_r}) if i % 2 == 0 else (other, x, {"x": other})
        give_y[i] = (keep_x[i, away] + in_x[i, away].astype(f32)).astype(bf16)
        begin(give_y.at[i], in_y.at[i], y_send.at[i], y_recv.at[i], **along)
        keep_x[i, stay] += in_x[i, stay].astype(f32)

    def on_second(i):
        c = farthest(g, i)
        arrived(in_y.at[i], y_send.at[i], y_recv.at[i], x)
        both = (keep_x[i, r if i % 2 == 0 else x] + in_y[i].astype(f32)).astype(bf16)
        part_a[c] = inner(scaled(c), wfull_ref[:, :wide_q]) + inner(both, wfull_ref[:, wide_q:])
        wg_kv[...] += outer(normed_ref[c], both)
        sums_ref[pl.ds(16 + g, 1), wide_q : wide_q + 2 * HW] += jnp.sum(both.astype(f32), axis=0, keepdims=True)

    by_sum[...] = bundle_ref[...].astype(f32) + by_in[...].astype(f32)
    on_sibling(0)
    go_first(0)
    on_sibling(1)
    go_first(1)
    pl.when(at_end)(lambda: steps(chain_b, 0, 1, 2))
    on_sibling(2)
    on_sibling(3)
    query_grad()
    pl.when(between)(lambda: steps(chain_b, 0))
    on_first(0)
    on_first(1)
    go_first(2)
    go_first(3)
    settled(q_move)
    q_pass[...] = (q_keep[other] + q_in[other].astype(f32)).astype(bf16)
    q_across = begin(q_pass, q_x, q_send.at[1], q_recv.at[1], x=other)
    on_second(0)
    on_second(1)
    pl.when(at_end)(lambda: steps(chain_a, 0, 1))
    pl.when(between)(lambda: steps(chain_b, 1, 2))
    on_first(2)
    on_first(3)
    chain_b.step(g)
    unit[...] = total_b[...].astype(bf16)
    up_rows = 96 + 48 * other
    begin(unit.at[pl.ds(up_rows, 48)], big_ref.at[core, r, g, pl.ds(96 + 48 * x, 48)], u_send.at[0], u_recv.at[0], x=other)
    copies = [
        pltpu.make_async_copy(unit.at[pl.ds(0, 96)], big_ref.at[core, r, g, pl.ds(0, 96)], l_sem.at[1]),
        pltpu.make_async_copy(
            unit.at[pl.ds(96 + 48 * x, 48)], big_ref.at[core, r, g, pl.ds(96 + 48 * x, 48)], l_sem.at[2]
        ),
        pltpu.make_async_copy(unit.at[pl.ds(192, 24)], big_ref.at[core, r, g, pl.ds(192, 24)], l_sem.at[3]),
    ]
    for copy in copies:
        copy.start()
    q_across.wait_recv()
    q_sum[...] = (q_keep[x] + q_in[x].astype(f32) + q_x[...].astype(f32)).astype(bf16)
    q_over = begin(q_sum, q_y, q_send.at[2], q_recv.at[2], r=far_r)
    on_second(2)
    on_second(3)
    pl.when(at_end)(lambda: steps(chain_a, 2))
    split(wg_kv, v_keep, v_give, 2 * HW)
    v_move = begin(v_give, v_in, v_send.at[0], v_recv.at[0], core=sib)
    for copy in copies:
        copy.wait()
    arrived(big_ref.at[core, r, g, pl.ds(up_rows, 48)], u_send.at[0], u_recv.at[0], x)
    ring_b.start()
    spread_b(g, 0)
    v_move.wait_recv()
    v_pass[...] = (v_keep[other] + v_in[other].astype(f32)).astype(bf16)
    v_across = begin(v_pass, v_x, v_send.at[1], v_recv.at[1], x=other)
    pl.when(between)(lambda: steps(chain_a, 0))
    settled(q_over)
    q_sum[...] = (q_sum[...].astype(f32) + q_y[...].astype(f32)).astype(bf16)
    store(q_sum, q_slot(g), l_sem.at[0])
    ring_q.start()
    begin(q_slot(g), q_slot(g), qs_send.at[0], qs_recv.at[0], core=sib)
    v_across.wait_recv()
    v_sum[...] = (v_keep[x] + v_in[x].astype(f32) + v_x[...].astype(f32)).astype(bf16)
    v_over = begin(v_sum, v_y, v_send.at[2], v_recv.at[2], r=far_r)
    spread_far(g, 0)
    pl.when(between)(lambda: steps(chain_a, 1, 2))
    settled(v_over)
    v_sum[...] = (v_sum[...].astype(f32) + v_y[...].astype(f32)).astype(bf16)
    store(v_sum, v_slot(g), l_sem.at[0])
    ring_v.start()
    begin(v_slot(g), v_slot(g), vs_send.at[0], vs_recv.at[0], core=sib)
    spread_b(ring_b.step(1), 1)
    z = ring_q.step(1)
    begin(q_slot(z), q_slot(z), qs_send.at[1], qs_recv.at[1], core=sib)
    z = ring_v.step(1)
    begin(v_slot(z), v_slot(z), vs_send.at[1], vs_recv.at[1], core=sib)
    chain_a.step(g)

    grad_first = total_a[...]
    values = tokens_ref[...].astype(f32)
    mean = jnp.mean(values, axis=-1, keepdims=True)
    centred = values - mean
    scale = lax.rsqrt(jnp.mean(centred * centred, axis=-1, keepdims=True) + EPS)
    n1 = centred * scale
    pulled = grad_first * small_ref[0:1]
    inward = pulled - jnp.mean(pulled, axis=-1, keepdims=True) - n1 * jnp.mean(pulled * n1, axis=-1, keepdims=True)
    tokens_grad_ref[...] = mgrad_ref[...] + inward * scale
    sums_ref[0:1] = jnp.sum(grad_first * n1, axis=0, keepdims=True)
    sums_ref[1:2] = jnp.sum(grad_first, axis=0, keepdims=True)
    s_sib = begin(sums_ref, sums_got.at[0], s_send.at[0], s_recv.at[0], core=sib)

    settled(s_sib)
    sums_ref[...] += sums_got[0]
    s_x = begin(sums_ref, sums_got.at[1], s_send.at[1], s_recv.at[1], x=other)
    spread_b(ring_b.step(2), 2)
    spread_far(nearest(g, 1), 1)
    settled(s_x)
    sums_ref[...] += sums_got[1]
    s_y = begin(sums_ref, sums_got.at[2], s_send.at[2], s_recv.at[2], r=far_r)
    z = ring_q.step(2)
    begin(q_slot(z), q_slot(z), qs_send.at[2], qs_recv.at[2], core=sib)
    z = ring_v.step(2)
    begin(v_slot(z), v_slot(z), vs_send.at[2], vs_recv.at[2], core=sib)
    settled(s_y)
    sums_ref[...] += sums_got[2]
    for away in range(1, GROUPS):
        begin(
            sums_ref, sums_got.at[2 + away], s_send.at[2 + away], s_recv.at[2 + away],
            g=lax.rem(g + away, GROUPS),
        )
    spread_b(ring_b.step(3), 3)
    spread_far(nearest(g, 2), 2)
    z = ring_q.step(3)
    begin(q_slot(z), q_slot(z), qs_send.at[3], qs_recv.at[3], core=sib)
    z = ring_v.step(3)
    begin(v_slot(z), v_slot(z), vs_send.at[3], vs_recv.at[3], core=sib)
    spread_far(nearest(g, 3), 3)

    for away in range(1, GROUPS):
        arrived(sums_got.at[2 + away], s_send.at[2 + away], s_recv.at[2 + away], x)
    for step in range(GROUPS):
        z = nearest(g, step)
        arrived(qout_ref.at[sib, z], qs_send.at[step], qs_recv.at[step], x)
        arrived(kvout_ref.at[sib, z], vs_send.at[step], vs_recv.at[step], x)
        arrived(big_ref.at[sib, r, z], fs_send.at[0, step], fs_recv.at[0, step], x)
        arrived(big_ref.at[sib, far_r, z], fs_send.at[1, step], fs_recv.at[1, step], x)
    for move in pending:
        move.wait_send()
    for item in (chain_a, chain_b, ring_q, ring_v, ring_b):
        item.finish()
    sums_ref[...] += sums_got[3] + sums_got[4] + sums_got[5]


def scatter(dkv, dq, normed, wfull, tokens, mgrad, small, bundle, over, sums):
    rows, width = tokens.shape
    fourth = width // 4
    dma = pltpu.SemaphoreType.DMA
    wide_q, wide_v = 2 * BLK, 2 * HW
    kv_block = (rows, wide_v)
    full = (rows, width)
    unit = (UNIT, width)

    def weight_scratch(wide):
        return [
            pltpu.VMEM((2, fourth, wide), f32),
            pltpu.VMEM((2, fourth, wide), bf16),
            pltpu.VMEM((2, fourth, wide), bf16),
            *[pltpu.VMEM((fourth, wide), bf16)] * 4,
        ]

    return pl.pallas_call(
        scatter_kernel,
        out_shape=(
            jax.ShapeDtypeStruct(full, f32),
            jax.ShapeDtypeStruct((2, 2, GROUPS, *unit), bf16),
            jax.ShapeDtypeStruct((2, GROUPS, fourth, wide_q), bf16),
            jax.ShapeDtypeStruct((2, GROUPS, fourth, wide_v), bf16),
            jax.ShapeDtypeStruct((24, width), f32),
        ),
        in_specs=[in_hbm()] + [whole_vmem()] * 9,
        out_specs=(whole_vmem(), anywhere(), anywhere(), anywhere(), whole_vmem()),
        scratch_shapes=[
            pltpu.VMEM((GROUPS, 4, *kv_block), bf16),
            pltpu.VMEM((GROUPS, 4, *kv_block), bf16),
            pltpu.VMEM((GROUPS, 2, *kv_block), f32),
            pltpu.VMEM((GROUPS, 2, *kv_block), bf16),
            pltpu.VMEM((GROUPS, 2, *kv_block), bf16),
            pltpu.VMEM((GROUPS, *kv_block), bf16),
            pltpu.VMEM((GROUPS, *kv_block), bf16),
            pltpu.VMEM((GROUPS, *full), f32),
            pltpu.VMEM(full, f32),
            pltpu.VMEM((2, GROUPS, *full), bf16),
            pltpu.VMEM((GROUPS, *full), bf16),
            pltpu.VMEM((width, wide_v), f32),
            pltpu.VMEM((GROUPS, *unit), f32),
            pltpu.VMEM(unit, f32),
            pltpu.VMEM((2, GROUPS, *unit), bf16),
            pltpu.VMEM((GROUPS, *unit), bf16),
            pltpu.VMEM(unit, bf16),
            *weight_scratch(wide_q),
            *weight_scratch(wide_v),
            pltpu.VMEM((6, 24, width), f32),
            dma((GROUPS, 4)), dma((GROUPS, 4)), dma((GROUPS, 4)), dma((GROUPS,)), dma((GROUPS,)), dma((GROUPS,)), dma((GROUPS,)),
            dma((GROUPS,)), dma((2, GROUPS)),
            dma((GROUPS,)), dma((2, GROUPS)), dma((1,)), dma((1,)), dma((2,)), dma((GROUPS,)), dma((GROUPS,)),
            dma((GROUPS,)), dma((GROUPS,)), dma((2, GROUPS)), dma((2, GROUPS)),
            dma((3,)), dma((3,)), dma((2,)), dma((GROUPS,)), dma((GROUPS,)), dma((GROUPS,)), dma((GROUPS,)),
            dma((3,)), dma((3,)), dma((2,)), dma((GROUPS,)), dma((GROUPS,)), dma((GROUPS,)), dma((GROUPS,)),
            dma((6,)), dma((6,)), dma((4,)),
        ],
        compiler_params=pltpu.CompilerParams(
            collective_id=2, has_side_effects=True, vmem_limit_bytes=51 << 20
        ),
        name="scatter",
    )(dkv, dq, normed, wfull, tokens, mgrad, small, bundle, over, sums)


def pack_kv(key_part, value_part):
    return jnp.concatenate(
        [key_part, value_part[..., 2 * DH :], value_part[..., : 2 * DH]], axis=-1
    )


def unpack_kv(both):
    return both[..., :HW], jnp.concatenate([both[..., HW + DH :], both[..., HW : HW + DH]], axis=-1)


def layout_kernel(
    big_ref, query_ref, kv_ref, sums_ref,
    up_out, down_out, wo_out, query_out, key_out, value_out,
    low_gain, low_shift, query_bias, value_bias, out_bias, high_gain, high_shift, up_bias, down_bias,
):
    x = lax.axis_index("x")
    width = big_ref.shape[-1]
    half = width // 2
    for core in range(2):
        down_out[core] = big_ref[core, 0, 0:96].astype(f32)
        wo_out[core] = big_ref[core, 0, 192:UNIT].astype(f32)
        for owner in range(2):
            lane = (2 * owner + core) * width
            up_out[:, lane : lane + width] = big_ref[core, 0, 96 + 48 * owner : 144 + 48 * owner].astype(f32)
        query_out[core] = jnp.concatenate(
            [query_ref[core, z].astype(f32)[:, :HW] for z in range(GROUPS)], axis=1
        )
        both = [unpack_kv(kv_ref[core, z].astype(f32)) for z in range(GROUPS)]
        key_out[core] = jnp.concatenate([item[0] for item in both], axis=1)
        value_out[core] = jnp.concatenate([item[1] for item in both], axis=1)

    @pl.when(pl.program_id(0) == 0)
    def _():
        def own_half(row):
            whole = sums_ref[row : row + 1]
            return jnp.where(x == 0, whole[:, :half], whole[:, half:]).reshape(half)

        for ref, row in (
            (low_gain, 0), (low_shift, 1), (out_bias, 2), (high_gain, 3), (high_shift, 4), (down_bias, 5),
        ):
            ref[...] = own_half(row)
        pair = [sums_ref[pl.ds(16 + 2 * x + i, 1)] for i in range(2)]
        query_bias[...] = jnp.concatenate([item[:, :HW] for item in pair], axis=1).reshape(half)
        value_bias[...] = jnp.concatenate(
            [unpack_kv(item[:, 2 * BLK : 2 * BLK + 2 * HW])[1] for item in pair], axis=1
        ).reshape(half)
        up_bias[...] = jnp.concatenate(
            [sums_ref[pl.ds(8 + 2 * x + i, 1)] for i in range(2)], axis=1
        ).reshape(2 * width)


def lay_out(big, query, kv, sums):
    width = big.shape[-1]
    half, fourth = width // 2, width // 4
    rows = fourth // PARTS

    def spec(shape, index):
        return pl.BlockSpec(shape, index)

    def fixed(wide):
        return pl.BlockSpec((wide,), lambda p: (0,))

    narrow = spec((2, rows, width), lambda p: (0, p, 0))
    vector = jax.ShapeDtypeStruct((half,), f32)
    return pl.pallas_call(
        layout_kernel,
        grid=(PARTS,),
        out_shape=(
            jax.ShapeDtypeStruct((half, 4 * width), f32),
            jax.ShapeDtypeStruct((2, width, width), f32),
            *[jax.ShapeDtypeStruct((2, fourth, width), f32)] * 4,
            *[vector] * 7,
            jax.ShapeDtypeStruct((2 * width,), f32),
            vector,
        ),
        in_specs=[
            spec((2, 1, UNIT, width), lambda p: (0, p, 0, 0)),
            spec((2, GROUPS, rows, query.shape[-1]), lambda p: (0, 0, p, 0)),
            spec((2, GROUPS, rows, kv.shape[-1]), lambda p: (0, 0, p, 0)),
            spec(sums.shape, lambda p: (0, 0)),
        ],
        out_specs=(
            spec((48, 4 * width), lambda p: (p, 0)),
            spec((2, 96, width), lambda p: (0, p, 0)),
            *[narrow] * 4,
            *[fixed(half)] * 7,
            fixed(2 * width),
            fixed(half),
        ),
        compiler_params=pltpu.CompilerParams(
            vmem_limit_bytes=VMEM_LIMIT, dimension_semantics=("arbitrary",)
        ),
        name="lay_out",
    )(big, query, kv, sums)


ROWS = ("s", "r", "core", "x")
ALL = ("g", "s", "r", "core", "x")


def shards(
    tokens, cotangent, doc_lengths, deal, first_gain, first_shift, query_weight, query_bias,
    key_weight, value_weight, value_bias, output_weight, output_bias, second_gain, second_shift,
    up_weight, up_bias, down_weight, down_bias,
):
    rows, width = tokens.shape
    half = width // 2
    blocks = deal.shape[0]
    kv, q, normed, small, wfull, up, wo = gather(
        tokens, query_weight, key_weight, value_weight, up_weight, output_weight,
        first_gain, first_shift, output_bias, second_gain, second_shift, down_bias, query_bias, value_bias, up_bias,
    )
    wide = blocks > 8 * 2 * GROUPS
    if wide:
        kv = lax.all_gather(kv, "s", axis=0, tiled=True)
    kv = kv.reshape(blocks, BLK, 2 * HW)
    q = q.reshape(2 * GROUPS, BLK, 2 * BLK)
    out_t, kept, lse = attend_forward(deal, doc_lengths, q, kv)
    result, grad_middle, grad_t, bundle, over, sums = dense(
        out_t, tokens, cotangent, small, up, wo, down_weight
    )
    over = lax.ppermute(over, "r", ((0, 1), (1, 0)))
    dq, dkv = attend_backward(deal, doc_lengths, q, kv, lse, grad_t, kept)
    dkv = dkv.reshape(-1, GROUPS, rows, 2 * HW)
    if wide:
        dkv = lax.psum_scatter(dkv, "s", scatter_dimension=0, tiled=True)
    dq = dq.reshape(GROUPS, rows, 2 * BLK)
    grad_tokens, big, query_own, kv_own, sums = scatter(
        dkv, dq, normed, wfull, tokens, grad_middle, small, bundle, over, sums
    )
    if wide:
        big, query_own, kv_own, sums = (
            lax.psum(item, "s") for item in (big, query_own, kv_own, sums)
        )

    (
        up_own, down_own, wo_own, query_own, key_own, value_own,
        low_gain, low_shift, query_sum, value_sum, out_sum, high_gain, high_shift, up_sum, down_sum,
    ) = lay_out(big.reshape(2, PARTS, UNIT, width), query_own, kv_own, sums)

    def flat(item):
        return item.reshape(-1, width)

    return (
        result,
        grad_tokens,
        low_gain,
        low_shift,
        flat(query_own),
        query_sum,
        flat(key_own),
        flat(value_own),
        value_sum,
        flat(wo_own),
        out_sum,
        high_gain,
        high_shift,
        up_own,
        up_sum,
        flat(down_own),
        down_sum,
    )


def solution(mesh):
    devices = mesh.devices
    inner_mesh = Mesh(devices.reshape(GROUPS, devices.shape[0] // (4 * GROUPS), 2, 2, 2), ALL)
    row = P(ALL, None)
    mat = P("x", None)
    vec = P("x")
    in_specs = (
        row, row, P(), P(), vec, vec, mat, vec, mat, mat, vec, mat, vec, vec, vec, mat, vec, mat, vec,
    )
    out_specs = (
        row, row, vec, vec, mat, vec, mat, mat, vec, mat, vec, vec, vec, mat, vec, mat, vec,
    )
    return jax.shard_map(
        shards, mesh=inner_mesh, in_specs=in_specs, out_specs=out_specs, check_vma=False
    )
```

```python
import jax
import jax.numpy as jnp
from jax import lax
from jax.experimental import pallas as pl
from jax.experimental.pallas import tpu as pltpu
from jax.sharding import Mesh
from jax.sharding import PartitionSpec as P

HEADS = 12
DH = 64
NSUM = 50
SEG = 2048
BLK = 128
GROUPS = 4
PER = HEADS // GROUPS
HW = PER * DH
WIDE = PER * BLK
CHUNK = 2 * BLK
EPS = 1e-05
SCALE = 0.125
MASKED = -1e30
ROOT_HALF = 0.7071067811865476
PDF_SCALE = 0.3989422804014327
VMEM_LIMIT = 56 << 20
bf16 = jnp.bfloat16
f32 = jnp.float32


def layer_norm(values, gain, shift):
    mean = jnp.mean(values, axis=-1, keepdims=True)
    centred = values - mean
    spread = jnp.mean(centred * centred, axis=-1, keepdims=True)
    return centred * lax.rsqrt(spread + EPS) * gain + shift


def outer(left, right):
    return lax.dot_general(left, right, (((0,), (0,)), ((), ())), preferred_element_type=f32)


def inner(left, right):
    return lax.dot_general(left, right, (((1,), (1,)), ((), ())), preferred_element_type=f32)


def dot(left, right):
    return jnp.dot(left, right, preferred_element_type=f32)


def survey(deal_ref, lengths_ref, where_ref, text_ref, low_ref, high_ref, first_ref):
    blocks = deal_ref.shape[0]
    per_group = blocks // (2 * GROUPS)
    rest = lax.axis_index(ROWS)

    def note(j, kept):
        pair = j // 2
        group = pair // per_group
        where_ref[deal_ref[j]] = ((pair - group * per_group) * GROUPS + group) * 2 + j % 2
        return kept

    lax.fori_loop(0, blocks, note, 0)
    starts = [jnp.int32(0)]
    for doc in range(lengths_ref.shape[0] - 1):
        starts.append(starts[-1] + lengths_ref[doc])

    def first_of(at):
        begin = jnp.zeros_like(at)
        for start in starts:
            begin = jnp.where(start <= at, jnp.maximum(begin, start), begin)
        return jnp.where(at - begin >= SEG + NSUM, begin + SEG, begin)

    for slot in range(2 * GROUPS):
        text = deal_ref[2 * ((slot // 2) * per_group + rest) + slot % 2]
        text_ref[slot] = text
        low_ref[slot] = first_of(text * BLK) // CHUNK
        high_ref[slot] = text // 2
        first_ref[slot] = first_of(text * BLK + lax.broadcasted_iota(jnp.int32, (1, BLK), 1))


def survey_scratch(blocks):
    slots = 2 * GROUPS
    return [
        pltpu.SMEM((blocks,), jnp.int32),
        pltpu.SMEM((slots,), jnp.int32),
        pltpu.SMEM((slots,), jnp.int32),
        pltpu.SMEM((slots,), jnp.int32),
        pltpu.VMEM((slots, 1, BLK), jnp.int32),
    ]


def spread_heads_t(part_t, order):
    rows = []
    zero = jnp.zeros((DH, BLK), part_t.dtype)
    for head in order:
        if head is None:
            rows.append(jnp.zeros((DH, WIDE), part_t.dtype))
        else:
            piece = part_t[DH * head : DH * head + DH]
            rows.append(
                jnp.concatenate([piece if h == head else zero for h in range(PER)], axis=1)
            )
    return jnp.concatenate(rows, axis=0)


K_ORDER = (0, 1, 2, None)
V_ORDER = (None, 2, 0, 1)


def visible(chunk, first, own):
    at = chunk * CHUNK + lax.broadcasted_iota(jnp.int32, (CHUNK, BLK), 0)
    allowed = (at >= first) & (at <= own)
    return jnp.concatenate([allowed] * PER, axis=1)


def load_chunk(kv_ref, where_ref, chunk):
    return jnp.concatenate(
        [kv_ref[where_ref[2 * chunk]], kv_ref[where_ref[2 * chunk + 1]]], axis=0
    )


def forward_kernel(
    deal_ref, lengths_ref, q_ref, kv_ref,
    out_ref, wide_ref, lse_ref,
    where_ref, text_ref, low_ref, high_ref, first_ref, vt_ref, acc_ref,
):
    survey(deal_ref, lengths_ref, where_ref, text_ref, low_ref, high_ref, first_ref)
    chunks = kv_ref.shape[0] // 2

    def turn(chunk, _):
        vt_ref[chunk] = load_chunk(kv_ref, where_ref, chunk)[:, BLK : 3 * BLK].T[DH:]
        return _

    lax.fori_loop(0, chunks, turn, 0)

    def one_slot(slot, _):
        wide_q = spread_heads_t(q_ref[slot].T[:HW], K_ORDER)
        first = first_ref[slot]
        own = text_ref[slot] * BLK + lax.broadcasted_iota(jnp.int32, (1, BLK), 1)
        acc_ref[...] = jnp.zeros_like(acc_ref)

        def step(chunk, carry):
            top, total = carry
            part = load_chunk(kv_ref, where_ref, chunk)
            scores = dot(part[:, : 2 * BLK], wide_q)
            scores = jnp.where(visible(chunk, first, own), scores, MASKED)
            fresh = jnp.maximum(top, jnp.max(scores, axis=0, keepdims=True))
            expo = jnp.exp(scores - fresh)
            shrink = jnp.exp(top - fresh)
            total = total * shrink + jnp.sum(expo, axis=0, keepdims=True)
            acc_ref[...] = acc_ref[...] * shrink + dot(vt_ref[chunk], expo.astype(bf16))
            return fresh, total

        top, total = lax.fori_loop(
            low_ref[slot],
            high_ref[slot] + 1,
            step,
            (jnp.full((1, WIDE), MASKED, f32), jnp.zeros((1, WIDE), f32)),
        )
        lse_ref[slot] = top + jnp.log(total)
        scaled = acc_ref[...] / total
        pieces = []
        for head in range(PER):
            row = DH * V_ORDER.index(head) - DH
            pieces.append(scaled[row : row + DH, BLK * head : BLK * head + BLK])
        kept = jnp.concatenate(pieces, axis=0)
        wide_ref[slot] = kept
        out_ref[slot] = kept.astype(bf16)
        return _

    lax.fori_loop(0, q_ref.shape[0], one_slot, 0)


def whole_vmem():
    return pl.BlockSpec(memory_space=pltpu.VMEM)


def whole_smem():
    return pl.BlockSpec(memory_space=pltpu.SMEM)


def attend_forward(deal, lengths, q, kv):
    slots = q.shape[0]
    blocks = kv.shape[0]
    return pl.pallas_call(
        forward_kernel,
        out_shape=(
            jax.ShapeDtypeStruct((slots, HW, BLK), bf16),
            jax.ShapeDtypeStruct((slots, HW, BLK), f32),
            jax.ShapeDtypeStruct((slots, 1, WIDE), f32),
        ),
        in_specs=[whole_smem()] * 2 + [whole_vmem()] * 2,
        out_specs=(whole_vmem(),) * 3,
        scratch_shapes=[
            *survey_scratch(blocks),
            pltpu.VMEM((blocks // 2, HW, CHUNK), bf16),
            pltpu.VMEM((HW, WIDE), f32),
        ],
        compiler_params=pltpu.CompilerParams(vmem_limit_bytes=(6 << 20) + kv.size // 5 * 16),
        name="attend_forward",
    )(deal, lengths, q, kv)


def backward_kernel(
    deal_ref, lengths_ref, q_ref, kv_ref, lse_ref, do_ref, wide_ref,
    dq_ref, dkv_ref, where_ref, text_ref, low_ref, high_ref, first_ref, qt_ref, qm_ref, dot_ref, dom_ref, delta_ref, acc_ref, dk_acc, dv_acc,
    packed_ref, out_sem,
):
    survey(deal_ref, lengths_ref, where_ref, text_ref, low_ref, high_ref, first_ref)
    slots = q_ref.shape[0]
    chunks = kv_ref.shape[0] // 2

    def ready(slot, _):
        q = q_ref[slot]
        qt_ref[slot] = spread_heads_t(q.T[:HW], K_ORDER)
        lane = lax.broadcasted_iota(jnp.int32, (BLK, 2 * BLK), 1) // DH
        zero = jnp.zeros_like(q)
        qm_ref[slot] = jnp.concatenate(
            [jnp.where(lane == K_ORDER.index(h), q, zero) for h in range(PER)], axis=0
        )
        grad_t = do_ref[slot]
        dot_ref[slot] = spread_heads_t(grad_t, V_ORDER)
        ordered = jnp.concatenate(
            [
                jnp.zeros((DH, BLK), bf16) if h is None else grad_t[DH * h : DH * h + DH]
                for h in V_ORDER
            ],
            axis=0,
        ).T
        dom_ref[slot] = jnp.concatenate(
            [jnp.where(lane == V_ORDER.index(h), ordered, zero) for h in range(PER)], axis=0
        )
        both = grad_t.astype(f32) * wide_ref[slot]
        delta_ref[slot] = jnp.concatenate(
            [jnp.sum(both[DH * h : DH * h + DH], axis=0, keepdims=True) for h in range(PER)],
            axis=1,
        )
        acc_ref[slot] = jnp.zeros((HW, WIDE), f32)
        return _

    lax.fori_loop(0, slots, ready, 0)

    def written(chunk, i):
        return pltpu.make_async_copy(
            packed_ref.at[chunk % 2, i], dkv_ref.at[where_ref[2 * chunk + i]], out_sem.at[chunk % 2, i]
        )

    def one_chunk(chunk, kept):
        part = load_chunk(kv_ref, where_ref, chunk)
        keys = part[:, : 2 * BLK]
        vals = part[:, BLK:]
        keys_t = keys.T[:HW]
        dk_acc[...] = jnp.zeros_like(dk_acc)
        dv_acc[...] = jnp.zeros_like(dv_acc)

        def one_slot(slot, kept):
            @pl.when((low_ref[slot] <= chunk) & (chunk <= high_ref[slot]))
            def _():
                own = text_ref[slot] * BLK + lax.broadcasted_iota(jnp.int32, (1, BLK), 1)
                scores = dot(keys, qt_ref[slot])
                probs = jnp.where(
                    visible(chunk, first_ref[slot], own), jnp.exp(scores - lse_ref[slot]), 0.0
                )
                dprobs = dot(vals, dot_ref[slot])
                dscores = (probs * (dprobs - delta_ref[slot])).astype(bf16)
                dv_acc[...] += dot(probs.astype(bf16), dom_ref[slot])
                dk_acc[...] += dot(dscores, qm_ref[slot])
                acc_ref[slot] += dot(keys_t, dscores)

            return kept

        lax.fori_loop(0, slots, one_slot, 0)
        packed = jnp.concatenate(
            [
                dk_acc[:, :BLK],
                dk_acc[:, BLK:] + dv_acc[:, :BLK],
                dv_acc[:, BLK:],
            ],
            axis=1,
        ).astype(bf16)

        @pl.when(chunk >= 2)
        def _():
            for i in range(2):
                written(chunk - 2, i).wait()

        for i in range(2):
            packed_ref[chunk % 2, i] = packed[BLK * i : BLK * i + BLK]
            written(chunk, i).start()
        return kept

    lax.fori_loop(0, chunks, one_chunk, 0)
    for last in range(2):
        for i in range(2):
            written(chunks - 2 + last, i).wait()

    def finish(slot, _):
        total = acc_ref[slot]
        kept = jnp.concatenate(
            [total[DH * h : DH * h + DH, BLK * h : BLK * h + BLK] for h in range(PER)]
            + [jnp.zeros((DH, BLK), f32)],
            axis=0,
        )
        dq_ref[slot] = kept.T.astype(bf16)
        return _

    lax.fori_loop(0, slots, finish, 0)


def attend_backward(deal, lengths, q, kv, lse, grad_t, wide):
    slots = q.shape[0]
    return pl.pallas_call(
        backward_kernel,
        out_shape=(
            jax.ShapeDtypeStruct((slots, BLK, 2 * BLK), bf16),
            jax.ShapeDtypeStruct(kv.shape, bf16),
        ),
        in_specs=[whole_smem()] * 2 + [whole_vmem()] * 5,
        out_specs=(whole_vmem(), in_hbm()),
        scratch_shapes=[
            *survey_scratch(kv.shape[0]),
            pltpu.VMEM((slots, 2 * BLK, WIDE), bf16),
            pltpu.VMEM((slots, WIDE, 2 * BLK), bf16),
            pltpu.VMEM((slots, 2 * BLK, WIDE), bf16),
            pltpu.VMEM((slots, WIDE, 2 * BLK), bf16),
            pltpu.VMEM((slots, 1, WIDE), f32),
            pltpu.VMEM((slots, HW, WIDE), f32),
            pltpu.VMEM((CHUNK, 2 * BLK), f32),
            pltpu.VMEM((CHUNK, 2 * BLK), f32),
            pltpu.VMEM((2, 2, BLK, 2 * HW), bf16),
            pltpu.SemaphoreType.DMA((2, 2)),
        ],
        compiler_params=pltpu.CompilerParams(
            vmem_limit_bytes=max(48 << 20, (17 << 20) + kv.size * 2)
        ),
        name="attend_backward",
    )(deal, lengths, q, kv, lse, grad_t, wide)


MESH = pl.DeviceIdType.MESH


def send(src, dst, out_sem, in_sem, **device):
    return pltpu.make_async_remote_copy(
        src_ref=src, dst_ref=dst, send_sem=out_sem, recv_sem=in_sem, device_id=device, device_id_type=MESH
    )


def place():
    return tuple(lax.axis_index(name) for name in ("g", "r", "core", "x"))


def seat(r, core, x):
    return (r * 2 + core) * 2 + x


def greet(g, r, core, x, line):
    barrier = pltpu.get_barrier_semaphore()

    def hello(**device):
        pl.semaphore_signal(barrier, inc=1, device_id=device, device_id_type=MESH)

    hello(core=1 - core)
    hello(x=1 - x)
    hello(r=1 - r)
    if line:
        for away in range(1, GROUPS):
            hello(g=lax.rem(g + away, GROUPS))
        pl.semaphore_wait(barrier, 3 + GROUPS - 1)
    else:
        pl.when(g > 0)(lambda: hello(g=g - 1))
        pl.when(g < GROUPS - 1)(lambda: hello(g=g + 1))
        pl.semaphore_wait(barrier, 5 - jnp.where(g == 0, 1, 0) - jnp.where(g == GROUPS - 1, 1, 0))


NEAREST = tuple(tuple(sorted(range(GROUPS), key=lambda s: (abs(s - z), s))) for z in range(GROUPS))


def nearest(g, step):
    picked = NEAREST[0][step]
    for z in range(1, GROUPS):
        picked = jnp.where(g == z, NEAREST[z][step], picked)
    return picked


def prepare(g, x, weights, lines, narrow_ref, small_ref):
    half = weights.shape[1]
    odd = lax.rem(g, 2) == 1

    def columns(i):
        low = pl.multiple_of(3 * g // 2 * BLK, BLK)
        window = weights[i, :, pl.ds(low, 2 * BLK)]
        moved = jnp.concatenate([window[:, DH:], window[:, :DH]], axis=1)
        return jnp.where(odd, moved, window)

    lane = lax.broadcasted_iota(jnp.int32, (half, 2 * BLK), 1)
    query = columns(0)
    narrow_ref[:, : 2 * BLK] = jnp.where(lane < HW, query, jnp.zeros_like(query))
    narrow_ref[:, 2 * BLK :] = pack_kv(columns(1)[:, :HW], columns(2)[:, :HW])

    def line(i):
        return lines[i][...].astype(f32).reshape(1, -1)

    zero = jnp.zeros((1, half), f32)
    small_ref[...] = jnp.zeros_like(small_ref)
    for row in range(6):
        small_ref[row : row + 1] = jnp.where(
            x == 0, jnp.concatenate([line(row), zero], axis=1), jnp.concatenate([zero, line(row)], axis=1)
        )
    ups = line(8)
    for i in range(2):
        small_ref[pl.ds(8 + 2 * x + i, 1)] = ups[:, 2 * half * i : 2 * half * i + 2 * half]

    def part(i):
        mine = jnp.where(odd, line(i)[:, HW:], line(i)[:, :HW])
        return jnp.where(g // 2 == x, mine, jnp.zeros_like(mine))

    value = part(7)
    small_ref[12:13] = jnp.concatenate(
        [part(6), jnp.zeros((1, 2 * BLK), f32), value[:, 2 * DH :], value[:, : 2 * DH], jnp.zeros((1, BLK), f32)], axis=1
    )


def gather_kernel(
    tokens_ref, query_any, key_any, value_any, wo_ref, l0, l1, l2, l3, l4, l5, l6, l7, l8,
    kv_ref, q_ref, normed_ref, small_out, wfull, wo_out,
    lined, attn_w, narrow_ref, small_ref, small_in, kvs,
    z_own, z_send, z_recv, s_sem, n_send, n_recv, kv_send, kv_recv, kv_local, w_send, w_recv, w_local, a_sem,
):
    g, r, core, x = place()
    other = 1 - x
    rows, width = tokens_ref.shape
    half = width // 2
    fourth = half // 2
    eighth = half // 4
    loads = [
        pltpu.make_async_copy(ref, attn_w.at[i], a_sem.at[i]) for i, ref in enumerate((query_any, key_any, value_any))
    ]
    for load in loads:
        load.start()
    greet(g, r, core, x, False)

    def along(source, away, sem):
        return send(lined.at[source], lined.at[source], sem, z_recv.at[source], g=g + away)

    lined[g] = tokens_ref[...]
    pl.when(g > 0)(lambda: along(g, -1, z_own.at[0]).start())
    pl.when(g < GROUPS - 1)(lambda: along(g, 1, z_own.at[1]).start())

    for load in loads:
        load.wait()
    prepare(g, x, attn_w, (l0, l1, l2, l3, l4, l5, l6, l7, l8), narrow_ref, small_ref)
    small_move = send(small_ref, small_in, s_sem.at[0], s_sem.at[1], x=other)
    small_move.start()
    mine = pl.ds(x * half + core * fourth, fourth)
    narrow_x = send(narrow_ref.at[pl.ds(core * fourth, fourth)], wfull.at[mine], n_send.at[0], n_recv.at[0], x=other)
    narrow_x.start()

    def wo_rows(owner, part):
        return wo_out.at[pl.ds(owner * half + core * fourth + part * eighth, eighth)]

    wo_x = send(wo_ref.at[pl.ds(core * fourth + r * eighth, eighth)], wo_rows(x, r), w_send.at[0], w_recv.at[0], x=other)
    wo_y = send(wo_rows(other, r), wo_rows(other, r), w_send.at[3], w_recv.at[3], r=1 - r)
    wo_s = [
        send(wo_rows(other, part), wo_rows(other, part), w_send.at[6 + i], w_recv.at[6 + i], core=1 - core)
        for i, part in enumerate((r, 1 - r))
    ]
    wo_x.start()
    locals_ = [pltpu.make_async_copy(wo_ref, wo_out.at[pl.ds(x * half, half)], w_local.at[0])]
    for item in locals_:
        item.start()

    wfull[pl.ds(x * half, half)] = narrow_ref[...]
    narrow_x.wait_recv()
    theirs = wfull.at[pl.ds(other * half + core * fourth, fourth)]
    narrow_s = send(theirs, theirs, n_send.at[1], n_recv.at[1], core=1 - core)
    narrow_s.start()
    small_move.wait_recv()
    small_out[...] = small_ref[...] + small_in[...]
    narrow_s.wait_recv()

    own = seat(r, core, x)

    def block(owner, source):
        return kv_ref.at[owner, source]

    def push(step, kind, what, **device):
        copy = send(what[0], what[1], kv_send.at[kind, step], kv_recv.at[kind, step], **device)
        copy.start()

    def settle(step, kind, owner, source):
        send(block(owner, source), block(owner, source), kv_send.at[kind, step], kv_recv.at[kind, step], x=other).wait_recv()

    def forward(step):
        source = nearest(g, step)
        by_x = block(seat(r, core, other), source)
        settle(step, 0, seat(r, core, other), source)
        if step % 2 == 0:
            push(step, 3, (by_x, by_x), r=1 - r)
        push(step, 4, (by_x, by_x), core=1 - core)
        by_y = block(seat(1 - r, core, x), source)
        settle(step, 1, seat(1 - r, core, x), source)
        if step % 2 == 1:
            push(step, 3, (by_y, by_y), x=other)
        push(step, 5, (by_y, by_y), core=1 - core)

    def forward_far(step):
        source = nearest(g, step)
        far = block(seat(1 - r, core, other), source)
        settle(step, 3, seat(1 - r, core, other), source)
        push(step, 6, (far, far), core=1 - core)

    for step in range(GROUPS):
        source = nearest(g, step)
        if step > 0:
            send(lined.at[source], lined.at[source], z_send.at[source], z_recv.at[source], x=other).wait_recv()
            pl.when((source < g) & (g < GROUPS - 1))(lambda: along(source, 1, z_send.at[source]).start())
            pl.when((source > g) & (g > 0))(lambda: along(source, -1, z_send.at[source]).start())
        values = lined[source].astype(f32)
        normed = layer_norm(values, small_out[0:1], small_out[1:2]).astype(bf16)
        normed_ref[source] = normed
        both = dot(normed, wfull[...]) + small_out[12:13, : wfull.shape[1]]
        q_ref[source] = (both[:, : 2 * BLK] * SCALE).astype(bf16)
        kvs[step] = both[:, 2 * BLK :].astype(bf16)
        here = (kvs.at[step], block(own, source))
        push(step, 0, here, x=other)
        push(step, 1, here, r=1 - r)
        push(step, 2, here, core=1 - core)
        pltpu.make_async_copy(kvs.at[step], block(own, source), kv_local.at[step]).start()
        if step > 0:
            forward(step - 1)
        if step > 1:
            forward_far(step - 2)
    wo_x.wait_recv()
    wo_y.start()
    wo_s[0].start()
    forward(GROUPS - 1)
    forward_far(GROUPS - 2)
    send(wo_rows(other, 1 - r), wo_rows(other, 1 - r), w_send.at[3], w_recv.at[3], r=1 - r).wait_recv()
    wo_s[1].start()
    forward_far(GROUPS - 1)

    for step in range(GROUPS):
        source = nearest(g, step)
        pltpu.make_async_copy(kvs.at[step], block(own, source), kv_local.at[step]).wait()
        settle(step, 2, seat(r, 1 - core, x), source)
        settle(step, 4, seat(r, 1 - core, other), source)
        settle(step, 5, seat(1 - r, 1 - core, x), source)
        settle(step, 6, seat(1 - r, 1 - core, other), source)
        for kind in range(7):
            send(kvs.at[step], block(own, source), kv_send.at[kind, step], kv_recv.at[kind, step], x=other).wait_send()
    pl.when(g > 0)(lambda: along(g, -1, z_own.at[0]).wait_send())
    pl.when(g < GROUPS - 1)(lambda: along(g, 1, z_own.at[1]).wait_send())
    for step in range(1, GROUPS):
        source = nearest(g, step)
        passed = ((source < g) & (g < GROUPS - 1)) | ((source > g) & (g > 0))
        pl.when(passed)(lambda: send(lined.at[source], lined.at[source], z_send.at[source], z_recv.at[source], x=other).wait_send())
    small_move.wait_send()
    narrow_x.wait_send()
    narrow_s.wait_send()
    for item in locals_:
        item.wait()
    for item in (wo_x, wo_y, *wo_s):
        item.wait_send()
    for i, part in enumerate((r, 1 - r)):
        there = wo_out.at[pl.ds(other * half + (1 - core) * fourth + part * eighth, eighth)]
        send(there, there, w_send.at[6 + i], w_recv.at[6 + i], core=1 - core).wait_recv()


def anywhere():
    return pl.BlockSpec(memory_space=pl.ANY)


def in_hbm():
    return pl.BlockSpec(memory_space=pltpu.HBM)


def gather(tokens, query, key, value, wo, *lines):
    rows, width = tokens.shape
    wide = 2 * BLK + 2 * HW
    small = (16, width)
    dma = pltpu.SemaphoreType.DMA
    return pl.pallas_call(
        gather_kernel,
        out_shape=(
            jax.ShapeDtypeStruct((8, GROUPS, rows, 2 * HW), bf16),
            jax.ShapeDtypeStruct((GROUPS, rows, 2 * BLK), bf16),
            jax.ShapeDtypeStruct((GROUPS, rows, width), bf16),
            jax.ShapeDtypeStruct(small, f32),
            jax.ShapeDtypeStruct((width, wide), bf16),
            jax.ShapeDtypeStruct((width, width), bf16),
        ),
        in_specs=[whole_vmem(), *[in_hbm()] * 4, *[whole_vmem()] * len(lines)],
        out_specs=(anywhere(), *(whole_vmem(),) * 5),
        scratch_shapes=[
            pltpu.VMEM((GROUPS, rows, width), bf16),
            pltpu.VMEM((3, width // 2, width), bf16),
            pltpu.VMEM((width // 2, wide), bf16),
            pltpu.VMEM(small, f32),
            pltpu.VMEM(small, f32),
            pltpu.VMEM((GROUPS, rows, 2 * HW), bf16),
            dma((2,)), dma((GROUPS,)), dma((GROUPS,)), dma((2,)), dma((2,)), dma((2,)),
            dma((7, GROUPS)), dma((7, GROUPS)), dma((GROUPS,)), dma((8,)), dma((8,)), dma((2,)), dma((3,)),
        ],
        compiler_params=pltpu.CompilerParams(
            collective_id=0, has_side_effects=True, vmem_limit_bytes=60 << 20
        ),
        name="gather",
    )(tokens, query, key, value, wo, *lines)


def erf_parts(values):
    below = 0.5 * (1.0 + lax.erf(values * ROOT_HALF))
    return below, PDF_SCALE * jnp.exp(-0.5 * values * values)


PARTS = 8
UNIT = 216


def dense_kernel(
    out_t_ref, tokens_ref, cot_ref, cot_x_ref, small_ref, wo_ref, up_mine, up_other, down_any,
    base_ref, y_give_ref, middle_grad_ref, grad_t_ref, keep_ref, give_ref, sums_ref,
    down_ref, up_ref, attn_in, attn_t, cots, h2s, mid_ref, n2_ref, scales, part_y, part_d, in_y, in_d, pass_y, pass_d,
    x_y, x_d, hids, dus, branch_ref, grad_out, wo_keep, wo_give, wo_in, wo_pass, wo_x,
    l_sem, a_send, a_recv, c_send, c_recv, h_send, h_recv, y_send, y_recv, d_send, d_recv, o_send, o_recv,
    w_send, w_recv,
):
    g, r, core, x = place()
    other, sib = 1 - x, 1 - core
    rows, width = tokens_ref.shape
    half = width // 2
    fourth = half // 2
    loads = [
        pltpu.make_async_copy(
            down_any.at[pl.ds(pl.multiple_of(core * width, width), width)], down_ref, l_sem.at[0]
        ),
        pltpu.make_async_copy(up_mine, up_ref.at[pl.ds(x * half, half)], l_sem.at[1]),
        pltpu.make_async_copy(up_other, up_ref.at[pl.ds(other * half, half)], l_sem.at[2]),
    ]
    for load in loads:
        load.start()
    greet(g, r, core, x, True)
    pending = []

    def begin(src, dst, out_sem, in_sem, **device):
        move = send(src, dst, out_sem, in_sem, **device)
        move.start()
        pending.append(move)
        return move

    def other_group(away):
        return lax.rem(g + away, GROUPS)

    def rows_of(b):
        return pl.ds(BLK * b, BLK)

    for b in range(2):
        for away in range(1, GROUPS):
            to = other_group(away)
            begin(out_t_ref.at[2 * to + b], attn_in.at[g, b], a_send.at[b, away], a_recv.at[b, g], g=to)
        attn_in[g, b] = out_t_ref[2 * g + b]
        cots[b, 0] = cot_ref[rows_of(b)]
        cots[b, 2] = cot_x_ref[rows_of(b)]
    cot_moves = [
        begin(cots.at[:, 2 * i], cots.at[:, 2 * i + 1], c_send.at[i], c_recv.at[i], core=sib) for i in range(2)
    ]
    sums_ref[...] = jnp.zeros_like(sums_ref)
    sums_ref[5:6] = jnp.sum(cot_ref[...].astype(f32), axis=0, keepdims=True)
    h2_moves = []

    def norm(b):
        for away in range(1, GROUPS):
            source = other_group(away)
            arrived(attn_in.at[source, b], a_send.at[b, away], a_recv.at[b, source], x)
        for source in range(GROUPS):
            attn_t[HW * source : HW * source + HW, BLK * b : BLK * b + BLK] = attn_in[source, b]
        middle = (
            tokens_ref[rows_of(b)].astype(f32)
            + outer(attn_t[:, BLK * b : BLK * b + BLK], wo_ref[...])
            + small_ref[2:3]
        )
        mid_ref[b] = middle
        mean = jnp.mean(middle, axis=-1, keepdims=True)
        centred = middle - mean
        scale = lax.rsqrt(jnp.mean(centred * centred, axis=-1, keepdims=True) + EPS)
        scales[b] = scale
        n2_ref[b] = centred * scale
        h2s[b, 0] = (n2_ref[b] * small_ref[3:4] + small_ref[4:5]).astype(bf16)
        h2_moves.append(
            (
                begin(h2s.at[b, 0], h2s.at[b, 2], h_send.at[b, 1], h_recv.at[b, 1], x=other),
                begin(h2s.at[b, 0], h2s.at[b, 1], h_send.at[b, 0], h_recv.at[b, 0], core=sib),
            )
        )

    def pass_on(b):
        h2_moves[b][0].wait_recv()
        return begin(h2s.at[b, 2], h2s.at[b, 3], h_send.at[b, 2], h_recv.at[b, 2], core=sib)

    bias_row = 8 + 2 * x + core

    def pair_of(ref, b, pair):
        return ref[b, 2 * pair : 2 * pair + 2].reshape(2 * BLK, width)

    def forward_backward(b, pair):
        cot = pair_of(cots, b, pair)
        expanded = dot(pair_of(h2s, b, pair), up_ref[...]) + small_ref[pl.ds(bias_row, 1)]
        below, density = erf_parts(expanded)
        hidden = (expanded * below).astype(bf16)
        hids[b, pair] = hidden
        slope = below + expanded * density
        grad_hidden = inner(cot, down_ref[...]).astype(bf16).astype(f32)
        grad_expand = (grad_hidden * slope).astype(bf16)
        dus[b, pair] = grad_expand
        part_d[b, pair] = inner(grad_expand, up_ref[...])
        part_y[b, pair] = dot(hidden, down_ref[...])
        sums_ref[pl.ds(bias_row, 1)] += jnp.sum(grad_expand.astype(f32), axis=0, keepdims=True)

    d_moves, y_passes = [None, None], [None, None]

    def near_pair(b):
        if b == 0:
            cot_moves[0].wait_recv()
        h2_moves[b][1].wait_recv()
        forward_backward(b, 0)
        return begin(part_d.at[b, 0, pl.ds(BLK, BLK)], in_d.at[b], d_send.at[b, 0], d_recv.at[b, 0], core=sib)

    def far_pair(b, passed):
        if b == 0:
            cot_moves[1].wait_recv()
        passed.wait_recv()
        forward_backward(b, 1)
        x_d[b, 0] = part_d[b, 1, BLK:].astype(bf16)
        across = begin(x_d.at[b, 0], pass_d.at[b], d_send.at[b, 1], d_recv.at[b, 1], core=sib)
        x_y[b] = part_y[b, 1, BLK:].astype(bf16)
        y_passes[b] = begin(x_y.at[b], pass_y.at[b], y_send.at[b, 1], y_recv.at[b, 1], core=sib)
        across.wait_recv()
        x_d[b, 1] = (part_d[b, 1, :BLK] + pass_d[b].astype(f32)).astype(bf16)
        return begin(x_d.at[b, 1], x_d.at[b, 2], d_send.at[b, 2], d_recv.at[b, 2], x=other)

    def back(b, near, far):
        near.wait_recv()
        far.wait_recv()
        grad_second = part_d[b, 0, :BLK] + in_d[b] + x_d[b, 2].astype(f32)
        n2 = n2_ref[b]
        sums_ref[3:4] += jnp.sum(grad_second * n2, axis=0, keepdims=True)
        sums_ref[4:5] += jnp.sum(grad_second, axis=0, keepdims=True)
        pulled = grad_second * small_ref[3:4]
        inward = (
            pulled - jnp.mean(pulled, axis=-1, keepdims=True) - n2 * jnp.mean(pulled * n2, axis=-1, keepdims=True)
        )
        grad_middle = cot_ref[rows_of(b)].astype(f32) + inward * scales[b]
        middle_grad_ref[rows_of(b)] = grad_middle
        branch = grad_middle.astype(bf16)
        branch_ref[rows_of(b)] = branch
        sums_ref[2:3] += jnp.sum(branch.astype(f32), axis=0, keepdims=True)
        grad_out_t = inner(wo_ref[...], branch).astype(bf16)
        for group in range(GROUPS):
            grad_out[group, b] = grad_out_t[HW * group : HW * group + HW]
        for away in range(1, GROUPS):
            to = other_group(away)
            begin(grad_out.at[to, b], grad_t_ref.at[2 * g + b], o_send.at[b, away], o_recv.at[b, g], g=to)
        grad_t_ref[2 * g + b] = grad_out[g, b]

    norm(0)
    norm(1)
    for load in loads:
        load.wait()
    near = [near_pair(0), None]
    passed = [pass_on(0), None]
    near[1] = near_pair(1)
    far = [far_pair(0, passed[0]), None]
    passed[1] = pass_on(1)
    far[1] = far_pair(1, passed[1])

    def over_rows(left, right):
        total = None
        for b in range(2):
            for pair in range(2):
                term = outer(left(b, pair), right(b, pair))
                total = term if total is None else total + term
        return total.astype(bf16)

    def parts(write):
        for y in range(2):
            pl.when(r == y)(lambda: write(keep_ref, y))
            pl.when(r != y)(lambda: write(give_ref, y))

    down_grad = over_rows(lambda b, pair: hids[b, pair], lambda b, pair: pair_of(cots, b, pair))

    def write_down(ref, y):
        for z in range(GROUPS):
            p = y * GROUPS + z
            ref[z, 0:96] = down_grad[96 * p : 96 * p + 96]

    parts(write_down)
    back(0, near[0], far[0])
    up_grad = over_rows(lambda b, pair: pair_of(h2s, b, pair), lambda b, pair: dus[b, pair])

    def write_up(ref, y):
        for z in range(GROUPS):
            p = y * GROUPS + z
            ref[z, 96:144] = up_grad[48 * p : 48 * p + 48]
            ref[z, 144:192] = up_grad[half + 48 * p : half + 48 * p + 48]

    parts(write_up)
    back(1, near[1], far[1])

    for owner in range(2):
        for c in range(2):
            piece = dot(attn_t[half * owner + fourth * c : half * owner + fourth * c + fourth], branch_ref[...])

            @pl.when(core == c)
            def _():
                wo_keep[owner] = piece

            @pl.when(core != c)
            def _():
                wo_give[owner] = piece.astype(bf16)

    w_sib = begin(wo_give, wo_in, w_send.at[0], w_recv.at[0], core=sib)
    y_sibs = [
        begin(part_y.at[b, 0, pl.ds(BLK, BLK)], in_y.at[b], y_send.at[b, 0], y_recv.at[b, 0], core=sib)
        for b in range(2)
    ]
    w_sib.wait_recv()
    wo_pass[...] = (wo_keep[other] + wo_in[other].astype(f32)).astype(bf16)
    w_x = begin(wo_pass, wo_x, w_send.at[1], w_recv.at[1], x=other)
    for b in range(2):
        y_passes[b].wait_recv()
        y_give_ref[rows_of(b)] = (part_y[b, 1, :BLK] + pass_y[b].astype(f32)).astype(bf16)
        y_sibs[b].wait_recv()
        base_ref[rows_of(b)] = mid_ref[b] + part_y[b, 0, :BLK] + in_y[b] + small_ref[5:6]
    mine = wo_keep[x] + wo_in[x].astype(f32)
    for b in range(2):
        for away in range(1, GROUPS):
            source = other_group(away)
            arrived(grad_t_ref.at[2 * source + b], o_send.at[b, away], o_recv.at[b, source], x)
    w_x.wait_recv()
    wo_sum = (mine + wo_x[...].astype(f32)).astype(bf16)

    def write_wo(ref, y):
        for z in range(GROUPS):
            p = y * GROUPS + z
            ref[z, 192:UNIT] = wo_sum[24 * p : 24 * p + 24]

    parts(write_wo)
    for move in pending:
        move.wait_send()


def dense(out_t, tokens, cot, cot_x, small, wo, up_mine, up_other, down):
    rows, width = tokens.shape
    dma = pltpu.SemaphoreType.DMA
    full = (rows, width)
    part = (BLK, width)
    pair = (2 * BLK, width)
    fourth = (width // 4, width)
    return pl.pallas_call(
        dense_kernel,
        out_shape=(
            jax.ShapeDtypeStruct(full, f32),
            jax.ShapeDtypeStruct(full, bf16),
            jax.ShapeDtypeStruct(full, f32),
            jax.ShapeDtypeStruct(out_t.shape, bf16),
            jax.ShapeDtypeStruct((GROUPS, UNIT, width), bf16),
            jax.ShapeDtypeStruct((GROUPS, UNIT, width), bf16),
            jax.ShapeDtypeStruct(small.shape, f32),
        ),
        in_specs=[whole_vmem()] * 6 + [anywhere()] * 3,
        out_specs=(whole_vmem(),) * 7,
        scratch_shapes=[
            pltpu.VMEM((width, width), bf16),
            pltpu.VMEM((width, width), bf16),
            pltpu.VMEM((GROUPS, 2, HW, BLK), bf16),
            pltpu.VMEM((width, rows), bf16),
            pltpu.VMEM((2, 4, *part), bf16),
            pltpu.VMEM((2, 4, *part), bf16),
            pltpu.VMEM((2, *part), f32),
            pltpu.VMEM((2, *part), f32),
            pltpu.VMEM((2, BLK, 1), f32),
            pltpu.VMEM((2, 2, *pair), f32),
            pltpu.VMEM((2, 2, *pair), f32),
            pltpu.VMEM((2, *part), f32),
            pltpu.VMEM((2, *part), f32),
            pltpu.VMEM((2, *part), bf16),
            pltpu.VMEM((2, *part), bf16),
            pltpu.VMEM((2, *part), bf16),
            pltpu.VMEM((2, 3, *part), bf16),
            pltpu.VMEM((2, 2, *pair), bf16),
            pltpu.VMEM((2, 2, *pair), bf16),
            pltpu.VMEM(full, bf16),
            pltpu.VMEM((GROUPS, 2, HW, BLK), bf16),
            pltpu.VMEM((2, *fourth), f32),
            pltpu.VMEM((2, *fourth), bf16),
            pltpu.VMEM((2, *fourth), bf16),
            pltpu.VMEM(fourth, bf16),
            pltpu.VMEM(fourth, bf16),
            dma((3,)), dma((2, GROUPS)), dma((2, GROUPS)), dma((2,)), dma((2,)), dma((2, 3)), dma((2, 3)),
            dma((2, 2)), dma((2, 2)), dma((2, 3)), dma((2, 3)), dma((2, GROUPS)), dma((2, GROUPS)), dma((2,)), dma((2,)),
        ],
        compiler_params=pltpu.CompilerParams(
            collective_id=1, has_side_effects=True, vmem_limit_bytes=40 << 20
        ),
        name="dense",
    )(out_t, tokens, cot, cot_x, small, wo, up_mine, up_other, down)


FARTHEST = ((3, 2, 1, 0), (3, 0, 2, 1), (0, 3, 1, 2), (0, 1, 2, 3))


def farthest(g, step):
    picked = FARTHEST[0][step]
    for z in range(1, GROUPS):
        picked = jnp.where(g == z, FARTHEST[z][step], picked)
    return picked


class Chain:
    def __init__(self, g, x, total, parts, inward, outward, out_sem, in_sem):
        self.g, self.x, self.total, self.parts = g, x, total, parts
        self.inward, self.outward, self.out_sem, self.in_sem = inward, outward, out_sem, in_sem

    def move(self, to, way):
        return send(
            self.outward.at[to], self.inward.at[way, to], self.out_sem.at[to], self.in_sem.at[way, to],
            g=jnp.clip(self.g + (1 if way == 0 else -1), 0, GROUPS - 1),
        )

    def step(self, to):
        g = self.g
        self.total[...] = self.parts[to].astype(f32)

        def take(way):
            arrived(self.inward.at[way, to], self.out_sem.at[to], self.in_sem.at[way, to], self.x)
            self.total[...] += self.inward[way, to].astype(f32)

        pl.when((to >= g) & (g > 0))(lambda: take(0))
        pl.when((to <= g) & (g < GROUPS - 1))(lambda: take(1))

        @pl.when(to != g)
        def _():
            self.outward[to] = self.total[...].astype(bf16)

        pl.when(to > g)(lambda: self.move(to, 0).start())
        pl.when(to < g)(lambda: self.move(to, 1).start())

    def finish(self):
        for step in range(GROUPS - 1):
            to = farthest(self.g, step)
            left(self.outward.at[to], self.out_sem.at[to], self.in_sem.at[0, to], self.x)


class Ring:
    def __init__(self, g, x, slot, own_sem, out_sem, in_sem):
        self.g, self.x, self.slot = g, x, slot
        self.own_sem, self.out_sem, self.in_sem = own_sem, out_sem, in_sem

    def move(self, source, way, sem):
        return send(
            self.slot(source), self.slot(source), sem, self.in_sem.at[source],
            g=jnp.clip(self.g + way, 0, GROUPS - 1),
        )

    def start(self):
        g = self.g
        pl.when(g > 0)(lambda: self.move(g, -1, self.own_sem.at[0]).start())
        pl.when(g < GROUPS - 1)(lambda: self.move(g, 1, self.own_sem.at[1]).start())

    def step(self, step):
        g, source = self.g, nearest(self.g, step)
        arrived(self.slot(source), self.out_sem.at[source], self.in_sem.at[source], self.x)
        pl.when((source < g) & (g < GROUPS - 1))(lambda: self.move(source, 1, self.out_sem.at[source]).start())
        pl.when((source > g) & (g > 0))(lambda: self.move(source, -1, self.out_sem.at[source]).start())
        return source

    def finish(self):
        g = self.g
        for i, there in enumerate((g > 0, g < GROUPS - 1)):
            pl.when(there)(lambda: left(self.slot(g), self.own_sem.at[i], self.in_sem.at[g], self.x))
        for step in range(1, GROUPS):
            source = nearest(g, step)
            passed = ((source < g) & (g < GROUPS - 1)) | ((source > g) & (g > 0))
            pl.when(passed)(
                lambda: left(self.slot(source), self.out_sem.at[source], self.in_sem.at[source], self.x)
            )


def arrived(what, out_sem, in_sem, x):
    send(what, what, out_sem, in_sem, x=1 - x).wait_recv()


def left(what, out_sem, in_sem, x):
    send(what, what, out_sem, in_sem, x=1 - x).wait_send()


def scatter_kernel(
    dkv_ref, dq_ref, normed_ref, wfull_ref, tokens_ref, mgrad_ref, small_ref, bundle_ref, by_in, sums_in,
    tokens_grad_ref, big_ref, qout_ref, kvout_ref, sums_ref,
    own_kv, sib_kv, keep_x, give_x, in_x, give_y, in_y, part_a, total_a, inward_a, outward_a, wg_kv,
    by_sum, total_b, inward_b, outward_b, unit,
    q_keep, q_give, q_in, q_pass, q_x, q_y, q_sum, v_keep, v_give, v_in, v_pass, v_x, v_y, v_sum,
    sums_got,
    own_sem, k_send, k_recv, x_send, x_recv, y_send, y_recv, ca_send, ca_recv,
    cb_send, cb_recv, u_send, u_recv, rb_own, rb_send, rb_recv,
    fy_send, fy_recv, fs_send, fs_recv,
    q_send, q_recv, rq_own, rq_send, rq_recv, qs_send, qs_recv,
    v_send, v_recv, rv_own, rv_send, rv_recv, vs_send, vs_recv,
    s_send, s_recv, l_sem,
):
    g, r, core, x = place()
    other, sib, far_r = 1 - x, 1 - core, 1 - r
    rows, width = tokens_ref.shape
    half = width // 2
    fourth = half // 2
    wide_q = 2 * BLK
    greet(g, r, core, x, True)
    pending = []

    def begin(src, dst, out_sem, in_sem, **device):
        move = send(src, dst, out_sem, in_sem, **device)
        move.start()
        pending.append(move)
        return move

    def settled(move):
        move.wait_recv()
        move.wait_send()
        pending[:] = [item for item in pending if item is not move]

    kv_moves = []
    for i in range(GROUPS):
        c = farthest(g, i)
        for spot in range(4):
            own = pltpu.make_async_copy(dkv_ref.at[seat(spot // 2, core, spot % 2), c], own_kv.at[i, spot], own_sem.at[i, spot])
            own.start()
            across = begin(
                dkv_ref.at[seat(spot // 2, sib, spot % 2), c], sib_kv.at[i, spot],
                k_send.at[i, spot], k_recv.at[i, spot], core=sib,
            )
            kv_moves.append((own, across))

    def split(total, keep, give, wide):
        for owner in range(2):
            for c in range(2):
                low = half * owner + fourth * c
                chunk = total[low : low + fourth]

                @pl.when(core == c)
                def _():
                    keep[owner] = chunk

                @pl.when(core != c)
                def _():
                    give[owner] = chunk.astype(bf16)

    def scaled(c):
        return dq_ref[c] * bf16(SCALE)

    def query_grad():
        query_total = outer(normed_ref[0], scaled(0))
        for c in range(1, GROUPS):
            query_total += outer(normed_ref[c], scaled(c))
        split(query_total, q_keep, q_give, wide_q)
        q_move.start()

    q_move = send(q_give, q_in, q_send.at[0], q_recv.at[0], core=sib)
    sums_ref[...] = jnp.zeros_like(sums_ref)
    sums_ref[0:16] = sums_in[...]
    line_q = scaled(0).astype(f32)
    for c in range(1, GROUPS):
        line_q += scaled(c).astype(f32)
    sums_ref[pl.ds(16 + g, 1), 0:wide_q] = jnp.sum(line_q, axis=0, keepdims=True)
    wg_kv[...] = jnp.zeros_like(wg_kv)

    def q_slot(z):
        return qout_ref.at[core, z]

    def v_slot(z):
        return kvout_ref.at[core, z]

    def b_slot(z):
        return big_ref.at[core, r, z]

    ring_q = Ring(g, x, q_slot, rq_own, rq_send, rq_recv)
    ring_v = Ring(g, x, v_slot, rv_own, rv_send, rv_recv)
    ring_b = Ring(g, x, b_slot, rb_own, rb_send, rb_recv)

    def store(value_ref, slot, sem):
        copy = pltpu.make_async_copy(value_ref, slot, sem)
        copy.start()
        copy.wait()

    def spread_b(z, step):
        begin(b_slot(z), b_slot(z), fy_send.at[step], fy_recv.at[step], r=far_r)
        begin(b_slot(z), b_slot(z), fs_send.at[0, step], fs_recv.at[0, step], core=sib)

    def spread_far(z, step):
        what = big_ref.at[core, far_r, z]
        arrived(what, fy_send.at[step], fy_recv.at[step], x)
        begin(what, what, fs_send.at[1, step], fs_recv.at[1, step], core=sib)

    chain_a = Chain(g, x, total_a, part_a, inward_a, outward_a, ca_send, ca_recv)
    chain_b = Chain(g, x, total_b, by_sum, inward_b, outward_b, cb_send, cb_recv)
    at_end = (g == 0) | (g == GROUPS - 1)
    between = jnp.logical_not(at_end)

    def steps(chain, *which):
        for i in which:
            chain.step(farthest(g, i))

    def on_sibling(i):
        for own, across in kv_moves[4 * i : 4 * i + 4]:
            own.wait()
            across.wait_recv()

        def total(row, column):
            spot = 2 * row + column
            return own_kv[i, spot].astype(f32) + sib_kv[i, spot].astype(f32)

        for k in range(2):
            give_x[i, k] = (total(k, other) if i % 2 == 0 else total(far_r, k)).astype(bf16)
            keep_x[i, k] = total(k, x) if i % 2 == 0 else total(r, k)

    def go_first(i):
        along = {"x": other} if i % 2 == 0 else {"r": far_r}
        begin(give_x.at[i], in_x.at[i], x_send.at[i], x_recv.at[i], **along)

    def on_first(i):
        arrived(in_x.at[i], x_send.at[i], x_recv.at[i], x)
        away, stay, along = (far_r, r, {"r": far_r}) if i % 2 == 0 else (other, x, {"x": other})
        give_y[i] = (keep_x[i, away] + in_x[i, away].astype(f32)).astype(bf16)
        begin(give_y.at[i], in_y.at[i], y_send.at[i], y_recv.at[i], **along)
        keep_x[i, stay] += in_x[i, stay].astype(f32)

    def on_second(i):
        c = farthest(g, i)
        arrived(in_y.at[i], y_send.at[i], y_recv.at[i], x)
        both = (keep_x[i, r if i % 2 == 0 else x] + in_y[i].astype(f32)).astype(bf16)
        part_a[c] = inner(scaled(c), wfull_ref[:, :wide_q]) + inner(both, wfull_ref[:, wide_q:])
        wg_kv[...] += outer(normed_ref[c], both)
        sums_ref[pl.ds(16 + g, 1), wide_q : wide_q + 2 * HW] += jnp.sum(both.astype(f32), axis=0, keepdims=True)

    by_sum[...] = bundle_ref[...].astype(f32) + by_in[...].astype(f32)
    on_sibling(0)
    go_first(0)
    on_sibling(1)
    go_first(1)
    pl.when(at_end)(lambda: steps(chain_b, 0, 1, 2))
    on_sibling(2)
    on_sibling(3)
    query_grad()
    pl.when(between)(lambda: steps(chain_b, 0))
    on_first(0)
    on_first(1)
    go_first(2)
    go_first(3)
    settled(q_move)
    q_pass[...] = (q_keep[other] + q_in[other].astype(f32)).astype(bf16)
    q_across = begin(q_pass, q_x, q_send.at[1], q_recv.at[1], x=other)
    on_second(0)
    on_second(1)
    pl.when(at_end)(lambda: steps(chain_a, 0, 1))
    pl.when(between)(lambda: steps(chain_b, 1, 2))
    on_first(2)
    on_first(3)
    chain_b.step(g)
    unit[...] = total_b[...].astype(bf16)
    up_rows = 96 + 48 * other
    begin(unit.at[pl.ds(up_rows, 48)], big_ref.at[core, r, g, pl.ds(96 + 48 * x, 48)], u_send.at[0], u_recv.at[0], x=other)
    copies = [
        pltpu.make_async_copy(unit.at[pl.ds(0, 96)], big_ref.at[core, r, g, pl.ds(0, 96)], l_sem.at[1]),
        pltpu.make_async_copy(
            unit.at[pl.ds(96 + 48 * x, 48)], big_ref.at[core, r, g, pl.ds(96 + 48 * x, 48)], l_sem.at[2]
        ),
        pltpu.make_async_copy(unit.at[pl.ds(192, 24)], big_ref.at[core, r, g, pl.ds(192, 24)], l_sem.at[3]),
    ]
    for copy in copies:
        copy.start()
    q_across.wait_recv()
    q_sum[...] = (q_keep[x] + q_in[x].astype(f32) + q_x[...].astype(f32)).astype(bf16)
    q_over = begin(q_sum, q_y, q_send.at[2], q_recv.at[2], r=far_r)
    on_second(2)
    on_second(3)
    pl.when(at_end)(lambda: steps(chain_a, 2))
    split(wg_kv, v_keep, v_give, 2 * HW)
    v_move = begin(v_give, v_in, v_send.at[0], v_recv.at[0], core=sib)
    for copy in copies:
        copy.wait()
    arrived(big_ref.at[core, r, g, pl.ds(up_rows, 48)], u_send.at[0], u_recv.at[0], x)
    ring_b.start()
    spread_b(g, 0)
    v_move.wait_recv()
    v_pass[...] = (v_keep[other] + v_in[other].astype(f32)).astype(bf16)
    v_across = begin(v_pass, v_x, v_send.at[1], v_recv.at[1], x=other)
    pl.when(between)(lambda: steps(chain_a, 0))
    settled(q_over)
    q_sum[...] = (q_sum[...].astype(f32) + q_y[...].astype(f32)).astype(bf16)
    store(q_sum, q_slot(g), l_sem.at[0])
    ring_q.start()
    begin(q_slot(g), q_slot(g), qs_send.at[0], qs_recv.at[0], core=sib)
    v_across.wait_recv()
    v_sum[...] = (v_keep[x] + v_in[x].astype(f32) + v_x[...].astype(f32)).astype(bf16)
    v_over = begin(v_sum, v_y, v_send.at[2], v_recv.at[2], r=far_r)
    spread_far(g, 0)
    pl.when(between)(lambda: steps(chain_a, 1, 2))
    settled(v_over)
    v_sum[...] = (v_sum[...].astype(f32) + v_y[...].astype(f32)).astype(bf16)
    store(v_sum, v_slot(g), l_sem.at[0])
    ring_v.start()
    begin(v_slot(g), v_slot(g), vs_send.at[0], vs_recv.at[0], core=sib)
    spread_b(ring_b.step(1), 1)
    z = ring_q.step(1)
    begin(q_slot(z), q_slot(z), qs_send.at[1], qs_recv.at[1], core=sib)
    z = ring_v.step(1)
    begin(v_slot(z), v_slot(z), vs_send.at[1], vs_recv.at[1], core=sib)
    chain_a.step(g)

    grad_first = total_a[...]
    values = tokens_ref[...].astype(f32)
    mean = jnp.mean(values, axis=-1, keepdims=True)
    centred = values - mean
    scale = lax.rsqrt(jnp.mean(centred * centred, axis=-1, keepdims=True) + EPS)
    n1 = centred * scale
    pulled = grad_first * small_ref[0:1]
    inward = pulled - jnp.mean(pulled, axis=-1, keepdims=True) - n1 * jnp.mean(pulled * n1, axis=-1, keepdims=True)
    tokens_grad_ref[...] = mgrad_ref[...] + inward * scale
    sums_ref[0:1] = jnp.sum(grad_first * n1, axis=0, keepdims=True)
    sums_ref[1:2] = jnp.sum(grad_first, axis=0, keepdims=True)
    s_sib = begin(sums_ref, sums_got.at[0], s_send.at[0], s_recv.at[0], core=sib)

    settled(s_sib)
    sums_ref[...] += sums_got[0]
    s_x = begin(sums_ref, sums_got.at[1], s_send.at[1], s_recv.at[1], x=other)
    spread_b(ring_b.step(2), 2)
    spread_far(nearest(g, 1), 1)
    settled(s_x)
    sums_ref[...] += sums_got[1]
    s_y = begin(sums_ref, sums_got.at[2], s_send.at[2], s_recv.at[2], r=far_r)
    z = ring_q.step(2)
    begin(q_slot(z), q_slot(z), qs_send.at[2], qs_recv.at[2], core=sib)
    z = ring_v.step(2)
    begin(v_slot(z), v_slot(z), vs_send.at[2], vs_recv.at[2], core=sib)
    settled(s_y)
    sums_ref[...] += sums_got[2]
    for away in range(1, GROUPS):
        begin(
            sums_ref, sums_got.at[2 + away], s_send.at[2 + away], s_recv.at[2 + away],
            g=lax.rem(g + away, GROUPS),
        )
    spread_b(ring_b.step(3), 3)
    spread_far(nearest(g, 2), 2)
    z = ring_q.step(3)
    begin(q_slot(z), q_slot(z), qs_send.at[3], qs_recv.at[3], core=sib)
    z = ring_v.step(3)
    begin(v_slot(z), v_slot(z), vs_send.at[3], vs_recv.at[3], core=sib)
    spread_far(nearest(g, 3), 3)

    for away in range(1, GROUPS):
        arrived(sums_got.at[2 + away], s_send.at[2 + away], s_recv.at[2 + away], x)
    for step in range(GROUPS):
        z = nearest(g, step)
        arrived(qout_ref.at[sib, z], qs_send.at[step], qs_recv.at[step], x)
        arrived(kvout_ref.at[sib, z], vs_send.at[step], vs_recv.at[step], x)
        arrived(big_ref.at[sib, r, z], fs_send.at[0, step], fs_recv.at[0, step], x)
        arrived(big_ref.at[sib, far_r, z], fs_send.at[1, step], fs_recv.at[1, step], x)
    for move in pending:
        move.wait_send()
    for item in (chain_a, chain_b, ring_q, ring_v, ring_b):
        item.finish()
    sums_ref[...] += sums_got[3] + sums_got[4] + sums_got[5]


def scatter(dkv, dq, normed, wfull, tokens, mgrad, small, bundle, over, sums):
    rows, width = tokens.shape
    fourth = width // 4
    dma = pltpu.SemaphoreType.DMA
    wide_q, wide_v = 2 * BLK, 2 * HW
    kv_block = (rows, wide_v)
    full = (rows, width)
    unit = (UNIT, width)

    def weight_scratch(wide):
        return [
            pltpu.VMEM((2, fourth, wide), f32),
            pltpu.VMEM((2, fourth, wide), bf16),
            pltpu.VMEM((2, fourth, wide), bf16),
            *[pltpu.VMEM((fourth, wide), bf16)] * 4,
        ]

    return pl.pallas_call(
        scatter_kernel,
        out_shape=(
            jax.ShapeDtypeStruct(full, f32),
            jax.ShapeDtypeStruct((2, 2, GROUPS, *unit), bf16),
            jax.ShapeDtypeStruct((2, GROUPS, fourth, wide_q), bf16),
            jax.ShapeDtypeStruct((2, GROUPS, fourth, wide_v), bf16),
            jax.ShapeDtypeStruct((24, width), f32),
        ),
        in_specs=[in_hbm()] + [whole_vmem()] * 9,
        out_specs=(whole_vmem(), anywhere(), anywhere(), anywhere(), whole_vmem()),
        scratch_shapes=[
            pltpu.VMEM((GROUPS, 4, *kv_block), bf16),
            pltpu.VMEM((GROUPS, 4, *kv_block), bf16),
            pltpu.VMEM((GROUPS, 2, *kv_block), f32),
            pltpu.VMEM((GROUPS, 2, *kv_block), bf16),
            pltpu.VMEM((GROUPS, 2, *kv_block), bf16),
            pltpu.VMEM((GROUPS, *kv_block), bf16),
            pltpu.VMEM((GROUPS, *kv_block), bf16),
            pltpu.VMEM((GROUPS, *full), f32),
            pltpu.VMEM(full, f32),
            pltpu.VMEM((2, GROUPS, *full), bf16),
            pltpu.VMEM((GROUPS, *full), bf16),
            pltpu.VMEM((width, wide_v), f32),
            pltpu.VMEM((GROUPS, *unit), f32),
            pltpu.VMEM(unit, f32),
            pltpu.VMEM((2, GROUPS, *unit), bf16),
            pltpu.VMEM((GROUPS, *unit), bf16),
            pltpu.VMEM(unit, bf16),
            *weight_scratch(wide_q),
            *weight_scratch(wide_v),
            pltpu.VMEM((6, 24, width), f32),
            dma((GROUPS, 4)), dma((GROUPS, 4)), dma((GROUPS, 4)), dma((GROUPS,)), dma((GROUPS,)), dma((GROUPS,)), dma((GROUPS,)),
            dma((GROUPS,)), dma((2, GROUPS)),
            dma((GROUPS,)), dma((2, GROUPS)), dma((1,)), dma((1,)), dma((2,)), dma((GROUPS,)), dma((GROUPS,)),
            dma((GROUPS,)), dma((GROUPS,)), dma((2, GROUPS)), dma((2, GROUPS)),
            dma((3,)), dma((3,)), dma((2,)), dma((GROUPS,)), dma((GROUPS,)), dma((GROUPS,)), dma((GROUPS,)),
            dma((3,)), dma((3,)), dma((2,)), dma((GROUPS,)), dma((GROUPS,)), dma((GROUPS,)), dma((GROUPS,)),
            dma((6,)), dma((6,)), dma((4,)),
        ],
        compiler_params=pltpu.CompilerParams(
            collective_id=2, has_side_effects=True, vmem_limit_bytes=51 << 20
        ),
        name="scatter",
    )(dkv, dq, normed, wfull, tokens, mgrad, small, bundle, over, sums)


def pack_kv(key_part, value_part):
    return jnp.concatenate(
        [key_part, value_part[..., 2 * DH :], value_part[..., : 2 * DH]], axis=-1
    )


def unpack_kv(both):
    return both[..., :HW], jnp.concatenate([both[..., HW + DH :], both[..., HW : HW + DH]], axis=-1)


def layout_kernel(
    big_ref, query_ref, kv_ref, sums_ref, base_ref, got_ref,
    up_out, down_out, wo_out, query_out, key_out, value_out,
    low_gain, low_shift, query_bias, value_bias, out_bias, high_gain, high_shift, up_bias, down_bias, result_out,
):
    x = lax.axis_index("x")
    width = big_ref.shape[-1]
    half = width // 2
    result_out[...] = (base_ref[...] + got_ref[...].astype(f32)).astype(bf16)
    for core in range(2):
        down_out[core] = big_ref[core, 0, 0:96].astype(f32)
        wo_out[core] = big_ref[core, 0, 192:UNIT].astype(f32)
        for owner in range(2):
            lane = (2 * owner + core) * width
            up_out[:, lane : lane + width] = big_ref[core, 0, 96 + 48 * owner : 144 + 48 * owner].astype(f32)
        query_out[core] = jnp.concatenate(
            [query_ref[core, z].astype(f32)[:, :HW] for z in range(GROUPS)], axis=1
        )
        both = [unpack_kv(kv_ref[core, z].astype(f32)) for z in range(GROUPS)]
        key_out[core] = jnp.concatenate([item[0] for item in both], axis=1)
        value_out[core] = jnp.concatenate([item[1] for item in both], axis=1)

    @pl.when(pl.program_id(0) == 0)
    def _():
        def own_half(row):
            whole = sums_ref[row : row + 1]
            return jnp.where(x == 0, whole[:, :half], whole[:, half:]).reshape(half)

        for ref, row in (
            (low_gain, 0), (low_shift, 1), (out_bias, 2), (high_gain, 3), (high_shift, 4), (down_bias, 5),
        ):
            ref[...] = own_half(row)
        pair = [sums_ref[pl.ds(16 + 2 * x + i, 1)] for i in range(2)]
        query_bias[...] = jnp.concatenate([item[:, :HW] for item in pair], axis=1).reshape(half)
        value_bias[...] = jnp.concatenate(
            [unpack_kv(item[:, 2 * BLK : 2 * BLK + 2 * HW])[1] for item in pair], axis=1
        ).reshape(half)
        up_bias[...] = jnp.concatenate(
            [sums_ref[pl.ds(8 + 2 * x + i, 1)] for i in range(2)], axis=1
        ).reshape(2 * width)


def lay_out(big, query, kv, sums, base, got):
    width = big.shape[-1]
    half, fourth = width // 2, width // 4
    rows = fourth // PARTS

    def spec(shape, index):
        return pl.BlockSpec(shape, index)

    def fixed(wide):
        return pl.BlockSpec((wide,), lambda p: (0,))

    narrow = spec((2, rows, width), lambda p: (0, p, 0))
    vector = jax.ShapeDtypeStruct((half,), f32)
    return pl.pallas_call(
        layout_kernel,
        grid=(PARTS,),
        out_shape=(
            jax.ShapeDtypeStruct((half, 4 * width), f32),
            jax.ShapeDtypeStruct((2, width, width), f32),
            *[jax.ShapeDtypeStruct((2, fourth, width), f32)] * 4,
            *[vector] * 7,
            jax.ShapeDtypeStruct((2 * width,), f32),
            vector,
            jax.ShapeDtypeStruct(base.shape, bf16),
        ),
        in_specs=[
            spec((2, 1, UNIT, width), lambda p: (0, p, 0, 0)),
            spec((2, GROUPS, rows, query.shape[-1]), lambda p: (0, 0, p, 0)),
            spec((2, GROUPS, rows, kv.shape[-1]), lambda p: (0, 0, p, 0)),
            spec(sums.shape, lambda p: (0, 0)),
            spec((base.shape[0] // PARTS, width), lambda p: (p, 0)),
            spec((base.shape[0] // PARTS, width), lambda p: (p, 0)),
        ],
        out_specs=(
            spec((48, 4 * width), lambda p: (p, 0)),
            spec((2, 96, width), lambda p: (0, p, 0)),
            *[narrow] * 4,
            *[fixed(half)] * 7,
            fixed(2 * width),
            fixed(half),
            spec((base.shape[0] // PARTS, width), lambda p: (p, 0)),
        ),
        compiler_params=pltpu.CompilerParams(
            vmem_limit_bytes=VMEM_LIMIT, dimension_semantics=("arbitrary",)
        ),
        name="lay_out",
    )(big, query, kv, sums, base, got)


ROWS = ("s", "r", "core", "x")
ALL = ("g", "s", "r", "core", "x")


def shards(
    tokens, cotangent, doc_lengths, deal, first_gain, first_shift, query_weight, query_bias,
    key_weight, value_weight, value_bias, output_weight, output_bias, second_gain, second_shift,
    up_weight, up_bias, down_weight, down_bias,
):
    rows, width = tokens.shape
    half = width // 2
    blocks = deal.shape[0]
    core, x = lax.axis_index("core"), lax.axis_index("x")
    swap = ((0, 1), (1, 0))

    def up_columns(owner):
        return lax.dynamic_slice_in_dim(up_weight, (2 * owner + core) * width, width, 1)

    kv, q, normed, small, wfull, wo = gather(
        tokens, query_weight, key_weight, value_weight, output_weight,
        first_gain, first_shift, output_bias, second_gain, second_shift, down_bias, query_bias, value_bias, up_bias,
    )
    wide = blocks > 8 * 2 * GROUPS
    if wide:
        kv = lax.all_gather(kv, "s", axis=0, tiled=True)
    kv = kv.reshape(blocks, BLK, 2 * HW)
    q = q.reshape(2 * GROUPS, BLK, 2 * BLK)
    cot_x, up_other, kv = lax.optimization_barrier((cotangent, up_columns(1 - x), kv))
    up_other = lax.ppermute(up_other, "x", swap)
    cot_x = lax.ppermute(cot_x, "x", swap)
    out_t, kept, lse = attend_forward(deal, doc_lengths, q, kv)
    base, y_give, grad_middle, grad_t, bundle, over, sums = dense(
        out_t, tokens, cotangent, cot_x, small, wo, up_columns(x), up_other, down_weight
    )
    y_got = lax.ppermute(y_give, "x", swap)
    over = lax.ppermute(over, "r", swap)
    dq, dkv = attend_backward(deal, doc_lengths, q, kv, lse, grad_t, kept)
    dkv = dkv.reshape(-1, GROUPS, rows, 2 * HW)
    if wide:
        dkv = lax.psum_scatter(dkv, "s", scatter_dimension=0, tiled=True)
    dq = dq.reshape(GROUPS, rows, 2 * BLK)
    grad_tokens, big, query_own, kv_own, sums = scatter(
        dkv, dq, normed, wfull, tokens, grad_middle, small, bundle, over, sums
    )
    if wide:
        big, query_own, kv_own, sums = (
            lax.psum(item, "s") for item in (big, query_own, kv_own, sums)
        )

    (
        up_own, down_own, wo_own, query_own, key_own, value_own,
        low_gain, low_shift, query_sum, value_sum, out_sum, high_gain, high_shift, up_sum, down_sum, result,
    ) = lay_out(big.reshape(2, PARTS, UNIT, width), query_own, kv_own, sums, base, y_got)

    def flat(item):
        return item.reshape(-1, width)

    return (
        result,
        grad_tokens,
        low_gain,
        low_shift,
        flat(query_own),
        query_sum,
        flat(key_own),
        flat(value_own),
        value_sum,
        flat(wo_own),
        out_sum,
        high_gain,
        high_shift,
        up_own,
        up_sum,
        flat(down_own),
        down_sum,
    )


def solution(mesh):
    devices = mesh.devices
    inner_mesh = Mesh(devices.reshape(GROUPS, devices.shape[0] // (4 * GROUPS), 2, 2, 2), ALL)
    row = P(ALL, None)
    mat = P("x", None)
    vec = P("x")
    in_specs = (
        row, row, P(), P(), vec, vec, mat, vec, mat, mat, vec, mat, vec, vec, vec, mat, vec, mat, vec,
    )
    out_specs = (
        row, row, vec, vec, mat, vec, mat, mat, vec, mat, vec, vec, vec, mat, vec, mat, vec,
    )
    return jax.shard_map(
        shards, mesh=inner_mesh, in_specs=in_specs, out_specs=out_specs, check_vma=False
    )
```

```python
import jax
import jax.numpy as jnp
from jax import lax
from jax.experimental import pallas as pl
from jax.experimental.pallas import tpu as pltpu
from jax.sharding import Mesh
from jax.sharding import PartitionSpec as P

HEADS = 12
DH = 64
NSUM = 50
SEG = 2048
BLK = 128
GROUPS = 4
PER = HEADS // GROUPS
HW = PER * DH
WIDE = PER * BLK
CHUNK = 2 * BLK
EPS = 1e-05
SCALE = 0.125
MASKED = -1e30
ROOT_HALF = 0.7071067811865476
PDF_SCALE = 0.3989422804014327
VMEM_LIMIT = 56 << 20
bf16 = jnp.bfloat16
f32 = jnp.float32


def layer_norm(values, gain, shift):
    mean = jnp.mean(values, axis=-1, keepdims=True)
    centred = values - mean
    spread = jnp.mean(centred * centred, axis=-1, keepdims=True)
    return centred * lax.rsqrt(spread + EPS) * gain + shift


def outer(left, right):
    return lax.dot_general(left, right, (((0,), (0,)), ((), ())), preferred_element_type=f32)


def inner(left, right):
    return lax.dot_general(left, right, (((1,), (1,)), ((), ())), preferred_element_type=f32)


def dot(left, right):
    return jnp.dot(left, right, preferred_element_type=f32)


def survey(deal_ref, lengths_ref, where_ref, text_ref, low_ref, high_ref, first_ref):
    blocks = deal_ref.shape[0]
    per_group = blocks // (2 * GROUPS)
    rest = lax.axis_index(ROWS)

    def note(j, kept):
        pair = j // 2
        group = pair // per_group
        where_ref[deal_ref[j]] = ((pair - group * per_group) * GROUPS + group) * 2 + j % 2
        return kept

    lax.fori_loop(0, blocks, note, 0)
    starts = [jnp.int32(0)]
    for doc in range(lengths_ref.shape[0] - 1):
        starts.append(starts[-1] + lengths_ref[doc])

    def first_of(at):
        begin = jnp.zeros_like(at)
        for start in starts:
            begin = jnp.where(start <= at, jnp.maximum(begin, start), begin)
        return jnp.where(at - begin >= SEG + NSUM, begin + SEG, begin)

    for slot in range(2 * GROUPS):
        text = deal_ref[2 * ((slot // 2) * per_group + rest) + slot % 2]
        text_ref[slot] = text
        low_ref[slot] = first_of(text * BLK) // CHUNK
        high_ref[slot] = text // 2
        first_ref[slot] = first_of(text * BLK + lax.broadcasted_iota(jnp.int32, (1, BLK), 1))


def survey_scratch(blocks):
    slots = 2 * GROUPS
    return [
        pltpu.SMEM((blocks,), jnp.int32),
        pltpu.SMEM((slots,), jnp.int32),
        pltpu.SMEM((slots,), jnp.int32),
        pltpu.SMEM((slots,), jnp.int32),
        pltpu.VMEM((slots, 1, BLK), jnp.int32),
    ]


def spread_heads_t(part_t, order):
    rows = []
    zero = jnp.zeros((DH, BLK), part_t.dtype)
    for head in order:
        if head is None:
            rows.append(jnp.zeros((DH, WIDE), part_t.dtype))
        else:
            piece = part_t[DH * head : DH * head + DH]
            rows.append(
                jnp.concatenate([piece if h == head else zero for h in range(PER)], axis=1)
            )
    return jnp.concatenate(rows, axis=0)


K_ORDER = (0, 1, 2, None)
V_ORDER = (None, 2, 0, 1)


def visible(chunk, first, own):
    at = chunk * CHUNK + lax.broadcasted_iota(jnp.int32, (CHUNK, BLK), 0)
    allowed = (at >= first) & (at <= own)
    return jnp.concatenate([allowed] * PER, axis=1)


def load_chunk(kv_ref, where_ref, chunk):
    return jnp.concatenate(
        [kv_ref[where_ref[2 * chunk]], kv_ref[where_ref[2 * chunk + 1]]], axis=0
    )


def forward_kernel(
    deal_ref, lengths_ref, q_ref, kv_ref,
    out_ref, wide_ref, lse_ref,
    where_ref, text_ref, low_ref, high_ref, first_ref, vt_ref, acc_ref,
):
    survey(deal_ref, lengths_ref, where_ref, text_ref, low_ref, high_ref, first_ref)
    chunks = kv_ref.shape[0] // 2

    def turn(chunk, _):
        vt_ref[chunk] = load_chunk(kv_ref, where_ref, chunk)[:, BLK : 3 * BLK].T[DH:]
        return _

    lax.fori_loop(0, chunks, turn, 0)

    def one_slot(slot, _):
        wide_q = spread_heads_t(q_ref[slot].T[:HW], K_ORDER)
        first = first_ref[slot]
        own = text_ref[slot] * BLK + lax.broadcasted_iota(jnp.int32, (1, BLK), 1)
        acc_ref[...] = jnp.zeros_like(acc_ref)

        def step(chunk, carry):
            top, total = carry
            part = load_chunk(kv_ref, where_ref, chunk)
            scores = dot(part[:, : 2 * BLK], wide_q)
            scores = jnp.where(visible(chunk, first, own), scores, MASKED)
            fresh = jnp.maximum(top, jnp.max(scores, axis=0, keepdims=True))
            expo = jnp.exp(scores - fresh)
            shrink = jnp.exp(top - fresh)
            total = total * shrink + jnp.sum(expo, axis=0, keepdims=True)
            acc_ref[...] = acc_ref[...] * shrink + dot(vt_ref[chunk], expo.astype(bf16))
            return fresh, total

        top, total = lax.fori_loop(
            low_ref[slot],
            high_ref[slot] + 1,
            step,
            (jnp.full((1, WIDE), MASKED, f32), jnp.zeros((1, WIDE), f32)),
        )
        lse_ref[slot] = top + jnp.log(total)
        scaled = acc_ref[...] / total
        pieces = []
        for head in range(PER):
            row = DH * V_ORDER.index(head) - DH
            pieces.append(scaled[row : row + DH, BLK * head : BLK * head + BLK])
        kept = jnp.concatenate(pieces, axis=0)
        wide_ref[slot] = kept
        out_ref[slot] = kept.astype(bf16)
        return _

    lax.fori_loop(0, q_ref.shape[0], one_slot, 0)


def whole_vmem():
    return pl.BlockSpec(memory_space=pltpu.VMEM)


def whole_smem():
    return pl.BlockSpec(memory_space=pltpu.SMEM)


def attend_forward(deal, lengths, q, kv):
    slots = q.shape[0]
    blocks = kv.shape[0]
    return pl.pallas_call(
        forward_kernel,
        out_shape=(
            jax.ShapeDtypeStruct((slots, HW, BLK), bf16),
            jax.ShapeDtypeStruct((slots, HW, BLK), f32),
            jax.ShapeDtypeStruct((slots, 1, WIDE), f32),
        ),
        in_specs=[whole_smem()] * 2 + [whole_vmem()] * 2,
        out_specs=(whole_vmem(),) * 3,
        scratch_shapes=[
            *survey_scratch(blocks),
            pltpu.VMEM((blocks // 2, HW, CHUNK), bf16),
            pltpu.VMEM((HW, WIDE), f32),
        ],
        compiler_params=pltpu.CompilerParams(vmem_limit_bytes=(6 << 20) + kv.size // 5 * 16),
        name="attend_forward",
    )(deal, lengths, q, kv)


def backward_kernel(
    deal_ref, lengths_ref, q_ref, kv_ref, lse_ref, do_ref, wide_ref,
    dq_ref, dkv_ref, where_ref, text_ref, low_ref, high_ref, first_ref, qt_ref, qm_ref, dot_ref, dom_ref, delta_ref, acc_ref, dk_acc, dv_acc,
    packed_ref, out_sem,
):
    survey(deal_ref, lengths_ref, where_ref, text_ref, low_ref, high_ref, first_ref)
    slots = q_ref.shape[0]
    chunks = kv_ref.shape[0] // 2

    def ready(slot, _):
        q = q_ref[slot]
        qt_ref[slot] = spread_heads_t(q.T[:HW], K_ORDER)
        lane = lax.broadcasted_iota(jnp.int32, (BLK, 2 * BLK), 1) // DH
        zero = jnp.zeros_like(q)
        qm_ref[slot] = jnp.concatenate(
            [jnp.where(lane == K_ORDER.index(h), q, zero) for h in range(PER)], axis=0
        )
        grad_t = do_ref[slot]
        dot_ref[slot] = spread_heads_t(grad_t, V_ORDER)
        ordered = jnp.concatenate(
            [
                jnp.zeros((DH, BLK), bf16) if h is None else grad_t[DH * h : DH * h + DH]
                for h in V_ORDER
            ],
            axis=0,
        ).T
        dom_ref[slot] = jnp.concatenate(
            [jnp.where(lane == V_ORDER.index(h), ordered, zero) for h in range(PER)], axis=0
        )
        both = grad_t.astype(f32) * wide_ref[slot]
        delta_ref[slot] = jnp.concatenate(
            [jnp.sum(both[DH * h : DH * h + DH], axis=0, keepdims=True) for h in range(PER)],
            axis=1,
        )
        acc_ref[slot] = jnp.zeros((HW, WIDE), f32)
        return _

    lax.fori_loop(0, slots, ready, 0)

    def written(chunk, i):
        return pltpu.make_async_copy(
            packed_ref.at[chunk % 2, i], dkv_ref.at[where_ref[2 * chunk + i]], out_sem.at[chunk % 2, i]
        )

    def one_chunk(chunk, kept):
        part = load_chunk(kv_ref, where_ref, chunk)
        keys = part[:, : 2 * BLK]
        vals = part[:, BLK:]
        keys_t = keys.T[:HW]
        dk_acc[...] = jnp.zeros_like(dk_acc)
        dv_acc[...] = jnp.zeros_like(dv_acc)

        def one_slot(slot, kept):
            @pl.when((low_ref[slot] <= chunk) & (chunk <= high_ref[slot]))
            def _():
                own = text_ref[slot] * BLK + lax.broadcasted_iota(jnp.int32, (1, BLK), 1)
                scores = dot(keys, qt_ref[slot])
                probs = jnp.where(
                    visible(chunk, first_ref[slot], own), jnp.exp(scores - lse_ref[slot]), 0.0
                )
                dprobs = dot(vals, dot_ref[slot])
                dscores = (probs * (dprobs - delta_ref[slot])).astype(bf16)
                dv_acc[...] += dot(probs.astype(bf16), dom_ref[slot])
                dk_acc[...] += dot(dscores, qm_ref[slot])
                acc_ref[slot] += dot(keys_t, dscores)

            return kept

        lax.fori_loop(0, slots, one_slot, 0)
        packed = jnp.concatenate(
            [
                dk_acc[:, :BLK],
                dk_acc[:, BLK:] + dv_acc[:, :BLK],
                dv_acc[:, BLK:],
            ],
            axis=1,
        ).astype(bf16)

        @pl.when(chunk >= 2)
        def _():
            for i in range(2):
                written(chunk - 2, i).wait()

        for i in range(2):
            packed_ref[chunk % 2, i] = packed[BLK * i : BLK * i + BLK]
            written(chunk, i).start()
        return kept

    lax.fori_loop(0, chunks, one_chunk, 0)
    for last in range(2):
        for i in range(2):
            written(chunks - 2 + last, i).wait()

    def finish(slot, _):
        total = acc_ref[slot]
        kept = jnp.concatenate(
            [total[DH * h : DH * h + DH, BLK * h : BLK * h + BLK] for h in range(PER)]
            + [jnp.zeros((DH, BLK), f32)],
            axis=0,
        )
        dq_ref[slot] = kept.T.astype(bf16)
        return _

    lax.fori_loop(0, slots, finish, 0)


def attend_backward(deal, lengths, q, kv, lse, grad_t, wide):
    slots = q.shape[0]
    return pl.pallas_call(
        backward_kernel,
        out_shape=(
            jax.ShapeDtypeStruct((slots, BLK, 2 * BLK), bf16),
            jax.ShapeDtypeStruct(kv.shape, bf16),
        ),
        in_specs=[whole_smem()] * 2 + [whole_vmem()] * 5,
        out_specs=(whole_vmem(), in_hbm()),
        scratch_shapes=[
            *survey_scratch(kv.shape[0]),
            pltpu.VMEM((slots, 2 * BLK, WIDE), bf16),
            pltpu.VMEM((slots, WIDE, 2 * BLK), bf16),
            pltpu.VMEM((slots, 2 * BLK, WIDE), bf16),
            pltpu.VMEM((slots, WIDE, 2 * BLK), bf16),
            pltpu.VMEM((slots, 1, WIDE), f32),
            pltpu.VMEM((slots, HW, WIDE), f32),
            pltpu.VMEM((CHUNK, 2 * BLK), f32),
            pltpu.VMEM((CHUNK, 2 * BLK), f32),
            pltpu.VMEM((2, 2, BLK, 2 * HW), bf16),
            pltpu.SemaphoreType.DMA((2, 2)),
        ],
        compiler_params=pltpu.CompilerParams(
            vmem_limit_bytes=max(48 << 20, (17 << 20) + kv.size * 2)
        ),
        name="attend_backward",
    )(deal, lengths, q, kv, lse, grad_t, wide)


MESH = pl.DeviceIdType.MESH


def send(src, dst, out_sem, in_sem, **device):
    return pltpu.make_async_remote_copy(
        src_ref=src, dst_ref=dst, send_sem=out_sem, recv_sem=in_sem, device_id=device, device_id_type=MESH
    )


def place():
    return tuple(lax.axis_index(name) for name in ("g", "r", "core", "x"))


def seat(r, core, x):
    return (r * 2 + core) * 2 + x


AROUND = ((0, 0, 1), (0, 1, 0), (0, 1, 1), (1, 0, 0), (1, 0, 1), (1, 1, 0), (1, 1, 1))


def neighbour(r, core, x, step):
    dr, dc, dx = AROUND[step]
    return {"r": 1 - r if dr else r, "core": 1 - core if dc else core, "x": 1 - x if dx else x}


def greet(g, r, core, x, line, around=False):
    barrier = pltpu.get_barrier_semaphore()

    def hello(**device):
        pl.semaphore_signal(barrier, inc=1, device_id=device, device_id_type=MESH)

    if around:
        for step in range(len(AROUND)):
            hello(**neighbour(r, core, x, step))
    else:
        hello(core=1 - core)
        hello(x=1 - x)
        hello(r=1 - r)
    near = len(AROUND) if around else 3
    if line:
        for away in range(1, GROUPS):
            hello(g=lax.rem(g + away, GROUPS))
        pl.semaphore_wait(barrier, near + GROUPS - 1)
    else:
        pl.when(g > 0)(lambda: hello(g=g - 1))
        pl.when(g < GROUPS - 1)(lambda: hello(g=g + 1))
        pl.semaphore_wait(barrier, near + 2 - jnp.where(g == 0, 1, 0) - jnp.where(g == GROUPS - 1, 1, 0))


NEAREST = ((0, 1, 2, 3), (1, 2, 0, 3), (2, 1, 3, 0), (3, 2, 1, 0))


def nearest(g, step):
    picked = NEAREST[0][step]
    for z in range(1, GROUPS):
        picked = jnp.where(g == z, NEAREST[z][step], picked)
    return picked


def prepare(g, x, weights, lines, narrow_ref, small_ref):
    half = weights.shape[1]
    odd = lax.rem(g, 2) == 1

    def columns(i):
        low = pl.multiple_of(3 * g // 2 * BLK, BLK)
        window = weights[i, :, pl.ds(low, 2 * BLK)]
        moved = jnp.concatenate([window[:, DH:], window[:, :DH]], axis=1)
        return jnp.where(odd, moved, window)

    lane = lax.broadcasted_iota(jnp.int32, (half, 2 * BLK), 1)
    query = columns(0)
    narrow_ref[:, : 2 * BLK] = jnp.where(lane < HW, query, jnp.zeros_like(query))
    narrow_ref[:, 2 * BLK :] = pack_kv(columns(1)[:, :HW], columns(2)[:, :HW])

    def line(i):
        return lines[i][...].astype(f32).reshape(1, -1)

    zero = jnp.zeros((1, half), f32)
    small_ref[...] = jnp.zeros_like(small_ref)
    for row in range(6):
        small_ref[row : row + 1] = jnp.where(
            x == 0, jnp.concatenate([line(row), zero], axis=1), jnp.concatenate([zero, line(row)], axis=1)
        )
    ups = line(8)
    for i in range(2):
        small_ref[pl.ds(8 + 2 * x + i, 1)] = ups[:, 2 * half * i : 2 * half * i + 2 * half]

    def part(i):
        mine = jnp.where(odd, line(i)[:, HW:], line(i)[:, :HW])
        return jnp.where(g // 2 == x, mine, jnp.zeros_like(mine))

    value = part(7)
    small_ref[12:13] = jnp.concatenate(
        [part(6), jnp.zeros((1, 2 * BLK), f32), value[:, 2 * DH :], value[:, : 2 * DH], jnp.zeros((1, BLK), f32)], axis=1
    )


def gather_kernel(
    tokens_ref, query_any, key_any, value_any, wo_ref, l0, l1, l2, l3, l4, l5, l6, l7, l8,
    kv_ref, q_ref, normed_ref, small_out, wfull, wo_out,
    lined, attn_w, narrow_ref, small_ref, small_in, kvs,
    z_own, z_send, z_recv, s_sem, n_send, n_recv, kv_send, kv_recv, kv_local, w_send, w_recv, w_local, a_sem,
):
    g, r, core, x = place()
    other = 1 - x
    rows, width = tokens_ref.shape
    half = width // 2
    fourth = half // 2
    eighth = half // 4
    loads = [
        pltpu.make_async_copy(ref, attn_w.at[i], a_sem.at[i]) for i, ref in enumerate((query_any, key_any, value_any))
    ]
    for load in loads:
        load.start()
    greet(g, r, core, x, False)

    def along(source, away, sem):
        return send(lined.at[source], lined.at[source], sem, z_recv.at[source], g=g + away)

    lined[g] = tokens_ref[...]
    pl.when(g > 0)(lambda: along(g, -1, z_own.at[0]).start())
    pl.when(g < GROUPS - 1)(lambda: along(g, 1, z_own.at[1]).start())

    for load in loads:
        load.wait()
    prepare(g, x, attn_w, (l0, l1, l2, l3, l4, l5, l6, l7, l8), narrow_ref, small_ref)
    small_move = send(small_ref, small_in, s_sem.at[0], s_sem.at[1], x=other)
    small_move.start()
    mine = pl.ds(x * half + core * fourth, fourth)
    narrow_x = send(narrow_ref.at[pl.ds(core * fourth, fourth)], wfull.at[mine], n_send.at[0], n_recv.at[0], x=other)
    narrow_x.start()

    def wo_rows(owner, part):
        return wo_out.at[pl.ds(owner * half + core * fourth + part * eighth, eighth)]

    wo_x = send(wo_ref.at[pl.ds(core * fourth + r * eighth, eighth)], wo_rows(x, r), w_send.at[0], w_recv.at[0], x=other)
    wo_y = send(wo_rows(other, r), wo_rows(other, r), w_send.at[3], w_recv.at[3], r=1 - r)
    wo_s = [
        send(wo_rows(other, part), wo_rows(other, part), w_send.at[6 + i], w_recv.at[6 + i], core=1 - core)
        for i, part in enumerate((r, 1 - r))
    ]
    wo_x.start()
    locals_ = [pltpu.make_async_copy(wo_ref, wo_out.at[pl.ds(x * half, half)], w_local.at[0])]
    for item in locals_:
        item.start()

    wfull[pl.ds(x * half, half)] = narrow_ref[...]
    narrow_x.wait_recv()
    theirs = wfull.at[pl.ds(other * half + core * fourth, fourth)]
    narrow_s = send(theirs, theirs, n_send.at[1], n_recv.at[1], core=1 - core)
    narrow_s.start()
    small_move.wait_recv()
    small_out[...] = small_ref[...] + small_in[...]
    narrow_s.wait_recv()

    own = seat(r, core, x)

    def block(owner, source):
        return kv_ref.at[owner, source]

    def push(step, kind, what, **device):
        copy = send(what[0], what[1], kv_send.at[kind, step], kv_recv.at[kind, step], **device)
        copy.start()

    def settle(step, kind, owner, source):
        send(block(owner, source), block(owner, source), kv_send.at[kind, step], kv_recv.at[kind, step], x=other).wait_recv()

    def forward(step):
        source = nearest(g, step)
        by_x = block(seat(r, core, other), source)
        settle(step, 0, seat(r, core, other), source)
        if step % 2 == 0:
            push(step, 3, (by_x, by_x), r=1 - r)
        push(step, 4, (by_x, by_x), core=1 - core)
        by_y = block(seat(1 - r, core, x), source)
        settle(step, 1, seat(1 - r, core, x), source)
        if step % 2 == 1:
            push(step, 3, (by_y, by_y), x=other)
        push(step, 5, (by_y, by_y), core=1 - core)

    def forward_far(step):
        source = nearest(g, step)
        far = block(seat(1 - r, core, other), source)
        settle(step, 3, seat(1 - r, core, other), source)
        push(step, 6, (far, far), core=1 - core)

    for step in range(GROUPS):
        source = nearest(g, step)
        if step > 0:
            send(lined.at[source], lined.at[source], z_send.at[source], z_recv.at[source], x=other).wait_recv()
            pl.when((source < g) & (g < GROUPS - 1))(lambda: along(source, 1, z_send.at[source]).start())
            pl.when((source > g) & (g > 0))(lambda: along(source, -1, z_send.at[source]).start())
        values = lined[source].astype(f32)
        normed = layer_norm(values, small_out[0:1], small_out[1:2]).astype(bf16)
        normed_ref[source] = normed
        both = dot(normed, wfull[...]) + small_out[12:13, : wfull.shape[1]]
        q_ref[source] = (both[:, : 2 * BLK] * SCALE).astype(bf16)
        kvs[step] = both[:, 2 * BLK :].astype(bf16)
        here = (kvs.at[step], block(own, source))
        push(step, 0, here, x=other)
        push(step, 1, here, r=1 - r)
        push(step, 2, here, core=1 - core)
        pltpu.make_async_copy(kvs.at[step], block(own, source), kv_local.at[step]).start()
        if step > 0:
            forward(step - 1)
        if step > 1:
            forward_far(step - 2)
    wo_x.wait_recv()
    wo_y.start()
    wo_s[0].start()
    forward(GROUPS - 1)
    forward_far(GROUPS - 2)
    send(wo_rows(other, 1 - r), wo_rows(other, 1 - r), w_send.at[3], w_recv.at[3], r=1 - r).wait_recv()
    wo_s[1].start()
    forward_far(GROUPS - 1)

    for step in range(GROUPS):
        source = nearest(g, step)
        pltpu.make_async_copy(kvs.at[step], block(own, source), kv_local.at[step]).wait()
        settle(step, 2, seat(r, 1 - core, x), source)
        settle(step, 4, seat(r, 1 - core, other), source)
        settle(step, 5, seat(1 - r, 1 - core, x), source)
        settle(step, 6, seat(1 - r, 1 - core, other), source)
        for kind in range(7):
            send(kvs.at[step], block(own, source), kv_send.at[kind, step], kv_recv.at[kind, step], x=other).wait_send()
    pl.when(g > 0)(lambda: along(g, -1, z_own.at[0]).wait_send())
    pl.when(g < GROUPS - 1)(lambda: along(g, 1, z_own.at[1]).wait_send())
    for step in range(1, GROUPS):
        source = nearest(g, step)
        passed = ((source < g) & (g < GROUPS - 1)) | ((source > g) & (g > 0))
        pl.when(passed)(lambda: send(lined.at[source], lined.at[source], z_send.at[source], z_recv.at[source], x=other).wait_send())
    small_move.wait_send()
    narrow_x.wait_send()
    narrow_s.wait_send()
    for item in locals_:
        item.wait()
    for item in (wo_x, wo_y, *wo_s):
        item.wait_send()
    for i, part in enumerate((r, 1 - r)):
        there = wo_out.at[pl.ds(other * half + (1 - core) * fourth + part * eighth, eighth)]
        send(there, there, w_send.at[6 + i], w_recv.at[6 + i], core=1 - core).wait_recv()


def anywhere():
    return pl.BlockSpec(memory_space=pl.ANY)


def in_hbm():
    return pl.BlockSpec(memory_space=pltpu.HBM)


def gather(tokens, query, key, value, wo, *lines):
    rows, width = tokens.shape
    wide = 2 * BLK + 2 * HW
    small = (16, width)
    dma = pltpu.SemaphoreType.DMA
    return pl.pallas_call(
        gather_kernel,
        out_shape=(
            jax.ShapeDtypeStruct((8, GROUPS, rows, 2 * HW), bf16),
            jax.ShapeDtypeStruct((GROUPS, rows, 2 * BLK), bf16),
            jax.ShapeDtypeStruct((GROUPS, rows, width), bf16),
            jax.ShapeDtypeStruct(small, f32),
            jax.ShapeDtypeStruct((width, wide), bf16),
            jax.ShapeDtypeStruct((width, width), bf16),
        ),
        in_specs=[whole_vmem(), *[in_hbm()] * 4, *[whole_vmem()] * len(lines)],
        out_specs=(anywhere(), *(whole_vmem(),) * 5),
        scratch_shapes=[
            pltpu.VMEM((GROUPS, rows, width), bf16),
            pltpu.VMEM((3, width // 2, width), bf16),
            pltpu.VMEM((width // 2, wide), bf16),
            pltpu.VMEM(small, f32),
            pltpu.VMEM(small, f32),
            pltpu.VMEM((GROUPS, rows, 2 * HW), bf16),
            dma((2,)), dma((GROUPS,)), dma((GROUPS,)), dma((2,)), dma((2,)), dma((2,)),
            dma((7, GROUPS)), dma((7, GROUPS)), dma((GROUPS,)), dma((8,)), dma((8,)), dma((2,)), dma((3,)),
        ],
        compiler_params=pltpu.CompilerParams(
            collective_id=0, has_side_effects=True, vmem_limit_bytes=60 << 20
        ),
        name="gather",
    )(tokens, query, key, value, wo, *lines)


def erf_parts(values):
    below = 0.5 * (1.0 + lax.erf(values * ROOT_HALF))
    return below, PDF_SCALE * jnp.exp(-0.5 * values * values)


PARTS = 8
UNIT = 216
KEPT = 168


def dense_kernel(
    out_t_ref, tokens_ref, cot_ref, cot_x_ref, small_ref, wo_ref, up_mine, up_other, down_any,
    base_ref, x_give_ref, middle_grad_ref, grad_t_ref, keep_ref, give_ref, far_ref, sums_ref,
    down_ref, up_ref, attn_in, attn_t, cots, h2s, mid_ref, n2_ref, scales, part_y, part_d, in_y, in_d, pass_y, pass_d,
    x_y, x_d, hids, dus, branch_ref, grad_out, wo_keep, wo_give, wo_in, wo_pass, wo_x,
    l_sem, a_send, a_recv, c_send, c_recv, h_send, h_recv, y_send, y_recv, d_send, d_recv, o_send, o_recv,
    w_send, w_recv,
):
    g, r, core, x = place()
    other, sib = 1 - x, 1 - core
    rows, width = tokens_ref.shape
    half = width // 2
    fourth = half // 2
    loads = [
        pltpu.make_async_copy(
            down_any.at[pl.ds(pl.multiple_of(core * width, width), width)], down_ref, l_sem.at[0]
        ),
        pltpu.make_async_copy(up_mine, up_ref.at[pl.ds(x * half, half)], l_sem.at[1]),
        pltpu.make_async_copy(up_other, up_ref.at[pl.ds(other * half, half)], l_sem.at[2]),
    ]
    for load in loads:
        load.start()
    greet(g, r, core, x, True)
    pending = []

    def begin(src, dst, out_sem, in_sem, **device):
        move = send(src, dst, out_sem, in_sem, **device)
        move.start()
        pending.append(move)
        return move

    def other_group(away):
        return lax.rem(g + away, GROUPS)

    def rows_of(b):
        return pl.ds(BLK * b, BLK)

    for b in range(2):
        for away in range(1, GROUPS):
            to = other_group(away)
            begin(out_t_ref.at[2 * to + b], attn_in.at[g, b], a_send.at[b, away], a_recv.at[b, g], g=to)
        attn_in[g, b] = out_t_ref[2 * g + b]
        cots[b, 0] = cot_ref[rows_of(b)]
        cots[b, 2] = cot_x_ref[rows_of(b)]
    cot_moves = [
        begin(cots.at[:, 2 * i], cots.at[:, 2 * i + 1], c_send.at[i], c_recv.at[i], core=sib) for i in range(2)
    ]
    sums_ref[...] = jnp.zeros_like(sums_ref)
    sums_ref[5:6] = jnp.sum(cot_ref[...].astype(f32), axis=0, keepdims=True)
    h2_moves = []

    def norm(b):
        for away in range(1, GROUPS):
            source = other_group(away)
            arrived(attn_in.at[source, b], a_send.at[b, away], a_recv.at[b, source], x)
        for source in range(GROUPS):
            attn_t[HW * source : HW * source + HW, BLK * b : BLK * b + BLK] = attn_in[source, b]
        middle = (
            tokens_ref[rows_of(b)].astype(f32)
            + outer(attn_t[:, BLK * b : BLK * b + BLK], wo_ref[...])
            + small_ref[2:3]
        )
        mid_ref[b] = middle
        mean = jnp.mean(middle, axis=-1, keepdims=True)
        centred = middle - mean
        scale = lax.rsqrt(jnp.mean(centred * centred, axis=-1, keepdims=True) + EPS)
        scales[b] = scale
        n2_ref[b] = centred * scale
        h2s[b, 0] = (n2_ref[b] * small_ref[3:4] + small_ref[4:5]).astype(bf16)
        h2_moves.append(
            (
                begin(h2s.at[b, 0], h2s.at[b, 2], h_send.at[b, 1], h_recv.at[b, 1], x=other),
                begin(h2s.at[b, 0], h2s.at[b, 1], h_send.at[b, 0], h_recv.at[b, 0], core=sib),
            )
        )

    def pass_on(b):
        h2_moves[b][0].wait_recv()
        return begin(h2s.at[b, 2], h2s.at[b, 3], h_send.at[b, 2], h_recv.at[b, 2], core=sib)

    bias_row = 8 + 2 * x + core

    def pair_of(ref, b, pair):
        return ref[b, 2 * pair : 2 * pair + 2].reshape(2 * BLK, width)

    def forward_backward(b, pair):
        cot = pair_of(cots, b, pair)
        expanded = dot(pair_of(h2s, b, pair), up_ref[...]) + small_ref[pl.ds(bias_row, 1)]
        below, density = erf_parts(expanded)
        hidden = (expanded * below).astype(bf16)
        hids[b, pair] = hidden
        slope = below + expanded * density
        grad_hidden = inner(cot, down_ref[...]).astype(bf16).astype(f32)
        grad_expand = (grad_hidden * slope).astype(bf16)
        dus[b, pair] = grad_expand
        part_d[b, pair] = inner(grad_expand, up_ref[...])
        part_y[b, pair] = dot(hidden, down_ref[...])
        sums_ref[pl.ds(bias_row, 1)] += jnp.sum(grad_expand.astype(f32), axis=0, keepdims=True)

    d_moves, y_passes = [None, None], [None, None]

    def near_pair(b):
        if b == 0:
            cot_moves[0].wait_recv()
        h2_moves[b][1].wait_recv()
        forward_backward(b, 0)
        return begin(part_d.at[b, 0, pl.ds(BLK, BLK)], in_d.at[b], d_send.at[b, 0], d_recv.at[b, 0], core=sib)

    def far_pair(b, passed):
        if b == 0:
            cot_moves[1].wait_recv()
        passed.wait_recv()
        forward_backward(b, 1)
        x_d[b, 0] = part_d[b, 1, BLK:].astype(bf16)
        across = begin(x_d.at[b, 0], pass_d.at[b], d_send.at[b, 1], d_recv.at[b, 1], core=sib)
        x_y[b] = part_y[b, 1, BLK:].astype(bf16)
        y_passes[b] = begin(x_y.at[b], pass_y.at[b], y_send.at[b, 1], y_recv.at[b, 1], core=sib)
        across.wait_recv()
        x_d[b, 1] = (part_d[b, 1, :BLK] + pass_d[b].astype(f32)).astype(bf16)
        return begin(x_d.at[b, 1], x_d.at[b, 2], d_send.at[b, 2], d_recv.at[b, 2], x=other)

    def back(b, near, far):
        near.wait_recv()
        far.wait_recv()
        grad_second = part_d[b, 0, :BLK] + in_d[b] + x_d[b, 2].astype(f32)
        n2 = n2_ref[b]
        sums_ref[3:4] += jnp.sum(grad_second * n2, axis=0, keepdims=True)
        sums_ref[4:5] += jnp.sum(grad_second, axis=0, keepdims=True)
        pulled = grad_second * small_ref[3:4]
        inward = (
            pulled - jnp.mean(pulled, axis=-1, keepdims=True) - n2 * jnp.mean(pulled * n2, axis=-1, keepdims=True)
        )
        grad_middle = cot_ref[rows_of(b)].astype(f32) + inward * scales[b]
        middle_grad_ref[rows_of(b)] = grad_middle
        branch = grad_middle.astype(bf16)
        branch_ref[rows_of(b)] = branch
        sums_ref[2:3] += jnp.sum(branch.astype(f32), axis=0, keepdims=True)
        grad_out_t = inner(wo_ref[...], branch).astype(bf16)
        for group in range(GROUPS):
            grad_out[group, b] = grad_out_t[HW * group : HW * group + HW]
        for away in range(1, GROUPS):
            to = other_group(away)
            begin(grad_out.at[to, b], grad_t_ref.at[2 * g + b], o_send.at[b, away], o_recv.at[b, g], g=to)
        grad_t_ref[2 * g + b] = grad_out[g, b]

    norm(0)
    norm(1)
    for load in loads:
        load.wait()
    near = [near_pair(0), None]
    passed = [pass_on(0), None]
    near[1] = near_pair(1)
    far = [far_pair(0, passed[0]), None]
    passed[1] = pass_on(1)
    far[1] = far_pair(1, passed[1])

    def over_rows(left, right):
        total = None
        for b in range(2):
            for pair in range(2):
                term = outer(left(b, pair), right(b, pair))
                total = term if total is None else total + term
        return total.astype(bf16)

    def parts(write):
        for y in range(2):
            pl.when(r == y)(lambda: write(keep_ref, y))
            pl.when(r != y)(lambda: write(give_ref, y))

    down_grad = over_rows(lambda b, pair: hids[b, pair], lambda b, pair: pair_of(cots, b, pair))

    def write_down(ref, y):
        for z in range(GROUPS):
            p = y * GROUPS + z
            ref[z, 0:96] = down_grad[96 * p : 96 * p + 96]

    parts(write_down)
    back(0, near[0], far[0])
    up_grad = over_rows(lambda b, pair: pair_of(h2s, b, pair), lambda b, pair: dus[b, pair])

    def up_part(p, h):
        return up_grad[half * h + 48 * p : half * h + 48 * p + 48]

    def write_up(y, h):
        @pl.when((r == y) & (x == h))
        def _():
            for z in range(GROUPS):
                keep_ref[z, 96:144] = up_part(y * GROUPS + z, h)

        @pl.when((r != y) & (x == h))
        def _():
            for z in range(GROUPS):
                give_ref[z, 96:144] = up_part(y * GROUPS + z, h)

        @pl.when((r == y) & (x != h))
        def _():
            for z in range(GROUPS):
                x_give_ref[rows + 48 * z : rows + 48 * z + 48] = up_part(y * GROUPS + z, h)

        @pl.when((r != y) & (x != h))
        def _():
            for z in range(GROUPS):
                far_ref[z] = up_part(y * GROUPS + z, h)

    for y in range(2):
        for h in range(2):
            write_up(y, h)
    back(1, near[1], far[1])

    for owner in range(2):
        for c in range(2):
            piece = dot(attn_t[half * owner + fourth * c : half * owner + fourth * c + fourth], branch_ref[...])

            @pl.when(core == c)
            def _():
                wo_keep[owner] = piece

            @pl.when(core != c)
            def _():
                wo_give[owner] = piece.astype(bf16)

    w_sib = begin(wo_give, wo_in, w_send.at[0], w_recv.at[0], core=sib)
    y_sibs = [
        begin(part_y.at[b, 0, pl.ds(BLK, BLK)], in_y.at[b], y_send.at[b, 0], y_recv.at[b, 0], core=sib)
        for b in range(2)
    ]
    w_sib.wait_recv()
    wo_pass[...] = (wo_keep[other] + wo_in[other].astype(f32)).astype(bf16)
    w_x = begin(wo_pass, wo_x, w_send.at[1], w_recv.at[1], x=other)
    for b in range(2):
        y_passes[b].wait_recv()
        x_give_ref[rows_of(b)] = (part_y[b, 1, :BLK] + pass_y[b].astype(f32)).astype(bf16)
        y_sibs[b].wait_recv()
        base_ref[rows_of(b)] = mid_ref[b] + part_y[b, 0, :BLK] + in_y[b] + small_ref[5:6]
    mine = wo_keep[x] + wo_in[x].astype(f32)
    for b in range(2):
        for away in range(1, GROUPS):
            source = other_group(away)
            arrived(grad_t_ref.at[2 * source + b], o_send.at[b, away], o_recv.at[b, source], x)
    w_x.wait_recv()
    wo_sum = (mine + wo_x[...].astype(f32)).astype(bf16)

    def write_wo(ref, y):
        for z in range(GROUPS):
            p = y * GROUPS + z
            ref[z, 144:KEPT] = wo_sum[24 * p : 24 * p + 24]

    parts(write_wo)
    for move in pending:
        move.wait_send()


def dense(out_t, tokens, cot, cot_x, small, wo, up_mine, up_other, down):
    rows, width = tokens.shape
    dma = pltpu.SemaphoreType.DMA
    full = (rows, width)
    part = (BLK, width)
    pair = (2 * BLK, width)
    fourth = (width // 4, width)
    return pl.pallas_call(
        dense_kernel,
        out_shape=(
            jax.ShapeDtypeStruct(full, f32),
            jax.ShapeDtypeStruct((rows + 48 * GROUPS, width), bf16),
            jax.ShapeDtypeStruct(full, f32),
            jax.ShapeDtypeStruct(out_t.shape, bf16),
            jax.ShapeDtypeStruct((GROUPS, KEPT, width), bf16),
            jax.ShapeDtypeStruct((GROUPS, KEPT, width), bf16),
            jax.ShapeDtypeStruct((GROUPS, 48, width), bf16),
            jax.ShapeDtypeStruct(small.shape, f32),
        ),
        in_specs=[whole_vmem()] * 6 + [anywhere()] * 3,
        out_specs=(whole_vmem(),) * 8,
        scratch_shapes=[
            pltpu.VMEM((width, width), bf16),
            pltpu.VMEM((width, width), bf16),
            pltpu.VMEM((GROUPS, 2, HW, BLK), bf16),
            pltpu.VMEM((width, rows), bf16),
            pltpu.VMEM((2, 4, *part), bf16),
            pltpu.VMEM((2, 4, *part), bf16),
            pltpu.VMEM((2, *part), f32),
            pltpu.VMEM((2, *part), f32),
            pltpu.VMEM((2, BLK, 1), f32),
            pltpu.VMEM((2, 2, *pair), f32),
            pltpu.VMEM((2, 2, *pair), f32),
            pltpu.VMEM((2, *part), f32),
            pltpu.VMEM((2, *part), f32),
            pltpu.VMEM((2, *part), bf16),
            pltpu.VMEM((2, *part), bf16),
            pltpu.VMEM((2, *part), bf16),
            pltpu.VMEM((2, 3, *part), bf16),
            pltpu.VMEM((2, 2, *pair), bf16),
            pltpu.VMEM((2, 2, *pair), bf16),
            pltpu.VMEM(full, bf16),
            pltpu.VMEM((GROUPS, 2, HW, BLK), bf16),
            pltpu.VMEM((2, *fourth), f32),
            pltpu.VMEM((2, *fourth), bf16),
            pltpu.VMEM((2, *fourth), bf16),
            pltpu.VMEM(fourth, bf16),
            pltpu.VMEM(fourth, bf16),
            dma((3,)), dma((2, GROUPS)), dma((2, GROUPS)), dma((2,)), dma((2,)), dma((2, 3)), dma((2, 3)),
            dma((2, 2)), dma((2, 2)), dma((2, 3)), dma((2, 3)), dma((2, GROUPS)), dma((2, GROUPS)), dma((2,)), dma((2,)),
        ],
        compiler_params=pltpu.CompilerParams(
            collective_id=1, has_side_effects=True, vmem_limit_bytes=40 << 20
        ),
        name="dense",
    )(out_t, tokens, cot, cot_x, small, wo, up_mine, up_other, down)


FARTHEST = ((3, 2, 1, 0), (3, 0, 2, 1), (0, 3, 1, 2), (0, 1, 2, 3))


def farthest(g, step):
    picked = FARTHEST[0][step]
    for z in range(1, GROUPS):
        picked = jnp.where(g == z, FARTHEST[z][step], picked)
    return picked


class Chain:
    def __init__(self, g, x, total, parts, inward, outward, out_sem, in_sem):
        self.g, self.x, self.total, self.parts = g, x, total, parts
        self.inward, self.outward, self.out_sem, self.in_sem = inward, outward, out_sem, in_sem

    def move(self, to, way):
        return send(
            self.outward.at[to], self.inward.at[way, to], self.out_sem.at[to], self.in_sem.at[way, to],
            g=jnp.clip(self.g + (1 if way == 0 else -1), 0, GROUPS - 1),
        )

    def step(self, to):
        g = self.g
        self.total[...] = self.parts[to].astype(f32)

        def take(way):
            arrived(self.inward.at[way, to], self.out_sem.at[to], self.in_sem.at[way, to], self.x)
            self.total[...] += self.inward[way, to].astype(f32)

        pl.when((to >= g) & (g > 0))(lambda: take(0))
        pl.when((to <= g) & (g < GROUPS - 1))(lambda: take(1))

        @pl.when(to != g)
        def _():
            self.outward[to] = self.total[...].astype(bf16)

        pl.when(to > g)(lambda: self.move(to, 0).start())
        pl.when(to < g)(lambda: self.move(to, 1).start())

    def finish(self):
        for step in range(GROUPS - 1):
            to = farthest(self.g, step)
            left(self.outward.at[to], self.out_sem.at[to], self.in_sem.at[0, to], self.x)


class Ring:
    def __init__(self, g, x, slot, own_sem, out_sem, in_sem):
        self.g, self.x, self.slot = g, x, slot
        self.own_sem, self.out_sem, self.in_sem = own_sem, out_sem, in_sem

    def move(self, source, way, sem):
        return send(
            self.slot(source), self.slot(source), sem, self.in_sem.at[source],
            g=jnp.clip(self.g + way, 0, GROUPS - 1),
        )

    def start(self):
        g = self.g
        pl.when(g > 0)(lambda: self.move(g, -1, self.own_sem.at[0]).start())
        pl.when(g < GROUPS - 1)(lambda: self.move(g, 1, self.own_sem.at[1]).start())

    def step(self, step):
        g, source = self.g, nearest(self.g, step)
        arrived(self.slot(source), self.out_sem.at[source], self.in_sem.at[source], self.x)
        pl.when((source < g) & (g < GROUPS - 1))(lambda: self.move(source, 1, self.out_sem.at[source]).start())
        pl.when((source > g) & (g > 0))(lambda: self.move(source, -1, self.out_sem.at[source]).start())
        return source

    def finish(self):
        g = self.g
        for i, there in enumerate((g > 0, g < GROUPS - 1)):
            pl.when(there)(lambda: left(self.slot(g), self.own_sem.at[i], self.in_sem.at[g], self.x))
        for step in range(1, GROUPS):
            source = nearest(g, step)
            passed = ((source < g) & (g < GROUPS - 1)) | ((source > g) & (g > 0))
            pl.when(passed)(
                lambda: left(self.slot(source), self.out_sem.at[source], self.in_sem.at[source], self.x)
            )


def arrived(what, out_sem, in_sem, x):
    send(what, what, out_sem, in_sem, x=1 - x).wait_recv()


def left(what, out_sem, in_sem, x):
    send(what, what, out_sem, in_sem, x=1 - x).wait_send()


def scatter_kernel(
    dkv_ref, dq_any, normed_any, wfull_any, tokens_any, mgrad_any, keep_any, over_any, near_any, far_any, small_ref, sums_in,
    tokens_grad_ref, big_ref, qout_ref, kvout_ref, sums_ref,
    dq_ref, normed_ref, wfull_ref, tokens_ref, mgrad_ref, kept, over, near, far,
    own_kv, sib_kv, keep_x, give_x, in_x, give_y, in_y, part_a, total_a, inward_a, outward_a, wg_kv,
    by_sum, total_b, inward_b, outward_b, unit,
    q_keep, q_give, q_in, q_pass, q_x, q_y, q_sum, v_keep, v_give, v_in, v_pass, v_x, v_y, v_sum,
    sums_got, late, late_sum, late_got,
    load_sem, own_sem, k_send, k_recv, x_send, x_recv, y_send, y_recv, ca_send, ca_recv,
    cb_send, cb_recv, rb_own, rb_send, rb_recv,
    fy_send, fy_recv, fs_send, fs_recv,
    q_send, q_recv, rq_own, rq_send, rq_recv, qs_send, qs_recv,
    v_send, v_recv, rv_own, rv_send, rv_recv, vs_send, vs_recv,
    s_send, s_recv, t_send, t_recv, l_sem,
):
    g, r, core, x = place()
    other, sib, far_r = 1 - x, 1 - core, 1 - r
    rows, width = tokens_ref.shape
    half = width // 2
    fourth = half // 2
    wide_q = 2 * BLK
    loads = [
        pltpu.make_async_copy(what, where, load_sem.at[i])
        for i, (what, where) in enumerate(
            (
                (keep_any, kept), (over_any, over), (near_any.at[pl.ds(rows, 48 * GROUPS)], near), (far_any, far),
                (dq_any, dq_ref), (normed_any, normed_ref), (wfull_any, wfull_ref), (tokens_any, tokens_ref),
                (mgrad_any, mgrad_ref),
            )
        )
    ]
    for load in loads:
        load.start()
    greet(g, r, core, x, True, True)
    pending = []

    def begin(src, dst, out_sem, in_sem, **device):
        move = send(src, dst, out_sem, in_sem, **device)
        move.start()
        pending.append(move)
        return move

    def settled(move):
        move.wait_recv()
        move.wait_send()
        pending[:] = [item for item in pending if item is not move]

    kv_moves = []
    for i in range(GROUPS):
        c = farthest(g, i)
        for spot in range(4):
            own = pltpu.make_async_copy(
                dkv_ref.at[seat(spot // 2, core, spot % 2), c], own_kv.at[i, spot], own_sem.at[i, spot]
            )
            own.start()
            across = begin(
                dkv_ref.at[seat(spot // 2, sib, spot % 2), c], sib_kv.at[i, spot],
                k_send.at[i, spot], k_recv.at[i, spot], core=sib,
            )
            kv_moves.append((own, across))

    def split(total, keep, give):
        for owner in range(2):
            for c in range(2):
                low = half * owner + fourth * c
                chunk = total[low : low + fourth]

                @pl.when(core == c)
                def _():
                    keep[owner] = chunk

                @pl.when(core != c)
                def _():
                    give[owner] = chunk.astype(bf16)

    def scaled(c):
        return dq_ref[c] * bf16(SCALE)

    q_move = send(q_give, q_in, q_send.at[0], q_recv.at[0], core=sib)

    def query_grad():
        loads[4].wait()
        loads[5].wait()
        query_total = outer(normed_ref[0], scaled(0))
        for c in range(1, GROUPS):
            query_total += outer(normed_ref[c], scaled(c))
        split(query_total, q_keep, q_give)
        q_move.start()
        line_q = scaled(0).astype(f32)
        for c in range(1, GROUPS):
            line_q += scaled(c).astype(f32)
        sums_ref[pl.ds(16 + g, 1), 0:wide_q] = jnp.sum(line_q, axis=0, keepdims=True)

    sums_ref[...] = jnp.zeros_like(sums_ref)
    sums_ref[0:16] = sums_in[...]
    wg_kv[...] = jnp.zeros_like(wg_kv)

    def q_slot(z):
        return qout_ref.at[core, z]

    def v_slot(z):
        return kvout_ref.at[core, z]

    def b_slot(z):
        return big_ref.at[core, r, z]

    ring_q = Ring(g, x, q_slot, rq_own, rq_send, rq_recv)
    ring_v = Ring(g, x, v_slot, rv_own, rv_send, rv_recv)
    ring_b = Ring(g, x, b_slot, rb_own, rb_send, rb_recv)

    def store(value_ref, slot, sem):
        copy = pltpu.make_async_copy(value_ref, slot, sem)
        copy.start()
        copy.wait()

    def spread_b(z, step):
        begin(b_slot(z), b_slot(z), fy_send.at[step], fy_recv.at[step], r=far_r)
        begin(b_slot(z), b_slot(z), fs_send.at[0, step], fs_recv.at[0, step], core=sib)

    def spread_far(step):
        what = big_ref.at[core, far_r, nearest(g, step)]
        arrived(what, fy_send.at[step], fy_recv.at[step], x)
        begin(what, what, fs_send.at[1, step], fs_recv.at[1, step], core=sib)

    def on_ring_b(step):
        spread_b(ring_b.step(step), step)

    def on_ring_q(step):
        z = ring_q.step(step)
        begin(q_slot(z), q_slot(z), qs_send.at[step], qs_recv.at[step], core=sib)

    def on_ring_v(step):
        z = ring_v.step(step)
        begin(v_slot(z), v_slot(z), vs_send.at[step], vs_recv.at[step], core=sib)

    chain_a = Chain(g, x, total_a, part_a, inward_a, outward_a, ca_send, ca_recv)
    chain_b = Chain(g, x, total_b, by_sum, inward_b, outward_b, cb_send, cb_recv)
    at_end = (g == 0) | (g == GROUPS - 1)
    between = jnp.logical_not(at_end)

    def steps(chain, *which):
        for i in which:
            chain.step(farthest(g, i))

    def on_sibling(i):
        for own, across in kv_moves[4 * i : 4 * i + 4]:
            own.wait()
            across.wait_recv()

        def total(row, column):
            spot = 2 * row + column
            return own_kv[i, spot].astype(f32) + sib_kv[i, spot].astype(f32)

        for k in range(2):
            give_x[i, k] = (total(k, other) if i % 2 == 0 else total(far_r, k)).astype(bf16)
            keep_x[i, k] = total(k, x) if i % 2 == 0 else total(r, k)

    def go_first(i):
        along = {"x": other} if i % 2 == 0 else {"r": far_r}
        begin(give_x.at[i], in_x.at[i], x_send.at[i], x_recv.at[i], **along)

    def on_first(i):
        arrived(in_x.at[i], x_send.at[i], x_recv.at[i], x)
        away, stay, along = (far_r, r, {"r": far_r}) if i % 2 == 0 else (other, x, {"x": other})
        give_y[i] = (keep_x[i, away] + in_x[i, away].astype(f32)).astype(bf16)
        begin(give_y.at[i], in_y.at[i], y_send.at[i], y_recv.at[i], **along)
        keep_x[i, stay] += in_x[i, stay].astype(f32)

    def on_second(i):
        c = farthest(g, i)
        arrived(in_y.at[i], y_send.at[i], y_recv.at[i], x)
        both = (keep_x[i, r if i % 2 == 0 else x] + in_y[i].astype(f32)).astype(bf16)
        part_a[c] = inner(scaled(c), wfull_ref[:, :wide_q]) + inner(both, wfull_ref[:, wide_q:])
        wg_kv[...] += outer(normed_ref[c], both)
        sums_ref[pl.ds(16 + g, 1), wide_q : wide_q + 2 * HW] += jnp.sum(both.astype(f32), axis=0, keepdims=True)

    for load in loads[:4]:
        load.wait()
    own_up = pl.ds(pl.multiple_of(96 + 48 * x, 48), 48)
    their_up = pl.ds(pl.multiple_of(96 + 48 * other, 48), 48)
    for z in range(GROUPS):
        pair = kept[z].astype(f32) + over[z].astype(f32)
        by_sum[z, 0:96] = pair[0:96]
        by_sum[z, own_up] = pair[96:144]
        by_sum[z, 192:UNIT] = pair[144:KEPT]
        by_sum[z, their_up] = near[48 * z : 48 * z + 48].astype(f32) + far[z].astype(f32)
    pl.when(at_end)(lambda: steps(chain_b, 0, 1, 2))
    on_sibling(0)
    go_first(0)
    on_sibling(1)
    go_first(1)
    on_sibling(2)
    on_sibling(3)
    pl.when(between)(lambda: steps(chain_b, 0))
    query_grad()
    on_first(0)
    on_first(1)
    go_first(2)
    go_first(3)
    pl.when(between)(lambda: steps(chain_b, 1, 2))
    settled(q_move)
    q_pass[...] = (q_keep[other] + q_in[other].astype(f32)).astype(bf16)
    q_across = begin(q_pass, q_x, q_send.at[1], q_recv.at[1], x=other)
    loads[6].wait()
    on_second(0)
    on_second(1)
    pl.when(at_end)(lambda: steps(chain_a, 0))
    chain_b.step(g)
    unit[...] = total_b[...].astype(bf16)
    store(unit, b_slot(g), l_sem.at[0])
    ring_b.start()
    spread_b(g, 0)
    pl.when(at_end)(lambda: steps(chain_a, 1))
    on_first(2)
    on_first(3)
    q_across.wait_recv()
    q_sum[...] = (q_keep[x] + q_in[x].astype(f32) + q_x[...].astype(f32)).astype(bf16)
    q_over = begin(q_sum, q_y, q_send.at[2], q_recv.at[2], r=far_r)
    pl.when(between)(lambda: steps(chain_a, 0))
    on_second(2)
    on_second(3)
    pl.when(at_end)(lambda: steps(chain_a, 2))
    split(wg_kv, v_keep, v_give)
    v_move = begin(v_give, v_in, v_send.at[0], v_recv.at[0], core=sib)
    s_sib = begin(sums_ref, sums_got.at[0], s_send.at[0], s_recv.at[0], core=sib)
    spread_far(0)
    settled(q_over)
    q_sum[...] = (q_sum[...].astype(f32) + q_y[...].astype(f32)).astype(bf16)
    store(q_sum, q_slot(g), l_sem.at[0])
    ring_q.start()
    begin(q_slot(g), q_slot(g), qs_send.at[0], qs_recv.at[0], core=sib)
    on_ring_b(1)
    v_move.wait_recv()
    v_pass[...] = (v_keep[other] + v_in[other].astype(f32)).astype(bf16)
    v_across = begin(v_pass, v_x, v_send.at[1], v_recv.at[1], x=other)
    settled(s_sib)
    sums_ref[...] += sums_got[0]
    s_x = begin(sums_ref, sums_got.at[1], s_send.at[1], s_recv.at[1], x=other)
    pl.when(between)(lambda: steps(chain_a, 1))
    v_across.wait_recv()
    v_sum[...] = (v_keep[x] + v_in[x].astype(f32) + v_x[...].astype(f32)).astype(bf16)
    v_over = begin(v_sum, v_y, v_send.at[2], v_recv.at[2], r=far_r)
    settled(s_x)
    sums_ref[...] += sums_got[1]
    s_y = begin(sums_ref, sums_got.at[2], s_send.at[2], s_recv.at[2], r=far_r)
    on_ring_b(2)
    pl.when(between)(lambda: steps(chain_a, 2))
    settled(v_over)
    v_sum[...] = (v_sum[...].astype(f32) + v_y[...].astype(f32)).astype(bf16)
    store(v_sum, v_slot(g), l_sem.at[0])
    ring_v.start()
    begin(v_slot(g), v_slot(g), vs_send.at[0], vs_recv.at[0], core=sib)
    settled(s_y)
    sums_ref[...] += sums_got[2]
    for away in range(1, GROUPS):
        begin(
            sums_ref, sums_got.at[2 + away], s_send.at[2 + away], s_recv.at[2 + away],
            g=lax.rem(g + away, GROUPS),
        )
    spread_far(1)
    on_ring_q(1)
    on_ring_b(3)
    chain_a.step(g)

    loads[7].wait()
    loads[8].wait()
    grad_first = total_a[...]
    values = tokens_ref[...].astype(f32)
    mean = jnp.mean(values, axis=-1, keepdims=True)
    centred = values - mean
    scale = lax.rsqrt(jnp.mean(centred * centred, axis=-1, keepdims=True) + EPS)
    n1 = centred * scale
    pulled = grad_first * small_ref[0:1]
    inward = pulled - jnp.mean(pulled, axis=-1, keepdims=True) - n1 * jnp.mean(pulled * n1, axis=-1, keepdims=True)
    tokens_grad_ref[...] = mgrad_ref[...] + inward * scale
    late[...] = jnp.zeros_like(late)
    late[0:1] = jnp.sum(grad_first * n1, axis=0, keepdims=True)
    late[1:2] = jnp.sum(grad_first, axis=0, keepdims=True)
    for step in range(len(AROUND)):
        begin(late, late_got.at[step], t_send.at[step], t_recv.at[step], **neighbour(r, core, x, step))
    on_ring_v(1)
    on_ring_q(2)
    on_ring_q(3)
    spread_far(2)
    on_ring_v(2)
    late_sum[...] = late[...]
    for step in range(len(AROUND)):
        arrived(late_got.at[step], t_send.at[step], t_recv.at[step], x)
        late_sum[...] += late_got[step]
    first_z = len(AROUND) - 1
    for away in range(1, GROUPS):
        begin(
            late_sum, late_got.at[first_z + away], t_send.at[first_z + away], t_recv.at[first_z + away],
            g=lax.rem(g + away, GROUPS),
        )
    on_ring_v(3)
    spread_far(3)

    for away in range(1, GROUPS):
        arrived(sums_got.at[2 + away], s_send.at[2 + away], s_recv.at[2 + away], x)
        arrived(late_got.at[first_z + away], t_send.at[first_z + away], t_recv.at[first_z + away], x)
    for step in range(GROUPS):
        z = nearest(g, step)
        arrived(qout_ref.at[sib, z], qs_send.at[step], qs_recv.at[step], x)
        arrived(kvout_ref.at[sib, z], vs_send.at[step], vs_recv.at[step], x)
        arrived(big_ref.at[sib, r, z], fs_send.at[0, step], fs_recv.at[0, step], x)
        arrived(big_ref.at[sib, far_r, z], fs_send.at[1, step], fs_recv.at[1, step], x)
    for move in pending:
        move.wait_send()
    for item in (chain_a, chain_b, ring_q, ring_v, ring_b):
        item.finish()
    sums_ref[...] += sums_got[3] + sums_got[4] + sums_got[5]
    total = late_sum[...] + late_got[first_z + 1] + late_got[first_z + 2] + late_got[first_z + 3]
    sums_ref[0:2] = total[0:2]


def scatter(dkv, dq, normed, wfull, tokens, mgrad, small, keep, over, near, far, sums):
    rows, width = tokens.shape
    fourth = width // 4
    dma = pltpu.SemaphoreType.DMA
    wide_q, wide_v = 2 * BLK, 2 * HW
    kv_block = (rows, wide_v)
    full = (rows, width)
    unit = (UNIT, width)

    def weight_scratch(wide):
        return [
            pltpu.VMEM((2, fourth, wide), f32),
            pltpu.VMEM((2, fourth, wide), bf16),
            pltpu.VMEM((2, fourth, wide), bf16),
            *[pltpu.VMEM((fourth, wide), bf16)] * 4,
        ]

    return pl.pallas_call(
        scatter_kernel,
        out_shape=(
            jax.ShapeDtypeStruct(full, f32),
            jax.ShapeDtypeStruct((2, 2, GROUPS, *unit), bf16),
            jax.ShapeDtypeStruct((2, GROUPS, fourth, wide_q), bf16),
            jax.ShapeDtypeStruct((2, GROUPS, fourth, wide_v), bf16),
            jax.ShapeDtypeStruct((24, width), f32),
        ),
        in_specs=[anywhere()] * 10 + [whole_vmem()] * 2,
        out_specs=(whole_vmem(), anywhere(), anywhere(), anywhere(), whole_vmem()),
        scratch_shapes=[
            *[
                pltpu.VMEM(item.shape, item.dtype)
                for item in (dq, normed, wfull, tokens, mgrad, keep, over)
            ],
            pltpu.VMEM((48 * GROUPS, width), bf16),
            pltpu.VMEM(far.shape, bf16),
            pltpu.VMEM((GROUPS, 4, *kv_block), bf16),
            pltpu.VMEM((GROUPS, 4, *kv_block), bf16),
            pltpu.VMEM((GROUPS, 2, *kv_block), f32),
            pltpu.VMEM((GROUPS, 2, *kv_block), bf16),
            pltpu.VMEM((GROUPS, 2, *kv_block), bf16),
            pltpu.VMEM((GROUPS, *kv_block), bf16),
            pltpu.VMEM((GROUPS, *kv_block), bf16),
            pltpu.VMEM((GROUPS, *full), f32),
            pltpu.VMEM(full, f32),
            pltpu.VMEM((2, GROUPS, *full), bf16),
            pltpu.VMEM((GROUPS, *full), bf16),
            pltpu.VMEM((width, wide_v), f32),
            pltpu.VMEM((GROUPS, *unit), f32),
            pltpu.VMEM(unit, f32),
            pltpu.VMEM((2, GROUPS, *unit), bf16),
            pltpu.VMEM((GROUPS, *unit), bf16),
            pltpu.VMEM(unit, bf16),
            *weight_scratch(wide_q),
            *weight_scratch(wide_v),
            pltpu.VMEM((6, 24, width), f32),
            pltpu.VMEM((8, width), f32),
            pltpu.VMEM((8, width), f32),
            pltpu.VMEM((len(AROUND) + GROUPS - 1, 8, width), f32),
            dma((9,)),
            dma((GROUPS, 4)), dma((GROUPS, 4)), dma((GROUPS, 4)), dma((GROUPS,)), dma((GROUPS,)), dma((GROUPS,)), dma((GROUPS,)),
            dma((GROUPS,)), dma((2, GROUPS)),
            dma((GROUPS,)), dma((2, GROUPS)), dma((2,)), dma((GROUPS,)), dma((GROUPS,)),
            dma((GROUPS,)), dma((GROUPS,)), dma((2, GROUPS)), dma((2, GROUPS)),
            dma((3,)), dma((3,)), dma((2,)), dma((GROUPS,)), dma((GROUPS,)), dma((GROUPS,)), dma((GROUPS,)),
            dma((3,)), dma((3,)), dma((2,)), dma((GROUPS,)), dma((GROUPS,)), dma((GROUPS,)), dma((GROUPS,)),
            dma((6,)), dma((6,)), dma((10,)), dma((10,)), dma((1,)),
        ],
        compiler_params=pltpu.CompilerParams(
            collective_id=2, has_side_effects=True, vmem_limit_bytes=54 << 20
        ),
        name="scatter",
    )(dkv, dq, normed, wfull, tokens, mgrad, keep, over, near, far, small, sums)


def pack_kv(key_part, value_part):
    return jnp.concatenate(
        [key_part, value_part[..., 2 * DH :], value_part[..., : 2 * DH]], axis=-1
    )


def unpack_kv(both):
    return both[..., :HW], jnp.concatenate([both[..., HW + DH :], both[..., HW : HW + DH]], axis=-1)


def layout_kernel(
    big_ref, query_ref, kv_ref, sums_ref, base_ref, got_ref,
    up_out, down_out, wo_out, query_out, key_out, value_out,
    low_gain, low_shift, query_bias, value_bias, out_bias, high_gain, high_shift, up_bias, down_bias, result_out,
):
    x = lax.axis_index("x")
    width = big_ref.shape[-1]
    half = width // 2
    result_out[...] = (base_ref[...] + got_ref[...].astype(f32)).astype(bf16)
    for core in range(2):
        down_out[core] = big_ref[core, 0, 0:96].astype(f32)
        wo_out[core] = big_ref[core, 0, 192:UNIT].astype(f32)
        for owner in range(2):
            lane = (2 * owner + core) * width
            up_out[:, lane : lane + width] = big_ref[core, 0, 96 + 48 * owner : 144 + 48 * owner].astype(f32)
        query_out[core] = jnp.concatenate(
            [query_ref[core, z].astype(f32)[:, :HW] for z in range(GROUPS)], axis=1
        )
        both = [unpack_kv(kv_ref[core, z].astype(f32)) for z in range(GROUPS)]
        key_out[core] = jnp.concatenate([item[0] for item in both], axis=1)
        value_out[core] = jnp.concatenate([item[1] for item in both], axis=1)

    @pl.when(pl.program_id(0) == 0)
    def _():
        def own_half(row):
            whole = sums_ref[row : row + 1]
            return jnp.where(x == 0, whole[:, :half], whole[:, half:]).reshape(half)

        for ref, row in (
            (low_gain, 0), (low_shift, 1), (out_bias, 2), (high_gain, 3), (high_shift, 4), (down_bias, 5),
        ):
            ref[...] = own_half(row)
        pair = [sums_ref[pl.ds(16 + 2 * x + i, 1)] for i in range(2)]
        query_bias[...] = jnp.concatenate([item[:, :HW] for item in pair], axis=1).reshape(half)
        value_bias[...] = jnp.concatenate(
            [unpack_kv(item[:, 2 * BLK : 2 * BLK + 2 * HW])[1] for item in pair], axis=1
        ).reshape(half)
        up_bias[...] = jnp.concatenate(
            [sums_ref[pl.ds(8 + 2 * x + i, 1)] for i in range(2)], axis=1
        ).reshape(2 * width)


def lay_out(big, query, kv, sums, base, got):
    width = big.shape[-1]
    half, fourth = width // 2, width // 4
    rows = fourth // PARTS

    def spec(shape, index):
        return pl.BlockSpec(shape, index)

    def fixed(wide):
        return pl.BlockSpec((wide,), lambda p: (0,))

    narrow = spec((2, rows, width), lambda p: (0, p, 0))
    vector = jax.ShapeDtypeStruct((half,), f32)
    return pl.pallas_call(
        layout_kernel,
        grid=(PARTS,),
        out_shape=(
            jax.ShapeDtypeStruct((half, 4 * width), f32),
            jax.ShapeDtypeStruct((2, width, width), f32),
            *[jax.ShapeDtypeStruct((2, fourth, width), f32)] * 4,
            *[vector] * 7,
            jax.ShapeDtypeStruct((2 * width,), f32),
            vector,
            jax.ShapeDtypeStruct(base.shape, bf16),
        ),
        in_specs=[
            spec((2, 1, UNIT, width), lambda p: (0, p, 0, 0)),
            spec((2, GROUPS, rows, query.shape[-1]), lambda p: (0, 0, p, 0)),
            spec((2, GROUPS, rows, kv.shape[-1]), lambda p: (0, 0, p, 0)),
            spec(sums.shape, lambda p: (0, 0)),
            spec((base.shape[0] // PARTS, width), lambda p: (p, 0)),
            spec((base.shape[0] // PARTS, width), lambda p: (p, 0)),
        ],
        out_specs=(
            spec((48, 4 * width), lambda p: (p, 0)),
            spec((2, 96, width), lambda p: (0, p, 0)),
            *[narrow] * 4,
            *[fixed(half)] * 7,
            fixed(2 * width),
            fixed(half),
            spec((base.shape[0] // PARTS, width), lambda p: (p, 0)),
        ),
        compiler_params=pltpu.CompilerParams(
            vmem_limit_bytes=VMEM_LIMIT, dimension_semantics=("arbitrary",)
        ),
        name="lay_out",
    )(big, query, kv, sums, base, got)


ROWS = ("s", "r", "core", "x")
ALL = ("g", "s", "r", "core", "x")


def shards(
    tokens, cotangent, doc_lengths, deal, first_gain, first_shift, query_weight, query_bias,
    key_weight, value_weight, value_bias, output_weight, output_bias, second_gain, second_shift,
    up_weight, up_bias, down_weight, down_bias,
):
    rows, width = tokens.shape
    half = width // 2
    blocks = deal.shape[0]
    core, x = lax.axis_index("core"), lax.axis_index("x")
    swap = ((0, 1), (1, 0))

    def up_columns(owner):
        return lax.dynamic_slice_in_dim(up_weight, (2 * owner + core) * width, width, 1)

    kv, q, normed, small, wfull, wo = gather(
        tokens, query_weight, key_weight, value_weight, output_weight,
        first_gain, first_shift, output_bias, second_gain, second_shift, down_bias, query_bias, value_bias, up_bias,
    )
    wide = blocks > 8 * 2 * GROUPS
    if wide:
        kv = lax.all_gather(kv, "s", axis=0, tiled=True)
    kv = kv.reshape(blocks, BLK, 2 * HW)
    q = q.reshape(2 * GROUPS, BLK, 2 * BLK)
    cot_x, up_other, kv = lax.optimization_barrier((cotangent, up_columns(1 - x), kv))
    up_other = lax.ppermute(up_other, "x", swap)
    cot_x = lax.ppermute(cot_x, "x", swap)
    out_t, kept, lse = attend_forward(deal, doc_lengths, q, kv)
    base, x_give, grad_middle, grad_t, kept_part, over, far, sums = dense(
        out_t, tokens, cotangent, cot_x, small, wo, up_columns(x), up_other, down_weight
    )
    over = lax.ppermute(over, "r", swap)
    x_got = lax.ppermute(x_give, "x", swap)
    far = lax.ppermute(far, ("r", "x"), ((0, 3), (1, 2), (2, 1), (3, 0)))
    dq, dkv = attend_backward(deal, doc_lengths, q, kv, lse, grad_t, kept)
    dkv = dkv.reshape(-1, GROUPS, rows, 2 * HW)
    if wide:
        dkv = lax.psum_scatter(dkv, "s", scatter_dimension=0, tiled=True)
    dq = dq.reshape(GROUPS, rows, 2 * BLK)
    grad_tokens, big, query_own, kv_own, sums = scatter(
        dkv, dq, normed, wfull, tokens, grad_middle, small, kept_part, over, x_got, far, sums
    )
    if wide:
        big, query_own, kv_own, sums = (
            lax.psum(item, "s") for item in (big, query_own, kv_own, sums)
        )

    (
        up_own, down_own, wo_own, query_own, key_own, value_own,
        low_gain, low_shift, query_sum, value_sum, out_sum, high_gain, high_shift, up_sum, down_sum, result,
    ) = lay_out(big.reshape(2, PARTS, UNIT, width), query_own, kv_own, sums, base, x_got)

    def flat(item):
        return item.reshape(-1, width)

    return (
        result,
        grad_tokens,
        low_gain,
        low_shift,
        flat(query_own),
        query_sum,
        flat(key_own),
        flat(value_own),
        value_sum,
        flat(wo_own),
        out_sum,
        high_gain,
        high_shift,
        up_own,
        up_sum,
        flat(down_own),
        down_sum,
    )


def solution(mesh):
    devices = mesh.devices
    inner_mesh = Mesh(devices.reshape(GROUPS, devices.shape[0] // (4 * GROUPS), 2, 2, 2), ALL)
    row = P(ALL, None)
    mat = P("x", None)
    vec = P("x")
    in_specs = (
        row, row, P(), P(), vec, vec, mat, vec, mat, mat, vec, mat, vec, vec, vec, mat, vec, mat, vec,
    )
    out_specs = (
        row, row, vec, vec, mat, vec, mat, mat, vec, mat, vec, vec, vec, mat, vec, mat, vec,
    )
    return jax.shard_map(
        shards, mesh=inner_mesh, in_specs=in_specs, out_specs=out_specs, check_vma=False
    )
```

```python
import jax
import jax.numpy as jnp
from jax import lax
from jax.experimental import pallas as pl
from jax.experimental.pallas import tpu as pltpu
from jax.sharding import Mesh
from jax.sharding import PartitionSpec as P

HEADS = 12
DH = 64
NSUM = 50
SEG = 2048
BLK = 128
GROUPS = 4
PER = HEADS // GROUPS
HW = PER * DH
WIDE = PER * BLK
CHUNK = 2 * BLK
EPS = 1e-05
SCALE = 0.125
MASKED = -1e30
ROOT_HALF = 0.7071067811865476
PDF_SCALE = 0.3989422804014327
VMEM_LIMIT = 56 << 20
bf16 = jnp.bfloat16
f32 = jnp.float32


def layer_norm(values, gain, shift):
    mean = jnp.mean(values, axis=-1, keepdims=True)
    centred = values - mean
    spread = jnp.mean(centred * centred, axis=-1, keepdims=True)
    return centred * lax.rsqrt(spread + EPS) * gain + shift


def outer(left, right):
    return lax.dot_general(left, right, (((0,), (0,)), ((), ())), preferred_element_type=f32)


def inner(left, right):
    return lax.dot_general(left, right, (((1,), (1,)), ((), ())), preferred_element_type=f32)


def dot(left, right):
    return jnp.dot(left, right, preferred_element_type=f32)


def survey(deal_ref, lengths_ref, where_ref, text_ref, low_ref, high_ref, first_ref):
    blocks = deal_ref.shape[0]
    per_group = blocks // (2 * GROUPS)
    rest = lax.axis_index(ROWS)

    def note(j, kept):
        pair = j // 2
        group = pair // per_group
        where_ref[deal_ref[j]] = ((pair - group * per_group) * GROUPS + group) * 2 + j % 2
        return kept

    lax.fori_loop(0, blocks, note, 0)
    starts = [jnp.int32(0)]
    for doc in range(lengths_ref.shape[0] - 1):
        starts.append(starts[-1] + lengths_ref[doc])

    def first_of(at):
        begin = jnp.zeros_like(at)
        for start in starts:
            begin = jnp.where(start <= at, jnp.maximum(begin, start), begin)
        return jnp.where(at - begin >= SEG + NSUM, begin + SEG, begin)

    for slot in range(2 * GROUPS):
        text = deal_ref[2 * ((slot // 2) * per_group + rest) + slot % 2]
        text_ref[slot] = text
        low_ref[slot] = first_of(text * BLK) // CHUNK
        high_ref[slot] = text // 2
        first_ref[slot] = first_of(text * BLK + lax.broadcasted_iota(jnp.int32, (1, BLK), 1))


def survey_scratch(blocks):
    slots = 2 * GROUPS
    return [
        pltpu.SMEM((blocks,), jnp.int32),
        pltpu.SMEM((slots,), jnp.int32),
        pltpu.SMEM((slots,), jnp.int32),
        pltpu.SMEM((slots,), jnp.int32),
        pltpu.VMEM((slots, 1, BLK), jnp.int32),
    ]


def spread_heads_t(part_t, order):
    rows = []
    zero = jnp.zeros((DH, BLK), part_t.dtype)
    for head in order:
        if head is None:
            rows.append(jnp.zeros((DH, WIDE), part_t.dtype))
        else:
            piece = part_t[DH * head : DH * head + DH]
            rows.append(
                jnp.concatenate([piece if h == head else zero for h in range(PER)], axis=1)
            )
    return jnp.concatenate(rows, axis=0)


K_ORDER = (0, 1, 2, None)
V_ORDER = (None, 2, 0, 1)


def visible(chunk, first, own):
    at = chunk * CHUNK + lax.broadcasted_iota(jnp.int32, (CHUNK, BLK), 0)
    allowed = (at >= first) & (at <= own)
    return jnp.concatenate([allowed] * PER, axis=1)


def load_chunk(kv_ref, where_ref, chunk):
    return jnp.concatenate(
        [kv_ref[where_ref[2 * chunk]], kv_ref[where_ref[2 * chunk + 1]]], axis=0
    )


def forward_kernel(
    deal_ref, lengths_ref, q_ref, kv_ref,
    out_ref, wide_ref, lse_ref,
    where_ref, text_ref, low_ref, high_ref, first_ref, acc_ref,
):
    survey(deal_ref, lengths_ref, where_ref, text_ref, low_ref, high_ref, first_ref)

    def one_slot(slot, kept):
        wide_q = spread_heads_t(q_ref[slot].T[:HW], K_ORDER)
        first = first_ref[slot]
        own = text_ref[slot] * BLK + lax.broadcasted_iota(jnp.int32, (1, BLK), 1)
        last_first = jnp.max(first)
        acc_ref[...] = jnp.zeros_like(acc_ref)

        def step(double, carry):
            top, total = carry
            scores = []
            for part in range(2):
                keys = load_chunk(kv_ref, where_ref, 2 * double + part)[:, : 2 * BLK]
                scores.append(jnp.where(visible(2 * double + part, first, own), dot(keys, wide_q), MASKED))
            scores = jnp.concatenate(scores, axis=0)
            fresh = jnp.maximum(top, jnp.max(scores, axis=0, keepdims=True))
            expo = jnp.exp(scores - fresh)
            shrink = jnp.exp(top - fresh)
            total = total * shrink + jnp.sum(expo, axis=0, keepdims=True)
            vals = jnp.concatenate([load_chunk(kv_ref, where_ref, 2 * double + part)[:, BLK:] for part in range(2)], axis=0)
            acc_ref[...] = acc_ref[...] * shrink + outer(vals, expo.astype(bf16))
            return fresh, total

        top, total = lax.fori_loop(
            low_ref[slot] // 2,
            high_ref[slot] // 2 + 1,
            step,
            (jnp.full((1, WIDE), MASKED, f32), jnp.zeros((1, WIDE), f32)),
        )
        lse_ref[slot] = top + jnp.log(total)
        scaled = acc_ref[...] / total
        pieces = []
        for head in range(PER):
            row = DH * V_ORDER.index(head)
            pieces.append(scaled[row : row + DH, BLK * head : BLK * head + BLK])
        whole = jnp.concatenate(pieces, axis=0)
        wide_ref[slot] = whole
        out_ref[slot] = whole.astype(bf16)
        return kept

    lax.fori_loop(0, q_ref.shape[0], one_slot, 0)


def whole_vmem():
    return pl.BlockSpec(memory_space=pltpu.VMEM)


def whole_smem():
    return pl.BlockSpec(memory_space=pltpu.SMEM)


def attend_forward(deal, lengths, q, kv):
    slots = q.shape[0]
    blocks = kv.shape[0]
    return pl.pallas_call(
        forward_kernel,
        out_shape=(
            jax.ShapeDtypeStruct((slots, HW, BLK), bf16),
            jax.ShapeDtypeStruct((slots, HW, BLK), f32),
            jax.ShapeDtypeStruct((slots, 1, WIDE), f32),
        ),
        in_specs=[whole_smem()] * 2 + [whole_vmem()] * 2,
        out_specs=(whole_vmem(),) * 3,
        scratch_shapes=[
            *survey_scratch(blocks),
            pltpu.VMEM((2 * BLK, WIDE), f32),
        ],
        compiler_params=pltpu.CompilerParams(vmem_limit_bytes=(6 << 20) + kv.size // 5 * 16),
        name="attend_forward",
    )(deal, lengths, q, kv)


def backward_kernel(
    deal_ref, lengths_ref, q_ref, kv_ref, lse_ref, do_ref, wide_ref,
    dq_ref, dkv_ref, where_ref, text_ref, low_ref, high_ref, first_ref, qt_ref, qm_ref, dot_ref, dom_ref, delta_ref, acc_ref, dk_acc, dv_acc,
    packed_ref, count_ref, list_ref, out_sem,
):
    survey(deal_ref, lengths_ref, where_ref, text_ref, low_ref, high_ref, first_ref)
    slots = q_ref.shape[0]
    chunks = kv_ref.shape[0] // 2

    def ready(slot, _):
        q = q_ref[slot]
        qt_ref[slot] = spread_heads_t(q.T[:HW], K_ORDER)
        lane = lax.broadcasted_iota(jnp.int32, (BLK, 2 * BLK), 1) // DH
        zero = jnp.zeros_like(q)
        qm_ref[slot] = jnp.concatenate(
            [jnp.where(lane == K_ORDER.index(h), q, zero) for h in range(PER)], axis=0
        )
        grad_t = do_ref[slot]
        dot_ref[slot] = spread_heads_t(grad_t, V_ORDER)
        ordered = jnp.concatenate(
            [
                jnp.zeros((DH, BLK), bf16) if h is None else grad_t[DH * h : DH * h + DH]
                for h in V_ORDER
            ],
            axis=0,
        ).T
        dom_ref[slot] = jnp.concatenate(
            [jnp.where(lane == V_ORDER.index(h), ordered, zero) for h in range(PER)], axis=0
        )
        both = grad_t.astype(f32) * wide_ref[slot]
        delta_ref[slot] = jnp.concatenate(
            [jnp.sum(both[DH * h : DH * h + DH], axis=0, keepdims=True) for h in range(PER)],
            axis=1,
        )
        acc_ref[slot] = jnp.zeros((HW, WIDE), f32)
        return _

    lax.fori_loop(0, slots, ready, 0)

    def clear(chunk, kept):
        count_ref[chunk] = 0
        return kept

    lax.fori_loop(0, chunks, clear, 0)

    def enlist(slot, kept):
        def seen(chunk, kept):
            count = count_ref[chunk]
            list_ref[chunk * slots + count] = slot
            count_ref[chunk] = count + 1
            return kept

        lax.fori_loop(low_ref[slot], high_ref[slot] + 1, seen, 0)
        return kept

    lax.fori_loop(0, slots, enlist, 0)

    def written(chunk, i):
        return pltpu.make_async_copy(
            packed_ref.at[chunk % 2, i], dkv_ref.at[where_ref[2 * chunk + i]], out_sem.at[chunk % 2, i]
        )

    def one_chunk(chunk, kept):
        part = load_chunk(kv_ref, where_ref, chunk)
        keys = part[:, : 2 * BLK]
        vals = part[:, BLK:]
        keys_t = keys.T[:HW]
        dk_acc[...] = jnp.zeros_like(dk_acc)
        dv_acc[...] = jnp.zeros_like(dv_acc)

        def one_slot(i, kept):
            for half in range(2):
                attend(list_ref[chunk * slots + 2 * i + half])
            return kept

        def attend(slot):
            own = text_ref[slot] * BLK + lax.broadcasted_iota(jnp.int32, (1, BLK), 1)
            scores = dot(keys, qt_ref[slot])
            dprobs = dot(vals, dot_ref[slot])
            probs = jnp.where(visible(chunk, first_ref[slot], own), jnp.exp(scores - lse_ref[slot]), 0.0)
            dscores = (probs * (dprobs - delta_ref[slot])).astype(bf16)
            dv_acc[...] += dot(probs.astype(bf16), dom_ref[slot])
            dk_acc[...] += dot(dscores, qm_ref[slot])
            acc_ref[slot] += dot(keys_t, dscores)

        lax.fori_loop(0, count_ref[chunk] // 2, one_slot, 0)
        pl.when(count_ref[chunk] % 2 == 1)(lambda: attend(list_ref[chunk * slots + count_ref[chunk] - 1]))
        packed = jnp.concatenate(
            [
                dk_acc[:, :BLK],
                dk_acc[:, BLK:] + dv_acc[:, :BLK],
                dv_acc[:, BLK:],
            ],
            axis=1,
        ).astype(bf16)

        @pl.when(chunk >= 2)
        def _():
            for i in range(2):
                written(chunk - 2, i).wait()

        for i in range(2):
            packed_ref[chunk % 2, i] = packed[BLK * i : BLK * i + BLK]
            written(chunk, i).start()
        return kept

    lax.fori_loop(0, chunks, one_chunk, 0)
    for last in range(2):
        for i in range(2):
            written(chunks - 2 + last, i).wait()

    def finish(slot, _):
        total = acc_ref[slot]
        kept = jnp.concatenate(
            [total[DH * h : DH * h + DH, BLK * h : BLK * h + BLK] for h in range(PER)]
            + [jnp.zeros((DH, BLK), f32)],
            axis=0,
        )
        dq_ref[slot] = kept.T.astype(bf16)
        return _

    lax.fori_loop(0, slots, finish, 0)


def attend_backward(deal, lengths, q, kv, lse, grad_t, wide):
    slots = q.shape[0]
    return pl.pallas_call(
        backward_kernel,
        out_shape=(
            jax.ShapeDtypeStruct((slots, BLK, 2 * BLK), bf16),
            jax.ShapeDtypeStruct(kv.shape, bf16),
        ),
        in_specs=[whole_smem()] * 2 + [whole_vmem()] * 5,
        out_specs=(whole_vmem(), in_hbm()),
        scratch_shapes=[
            *survey_scratch(kv.shape[0]),
            pltpu.VMEM((slots, 2 * BLK, WIDE), bf16),
            pltpu.VMEM((slots, WIDE, 2 * BLK), bf16),
            pltpu.VMEM((slots, 2 * BLK, WIDE), bf16),
            pltpu.VMEM((slots, WIDE, 2 * BLK), bf16),
            pltpu.VMEM((slots, 1, WIDE), f32),
            pltpu.VMEM((slots, HW, WIDE), f32),
            pltpu.VMEM((CHUNK, 2 * BLK), f32),
            pltpu.VMEM((CHUNK, 2 * BLK), f32),
            pltpu.VMEM((2, 2, BLK, 2 * HW), bf16),
            pltpu.SMEM((kv.shape[0] // 2,), jnp.int32),
            pltpu.SMEM((kv.shape[0] // 2 * slots,), jnp.int32),
            pltpu.SemaphoreType.DMA((2, 2)),
        ],
        compiler_params=pltpu.CompilerParams(
            vmem_limit_bytes=max(48 << 20, (17 << 20) + kv.size * 2)
        ),
        name="attend_backward",
    )(deal, lengths, q, kv, lse, grad_t, wide)


MESH = pl.DeviceIdType.MESH


def send(src, dst, out_sem, in_sem, **device):
    return pltpu.make_async_remote_copy(
        src_ref=src, dst_ref=dst, send_sem=out_sem, recv_sem=in_sem, device_id=device, device_id_type=MESH
    )


def place():
    return tuple(lax.axis_index(name) for name in ("g", "r", "core", "x"))


def seat(r, core, x):
    return (r * 2 + core) * 2 + x


AROUND = ((0, 0, 1), (0, 1, 0), (0, 1, 1), (1, 0, 0), (1, 0, 1), (1, 1, 0), (1, 1, 1))


def neighbour(r, core, x, step):
    dr, dc, dx = AROUND[step]
    return {"r": 1 - r if dr else r, "core": 1 - core if dc else core, "x": 1 - x if dx else x}


def greet(g, r, core, x, line, around=False):
    barrier = pltpu.get_barrier_semaphore()

    def hello(**device):
        pl.semaphore_signal(barrier, inc=1, device_id=device, device_id_type=MESH)

    if around:
        for step in range(len(AROUND)):
            hello(**neighbour(r, core, x, step))
    else:
        hello(core=1 - core)
        hello(x=1 - x)
        hello(r=1 - r)
    near = len(AROUND) if around else 3
    if line:
        for away in range(1, GROUPS):
            hello(g=lax.rem(g + away, GROUPS))
        pl.semaphore_wait(barrier, near + GROUPS - 1)
    else:
        pl.when(g > 0)(lambda: hello(g=g - 1))
        pl.when(g < GROUPS - 1)(lambda: hello(g=g + 1))
        pl.semaphore_wait(barrier, near + 2 - jnp.where(g == 0, 1, 0) - jnp.where(g == GROUPS - 1, 1, 0))


NEAREST = ((0, 1, 2, 3), (1, 2, 0, 3), (2, 1, 3, 0), (3, 2, 1, 0))


def nearest(g, step):
    picked = NEAREST[0][step]
    for z in range(1, GROUPS):
        picked = jnp.where(g == z, NEAREST[z][step], picked)
    return picked


def prepare(g, x, weights, lines, narrow_ref, small_ref):
    half = weights.shape[1]
    odd = lax.rem(g, 2) == 1

    def columns(i):
        low = pl.multiple_of(3 * g // 2 * BLK, BLK)
        window = weights[i, :, pl.ds(low, 2 * BLK)]
        moved = jnp.concatenate([window[:, DH:], window[:, :DH]], axis=1)
        return jnp.where(odd, moved, window)

    lane = lax.broadcasted_iota(jnp.int32, (half, 2 * BLK), 1)
    query = columns(0)
    narrow_ref[:, : 2 * BLK] = jnp.where(lane < HW, query, jnp.zeros_like(query))
    narrow_ref[:, 2 * BLK :] = pack_kv(columns(1)[:, :HW], columns(2)[:, :HW])

    def line(i):
        return lines[i][...].astype(f32).reshape(1, -1)

    zero = jnp.zeros((1, half), f32)
    small_ref[...] = jnp.zeros_like(small_ref)
    for row in range(6):
        small_ref[row : row + 1] = jnp.where(
            x == 0, jnp.concatenate([line(row), zero], axis=1), jnp.concatenate([zero, line(row)], axis=1)
        )
    ups = line(8)
    for i in range(2):
        small_ref[pl.ds(8 + 2 * x + i, 1)] = ups[:, 2 * half * i : 2 * half * i + 2 * half]

    def part(i):
        mine = jnp.where(odd, line(i)[:, HW:], line(i)[:, :HW])
        return jnp.where(g // 2 == x, mine, jnp.zeros_like(mine))

    value = part(7)
    small_ref[12:13] = jnp.concatenate(
        [part(6), jnp.zeros((1, 2 * BLK), f32), value[:, 2 * DH :], value[:, : 2 * DH], jnp.zeros((1, BLK), f32)], axis=1
    )


def gather_kernel(
    tokens_ref, query_any, key_any, value_any, wo_ref, l0, l1, l2, l3, l4, l5, l6, l7, l8,
    kv_ref, q_ref, normed_ref, small_out, wfull, wo_out,
    lined, attn_w, narrow_ref, small_ref, small_in, kvs,
    z_own, z_send, z_recv, s_sem, n_send, n_recv, kv_send, kv_recv, kv_local, w_send, w_recv, w_local, a_sem,
):
    g, r, core, x = place()
    other = 1 - x
    rows, width = tokens_ref.shape
    half = width // 2
    fourth = half // 2
    eighth = half // 4
    loads = [
        pltpu.make_async_copy(ref, attn_w.at[i], a_sem.at[i]) for i, ref in enumerate((query_any, key_any, value_any))
    ]
    for load in loads:
        load.start()
    greet(g, r, core, x, False)

    def along(source, away, sem):
        return send(lined.at[source], lined.at[source], sem, z_recv.at[source], g=g + away)

    lined[g] = tokens_ref[...]
    pl.when(g > 0)(lambda: along(g, -1, z_own.at[0]).start())
    pl.when(g < GROUPS - 1)(lambda: along(g, 1, z_own.at[1]).start())

    for load in loads:
        load.wait()
    prepare(g, x, attn_w, (l0, l1, l2, l3, l4, l5, l6, l7, l8), narrow_ref, small_ref)
    small_move = send(small_ref, small_in, s_sem.at[0], s_sem.at[1], x=other)
    small_move.start()
    mine = pl.ds(x * half + core * fourth, fourth)
    narrow_x = send(narrow_ref.at[pl.ds(core * fourth, fourth)], wfull.at[mine], n_send.at[0], n_recv.at[0], x=other)
    narrow_x.start()

    def wo_rows(owner, part):
        return wo_out.at[pl.ds(owner * half + core * fourth + part * eighth, eighth)]

    wo_x = send(wo_ref.at[pl.ds(core * fourth + r * eighth, eighth)], wo_rows(x, r), w_send.at[0], w_recv.at[0], x=other)
    wo_y = send(wo_rows(other, r), wo_rows(other, r), w_send.at[3], w_recv.at[3], r=1 - r)
    wo_s = [
        send(wo_rows(other, part), wo_rows(other, part), w_send.at[6 + i], w_recv.at[6 + i], core=1 - core)
        for i, part in enumerate((r, 1 - r))
    ]
    wo_x.start()
    locals_ = [pltpu.make_async_copy(wo_ref, wo_out.at[pl.ds(x * half, half)], w_local.at[0])]
    for item in locals_:
        item.start()

    wfull[pl.ds(x * half, half)] = narrow_ref[...]
    narrow_x.wait_recv()
    theirs = wfull.at[pl.ds(other * half + core * fourth, fourth)]
    narrow_s = send(theirs, theirs, n_send.at[1], n_recv.at[1], core=1 - core)
    narrow_s.start()
    small_move.wait_recv()
    small_out[...] = small_ref[...] + small_in[...]
    narrow_s.wait_recv()

    own = seat(r, core, x)

    def block(owner, source):
        return kv_ref.at[owner, source]

    def push(step, kind, what, **device):
        copy = send(what[0], what[1], kv_send.at[kind, step], kv_recv.at[kind, step], **device)
        copy.start()

    def settle(step, kind, owner, source):
        send(block(owner, source), block(owner, source), kv_send.at[kind, step], kv_recv.at[kind, step], x=other).wait_recv()

    def forward(step):
        source = nearest(g, step)
        by_x = block(seat(r, core, other), source)
        settle(step, 0, seat(r, core, other), source)
        if step % 2 == 0:
            push(step, 3, (by_x, by_x), r=1 - r)
        push(step, 4, (by_x, by_x), core=1 - core)
        by_y = block(seat(1 - r, core, x), source)
        settle(step, 1, seat(1 - r, core, x), source)
        if step % 2 == 1:
            push(step, 3, (by_y, by_y), x=other)
        push(step, 5, (by_y, by_y), core=1 - core)

    def forward_far(step):
        source = nearest(g, step)
        far = block(seat(1 - r, core, other), source)
        settle(step, 3, seat(1 - r, core, other), source)
        push(step, 6, (far, far), core=1 - core)

    for step in range(GROUPS):
        source = nearest(g, step)
        if step > 0:
            send(lined.at[source], lined.at[source], z_send.at[source], z_recv.at[source], x=other).wait_recv()
            pl.when((source < g) & (g < GROUPS - 1))(lambda: along(source, 1, z_send.at[source]).start())
            pl.when((source > g) & (g > 0))(lambda: along(source, -1, z_send.at[source]).start())
        values = lined[source].astype(f32)
        normed = layer_norm(values, small_out[0:1], small_out[1:2]).astype(bf16)
        normed_ref[source] = normed
        both = dot(normed, wfull[...]) + small_out[12:13, : wfull.shape[1]]
        q_ref[source] = (both[:, : 2 * BLK] * SCALE).astype(bf16)
        kvs[step] = both[:, 2 * BLK :].astype(bf16)
        here = (kvs.at[step], block(own, source))
        push(step, 0, here, x=other)
        push(step, 1, here, r=1 - r)
        push(step, 2, here, core=1 - core)
        pltpu.make_async_copy(kvs.at[step], block(own, source), kv_local.at[step]).start()
        if step > 0:
            forward(step - 1)
        if step > 1:
            forward_far(step - 2)
    wo_x.wait_recv()
    wo_y.start()
    wo_s[0].start()
    forward(GROUPS - 1)
    forward_far(GROUPS - 2)
    send(wo_rows(other, 1 - r), wo_rows(other, 1 - r), w_send.at[3], w_recv.at[3], r=1 - r).wait_recv()
    wo_s[1].start()
    forward_far(GROUPS - 1)

    for step in range(GROUPS):
        source = nearest(g, step)
        pltpu.make_async_copy(kvs.at[step], block(own, source), kv_local.at[step]).wait()
        settle(step, 2, seat(r, 1 - core, x), source)
        settle(step, 4, seat(r, 1 - core, other), source)
        settle(step, 5, seat(1 - r, 1 - core, x), source)
        settle(step, 6, seat(1 - r, 1 - core, other), source)
        for kind in range(7):
            send(kvs.at[step], block(own, source), kv_send.at[kind, step], kv_recv.at[kind, step], x=other).wait_send()
    pl.when(g > 0)(lambda: along(g, -1, z_own.at[0]).wait_send())
    pl.when(g < GROUPS - 1)(lambda: along(g, 1, z_own.at[1]).wait_send())
    for step in range(1, GROUPS):
        source = nearest(g, step)
        passed = ((source < g) & (g < GROUPS - 1)) | ((source > g) & (g > 0))
        pl.when(passed)(lambda: send(lined.at[source], lined.at[source], z_send.at[source], z_recv.at[source], x=other).wait_send())
    small_move.wait_send()
    narrow_x.wait_send()
    narrow_s.wait_send()
    for item in locals_:
        item.wait()
    for item in (wo_x, wo_y, *wo_s):
        item.wait_send()
    for i, part in enumerate((r, 1 - r)):
        there = wo_out.at[pl.ds(other * half + (1 - core) * fourth + part * eighth, eighth)]
        send(there, there, w_send.at[6 + i], w_recv.at[6 + i], core=1 - core).wait_recv()


def anywhere():
    return pl.BlockSpec(memory_space=pl.ANY)


def in_hbm():
    return pl.BlockSpec(memory_space=pltpu.HBM)


def gather(tokens, query, key, value, wo, *lines):
    rows, width = tokens.shape
    wide = 2 * BLK + 2 * HW
    small = (16, width)
    dma = pltpu.SemaphoreType.DMA
    return pl.pallas_call(
        gather_kernel,
        out_shape=(
            jax.ShapeDtypeStruct((8, GROUPS, rows, 2 * HW), bf16),
            jax.ShapeDtypeStruct((GROUPS, rows, 2 * BLK), bf16),
            jax.ShapeDtypeStruct((GROUPS, rows, width), bf16),
            jax.ShapeDtypeStruct(small, f32),
            jax.ShapeDtypeStruct((width, wide), bf16),
            jax.ShapeDtypeStruct((width, width), bf16),
        ),
        in_specs=[whole_vmem(), *[in_hbm()] * 4, *[whole_vmem()] * len(lines)],
        out_specs=(anywhere(), *(whole_vmem(),) * 5),
        scratch_shapes=[
            pltpu.VMEM((GROUPS, rows, width), bf16),
            pltpu.VMEM((3, width // 2, width), bf16),
            pltpu.VMEM((width // 2, wide), bf16),
            pltpu.VMEM(small, f32),
            pltpu.VMEM(small, f32),
            pltpu.VMEM((GROUPS, rows, 2 * HW), bf16),
            dma((2,)), dma((GROUPS,)), dma((GROUPS,)), dma((2,)), dma((2,)), dma((2,)),
            dma((7, GROUPS)), dma((7, GROUPS)), dma((GROUPS,)), dma((8,)), dma((8,)), dma((2,)), dma((3,)),
        ],
        compiler_params=pltpu.CompilerParams(
            collective_id=0, has_side_effects=True, vmem_limit_bytes=60 << 20
        ),
        name="gather",
    )(tokens, query, key, value, wo, *lines)


def erf_parts(values):
    below = 0.5 * (1.0 + lax.erf(values * ROOT_HALF))
    return below, PDF_SCALE * jnp.exp(-0.5 * values * values)


PARTS = 8
UNIT = 216
KEPT = 168


def dense_kernel(
    out_t_ref, tokens_ref, cot_ref, cot_x_ref, small_ref, wo_ref, up_mine, up_other, down_any,
    base_ref, x_give_ref, middle_grad_ref, grad_t_ref, keep_ref, give_ref, far_ref, sums_ref,
    down_ref, up_ref, attn_in, attn_t, cots, h2s, mid_ref, n2_ref, scales, part_y, part_d, in_y, in_d, pass_y, pass_d,
    x_y, x_d, hids, dus, branch_ref, grad_out, wo_keep, wo_give, wo_in, wo_pass, wo_x,
    l_sem, a_send, a_recv, c_send, c_recv, h_send, h_recv, y_send, y_recv, d_send, d_recv, o_send, o_recv,
    w_send, w_recv,
):
    g, r, core, x = place()
    other, sib = 1 - x, 1 - core
    rows, width = tokens_ref.shape
    half = width // 2
    fourth = half // 2
    loads = [
        pltpu.make_async_copy(
            down_any.at[pl.ds(pl.multiple_of(core * width, width), width)], down_ref, l_sem.at[0]
        ),
        pltpu.make_async_copy(up_mine, up_ref.at[pl.ds(x * half, half)], l_sem.at[1]),
        pltpu.make_async_copy(up_other, up_ref.at[pl.ds(other * half, half)], l_sem.at[2]),
    ]
    for load in loads:
        load.start()
    greet(g, r, core, x, True)
    pending = []

    def begin(src, dst, out_sem, in_sem, **device):
        move = send(src, dst, out_sem, in_sem, **device)
        move.start()
        pending.append(move)
        return move

    def other_group(away):
        return lax.rem(g + away, GROUPS)

    def rows_of(b):
        return pl.ds(BLK * b, BLK)

    for b in range(2):
        for away in range(1, GROUPS):
            to = other_group(away)
            begin(out_t_ref.at[2 * to + b], attn_in.at[g, b], a_send.at[b, away], a_recv.at[b, g], g=to)
        attn_in[g, b] = out_t_ref[2 * g + b]
        cots[b, 0] = cot_ref[rows_of(b)]
        cots[b, 2] = cot_x_ref[rows_of(b)]
    cot_moves = [
        begin(cots.at[:, 2 * i], cots.at[:, 2 * i + 1], c_send.at[i], c_recv.at[i], core=sib) for i in range(2)
    ]
    sums_ref[...] = jnp.zeros_like(sums_ref)
    sums_ref[5:6] = jnp.sum(cot_ref[...].astype(f32), axis=0, keepdims=True)
    h2_moves = []

    def norm(b):
        for away in range(1, GROUPS):
            source = other_group(away)
            arrived(attn_in.at[source, b], a_send.at[b, away], a_recv.at[b, source], x)
        for source in range(GROUPS):
            attn_t[HW * source : HW * source + HW, BLK * b : BLK * b + BLK] = attn_in[source, b]
        middle = (
            tokens_ref[rows_of(b)].astype(f32)
            + outer(attn_t[:, BLK * b : BLK * b + BLK], wo_ref[...])
            + small_ref[2:3]
        )
        mid_ref[b] = middle
        mean = jnp.mean(middle, axis=-1, keepdims=True)
        centred = middle - mean
        scale = lax.rsqrt(jnp.mean(centred * centred, axis=-1, keepdims=True) + EPS)
        scales[b] = scale
        n2_ref[b] = centred * scale
        h2s[b, 0] = (n2_ref[b] * small_ref[3:4] + small_ref[4:5]).astype(bf16)
        h2_moves.append(
            (
                begin(h2s.at[b, 0], h2s.at[b, 2], h_send.at[b, 1], h_recv.at[b, 1], x=other),
                begin(h2s.at[b, 0], h2s.at[b, 1], h_send.at[b, 0], h_recv.at[b, 0], core=sib),
            )
        )

    def pass_on(b):
        h2_moves[b][0].wait_recv()
        return begin(h2s.at[b, 2], h2s.at[b, 3], h_send.at[b, 2], h_recv.at[b, 2], core=sib)

    bias_row = 8 + 2 * x + core

    def pair_of(ref, b, pair):
        return ref[b, 2 * pair : 2 * pair + 2].reshape(2 * BLK, width)

    def forward_backward(b, pair):
        cot = pair_of(cots, b, pair)
        expanded = dot(pair_of(h2s, b, pair), up_ref[...]) + small_ref[pl.ds(bias_row, 1)]
        below, density = erf_parts(expanded)
        hidden = (expanded * below).astype(bf16)
        hids[b, pair] = hidden
        slope = below + expanded * density
        grad_hidden = inner(cot, down_ref[...]).astype(bf16).astype(f32)
        grad_expand = (grad_hidden * slope).astype(bf16)
        dus[b, pair] = grad_expand
        part_d[b, pair] = inner(grad_expand, up_ref[...])
        part_y[b, pair] = dot(hidden, down_ref[...])
        sums_ref[pl.ds(bias_row, 1)] += jnp.sum(grad_expand.astype(f32), axis=0, keepdims=True)

    d_moves, y_passes = [None, None], [None, None]

    def near_pair(b):
        if b == 0:
            cot_moves[0].wait_recv()
        h2_moves[b][1].wait_recv()
        forward_backward(b, 0)
        return begin(part_d.at[b, 0, pl.ds(BLK, BLK)], in_d.at[b], d_send.at[b, 0], d_recv.at[b, 0], core=sib)

    def far_pair(b, passed):
        if b == 0:
            cot_moves[1].wait_recv()
        passed.wait_recv()
        forward_backward(b, 1)
        x_d[b, 0] = part_d[b, 1, BLK:].astype(bf16)
        across = begin(x_d.at[b, 0], pass_d.at[b], d_send.at[b, 1], d_recv.at[b, 1], core=sib)
        x_y[b] = part_y[b, 1, BLK:].astype(bf16)
        y_passes[b] = begin(x_y.at[b], pass_y.at[b], y_send.at[b, 1], y_recv.at[b, 1], core=sib)
        across.wait_recv()
        x_d[b, 1] = (part_d[b, 1, :BLK] + pass_d[b].astype(f32)).astype(bf16)
        return begin(x_d.at[b, 1], x_d.at[b, 2], d_send.at[b, 2], d_recv.at[b, 2], x=other)

    def back(b, near, far):
        near.wait_recv()
        far.wait_recv()
        grad_second = part_d[b, 0, :BLK] + in_d[b] + x_d[b, 2].astype(f32)
        n2 = n2_ref[b]
        sums_ref[3:4] += jnp.sum(grad_second * n2, axis=0, keepdims=True)
        sums_ref[4:5] += jnp.sum(grad_second, axis=0, keepdims=True)
        pulled = grad_second * small_ref[3:4]
        inward = (
            pulled - jnp.mean(pulled, axis=-1, keepdims=True) - n2 * jnp.mean(pulled * n2, axis=-1, keepdims=True)
        )
        grad_middle = cot_ref[rows_of(b)].astype(f32) + inward * scales[b]
        middle_grad_ref[rows_of(b)] = grad_middle
        branch = grad_middle.astype(bf16)
        branch_ref[rows_of(b)] = branch
        sums_ref[2:3] += jnp.sum(branch.astype(f32), axis=0, keepdims=True)
        grad_out_t = inner(wo_ref[...], branch).astype(bf16)
        for group in range(GROUPS):
            grad_out[group, b] = grad_out_t[HW * group : HW * group + HW]
        for away in range(1, GROUPS):
            to = other_group(away)
            begin(grad_out.at[to, b], grad_t_ref.at[2 * g + b], o_send.at[b, away], o_recv.at[b, g], g=to)
        grad_t_ref[2 * g + b] = grad_out[g, b]

    norm(0)
    norm(1)
    for load in loads:
        load.wait()
    near = [near_pair(0), None]
    passed = [pass_on(0), None]
    near[1] = near_pair(1)
    far = [far_pair(0, passed[0]), None]
    passed[1] = pass_on(1)
    far[1] = far_pair(1, passed[1])

    def over_rows(left, right):
        total = None
        for b in range(2):
            for pair in range(2):
                term = outer(left(b, pair), right(b, pair))
                total = term if total is None else total + term
        return total.astype(bf16)

    def parts(write):
        for y in range(2):
            pl.when(r == y)(lambda: write(keep_ref, y))
            pl.when(r != y)(lambda: write(give_ref, y))

    down_grad = over_rows(lambda b, pair: hids[b, pair], lambda b, pair: pair_of(cots, b, pair))

    def write_down(ref, y):
        for z in range(GROUPS):
            p = y * GROUPS + z
            ref[z, 0:96] = down_grad[96 * p : 96 * p + 96]

    parts(write_down)
    back(0, near[0], far[0])
    up_grad = over_rows(lambda b, pair: pair_of(h2s, b, pair), lambda b, pair: dus[b, pair])

    def up_part(p, h):
        return up_grad[half * h + 48 * p : half * h + 48 * p + 48]

    def write_up(y, h):
        @pl.when((r == y) & (x == h))
        def _():
            for z in range(GROUPS):
                keep_ref[z, 96:144] = up_part(y * GROUPS + z, h)

        @pl.when((r != y) & (x == h))
        def _():
            for z in range(GROUPS):
                give_ref[z, 96:144] = up_part(y * GROUPS + z, h)

        @pl.when((r == y) & (x != h))
        def _():
            for z in range(GROUPS):
                x_give_ref[rows + 48 * z : rows + 48 * z + 48] = up_part(y * GROUPS + z, h)

        @pl.when((r != y) & (x != h))
        def _():
            for z in range(GROUPS):
                far_ref[z] = up_part(y * GROUPS + z, h)

    for y in range(2):
        for h in range(2):
            write_up(y, h)
    back(1, near[1], far[1])

    for owner in range(2):
        for c in range(2):
            piece = dot(attn_t[half * owner + fourth * c : half * owner + fourth * c + fourth], branch_ref[...])

            @pl.when(core == c)
            def _():
                wo_keep[owner] = piece

            @pl.when(core != c)
            def _():
                wo_give[owner] = piece.astype(bf16)

    w_sib = begin(wo_give, wo_in, w_send.at[0], w_recv.at[0], core=sib)
    y_sibs = [
        begin(part_y.at[b, 0, pl.ds(BLK, BLK)], in_y.at[b], y_send.at[b, 0], y_recv.at[b, 0], core=sib)
        for b in range(2)
    ]
    w_sib.wait_recv()
    wo_pass[...] = (wo_keep[other] + wo_in[other].astype(f32)).astype(bf16)
    w_x = begin(wo_pass, wo_x, w_send.at[1], w_recv.at[1], x=other)
    for b in range(2):
        y_passes[b].wait_recv()
        x_give_ref[rows_of(b)] = (part_y[b, 1, :BLK] + pass_y[b].astype(f32)).astype(bf16)
        y_sibs[b].wait_recv()
        base_ref[rows_of(b)] = mid_ref[b] + part_y[b, 0, :BLK] + in_y[b] + small_ref[5:6]
    mine = wo_keep[x] + wo_in[x].astype(f32)
    for b in range(2):
        for away in range(1, GROUPS):
            source = other_group(away)
            arrived(grad_t_ref.at[2 * source + b], o_send.at[b, away], o_recv.at[b, source], x)
    w_x.wait_recv()
    wo_sum = (mine + wo_x[...].astype(f32)).astype(bf16)

    def write_wo(ref, y):
        for z in range(GROUPS):
            p = y * GROUPS + z
            ref[z, 144:KEPT] = wo_sum[24 * p : 24 * p + 24]

    parts(write_wo)
    for move in pending:
        move.wait_send()


def dense(out_t, tokens, cot, cot_x, small, wo, up_mine, up_other, down):
    rows, width = tokens.shape
    dma = pltpu.SemaphoreType.DMA
    full = (rows, width)
    part = (BLK, width)
    pair = (2 * BLK, width)
    fourth = (width // 4, width)
    return pl.pallas_call(
        dense_kernel,
        out_shape=(
            jax.ShapeDtypeStruct(full, f32),
            jax.ShapeDtypeStruct((rows + 48 * GROUPS, width), bf16),
            jax.ShapeDtypeStruct(full, f32),
            jax.ShapeDtypeStruct(out_t.shape, bf16),
            jax.ShapeDtypeStruct((GROUPS, KEPT, width), bf16),
            jax.ShapeDtypeStruct((GROUPS, KEPT, width), bf16),
            jax.ShapeDtypeStruct((GROUPS, 48, width), bf16),
            jax.ShapeDtypeStruct(small.shape, f32),
        ),
        in_specs=[whole_vmem()] * 6 + [anywhere()] * 3,
        out_specs=(whole_vmem(),) * 8,
        scratch_shapes=[
            pltpu.VMEM((width, width), bf16),
            pltpu.VMEM((width, width), bf16),
            pltpu.VMEM((GROUPS, 2, HW, BLK), bf16),
            pltpu.VMEM((width, rows), bf16),
            pltpu.VMEM((2, 4, *part), bf16),
            pltpu.VMEM((2, 4, *part), bf16),
            pltpu.VMEM((2, *part), f32),
            pltpu.VMEM((2, *part), f32),
            pltpu.VMEM((2, BLK, 1), f32),
            pltpu.VMEM((2, 2, *pair), f32),
            pltpu.VMEM((2, 2, *pair), f32),
            pltpu.VMEM((2, *part), f32),
            pltpu.VMEM((2, *part), f32),
            pltpu.VMEM((2, *part), bf16),
            pltpu.VMEM((2, *part), bf16),
            pltpu.VMEM((2, *part), bf16),
            pltpu.VMEM((2, 3, *part), bf16),
            pltpu.VMEM((2, 2, *pair), bf16),
            pltpu.VMEM((2, 2, *pair), bf16),
            pltpu.VMEM(full, bf16),
            pltpu.VMEM((GROUPS, 2, HW, BLK), bf16),
            pltpu.VMEM((2, *fourth), f32),
            pltpu.VMEM((2, *fourth), bf16),
            pltpu.VMEM((2, *fourth), bf16),
            pltpu.VMEM(fourth, bf16),
            pltpu.VMEM(fourth, bf16),
            dma((3,)), dma((2, GROUPS)), dma((2, GROUPS)), dma((2,)), dma((2,)), dma((2, 3)), dma((2, 3)),
            dma((2, 2)), dma((2, 2)), dma((2, 3)), dma((2, 3)), dma((2, GROUPS)), dma((2, GROUPS)), dma((2,)), dma((2,)),
        ],
        compiler_params=pltpu.CompilerParams(
            collective_id=1, has_side_effects=True, vmem_limit_bytes=40 << 20
        ),
        name="dense",
    )(out_t, tokens, cot, cot_x, small, wo, up_mine, up_other, down)


FARTHEST = ((3, 2, 1, 0), (3, 0, 2, 1), (0, 3, 1, 2), (0, 1, 2, 3))


def farthest(g, step):
    picked = FARTHEST[0][step]
    for z in range(1, GROUPS):
        picked = jnp.where(g == z, FARTHEST[z][step], picked)
    return picked


class Chain:
    def __init__(self, g, x, total, parts, inward, outward, out_sem, in_sem):
        self.g, self.x, self.total, self.parts = g, x, total, parts
        self.inward, self.outward, self.out_sem, self.in_sem = inward, outward, out_sem, in_sem

    def move(self, to, way):
        return send(
            self.outward.at[to], self.inward.at[way, to], self.out_sem.at[to], self.in_sem.at[way, to],
            g=jnp.clip(self.g + (1 if way == 0 else -1), 0, GROUPS - 1),
        )

    def step(self, to):
        g = self.g
        self.total[...] = self.parts[to].astype(f32)

        def take(way):
            arrived(self.inward.at[way, to], self.out_sem.at[to], self.in_sem.at[way, to], self.x)
            self.total[...] += self.inward[way, to].astype(f32)

        pl.when((to >= g) & (g > 0))(lambda: take(0))
        pl.when((to <= g) & (g < GROUPS - 1))(lambda: take(1))

        @pl.when(to != g)
        def _():
            self.outward[to] = self.total[...].astype(bf16)

        pl.when(to > g)(lambda: self.move(to, 0).start())
        pl.when(to < g)(lambda: self.move(to, 1).start())

    def finish(self):
        for step in range(GROUPS - 1):
            to = farthest(self.g, step)
            left(self.outward.at[to], self.out_sem.at[to], self.in_sem.at[0, to], self.x)


class Ring:
    def __init__(self, g, x, slot, own_sem, out_sem, in_sem):
        self.g, self.x, self.slot = g, x, slot
        self.own_sem, self.out_sem, self.in_sem = own_sem, out_sem, in_sem

    def move(self, source, way, sem):
        return send(
            self.slot(source), self.slot(source), sem, self.in_sem.at[source],
            g=jnp.clip(self.g + way, 0, GROUPS - 1),
        )

    def start(self):
        g = self.g
        pl.when(g > 0)(lambda: self.move(g, -1, self.own_sem.at[0]).start())
        pl.when(g < GROUPS - 1)(lambda: self.move(g, 1, self.own_sem.at[1]).start())

    def step(self, step):
        g, source = self.g, nearest(self.g, step)
        arrived(self.slot(source), self.out_sem.at[source], self.in_sem.at[source], self.x)
        pl.when((source < g) & (g < GROUPS - 1))(lambda: self.move(source, 1, self.out_sem.at[source]).start())
        pl.when((source > g) & (g > 0))(lambda: self.move(source, -1, self.out_sem.at[source]).start())
        return source

    def finish(self):
        g = self.g
        for i, there in enumerate((g > 0, g < GROUPS - 1)):
            pl.when(there)(lambda: left(self.slot(g), self.own_sem.at[i], self.in_sem.at[g], self.x))
        for step in range(1, GROUPS):
            source = nearest(g, step)
            passed = ((source < g) & (g < GROUPS - 1)) | ((source > g) & (g > 0))
            pl.when(passed)(
                lambda: left(self.slot(source), self.out_sem.at[source], self.in_sem.at[source], self.x)
            )


def arrived(what, out_sem, in_sem, x):
    send(what, what, out_sem, in_sem, x=1 - x).wait_recv()


def left(what, out_sem, in_sem, x):
    send(what, what, out_sem, in_sem, x=1 - x).wait_send()


def scatter_kernel(
    dkv_ref, dq_any, normed_any, wfull_any, tokens_any, mgrad_any, keep_any, over_any, near_any, far_any, small_ref, sums_in,
    tokens_grad_ref, big_ref, qout_ref, kvout_ref, sums_ref,
    dq_ref, normed_ref, wfull_ref, tokens_ref, mgrad_ref, kept, over, near, far,
    own_kv, sib_kv, keep_x, give_x, in_x, give_y, in_y, part_a, total_a, inward_a, outward_a, wg_kv,
    by_sum, total_b, inward_b, outward_b, unit,
    q_keep, q_give, q_in, q_pass, q_x, q_y, q_sum, v_keep, v_give, v_in, v_pass, v_x, v_y, v_sum,
    sums_got, late, late_sum, late_got,
    load_sem, own_sem, k_send, k_recv, x_send, x_recv, y_send, y_recv, ca_send, ca_recv,
    cb_send, cb_recv, rb_own, rb_send, rb_recv,
    fy_send, fy_recv, fs_send, fs_recv,
    q_send, q_recv, rq_own, rq_send, rq_recv, qs_send, qs_recv,
    v_send, v_recv, rv_own, rv_send, rv_recv, vs_send, vs_recv,
    s_send, s_recv, t_send, t_recv, l_sem,
):
    g, r, core, x = place()
    other, sib, far_r = 1 - x, 1 - core, 1 - r
    rows, width = tokens_ref.shape
    half = width // 2
    fourth = half // 2
    wide_q = 2 * BLK
    loads = [
        pltpu.make_async_copy(what, where, load_sem.at[i])
        for i, (what, where) in enumerate(
            (
                (keep_any, kept), (over_any, over), (near_any.at[pl.ds(rows, 48 * GROUPS)], near), (far_any, far),
                (dq_any, dq_ref), (normed_any, normed_ref), (wfull_any, wfull_ref), (tokens_any, tokens_ref),
                (mgrad_any, mgrad_ref),
            )
        )
    ]
    for load in loads:
        load.start()
    greet(g, r, core, x, True, True)
    pending = []

    def begin(src, dst, out_sem, in_sem, **device):
        move = send(src, dst, out_sem, in_sem, **device)
        move.start()
        pending.append(move)
        return move

    def settled(move):
        move.wait_recv()
        move.wait_send()
        pending[:] = [item for item in pending if item is not move]

    kv_moves = []
    for i in range(GROUPS):
        c = farthest(g, i)
        for spot in range(4):
            own = pltpu.make_async_copy(
                dkv_ref.at[seat(spot // 2, core, spot % 2), c], own_kv.at[i, spot], own_sem.at[i, spot]
            )
            own.start()
            across = begin(
                dkv_ref.at[seat(spot // 2, sib, spot % 2), c], sib_kv.at[i, spot],
                k_send.at[i, spot], k_recv.at[i, spot], core=sib,
            )
            kv_moves.append((own, across))

    def split(total, keep, give):
        for owner in range(2):
            for c in range(2):
                low = half * owner + fourth * c
                chunk = total[low : low + fourth]

                @pl.when(core == c)
                def _():
                    keep[owner] = chunk

                @pl.when(core != c)
                def _():
                    give[owner] = chunk.astype(bf16)

    def scaled(c):
        return dq_ref[c] * bf16(SCALE)

    q_move = send(q_give, q_in, q_send.at[0], q_recv.at[0], core=sib)

    def query_grad():
        loads[4].wait()
        loads[5].wait()
        query_total = outer(normed_ref[0], scaled(0))
        for c in range(1, GROUPS):
            query_total += outer(normed_ref[c], scaled(c))
        split(query_total, q_keep, q_give)
        q_move.start()
        line_q = scaled(0).astype(f32)
        for c in range(1, GROUPS):
            line_q += scaled(c).astype(f32)
        sums_ref[pl.ds(16 + g, 1), 0:wide_q] = jnp.sum(line_q, axis=0, keepdims=True)

    sums_ref[...] = jnp.zeros_like(sums_ref)
    sums_ref[0:16] = sums_in[...]
    wg_kv[...] = jnp.zeros_like(wg_kv)

    def q_slot(z):
        return qout_ref.at[core, z]

    def v_slot(z):
        return kvout_ref.at[core, z]

    def b_slot(z):
        return big_ref.at[core, r, z]

    ring_q = Ring(g, x, q_slot, rq_own, rq_send, rq_recv)
    ring_v = Ring(g, x, v_slot, rv_own, rv_send, rv_recv)
    ring_b = Ring(g, x, b_slot, rb_own, rb_send, rb_recv)

    def store(value_ref, slot, sem):
        copy = pltpu.make_async_copy(value_ref, slot, sem)
        copy.start()
        copy.wait()

    def spread_b(z, step):
        begin(b_slot(z), b_slot(z), fy_send.at[step], fy_recv.at[step], r=far_r)
        begin(b_slot(z), b_slot(z), fs_send.at[0, step], fs_recv.at[0, step], core=sib)

    def spread_far(step):
        what = big_ref.at[core, far_r, nearest(g, step)]
        arrived(what, fy_send.at[step], fy_recv.at[step], x)
        begin(what, what, fs_send.at[1, step], fs_recv.at[1, step], core=sib)

    def on_ring_b(step):
        spread_b(ring_b.step(step), step)

    def on_ring_q(step):
        z = ring_q.step(step)
        begin(q_slot(z), q_slot(z), qs_send.at[step], qs_recv.at[step], core=sib)

    def on_ring_v(step):
        z = ring_v.step(step)
        begin(v_slot(z), v_slot(z), vs_send.at[step], vs_recv.at[step], core=sib)

    chain_a = Chain(g, x, total_a, part_a, inward_a, outward_a, ca_send, ca_recv)
    chain_b = Chain(g, x, total_b, by_sum, inward_b, outward_b, cb_send, cb_recv)
    at_end = (g == 0) | (g == GROUPS - 1)
    between = jnp.logical_not(at_end)

    def steps(chain, *which):
        for i in which:
            chain.step(farthest(g, i))

    def on_sibling(i):
        for own, across in kv_moves[4 * i : 4 * i + 4]:
            own.wait()
            across.wait_recv()

        def total(row, column):
            spot = 2 * row + column
            return own_kv[i, spot].astype(f32) + sib_kv[i, spot].astype(f32)

        for k in range(2):
            give_x[i, k] = (total(k, other) if i % 2 == 0 else total(far_r, k)).astype(bf16)
            keep_x[i, k] = total(k, x) if i % 2 == 0 else total(r, k)

    def go_first(i):
        along = {"x": other} if i % 2 == 0 else {"r": far_r}
        begin(give_x.at[i], in_x.at[i], x_send.at[i], x_recv.at[i], **along)

    def on_first(i):
        arrived(in_x.at[i], x_send.at[i], x_recv.at[i], x)
        away, stay, along = (far_r, r, {"r": far_r}) if i % 2 == 0 else (other, x, {"x": other})
        give_y[i] = (keep_x[i, away] + in_x[i, away].astype(f32)).astype(bf16)
        begin(give_y.at[i], in_y.at[i], y_send.at[i], y_recv.at[i], **along)
        keep_x[i, stay] += in_x[i, stay].astype(f32)

    def on_second(i):
        c = farthest(g, i)
        arrived(in_y.at[i], y_send.at[i], y_recv.at[i], x)
        both = (keep_x[i, r if i % 2 == 0 else x] + in_y[i].astype(f32)).astype(bf16)
        part_a[c] = inner(scaled(c), wfull_ref[:, :wide_q]) + inner(both, wfull_ref[:, wide_q:])
        wg_kv[...] += outer(normed_ref[c], both)
        sums_ref[pl.ds(16 + g, 1), wide_q : wide_q + 2 * HW] += jnp.sum(both.astype(f32), axis=0, keepdims=True)

    for load in loads[:4]:
        load.wait()
    own_up = pl.ds(pl.multiple_of(96 + 48 * x, 48), 48)
    their_up = pl.ds(pl.multiple_of(96 + 48 * other, 48), 48)
    for z in range(GROUPS):
        pair = kept[z].astype(f32) + over[z].astype(f32)
        by_sum[z, 0:96] = pair[0:96]
        by_sum[z, own_up] = pair[96:144]
        by_sum[z, 192:UNIT] = pair[144:KEPT]
        by_sum[z, their_up] = near[48 * z : 48 * z + 48].astype(f32) + far[z].astype(f32)
    pl.when(at_end)(lambda: steps(chain_b, 0, 1, 2))
    on_sibling(0)
    go_first(0)
    on_sibling(1)
    go_first(1)
    on_sibling(2)
    on_sibling(3)
    pl.when(between)(lambda: steps(chain_b, 0))
    query_grad()
    on_first(0)
    on_first(1)
    go_first(2)
    go_first(3)
    pl.when(between)(lambda: steps(chain_b, 1, 2))
    settled(q_move)
    q_pass[...] = (q_keep[other] + q_in[other].astype(f32)).astype(bf16)
    q_across = begin(q_pass, q_x, q_send.at[1], q_recv.at[1], x=other)
    loads[6].wait()
    on_second(0)
    on_second(1)
    pl.when(at_end)(lambda: steps(chain_a, 0))
    chain_b.step(g)
    unit[...] = total_b[...].astype(bf16)
    store(unit, b_slot(g), l_sem.at[0])
    ring_b.start()
    spread_b(g, 0)
    pl.when(at_end)(lambda: steps(chain_a, 1))
    on_first(2)
    on_first(3)
    q_across.wait_recv()
    q_sum[...] = (q_keep[x] + q_in[x].astype(f32) + q_x[...].astype(f32)).astype(bf16)
    q_over = begin(q_sum, q_y, q_send.at[2], q_recv.at[2], r=far_r)
    pl.when(between)(lambda: steps(chain_a, 0))
    on_second(2)
    on_second(3)
    pl.when(at_end)(lambda: steps(chain_a, 2))
    split(wg_kv, v_keep, v_give)
    v_move = begin(v_give, v_in, v_send.at[0], v_recv.at[0], core=sib)
    s_sib = begin(sums_ref, sums_got.at[0], s_send.at[0], s_recv.at[0], core=sib)
    spread_far(0)
    settled(q_over)
    q_sum[...] = (q_sum[...].astype(f32) + q_y[...].astype(f32)).astype(bf16)
    store(q_sum, q_slot(g), l_sem.at[0])
    ring_q.start()
    begin(q_slot(g), q_slot(g), qs_send.at[0], qs_recv.at[0], core=sib)
    on_ring_b(1)
    v_move.wait_recv()
    v_pass[...] = (v_keep[other] + v_in[other].astype(f32)).astype(bf16)
    v_across = begin(v_pass, v_x, v_send.at[1], v_recv.at[1], x=other)
    settled(s_sib)
    sums_ref[...] += sums_got[0]
    s_x = begin(sums_ref, sums_got.at[1], s_send.at[1], s_recv.at[1], x=other)
    pl.when(between)(lambda: steps(chain_a, 1))
    v_across.wait_recv()
    v_sum[...] = (v_keep[x] + v_in[x].astype(f32) + v_x[...].astype(f32)).astype(bf16)
    v_over = begin(v_sum, v_y, v_send.at[2], v_recv.at[2], r=far_r)
    settled(s_x)
    sums_ref[...] += sums_got[1]
    s_y = begin(sums_ref, sums_got.at[2], s_send.at[2], s_recv.at[2], r=far_r)
    on_ring_b(2)
    pl.when(between)(lambda: steps(chain_a, 2))
    settled(v_over)
    v_sum[...] = (v_sum[...].astype(f32) + v_y[...].astype(f32)).astype(bf16)
    store(v_sum, v_slot(g), l_sem.at[0])
    ring_v.start()
    begin(v_slot(g), v_slot(g), vs_send.at[0], vs_recv.at[0], core=sib)
    settled(s_y)
    sums_ref[...] += sums_got[2]
    for away in range(1, GROUPS):
        begin(
            sums_ref, sums_got.at[2 + away], s_send.at[2 + away], s_recv.at[2 + away],
            g=lax.rem(g + away, GROUPS),
        )
    spread_far(1)
    on_ring_q(1)
    on_ring_b(3)
    chain_a.step(g)

    loads[7].wait()
    loads[8].wait()
    grad_first = total_a[...]
    values = tokens_ref[...].astype(f32)
    mean = jnp.mean(values, axis=-1, keepdims=True)
    centred = values - mean
    scale = lax.rsqrt(jnp.mean(centred * centred, axis=-1, keepdims=True) + EPS)
    n1 = centred * scale
    pulled = grad_first * small_ref[0:1]
    inward = pulled - jnp.mean(pulled, axis=-1, keepdims=True) - n1 * jnp.mean(pulled * n1, axis=-1, keepdims=True)
    tokens_grad_ref[...] = mgrad_ref[...] + inward * scale
    late[...] = jnp.zeros_like(late)
    late[0:1] = jnp.sum(grad_first * n1, axis=0, keepdims=True)
    late[1:2] = jnp.sum(grad_first, axis=0, keepdims=True)
    for step in range(len(AROUND)):
        begin(late, late_got.at[step], t_send.at[step], t_recv.at[step], **neighbour(r, core, x, step))
    on_ring_v(1)
    on_ring_q(2)
    on_ring_q(3)
    spread_far(2)
    on_ring_v(2)
    late_sum[...] = late[...]
    for step in range(len(AROUND)):
        arrived(late_got.at[step], t_send.at[step], t_recv.at[step], x)
        late_sum[...] += late_got[step]
    first_z = len(AROUND) - 1
    for away in range(1, GROUPS):
        begin(
            late_sum, late_got.at[first_z + away], t_send.at[first_z + away], t_recv.at[first_z + away],
            g=lax.rem(g + away, GROUPS),
        )
    on_ring_v(3)
    spread_far(3)

    for away in range(1, GROUPS):
        arrived(sums_got.at[2 + away], s_send.at[2 + away], s_recv.at[2 + away], x)
        arrived(late_got.at[first_z + away], t_send.at[first_z + away], t_recv.at[first_z + away], x)
    for step in range(GROUPS):
        z = nearest(g, step)
        arrived(qout_ref.at[sib, z], qs_send.at[step], qs_recv.at[step], x)
        arrived(kvout_ref.at[sib, z], vs_send.at[step], vs_recv.at[step], x)
        arrived(big_ref.at[sib, r, z], fs_send.at[0, step], fs_recv.at[0, step], x)
        arrived(big_ref.at[sib, far_r, z], fs_send.at[1, step], fs_recv.at[1, step], x)
    for move in pending:
        move.wait_send()
    for item in (chain_a, chain_b, ring_q, ring_v, ring_b):
        item.finish()
    sums_ref[...] += sums_got[3] + sums_got[4] + sums_got[5]
    total = late_sum[...] + late_got[first_z + 1] + late_got[first_z + 2] + late_got[first_z + 3]
    sums_ref[0:2] = total[0:2]


def scatter(dkv, dq, normed, wfull, tokens, mgrad, small, keep, over, near, far, sums):
    rows, width = tokens.shape
    fourth = width // 4
    dma = pltpu.SemaphoreType.DMA
    wide_q, wide_v = 2 * BLK, 2 * HW
    kv_block = (rows, wide_v)
    full = (rows, width)
    unit = (UNIT, width)

    def weight_scratch(wide):
        return [
            pltpu.VMEM((2, fourth, wide), f32),
            pltpu.VMEM((2, fourth, wide), bf16),
            pltpu.VMEM((2, fourth, wide), bf16),
            *[pltpu.VMEM((fourth, wide), bf16)] * 4,
        ]

    return pl.pallas_call(
        scatter_kernel,
        out_shape=(
            jax.ShapeDtypeStruct(full, f32),
            jax.ShapeDtypeStruct((2, 2, GROUPS, *unit), bf16),
            jax.ShapeDtypeStruct((2, GROUPS, fourth, wide_q), bf16),
            jax.ShapeDtypeStruct((2, GROUPS, fourth, wide_v), bf16),
            jax.ShapeDtypeStruct((24, width), f32),
        ),
        in_specs=[anywhere()] * 10 + [whole_vmem()] * 2,
        out_specs=(whole_vmem(), anywhere(), anywhere(), anywhere(), whole_vmem()),
        scratch_shapes=[
            *[
                pltpu.VMEM(item.shape, item.dtype)
                for item in (dq, normed, wfull, tokens, mgrad, keep, over)
            ],
            pltpu.VMEM((48 * GROUPS, width), bf16),
            pltpu.VMEM(far.shape, bf16),
            pltpu.VMEM((GROUPS, 4, *kv_block), bf16),
            pltpu.VMEM((GROUPS, 4, *kv_block), bf16),
            pltpu.VMEM((GROUPS, 2, *kv_block), f32),
            pltpu.VMEM((GROUPS, 2, *kv_block), bf16),
            pltpu.VMEM((GROUPS, 2, *kv_block), bf16),
            pltpu.VMEM((GROUPS, *kv_block), bf16),
            pltpu.VMEM((GROUPS, *kv_block), bf16),
            pltpu.VMEM((GROUPS, *full), f32),
            pltpu.VMEM(full, f32),
            pltpu.VMEM((2, GROUPS, *full), bf16),
            pltpu.VMEM((GROUPS, *full), bf16),
            pltpu.VMEM((width, wide_v), f32),
            pltpu.VMEM((GROUPS, *unit), f32),
            pltpu.VMEM(unit, f32),
            pltpu.VMEM((2, GROUPS, *unit), bf16),
            pltpu.VMEM((GROUPS, *unit), bf16),
            pltpu.VMEM(unit, bf16),
            *weight_scratch(wide_q),
            *weight_scratch(wide_v),
            pltpu.VMEM((6, 24, width), f32),
            pltpu.VMEM((8, width), f32),
            pltpu.VMEM((8, width), f32),
            pltpu.VMEM((len(AROUND) + GROUPS - 1, 8, width), f32),
            dma((9,)),
            dma((GROUPS, 4)), dma((GROUPS, 4)), dma((GROUPS, 4)), dma((GROUPS,)), dma((GROUPS,)), dma((GROUPS,)), dma((GROUPS,)),
            dma((GROUPS,)), dma((2, GROUPS)),
            dma((GROUPS,)), dma((2, GROUPS)), dma((2,)), dma((GROUPS,)), dma((GROUPS,)),
            dma((GROUPS,)), dma((GROUPS,)), dma((2, GROUPS)), dma((2, GROUPS)),
            dma((3,)), dma((3,)), dma((2,)), dma((GROUPS,)), dma((GROUPS,)), dma((GROUPS,)), dma((GROUPS,)),
            dma((3,)), dma((3,)), dma((2,)), dma((GROUPS,)), dma((GROUPS,)), dma((GROUPS,)), dma((GROUPS,)),
            dma((6,)), dma((6,)), dma((10,)), dma((10,)), dma((1,)),
        ],
        compiler_params=pltpu.CompilerParams(
            collective_id=2, has_side_effects=True, vmem_limit_bytes=54 << 20
        ),
        name="scatter",
    )(dkv, dq, normed, wfull, tokens, mgrad, keep, over, near, far, small, sums)


def pack_kv(key_part, value_part):
    return jnp.concatenate(
        [key_part, value_part[..., 2 * DH :], value_part[..., : 2 * DH]], axis=-1
    )


def unpack_kv(both):
    return both[..., :HW], jnp.concatenate([both[..., HW + DH :], both[..., HW : HW + DH]], axis=-1)


def layout_kernel(
    big_ref, query_ref, kv_ref, sums_ref, base_ref, got_ref,
    up_out, down_out, wo_out, query_out, key_out, value_out,
    low_gain, low_shift, query_bias, value_bias, out_bias, high_gain, high_shift, up_bias, down_bias, result_out,
):
    x = lax.axis_index("x")
    width = big_ref.shape[-1]
    half = width // 2
    result_out[...] = (base_ref[...] + got_ref[...].astype(f32)).astype(bf16)
    for core in range(2):
        down_out[core] = big_ref[core, 0, 0:96].astype(f32)
        wo_out[core] = big_ref[core, 0, 192:UNIT].astype(f32)
        for owner in range(2):
            lane = (2 * owner + core) * width
            up_out[:, lane : lane + width] = big_ref[core, 0, 96 + 48 * owner : 144 + 48 * owner].astype(f32)
        query_out[core] = jnp.concatenate(
            [query_ref[core, z].astype(f32)[:, :HW] for z in range(GROUPS)], axis=1
        )
        both = [unpack_kv(kv_ref[core, z].astype(f32)) for z in range(GROUPS)]
        key_out[core] = jnp.concatenate([item[0] for item in both], axis=1)
        value_out[core] = jnp.concatenate([item[1] for item in both], axis=1)

    @pl.when(pl.program_id(0) == 0)
    def _():
        def own_half(row):
            whole = sums_ref[row : row + 1]
            return jnp.where(x == 0, whole[:, :half], whole[:, half:]).reshape(half)

        for ref, row in (
            (low_gain, 0), (low_shift, 1), (out_bias, 2), (high_gain, 3), (high_shift, 4), (down_bias, 5),
        ):
            ref[...] = own_half(row)
        pair = [sums_ref[pl.ds(16 + 2 * x + i, 1)] for i in range(2)]
        query_bias[...] = jnp.concatenate([item[:, :HW] for item in pair], axis=1).reshape(half)
        value_bias[...] = jnp.concatenate(
            [unpack_kv(item[:, 2 * BLK : 2 * BLK + 2 * HW])[1] for item in pair], axis=1
        ).reshape(half)
        up_bias[...] = jnp.concatenate(
            [sums_ref[pl.ds(8 + 2 * x + i, 1)] for i in range(2)], axis=1
        ).reshape(2 * width)


def lay_out(big, query, kv, sums, base, got):
    width = big.shape[-1]
    half, fourth = width // 2, width // 4
    rows = fourth // PARTS

    def spec(shape, index):
        return pl.BlockSpec(shape, index)

    def fixed(wide):
        return pl.BlockSpec((wide,), lambda p: (0,))

    narrow = spec((2, rows, width), lambda p: (0, p, 0))
    vector = jax.ShapeDtypeStruct((half,), f32)
    return pl.pallas_call(
        layout_kernel,
        grid=(PARTS,),
        out_shape=(
            jax.ShapeDtypeStruct((half, 4 * width), f32),
            jax.ShapeDtypeStruct((2, width, width), f32),
            *[jax.ShapeDtypeStruct((2, fourth, width), f32)] * 4,
            *[vector] * 7,
            jax.ShapeDtypeStruct((2 * width,), f32),
            vector,
            jax.ShapeDtypeStruct(base.shape, bf16),
        ),
        in_specs=[
            spec((2, 1, UNIT, width), lambda p: (0, p, 0, 0)),
            spec((2, GROUPS, rows, query.shape[-1]), lambda p: (0, 0, p, 0)),
            spec((2, GROUPS, rows, kv.shape[-1]), lambda p: (0, 0, p, 0)),
            spec(sums.shape, lambda p: (0, 0)),
            spec((base.shape[0] // PARTS, width), lambda p: (p, 0)),
            spec((base.shape[0] // PARTS, width), lambda p: (p, 0)),
        ],
        out_specs=(
            spec((48, 4 * width), lambda p: (p, 0)),
            spec((2, 96, width), lambda p: (0, p, 0)),
            *[narrow] * 4,
            *[fixed(half)] * 7,
            fixed(2 * width),
            fixed(half),
            spec((base.shape[0] // PARTS, width), lambda p: (p, 0)),
        ),
        compiler_params=pltpu.CompilerParams(
            vmem_limit_bytes=VMEM_LIMIT, dimension_semantics=("arbitrary",)
        ),
        name="lay_out",
    )(big, query, kv, sums, base, got)


ROWS = ("s", "r", "core", "x")
ALL = ("g", "s", "r", "core", "x")


def shards(
    tokens, cotangent, doc_lengths, deal, first_gain, first_shift, query_weight, query_bias,
    key_weight, value_weight, value_bias, output_weight, output_bias, second_gain, second_shift,
    up_weight, up_bias, down_weight, down_bias,
):
    rows, width = tokens.shape
    half = width // 2
    blocks = deal.shape[0]
    core, x = lax.axis_index("core"), lax.axis_index("x")
    swap = ((0, 1), (1, 0))

    def up_columns(owner):
        return lax.dynamic_slice_in_dim(up_weight, (2 * owner + core) * width, width, 1)

    kv, q, normed, small, wfull, wo = gather(
        tokens, query_weight, key_weight, value_weight, output_weight,
        first_gain, first_shift, output_bias, second_gain, second_shift, down_bias, query_bias, value_bias, up_bias,
    )
    wide = blocks > 8 * 2 * GROUPS
    if wide:
        kv = lax.all_gather(kv, "s", axis=0, tiled=True)
    kv = kv.reshape(blocks, BLK, 2 * HW)
    q = q.reshape(2 * GROUPS, BLK, 2 * BLK)
    cot_x, up_other, kv = lax.optimization_barrier((cotangent, up_columns(1 - x), kv))
    up_other = lax.ppermute(up_other, "x", swap)
    cot_x = lax.ppermute(cot_x, "x", swap)
    out_t, kept, lse = attend_forward(deal, doc_lengths, q, kv)
    base, x_give, grad_middle, grad_t, kept_part, over, far, sums = dense(
        out_t, tokens, cotangent, cot_x, small, wo, up_columns(x), up_other, down_weight
    )
    over = lax.ppermute(over, "r", swap)
    x_got = lax.ppermute(x_give, "x", swap)
    far = lax.ppermute(far, ("r", "x"), ((0, 3), (1, 2), (2, 1), (3, 0)))
    dq, dkv = attend_backward(deal, doc_lengths, q, kv, lse, grad_t, kept)
    dkv = dkv.reshape(-1, GROUPS, rows, 2 * HW)
    if wide:
        dkv = lax.psum_scatter(dkv, "s", scatter_dimension=0, tiled=True)
    dq = dq.reshape(GROUPS, rows, 2 * BLK)
    grad_tokens, big, query_own, kv_own, sums = scatter(
        dkv, dq, normed, wfull, tokens, grad_middle, small, kept_part, over, x_got, far, sums
    )
    if wide:
        big, query_own, kv_own, sums = (
            lax.psum(item, "s") for item in (big, query_own, kv_own, sums)
        )

    (
        up_own, down_own, wo_own, query_own, key_own, value_own,
        low_gain, low_shift, query_sum, value_sum, out_sum, high_gain, high_shift, up_sum, down_sum, result,
    ) = lay_out(big.reshape(2, PARTS, UNIT, width), query_own, kv_own, sums, base, x_got)

    def flat(item):
        return item.reshape(-1, width)

    return (
        result,
        grad_tokens,
        low_gain,
        low_shift,
        flat(query_own),
        query_sum,
        flat(key_own),
        flat(value_own),
        value_sum,
        flat(wo_own),
        out_sum,
        high_gain,
        high_shift,
        up_own,
        up_sum,
        flat(down_own),
        down_sum,
    )


def solution(mesh):
    devices = mesh.devices
    inner_mesh = Mesh(devices.reshape(GROUPS, devices.shape[0] // (4 * GROUPS), 2, 2, 2), ALL)
    row = P(ALL, None)
    mat = P("x", None)
    vec = P("x")
    in_specs = (
        row, row, P(), P(), vec, vec, mat, vec, mat, mat, vec, mat, vec, vec, vec, mat, vec, mat, vec,
    )
    out_specs = (
        row, row, vec, vec, mat, vec, mat, mat, vec, mat, vec, vec, vec, mat, vec, mat, vec,
    )
    return jax.shard_map(
        shards, mesh=inner_mesh, in_specs=in_specs, out_specs=out_specs, check_vma=False
    )
```

```python
import jax
import jax.numpy as jnp
from jax import lax
from jax.experimental import pallas as pl
from jax.experimental.pallas import tpu as pltpu
from jax.sharding import Mesh
from jax.sharding import PartitionSpec as P

HEADS = 12
DH = 64
NSUM = 50
SEG = 2048
BLK = 128
GROUPS = 4
PER = HEADS // GROUPS
HW = PER * DH
WIDE = PER * BLK
CHUNK = 2 * BLK
DEPTH = 8
EPS = 1e-05
SCALE = 0.125
MASKED = -1e30
ROOT_HALF = 0.7071067811865476
PDF_SCALE = 0.3989422804014327
VMEM_LIMIT = 56 << 20
bf16 = jnp.bfloat16
f32 = jnp.float32


def layer_norm(values, gain, shift):
    mean = jnp.mean(values, axis=-1, keepdims=True)
    centred = values - mean
    spread = jnp.mean(centred * centred, axis=-1, keepdims=True)
    return centred * lax.rsqrt(spread + EPS) * gain + shift


def outer(left, right):
    return lax.dot_general(left, right, (((0,), (0,)), ((), ())), preferred_element_type=f32)


def inner(left, right):
    return lax.dot_general(left, right, (((1,), (1,)), ((), ())), preferred_element_type=f32)


def dot(left, right):
    return jnp.dot(left, right, preferred_element_type=f32)


def survey(deal_ref, lengths_ref, where_ref, text_ref, low_ref, high_ref, first_ref):
    blocks = deal_ref.shape[0]
    per_group = blocks // (2 * GROUPS)
    rest = lax.axis_index(ROWS)

    def note(j, kept):
        pair = j // 2
        group = pair // per_group
        where_ref[deal_ref[j]] = ((pair - group * per_group) * GROUPS + group) * 2 + j % 2
        return kept

    lax.fori_loop(0, blocks, note, 0)
    starts = [jnp.int32(0)]
    for doc in range(lengths_ref.shape[0] - 1):
        starts.append(starts[-1] + lengths_ref[doc])

    def first_of(at):
        begin = jnp.zeros_like(at)
        for start in starts:
            begin = jnp.where(start <= at, jnp.maximum(begin, start), begin)
        return jnp.where(at - begin >= SEG + NSUM, begin + SEG, begin)

    for slot in range(2 * GROUPS):
        text = deal_ref[2 * ((slot // 2) * per_group + rest) + slot % 2]
        text_ref[slot] = text
        low_ref[slot] = first_of(text * BLK) // CHUNK
        high_ref[slot] = text // 2
        first_ref[slot] = first_of(text * BLK + lax.broadcasted_iota(jnp.int32, (1, BLK), 1))


def survey_scratch(blocks):
    slots = 2 * GROUPS
    return [
        pltpu.SMEM((blocks,), jnp.int32),
        pltpu.SMEM((slots,), jnp.int32),
        pltpu.SMEM((slots,), jnp.int32),
        pltpu.SMEM((slots,), jnp.int32),
        pltpu.VMEM((slots, 1, BLK), jnp.int32),
    ]


def spread_heads_t(part_t, order):
    rows = []
    zero = jnp.zeros((DH, BLK), part_t.dtype)
    for head in order:
        if head is None:
            rows.append(jnp.zeros((DH, WIDE), part_t.dtype))
        else:
            piece = part_t[DH * head : DH * head + DH]
            rows.append(
                jnp.concatenate([piece if h == head else zero for h in range(PER)], axis=1)
            )
    return jnp.concatenate(rows, axis=0)


K_ORDER = (0, 1, 2, None)
V_ORDER = (None, 2, 0, 1)


def visible(chunk, first, own):
    at = chunk * CHUNK + lax.broadcasted_iota(jnp.int32, (CHUNK, BLK), 0)
    allowed = (at >= first) & (at <= own)
    return jnp.concatenate([allowed] * PER, axis=1)


def load_chunk(kv_ref, where_ref, chunk):
    return jnp.concatenate(
        [kv_ref[where_ref[2 * chunk]], kv_ref[where_ref[2 * chunk + 1]]], axis=0
    )


def forward_kernel(
    deal_ref, lengths_ref, q_ref, kv_ref,
    out_ref, wide_ref, lse_ref,
    where_ref, text_ref, low_ref, high_ref, first_ref, acc_ref,
):
    survey(deal_ref, lengths_ref, where_ref, text_ref, low_ref, high_ref, first_ref)

    def one_slot(slot, kept):
        wide_q = spread_heads_t(q_ref[slot].T[:HW], K_ORDER)
        first = first_ref[slot]
        own = text_ref[slot] * BLK + lax.broadcasted_iota(jnp.int32, (1, BLK), 1)
        last_first = jnp.max(first)
        acc_ref[...] = jnp.zeros_like(acc_ref)

        def step(double, carry):
            top, total = carry
            scores = []
            for part in range(2):
                keys = load_chunk(kv_ref, where_ref, 2 * double + part)[:, : 2 * BLK]
                scores.append(jnp.where(visible(2 * double + part, first, own), dot(keys, wide_q), MASKED))
            scores = jnp.concatenate(scores, axis=0)
            fresh = jnp.maximum(top, jnp.max(scores, axis=0, keepdims=True))
            expo = jnp.exp(scores - fresh)
            shrink = jnp.exp(top - fresh)
            total = total * shrink + jnp.sum(expo, axis=0, keepdims=True)
            vals = jnp.concatenate([load_chunk(kv_ref, where_ref, 2 * double + part)[:, BLK:] for part in range(2)], axis=0)
            acc_ref[...] = acc_ref[...] * shrink + outer(vals, expo.astype(bf16))
            return fresh, total

        top, total = lax.fori_loop(
            low_ref[slot] // 2,
            high_ref[slot] // 2 + 1,
            step,
            (jnp.full((1, WIDE), MASKED, f32), jnp.zeros((1, WIDE), f32)),
        )
        lse_ref[slot] = top + jnp.log(total)
        scaled = acc_ref[...] / total
        pieces = []
        for head in range(PER):
            row = DH * V_ORDER.index(head)
            pieces.append(scaled[row : row + DH, BLK * head : BLK * head + BLK])
        whole = jnp.concatenate(pieces, axis=0)
        wide_ref[slot] = whole
        out_ref[slot] = whole.astype(bf16)
        return kept

    lax.fori_loop(0, q_ref.shape[0], one_slot, 0)


def whole_vmem():
    return pl.BlockSpec(memory_space=pltpu.VMEM)


def whole_smem():
    return pl.BlockSpec(memory_space=pltpu.SMEM)


def attend_forward(deal, lengths, q, kv):
    slots = q.shape[0]
    blocks = kv.shape[0]
    return pl.pallas_call(
        forward_kernel,
        out_shape=(
            jax.ShapeDtypeStruct((slots, HW, BLK), bf16),
            jax.ShapeDtypeStruct((slots, HW, BLK), f32),
            jax.ShapeDtypeStruct((slots, 1, WIDE), f32),
        ),
        in_specs=[whole_smem()] * 2 + [whole_vmem()] * 2,
        out_specs=(whole_vmem(),) * 3,
        scratch_shapes=[
            *survey_scratch(blocks),
            pltpu.VMEM((2 * BLK, WIDE), f32),
        ],
        compiler_params=pltpu.CompilerParams(vmem_limit_bytes=(6 << 20) + kv.size // 5 * 16),
        name="attend_forward",
    )(deal, lengths, q, kv)


def backward_kernel(
    deal_ref, lengths_ref, q_ref, kv_ref, lse_ref, do_ref, wide_ref,
    dq_ref, dkv_ref, where_ref, text_ref, low_ref, high_ref, first_ref, qt_ref, qm_ref, dot_ref, dom_ref, delta_ref, acc_ref, dk_acc, dv_acc,
    packed_ref, count_ref, list_ref, out_sem,
):
    survey(deal_ref, lengths_ref, where_ref, text_ref, low_ref, high_ref, first_ref)
    slots = q_ref.shape[0]
    chunks = kv_ref.shape[0] // 2

    def ready(slot, _):
        q = q_ref[slot]
        qt_ref[slot] = spread_heads_t(q.T[:HW], K_ORDER)
        lane = lax.broadcasted_iota(jnp.int32, (BLK, 2 * BLK), 1) // DH
        zero = jnp.zeros_like(q)
        qm_ref[slot] = jnp.concatenate(
            [jnp.where(lane == K_ORDER.index(h), q, zero) for h in range(PER)], axis=0
        )
        grad_t = do_ref[slot]
        dot_ref[slot] = spread_heads_t(grad_t, V_ORDER)
        ordered = jnp.concatenate(
            [
                jnp.zeros((DH, BLK), bf16) if h is None else grad_t[DH * h : DH * h + DH]
                for h in V_ORDER
            ],
            axis=0,
        ).T
        dom_ref[slot] = jnp.concatenate(
            [jnp.where(lane == V_ORDER.index(h), ordered, zero) for h in range(PER)], axis=0
        )
        both = grad_t.astype(f32) * wide_ref[slot]
        delta_ref[slot] = jnp.concatenate(
            [jnp.sum(both[DH * h : DH * h + DH], axis=0, keepdims=True) for h in range(PER)],
            axis=1,
        )
        acc_ref[slot] = jnp.zeros((HW, WIDE), f32)
        return _

    lax.fori_loop(0, slots, ready, 0)

    def clear(chunk, kept):
        count_ref[chunk] = 0
        return kept

    lax.fori_loop(0, chunks, clear, 0)

    def enlist(slot, kept):
        def seen(chunk, kept):
            count = count_ref[chunk]
            list_ref[chunk * slots + count] = slot
            count_ref[chunk] = count + 1
            return kept

        lax.fori_loop(low_ref[slot], high_ref[slot] + 1, seen, 0)
        return kept

    lax.fori_loop(0, slots, enlist, 0)

    def written(chunk, i):
        return pltpu.make_async_copy(
            packed_ref.at[chunk % DEPTH, i], dkv_ref.at[where_ref[2 * chunk + i]], out_sem.at[chunk % DEPTH, i]
        )

    def one_chunk(chunk, kept):
        part = load_chunk(kv_ref, where_ref, chunk)
        keys = part[:, : 2 * BLK]
        vals = part[:, BLK:]
        keys_t = keys.T[:HW]
        dk_acc[...] = jnp.zeros_like(dk_acc)
        dv_acc[...] = jnp.zeros_like(dv_acc)

        def one_slot(i, kept):
            for half in range(2):
                attend(list_ref[chunk * slots + 2 * i + half])
            return kept

        def attend(slot):
            own = text_ref[slot] * BLK + lax.broadcasted_iota(jnp.int32, (1, BLK), 1)
            scores = dot(keys, qt_ref[slot])
            dprobs = dot(vals, dot_ref[slot])
            probs = jnp.where(visible(chunk, first_ref[slot], own), jnp.exp(scores - lse_ref[slot]), 0.0)
            dscores = (probs * (dprobs - delta_ref[slot])).astype(bf16)
            dv_acc[...] += dot(probs.astype(bf16), dom_ref[slot])
            dk_acc[...] += dot(dscores, qm_ref[slot])
            acc_ref[slot] += dot(keys_t, dscores)

        lax.fori_loop(0, count_ref[chunk] // 2, one_slot, 0)
        pl.when(count_ref[chunk] % 2 == 1)(lambda: attend(list_ref[chunk * slots + count_ref[chunk] - 1]))
        packed = jnp.concatenate(
            [
                dk_acc[:, :BLK],
                dk_acc[:, BLK:] + dv_acc[:, :BLK],
                dv_acc[:, BLK:],
            ],
            axis=1,
        ).astype(bf16)

        @pl.when(chunk >= DEPTH)
        def _():
            for i in range(2):
                written(chunk - DEPTH, i).wait()

        for i in range(2):
            packed_ref[chunk % DEPTH, i] = packed[BLK * i : BLK * i + BLK]
            written(chunk, i).start()
        return kept

    lax.fori_loop(0, chunks, one_chunk, 0)
    for last in range(DEPTH):
        for i in range(2):
            written(chunks - DEPTH + last, i).wait()

    def finish(slot, _):
        total = acc_ref[slot]
        kept = jnp.concatenate(
            [total[DH * h : DH * h + DH, BLK * h : BLK * h + BLK] for h in range(PER)]
            + [jnp.zeros((DH, BLK), f32)],
            axis=0,
        )
        dq_ref[slot] = kept.T.astype(bf16)
        return _

    lax.fori_loop(0, slots, finish, 0)


def attend_backward(deal, lengths, q, kv, lse, grad_t, wide):
    slots = q.shape[0]
    return pl.pallas_call(
        backward_kernel,
        out_shape=(
            jax.ShapeDtypeStruct((slots, BLK, 2 * BLK), bf16),
            jax.ShapeDtypeStruct(kv.shape, bf16),
        ),
        in_specs=[whole_smem()] * 2 + [whole_vmem()] * 5,
        out_specs=(whole_vmem(), in_hbm()),
        scratch_shapes=[
            *survey_scratch(kv.shape[0]),
            pltpu.VMEM((slots, 2 * BLK, WIDE), bf16),
            pltpu.VMEM((slots, WIDE, 2 * BLK), bf16),
            pltpu.VMEM((slots, 2 * BLK, WIDE), bf16),
            pltpu.VMEM((slots, WIDE, 2 * BLK), bf16),
            pltpu.VMEM((slots, 1, WIDE), f32),
            pltpu.VMEM((slots, HW, WIDE), f32),
            pltpu.VMEM((CHUNK, 2 * BLK), f32),
            pltpu.VMEM((CHUNK, 2 * BLK), f32),
            pltpu.VMEM((DEPTH, 2, BLK, 2 * HW), bf16),
            pltpu.SMEM((kv.shape[0] // 2,), jnp.int32),
            pltpu.SMEM((kv.shape[0] // 2 * slots,), jnp.int32),
            pltpu.SemaphoreType.DMA((DEPTH, 2)),
        ],
        compiler_params=pltpu.CompilerParams(
            vmem_limit_bytes=max(48 << 20, (17 << 20) + kv.size * 2)
        ),
        name="attend_backward",
    )(deal, lengths, q, kv, lse, grad_t, wide)


MESH = pl.DeviceIdType.MESH


def send(src, dst, out_sem, in_sem, **device):
    return pltpu.make_async_remote_copy(
        src_ref=src, dst_ref=dst, send_sem=out_sem, recv_sem=in_sem, device_id=device, device_id_type=MESH
    )


def place():
    return tuple(lax.axis_index(name) for name in ("g", "r", "core", "x"))


def seat(r, core, x):
    return (r * 2 + core) * 2 + x


AROUND = ((0, 0, 1), (0, 1, 0), (0, 1, 1), (1, 0, 0), (1, 0, 1), (1, 1, 0), (1, 1, 1))


def neighbour(r, core, x, step):
    dr, dc, dx = AROUND[step]
    return {"r": 1 - r if dr else r, "core": 1 - core if dc else core, "x": 1 - x if dx else x}


def greet(g, r, core, x, line, around=False):
    barrier = pltpu.get_barrier_semaphore()

    def hello(**device):
        pl.semaphore_signal(barrier, inc=1, device_id=device, device_id_type=MESH)

    if around:
        for step in range(len(AROUND)):
            hello(**neighbour(r, core, x, step))
    else:
        hello(core=1 - core)
        hello(x=1 - x)
        hello(r=1 - r)
    near = len(AROUND) if around else 3
    if line:
        for away in range(1, GROUPS):
            hello(g=lax.rem(g + away, GROUPS))
        pl.semaphore_wait(barrier, near + GROUPS - 1)
    else:
        pl.when(g > 0)(lambda: hello(g=g - 1))
        pl.when(g < GROUPS - 1)(lambda: hello(g=g + 1))
        pl.semaphore_wait(barrier, near + 2 - jnp.where(g == 0, 1, 0) - jnp.where(g == GROUPS - 1, 1, 0))


NEAREST = ((0, 1, 2, 3), (1, 2, 0, 3), (2, 1, 3, 0), (3, 2, 1, 0))


def nearest(g, step):
    picked = NEAREST[0][step]
    for z in range(1, GROUPS):
        picked = jnp.where(g == z, NEAREST[z][step], picked)
    return picked


def prepare(g, x, weights, lines, narrow_ref, small_ref):
    half = weights.shape[1]
    odd = lax.rem(g, 2) == 1

    def columns(i):
        low = pl.multiple_of(3 * g // 2 * BLK, BLK)
        window = weights[i, :, pl.ds(low, 2 * BLK)]
        moved = jnp.concatenate([window[:, DH:], window[:, :DH]], axis=1)
        return jnp.where(odd, moved, window)

    lane = lax.broadcasted_iota(jnp.int32, (half, 2 * BLK), 1)
    query = columns(0)
    narrow_ref[:, : 2 * BLK] = jnp.where(lane < HW, query, jnp.zeros_like(query))
    narrow_ref[:, 2 * BLK :] = pack_kv(columns(1)[:, :HW], columns(2)[:, :HW])

    def line(i):
        return lines[i][...].astype(f32).reshape(1, -1)

    zero = jnp.zeros((1, half), f32)
    small_ref[...] = jnp.zeros_like(small_ref)
    for row in range(6):
        small_ref[row : row + 1] = jnp.where(
            x == 0, jnp.concatenate([line(row), zero], axis=1), jnp.concatenate([zero, line(row)], axis=1)
        )
    ups = line(8)
    for i in range(2):
        small_ref[pl.ds(8 + 2 * x + i, 1)] = ups[:, 2 * half * i : 2 * half * i + 2 * half]

    def part(i):
        mine = jnp.where(odd, line(i)[:, HW:], line(i)[:, :HW])
        return jnp.where(g // 2 == x, mine, jnp.zeros_like(mine))

    value = part(7)
    small_ref[12:13] = jnp.concatenate(
        [part(6), jnp.zeros((1, 2 * BLK), f32), value[:, 2 * DH :], value[:, : 2 * DH], jnp.zeros((1, BLK), f32)], axis=1
    )


def gather_kernel(
    tokens_ref, query_any, key_any, value_any, wo_ref, l0, l1, l2, l3, l4, l5, l6, l7, l8,
    kv_ref, q_ref, normed_ref, small_out, wfull, wo_out,
    lined, attn_w, narrow_ref, small_ref, small_in, kvs,
    z_own, z_send, z_recv, s_sem, n_send, n_recv, kv_send, kv_recv, kv_local, w_send, w_recv, w_local, a_sem,
):
    g, r, core, x = place()
    other = 1 - x
    rows, width = tokens_ref.shape
    half = width // 2
    fourth = half // 2
    eighth = half // 4
    loads = [
        pltpu.make_async_copy(ref, attn_w.at[i], a_sem.at[i]) for i, ref in enumerate((query_any, key_any, value_any))
    ]
    for load in loads:
        load.start()
    greet(g, r, core, x, False)

    def half_of(source, part):
        return lined.at[source, pl.ds(BLK * part, BLK)]

    def along(source, part, away, sem):
        return send(half_of(source, part), half_of(source, part), sem, z_recv.at[source, part], g=g + away)

    lined[g] = tokens_ref[...]
    for part in range(2):
        pl.when(g > 0)(lambda: along(g, part, -1, z_own.at[0, part]).start())
        pl.when(g < GROUPS - 1)(lambda: along(g, part, 1, z_own.at[1, part]).start())

    for load in loads:
        load.wait()
    prepare(g, x, attn_w, (l0, l1, l2, l3, l4, l5, l6, l7, l8), narrow_ref, small_ref)
    small_move = send(small_ref, small_in, s_sem.at[0], s_sem.at[1], x=other)
    small_move.start()
    mine = pl.ds(x * half + core * fourth, fourth)
    narrow_x = send(narrow_ref.at[pl.ds(core * fourth, fourth)], wfull.at[mine], n_send.at[0], n_recv.at[0], x=other)
    narrow_x.start()

    def wo_rows(owner, part):
        return wo_out.at[pl.ds(owner * half + core * fourth + part * eighth, eighth)]

    wo_x = send(wo_ref.at[pl.ds(core * fourth + r * eighth, eighth)], wo_rows(x, r), w_send.at[0], w_recv.at[0], x=other)
    wo_y = send(wo_rows(other, r), wo_rows(other, r), w_send.at[3], w_recv.at[3], r=1 - r)
    wo_s = [
        send(wo_rows(other, part), wo_rows(other, part), w_send.at[6 + i], w_recv.at[6 + i], core=1 - core)
        for i, part in enumerate((r, 1 - r))
    ]
    wo_x.start()
    locals_ = [pltpu.make_async_copy(wo_ref, wo_out.at[pl.ds(x * half, half)], w_local.at[0])]
    for item in locals_:
        item.start()

    wfull[pl.ds(x * half, half)] = narrow_ref[...]
    narrow_x.wait_recv()
    theirs = wfull.at[pl.ds(other * half + core * fourth, fourth)]
    narrow_s = send(theirs, theirs, n_send.at[1], n_recv.at[1], core=1 - core)
    narrow_s.start()
    small_move.wait_recv()
    small_out[...] = small_ref[...] + small_in[...]
    narrow_s.wait_recv()

    own = seat(r, core, x)

    def span(step):
        return (step, 0, rows) if step < GROUPS - 1 else (GROUPS - 1, BLK * (step - GROUPS + 1), BLK)

    def block(owner, step):
        nth, low, count = span(step)
        return kv_ref.at[owner, nearest(g, nth), pl.ds(low, count)]

    def made(step):
        nth, low, count = span(step)
        return kvs.at[nth, pl.ds(low, count)]

    def push(step, kind, src, dst, **device):
        send(src, dst, kv_send.at[kind, step], kv_recv.at[kind, step], **device).start()

    def settle(step, kind, owner):
        arrived(block(owner, step), kv_send.at[kind, step], kv_recv.at[kind, step], x)

    def forward(step):
        by_x = block(seat(r, core, other), step)
        settle(step, 0, seat(r, core, other))
        if step % 2 == 0:
            push(step, 3, by_x, by_x, r=1 - r)
        push(step, 4, by_x, by_x, core=1 - core)
        by_y = block(seat(1 - r, core, x), step)
        settle(step, 1, seat(1 - r, core, x))
        if step % 2 == 1:
            push(step, 3, by_y, by_y, x=other)
        push(step, 5, by_y, by_y, core=1 - core)

    def forward_far(step):
        far = block(seat(1 - r, core, other), step)
        settle(step, 3, seat(1 - r, core, other))
        push(step, 6, far, far, core=1 - core)

    def take(nth, part):
        source = nearest(g, nth)
        arrived(half_of(source, part), z_send.at[source, part], z_recv.at[source, part], x)
        pl.when((source < g) & (g < GROUPS - 1))(lambda: along(source, part, 1, z_send.at[source, part]).start())
        pl.when((source > g) & (g > 0))(lambda: along(source, part, -1, z_send.at[source, part]).start())

    def project(step):
        nth, low, count = span(step)
        source = nearest(g, nth)
        taken = pl.ds(low, count)
        values = lined[source, taken].astype(f32)
        normed = layer_norm(values, small_out[0:1], small_out[1:2]).astype(bf16)
        normed_ref[source, taken] = normed
        both = dot(normed, wfull[...]) + small_out[12:13, : wfull.shape[1]]
        kvs[nth, taken] = both[:, 2 * BLK :].astype(bf16)
        push(step, 0, made(step), block(own, step), x=other)
        push(step, 1, made(step), block(own, step), r=1 - r)
        push(step, 2, made(step), block(own, step), core=1 - core)
        q_ref[source, taken] = (both[:, : 2 * BLK] * SCALE).astype(bf16)
        pltpu.make_async_copy(made(step), block(own, step), kv_local.at[step]).start()

    at_end = (g == 0) | (g == GROUPS - 1)
    between = jnp.logical_not(at_end)
    project(0)
    take(1, 0)
    take(1, 1)

    @pl.when(between)
    def _():
        take(2, 0)
        take(2, 1)

    project(1)
    forward(0)

    @pl.when(at_end)
    def _():
        take(2, 0)
        take(2, 1)

    project(2)

    @pl.when(at_end)
    def _():
        forward(1)
        forward_far(0)

    take(3, 0)
    pl.when(between)(lambda: take(3, 1))
    project(3)
    pl.when(at_end)(lambda: take(3, 1))
    project(4)

    @pl.when(between)
    def _():
        forward(1)
        forward_far(0)

    wo_x.wait_recv()
    wo_y.start()
    wo_s[0].start()
    forward(2)
    forward_far(1)
    forward(3)
    forward_far(2)
    forward(4)
    forward_far(3)
    arrived(wo_rows(other, 1 - r), w_send.at[3], w_recv.at[3], x)
    wo_s[1].start()
    forward_far(4)

    for step in range(GROUPS + 1):
        pltpu.make_async_copy(made(step), block(own, step), kv_local.at[step]).wait()
        settle(step, 2, seat(r, 1 - core, x))
        settle(step, 4, seat(r, 1 - core, other))
        settle(step, 5, seat(1 - r, 1 - core, x))
        settle(step, 6, seat(1 - r, 1 - core, other))
        for kind in range(7):
            left(made(step), kv_send.at[kind, step], kv_recv.at[kind, step], x)
    for part in range(2):
        pl.when(g > 0)(lambda: left(half_of(g, part), z_own.at[0, part], z_recv.at[g, part], x))
        pl.when(g < GROUPS - 1)(lambda: left(half_of(g, part), z_own.at[1, part], z_recv.at[g, part], x))
        for nth in range(1, GROUPS):
            source = nearest(g, nth)
            passed = ((source < g) & (g < GROUPS - 1)) | ((source > g) & (g > 0))
            pl.when(passed)(
                lambda: left(half_of(source, part), z_send.at[source, part], z_recv.at[source, part], x)
            )
    small_move.wait_send()
    narrow_x.wait_send()
    narrow_s.wait_send()
    for item in locals_:
        item.wait()
    for item in (wo_x, wo_y, *wo_s):
        item.wait_send()
    for i, part in enumerate((r, 1 - r)):
        there = wo_out.at[pl.ds(other * half + (1 - core) * fourth + part * eighth, eighth)]
        send(there, there, w_send.at[6 + i], w_recv.at[6 + i], core=1 - core).wait_recv()


def anywhere():
    return pl.BlockSpec(memory_space=pl.ANY)


def in_hbm():
    return pl.BlockSpec(memory_space=pltpu.HBM)


def gather(tokens, query, key, value, wo, *lines):
    rows, width = tokens.shape
    wide = 2 * BLK + 2 * HW
    small = (16, width)
    dma = pltpu.SemaphoreType.DMA
    return pl.pallas_call(
        gather_kernel,
        out_shape=(
            jax.ShapeDtypeStruct((8, GROUPS, rows, 2 * HW), bf16),
            jax.ShapeDtypeStruct((GROUPS, rows, 2 * BLK), bf16),
            jax.ShapeDtypeStruct((GROUPS, rows, width), bf16),
            jax.ShapeDtypeStruct(small, f32),
            jax.ShapeDtypeStruct((width, wide), bf16),
            jax.ShapeDtypeStruct((width, width), bf16),
        ),
        in_specs=[whole_vmem(), *[in_hbm()] * 4, *[whole_vmem()] * len(lines)],
        out_specs=(anywhere(), *(whole_vmem(),) * 5),
        scratch_shapes=[
            pltpu.VMEM((GROUPS, rows, width), bf16),
            pltpu.VMEM((3, width // 2, width), bf16),
            pltpu.VMEM((width // 2, wide), bf16),
            pltpu.VMEM(small, f32),
            pltpu.VMEM(small, f32),
            pltpu.VMEM((GROUPS, rows, 2 * HW), bf16),
            dma((2, 2)), dma((GROUPS, 2)), dma((GROUPS, 2)), dma((2,)), dma((2,)), dma((2,)),
            dma((7, GROUPS + 1)), dma((7, GROUPS + 1)), dma((GROUPS + 1,)), dma((8,)), dma((8,)), dma((2,)), dma((3,)),
        ],
        compiler_params=pltpu.CompilerParams(
            collective_id=0, has_side_effects=True, vmem_limit_bytes=60 << 20
        ),
        name="gather",
    )(tokens, query, key, value, wo, *lines)


def erf_parts(values):
    below = 0.5 * (1.0 + lax.erf(values * ROOT_HALF))
    return below, PDF_SCALE * jnp.exp(-0.5 * values * values)


PARTS = 8
UNIT = 216
KEPT = 168


def dense_kernel(
    out_t_ref, tokens_ref, cot_ref, cot_x_ref, small_ref, wo_ref, up_mine, up_other, down_any,
    base_ref, x_give_ref, middle_grad_ref, grad_t_ref, keep_ref, give_ref, far_ref, sums_ref,
    down_ref, up_ref, attn_in, attn_t, cots, h2s, mid_ref, n2_ref, scales, part_y, part_d, in_y, in_d, pass_y, pass_d,
    x_y, x_d, hids, dus, branch_ref, grad_out, wo_keep, wo_give, wo_in, wo_pass, wo_x,
    l_sem, a_send, a_recv, c_send, c_recv, h_send, h_recv, y_send, y_recv, d_send, d_recv, o_send, o_recv,
    w_send, w_recv,
):
    g, r, core, x = place()
    other, sib = 1 - x, 1 - core
    rows, width = tokens_ref.shape
    half = width // 2
    fourth = half // 2
    loads = [
        pltpu.make_async_copy(
            down_any.at[pl.ds(pl.multiple_of(core * width, width), width)], down_ref, l_sem.at[0]
        ),
        pltpu.make_async_copy(up_mine, up_ref.at[pl.ds(x * half, half)], l_sem.at[1]),
        pltpu.make_async_copy(up_other, up_ref.at[pl.ds(other * half, half)], l_sem.at[2]),
    ]
    for load in loads:
        load.start()
    greet(g, r, core, x, True)
    pending = []

    def begin(src, dst, out_sem, in_sem, **device):
        move = send(src, dst, out_sem, in_sem, **device)
        move.start()
        pending.append(move)
        return move

    def other_group(away):
        return lax.rem(g + away, GROUPS)

    def rows_of(b):
        return pl.ds(BLK * b, BLK)

    for b in range(2):
        for away in range(1, GROUPS):
            to = other_group(away)
            begin(out_t_ref.at[2 * to + b], attn_in.at[g, b], a_send.at[b, away], a_recv.at[b, g], g=to)
        attn_in[g, b] = out_t_ref[2 * g + b]
        cots[b, 0] = cot_ref[rows_of(b)]
        cots[b, 2] = cot_x_ref[rows_of(b)]
    cot_moves = [
        begin(cots.at[:, 2 * i], cots.at[:, 2 * i + 1], c_send.at[i], c_recv.at[i], core=sib) for i in range(2)
    ]
    sums_ref[...] = jnp.zeros_like(sums_ref)
    sums_ref[5:6] = jnp.sum(cot_ref[...].astype(f32), axis=0, keepdims=True)
    h2_moves = []

    def norm(b):
        for away in range(1, GROUPS):
            source = other_group(away)
            arrived(attn_in.at[source, b], a_send.at[b, away], a_recv.at[b, source], x)
        for source in range(GROUPS):
            attn_t[HW * source : HW * source + HW, BLK * b : BLK * b + BLK] = attn_in[source, b]
        middle = (
            tokens_ref[rows_of(b)].astype(f32)
            + outer(attn_t[:, BLK * b : BLK * b + BLK], wo_ref[...])
            + small_ref[2:3]
        )
        mid_ref[b] = middle
        mean = jnp.mean(middle, axis=-1, keepdims=True)
        centred = middle - mean
        scale = lax.rsqrt(jnp.mean(centred * centred, axis=-1, keepdims=True) + EPS)
        scales[b] = scale
        n2_ref[b] = centred * scale
        h2s[b, 0] = (n2_ref[b] * small_ref[3:4] + small_ref[4:5]).astype(bf16)
        h2_moves.append(
            (
                begin(h2s.at[b, 0], h2s.at[b, 2], h_send.at[b, 1], h_recv.at[b, 1], x=other),
                begin(h2s.at[b, 0], h2s.at[b, 1], h_send.at[b, 0], h_recv.at[b, 0], core=sib),
            )
        )

    def pass_on(b):
        h2_moves[b][0].wait_recv()
        return begin(h2s.at[b, 2], h2s.at[b, 3], h_send.at[b, 2], h_recv.at[b, 2], core=sib)

    bias_row = 8 + 2 * x + core

    def pair_of(ref, b, pair):
        return ref[b, 2 * pair : 2 * pair + 2].reshape(2 * BLK, width)

    def forward_backward(b, pair):
        cot = pair_of(cots, b, pair)
        expanded = dot(pair_of(h2s, b, pair), up_ref[...]) + small_ref[pl.ds(bias_row, 1)]
        below, density = erf_parts(expanded)
        hidden = (expanded * below).astype(bf16)
        hids[b, pair] = hidden
        slope = below + expanded * density
        grad_hidden = inner(cot, down_ref[...]).astype(bf16).astype(f32)
        grad_expand = (grad_hidden * slope).astype(bf16)
        dus[b, pair] = grad_expand
        part_d[b, pair] = inner(grad_expand, up_ref[...])
        part_y[b, pair] = dot(hidden, down_ref[...])
        sums_ref[pl.ds(bias_row, 1)] += jnp.sum(grad_expand.astype(f32), axis=0, keepdims=True)

    d_moves, y_passes = [None, None], [None, None]

    def near_pair(b):
        if b == 0:
            cot_moves[0].wait_recv()
        h2_moves[b][1].wait_recv()
        forward_backward(b, 0)
        return begin(part_d.at[b, 0, pl.ds(BLK, BLK)], in_d.at[b], d_send.at[b, 0], d_recv.at[b, 0], core=sib)

    def far_pair(b, passed):
        if b == 0:
            cot_moves[1].wait_recv()
        passed.wait_recv()
        forward_backward(b, 1)
        x_d[b, 0] = part_d[b, 1, BLK:].astype(bf16)
        across = begin(x_d.at[b, 0], pass_d.at[b], d_send.at[b, 1], d_recv.at[b, 1], core=sib)
        x_y[b] = part_y[b, 1, BLK:].astype(bf16)
        y_passes[b] = begin(x_y.at[b], pass_y.at[b], y_send.at[b, 1], y_recv.at[b, 1], core=sib)
        across.wait_recv()
        x_d[b, 1] = (part_d[b, 1, :BLK] + pass_d[b].astype(f32)).astype(bf16)
        return begin(x_d.at[b, 1], x_d.at[b, 2], d_send.at[b, 2], d_recv.at[b, 2], x=other)

    def back(b, near, far):
        near.wait_recv()
        far.wait_recv()
        grad_second = part_d[b, 0, :BLK] + in_d[b] + x_d[b, 2].astype(f32)
        n2 = n2_ref[b]
        sums_ref[3:4] += jnp.sum(grad_second * n2, axis=0, keepdims=True)
        sums_ref[4:5] += jnp.sum(grad_second, axis=0, keepdims=True)
        pulled = grad_second * small_ref[3:4]
        inward = (
            pulled - jnp.mean(pulled, axis=-1, keepdims=True) - n2 * jnp.mean(pulled * n2, axis=-1, keepdims=True)
        )
        grad_middle = cot_ref[rows_of(b)].astype(f32) + inward * scales[b]
        middle_grad_ref[rows_of(b)] = grad_middle
        branch = grad_middle.astype(bf16)
        branch_ref[rows_of(b)] = branch
        sums_ref[2:3] += jnp.sum(branch.astype(f32), axis=0, keepdims=True)
        grad_out_t = inner(wo_ref[...], branch).astype(bf16)
        for group in range(GROUPS):
            grad_out[group, b] = grad_out_t[HW * group : HW * group + HW]
        for away in range(1, GROUPS):
            to = other_group(away)
            begin(grad_out.at[to, b], grad_t_ref.at[2 * g + b], o_send.at[b, away], o_recv.at[b, g], g=to)
        grad_t_ref[2 * g + b] = grad_out[g, b]

    norm(0)
    norm(1)
    for load in loads:
        load.wait()
    near = [near_pair(0), None]
    passed = [pass_on(0), None]
    near[1] = near_pair(1)
    far = [far_pair(0, passed[0]), None]
    passed[1] = pass_on(1)
    far[1] = far_pair(1, passed[1])

    def over_rows(left, right):
        total = None
        for b in range(2):
            for pair in range(2):
                term = outer(left(b, pair), right(b, pair))
                total = term if total is None else total + term
        return total.astype(bf16)

    def parts(write):
        for y in range(2):
            pl.when(r == y)(lambda: write(keep_ref, y))
            pl.when(r != y)(lambda: write(give_ref, y))

    down_grad = over_rows(lambda b, pair: hids[b, pair], lambda b, pair: pair_of(cots, b, pair))

    def write_down(ref, y):
        for z in range(GROUPS):
            p = y * GROUPS + z
            ref[z, 0:96] = down_grad[96 * p : 96 * p + 96]

    parts(write_down)
    back(0, near[0], far[0])
    up_grad = over_rows(lambda b, pair: pair_of(h2s, b, pair), lambda b, pair: dus[b, pair])

    def up_part(p, h):
        return up_grad[half * h + 48 * p : half * h + 48 * p + 48]

    def write_up(y, h):
        @pl.when((r == y) & (x == h))
        def _():
            for z in range(GROUPS):
                keep_ref[z, 96:144] = up_part(y * GROUPS + z, h)

        @pl.when((r != y) & (x == h))
        def _():
            for z in range(GROUPS):
                give_ref[z, 96:144] = up_part(y * GROUPS + z, h)

        @pl.when((r == y) & (x != h))
        def _():
            for z in range(GROUPS):
                x_give_ref[rows + 48 * z : rows + 48 * z + 48] = up_part(y * GROUPS + z, h)

        @pl.when((r != y) & (x != h))
        def _():
            for z in range(GROUPS):
                far_ref[z] = up_part(y * GROUPS + z, h)

    for y in range(2):
        for h in range(2):
            write_up(y, h)
    back(1, near[1], far[1])

    for owner in range(2):
        for c in range(2):
            piece = dot(attn_t[half * owner + fourth * c : half * owner + fourth * c + fourth], branch_ref[...])

            @pl.when(core == c)
            def _():
                wo_keep[owner] = piece

            @pl.when(core != c)
            def _():
                wo_give[owner] = piece.astype(bf16)

    w_sib = begin(wo_give, wo_in, w_send.at[0], w_recv.at[0], core=sib)
    y_sibs = [
        begin(part_y.at[b, 0, pl.ds(BLK, BLK)], in_y.at[b], y_send.at[b, 0], y_recv.at[b, 0], core=sib)
        for b in range(2)
    ]
    w_sib.wait_recv()
    wo_pass[...] = (wo_keep[other] + wo_in[other].astype(f32)).astype(bf16)
    w_x = begin(wo_pass, wo_x, w_send.at[1], w_recv.at[1], x=other)
    for b in range(2):
        y_passes[b].wait_recv()
        x_give_ref[rows_of(b)] = (part_y[b, 1, :BLK] + pass_y[b].astype(f32)).astype(bf16)
        y_sibs[b].wait_recv()
        base_ref[rows_of(b)] = mid_ref[b] + part_y[b, 0, :BLK] + in_y[b] + small_ref[5:6]
    mine = wo_keep[x] + wo_in[x].astype(f32)
    for b in range(2):
        for away in range(1, GROUPS):
            source = other_group(away)
            arrived(grad_t_ref.at[2 * source + b], o_send.at[b, away], o_recv.at[b, source], x)
    w_x.wait_recv()
    wo_sum = (mine + wo_x[...].astype(f32)).astype(bf16)

    def write_wo(ref, y):
        for z in range(GROUPS):
            p = y * GROUPS + z
            ref[z, 144:KEPT] = wo_sum[24 * p : 24 * p + 24]

    parts(write_wo)
    for move in pending:
        move.wait_send()


def dense(out_t, tokens, cot, cot_x, small, wo, up_mine, up_other, down):
    rows, width = tokens.shape
    dma = pltpu.SemaphoreType.DMA
    full = (rows, width)
    part = (BLK, width)
    pair = (2 * BLK, width)
    fourth = (width // 4, width)
    return pl.pallas_call(
        dense_kernel,
        out_shape=(
            jax.ShapeDtypeStruct(full, f32),
            jax.ShapeDtypeStruct((rows + 48 * GROUPS, width), bf16),
            jax.ShapeDtypeStruct(full, f32),
            jax.ShapeDtypeStruct(out_t.shape, bf16),
            jax.ShapeDtypeStruct((GROUPS, KEPT, width), bf16),
            jax.ShapeDtypeStruct((GROUPS, KEPT, width), bf16),
            jax.ShapeDtypeStruct((GROUPS, 48, width), bf16),
            jax.ShapeDtypeStruct(small.shape, f32),
        ),
        in_specs=[whole_vmem()] * 6 + [anywhere()] * 3,
        out_specs=(whole_vmem(),) * 8,
        scratch_shapes=[
            pltpu.VMEM((width, width), bf16),
            pltpu.VMEM((width, width), bf16),
            pltpu.VMEM((GROUPS, 2, HW, BLK), bf16),
            pltpu.VMEM((width, rows), bf16),
            pltpu.VMEM((2, 4, *part), bf16),
            pltpu.VMEM((2, 4, *part), bf16),
            pltpu.VMEM((2, *part), f32),
            pltpu.VMEM((2, *part), f32),
            pltpu.VMEM((2, BLK, 1), f32),
            pltpu.VMEM((2, 2, *pair), f32),
            pltpu.VMEM((2, 2, *pair), f32),
            pltpu.VMEM((2, *part), f32),
            pltpu.VMEM((2, *part), f32),
            pltpu.VMEM((2, *part), bf16),
            pltpu.VMEM((2, *part), bf16),
            pltpu.VMEM((2, *part), bf16),
            pltpu.VMEM((2, 3, *part), bf16),
            pltpu.VMEM((2, 2, *pair), bf16),
            pltpu.VMEM((2, 2, *pair), bf16),
            pltpu.VMEM(full, bf16),
            pltpu.VMEM((GROUPS, 2, HW, BLK), bf16),
            pltpu.VMEM((2, *fourth), f32),
            pltpu.VMEM((2, *fourth), bf16),
            pltpu.VMEM((2, *fourth), bf16),
            pltpu.VMEM(fourth, bf16),
            pltpu.VMEM(fourth, bf16),
            dma((3,)), dma((2, GROUPS)), dma((2, GROUPS)), dma((2,)), dma((2,)), dma((2, 3)), dma((2, 3)),
            dma((2, 2)), dma((2, 2)), dma((2, 3)), dma((2, 3)), dma((2, GROUPS)), dma((2, GROUPS)), dma((2,)), dma((2,)),
        ],
        compiler_params=pltpu.CompilerParams(
            collective_id=1, has_side_effects=True, vmem_limit_bytes=40 << 20
        ),
        name="dense",
    )(out_t, tokens, cot, cot_x, small, wo, up_mine, up_other, down)


FARTHEST = ((3, 2, 1, 0), (3, 0, 2, 1), (0, 3, 1, 2), (0, 1, 2, 3))


def farthest(g, step):
    picked = FARTHEST[0][step]
    for z in range(1, GROUPS):
        picked = jnp.where(g == z, FARTHEST[z][step], picked)
    return picked


class Chain:
    def __init__(self, g, x, total, parts, inward, outward, out_sem, in_sem):
        self.g, self.x, self.total, self.parts = g, x, total, parts
        self.inward, self.outward, self.out_sem, self.in_sem = inward, outward, out_sem, in_sem

    def move(self, to, way):
        return send(
            self.outward.at[to], self.inward.at[way, to], self.out_sem.at[to], self.in_sem.at[way, to],
            g=jnp.clip(self.g + (1 if way == 0 else -1), 0, GROUPS - 1),
        )

    def step(self, to):
        g = self.g
        self.total[...] = self.parts[to].astype(f32)

        def take(way):
            arrived(self.inward.at[way, to], self.out_sem.at[to], self.in_sem.at[way, to], self.x)
            self.total[...] += self.inward[way, to].astype(f32)

        pl.when((to >= g) & (g > 0))(lambda: take(0))
        pl.when((to <= g) & (g < GROUPS - 1))(lambda: take(1))

        @pl.when(to != g)
        def _():
            self.outward[to] = self.total[...].astype(bf16)

        pl.when(to > g)(lambda: self.move(to, 0).start())
        pl.when(to < g)(lambda: self.move(to, 1).start())

    def finish(self):
        for step in range(GROUPS - 1):
            to = farthest(self.g, step)
            left(self.outward.at[to], self.out_sem.at[to], self.in_sem.at[0, to], self.x)


class Ring:
    def __init__(self, g, x, slot, own_sem, out_sem, in_sem):
        self.g, self.x, self.slot = g, x, slot
        self.own_sem, self.out_sem, self.in_sem = own_sem, out_sem, in_sem

    def move(self, source, way, sem):
        return send(
            self.slot(source), self.slot(source), sem, self.in_sem.at[source],
            g=jnp.clip(self.g + way, 0, GROUPS - 1),
        )

    def start(self):
        g = self.g
        pl.when(g > 0)(lambda: self.move(g, -1, self.own_sem.at[0]).start())
        pl.when(g < GROUPS - 1)(lambda: self.move(g, 1, self.own_sem.at[1]).start())

    def step(self, step):
        g, source = self.g, nearest(self.g, step)
        arrived(self.slot(source), self.out_sem.at[source], self.in_sem.at[source], self.x)
        pl.when((source < g) & (g < GROUPS - 1))(lambda: self.move(source, 1, self.out_sem.at[source]).start())
        pl.when((source > g) & (g > 0))(lambda: self.move(source, -1, self.out_sem.at[source]).start())
        return source

    def finish(self):
        g = self.g
        for i, there in enumerate((g > 0, g < GROUPS - 1)):
            pl.when(there)(lambda: left(self.slot(g), self.own_sem.at[i], self.in_sem.at[g], self.x))
        for step in range(1, GROUPS):
            source = nearest(g, step)
            passed = ((source < g) & (g < GROUPS - 1)) | ((source > g) & (g > 0))
            pl.when(passed)(
                lambda: left(self.slot(source), self.out_sem.at[source], self.in_sem.at[source], self.x)
            )


def arrived(what, out_sem, in_sem, x):
    send(what, what, out_sem, in_sem, x=1 - x).wait_recv()


def left(what, out_sem, in_sem, x):
    send(what, what, out_sem, in_sem, x=1 - x).wait_send()


def scatter_kernel(
    dkv_ref, dq_any, normed_any, wfull_any, tokens_any, mgrad_any, keep_any, over_any, near_any, far_any, small_ref, sums_in,
    tokens_grad_ref, big_ref, qout_ref, kvout_ref, sums_ref,
    dq_ref, normed_ref, wfull_ref, tokens_ref, mgrad_ref, kept, over, near, far,
    own_kv, sib_kv, keep_x, give_x, in_x, give_y, in_y, part_a, total_a, inward_a, outward_a, wg_kv,
    by_sum, total_b, inward_b, outward_b, unit,
    q_keep, q_give, q_in, q_pass, q_x, q_y, q_sum, v_keep, v_give, v_in, v_pass, v_x, v_y, v_sum,
    sums_got, late, late_sum, late_got,
    load_sem, own_sem, k_send, k_recv, x_send, x_recv, y_send, y_recv, ca_send, ca_recv,
    cb_send, cb_recv, rb_own, rb_send, rb_recv,
    fy_send, fy_recv, fs_send, fs_recv,
    q_send, q_recv, rq_own, rq_send, rq_recv, qs_send, qs_recv,
    v_send, v_recv, rv_own, rv_send, rv_recv, vs_send, vs_recv,
    s_send, s_recv, t_send, t_recv, l_sem,
):
    g, r, core, x = place()
    other, sib, far_r = 1 - x, 1 - core, 1 - r
    rows, width = tokens_ref.shape
    half = width // 2
    fourth = half // 2
    wide_q = 2 * BLK
    loads = [
        pltpu.make_async_copy(what, where, load_sem.at[i])
        for i, (what, where) in enumerate(
            (
                (keep_any, kept), (over_any, over), (near_any.at[pl.ds(rows, 48 * GROUPS)], near), (far_any, far),
                (dq_any, dq_ref), (normed_any, normed_ref), (wfull_any, wfull_ref), (tokens_any, tokens_ref),
                (mgrad_any, mgrad_ref),
            )
        )
    ]
    for load in loads:
        load.start()
    greet(g, r, core, x, True, True)
    pending = []

    def begin(src, dst, out_sem, in_sem, **device):
        move = send(src, dst, out_sem, in_sem, **device)
        move.start()
        pending.append(move)
        return move

    def settled(move):
        move.wait_recv()
        move.wait_send()
        pending[:] = [item for item in pending if item is not move]

    kv_moves = []
    for i in range(GROUPS):
        c = farthest(g, i)
        for spot in range(4):
            own = pltpu.make_async_copy(
                dkv_ref.at[seat(spot // 2, core, spot % 2), c], own_kv.at[i, spot], own_sem.at[i, spot]
            )
            own.start()
            across = begin(
                dkv_ref.at[seat(spot // 2, sib, spot % 2), c], sib_kv.at[i, spot],
                k_send.at[i, spot], k_recv.at[i, spot], core=sib,
            )
            kv_moves.append((own, across))

    def split(total, keep, give):
        for owner in range(2):
            for c in range(2):
                low = half * owner + fourth * c
                chunk = total[low : low + fourth]

                @pl.when(core == c)
                def _():
                    keep[owner] = chunk

                @pl.when(core != c)
                def _():
                    give[owner] = chunk.astype(bf16)

    def scaled(c):
        return dq_ref[c] * bf16(SCALE)

    q_move = send(q_give, q_in, q_send.at[0], q_recv.at[0], core=sib)

    def query_grad():
        loads[4].wait()
        loads[5].wait()
        query_total = outer(normed_ref[0], scaled(0))
        for c in range(1, GROUPS):
            query_total += outer(normed_ref[c], scaled(c))
        split(query_total, q_keep, q_give)
        q_move.start()
        line_q = scaled(0).astype(f32)
        for c in range(1, GROUPS):
            line_q += scaled(c).astype(f32)
        sums_ref[pl.ds(16 + g, 1), 0:wide_q] = jnp.sum(line_q, axis=0, keepdims=True)

    sums_ref[...] = jnp.zeros_like(sums_ref)
    sums_ref[0:16] = sums_in[...]
    wg_kv[...] = jnp.zeros_like(wg_kv)

    def q_slot(z):
        return qout_ref.at[core, z]

    def v_slot(z):
        return kvout_ref.at[core, z]

    def b_slot(z):
        return big_ref.at[core, r, z]

    ring_q = Ring(g, x, q_slot, rq_own, rq_send, rq_recv)
    ring_v = Ring(g, x, v_slot, rv_own, rv_send, rv_recv)
    ring_b = Ring(g, x, b_slot, rb_own, rb_send, rb_recv)

    def store(value_ref, slot, sem):
        copy = pltpu.make_async_copy(value_ref, slot, sem)
        copy.start()
        copy.wait()

    def spread_b(z, step):
        begin(b_slot(z), b_slot(z), fy_send.at[step], fy_recv.at[step], r=far_r)
        begin(b_slot(z), b_slot(z), fs_send.at[0, step], fs_recv.at[0, step], core=sib)

    def spread_far(step):
        what = big_ref.at[core, far_r, nearest(g, step)]
        arrived(what, fy_send.at[step], fy_recv.at[step], x)
        begin(what, what, fs_send.at[1, step], fs_recv.at[1, step], core=sib)

    def on_ring_b(step):
        spread_b(ring_b.step(step), step)

    def on_ring_q(step):
        z = ring_q.step(step)
        begin(q_slot(z), q_slot(z), qs_send.at[step], qs_recv.at[step], core=sib)

    def on_ring_v(step):
        z = ring_v.step(step)
        begin(v_slot(z), v_slot(z), vs_send.at[step], vs_recv.at[step], core=sib)

    chain_a = Chain(g, x, total_a, part_a, inward_a, outward_a, ca_send, ca_recv)
    chain_b = Chain(g, x, total_b, by_sum, inward_b, outward_b, cb_send, cb_recv)
    at_end = (g == 0) | (g == GROUPS - 1)
    between = jnp.logical_not(at_end)

    def steps(chain, *which):
        for i in which:
            chain.step(farthest(g, i))

    def on_sibling(i):
        for own, across in kv_moves[4 * i : 4 * i + 4]:
            own.wait()
            across.wait_recv()

        def total(row, column):
            spot = 2 * row + column
            return own_kv[i, spot].astype(f32) + sib_kv[i, spot].astype(f32)

        for k in range(2):
            give_x[i, k] = (total(k, other) if i % 2 == 0 else total(far_r, k)).astype(bf16)
            keep_x[i, k] = total(k, x) if i % 2 == 0 else total(r, k)

    def go_first(i):
        along = {"x": other} if i % 2 == 0 else {"r": far_r}
        begin(give_x.at[i], in_x.at[i], x_send.at[i], x_recv.at[i], **along)

    def on_first(i):
        arrived(in_x.at[i], x_send.at[i], x_recv.at[i], x)
        away, stay, along = (far_r, r, {"r": far_r}) if i % 2 == 0 else (other, x, {"x": other})
        give_y[i] = (keep_x[i, away] + in_x[i, away].astype(f32)).astype(bf16)
        begin(give_y.at[i], in_y.at[i], y_send.at[i], y_recv.at[i], **along)
        keep_x[i, stay] += in_x[i, stay].astype(f32)

    def on_second(i):
        c = farthest(g, i)
        arrived(in_y.at[i], y_send.at[i], y_recv.at[i], x)
        both = (keep_x[i, r if i % 2 == 0 else x] + in_y[i].astype(f32)).astype(bf16)
        part_a[c] = inner(scaled(c), wfull_ref[:, :wide_q]) + inner(both, wfull_ref[:, wide_q:])
        wg_kv[...] += outer(normed_ref[c], both)
        sums_ref[pl.ds(16 + g, 1), wide_q : wide_q + 2 * HW] += jnp.sum(both.astype(f32), axis=0, keepdims=True)

    for load in loads[:4]:
        load.wait()
    own_up = pl.ds(pl.multiple_of(96 + 48 * x, 48), 48)
    their_up = pl.ds(pl.multiple_of(96 + 48 * other, 48), 48)
    for z in range(GROUPS):
        pair = kept[z].astype(f32) + over[z].astype(f32)
        by_sum[z, 0:96] = pair[0:96]
        by_sum[z, own_up] = pair[96:144]
        by_sum[z, 192:UNIT] = pair[144:KEPT]
        by_sum[z, their_up] = near[48 * z : 48 * z + 48].astype(f32) + far[z].astype(f32)
    pl.when(at_end)(lambda: steps(chain_b, 0, 1, 2))
    on_sibling(0)
    go_first(0)
    on_sibling(1)
    go_first(1)
    on_sibling(2)
    on_sibling(3)
    pl.when(between)(lambda: steps(chain_b, 0))
    query_grad()
    on_first(0)
    on_first(1)
    go_first(2)
    go_first(3)
    pl.when(between)(lambda: steps(chain_b, 1, 2))
    settled(q_move)
    q_pass[...] = (q_keep[other] + q_in[other].astype(f32)).astype(bf16)
    q_across = begin(q_pass, q_x, q_send.at[1], q_recv.at[1], x=other)
    loads[6].wait()
    on_second(0)
    on_second(1)
    pl.when(at_end)(lambda: steps(chain_a, 0))
    chain_b.step(g)
    unit[...] = total_b[...].astype(bf16)
    store(unit, b_slot(g), l_sem.at[0])
    ring_b.start()
    spread_b(g, 0)
    pl.when(at_end)(lambda: steps(chain_a, 1))
    on_first(2)
    on_first(3)
    q_across.wait_recv()
    q_sum[...] = (q_keep[x] + q_in[x].astype(f32) + q_x[...].astype(f32)).astype(bf16)
    q_over = begin(q_sum, q_y, q_send.at[2], q_recv.at[2], r=far_r)
    pl.when(between)(lambda: steps(chain_a, 0))
    on_second(2)
    on_second(3)
    pl.when(at_end)(lambda: steps(chain_a, 2))
    split(wg_kv, v_keep, v_give)
    v_move = begin(v_give, v_in, v_send.at[0], v_recv.at[0], core=sib)
    s_sib = begin(sums_ref, sums_got.at[0], s_send.at[0], s_recv.at[0], core=sib)
    spread_far(0)
    settled(q_over)
    q_sum[...] = (q_sum[...].astype(f32) + q_y[...].astype(f32)).astype(bf16)
    store(q_sum, q_slot(g), l_sem.at[0])
    ring_q.start()
    begin(q_slot(g), q_slot(g), qs_send.at[0], qs_recv.at[0], core=sib)
    on_ring_b(1)
    v_move.wait_recv()
    v_pass[...] = (v_keep[other] + v_in[other].astype(f32)).astype(bf16)
    v_across = begin(v_pass, v_x, v_send.at[1], v_recv.at[1], x=other)
    settled(s_sib)
    sums_ref[...] += sums_got[0]
    s_x = begin(sums_ref, sums_got.at[1], s_send.at[1], s_recv.at[1], x=other)
    pl.when(between)(lambda: steps(chain_a, 1))
    v_across.wait_recv()
    v_sum[...] = (v_keep[x] + v_in[x].astype(f32) + v_x[...].astype(f32)).astype(bf16)
    v_over = begin(v_sum, v_y, v_send.at[2], v_recv.at[2], r=far_r)
    settled(s_x)
    sums_ref[...] += sums_got[1]
    s_y = begin(sums_ref, sums_got.at[2], s_send.at[2], s_recv.at[2], r=far_r)
    on_ring_b(2)
    pl.when(between)(lambda: steps(chain_a, 2))
    settled(v_over)
    v_sum[...] = (v_sum[...].astype(f32) + v_y[...].astype(f32)).astype(bf16)
    store(v_sum, v_slot(g), l_sem.at[0])
    ring_v.start()
    begin(v_slot(g), v_slot(g), vs_send.at[0], vs_recv.at[0], core=sib)
    settled(s_y)
    sums_ref[...] += sums_got[2]
    for away in range(1, GROUPS):
        begin(
            sums_ref, sums_got.at[2 + away], s_send.at[2 + away], s_recv.at[2 + away],
            g=lax.rem(g + away, GROUPS),
        )
    spread_far(1)
    on_ring_q(1)
    on_ring_b(3)
    chain_a.step(g)

    loads[7].wait()
    loads[8].wait()
    grad_first = total_a[...]
    values = tokens_ref[...].astype(f32)
    mean = jnp.mean(values, axis=-1, keepdims=True)
    centred = values - mean
    scale = lax.rsqrt(jnp.mean(centred * centred, axis=-1, keepdims=True) + EPS)
    n1 = centred * scale
    pulled = grad_first * small_ref[0:1]
    inward = pulled - jnp.mean(pulled, axis=-1, keepdims=True) - n1 * jnp.mean(pulled * n1, axis=-1, keepdims=True)
    tokens_grad_ref[...] = mgrad_ref[...] + inward * scale
    late[...] = jnp.zeros_like(late)
    late[0:1] = jnp.sum(grad_first * n1, axis=0, keepdims=True)
    late[1:2] = jnp.sum(grad_first, axis=0, keepdims=True)
    for step in range(len(AROUND)):
        begin(late, late_got.at[step], t_send.at[step], t_recv.at[step], **neighbour(r, core, x, step))
    on_ring_v(1)
    on_ring_q(2)
    on_ring_q(3)
    spread_far(2)
    on_ring_v(2)
    late_sum[...] = late[...]
    for step in range(len(AROUND)):
        arrived(late_got.at[step], t_send.at[step], t_recv.at[step], x)
        late_sum[...] += late_got[step]
    first_z = len(AROUND) - 1
    for away in range(1, GROUPS):
        begin(
            late_sum, late_got.at[first_z + away], t_send.at[first_z + away], t_recv.at[first_z + away],
            g=lax.rem(g + away, GROUPS),
        )
    on_ring_v(3)
    spread_far(3)

    for away in range(1, GROUPS):
        arrived(sums_got.at[2 + away], s_send.at[2 + away], s_recv.at[2 + away], x)
        arrived(late_got.at[first_z + away], t_send.at[first_z + away], t_recv.at[first_z + away], x)
    for step in range(GROUPS):
        z = nearest(g, step)
        arrived(qout_ref.at[sib, z], qs_send.at[step], qs_recv.at[step], x)
        arrived(kvout_ref.at[sib, z], vs_send.at[step], vs_recv.at[step], x)
        arrived(big_ref.at[sib, r, z], fs_send.at[0, step], fs_recv.at[0, step], x)
        arrived(big_ref.at[sib, far_r, z], fs_send.at[1, step], fs_recv.at[1, step], x)
    for move in pending:
        move.wait_send()
    for item in (chain_a, chain_b, ring_q, ring_v, ring_b):
        item.finish()
    sums_ref[...] += sums_got[3] + sums_got[4] + sums_got[5]
    total = late_sum[...] + late_got[first_z + 1] + late_got[first_z + 2] + late_got[first_z + 3]
    sums_ref[0:2] = total[0:2]


def scatter(dkv, dq, normed, wfull, tokens, mgrad, small, keep, over, near, far, sums):
    rows, width = tokens.shape
    fourth = width // 4
    dma = pltpu.SemaphoreType.DMA
    wide_q, wide_v = 2 * BLK, 2 * HW
    kv_block = (rows, wide_v)
    full = (rows, width)
    unit = (UNIT, width)

    def weight_scratch(wide):
        return [
            pltpu.VMEM((2, fourth, wide), f32),
            pltpu.VMEM((2, fourth, wide), bf16),
            pltpu.VMEM((2, fourth, wide), bf16),
            *[pltpu.VMEM((fourth, wide), bf16)] * 4,
        ]

    return pl.pallas_call(
        scatter_kernel,
        out_shape=(
            jax.ShapeDtypeStruct(full, f32),
            jax.ShapeDtypeStruct((2, 2, GROUPS, *unit), bf16),
            jax.ShapeDtypeStruct((2, GROUPS, fourth, wide_q), bf16),
            jax.ShapeDtypeStruct((2, GROUPS, fourth, wide_v), bf16),
            jax.ShapeDtypeStruct((24, width), f32),
        ),
        in_specs=[anywhere()] * 10 + [whole_vmem()] * 2,
        out_specs=(whole_vmem(), anywhere(), anywhere(), anywhere(), whole_vmem()),
        scratch_shapes=[
            *[
                pltpu.VMEM(item.shape, item.dtype)
                for item in (dq, normed, wfull, tokens, mgrad, keep, over)
            ],
            pltpu.VMEM((48 * GROUPS, width), bf16),
            pltpu.VMEM(far.shape, bf16),
            pltpu.VMEM((GROUPS, 4, *kv_block), bf16),
            pltpu.VMEM((GROUPS, 4, *kv_block), bf16),
            pltpu.VMEM((GROUPS, 2, *kv_block), f32),
            pltpu.VMEM((GROUPS, 2, *kv_block), bf16),
            pltpu.VMEM((GROUPS, 2, *kv_block), bf16),
            pltpu.VMEM((GROUPS, *kv_block), bf16),
            pltpu.VMEM((GROUPS, *kv_block), bf16),
            pltpu.VMEM((GROUPS, *full), f32),
            pltpu.VMEM(full, f32),
            pltpu.VMEM((2, GROUPS, *full), bf16),
            pltpu.VMEM((GROUPS, *full), bf16),
            pltpu.VMEM((width, wide_v), f32),
            pltpu.VMEM((GROUPS, *unit), f32),
            pltpu.VMEM(unit, f32),
            pltpu.VMEM((2, GROUPS, *unit), bf16),
            pltpu.VMEM((GROUPS, *unit), bf16),
            pltpu.VMEM(unit, bf16),
            *weight_scratch(wide_q),
            *weight_scratch(wide_v),
            pltpu.VMEM((6, 24, width), f32),
            pltpu.VMEM((8, width), f32),
            pltpu.VMEM((8, width), f32),
            pltpu.VMEM((len(AROUND) + GROUPS - 1, 8, width), f32),
            dma((9,)),
            dma((GROUPS, 4)), dma((GROUPS, 4)), dma((GROUPS, 4)), dma((GROUPS,)), dma((GROUPS,)), dma((GROUPS,)), dma((GROUPS,)),
            dma((GROUPS,)), dma((2, GROUPS)),
            dma((GROUPS,)), dma((2, GROUPS)), dma((2,)), dma((GROUPS,)), dma((GROUPS,)),
            dma((GROUPS,)), dma((GROUPS,)), dma((2, GROUPS)), dma((2, GROUPS)),
            dma((3,)), dma((3,)), dma((2,)), dma((GROUPS,)), dma((GROUPS,)), dma((GROUPS,)), dma((GROUPS,)),
            dma((3,)), dma((3,)), dma((2,)), dma((GROUPS,)), dma((GROUPS,)), dma((GROUPS,)), dma((GROUPS,)),
            dma((6,)), dma((6,)), dma((10,)), dma((10,)), dma((1,)),
        ],
        compiler_params=pltpu.CompilerParams(
            collective_id=2, has_side_effects=True, vmem_limit_bytes=54 << 20
        ),
        name="scatter",
    )(dkv, dq, normed, wfull, tokens, mgrad, keep, over, near, far, small, sums)


def pack_kv(key_part, value_part):
    return jnp.concatenate(
        [key_part, value_part[..., 2 * DH :], value_part[..., : 2 * DH]], axis=-1
    )


def unpack_kv(both):
    return both[..., :HW], jnp.concatenate([both[..., HW + DH :], both[..., HW : HW + DH]], axis=-1)


def layout_kernel(
    big_ref, query_ref, kv_ref, sums_ref, base_ref, got_ref,
    up_out, down_out, wo_out, query_out, key_out, value_out,
    low_gain, low_shift, query_bias, value_bias, out_bias, high_gain, high_shift, up_bias, down_bias, result_out,
):
    x = lax.axis_index("x")
    width = big_ref.shape[-1]
    half = width // 2
    result_out[...] = (base_ref[...] + got_ref[...].astype(f32)).astype(bf16)
    for core in range(2):
        down_out[core] = big_ref[core, 0, 0:96].astype(f32)
        wo_out[core] = big_ref[core, 0, 192:UNIT].astype(f32)
        for owner in range(2):
            lane = (2 * owner + core) * width
            up_out[:, lane : lane + width] = big_ref[core, 0, 96 + 48 * owner : 144 + 48 * owner].astype(f32)
        query_out[core] = jnp.concatenate(
            [query_ref[core, z].astype(f32)[:, :HW] for z in range(GROUPS)], axis=1
        )
        both = [unpack_kv(kv_ref[core, z].astype(f32)) for z in range(GROUPS)]
        key_out[core] = jnp.concatenate([item[0] for item in both], axis=1)
        value_out[core] = jnp.concatenate([item[1] for item in both], axis=1)

    @pl.when(pl.program_id(0) == 0)
    def _():
        def own_half(row):
            whole = sums_ref[row : row + 1]
            return jnp.where(x == 0, whole[:, :half], whole[:, half:]).reshape(half)

        for ref, row in (
            (low_gain, 0), (low_shift, 1), (out_bias, 2), (high_gain, 3), (high_shift, 4), (down_bias, 5),
        ):
            ref[...] = own_half(row)
        pair = [sums_ref[pl.ds(16 + 2 * x + i, 1)] for i in range(2)]
        query_bias[...] = jnp.concatenate([item[:, :HW] for item in pair], axis=1).reshape(half)
        value_bias[...] = jnp.concatenate(
            [unpack_kv(item[:, 2 * BLK : 2 * BLK + 2 * HW])[1] for item in pair], axis=1
        ).reshape(half)
        up_bias[...] = jnp.concatenate(
            [sums_ref[pl.ds(8 + 2 * x + i, 1)] for i in range(2)], axis=1
        ).reshape(2 * width)


def lay_out(big, query, kv, sums, base, got):
    width = big.shape[-1]
    half, fourth = width // 2, width // 4
    rows = fourth // PARTS

    def spec(shape, index):
        return pl.BlockSpec(shape, index)

    def fixed(wide):
        return pl.BlockSpec((wide,), lambda p: (0,))

    narrow = spec((2, rows, width), lambda p: (0, p, 0))
    vector = jax.ShapeDtypeStruct((half,), f32)
    return pl.pallas_call(
        layout_kernel,
        grid=(PARTS,),
        out_shape=(
            jax.ShapeDtypeStruct((half, 4 * width), f32),
            jax.ShapeDtypeStruct((2, width, width), f32),
            *[jax.ShapeDtypeStruct((2, fourth, width), f32)] * 4,
            *[vector] * 7,
            jax.ShapeDtypeStruct((2 * width,), f32),
            vector,
            jax.ShapeDtypeStruct(base.shape, bf16),
        ),
        in_specs=[
            spec((2, 1, UNIT, width), lambda p: (0, p, 0, 0)),
            spec((2, GROUPS, rows, query.shape[-1]), lambda p: (0, 0, p, 0)),
            spec((2, GROUPS, rows, kv.shape[-1]), lambda p: (0, 0, p, 0)),
            spec(sums.shape, lambda p: (0, 0)),
            spec((base.shape[0] // PARTS, width), lambda p: (p, 0)),
            spec((base.shape[0] // PARTS, width), lambda p: (p, 0)),
        ],
        out_specs=(
            spec((48, 4 * width), lambda p: (p, 0)),
            spec((2, 96, width), lambda p: (0, p, 0)),
            *[narrow] * 4,
            *[fixed(half)] * 7,
            fixed(2 * width),
            fixed(half),
            spec((base.shape[0] // PARTS, width), lambda p: (p, 0)),
        ),
        compiler_params=pltpu.CompilerParams(
            vmem_limit_bytes=VMEM_LIMIT, dimension_semantics=("arbitrary",)
        ),
        name="lay_out",
    )(big, query, kv, sums, base, got)


ROWS = ("s", "r", "core", "x")
ALL = ("g", "s", "r", "core", "x")


def shards(
    tokens, cotangent, doc_lengths, deal, first_gain, first_shift, query_weight, query_bias,
    key_weight, value_weight, value_bias, output_weight, output_bias, second_gain, second_shift,
    up_weight, up_bias, down_weight, down_bias,
):
    rows, width = tokens.shape
    half = width // 2
    blocks = deal.shape[0]
    core, x = lax.axis_index("core"), lax.axis_index("x")
    swap = ((0, 1), (1, 0))

    def up_columns(owner):
        return lax.dynamic_slice_in_dim(up_weight, (2 * owner + core) * width, width, 1)

    kv, q, normed, small, wfull, wo = gather(
        tokens, query_weight, key_weight, value_weight, output_weight,
        first_gain, first_shift, output_bias, second_gain, second_shift, down_bias, query_bias, value_bias, up_bias,
    )
    wide = blocks > 8 * 2 * GROUPS
    if wide:
        kv = lax.all_gather(kv, "s", axis=0, tiled=True)
    kv = kv.reshape(blocks, BLK, 2 * HW)
    q = q.reshape(2 * GROUPS, BLK, 2 * BLK)
    cot_x, up_other, kv = lax.optimization_barrier((cotangent, up_columns(1 - x), kv))
    up_other = lax.ppermute(up_other, "x", swap)
    cot_x = lax.ppermute(cot_x, "x", swap)
    out_t, kept, lse = attend_forward(deal, doc_lengths, q, kv)
    base, x_give, grad_middle, grad_t, kept_part, over, far, sums = dense(
        out_t, tokens, cotangent, cot_x, small, wo, up_columns(x), up_other, down_weight
    )
    over = lax.ppermute(over, "r", swap)
    x_got = lax.ppermute(x_give, "x", swap)
    far = lax.ppermute(far, ("r", "x"), ((0, 3), (1, 2), (2, 1), (3, 0)))
    dq, dkv = attend_backward(deal, doc_lengths, q, kv, lse, grad_t, kept)
    dkv = dkv.reshape(-1, GROUPS, rows, 2 * HW)
    if wide:
        dkv = lax.psum_scatter(dkv, "s", scatter_dimension=0, tiled=True)
    dq = dq.reshape(GROUPS, rows, 2 * BLK)
    grad_tokens, big, query_own, kv_own, sums = scatter(
        dkv, dq, normed, wfull, tokens, grad_middle, small, kept_part, over, x_got, far, sums
    )
    if wide:
        big, query_own, kv_own, sums = (
            lax.psum(item, "s") for item in (big, query_own, kv_own, sums)
        )

    (
        up_own, down_own, wo_own, query_own, key_own, value_own,
        low_gain, low_shift, query_sum, value_sum, out_sum, high_gain, high_shift, up_sum, down_sum, result,
    ) = lay_out(big.reshape(2, PARTS, UNIT, width), query_own, kv_own, sums, base, x_got)

    def flat(item):
        return item.reshape(-1, width)

    return (
        result,
        grad_tokens,
        low_gain,
        low_shift,
        flat(query_own),
        query_sum,
        flat(key_own),
        flat(value_own),
        value_sum,
        flat(wo_own),
        out_sum,
        high_gain,
        high_shift,
        up_own,
        up_sum,
        flat(down_own),
        down_sum,
    )


def solution(mesh):
    devices = mesh.devices
    inner_mesh = Mesh(devices.reshape(GROUPS, devices.shape[0] // (4 * GROUPS), 2, 2, 2), ALL)
    row = P(ALL, None)
    mat = P("x", None)
    vec = P("x")
    in_specs = (
        row, row, P(), P(), vec, vec, mat, vec, mat, mat, vec, mat, vec, vec, vec, mat, vec, mat, vec,
    )
    out_specs = (
        row, row, vec, vec, mat, vec, mat, mat, vec, mat, vec, vec, vec, mat, vec, mat, vec,
    )
    return jax.shard_map(
        shards, mesh=inner_mesh, in_specs=in_specs, out_specs=out_specs, check_vma=False
    )
```

```python
import jax
import jax.numpy as jnp
from jax import lax
from jax.experimental import pallas as pl
from jax.experimental.pallas import tpu as pltpu
from jax.sharding import Mesh
from jax.sharding import PartitionSpec as P

HEADS = 12
DH = 64
NSUM = 50
SEG = 2048
BLK = 128
GROUPS = 4
PER = HEADS // GROUPS
HW = PER * DH
WIDE = PER * BLK
CHUNK = 2 * BLK
DEPTH = 8
EPS = 1e-05
SCALE = 0.125
MASKED = -1e30
ROOT_HALF = 0.7071067811865476
PDF_SCALE = 0.3989422804014327
VMEM_LIMIT = 56 << 20
bf16 = jnp.bfloat16
f32 = jnp.float32


def layer_norm(values, gain, shift):
    mean = jnp.mean(values, axis=-1, keepdims=True)
    centred = values - mean
    spread = jnp.mean(centred * centred, axis=-1, keepdims=True)
    return centred * lax.rsqrt(spread + EPS) * gain + shift


def outer(left, right):
    return lax.dot_general(left, right, (((0,), (0,)), ((), ())), preferred_element_type=f32)


def inner(left, right):
    return lax.dot_general(left, right, (((1,), (1,)), ((), ())), preferred_element_type=f32)


def dot(left, right):
    return jnp.dot(left, right, preferred_element_type=f32)


def survey(deal_ref, lengths_ref, where_ref, text_ref, low_ref, high_ref, first_ref):
    blocks = deal_ref.shape[0]
    per_group = blocks // (2 * GROUPS)
    rest = lax.axis_index(ROWS)

    def note(j, kept):
        pair = j // 2
        group = pair // per_group
        where_ref[deal_ref[j]] = ((pair - group * per_group) * GROUPS + group) * 2 + j % 2
        return kept

    lax.fori_loop(0, blocks, note, 0)
    starts = [jnp.int32(0)]
    for doc in range(lengths_ref.shape[0] - 1):
        starts.append(starts[-1] + lengths_ref[doc])

    def first_of(at):
        begin = jnp.zeros_like(at)
        for start in starts:
            begin = jnp.where(start <= at, jnp.maximum(begin, start), begin)
        return jnp.where(at - begin >= SEG + NSUM, begin + SEG, begin)

    for slot in range(2 * GROUPS):
        text = deal_ref[2 * ((slot // 2) * per_group + rest) + slot % 2]
        text_ref[slot] = text
        low_ref[slot] = first_of(text * BLK) // CHUNK
        high_ref[slot] = text // 2
        first_ref[slot] = first_of(text * BLK + lax.broadcasted_iota(jnp.int32, (1, BLK), 1))


def survey_scratch(blocks):
    slots = 2 * GROUPS
    return [
        pltpu.SMEM((blocks,), jnp.int32),
        pltpu.SMEM((slots,), jnp.int32),
        pltpu.SMEM((slots,), jnp.int32),
        pltpu.SMEM((slots,), jnp.int32),
        pltpu.VMEM((slots, 1, BLK), jnp.int32),
    ]


def spread_heads_t(part_t, order):
    rows = []
    zero = jnp.zeros((DH, BLK), part_t.dtype)
    for head in order:
        if head is None:
            rows.append(jnp.zeros((DH, WIDE), part_t.dtype))
        else:
            piece = part_t[DH * head : DH * head + DH]
            rows.append(
                jnp.concatenate([piece if h == head else zero for h in range(PER)], axis=1)
            )
    return jnp.concatenate(rows, axis=0)


K_ORDER = (0, 1, 2, None)
V_ORDER = (None, 2, 0, 1)


def visible(chunk, first, own):
    at = chunk * CHUNK + lax.broadcasted_iota(jnp.int32, (CHUNK, BLK), 0)
    allowed = (at >= first) & (at <= own)
    return jnp.concatenate([allowed] * PER, axis=1)


def load_chunk(kv_ref, where_ref, chunk):
    return jnp.concatenate(
        [kv_ref[where_ref[2 * chunk]], kv_ref[where_ref[2 * chunk + 1]]], axis=0
    )


def forward_kernel(
    deal_ref, lengths_ref, q_ref, kv_ref,
    out_ref, wide_ref, lse_ref,
    where_ref, text_ref, low_ref, high_ref, first_ref, acc_ref,
):
    survey(deal_ref, lengths_ref, where_ref, text_ref, low_ref, high_ref, first_ref)

    def one_slot(slot, kept):
        wide_q = spread_heads_t(q_ref[slot].T[:HW], K_ORDER)
        first = first_ref[slot]
        own = text_ref[slot] * BLK + lax.broadcasted_iota(jnp.int32, (1, BLK), 1)
        last_first = jnp.max(first)
        acc_ref[...] = jnp.zeros_like(acc_ref)

        def step(double, carry):
            top, total = carry
            scores = []
            for part in range(2):
                keys = load_chunk(kv_ref, where_ref, 2 * double + part)[:, : 2 * BLK]
                scores.append(jnp.where(visible(2 * double + part, first, own), dot(keys, wide_q), MASKED))
            scores = jnp.concatenate(scores, axis=0)
            fresh = jnp.maximum(top, jnp.max(scores, axis=0, keepdims=True))
            expo = jnp.exp(scores - fresh)
            shrink = jnp.exp(top - fresh)
            total = total * shrink + jnp.sum(expo, axis=0, keepdims=True)
            vals = jnp.concatenate([load_chunk(kv_ref, where_ref, 2 * double + part)[:, BLK:] for part in range(2)], axis=0)
            acc_ref[...] = acc_ref[...] * shrink + outer(vals, expo.astype(bf16))
            return fresh, total

        top, total = lax.fori_loop(
            low_ref[slot] // 2,
            high_ref[slot] // 2 + 1,
            step,
            (jnp.full((1, WIDE), MASKED, f32), jnp.zeros((1, WIDE), f32)),
        )
        lse_ref[slot] = top + jnp.log(total)
        scaled = acc_ref[...] / total
        pieces = []
        for head in range(PER):
            row = DH * V_ORDER.index(head)
            pieces.append(scaled[row : row + DH, BLK * head : BLK * head + BLK])
        whole = jnp.concatenate(pieces, axis=0)
        wide_ref[slot] = whole
        out_ref[slot] = whole.astype(bf16)
        return kept

    lax.fori_loop(0, q_ref.shape[0], one_slot, 0)


def whole_vmem():
    return pl.BlockSpec(memory_space=pltpu.VMEM)


def whole_smem():
    return pl.BlockSpec(memory_space=pltpu.SMEM)


def attend_forward(deal, lengths, q, kv):
    slots = q.shape[0]
    blocks = kv.shape[0]
    return pl.pallas_call(
        forward_kernel,
        out_shape=(
            jax.ShapeDtypeStruct((slots, HW, BLK), bf16),
            jax.ShapeDtypeStruct((slots, HW, BLK), f32),
            jax.ShapeDtypeStruct((slots, 1, WIDE), f32),
        ),
        in_specs=[whole_smem()] * 2 + [whole_vmem()] * 2,
        out_specs=(whole_vmem(),) * 3,
        scratch_shapes=[
            *survey_scratch(blocks),
            pltpu.VMEM((2 * BLK, WIDE), f32),
        ],
        compiler_params=pltpu.CompilerParams(vmem_limit_bytes=(6 << 20) + kv.size // 5 * 16),
        name="attend_forward",
    )(deal, lengths, q, kv)


def backward_kernel(
    deal_ref, lengths_ref, q_ref, kv_ref, lse_ref, do_ref, wide_ref,
    dq_ref, dkv_ref, where_ref, text_ref, low_ref, high_ref, first_ref, qt_ref, qm_ref, dot_ref, dom_ref, delta_ref, acc_ref, dk_acc, dv_acc,
    packed_ref, count_ref, list_ref, out_sem,
):
    survey(deal_ref, lengths_ref, where_ref, text_ref, low_ref, high_ref, first_ref)
    slots = q_ref.shape[0]
    chunks = kv_ref.shape[0] // 2

    def ready(slot, _):
        q = q_ref[slot]
        qt_ref[slot] = spread_heads_t(q.T[:HW], K_ORDER)
        lane = lax.broadcasted_iota(jnp.int32, (BLK, 2 * BLK), 1) // DH
        zero = jnp.zeros_like(q)
        qm_ref[slot] = jnp.concatenate(
            [jnp.where(lane == K_ORDER.index(h), q, zero) for h in range(PER)], axis=0
        )
        grad_t = do_ref[slot]
        dot_ref[slot] = spread_heads_t(grad_t, V_ORDER)
        ordered = jnp.concatenate(
            [
                jnp.zeros((DH, BLK), bf16) if h is None else grad_t[DH * h : DH * h + DH]
                for h in V_ORDER
            ],
            axis=0,
        ).T
        dom_ref[slot] = jnp.concatenate(
            [jnp.where(lane == V_ORDER.index(h), ordered, zero) for h in range(PER)], axis=0
        )
        both = grad_t.astype(f32) * wide_ref[slot]
        delta_ref[slot] = jnp.concatenate(
            [jnp.sum(both[DH * h : DH * h + DH], axis=0, keepdims=True) for h in range(PER)],
            axis=1,
        )
        acc_ref[slot] = jnp.zeros((HW, WIDE), f32)
        return _

    lax.fori_loop(0, slots, ready, 0)

    def clear(chunk, kept):
        count_ref[chunk] = 0
        return kept

    lax.fori_loop(0, chunks, clear, 0)

    def enlist(slot, kept):
        def seen(chunk, kept):
            count = count_ref[chunk]
            list_ref[chunk * slots + count] = slot
            count_ref[chunk] = count + 1
            return kept

        lax.fori_loop(low_ref[slot], high_ref[slot] + 1, seen, 0)
        return kept

    lax.fori_loop(0, slots, enlist, 0)

    def written(chunk, i):
        return pltpu.make_async_copy(
            packed_ref.at[chunk % DEPTH, i], dkv_ref.at[where_ref[2 * chunk + i]], out_sem.at[chunk % DEPTH, i]
        )

    def one_chunk(chunk, kept):
        part = load_chunk(kv_ref, where_ref, chunk)
        keys = part[:, : 2 * BLK]
        vals = part[:, BLK:]
        keys_t = keys.T[:HW]
        dk_acc[...] = jnp.zeros_like(dk_acc)
        dv_acc[...] = jnp.zeros_like(dv_acc)

        def one_slot(i, kept):
            for half in range(2):
                attend(list_ref[chunk * slots + 2 * i + half])
            return kept

        def attend(slot):
            own = text_ref[slot] * BLK + lax.broadcasted_iota(jnp.int32, (1, BLK), 1)
            scores = dot(keys, qt_ref[slot])
            dprobs = dot(vals, dot_ref[slot])
            probs = jnp.where(visible(chunk, first_ref[slot], own), jnp.exp(scores - lse_ref[slot]), 0.0)
            dscores = (probs * (dprobs - delta_ref[slot])).astype(bf16)
            dv_acc[...] += dot(probs.astype(bf16), dom_ref[slot])
            dk_acc[...] += dot(dscores, qm_ref[slot])
            acc_ref[slot] += dot(keys_t, dscores)

        lax.fori_loop(0, count_ref[chunk] // 2, one_slot, 0)
        pl.when(count_ref[chunk] % 2 == 1)(lambda: attend(list_ref[chunk * slots + count_ref[chunk] - 1]))
        packed = jnp.concatenate(
            [
                dk_acc[:, :BLK],
                dk_acc[:, BLK:] + dv_acc[:, :BLK],
                dv_acc[:, BLK:],
            ],
            axis=1,
        ).astype(bf16)

        @pl.when(chunk >= DEPTH)
        def _():
            for i in range(2):
                written(chunk - DEPTH, i).wait()

        for i in range(2):
            packed_ref[chunk % DEPTH, i] = packed[BLK * i : BLK * i + BLK]
            written(chunk, i).start()
        return kept

    lax.fori_loop(0, chunks, one_chunk, 0)
    for last in range(DEPTH):
        for i in range(2):
            written(chunks - DEPTH + last, i).wait()

    def finish(slot, _):
        total = acc_ref[slot]
        kept = jnp.concatenate(
            [total[DH * h : DH * h + DH, BLK * h : BLK * h + BLK] for h in range(PER)]
            + [jnp.zeros((DH, BLK), f32)],
            axis=0,
        )
        dq_ref[slot] = kept.T.astype(bf16)
        return _

    lax.fori_loop(0, slots, finish, 0)


def attend_backward(deal, lengths, q, kv, lse, grad_t, wide):
    slots = q.shape[0]
    return pl.pallas_call(
        backward_kernel,
        out_shape=(
            jax.ShapeDtypeStruct((slots, BLK, 2 * BLK), bf16),
            jax.ShapeDtypeStruct(kv.shape, bf16),
        ),
        in_specs=[whole_smem()] * 2 + [whole_vmem()] * 5,
        out_specs=(whole_vmem(), in_hbm()),
        scratch_shapes=[
            *survey_scratch(kv.shape[0]),
            pltpu.VMEM((slots, 2 * BLK, WIDE), bf16),
            pltpu.VMEM((slots, WIDE, 2 * BLK), bf16),
            pltpu.VMEM((slots, 2 * BLK, WIDE), bf16),
            pltpu.VMEM((slots, WIDE, 2 * BLK), bf16),
            pltpu.VMEM((slots, 1, WIDE), f32),
            pltpu.VMEM((slots, HW, WIDE), f32),
            pltpu.VMEM((CHUNK, 2 * BLK), f32),
            pltpu.VMEM((CHUNK, 2 * BLK), f32),
            pltpu.VMEM((DEPTH, 2, BLK, 2 * HW), bf16),
            pltpu.SMEM((kv.shape[0] // 2,), jnp.int32),
            pltpu.SMEM((kv.shape[0] // 2 * slots,), jnp.int32),
            pltpu.SemaphoreType.DMA((DEPTH, 2)),
        ],
        compiler_params=pltpu.CompilerParams(
            vmem_limit_bytes=max(30 << 20, (17 << 20) + kv.size * 2)
        ),
        name="attend_backward",
    )(deal, lengths, q, kv, lse, grad_t, wide)


MESH = pl.DeviceIdType.MESH


def send(src, dst, out_sem, in_sem, **device):
    return pltpu.make_async_remote_copy(
        src_ref=src, dst_ref=dst, send_sem=out_sem, recv_sem=in_sem, device_id=device, device_id_type=MESH
    )


def place():
    return tuple(lax.axis_index(name) for name in ("g", "r", "core", "x"))


def seat(r, core, x):
    return (r * 2 + core) * 2 + x


AROUND = ((0, 0, 1), (0, 1, 0), (0, 1, 1), (1, 0, 0), (1, 0, 1), (1, 1, 0), (1, 1, 1))


def neighbour(r, core, x, step):
    dr, dc, dx = AROUND[step]
    return {"r": 1 - r if dr else r, "core": 1 - core if dc else core, "x": 1 - x if dx else x}


def greet(g, r, core, x, line, around=False):
    barrier = pltpu.get_barrier_semaphore()

    def hello(**device):
        pl.semaphore_signal(barrier, inc=1, device_id=device, device_id_type=MESH)

    if around:
        for step in range(len(AROUND)):
            hello(**neighbour(r, core, x, step))
    else:
        hello(core=1 - core)
        hello(x=1 - x)
        hello(r=1 - r)
    near = len(AROUND) if around else 3
    if line:
        for away in range(1, GROUPS):
            hello(g=lax.rem(g + away, GROUPS))
        pl.semaphore_wait(barrier, near + GROUPS - 1)
    else:
        pl.when(g > 0)(lambda: hello(g=g - 1))
        pl.when(g < GROUPS - 1)(lambda: hello(g=g + 1))
        pl.semaphore_wait(barrier, near + 2 - jnp.where(g == 0, 1, 0) - jnp.where(g == GROUPS - 1, 1, 0))


NEAREST = ((0, 1, 2, 3), (1, 2, 0, 3), (2, 1, 3, 0), (3, 2, 1, 0))


def nearest(g, step):
    picked = NEAREST[0][step]
    for z in range(1, GROUPS):
        picked = jnp.where(g == z, NEAREST[z][step], picked)
    return picked


def prepare(g, x, weights, lines, narrow_ref, small_ref):
    half = weights.shape[1]
    odd = lax.rem(g, 2) == 1

    def columns(i):
        low = pl.multiple_of(3 * g // 2 * BLK, BLK)
        window = weights[i, :, pl.ds(low, 2 * BLK)]
        moved = jnp.concatenate([window[:, DH:], window[:, :DH]], axis=1)
        return jnp.where(odd, moved, window)

    lane = lax.broadcasted_iota(jnp.int32, (half, 2 * BLK), 1)
    query = columns(0)
    narrow_ref[:, : 2 * BLK] = jnp.where(lane < HW, query, jnp.zeros_like(query))
    narrow_ref[:, 2 * BLK :] = pack_kv(columns(1)[:, :HW], columns(2)[:, :HW])

    def line(i):
        return lines[i][...].astype(f32).reshape(1, -1)

    zero = jnp.zeros((1, half), f32)
    small_ref[...] = jnp.zeros_like(small_ref)
    for row in range(6):
        small_ref[row : row + 1] = jnp.where(
            x == 0, jnp.concatenate([line(row), zero], axis=1), jnp.concatenate([zero, line(row)], axis=1)
        )
    ups = line(8)
    for i in range(2):
        small_ref[pl.ds(8 + 2 * x + i, 1)] = ups[:, 2 * half * i : 2 * half * i + 2 * half]

    def part(i):
        mine = jnp.where(odd, line(i)[:, HW:], line(i)[:, :HW])
        return jnp.where(g // 2 == x, mine, jnp.zeros_like(mine))

    value = part(7)
    small_ref[12:13] = jnp.concatenate(
        [part(6), jnp.zeros((1, 2 * BLK), f32), value[:, 2 * DH :], value[:, : 2 * DH], jnp.zeros((1, BLK), f32)], axis=1
    )


def gather_kernel(
    tokens_ref, query_any, key_any, value_any, wo_ref, l0, l1, l2, l3, l4, l5, l6, l7, l8,
    kv_ref, q_ref, normed_ref, small_out, wfull, wo_out,
    lined, attn_w, narrow_ref, small_ref, small_in, kvs,
    z_own, z_send, z_recv, s_sem, n_send, n_recv, kv_send, kv_recv, kv_local, w_send, w_recv, w_local, a_sem,
):
    g, r, core, x = place()
    other = 1 - x
    rows, width = tokens_ref.shape
    half = width // 2
    fourth = half // 2
    eighth = half // 4
    loads = [
        pltpu.make_async_copy(ref, attn_w.at[i], a_sem.at[i]) for i, ref in enumerate((query_any, key_any, value_any))
    ]
    for load in loads:
        load.start()
    greet(g, r, core, x, False)

    def half_of(source, part):
        return lined.at[source, pl.ds(BLK * part, BLK)]

    def along(source, part, away, sem):
        return send(half_of(source, part), half_of(source, part), sem, z_recv.at[source, part], g=g + away)

    lined[g] = tokens_ref[...]
    for part in range(2):
        pl.when(g > 0)(lambda: along(g, part, -1, z_own.at[0, part]).start())
        pl.when(g < GROUPS - 1)(lambda: along(g, part, 1, z_own.at[1, part]).start())

    for load in loads:
        load.wait()
    prepare(g, x, attn_w, (l0, l1, l2, l3, l4, l5, l6, l7, l8), narrow_ref, small_ref)
    small_move = send(small_ref, small_in, s_sem.at[0], s_sem.at[1], x=other)
    small_move.start()
    mine = pl.ds(x * half + core * fourth, fourth)
    narrow_x = send(narrow_ref.at[pl.ds(core * fourth, fourth)], wfull.at[mine], n_send.at[0], n_recv.at[0], x=other)
    narrow_x.start()

    def wo_rows(owner, part):
        return wo_out.at[pl.ds(owner * half + core * fourth + part * eighth, eighth)]

    wo_x = send(wo_ref.at[pl.ds(core * fourth + r * eighth, eighth)], wo_rows(x, r), w_send.at[0], w_recv.at[0], x=other)
    wo_y = send(wo_rows(other, r), wo_rows(other, r), w_send.at[3], w_recv.at[3], r=1 - r)
    wo_s = [
        send(wo_rows(other, part), wo_rows(other, part), w_send.at[6 + i], w_recv.at[6 + i], core=1 - core)
        for i, part in enumerate((r, 1 - r))
    ]
    wo_x.start()
    locals_ = [pltpu.make_async_copy(wo_ref, wo_out.at[pl.ds(x * half, half)], w_local.at[0])]
    for item in locals_:
        item.start()

    wfull[pl.ds(x * half, half)] = narrow_ref[...]
    narrow_x.wait_recv()
    theirs = wfull.at[pl.ds(other * half + core * fourth, fourth)]
    narrow_s = send(theirs, theirs, n_send.at[1], n_recv.at[1], core=1 - core)
    narrow_s.start()
    small_move.wait_recv()
    small_out[...] = small_ref[...] + small_in[...]
    narrow_s.wait_recv()

    own = seat(r, core, x)

    def span(step):
        return (step, 0, rows) if step < GROUPS - 1 else (GROUPS - 1, BLK * (step - GROUPS + 1), BLK)

    def block(owner, step):
        nth, low, count = span(step)
        return kv_ref.at[owner, nearest(g, nth), pl.ds(low, count)]

    def made(step):
        nth, low, count = span(step)
        return kvs.at[nth, pl.ds(low, count)]

    def push(step, kind, src, dst, **device):
        send(src, dst, kv_send.at[kind, step], kv_recv.at[kind, step], **device).start()

    def settle(step, kind, owner):
        arrived(block(owner, step), kv_send.at[kind, step], kv_recv.at[kind, step], x)

    def forward(step):
        by_x = block(seat(r, core, other), step)
        settle(step, 0, seat(r, core, other))
        if step % 2 == 0:
            push(step, 3, by_x, by_x, r=1 - r)
        push(step, 4, by_x, by_x, core=1 - core)
        by_y = block(seat(1 - r, core, x), step)
        settle(step, 1, seat(1 - r, core, x))
        if step % 2 == 1:
            push(step, 3, by_y, by_y, x=other)
        push(step, 5, by_y, by_y, core=1 - core)

    def forward_far(step):
        far = block(seat(1 - r, core, other), step)
        settle(step, 3, seat(1 - r, core, other))
        push(step, 6, far, far, core=1 - core)

    def take(nth, part):
        source = nearest(g, nth)
        arrived(half_of(source, part), z_send.at[source, part], z_recv.at[source, part], x)
        pl.when((source < g) & (g < GROUPS - 1))(lambda: along(source, part, 1, z_send.at[source, part]).start())
        pl.when((source > g) & (g > 0))(lambda: along(source, part, -1, z_send.at[source, part]).start())

    def project(step):
        nth, low, count = span(step)
        source = nearest(g, nth)
        taken = pl.ds(low, count)
        values = lined[source, taken].astype(f32)
        normed = layer_norm(values, small_out[0:1], small_out[1:2]).astype(bf16)
        normed_ref[source, taken] = normed
        both = dot(normed, wfull[...]) + small_out[12:13, : wfull.shape[1]]
        kvs[nth, taken] = both[:, 2 * BLK :].astype(bf16)
        push(step, 0, made(step), block(own, step), x=other)
        push(step, 1, made(step), block(own, step), r=1 - r)
        push(step, 2, made(step), block(own, step), core=1 - core)
        q_ref[source, taken] = (both[:, : 2 * BLK] * SCALE).astype(bf16)
        pltpu.make_async_copy(made(step), block(own, step), kv_local.at[step]).start()

    at_end = (g == 0) | (g == GROUPS - 1)
    between = jnp.logical_not(at_end)
    project(0)
    take(1, 0)
    take(1, 1)

    @pl.when(between)
    def _():
        take(2, 0)
        take(2, 1)

    project(1)
    forward(0)

    @pl.when(at_end)
    def _():
        take(2, 0)
        take(2, 1)

    project(2)

    @pl.when(at_end)
    def _():
        forward(1)
        forward_far(0)

    take(3, 0)
    pl.when(between)(lambda: take(3, 1))
    project(3)
    pl.when(at_end)(lambda: take(3, 1))
    project(4)

    @pl.when(between)
    def _():
        forward(1)
        forward_far(0)

    wo_x.wait_recv()
    wo_y.start()
    wo_s[0].start()
    forward(2)
    forward_far(1)
    forward(3)
    forward_far(2)
    forward(4)
    forward_far(3)
    arrived(wo_rows(other, 1 - r), w_send.at[3], w_recv.at[3], x)
    wo_s[1].start()
    forward_far(4)

    for step in range(GROUPS + 1):
        pltpu.make_async_copy(made(step), block(own, step), kv_local.at[step]).wait()
        settle(step, 2, seat(r, 1 - core, x))
        settle(step, 4, seat(r, 1 - core, other))
        settle(step, 5, seat(1 - r, 1 - core, x))
        settle(step, 6, seat(1 - r, 1 - core, other))
        for kind in range(7):
            left(made(step), kv_send.at[kind, step], kv_recv.at[kind, step], x)
    for part in range(2):
        pl.when(g > 0)(lambda: left(half_of(g, part), z_own.at[0, part], z_recv.at[g, part], x))
        pl.when(g < GROUPS - 1)(lambda: left(half_of(g, part), z_own.at[1, part], z_recv.at[g, part], x))
        for nth in range(1, GROUPS):
            source = nearest(g, nth)
            passed = ((source < g) & (g < GROUPS - 1)) | ((source > g) & (g > 0))
            pl.when(passed)(
                lambda: left(half_of(source, part), z_send.at[source, part], z_recv.at[source, part], x)
            )
    small_move.wait_send()
    narrow_x.wait_send()
    narrow_s.wait_send()
    for item in locals_:
        item.wait()
    for item in (wo_x, wo_y, *wo_s):
        item.wait_send()
    for i, part in enumerate((r, 1 - r)):
        there = wo_out.at[pl.ds(other * half + (1 - core) * fourth + part * eighth, eighth)]
        send(there, there, w_send.at[6 + i], w_recv.at[6 + i], core=1 - core).wait_recv()


def anywhere():
    return pl.BlockSpec(memory_space=pl.ANY)


def in_hbm():
    return pl.BlockSpec(memory_space=pltpu.HBM)


def gather(tokens, query, key, value, wo, *lines):
    rows, width = tokens.shape
    wide = 2 * BLK + 2 * HW
    small = (16, width)
    dma = pltpu.SemaphoreType.DMA
    return pl.pallas_call(
        gather_kernel,
        out_shape=(
            jax.ShapeDtypeStruct((8, GROUPS, rows, 2 * HW), bf16),
            jax.ShapeDtypeStruct((GROUPS, rows, 2 * BLK), bf16),
            jax.ShapeDtypeStruct((GROUPS, rows, width), bf16),
            jax.ShapeDtypeStruct(small, f32),
            jax.ShapeDtypeStruct((width, wide), bf16),
            jax.ShapeDtypeStruct((width, width), bf16),
        ),
        in_specs=[whole_vmem(), *[in_hbm()] * 4, *[whole_vmem()] * len(lines)],
        out_specs=(anywhere(), *(whole_vmem(),) * 5),
        scratch_shapes=[
            pltpu.VMEM((GROUPS, rows, width), bf16),
            pltpu.VMEM((3, width // 2, width), bf16),
            pltpu.VMEM((width // 2, wide), bf16),
            pltpu.VMEM(small, f32),
            pltpu.VMEM(small, f32),
            pltpu.VMEM((GROUPS, rows, 2 * HW), bf16),
            dma((2, 2)), dma((GROUPS, 2)), dma((GROUPS, 2)), dma((2,)), dma((2,)), dma((2,)),
            dma((7, GROUPS + 1)), dma((7, GROUPS + 1)), dma((GROUPS + 1,)), dma((8,)), dma((8,)), dma((2,)), dma((3,)),
        ],
        compiler_params=pltpu.CompilerParams(
            collective_id=0, has_side_effects=True, vmem_limit_bytes=16 << 20
        ),
        name="gather",
    )(tokens, query, key, value, wo, *lines)


def erf_parts(values):
    below = 0.5 * (1.0 + lax.erf(values * ROOT_HALF))
    return below, PDF_SCALE * jnp.exp(-0.5 * values * values)


PARTS = 8
UNIT = 216
KEPT = 168


def dense_kernel(
    out_t_ref, tokens_ref, cot_ref, cot_x_ref, small_ref, wo_ref, up_mine, up_other, down_any,
    base_ref, x_give_ref, middle_grad_ref, grad_t_ref, keep_ref, give_ref, far_ref, sums_ref,
    down_ref, up_ref, attn_in, attn_t, cots, h2s, mid_ref, n2_ref, scales, part_y, part_d, in_y, in_d, pass_y, pass_d,
    x_y, x_d, hids, dus, branch_ref, grad_out, wo_keep, wo_give, wo_in, wo_pass, wo_x,
    l_sem, a_send, a_recv, c_send, c_recv, h_send, h_recv, y_send, y_recv, d_send, d_recv, o_send, o_recv,
    w_send, w_recv,
):
    g, r, core, x = place()
    other, sib = 1 - x, 1 - core
    rows, width = tokens_ref.shape
    half = width // 2
    fourth = half // 2
    loads = [
        pltpu.make_async_copy(
            down_any.at[pl.ds(pl.multiple_of(core * width, width), width)], down_ref, l_sem.at[0]
        ),
        pltpu.make_async_copy(up_mine, up_ref.at[pl.ds(x * half, half)], l_sem.at[1]),
        pltpu.make_async_copy(up_other, up_ref.at[pl.ds(other * half, half)], l_sem.at[2]),
    ]
    for load in loads:
        load.start()
    greet(g, r, core, x, True)
    pending = []

    def begin(src, dst, out_sem, in_sem, **device):
        move = send(src, dst, out_sem, in_sem, **device)
        move.start()
        pending.append(move)
        return move

    def other_group(away):
        return lax.rem(g + away, GROUPS)

    def rows_of(b):
        return pl.ds(BLK * b, BLK)

    for b in range(2):
        for away in range(1, GROUPS):
            to = other_group(away)
            begin(out_t_ref.at[2 * to + b], attn_in.at[g, b], a_send.at[b, away], a_recv.at[b, g], g=to)
        attn_in[g, b] = out_t_ref[2 * g + b]
        cots[b, 0] = cot_ref[rows_of(b)]
        cots[b, 2] = cot_x_ref[rows_of(b)]
    cot_moves = [
        begin(cots.at[:, 2 * i], cots.at[:, 2 * i + 1], c_send.at[i], c_recv.at[i], core=sib) for i in range(2)
    ]
    sums_ref[...] = jnp.zeros_like(sums_ref)
    sums_ref[5:6] = jnp.sum(cot_ref[...].astype(f32), axis=0, keepdims=True)
    h2_moves = []

    def norm(b):
        for away in range(1, GROUPS):
            source = other_group(away)
            arrived(attn_in.at[source, b], a_send.at[b, away], a_recv.at[b, source], x)
        for source in range(GROUPS):
            attn_t[HW * source : HW * source + HW, BLK * b : BLK * b + BLK] = attn_in[source, b]
        middle = (
            tokens_ref[rows_of(b)].astype(f32)
            + outer(attn_t[:, BLK * b : BLK * b + BLK], wo_ref[...])
            + small_ref[2:3]
        )
        mid_ref[b] = middle
        mean = jnp.mean(middle, axis=-1, keepdims=True)
        centred = middle - mean
        scale = lax.rsqrt(jnp.mean(centred * centred, axis=-1, keepdims=True) + EPS)
        scales[b] = scale
        n2_ref[b] = centred * scale
        h2s[b, 0] = (n2_ref[b] * small_ref[3:4] + small_ref[4:5]).astype(bf16)
        h2_moves.append(
            (
                begin(h2s.at[b, 0], h2s.at[b, 2], h_send.at[b, 1], h_recv.at[b, 1], x=other),
                begin(h2s.at[b, 0], h2s.at[b, 1], h_send.at[b, 0], h_recv.at[b, 0], core=sib),
            )
        )

    def pass_on(b):
        h2_moves[b][0].wait_recv()
        return begin(h2s.at[b, 2], h2s.at[b, 3], h_send.at[b, 2], h_recv.at[b, 2], core=sib)

    bias_row = 8 + 2 * x + core

    def pair_of(ref, b, pair):
        return ref[b, 2 * pair : 2 * pair + 2].reshape(2 * BLK, width)

    def forward_backward(b, pair):
        cot = pair_of(cots, b, pair)
        expanded = dot(pair_of(h2s, b, pair), up_ref[...]) + small_ref[pl.ds(bias_row, 1)]
        below, density = erf_parts(expanded)
        hidden = (expanded * below).astype(bf16)
        hids[b, pair] = hidden
        slope = below + expanded * density
        grad_hidden = inner(cot, down_ref[...]).astype(bf16).astype(f32)
        grad_expand = (grad_hidden * slope).astype(bf16)
        dus[b, pair] = grad_expand
        part_d[b, pair] = inner(grad_expand, up_ref[...])
        part_y[b, pair] = dot(hidden, down_ref[...])
        sums_ref[pl.ds(bias_row, 1)] += jnp.sum(grad_expand.astype(f32), axis=0, keepdims=True)

    d_moves, y_passes = [None, None], [None, None]

    def near_pair(b):
        if b == 0:
            cot_moves[0].wait_recv()
        h2_moves[b][1].wait_recv()
        forward_backward(b, 0)
        return begin(part_d.at[b, 0, pl.ds(BLK, BLK)], in_d.at[b], d_send.at[b, 0], d_recv.at[b, 0], core=sib)

    def far_pair(b, passed):
        if b == 0:
            cot_moves[1].wait_recv()
        passed.wait_recv()
        forward_backward(b, 1)
        x_d[b, 0] = part_d[b, 1, BLK:].astype(bf16)
        across = begin(x_d.at[b, 0], pass_d.at[b], d_send.at[b, 1], d_recv.at[b, 1], core=sib)
        x_y[b] = part_y[b, 1, BLK:].astype(bf16)
        y_passes[b] = begin(x_y.at[b], pass_y.at[b], y_send.at[b, 1], y_recv.at[b, 1], core=sib)
        across.wait_recv()
        x_d[b, 1] = (part_d[b, 1, :BLK] + pass_d[b].astype(f32)).astype(bf16)
        return begin(x_d.at[b, 1], x_d.at[b, 2], d_send.at[b, 2], d_recv.at[b, 2], x=other)

    def back(b, near, far):
        near.wait_recv()
        far.wait_recv()
        grad_second = part_d[b, 0, :BLK] + in_d[b] + x_d[b, 2].astype(f32)
        n2 = n2_ref[b]
        sums_ref[3:4] += jnp.sum(grad_second * n2, axis=0, keepdims=True)
        sums_ref[4:5] += jnp.sum(grad_second, axis=0, keepdims=True)
        pulled = grad_second * small_ref[3:4]
        inward = (
            pulled - jnp.mean(pulled, axis=-1, keepdims=True) - n2 * jnp.mean(pulled * n2, axis=-1, keepdims=True)
        )
        grad_middle = cot_ref[rows_of(b)].astype(f32) + inward * scales[b]
        middle_grad_ref[rows_of(b)] = grad_middle
        branch = grad_middle.astype(bf16)
        branch_ref[rows_of(b)] = branch
        sums_ref[2:3] += jnp.sum(branch.astype(f32), axis=0, keepdims=True)
        grad_out_t = inner(wo_ref[...], branch).astype(bf16)
        for group in range(GROUPS):
            grad_out[group, b] = grad_out_t[HW * group : HW * group + HW]
        for away in range(1, GROUPS):
            to = other_group(away)
            begin(grad_out.at[to, b], grad_t_ref.at[2 * g + b], o_send.at[b, away], o_recv.at[b, g], g=to)
        grad_t_ref[2 * g + b] = grad_out[g, b]

    norm(0)
    norm(1)
    for load in loads:
        load.wait()
    near = [near_pair(0), None]
    passed = [pass_on(0), None]
    near[1] = near_pair(1)
    far = [far_pair(0, passed[0]), None]
    passed[1] = pass_on(1)
    far[1] = far_pair(1, passed[1])

    def over_rows(left, right):
        total = None
        for b in range(2):
            for pair in range(2):
                term = outer(left(b, pair), right(b, pair))
                total = term if total is None else total + term
        return total.astype(bf16)

    def parts(write):
        for y in range(2):
            pl.when(r == y)(lambda: write(keep_ref, y))
            pl.when(r != y)(lambda: write(give_ref, y))

    down_grad = over_rows(lambda b, pair: hids[b, pair], lambda b, pair: pair_of(cots, b, pair))

    def write_down(ref, y):
        for z in range(GROUPS):
            p = y * GROUPS + z
            ref[z, 0:96] = down_grad[96 * p : 96 * p + 96]

    parts(write_down)
    back(0, near[0], far[0])
    up_grad = over_rows(lambda b, pair: pair_of(h2s, b, pair), lambda b, pair: dus[b, pair])

    def up_part(p, h):
        return up_grad[half * h + 48 * p : half * h + 48 * p + 48]

    def write_up(y, h):
        @pl.when((r == y) & (x == h))
        def _():
            for z in range(GROUPS):
                keep_ref[z, 96:144] = up_part(y * GROUPS + z, h)

        @pl.when((r != y) & (x == h))
        def _():
            for z in range(GROUPS):
                give_ref[z, 96:144] = up_part(y * GROUPS + z, h)

        @pl.when((r == y) & (x != h))
        def _():
            for z in range(GROUPS):
                x_give_ref[rows + 48 * z : rows + 48 * z + 48] = up_part(y * GROUPS + z, h)

        @pl.when((r != y) & (x != h))
        def _():
            for z in range(GROUPS):
                far_ref[z] = up_part(y * GROUPS + z, h)

    for y in range(2):
        for h in range(2):
            write_up(y, h)
    back(1, near[1], far[1])

    for owner in range(2):
        for c in range(2):
            piece = dot(attn_t[half * owner + fourth * c : half * owner + fourth * c + fourth], branch_ref[...])

            @pl.when(core == c)
            def _():
                wo_keep[owner] = piece

            @pl.when(core != c)
            def _():
                wo_give[owner] = piece.astype(bf16)

    w_sib = begin(wo_give, wo_in, w_send.at[0], w_recv.at[0], core=sib)
    y_sibs = [
        begin(part_y.at[b, 0, pl.ds(BLK, BLK)], in_y.at[b], y_send.at[b, 0], y_recv.at[b, 0], core=sib)
        for b in range(2)
    ]
    w_sib.wait_recv()
    wo_pass[...] = (wo_keep[other] + wo_in[other].astype(f32)).astype(bf16)
    w_x = begin(wo_pass, wo_x, w_send.at[1], w_recv.at[1], x=other)
    for b in range(2):
        y_passes[b].wait_recv()
        x_give_ref[rows_of(b)] = (part_y[b, 1, :BLK] + pass_y[b].astype(f32)).astype(bf16)
        y_sibs[b].wait_recv()
        base_ref[rows_of(b)] = mid_ref[b] + part_y[b, 0, :BLK] + in_y[b] + small_ref[5:6]
    mine = wo_keep[x] + wo_in[x].astype(f32)
    for b in range(2):
        for away in range(1, GROUPS):
            source = other_group(away)
            arrived(grad_t_ref.at[2 * source + b], o_send.at[b, away], o_recv.at[b, source], x)
    w_x.wait_recv()
    wo_sum = (mine + wo_x[...].astype(f32)).astype(bf16)

    def write_wo(ref, y):
        for z in range(GROUPS):
            p = y * GROUPS + z
            ref[z, 144:KEPT] = wo_sum[24 * p : 24 * p + 24]

    parts(write_wo)
    for move in pending:
        move.wait_send()


def dense(out_t, tokens, cot, cot_x, small, wo, up_mine, up_other, down):
    rows, width = tokens.shape
    dma = pltpu.SemaphoreType.DMA
    full = (rows, width)
    part = (BLK, width)
    pair = (2 * BLK, width)
    fourth = (width // 4, width)
    return pl.pallas_call(
        dense_kernel,
        out_shape=(
            jax.ShapeDtypeStruct(full, f32),
            jax.ShapeDtypeStruct((rows + 48 * GROUPS, width), bf16),
            jax.ShapeDtypeStruct(full, f32),
            jax.ShapeDtypeStruct(out_t.shape, bf16),
            jax.ShapeDtypeStruct((GROUPS, KEPT, width), bf16),
            jax.ShapeDtypeStruct((GROUPS, KEPT, width), bf16),
            jax.ShapeDtypeStruct((GROUPS, 48, width), bf16),
            jax.ShapeDtypeStruct(small.shape, f32),
        ),
        in_specs=[whole_vmem()] * 6 + [anywhere()] * 3,
        out_specs=(whole_vmem(),) * 8,
        scratch_shapes=[
            pltpu.VMEM((width, width), bf16),
            pltpu.VMEM((width, width), bf16),
            pltpu.VMEM((GROUPS, 2, HW, BLK), bf16),
            pltpu.VMEM((width, rows), bf16),
            pltpu.VMEM((2, 4, *part), bf16),
            pltpu.VMEM((2, 4, *part), bf16),
            pltpu.VMEM((2, *part), f32),
            pltpu.VMEM((2, *part), f32),
            pltpu.VMEM((2, BLK, 1), f32),
            pltpu.VMEM((2, 2, *pair), f32),
            pltpu.VMEM((2, 2, *pair), f32),
            pltpu.VMEM((2, *part), f32),
            pltpu.VMEM((2, *part), f32),
            pltpu.VMEM((2, *part), bf16),
            pltpu.VMEM((2, *part), bf16),
            pltpu.VMEM((2, *part), bf16),
            pltpu.VMEM((2, 3, *part), bf16),
            pltpu.VMEM((2, 2, *pair), bf16),
            pltpu.VMEM((2, 2, *pair), bf16),
            pltpu.VMEM(full, bf16),
            pltpu.VMEM((GROUPS, 2, HW, BLK), bf16),
            pltpu.VMEM((2, *fourth), f32),
            pltpu.VMEM((2, *fourth), bf16),
            pltpu.VMEM((2, *fourth), bf16),
            pltpu.VMEM(fourth, bf16),
            pltpu.VMEM(fourth, bf16),
            dma((3,)), dma((2, GROUPS)), dma((2, GROUPS)), dma((2,)), dma((2,)), dma((2, 3)), dma((2, 3)),
            dma((2, 2)), dma((2, 2)), dma((2, 3)), dma((2, 3)), dma((2, GROUPS)), dma((2, GROUPS)), dma((2,)), dma((2,)),
        ],
        compiler_params=pltpu.CompilerParams(
            collective_id=1, has_side_effects=True, vmem_limit_bytes=40 << 20
        ),
        name="dense",
    )(out_t, tokens, cot, cot_x, small, wo, up_mine, up_other, down)


FARTHEST = ((3, 2, 1, 0), (3, 0, 2, 1), (0, 3, 1, 2), (0, 1, 2, 3))


def farthest(g, step):
    picked = FARTHEST[0][step]
    for z in range(1, GROUPS):
        picked = jnp.where(g == z, FARTHEST[z][step], picked)
    return picked


class Chain:
    def __init__(self, g, x, total, parts, inward, outward, out_sem, in_sem):
        self.g, self.x, self.total, self.parts = g, x, total, parts
        self.inward, self.outward, self.out_sem, self.in_sem = inward, outward, out_sem, in_sem

    def move(self, to, way):
        return send(
            self.outward.at[to], self.inward.at[way, to], self.out_sem.at[to], self.in_sem.at[way, to],
            g=jnp.clip(self.g + (1 if way == 0 else -1), 0, GROUPS - 1),
        )

    def step(self, to):
        g = self.g
        self.total[...] = self.parts[to].astype(f32)

        def take(way):
            arrived(self.inward.at[way, to], self.out_sem.at[to], self.in_sem.at[way, to], self.x)
            self.total[...] += self.inward[way, to].astype(f32)

        pl.when((to >= g) & (g > 0))(lambda: take(0))
        pl.when((to <= g) & (g < GROUPS - 1))(lambda: take(1))

        @pl.when(to != g)
        def _():
            self.outward[to] = self.total[...].astype(bf16)

        pl.when(to > g)(lambda: self.move(to, 0).start())
        pl.when(to < g)(lambda: self.move(to, 1).start())

    def finish(self):
        for step in range(GROUPS - 1):
            to = farthest(self.g, step)
            left(self.outward.at[to], self.out_sem.at[to], self.in_sem.at[0, to], self.x)


class Ring:
    def __init__(self, g, x, slot, own_sem, out_sem, in_sem):
        self.g, self.x, self.slot = g, x, slot
        self.own_sem, self.out_sem, self.in_sem = own_sem, out_sem, in_sem

    def move(self, source, way, sem):
        return send(
            self.slot(source), self.slot(source), sem, self.in_sem.at[source],
            g=jnp.clip(self.g + way, 0, GROUPS - 1),
        )

    def start(self):
        g = self.g
        pl.when(g > 0)(lambda: self.move(g, -1, self.own_sem.at[0]).start())
        pl.when(g < GROUPS - 1)(lambda: self.move(g, 1, self.own_sem.at[1]).start())

    def step(self, step):
        g, source = self.g, nearest(self.g, step)
        arrived(self.slot(source), self.out_sem.at[source], self.in_sem.at[source], self.x)
        pl.when((source < g) & (g < GROUPS - 1))(lambda: self.move(source, 1, self.out_sem.at[source]).start())
        pl.when((source > g) & (g > 0))(lambda: self.move(source, -1, self.out_sem.at[source]).start())
        return source

    def finish(self):
        g = self.g
        for i, there in enumerate((g > 0, g < GROUPS - 1)):
            pl.when(there)(lambda: left(self.slot(g), self.own_sem.at[i], self.in_sem.at[g], self.x))
        for step in range(1, GROUPS):
            source = nearest(g, step)
            passed = ((source < g) & (g < GROUPS - 1)) | ((source > g) & (g > 0))
            pl.when(passed)(
                lambda: left(self.slot(source), self.out_sem.at[source], self.in_sem.at[source], self.x)
            )


def arrived(what, out_sem, in_sem, x):
    send(what, what, out_sem, in_sem, x=1 - x).wait_recv()


def left(what, out_sem, in_sem, x):
    send(what, what, out_sem, in_sem, x=1 - x).wait_send()


def scatter_kernel(
    dkv_ref, dq_any, normed_any, wfull_any, tokens_any, mgrad_any, keep_any, over_any, near_any, far_any, small_ref, sums_in,
    tokens_grad_ref, big_ref, qout_ref, kvout_ref, sums_ref,
    dq_ref, normed_ref, wfull_ref, tokens_ref, mgrad_ref, kept, over, near, far,
    own_kv, sib_kv, keep_x, give_x, in_x, give_y, in_y, part_a, total_a, inward_a, outward_a, wg_kv,
    by_sum, total_b, inward_b, outward_b, unit,
    q_keep, q_give, q_in, q_pass, q_x, q_y, q_sum, v_keep, v_give, v_in, v_pass, v_x, v_y, v_sum,
    sums_got, late, late_sum, late_got,
    load_sem, own_sem, k_send, k_recv, x_send, x_recv, y_send, y_recv, ca_send, ca_recv,
    cb_send, cb_recv, rb_own, rb_send, rb_recv,
    fy_send, fy_recv, fs_send, fs_recv,
    q_send, q_recv, rq_own, rq_send, rq_recv, qs_send, qs_recv,
    v_send, v_recv, rv_own, rv_send, rv_recv, vs_send, vs_recv,
    s_send, s_recv, t_send, t_recv, l_sem,
):
    g, r, core, x = place()
    other, sib, far_r = 1 - x, 1 - core, 1 - r
    rows, width = tokens_ref.shape
    half = width // 2
    fourth = half // 2
    wide_q = 2 * BLK
    loads = [
        pltpu.make_async_copy(what, where, load_sem.at[i])
        for i, (what, where) in enumerate(
            (
                (keep_any, kept), (over_any, over), (near_any.at[pl.ds(rows, 48 * GROUPS)], near), (far_any, far),
                (dq_any, dq_ref), (normed_any, normed_ref), (wfull_any, wfull_ref), (tokens_any, tokens_ref),
                (mgrad_any, mgrad_ref),
            )
        )
    ]
    for load in loads:
        load.start()
    greet(g, r, core, x, True, True)
    pending = []

    def begin(src, dst, out_sem, in_sem, **device):
        move = send(src, dst, out_sem, in_sem, **device)
        move.start()
        pending.append(move)
        return move

    def settled(move):
        move.wait_recv()
        move.wait_send()
        pending[:] = [item for item in pending if item is not move]

    kv_moves = []
    for i in range(GROUPS):
        c = farthest(g, i)
        for spot in range(4):
            own = pltpu.make_async_copy(
                dkv_ref.at[seat(spot // 2, core, spot % 2), c], own_kv.at[i, spot], own_sem.at[i, spot]
            )
            own.start()
            across = begin(
                dkv_ref.at[seat(spot // 2, sib, spot % 2), c], sib_kv.at[i, spot],
                k_send.at[i, spot], k_recv.at[i, spot], core=sib,
            )
            kv_moves.append((own, across))

    def split(total, keep, give):
        for owner in range(2):
            for c in range(2):
                low = half * owner + fourth * c
                chunk = total[low : low + fourth]

                @pl.when(core == c)
                def _():
                    keep[owner] = chunk

                @pl.when(core != c)
                def _():
                    give[owner] = chunk.astype(bf16)

    def scaled(c):
        return dq_ref[c] * bf16(SCALE)

    q_move = send(q_give, q_in, q_send.at[0], q_recv.at[0], core=sib)

    def query_grad():
        loads[4].wait()
        loads[5].wait()
        query_total = outer(normed_ref[0], scaled(0))
        for c in range(1, GROUPS):
            query_total += outer(normed_ref[c], scaled(c))
        split(query_total, q_keep, q_give)
        q_move.start()
        line_q = scaled(0).astype(f32)
        for c in range(1, GROUPS):
            line_q += scaled(c).astype(f32)
        sums_ref[pl.ds(16 + g, 1), 0:wide_q] = jnp.sum(line_q, axis=0, keepdims=True)

    sums_ref[...] = jnp.zeros_like(sums_ref)
    sums_ref[0:16] = sums_in[...]
    wg_kv[...] = jnp.zeros_like(wg_kv)

    def q_slot(z):
        return qout_ref.at[core, z]

    def v_slot(z):
        return kvout_ref.at[core, z]

    def b_slot(z):
        return big_ref.at[core, r, z]

    ring_q = Ring(g, x, q_slot, rq_own, rq_send, rq_recv)
    ring_v = Ring(g, x, v_slot, rv_own, rv_send, rv_recv)
    ring_b = Ring(g, x, b_slot, rb_own, rb_send, rb_recv)

    def store(value_ref, slot, sem):
        copy = pltpu.make_async_copy(value_ref, slot, sem)
        copy.start()
        copy.wait()

    def spread_b(z, step):
        begin(b_slot(z), b_slot(z), fy_send.at[step], fy_recv.at[step], r=far_r)
        begin(b_slot(z), b_slot(z), fs_send.at[0, step], fs_recv.at[0, step], core=sib)

    def spread_far(step):
        what = big_ref.at[core, far_r, nearest(g, step)]
        arrived(what, fy_send.at[step], fy_recv.at[step], x)
        begin(what, what, fs_send.at[1, step], fs_recv.at[1, step], core=sib)

    def on_ring_b(step):
        spread_b(ring_b.step(step), step)

    def on_ring_q(step):
        z = ring_q.step(step)
        begin(q_slot(z), q_slot(z), qs_send.at[step], qs_recv.at[step], core=sib)

    def on_ring_v(step):
        z = ring_v.step(step)
        begin(v_slot(z), v_slot(z), vs_send.at[step], vs_recv.at[step], core=sib)

    chain_a = Chain(g, x, total_a, part_a, inward_a, outward_a, ca_send, ca_recv)
    chain_b = Chain(g, x, total_b, by_sum, inward_b, outward_b, cb_send, cb_recv)
    at_end = (g == 0) | (g == GROUPS - 1)
    between = jnp.logical_not(at_end)

    def steps(chain, *which):
        for i in which:
            chain.step(farthest(g, i))

    def on_sibling(i):
        for own, across in kv_moves[4 * i : 4 * i + 4]:
            own.wait()
            across.wait_recv()

        def total(row, column):
            spot = 2 * row + column
            return own_kv[i, spot].astype(f32) + sib_kv[i, spot].astype(f32)

        for k in range(2):
            give_x[i, k] = (total(k, other) if i % 2 == 0 else total(far_r, k)).astype(bf16)
            keep_x[i, k] = total(k, x) if i % 2 == 0 else total(r, k)

    def go_first(i):
        along = {"x": other} if i % 2 == 0 else {"r": far_r}
        begin(give_x.at[i], in_x.at[i], x_send.at[i], x_recv.at[i], **along)

    def on_first(i):
        arrived(in_x.at[i], x_send.at[i], x_recv.at[i], x)
        away, stay, along = (far_r, r, {"r": far_r}) if i % 2 == 0 else (other, x, {"x": other})
        give_y[i] = (keep_x[i, away] + in_x[i, away].astype(f32)).astype(bf16)
        begin(give_y.at[i], in_y.at[i], y_send.at[i], y_recv.at[i], **along)
        keep_x[i, stay] += in_x[i, stay].astype(f32)

    def on_second(i):
        c = farthest(g, i)
        arrived(in_y.at[i], y_send.at[i], y_recv.at[i], x)
        both = (keep_x[i, r if i % 2 == 0 else x] + in_y[i].astype(f32)).astype(bf16)
        part_a[c] = inner(scaled(c), wfull_ref[:, :wide_q]) + inner(both, wfull_ref[:, wide_q:])
        wg_kv[...] += outer(normed_ref[c], both)
        sums_ref[pl.ds(16 + g, 1), wide_q : wide_q + 2 * HW] += jnp.sum(both.astype(f32), axis=0, keepdims=True)

    for load in loads[:4]:
        load.wait()
    own_up = pl.ds(pl.multiple_of(96 + 48 * x, 48), 48)
    their_up = pl.ds(pl.multiple_of(96 + 48 * other, 48), 48)
    for z in range(GROUPS):
        pair = kept[z].astype(f32) + over[z].astype(f32)
        by_sum[z, 0:96] = pair[0:96]
        by_sum[z, own_up] = pair[96:144]
        by_sum[z, 192:UNIT] = pair[144:KEPT]
        by_sum[z, their_up] = near[48 * z : 48 * z + 48].astype(f32) + far[z].astype(f32)
    pl.when(at_end)(lambda: steps(chain_b, 0, 1, 2))
    on_sibling(0)
    go_first(0)
    on_sibling(1)
    go_first(1)
    on_sibling(2)
    on_sibling(3)
    pl.when(between)(lambda: steps(chain_b, 0))
    query_grad()
    on_first(0)
    on_first(1)
    go_first(2)
    go_first(3)
    pl.when(between)(lambda: steps(chain_b, 1, 2))
    settled(q_move)
    q_pass[...] = (q_keep[other] + q_in[other].astype(f32)).astype(bf16)
    q_across = begin(q_pass, q_x, q_send.at[1], q_recv.at[1], x=other)
    loads[6].wait()
    on_second(0)
    on_second(1)
    pl.when(at_end)(lambda: steps(chain_a, 0))
    chain_b.step(g)
    unit[...] = total_b[...].astype(bf16)
    store(unit, b_slot(g), l_sem.at[0])
    ring_b.start()
    spread_b(g, 0)
    pl.when(at_end)(lambda: steps(chain_a, 1))
    on_first(2)
    on_first(3)
    q_across.wait_recv()
    q_sum[...] = (q_keep[x] + q_in[x].astype(f32) + q_x[...].astype(f32)).astype(bf16)
    q_over = begin(q_sum, q_y, q_send.at[2], q_recv.at[2], r=far_r)
    pl.when(between)(lambda: steps(chain_a, 0))
    on_second(2)
    on_second(3)
    pl.when(at_end)(lambda: steps(chain_a, 2))
    split(wg_kv, v_keep, v_give)
    v_move = begin(v_give, v_in, v_send.at[0], v_recv.at[0], core=sib)
    s_sib = begin(sums_ref, sums_got.at[0], s_send.at[0], s_recv.at[0], core=sib)
    spread_far(0)
    settled(q_over)
    q_sum[...] = (q_sum[...].astype(f32) + q_y[...].astype(f32)).astype(bf16)
    store(q_sum, q_slot(g), l_sem.at[0])
    ring_q.start()
    begin(q_slot(g), q_slot(g), qs_send.at[0], qs_recv.at[0], core=sib)
    on_ring_b(1)
    v_move.wait_recv()
    v_pass[...] = (v_keep[other] + v_in[other].astype(f32)).astype(bf16)
    v_across = begin(v_pass, v_x, v_send.at[1], v_recv.at[1], x=other)
    settled(s_sib)
    sums_ref[...] += sums_got[0]
    s_x = begin(sums_ref, sums_got.at[1], s_send.at[1], s_recv.at[1], x=other)
    pl.when(between)(lambda: steps(chain_a, 1))
    v_across.wait_recv()
    v_sum[...] = (v_keep[x] + v_in[x].astype(f32) + v_x[...].astype(f32)).astype(bf16)
    v_over = begin(v_sum, v_y, v_send.at[2], v_recv.at[2], r=far_r)
    settled(s_x)
    sums_ref[...] += sums_got[1]
    s_y = begin(sums_ref, sums_got.at[2], s_send.at[2], s_recv.at[2], r=far_r)
    on_ring_b(2)
    pl.when(between)(lambda: steps(chain_a, 2))
    settled(v_over)
    v_sum[...] = (v_sum[...].astype(f32) + v_y[...].astype(f32)).astype(bf16)
    store(v_sum, v_slot(g), l_sem.at[0])
    ring_v.start()
    begin(v_slot(g), v_slot(g), vs_send.at[0], vs_recv.at[0], core=sib)
    settled(s_y)
    sums_ref[...] += sums_got[2]
    for away in range(1, GROUPS):
        begin(
            sums_ref, sums_got.at[2 + away], s_send.at[2 + away], s_recv.at[2 + away],
            g=lax.rem(g + away, GROUPS),
        )
    spread_far(1)
    on_ring_q(1)
    on_ring_b(3)
    chain_a.step(g)

    loads[7].wait()
    loads[8].wait()
    grad_first = total_a[...]
    values = tokens_ref[...].astype(f32)
    mean = jnp.mean(values, axis=-1, keepdims=True)
    centred = values - mean
    scale = lax.rsqrt(jnp.mean(centred * centred, axis=-1, keepdims=True) + EPS)
    n1 = centred * scale
    pulled = grad_first * small_ref[0:1]
    inward = pulled - jnp.mean(pulled, axis=-1, keepdims=True) - n1 * jnp.mean(pulled * n1, axis=-1, keepdims=True)
    tokens_grad_ref[...] = mgrad_ref[...] + inward * scale
    late[...] = jnp.zeros_like(late)
    late[0:1] = jnp.sum(grad_first * n1, axis=0, keepdims=True)
    late[1:2] = jnp.sum(grad_first, axis=0, keepdims=True)
    for step in range(len(AROUND)):
        begin(late, late_got.at[step], t_send.at[step], t_recv.at[step], **neighbour(r, core, x, step))
    on_ring_v(1)
    on_ring_q(2)
    on_ring_q(3)
    spread_far(2)
    on_ring_v(2)
    late_sum[...] = late[...]
    for step in range(len(AROUND)):
        arrived(late_got.at[step], t_send.at[step], t_recv.at[step], x)
        late_sum[...] += late_got[step]
    first_z = len(AROUND) - 1
    for away in range(1, GROUPS):
        begin(
            late_sum, late_got.at[first_z + away], t_send.at[first_z + away], t_recv.at[first_z + away],
            g=lax.rem(g + away, GROUPS),
        )
    on_ring_v(3)
    spread_far(3)

    for away in range(1, GROUPS):
        arrived(sums_got.at[2 + away], s_send.at[2 + away], s_recv.at[2 + away], x)
        arrived(late_got.at[first_z + away], t_send.at[first_z + away], t_recv.at[first_z + away], x)
    for step in range(GROUPS):
        z = nearest(g, step)
        arrived(qout_ref.at[sib, z], qs_send.at[step], qs_recv.at[step], x)
        arrived(kvout_ref.at[sib, z], vs_send.at[step], vs_recv.at[step], x)
        arrived(big_ref.at[sib, r, z], fs_send.at[0, step], fs_recv.at[0, step], x)
        arrived(big_ref.at[sib, far_r, z], fs_send.at[1, step], fs_recv.at[1, step], x)
    for move in pending:
        move.wait_send()
    for item in (chain_a, chain_b, ring_q, ring_v, ring_b):
        item.finish()
    sums_ref[...] += sums_got[3] + sums_got[4] + sums_got[5]
    total = late_sum[...] + late_got[first_z + 1] + late_got[first_z + 2] + late_got[first_z + 3]
    sums_ref[0:2] = total[0:2]


def scatter(dkv, dq, normed, wfull, tokens, mgrad, small, keep, over, near, far, sums):
    rows, width = tokens.shape
    fourth = width // 4
    dma = pltpu.SemaphoreType.DMA
    wide_q, wide_v = 2 * BLK, 2 * HW
    kv_block = (rows, wide_v)
    full = (rows, width)
    unit = (UNIT, width)

    def weight_scratch(wide):
        return [
            pltpu.VMEM((2, fourth, wide), f32),
            pltpu.VMEM((2, fourth, wide), bf16),
            pltpu.VMEM((2, fourth, wide), bf16),
            *[pltpu.VMEM((fourth, wide), bf16)] * 4,
        ]

    return pl.pallas_call(
        scatter_kernel,
        out_shape=(
            jax.ShapeDtypeStruct(full, f32),
            jax.ShapeDtypeStruct((2, 2, GROUPS, *unit), bf16),
            jax.ShapeDtypeStruct((2, GROUPS, fourth, wide_q), bf16),
            jax.ShapeDtypeStruct((2, GROUPS, fourth, wide_v), bf16),
            jax.ShapeDtypeStruct((24, width), f32),
        ),
        in_specs=[anywhere()] * 10 + [whole_vmem()] * 2,
        out_specs=(whole_vmem(), anywhere(), anywhere(), anywhere(), whole_vmem()),
        scratch_shapes=[
            *[
                pltpu.VMEM(item.shape, item.dtype)
                for item in (dq, normed, wfull, tokens, mgrad, keep, over)
            ],
            pltpu.VMEM((48 * GROUPS, width), bf16),
            pltpu.VMEM(far.shape, bf16),
            pltpu.VMEM((GROUPS, 4, *kv_block), bf16),
            pltpu.VMEM((GROUPS, 4, *kv_block), bf16),
            pltpu.VMEM((GROUPS, 2, *kv_block), f32),
            pltpu.VMEM((GROUPS, 2, *kv_block), bf16),
            pltpu.VMEM((GROUPS, 2, *kv_block), bf16),
            pltpu.VMEM((GROUPS, *kv_block), bf16),
            pltpu.VMEM((GROUPS, *kv_block), bf16),
            pltpu.VMEM((GROUPS, *full), f32),
            pltpu.VMEM(full, f32),
            pltpu.VMEM((2, GROUPS, *full), bf16),
            pltpu.VMEM((GROUPS, *full), bf16),
            pltpu.VMEM((width, wide_v), f32),
            pltpu.VMEM((GROUPS, *unit), f32),
            pltpu.VMEM(unit, f32),
            pltpu.VMEM((2, GROUPS, *unit), bf16),
            pltpu.VMEM((GROUPS, *unit), bf16),
            pltpu.VMEM(unit, bf16),
            *weight_scratch(wide_q),
            *weight_scratch(wide_v),
            pltpu.VMEM((6, 24, width), f32),
            pltpu.VMEM((8, width), f32),
            pltpu.VMEM((8, width), f32),
            pltpu.VMEM((len(AROUND) + GROUPS - 1, 8, width), f32),
            dma((9,)),
            dma((GROUPS, 4)), dma((GROUPS, 4)), dma((GROUPS, 4)), dma((GROUPS,)), dma((GROUPS,)), dma((GROUPS,)), dma((GROUPS,)),
            dma((GROUPS,)), dma((2, GROUPS)),
            dma((GROUPS,)), dma((2, GROUPS)), dma((2,)), dma((GROUPS,)), dma((GROUPS,)),
            dma((GROUPS,)), dma((GROUPS,)), dma((2, GROUPS)), dma((2, GROUPS)),
            dma((3,)), dma((3,)), dma((2,)), dma((GROUPS,)), dma((GROUPS,)), dma((GROUPS,)), dma((GROUPS,)),
            dma((3,)), dma((3,)), dma((2,)), dma((GROUPS,)), dma((GROUPS,)), dma((GROUPS,)), dma((GROUPS,)),
            dma((6,)), dma((6,)), dma((10,)), dma((10,)), dma((1,)),
        ],
        compiler_params=pltpu.CompilerParams(
            collective_id=2, has_side_effects=True, vmem_limit_bytes=54 << 20
        ),
        name="scatter",
    )(dkv, dq, normed, wfull, tokens, mgrad, keep, over, near, far, small, sums)


def pack_kv(key_part, value_part):
    return jnp.concatenate(
        [key_part, value_part[..., 2 * DH :], value_part[..., : 2 * DH]], axis=-1
    )


def unpack_kv(both):
    return both[..., :HW], jnp.concatenate([both[..., HW + DH :], both[..., HW : HW + DH]], axis=-1)


def layout_kernel(
    big_ref, query_ref, kv_ref, sums_ref, base_ref, got_ref,
    up_out, down_out, wo_out, query_out, key_out, value_out,
    low_gain, low_shift, query_bias, value_bias, out_bias, high_gain, high_shift, up_bias, down_bias, result_out,
):
    x = lax.axis_index("x")
    width = big_ref.shape[-1]
    half = width // 2
    result_out[...] = (base_ref[...] + got_ref[...].astype(f32)).astype(bf16)
    for core in range(2):
        down_out[core] = big_ref[core, 0, 0:96].astype(f32)
        wo_out[core] = big_ref[core, 0, 192:UNIT].astype(f32)
        for owner in range(2):
            lane = (2 * owner + core) * width
            up_out[:, lane : lane + width] = big_ref[core, 0, 96 + 48 * owner : 144 + 48 * owner].astype(f32)
        query_out[core] = jnp.concatenate(
            [query_ref[core, z].astype(f32)[:, :HW] for z in range(GROUPS)], axis=1
        )
        both = [unpack_kv(kv_ref[core, z].astype(f32)) for z in range(GROUPS)]
        key_out[core] = jnp.concatenate([item[0] for item in both], axis=1)
        value_out[core] = jnp.concatenate([item[1] for item in both], axis=1)

    @pl.when(pl.program_id(0) == 0)
    def _():
        def own_half(row):
            whole = sums_ref[row : row + 1]
            return jnp.where(x == 0, whole[:, :half], whole[:, half:]).reshape(half)

        for ref, row in (
            (low_gain, 0), (low_shift, 1), (out_bias, 2), (high_gain, 3), (high_shift, 4), (down_bias, 5),
        ):
            ref[...] = own_half(row)
        pair = [sums_ref[pl.ds(16 + 2 * x + i, 1)] for i in range(2)]
        query_bias[...] = jnp.concatenate([item[:, :HW] for item in pair], axis=1).reshape(half)
        value_bias[...] = jnp.concatenate(
            [unpack_kv(item[:, 2 * BLK : 2 * BLK + 2 * HW])[1] for item in pair], axis=1
        ).reshape(half)
        up_bias[...] = jnp.concatenate(
            [sums_ref[pl.ds(8 + 2 * x + i, 1)] for i in range(2)], axis=1
        ).reshape(2 * width)


def lay_out(big, query, kv, sums, base, got):
    width = big.shape[-1]
    half, fourth = width // 2, width // 4
    rows = fourth // PARTS

    def spec(shape, index):
        return pl.BlockSpec(shape, index)

    def fixed(wide):
        return pl.BlockSpec((wide,), lambda p: (0,))

    narrow = spec((2, rows, width), lambda p: (0, p, 0))
    vector = jax.ShapeDtypeStruct((half,), f32)
    return pl.pallas_call(
        layout_kernel,
        grid=(PARTS,),
        out_shape=(
            jax.ShapeDtypeStruct((half, 4 * width), f32),
            jax.ShapeDtypeStruct((2, width, width), f32),
            *[jax.ShapeDtypeStruct((2, fourth, width), f32)] * 4,
            *[vector] * 7,
            jax.ShapeDtypeStruct((2 * width,), f32),
            vector,
            jax.ShapeDtypeStruct(base.shape, bf16),
        ),
        in_specs=[
            spec((2, 1, UNIT, width), lambda p: (0, p, 0, 0)),
            spec((2, GROUPS, rows, query.shape[-1]), lambda p: (0, 0, p, 0)),
            spec((2, GROUPS, rows, kv.shape[-1]), lambda p: (0, 0, p, 0)),
            spec(sums.shape, lambda p: (0, 0)),
            spec((base.shape[0] // PARTS, width), lambda p: (p, 0)),
            spec((base.shape[0] // PARTS, width), lambda p: (p, 0)),
        ],
        out_specs=(
            spec((48, 4 * width), lambda p: (p, 0)),
            spec((2, 96, width), lambda p: (0, p, 0)),
            *[narrow] * 4,
            *[fixed(half)] * 7,
            fixed(2 * width),
            fixed(half),
            spec((base.shape[0] // PARTS, width), lambda p: (p, 0)),
        ),
        compiler_params=pltpu.CompilerParams(
            vmem_limit_bytes=VMEM_LIMIT, dimension_semantics=("arbitrary",)
        ),
        name="lay_out",
    )(big, query, kv, sums, base, got)


ROWS = ("s", "r", "core", "x")
ALL = ("g", "s", "r", "core", "x")


def shards(
    tokens, cotangent, doc_lengths, deal, first_gain, first_shift, query_weight, query_bias,
    key_weight, value_weight, value_bias, output_weight, output_bias, second_gain, second_shift,
    up_weight, up_bias, down_weight, down_bias,
):
    rows, width = tokens.shape
    half = width // 2
    blocks = deal.shape[0]
    core, x = lax.axis_index("core"), lax.axis_index("x")
    swap = ((0, 1), (1, 0))

    def up_columns(owner):
        return lax.dynamic_slice_in_dim(up_weight, (2 * owner + core) * width, width, 1)

    def stay(*items):
        return tuple(pltpu.with_memory_space_constraint(item, pltpu.HBM) for item in items)

    kv, q, normed, small, wfull, wo = gather(
        *stay(
            tokens, query_weight, key_weight, value_weight, output_weight,
            first_gain, first_shift, output_bias, second_gain, second_shift, down_bias, query_bias, value_bias, up_bias,
        )
    )
    wide = blocks > 8 * 2 * GROUPS
    if wide:
        kv = lax.all_gather(kv, "s", axis=0, tiled=True)
    kv = kv.reshape(blocks, BLK, 2 * HW)
    q = q.reshape(2 * GROUPS, BLK, 2 * BLK)
    cot_x, up_other, kv = lax.optimization_barrier((cotangent, up_columns(1 - x), kv))
    up_other = lax.ppermute(up_other, "x", swap)
    cot_x = lax.ppermute(cot_x, "x", swap)
    out_t, kept, lse = attend_forward(deal, doc_lengths, q, kv)
    base, x_give, grad_middle, grad_t, kept_part, over, far, sums = dense(
        out_t, tokens, cotangent, cot_x, small, wo, up_columns(x), up_other, down_weight
    )
    over = lax.ppermute(over, "r", swap)
    x_got = lax.ppermute(x_give, "x", swap)
    far = lax.ppermute(far, ("r", "x"), ((0, 3), (1, 2), (2, 1), (3, 0)))
    dq, dkv = attend_backward(deal, doc_lengths, q, kv, lse, grad_t, kept)
    dkv = dkv.reshape(-1, GROUPS, rows, 2 * HW)
    if wide:
        dkv = lax.psum_scatter(dkv, "s", scatter_dimension=0, tiled=True)
    dq = dq.reshape(GROUPS, rows, 2 * BLK)
    grad_tokens, big, query_own, kv_own, sums = scatter(
        *stay(dkv, dq, normed, wfull, tokens, grad_middle), small, *stay(kept_part, over, x_got, far), sums
    )
    if wide:
        big, query_own, kv_own, sums = (
            lax.psum(item, "s") for item in (big, query_own, kv_own, sums)
        )

    (
        up_own, down_own, wo_own, query_own, key_own, value_own,
        low_gain, low_shift, query_sum, value_sum, out_sum, high_gain, high_shift, up_sum, down_sum, result,
    ) = lay_out(big.reshape(2, PARTS, UNIT, width), query_own, kv_own, sums, *stay(base, x_got))

    def flat(item):
        return item.reshape(-1, width)

    return (
        result,
        grad_tokens,
        low_gain,
        low_shift,
        flat(query_own),
        query_sum,
        flat(key_own),
        flat(value_own),
        value_sum,
        flat(wo_own),
        out_sum,
        high_gain,
        high_shift,
        up_own,
        up_sum,
        flat(down_own),
        down_sum,
    )


def solution(mesh):
    devices = mesh.devices
    inner_mesh = Mesh(devices.reshape(GROUPS, devices.shape[0] // (4 * GROUPS), 2, 2, 2), ALL)
    row = P(ALL, None)
    mat = P("x", None)
    vec = P("x")
    in_specs = (
        row, row, P(), P(), vec, vec, mat, vec, mat, mat, vec, mat, vec, vec, vec, mat, vec, mat, vec,
    )
    out_specs = (
        row, row, vec, vec, mat, vec, mat, mat, vec, mat, vec, vec, vec, mat, vec, mat, vec,
    )
    return jax.shard_map(
        shards, mesh=inner_mesh, in_specs=in_specs, out_specs=out_specs, check_vma=False
    )
```

```python
import jax
import jax.numpy as jnp
from jax import lax
from jax.experimental import pallas as pl
from jax.experimental.pallas import tpu as pltpu
from jax.sharding import Mesh
from jax.sharding import PartitionSpec as P

HEADS = 12
DH = 64
NSUM = 50
SEG = 2048
BLK = 128
GROUPS = 4
PER = HEADS // GROUPS
HW = PER * DH
WIDE = PER * BLK
CHUNK = 2 * BLK
DEPTH = 8
EPS = 1e-05
SCALE = 0.125
MASKED = -1e30
ROOT_HALF = 0.7071067811865476
PDF_SCALE = 0.3989422804014327
VMEM_LIMIT = 56 << 20
bf16 = jnp.bfloat16
f32 = jnp.float32


def layer_norm(values, gain, shift):
    mean = jnp.mean(values, axis=-1, keepdims=True)
    centred = values - mean
    spread = jnp.mean(centred * centred, axis=-1, keepdims=True)
    return centred * lax.rsqrt(spread + EPS) * gain + shift


def outer(left, right):
    return lax.dot_general(left, right, (((0,), (0,)), ((), ())), preferred_element_type=f32)


def inner(left, right):
    return lax.dot_general(left, right, (((1,), (1,)), ((), ())), preferred_element_type=f32)


def dot(left, right):
    return jnp.dot(left, right, preferred_element_type=f32)


def survey(deal_ref, lengths_ref, where_ref, text_ref, low_ref, high_ref, first_ref):
    blocks = deal_ref.shape[0]
    per_group = blocks // (2 * GROUPS)
    rest = lax.axis_index(ROWS)

    def note(j, kept):
        pair = j // 2
        group = pair // per_group
        where_ref[deal_ref[j]] = ((pair - group * per_group) * GROUPS + group) * 2 + j % 2
        return kept

    lax.fori_loop(0, blocks, note, 0)
    starts = [jnp.int32(0)]
    for doc in range(lengths_ref.shape[0] - 1):
        starts.append(starts[-1] + lengths_ref[doc])

    def first_of(at):
        begin = jnp.zeros_like(at)
        for start in starts:
            begin = jnp.where(start <= at, jnp.maximum(begin, start), begin)
        return jnp.where(at - begin >= SEG + NSUM, begin + SEG, begin)

    for slot in range(2 * GROUPS):
        text = deal_ref[2 * ((slot // 2) * per_group + rest) + slot % 2]
        text_ref[slot] = text
        low_ref[slot] = first_of(text * BLK) // CHUNK
        high_ref[slot] = text // 2
        first_ref[slot] = first_of(text * BLK + lax.broadcasted_iota(jnp.int32, (1, BLK), 1))


def survey_scratch(blocks):
    slots = 2 * GROUPS
    return [
        pltpu.SMEM((blocks,), jnp.int32),
        pltpu.SMEM((slots,), jnp.int32),
        pltpu.SMEM((slots,), jnp.int32),
        pltpu.SMEM((slots,), jnp.int32),
        pltpu.VMEM((slots, 1, BLK), jnp.int32),
    ]


def spread_heads_t(part_t, order):
    rows = []
    zero = jnp.zeros((DH, BLK), part_t.dtype)
    for head in order:
        if head is None:
            rows.append(jnp.zeros((DH, WIDE), part_t.dtype))
        else:
            piece = part_t[DH * head : DH * head + DH]
            rows.append(
                jnp.concatenate([piece if h == head else zero for h in range(PER)], axis=1)
            )
    return jnp.concatenate(rows, axis=0)


K_ORDER = (0, 1, 2, None)
V_ORDER = (None, 2, 0, 1)


def visible(chunk, first, own):
    at = chunk * CHUNK + lax.broadcasted_iota(jnp.int32, (CHUNK, BLK), 0)
    allowed = (at >= first) & (at <= own)
    return jnp.concatenate([allowed] * PER, axis=1)


def load_chunk(kv_ref, where_ref, chunk):
    return jnp.concatenate(
        [kv_ref[where_ref[2 * chunk]], kv_ref[where_ref[2 * chunk + 1]]], axis=0
    )


def forward_kernel(
    deal_ref, lengths_ref, q_ref, kv_ref,
    out_ref, wide_ref, lse_ref,
    where_ref, text_ref, low_ref, high_ref, first_ref, acc_ref,
):
    survey(deal_ref, lengths_ref, where_ref, text_ref, low_ref, high_ref, first_ref)

    def one_slot(slot, kept):
        wide_q = spread_heads_t(q_ref[slot].T[:HW], K_ORDER)
        first = first_ref[slot]
        own = text_ref[slot] * BLK + lax.broadcasted_iota(jnp.int32, (1, BLK), 1)
        last_first = jnp.max(first)
        acc_ref[...] = jnp.zeros_like(acc_ref)

        def step(double, carry):
            top, total = carry
            scores = []
            for part in range(2):
                keys = load_chunk(kv_ref, where_ref, 2 * double + part)[:, : 2 * BLK]
                scores.append(jnp.where(visible(2 * double + part, first, own), dot(keys, wide_q), MASKED))
            scores = jnp.concatenate(scores, axis=0)
            fresh = jnp.maximum(top, jnp.max(scores, axis=0, keepdims=True))
            expo = jnp.exp(scores - fresh)
            shrink = jnp.exp(top - fresh)
            total = total * shrink + jnp.sum(expo, axis=0, keepdims=True)
            vals = jnp.concatenate([load_chunk(kv_ref, where_ref, 2 * double + part)[:, BLK:] for part in range(2)], axis=0)
            acc_ref[...] = acc_ref[...] * shrink + outer(vals, expo.astype(bf16))
            return fresh, total

        top, total = lax.fori_loop(
            low_ref[slot] // 2,
            high_ref[slot] // 2 + 1,
            step,
            (jnp.full((1, WIDE), MASKED, f32), jnp.zeros((1, WIDE), f32)),
        )
        lse_ref[slot] = top + jnp.log(total)
        scaled = acc_ref[...] / total
        pieces = []
        for head in range(PER):
            row = DH * V_ORDER.index(head)
            pieces.append(scaled[row : row + DH, BLK * head : BLK * head + BLK])
        whole = jnp.concatenate(pieces, axis=0)
        wide_ref[slot] = whole
        out_ref[slot] = whole.astype(bf16)
        return kept

    lax.fori_loop(0, q_ref.shape[0], one_slot, 0)


def whole_vmem():
    return pl.BlockSpec(memory_space=pltpu.VMEM)


def whole_smem():
    return pl.BlockSpec(memory_space=pltpu.SMEM)


def attend_forward(deal, lengths, q, kv):
    slots = q.shape[0]
    blocks = kv.shape[0]
    return pl.pallas_call(
        forward_kernel,
        out_shape=(
            jax.ShapeDtypeStruct((slots, HW, BLK), bf16),
            jax.ShapeDtypeStruct((slots, HW, BLK), f32),
            jax.ShapeDtypeStruct((slots, 1, WIDE), f32),
        ),
        in_specs=[whole_smem()] * 2 + [whole_vmem()] * 2,
        out_specs=(whole_vmem(),) * 3,
        scratch_shapes=[
            *survey_scratch(blocks),
            pltpu.VMEM((2 * BLK, WIDE), f32),
        ],
        compiler_params=pltpu.CompilerParams(vmem_limit_bytes=(6 << 20) + kv.size // 5 * 16),
        name="attend_forward",
    )(deal, lengths, q, kv)


def backward_kernel(
    deal_ref, lengths_ref, q_ref, kv_ref, lse_ref, do_ref, wide_ref,
    dq_ref, dkv_ref, where_ref, text_ref, low_ref, high_ref, first_ref, qt_ref, qm_ref, dot_ref, dom_ref, delta_ref, acc_ref, dk_acc, dv_acc,
    packed_ref, count_ref, list_ref, out_sem,
):
    survey(deal_ref, lengths_ref, where_ref, text_ref, low_ref, high_ref, first_ref)
    slots = q_ref.shape[0]
    chunks = kv_ref.shape[0] // 2

    def ready(slot, _):
        q = q_ref[slot]
        qt_ref[slot] = spread_heads_t(q.T[:HW], K_ORDER)
        lane = lax.broadcasted_iota(jnp.int32, (BLK, 2 * BLK), 1) // DH
        zero = jnp.zeros_like(q)
        qm_ref[slot] = jnp.concatenate(
            [jnp.where(lane == K_ORDER.index(h), q, zero) for h in range(PER)], axis=0
        )
        grad_t = do_ref[slot]
        dot_ref[slot] = spread_heads_t(grad_t, V_ORDER)
        ordered = jnp.concatenate(
            [
                jnp.zeros((DH, BLK), bf16) if h is None else grad_t[DH * h : DH * h + DH]
                for h in V_ORDER
            ],
            axis=0,
        ).T
        dom_ref[slot] = jnp.concatenate(
            [jnp.where(lane == V_ORDER.index(h), ordered, zero) for h in range(PER)], axis=0
        )
        both = grad_t.astype(f32) * wide_ref[slot]
        delta_ref[slot] = jnp.concatenate(
            [jnp.sum(both[DH * h : DH * h + DH], axis=0, keepdims=True) for h in range(PER)],
            axis=1,
        )
        acc_ref[slot] = jnp.zeros((HW, WIDE), f32)
        return _

    lax.fori_loop(0, slots, ready, 0)

    def clear(chunk, kept):
        count_ref[chunk] = 0
        return kept

    lax.fori_loop(0, chunks, clear, 0)

    def enlist(slot, kept):
        def seen(chunk, kept):
            count = count_ref[chunk]
            list_ref[chunk * slots + count] = slot
            count_ref[chunk] = count + 1
            return kept

        lax.fori_loop(low_ref[slot], high_ref[slot] + 1, seen, 0)
        return kept

    lax.fori_loop(0, slots, enlist, 0)

    def written(chunk, i):
        return pltpu.make_async_copy(
            packed_ref.at[chunk % DEPTH, i], dkv_ref.at[where_ref[2 * chunk + i]], out_sem.at[chunk % DEPTH, i]
        )

    def one_chunk(chunk, kept):
        part = load_chunk(kv_ref, where_ref, chunk)
        keys = part[:, : 2 * BLK]
        vals = part[:, BLK:]
        keys_t = keys.T[:HW]
        dk_acc[...] = jnp.zeros_like(dk_acc)
        dv_acc[...] = jnp.zeros_like(dv_acc)

        def one_slot(i, kept):
            for half in range(2):
                attend(list_ref[chunk * slots + 2 * i + half])
            return kept

        def attend(slot):
            own = text_ref[slot] * BLK + lax.broadcasted_iota(jnp.int32, (1, BLK), 1)
            scores = dot(keys, qt_ref[slot])
            dprobs = dot(vals, dot_ref[slot])
            probs = jnp.where(visible(chunk, first_ref[slot], own), jnp.exp(scores - lse_ref[slot]), 0.0)
            dscores = (probs * (dprobs - delta_ref[slot])).astype(bf16)
            dv_acc[...] += dot(probs.astype(bf16), dom_ref[slot])
            dk_acc[...] += dot(dscores, qm_ref[slot])
            acc_ref[slot] += dot(keys_t, dscores)

        lax.fori_loop(0, count_ref[chunk] // 2, one_slot, 0)
        pl.when(count_ref[chunk] % 2 == 1)(lambda: attend(list_ref[chunk * slots + count_ref[chunk] - 1]))
        packed = jnp.concatenate(
            [
                dk_acc[:, :BLK],
                dk_acc[:, BLK:] + dv_acc[:, :BLK],
                dv_acc[:, BLK:],
            ],
            axis=1,
        ).astype(bf16)

        @pl.when(chunk >= DEPTH)
        def _():
            for i in range(2):
                written(chunk - DEPTH, i).wait()

        for i in range(2):
            packed_ref[chunk % DEPTH, i] = packed[BLK * i : BLK * i + BLK]
            written(chunk, i).start()
        return kept

    lax.fori_loop(0, chunks, one_chunk, 0)
    for last in range(DEPTH):
        for i in range(2):
            written(chunks - DEPTH + last, i).wait()

    def finish(slot, _):
        total = acc_ref[slot]
        kept = jnp.concatenate(
            [total[DH * h : DH * h + DH, BLK * h : BLK * h + BLK] for h in range(PER)]
            + [jnp.zeros((DH, BLK), f32)],
            axis=0,
        )
        dq_ref[slot] = kept.T.astype(bf16)
        return _

    lax.fori_loop(0, slots, finish, 0)


def attend_backward(deal, lengths, q, kv, lse, grad_t, wide):
    slots = q.shape[0]
    return pl.pallas_call(
        backward_kernel,
        out_shape=(
            jax.ShapeDtypeStruct((slots, BLK, 2 * BLK), bf16),
            jax.ShapeDtypeStruct(kv.shape, bf16),
        ),
        in_specs=[whole_smem()] * 2 + [whole_vmem()] * 5,
        out_specs=(whole_vmem(), in_hbm()),
        scratch_shapes=[
            *survey_scratch(kv.shape[0]),
            pltpu.VMEM((slots, 2 * BLK, WIDE), bf16),
            pltpu.VMEM((slots, WIDE, 2 * BLK), bf16),
            pltpu.VMEM((slots, 2 * BLK, WIDE), bf16),
            pltpu.VMEM((slots, WIDE, 2 * BLK), bf16),
            pltpu.VMEM((slots, 1, WIDE), f32),
            pltpu.VMEM((slots, HW, WIDE), f32),
            pltpu.VMEM((CHUNK, 2 * BLK), f32),
            pltpu.VMEM((CHUNK, 2 * BLK), f32),
            pltpu.VMEM((DEPTH, 2, BLK, 2 * HW), bf16),
            pltpu.SMEM((kv.shape[0] // 2,), jnp.int32),
            pltpu.SMEM((kv.shape[0] // 2 * slots,), jnp.int32),
            pltpu.SemaphoreType.DMA((DEPTH, 2)),
        ],
        compiler_params=pltpu.CompilerParams(
            vmem_limit_bytes=max(46 << 20, (17 << 20) + kv.size * 2)
        ),
        name="attend_backward",
    )(deal, lengths, q, kv, lse, grad_t, wide)


MESH = pl.DeviceIdType.MESH


def send(src, dst, out_sem, in_sem, **device):
    return pltpu.make_async_remote_copy(
        src_ref=src, dst_ref=dst, send_sem=out_sem, recv_sem=in_sem, device_id=device, device_id_type=MESH
    )


def place():
    return tuple(lax.axis_index(name) for name in ("g", "r", "core", "x"))


def seat(r, core, x):
    return (r * 2 + core) * 2 + x


AROUND = ((0, 0, 1), (0, 1, 0), (0, 1, 1), (1, 0, 0), (1, 0, 1), (1, 1, 0), (1, 1, 1))


def neighbour(r, core, x, step):
    dr, dc, dx = AROUND[step]
    return {"r": 1 - r if dr else r, "core": 1 - core if dc else core, "x": 1 - x if dx else x}


def greet(g, r, core, x, line, around=False):
    barrier = pltpu.get_barrier_semaphore()

    def hello(**device):
        pl.semaphore_signal(barrier, inc=1, device_id=device, device_id_type=MESH)

    if around:
        for step in range(len(AROUND)):
            hello(**neighbour(r, core, x, step))
    else:
        hello(core=1 - core)
        hello(x=1 - x)
        hello(r=1 - r)
    near = len(AROUND) if around else 3
    if line:
        for away in range(1, GROUPS):
            hello(g=lax.rem(g + away, GROUPS))
        pl.semaphore_wait(barrier, near + GROUPS - 1)
    else:
        pl.when(g > 0)(lambda: hello(g=g - 1))
        pl.when(g < GROUPS - 1)(lambda: hello(g=g + 1))
        pl.semaphore_wait(barrier, near + 2 - jnp.where(g == 0, 1, 0) - jnp.where(g == GROUPS - 1, 1, 0))


NEAREST = ((0, 1, 2, 3), (1, 2, 0, 3), (2, 1, 3, 0), (3, 2, 1, 0))


def nearest(g, step):
    picked = NEAREST[0][step]
    for z in range(1, GROUPS):
        picked = jnp.where(g == z, NEAREST[z][step], picked)
    return picked


def prepare(g, x, weights, lines, narrow_ref, small_ref):
    half = weights.shape[1]
    odd = lax.rem(g, 2) == 1

    def columns(i):
        low = pl.multiple_of(3 * g // 2 * BLK, BLK)
        window = weights[i, :, pl.ds(low, 2 * BLK)]
        moved = jnp.concatenate([window[:, DH:], window[:, :DH]], axis=1)
        return jnp.where(odd, moved, window)

    lane = lax.broadcasted_iota(jnp.int32, (half, 2 * BLK), 1)
    query = columns(0)
    narrow_ref[:, : 2 * BLK] = jnp.where(lane < HW, query, jnp.zeros_like(query))
    narrow_ref[:, 2 * BLK :] = pack_kv(columns(1)[:, :HW], columns(2)[:, :HW])

    def line(i):
        return lines[i][...].astype(f32).reshape(1, -1)

    zero = jnp.zeros((1, half), f32)
    small_ref[...] = jnp.zeros_like(small_ref)
    for row in range(6):
        small_ref[row : row + 1] = jnp.where(
            x == 0, jnp.concatenate([line(row), zero], axis=1), jnp.concatenate([zero, line(row)], axis=1)
        )
    ups = line(8)
    for i in range(2):
        small_ref[pl.ds(8 + 2 * x + i, 1)] = ups[:, 2 * half * i : 2 * half * i + 2 * half]

    def part(i):
        mine = jnp.where(odd, line(i)[:, HW:], line(i)[:, :HW])
        return jnp.where(g // 2 == x, mine, jnp.zeros_like(mine))

    value = part(7)
    small_ref[12:13] = jnp.concatenate(
        [part(6), jnp.zeros((1, 2 * BLK), f32), value[:, 2 * DH :], value[:, : 2 * DH], jnp.zeros((1, BLK), f32)], axis=1
    )


def gather_kernel(
    tokens_ref, query_any, key_any, value_any, wo_ref, l0, l1, l2, l3, l4, l5, l6, l7, l8,
    kv_ref, q_ref, normed_ref, small_out, wfull, wo_out,
    lined, attn_w, narrow_ref, small_ref, small_in, kvs,
    z_own, z_send, z_recv, s_sem, n_send, n_recv, kv_send, kv_recv, kv_local, w_send, w_recv, w_local, a_sem,
):
    g, r, core, x = place()
    other = 1 - x
    rows, width = tokens_ref.shape
    half = width // 2
    fourth = half // 2
    eighth = half // 4
    loads = [
        pltpu.make_async_copy(ref, attn_w.at[i], a_sem.at[i]) for i, ref in enumerate((query_any, key_any, value_any))
    ]
    for load in loads:
        load.start()
    greet(g, r, core, x, False)

    def half_of(source, part):
        return lined.at[source, pl.ds(BLK * part, BLK)]

    def along(source, part, away, sem):
        return send(half_of(source, part), half_of(source, part), sem, z_recv.at[source, part], g=g + away)

    lined[g] = tokens_ref[...]
    for part in range(2):
        pl.when(g > 0)(lambda: along(g, part, -1, z_own.at[0, part]).start())
        pl.when(g < GROUPS - 1)(lambda: along(g, part, 1, z_own.at[1, part]).start())

    for load in loads:
        load.wait()
    prepare(g, x, attn_w, (l0, l1, l2, l3, l4, l5, l6, l7, l8), narrow_ref, small_ref)
    small_move = send(small_ref, small_in, s_sem.at[0], s_sem.at[1], x=other)
    small_move.start()
    mine = pl.ds(x * half + core * fourth, fourth)
    narrow_x = send(narrow_ref.at[pl.ds(core * fourth, fourth)], wfull.at[mine], n_send.at[0], n_recv.at[0], x=other)
    narrow_x.start()

    def wo_rows(owner, part):
        return wo_out.at[pl.ds(owner * half + core * fourth + part * eighth, eighth)]

    wo_x = send(wo_ref.at[pl.ds(core * fourth + r * eighth, eighth)], wo_rows(x, r), w_send.at[0], w_recv.at[0], x=other)
    wo_y = send(wo_rows(other, r), wo_rows(other, r), w_send.at[3], w_recv.at[3], r=1 - r)
    wo_s = [
        send(wo_rows(other, part), wo_rows(other, part), w_send.at[6 + i], w_recv.at[6 + i], core=1 - core)
        for i, part in enumerate((r, 1 - r))
    ]
    wo_x.start()
    locals_ = [pltpu.make_async_copy(wo_ref, wo_out.at[pl.ds(x * half, half)], w_local.at[0])]
    for item in locals_:
        item.start()

    wfull[pl.ds(x * half, half)] = narrow_ref[...]
    narrow_x.wait_recv()
    theirs = wfull.at[pl.ds(other * half + core * fourth, fourth)]
    narrow_s = send(theirs, theirs, n_send.at[1], n_recv.at[1], core=1 - core)
    narrow_s.start()
    small_move.wait_recv()
    small_out[...] = small_ref[...] + small_in[...]
    narrow_s.wait_recv()

    own = seat(r, core, x)

    def span(step):
        return (step, 0, rows) if step < GROUPS - 1 else (GROUPS - 1, BLK * (step - GROUPS + 1), BLK)

    def block(owner, step):
        nth, low, count = span(step)
        return kv_ref.at[owner, nearest(g, nth), pl.ds(low, count)]

    def made(step):
        nth, low, count = span(step)
        return kvs.at[nth, pl.ds(low, count)]

    def push(step, kind, src, dst, **device):
        send(src, dst, kv_send.at[kind, step], kv_recv.at[kind, step], **device).start()

    def settle(step, kind, owner):
        arrived(block(owner, step), kv_send.at[kind, step], kv_recv.at[kind, step], x)

    def forward(step):
        by_x = block(seat(r, core, other), step)
        settle(step, 0, seat(r, core, other))
        if step % 2 == 0:
            push(step, 3, by_x, by_x, r=1 - r)
        push(step, 4, by_x, by_x, core=1 - core)
        by_y = block(seat(1 - r, core, x), step)
        settle(step, 1, seat(1 - r, core, x))
        if step % 2 == 1:
            push(step, 3, by_y, by_y, x=other)
        push(step, 5, by_y, by_y, core=1 - core)

    def forward_far(step):
        far = block(seat(1 - r, core, other), step)
        settle(step, 3, seat(1 - r, core, other))
        push(step, 6, far, far, core=1 - core)

    def take(nth, part):
        source = nearest(g, nth)
        arrived(half_of(source, part), z_send.at[source, part], z_recv.at[source, part], x)
        pl.when((source < g) & (g < GROUPS - 1))(lambda: along(source, part, 1, z_send.at[source, part]).start())
        pl.when((source > g) & (g > 0))(lambda: along(source, part, -1, z_send.at[source, part]).start())

    def project(step):
        nth, low, count = span(step)
        source = nearest(g, nth)
        taken = pl.ds(low, count)
        values = lined[source, taken].astype(f32)
        normed = layer_norm(values, small_out[0:1], small_out[1:2]).astype(bf16)
        normed_ref[source, taken] = normed
        both = dot(normed, wfull[...]) + small_out[12:13, : wfull.shape[1]]
        kvs[nth, taken] = both[:, 2 * BLK :].astype(bf16)
        push(step, 0, made(step), block(own, step), x=other)
        push(step, 1, made(step), block(own, step), r=1 - r)
        push(step, 2, made(step), block(own, step), core=1 - core)
        q_ref[source, taken] = (both[:, : 2 * BLK] * SCALE).astype(bf16)
        pltpu.make_async_copy(made(step), block(own, step), kv_local.at[step]).start()

    at_end = (g == 0) | (g == GROUPS - 1)
    between = jnp.logical_not(at_end)
    project(0)
    take(1, 0)
    take(1, 1)

    @pl.when(between)
    def _():
        take(2, 0)
        take(2, 1)

    project(1)
    forward(0)

    @pl.when(at_end)
    def _():
        take(2, 0)
        take(2, 1)

    project(2)

    @pl.when(at_end)
    def _():
        forward(1)
        forward_far(0)

    take(3, 0)
    pl.when(between)(lambda: take(3, 1))
    project(3)
    pl.when(at_end)(lambda: take(3, 1))
    project(4)

    @pl.when(between)
    def _():
        forward(1)
        forward_far(0)

    wo_x.wait_recv()
    wo_y.start()
    wo_s[0].start()
    forward(2)
    forward_far(1)
    forward(3)
    forward_far(2)
    forward(4)
    forward_far(3)
    arrived(wo_rows(other, 1 - r), w_send.at[3], w_recv.at[3], x)
    wo_s[1].start()
    forward_far(4)

    for step in range(GROUPS + 1):
        pltpu.make_async_copy(made(step), block(own, step), kv_local.at[step]).wait()
        settle(step, 2, seat(r, 1 - core, x))
        settle(step, 4, seat(r, 1 - core, other))
        settle(step, 5, seat(1 - r, 1 - core, x))
        settle(step, 6, seat(1 - r, 1 - core, other))
        for kind in range(7):
            left(made(step), kv_send.at[kind, step], kv_recv.at[kind, step], x)
    for part in range(2):
        pl.when(g > 0)(lambda: left(half_of(g, part), z_own.at[0, part], z_recv.at[g, part], x))
        pl.when(g < GROUPS - 1)(lambda: left(half_of(g, part), z_own.at[1, part], z_recv.at[g, part], x))
        for nth in range(1, GROUPS):
            source = nearest(g, nth)
            passed = ((source < g) & (g < GROUPS - 1)) | ((source > g) & (g > 0))
            pl.when(passed)(
                lambda: left(half_of(source, part), z_send.at[source, part], z_recv.at[source, part], x)
            )
    small_move.wait_send()
    narrow_x.wait_send()
    narrow_s.wait_send()
    for item in locals_:
        item.wait()
    for item in (wo_x, wo_y, *wo_s):
        item.wait_send()
    for i, part in enumerate((r, 1 - r)):
        there = wo_out.at[pl.ds(other * half + (1 - core) * fourth + part * eighth, eighth)]
        send(there, there, w_send.at[6 + i], w_recv.at[6 + i], core=1 - core).wait_recv()


def anywhere():
    return pl.BlockSpec(memory_space=pl.ANY)


def in_hbm():
    return pl.BlockSpec(memory_space=pltpu.HBM)


def gather(tokens, query, key, value, wo, *lines):
    rows, width = tokens.shape
    wide = 2 * BLK + 2 * HW
    small = (16, width)
    dma = pltpu.SemaphoreType.DMA
    return pl.pallas_call(
        gather_kernel,
        out_shape=(
            jax.ShapeDtypeStruct((8, GROUPS, rows, 2 * HW), bf16),
            jax.ShapeDtypeStruct((GROUPS, rows, 2 * BLK), bf16),
            jax.ShapeDtypeStruct((GROUPS, rows, width), bf16),
            jax.ShapeDtypeStruct(small, f32),
            jax.ShapeDtypeStruct((width, wide), bf16),
            jax.ShapeDtypeStruct((width, width), bf16),
        ),
        in_specs=[whole_vmem(), *[in_hbm()] * 4, *[whole_vmem()] * len(lines)],
        out_specs=(anywhere(), *(whole_vmem(),) * 5),
        scratch_shapes=[
            pltpu.VMEM((GROUPS, rows, width), bf16),
            pltpu.VMEM((3, width // 2, width), bf16),
            pltpu.VMEM((width // 2, wide), bf16),
            pltpu.VMEM(small, f32),
            pltpu.VMEM(small, f32),
            pltpu.VMEM((GROUPS, rows, 2 * HW), bf16),
            dma((2, 2)), dma((GROUPS, 2)), dma((GROUPS, 2)), dma((2,)), dma((2,)), dma((2,)),
            dma((7, GROUPS + 1)), dma((7, GROUPS + 1)), dma((GROUPS + 1,)), dma((8,)), dma((8,)), dma((2,)), dma((3,)),
        ],
        compiler_params=pltpu.CompilerParams(
            collective_id=0, has_side_effects=True, vmem_limit_bytes=16 << 20
        ),
        name="gather",
    )(tokens, query, key, value, wo, *lines)


def erf_parts(values):
    below = 0.5 * (1.0 + lax.erf(values * ROOT_HALF))
    return below, PDF_SCALE * jnp.exp(-0.5 * values * values)


PARTS = 8
UNIT = 216
KEPT = 168


def dense_kernel(
    out_t_ref, tokens_ref, cot_ref, small_ref, wo_ref, up_mine, up_other, down_any,
    base_ref, x_give_ref, middle_grad_ref, grad_t_ref, keep_ref, give_ref, far_ref, sums_ref,
    down_ref, up_ref, attn_in, attn_t, cots, h2s, mid_ref, n2_ref, scales, part_y, part_d, in_y, in_d, pass_y, pass_d,
    x_y, x_d, hids, dus, branch_ref, grad_out, wo_keep, wo_give, wo_in, wo_pass, wo_x,
    l_sem, a_send, a_recv, c_send, c_recv, h_send, h_recv, y_send, y_recv, d_send, d_recv, o_send, o_recv,
    w_send, w_recv,
):
    g, r, core, x = place()
    other, sib = 1 - x, 1 - core
    rows, width = tokens_ref.shape
    half = width // 2
    fourth = half // 2
    loads = [
        pltpu.make_async_copy(
            down_any.at[pl.ds(pl.multiple_of(core * width, width), width)], down_ref, l_sem.at[0]
        ),
        pltpu.make_async_copy(up_mine, up_ref.at[pl.ds(x * half, half)], l_sem.at[1]),
        pltpu.make_async_copy(up_other, up_ref.at[pl.ds(other * half, half)], l_sem.at[2]),
    ]
    for load in loads:
        load.start()
    greet(g, r, core, x, True)
    pending = []

    def begin(src, dst, out_sem, in_sem, **device):
        move = send(src, dst, out_sem, in_sem, **device)
        move.start()
        pending.append(move)
        return move

    def other_group(away):
        return lax.rem(g + away, GROUPS)

    def rows_of(b):
        return pl.ds(BLK * b, BLK)

    for b in range(2):
        for away in range(1, GROUPS):
            to = other_group(away)
            begin(out_t_ref.at[2 * to + b], attn_in.at[g, b], a_send.at[b, away], a_recv.at[b, g], g=to)
        attn_in[g, b] = out_t_ref[2 * g + b]
        cots[b, 0] = cot_ref[rows_of(b)]
    cot_x = begin(cots.at[:, 0], cots.at[:, 2], c_send.at[2], c_recv.at[2], x=other)
    cot_moves = [begin(cots.at[:, 0], cots.at[:, 1], c_send.at[0], c_recv.at[0], core=sib)]
    sums_ref[...] = jnp.zeros_like(sums_ref)
    sums_ref[5:6] = jnp.sum(cot_ref[...].astype(f32), axis=0, keepdims=True)
    h2_moves = []

    def norm(b):
        for away in range(1, GROUPS):
            source = other_group(away)
            arrived(attn_in.at[source, b], a_send.at[b, away], a_recv.at[b, source], x)
        for source in range(GROUPS):
            attn_t[HW * source : HW * source + HW, BLK * b : BLK * b + BLK] = attn_in[source, b]
        middle = (
            tokens_ref[rows_of(b)].astype(f32)
            + outer(attn_t[:, BLK * b : BLK * b + BLK], wo_ref[...])
            + small_ref[2:3]
        )
        mid_ref[b] = middle
        mean = jnp.mean(middle, axis=-1, keepdims=True)
        centred = middle - mean
        scale = lax.rsqrt(jnp.mean(centred * centred, axis=-1, keepdims=True) + EPS)
        scales[b] = scale
        n2_ref[b] = centred * scale
        h2s[b, 0] = (n2_ref[b] * small_ref[3:4] + small_ref[4:5]).astype(bf16)
        h2_moves.append(
            (
                begin(h2s.at[b, 0], h2s.at[b, 2], h_send.at[b, 1], h_recv.at[b, 1], x=other),
                begin(h2s.at[b, 0], h2s.at[b, 1], h_send.at[b, 0], h_recv.at[b, 0], core=sib),
            )
        )

    def pass_on(b):
        h2_moves[b][0].wait_recv()
        return begin(h2s.at[b, 2], h2s.at[b, 3], h_send.at[b, 2], h_recv.at[b, 2], core=sib)

    bias_row = 8 + 2 * x + core

    def pair_of(ref, b, pair):
        return ref[b, 2 * pair : 2 * pair + 2].reshape(2 * BLK, width)

    def forward_backward(b, pair):
        cot = pair_of(cots, b, pair)
        expanded = dot(pair_of(h2s, b, pair), up_ref[...]) + small_ref[pl.ds(bias_row, 1)]
        below, density = erf_parts(expanded)
        hidden = (expanded * below).astype(bf16)
        hids[b, pair] = hidden
        slope = below + expanded * density
        grad_hidden = inner(cot, down_ref[...]).astype(bf16).astype(f32)
        grad_expand = (grad_hidden * slope).astype(bf16)
        dus[b, pair] = grad_expand
        part_d[b, pair] = inner(grad_expand, up_ref[...])
        part_y[b, pair] = dot(hidden, down_ref[...])
        sums_ref[pl.ds(bias_row, 1)] += jnp.sum(grad_expand.astype(f32), axis=0, keepdims=True)

    d_moves, y_passes = [None, None], [None, None]

    def near_pair(b):
        if b == 0:
            cot_moves[0].wait_recv()
        h2_moves[b][1].wait_recv()
        forward_backward(b, 0)
        return begin(part_d.at[b, 0, pl.ds(BLK, BLK)], in_d.at[b], d_send.at[b, 0], d_recv.at[b, 0], core=sib)

    def far_pair(b, passed):
        if b == 0:
            cot_moves[1].wait_recv()
        passed.wait_recv()
        forward_backward(b, 1)
        x_d[b, 0] = part_d[b, 1, BLK:].astype(bf16)
        across = begin(x_d.at[b, 0], pass_d.at[b], d_send.at[b, 1], d_recv.at[b, 1], core=sib)
        x_y[b] = part_y[b, 1, BLK:].astype(bf16)
        y_passes[b] = begin(x_y.at[b], pass_y.at[b], y_send.at[b, 1], y_recv.at[b, 1], core=sib)
        across.wait_recv()
        x_d[b, 1] = (part_d[b, 1, :BLK] + pass_d[b].astype(f32)).astype(bf16)
        return begin(x_d.at[b, 1], x_d.at[b, 2], d_send.at[b, 2], d_recv.at[b, 2], x=other)

    def back(b, near, far):
        near.wait_recv()
        far.wait_recv()
        grad_second = part_d[b, 0, :BLK] + in_d[b] + x_d[b, 2].astype(f32)
        n2 = n2_ref[b]
        sums_ref[3:4] += jnp.sum(grad_second * n2, axis=0, keepdims=True)
        sums_ref[4:5] += jnp.sum(grad_second, axis=0, keepdims=True)
        pulled = grad_second * small_ref[3:4]
        inward = (
            pulled - jnp.mean(pulled, axis=-1, keepdims=True) - n2 * jnp.mean(pulled * n2, axis=-1, keepdims=True)
        )
        grad_middle = cot_ref[rows_of(b)].astype(f32) + inward * scales[b]
        middle_grad_ref[rows_of(b)] = grad_middle
        branch = grad_middle.astype(bf16)
        branch_ref[rows_of(b)] = branch
        sums_ref[2:3] += jnp.sum(branch.astype(f32), axis=0, keepdims=True)
        grad_out_t = inner(wo_ref[...], branch).astype(bf16)
        for group in range(GROUPS):
            grad_out[group, b] = grad_out_t[HW * group : HW * group + HW]
        for away in range(1, GROUPS):
            to = other_group(away)
            begin(grad_out.at[to, b], grad_t_ref.at[2 * g + b], o_send.at[b, away], o_recv.at[b, g], g=to)
        grad_t_ref[2 * g + b] = grad_out[g, b]

    norm(0)
    norm(1)
    for load in loads:
        load.wait()
    near = [near_pair(0), None]
    cot_x.wait_recv()
    cot_moves.append(begin(cots.at[:, 2], cots.at[:, 3], c_send.at[1], c_recv.at[1], core=sib))
    passed = [pass_on(0), None]
    near[1] = near_pair(1)
    far = [far_pair(0, passed[0]), None]
    passed[1] = pass_on(1)
    far[1] = far_pair(1, passed[1])

    def over_rows(left, right):
        total = None
        for b in range(2):
            for pair in range(2):
                term = outer(left(b, pair), right(b, pair))
                total = term if total is None else total + term
        return total.astype(bf16)

    def parts(write):
        for y in range(2):
            pl.when(r == y)(lambda: write(keep_ref, y))
            pl.when(r != y)(lambda: write(give_ref, y))

    down_grad = over_rows(lambda b, pair: hids[b, pair], lambda b, pair: pair_of(cots, b, pair))

    def write_down(ref, y):
        for z in range(GROUPS):
            p = y * GROUPS + z
            ref[z, 0:96] = down_grad[96 * p : 96 * p + 96]

    parts(write_down)
    back(0, near[0], far[0])
    up_grad = over_rows(lambda b, pair: pair_of(h2s, b, pair), lambda b, pair: dus[b, pair])

    def up_part(p, h):
        return up_grad[half * h + 48 * p : half * h + 48 * p + 48]

    def write_up(y, h):
        @pl.when((r == y) & (x == h))
        def _():
            for z in range(GROUPS):
                keep_ref[z, 96:144] = up_part(y * GROUPS + z, h)

        @pl.when((r != y) & (x == h))
        def _():
            for z in range(GROUPS):
                give_ref[z, 96:144] = up_part(y * GROUPS + z, h)

        @pl.when((r == y) & (x != h))
        def _():
            for z in range(GROUPS):
                x_give_ref[rows + 48 * z : rows + 48 * z + 48] = up_part(y * GROUPS + z, h)

        @pl.when((r != y) & (x != h))
        def _():
            for z in range(GROUPS):
                far_ref[z] = up_part(y * GROUPS + z, h)

    for y in range(2):
        for h in range(2):
            write_up(y, h)
    back(1, near[1], far[1])

    for owner in range(2):
        for c in range(2):
            piece = dot(attn_t[half * owner + fourth * c : half * owner + fourth * c + fourth], branch_ref[...])

            @pl.when(core == c)
            def _():
                wo_keep[owner] = piece

            @pl.when(core != c)
            def _():
                wo_give[owner] = piece.astype(bf16)

    w_sib = begin(wo_give, wo_in, w_send.at[0], w_recv.at[0], core=sib)
    y_sibs = [
        begin(part_y.at[b, 0, pl.ds(BLK, BLK)], in_y.at[b], y_send.at[b, 0], y_recv.at[b, 0], core=sib)
        for b in range(2)
    ]
    w_sib.wait_recv()
    wo_pass[...] = (wo_keep[other] + wo_in[other].astype(f32)).astype(bf16)
    w_x = begin(wo_pass, wo_x, w_send.at[1], w_recv.at[1], x=other)
    for b in range(2):
        y_passes[b].wait_recv()
        x_give_ref[rows_of(b)] = (part_y[b, 1, :BLK] + pass_y[b].astype(f32)).astype(bf16)
        y_sibs[b].wait_recv()
        base_ref[rows_of(b)] = mid_ref[b] + part_y[b, 0, :BLK] + in_y[b] + small_ref[5:6]
    mine = wo_keep[x] + wo_in[x].astype(f32)
    for b in range(2):
        for away in range(1, GROUPS):
            source = other_group(away)
            arrived(grad_t_ref.at[2 * source + b], o_send.at[b, away], o_recv.at[b, source], x)
    w_x.wait_recv()
    wo_sum = (mine + wo_x[...].astype(f32)).astype(bf16)

    def write_wo(ref, y):
        for z in range(GROUPS):
            p = y * GROUPS + z
            ref[z, 144:KEPT] = wo_sum[24 * p : 24 * p + 24]

    parts(write_wo)
    for move in pending:
        move.wait_send()


def dense(out_t, tokens, cot, small, wo, up_mine, up_other, down):
    rows, width = tokens.shape
    dma = pltpu.SemaphoreType.DMA
    full = (rows, width)
    part = (BLK, width)
    pair = (2 * BLK, width)
    fourth = (width // 4, width)
    return pl.pallas_call(
        dense_kernel,
        out_shape=(
            jax.ShapeDtypeStruct(full, f32),
            jax.ShapeDtypeStruct((rows + 48 * GROUPS, width), bf16),
            jax.ShapeDtypeStruct(full, f32),
            jax.ShapeDtypeStruct(out_t.shape, bf16),
            jax.ShapeDtypeStruct((GROUPS, KEPT, width), bf16),
            jax.ShapeDtypeStruct((GROUPS, KEPT, width), bf16),
            jax.ShapeDtypeStruct((GROUPS, 48, width), bf16),
            jax.ShapeDtypeStruct(small.shape, f32),
        ),
        in_specs=[whole_vmem()] * 5 + [anywhere()] * 3,
        out_specs=(whole_vmem(),) * 8,
        scratch_shapes=[
            pltpu.VMEM((width, width), bf16),
            pltpu.VMEM((width, width), bf16),
            pltpu.VMEM((GROUPS, 2, HW, BLK), bf16),
            pltpu.VMEM((width, rows), bf16),
            pltpu.VMEM((2, 4, *part), bf16),
            pltpu.VMEM((2, 4, *part), bf16),
            pltpu.VMEM((2, *part), f32),
            pltpu.VMEM((2, *part), f32),
            pltpu.VMEM((2, BLK, 1), f32),
            pltpu.VMEM((2, 2, *pair), f32),
            pltpu.VMEM((2, 2, *pair), f32),
            pltpu.VMEM((2, *part), f32),
            pltpu.VMEM((2, *part), f32),
            pltpu.VMEM((2, *part), bf16),
            pltpu.VMEM((2, *part), bf16),
            pltpu.VMEM((2, *part), bf16),
            pltpu.VMEM((2, 3, *part), bf16),
            pltpu.VMEM((2, 2, *pair), bf16),
            pltpu.VMEM((2, 2, *pair), bf16),
            pltpu.VMEM(full, bf16),
            pltpu.VMEM((GROUPS, 2, HW, BLK), bf16),
            pltpu.VMEM((2, *fourth), f32),
            pltpu.VMEM((2, *fourth), bf16),
            pltpu.VMEM((2, *fourth), bf16),
            pltpu.VMEM(fourth, bf16),
            pltpu.VMEM(fourth, bf16),
            dma((3,)), dma((2, GROUPS)), dma((2, GROUPS)), dma((3,)), dma((3,)), dma((2, 3)), dma((2, 3)),
            dma((2, 2)), dma((2, 2)), dma((2, 3)), dma((2, 3)), dma((2, GROUPS)), dma((2, GROUPS)), dma((2,)), dma((2,)),
        ],
        compiler_params=pltpu.CompilerParams(
            collective_id=1, has_side_effects=True, vmem_limit_bytes=40 << 20
        ),
        name="dense",
    )(out_t, tokens, cot, small, wo, up_mine, up_other, down)


FARTHEST = ((3, 2, 1, 0), (3, 0, 2, 1), (0, 3, 1, 2), (0, 1, 2, 3))


def farthest(g, step):
    picked = FARTHEST[0][step]
    for z in range(1, GROUPS):
        picked = jnp.where(g == z, FARTHEST[z][step], picked)
    return picked


class Chain:
    def __init__(self, g, x, total, parts, inward, outward, out_sem, in_sem):
        self.g, self.x, self.total, self.parts = g, x, total, parts
        self.inward, self.outward, self.out_sem, self.in_sem = inward, outward, out_sem, in_sem

    def move(self, to, way):
        return send(
            self.outward.at[to], self.inward.at[way, to], self.out_sem.at[to], self.in_sem.at[way, to],
            g=jnp.clip(self.g + (1 if way == 0 else -1), 0, GROUPS - 1),
        )

    def step(self, to):
        g = self.g
        self.total[...] = self.parts[to].astype(f32)

        def take(way):
            arrived(self.inward.at[way, to], self.out_sem.at[to], self.in_sem.at[way, to], self.x)
            self.total[...] += self.inward[way, to].astype(f32)

        pl.when((to >= g) & (g > 0))(lambda: take(0))
        pl.when((to <= g) & (g < GROUPS - 1))(lambda: take(1))

        @pl.when(to != g)
        def _():
            self.outward[to] = self.total[...].astype(bf16)

        pl.when(to > g)(lambda: self.move(to, 0).start())
        pl.when(to < g)(lambda: self.move(to, 1).start())

    def finish(self):
        for step in range(GROUPS - 1):
            to = farthest(self.g, step)
            left(self.outward.at[to], self.out_sem.at[to], self.in_sem.at[0, to], self.x)


class Ring:
    def __init__(self, g, x, slot, own_sem, out_sem, in_sem):
        self.g, self.x, self.slot = g, x, slot
        self.own_sem, self.out_sem, self.in_sem = own_sem, out_sem, in_sem

    def move(self, source, way, sem):
        return send(
            self.slot(source), self.slot(source), sem, self.in_sem.at[source],
            g=jnp.clip(self.g + way, 0, GROUPS - 1),
        )

    def start(self):
        g = self.g
        pl.when(g > 0)(lambda: self.move(g, -1, self.own_sem.at[0]).start())
        pl.when(g < GROUPS - 1)(lambda: self.move(g, 1, self.own_sem.at[1]).start())

    def step(self, step):
        g, source = self.g, nearest(self.g, step)
        arrived(self.slot(source), self.out_sem.at[source], self.in_sem.at[source], self.x)
        pl.when((source < g) & (g < GROUPS - 1))(lambda: self.move(source, 1, self.out_sem.at[source]).start())
        pl.when((source > g) & (g > 0))(lambda: self.move(source, -1, self.out_sem.at[source]).start())
        return source

    def finish(self):
        g = self.g
        for i, there in enumerate((g > 0, g < GROUPS - 1)):
            pl.when(there)(lambda: left(self.slot(g), self.own_sem.at[i], self.in_sem.at[g], self.x))
        for step in range(1, GROUPS):
            source = nearest(g, step)
            passed = ((source < g) & (g < GROUPS - 1)) | ((source > g) & (g > 0))
            pl.when(passed)(
                lambda: left(self.slot(source), self.out_sem.at[source], self.in_sem.at[source], self.x)
            )


def arrived(what, out_sem, in_sem, x):
    send(what, what, out_sem, in_sem, x=1 - x).wait_recv()


def left(what, out_sem, in_sem, x):
    send(what, what, out_sem, in_sem, x=1 - x).wait_send()


def scatter_kernel(
    dkv_ref, dq_any, normed_any, wfull_any, tokens_any, mgrad_any, keep_any, over_any, near_any, far_any, small_ref, sums_in,
    tokens_grad_ref, big_ref, qout_ref, kvout_ref, sums_ref,
    dq_ref, normed_ref, wfull_ref, tokens_ref, mgrad_ref, kept, over, near, far,
    own_kv, sib_kv, keep_x, give_x, in_x, give_y, in_y, part_a, total_a, inward_a, outward_a, wg_kv,
    by_sum, total_b, inward_b, outward_b, unit,
    q_keep, q_give, q_in, q_pass, q_x, q_y, q_sum, v_keep, v_give, v_in, v_pass, v_x, v_y, v_sum,
    sums_got, late, late_sum, late_got,
    load_sem, own_sem, k_send, k_recv, x_send, x_recv, y_send, y_recv, ca_send, ca_recv,
    cb_send, cb_recv, rb_own, rb_send, rb_recv,
    fy_send, fy_recv, fs_send, fs_recv,
    q_send, q_recv, rq_own, rq_send, rq_recv, qs_send, qs_recv,
    v_send, v_recv, rv_own, rv_send, rv_recv, vs_send, vs_recv,
    s_send, s_recv, t_send, t_recv, l_sem,
):
    g, r, core, x = place()
    other, sib, far_r = 1 - x, 1 - core, 1 - r
    rows, width = tokens_ref.shape
    half = width // 2
    fourth = half // 2
    wide_q = 2 * BLK
    loads = [
        pltpu.make_async_copy(what, where, load_sem.at[i])
        for i, (what, where) in enumerate(
            (
                (keep_any, kept), (over_any, over), (near_any.at[pl.ds(rows, 48 * GROUPS)], near), (far_any, far),
                (dq_any, dq_ref), (normed_any, normed_ref), (wfull_any, wfull_ref), (tokens_any, tokens_ref),
                (mgrad_any, mgrad_ref),
            )
        )
    ]
    for load in loads:
        load.start()
    greet(g, r, core, x, True, True)
    pending = []

    def begin(src, dst, out_sem, in_sem, **device):
        move = send(src, dst, out_sem, in_sem, **device)
        move.start()
        pending.append(move)
        return move

    def settled(move):
        move.wait_recv()
        move.wait_send()
        pending[:] = [item for item in pending if item is not move]

    kv_moves = []
    for i in range(GROUPS):
        c = farthest(g, i)
        for spot in range(4):
            own = pltpu.make_async_copy(
                dkv_ref.at[seat(spot // 2, core, spot % 2), c], own_kv.at[i, spot], own_sem.at[i, spot]
            )
            own.start()
            across = begin(
                dkv_ref.at[seat(spot // 2, sib, spot % 2), c], sib_kv.at[i, spot],
                k_send.at[i, spot], k_recv.at[i, spot], core=sib,
            )
            kv_moves.append((own, across))

    def split(total, keep, give):
        for owner in range(2):
            for c in range(2):
                low = half * owner + fourth * c
                chunk = total[low : low + fourth]

                @pl.when(core == c)
                def _():
                    keep[owner] = chunk

                @pl.when(core != c)
                def _():
                    give[owner] = chunk.astype(bf16)

    def scaled(c):
        return dq_ref[c] * bf16(SCALE)

    q_move = send(q_give, q_in, q_send.at[0], q_recv.at[0], core=sib)

    def query_grad():
        loads[4].wait()
        loads[5].wait()
        query_total = outer(normed_ref[0], scaled(0))
        for c in range(1, GROUPS):
            query_total += outer(normed_ref[c], scaled(c))
        split(query_total, q_keep, q_give)
        q_move.start()
        line_q = scaled(0).astype(f32)
        for c in range(1, GROUPS):
            line_q += scaled(c).astype(f32)
        sums_ref[pl.ds(16 + g, 1), 0:wide_q] = jnp.sum(line_q, axis=0, keepdims=True)

    sums_ref[...] = jnp.zeros_like(sums_ref)
    sums_ref[0:16] = sums_in[...]
    wg_kv[...] = jnp.zeros_like(wg_kv)

    def q_slot(z):
        return qout_ref.at[core, z]

    def v_slot(z):
        return kvout_ref.at[core, z]

    def b_slot(z):
        return big_ref.at[core, r, z]

    ring_q = Ring(g, x, q_slot, rq_own, rq_send, rq_recv)
    ring_v = Ring(g, x, v_slot, rv_own, rv_send, rv_recv)
    ring_b = Ring(g, x, b_slot, rb_own, rb_send, rb_recv)

    def store(value_ref, slot, sem):
        copy = pltpu.make_async_copy(value_ref, slot, sem)
        copy.start()
        copy.wait()

    def spread_b(z, step):
        begin(b_slot(z), b_slot(z), fy_send.at[step], fy_recv.at[step], r=far_r)
        begin(b_slot(z), b_slot(z), fs_send.at[0, step], fs_recv.at[0, step], core=sib)

    def spread_far(step):
        what = big_ref.at[core, far_r, nearest(g, step)]
        arrived(what, fy_send.at[step], fy_recv.at[step], x)
        begin(what, what, fs_send.at[1, step], fs_recv.at[1, step], core=sib)

    def on_ring_b(step):
        spread_b(ring_b.step(step), step)

    def on_ring_q(step):
        z = ring_q.step(step)
        begin(q_slot(z), q_slot(z), qs_send.at[step], qs_recv.at[step], core=sib)

    def on_ring_v(step):
        z = ring_v.step(step)
        begin(v_slot(z), v_slot(z), vs_send.at[step], vs_recv.at[step], core=sib)

    chain_a = Chain(g, x, total_a, part_a, inward_a, outward_a, ca_send, ca_recv)
    chain_b = Chain(g, x, total_b, by_sum, inward_b, outward_b, cb_send, cb_recv)
    at_end = (g == 0) | (g == GROUPS - 1)
    between = jnp.logical_not(at_end)

    def steps(chain, *which):
        for i in which:
            chain.step(farthest(g, i))

    def on_sibling(i):
        for own, across in kv_moves[4 * i : 4 * i + 4]:
            own.wait()
            across.wait_recv()

        def total(row, column):
            spot = 2 * row + column
            return own_kv[i, spot].astype(f32) + sib_kv[i, spot].astype(f32)

        for k in range(2):
            give_x[i, k] = (total(k, other) if i % 2 == 0 else total(far_r, k)).astype(bf16)
            keep_x[i, k] = total(k, x) if i % 2 == 0 else total(r, k)

    def go_first(i):
        along = {"x": other} if i % 2 == 0 else {"r": far_r}
        begin(give_x.at[i], in_x.at[i], x_send.at[i], x_recv.at[i], **along)

    def on_first(i):
        arrived(in_x.at[i], x_send.at[i], x_recv.at[i], x)
        away, stay, along = (far_r, r, {"r": far_r}) if i % 2 == 0 else (other, x, {"x": other})
        give_y[i] = (keep_x[i, away] + in_x[i, away].astype(f32)).astype(bf16)
        begin(give_y.at[i], in_y.at[i], y_send.at[i], y_recv.at[i], **along)
        keep_x[i, stay] += in_x[i, stay].astype(f32)

    def on_second(i):
        c = farthest(g, i)
        arrived(in_y.at[i], y_send.at[i], y_recv.at[i], x)
        both = (keep_x[i, r if i % 2 == 0 else x] + in_y[i].astype(f32)).astype(bf16)
        part_a[c] = inner(scaled(c), wfull_ref[:, :wide_q]) + inner(both, wfull_ref[:, wide_q:])
        wg_kv[...] += outer(normed_ref[c], both)
        sums_ref[pl.ds(16 + g, 1), wide_q : wide_q + 2 * HW] += jnp.sum(both.astype(f32), axis=0, keepdims=True)

    for load in loads[:4]:
        load.wait()
    own_up = pl.ds(pl.multiple_of(96 + 48 * x, 48), 48)
    their_up = pl.ds(pl.multiple_of(96 + 48 * other, 48), 48)
    for z in range(GROUPS):
        pair = kept[z].astype(f32) + over[z].astype(f32)
        by_sum[z, 0:96] = pair[0:96]
        by_sum[z, own_up] = pair[96:144]
        by_sum[z, 192:UNIT] = pair[144:KEPT]
        by_sum[z, their_up] = near[48 * z : 48 * z + 48].astype(f32) + far[z].astype(f32)
    pl.when(at_end)(lambda: steps(chain_b, 0, 1, 2))
    on_sibling(0)
    go_first(0)
    on_sibling(1)
    go_first(1)
    on_sibling(2)
    on_sibling(3)
    pl.when(between)(lambda: steps(chain_b, 0))
    query_grad()
    on_first(0)
    on_first(1)
    go_first(2)
    go_first(3)
    pl.when(between)(lambda: steps(chain_b, 1, 2))
    settled(q_move)
    q_pass[...] = (q_keep[other] + q_in[other].astype(f32)).astype(bf16)
    q_across = begin(q_pass, q_x, q_send.at[1], q_recv.at[1], x=other)
    loads[6].wait()
    on_second(0)
    on_second(1)
    pl.when(at_end)(lambda: steps(chain_a, 0))
    chain_b.step(g)
    unit[...] = total_b[...].astype(bf16)
    store(unit, b_slot(g), l_sem.at[0])
    ring_b.start()
    spread_b(g, 0)
    pl.when(at_end)(lambda: steps(chain_a, 1))
    on_first(2)
    on_first(3)
    q_across.wait_recv()
    q_sum[...] = (q_keep[x] + q_in[x].astype(f32) + q_x[...].astype(f32)).astype(bf16)
    q_over = begin(q_sum, q_y, q_send.at[2], q_recv.at[2], r=far_r)
    pl.when(between)(lambda: steps(chain_a, 0))
    on_second(2)
    on_second(3)
    pl.when(at_end)(lambda: steps(chain_a, 2))
    split(wg_kv, v_keep, v_give)
    v_move = begin(v_give, v_in, v_send.at[0], v_recv.at[0], core=sib)
    s_sib = begin(sums_ref, sums_got.at[0], s_send.at[0], s_recv.at[0], core=sib)
    spread_far(0)
    settled(q_over)
    q_sum[...] = (q_sum[...].astype(f32) + q_y[...].astype(f32)).astype(bf16)
    store(q_sum, q_slot(g), l_sem.at[0])
    ring_q.start()
    begin(q_slot(g), q_slot(g), qs_send.at[0], qs_recv.at[0], core=sib)
    on_ring_b(1)
    v_move.wait_recv()
    v_pass[...] = (v_keep[other] + v_in[other].astype(f32)).astype(bf16)
    v_across = begin(v_pass, v_x, v_send.at[1], v_recv.at[1], x=other)
    settled(s_sib)
    sums_ref[...] += sums_got[0]
    s_x = begin(sums_ref, sums_got.at[1], s_send.at[1], s_recv.at[1], x=other)
    pl.when(between)(lambda: steps(chain_a, 1))
    v_across.wait_recv()
    v_sum[...] = (v_keep[x] + v_in[x].astype(f32) + v_x[...].astype(f32)).astype(bf16)
    v_over = begin(v_sum, v_y, v_send.at[2], v_recv.at[2], r=far_r)
    settled(s_x)
    sums_ref[...] += sums_got[1]
    s_y = begin(sums_ref, sums_got.at[2], s_send.at[2], s_recv.at[2], r=far_r)
    on_ring_b(2)
    pl.when(between)(lambda: steps(chain_a, 2))
    settled(v_over)
    v_sum[...] = (v_sum[...].astype(f32) + v_y[...].astype(f32)).astype(bf16)
    store(v_sum, v_slot(g), l_sem.at[0])
    ring_v.start()
    begin(v_slot(g), v_slot(g), vs_send.at[0], vs_recv.at[0], core=sib)
    settled(s_y)
    sums_ref[...] += sums_got[2]
    for away in range(1, GROUPS):
        begin(
            sums_ref, sums_got.at[2 + away], s_send.at[2 + away], s_recv.at[2 + away],
            g=lax.rem(g + away, GROUPS),
        )
    spread_far(1)
    on_ring_q(1)
    on_ring_b(3)
    chain_a.step(g)

    loads[7].wait()
    loads[8].wait()
    grad_first = total_a[...]
    values = tokens_ref[...].astype(f32)
    mean = jnp.mean(values, axis=-1, keepdims=True)
    centred = values - mean
    scale = lax.rsqrt(jnp.mean(centred * centred, axis=-1, keepdims=True) + EPS)
    n1 = centred * scale
    pulled = grad_first * small_ref[0:1]
    inward = pulled - jnp.mean(pulled, axis=-1, keepdims=True) - n1 * jnp.mean(pulled * n1, axis=-1, keepdims=True)
    tokens_grad_ref[...] = mgrad_ref[...] + inward * scale
    late[...] = jnp.zeros_like(late)
    late[0:1] = jnp.sum(grad_first * n1, axis=0, keepdims=True)
    late[1:2] = jnp.sum(grad_first, axis=0, keepdims=True)
    for step in range(len(AROUND)):
        begin(late, late_got.at[step], t_send.at[step], t_recv.at[step], **neighbour(r, core, x, step))
    on_ring_v(1)
    on_ring_q(2)
    on_ring_q(3)
    spread_far(2)
    on_ring_v(2)
    late_sum[...] = late[...]
    for step in range(len(AROUND)):
        arrived(late_got.at[step], t_send.at[step], t_recv.at[step], x)
        late_sum[...] += late_got[step]
    first_z = len(AROUND) - 1
    for away in range(1, GROUPS):
        begin(
            late_sum, late_got.at[first_z + away], t_send.at[first_z + away], t_recv.at[first_z + away],
            g=lax.rem(g + away, GROUPS),
        )
    on_ring_v(3)
    spread_far(3)

    for away in range(1, GROUPS):
        arrived(sums_got.at[2 + away], s_send.at[2 + away], s_recv.at[2 + away], x)
        arrived(late_got.at[first_z + away], t_send.at[first_z + away], t_recv.at[first_z + away], x)
    for step in range(GROUPS):
        z = nearest(g, step)
        arrived(qout_ref.at[sib, z], qs_send.at[step], qs_recv.at[step], x)
        arrived(kvout_ref.at[sib, z], vs_send.at[step], vs_recv.at[step], x)
        arrived(big_ref.at[sib, r, z], fs_send.at[0, step], fs_recv.at[0, step], x)
        arrived(big_ref.at[sib, far_r, z], fs_send.at[1, step], fs_recv.at[1, step], x)
    for move in pending:
        move.wait_send()
    for item in (chain_a, chain_b, ring_q, ring_v, ring_b):
        item.finish()
    sums_ref[...] += sums_got[3] + sums_got[4] + sums_got[5]
    total = late_sum[...] + late_got[first_z + 1] + late_got[first_z + 2] + late_got[first_z + 3]
    sums_ref[0:2] = total[0:2]


def scatter(dkv, dq, normed, wfull, tokens, mgrad, small, keep, over, near, far, sums):
    rows, width = tokens.shape
    fourth = width // 4
    dma = pltpu.SemaphoreType.DMA
    wide_q, wide_v = 2 * BLK, 2 * HW
    kv_block = (rows, wide_v)
    full = (rows, width)
    unit = (UNIT, width)

    def weight_scratch(wide):
        return [
            pltpu.VMEM((2, fourth, wide), f32),
            pltpu.VMEM((2, fourth, wide), bf16),
            pltpu.VMEM((2, fourth, wide), bf16),
            *[pltpu.VMEM((fourth, wide), bf16)] * 4,
        ]

    return pl.pallas_call(
        scatter_kernel,
        out_shape=(
            jax.ShapeDtypeStruct(full, f32),
            jax.ShapeDtypeStruct((2, 2, GROUPS, *unit), bf16),
            jax.ShapeDtypeStruct((2, GROUPS, fourth, wide_q), bf16),
            jax.ShapeDtypeStruct((2, GROUPS, fourth, wide_v), bf16),
            jax.ShapeDtypeStruct((24, width), f32),
        ),
        in_specs=[anywhere()] * 10 + [whole_vmem()] * 2,
        out_specs=(whole_vmem(), anywhere(), anywhere(), anywhere(), whole_vmem()),
        scratch_shapes=[
            *[
                pltpu.VMEM(item.shape, item.dtype)
                for item in (dq, normed, wfull, tokens, mgrad, keep, over)
            ],
            pltpu.VMEM((48 * GROUPS, width), bf16),
            pltpu.VMEM(far.shape, bf16),
            pltpu.VMEM((GROUPS, 4, *kv_block), bf16),
            pltpu.VMEM((GROUPS, 4, *kv_block), bf16),
            pltpu.VMEM((GROUPS, 2, *kv_block), f32),
            pltpu.VMEM((GROUPS, 2, *kv_block), bf16),
            pltpu.VMEM((GROUPS, 2, *kv_block), bf16),
            pltpu.VMEM((GROUPS, *kv_block), bf16),
            pltpu.VMEM((GROUPS, *kv_block), bf16),
            pltpu.VMEM((GROUPS, *full), f32),
            pltpu.VMEM(full, f32),
            pltpu.VMEM((2, GROUPS, *full), bf16),
            pltpu.VMEM((GROUPS, *full), bf16),
            pltpu.VMEM((width, wide_v), f32),
            pltpu.VMEM((GROUPS, *unit), f32),
            pltpu.VMEM(unit, f32),
            pltpu.VMEM((2, GROUPS, *unit), bf16),
            pltpu.VMEM((GROUPS, *unit), bf16),
            pltpu.VMEM(unit, bf16),
            *weight_scratch(wide_q),
            *weight_scratch(wide_v),
            pltpu.VMEM((6, 24, width), f32),
            pltpu.VMEM((8, width), f32),
            pltpu.VMEM((8, width), f32),
            pltpu.VMEM((len(AROUND) + GROUPS - 1, 8, width), f32),
            dma((9,)),
            dma((GROUPS, 4)), dma((GROUPS, 4)), dma((GROUPS, 4)), dma((GROUPS,)), dma((GROUPS,)), dma((GROUPS,)), dma((GROUPS,)),
            dma((GROUPS,)), dma((2, GROUPS)),
            dma((GROUPS,)), dma((2, GROUPS)), dma((2,)), dma((GROUPS,)), dma((GROUPS,)),
            dma((GROUPS,)), dma((GROUPS,)), dma((2, GROUPS)), dma((2, GROUPS)),
            dma((3,)), dma((3,)), dma((2,)), dma((GROUPS,)), dma((GROUPS,)), dma((GROUPS,)), dma((GROUPS,)),
            dma((3,)), dma((3,)), dma((2,)), dma((GROUPS,)), dma((GROUPS,)), dma((GROUPS,)), dma((GROUPS,)),
            dma((6,)), dma((6,)), dma((10,)), dma((10,)), dma((1,)),
        ],
        compiler_params=pltpu.CompilerParams(
            collective_id=2, has_side_effects=True, vmem_limit_bytes=54 << 20
        ),
        name="scatter",
    )(dkv, dq, normed, wfull, tokens, mgrad, keep, over, near, far, small, sums)


def pack_kv(key_part, value_part):
    return jnp.concatenate(
        [key_part, value_part[..., 2 * DH :], value_part[..., : 2 * DH]], axis=-1
    )


def unpack_kv(both):
    return both[..., :HW], jnp.concatenate([both[..., HW + DH :], both[..., HW : HW + DH]], axis=-1)


def layout_kernel(
    big_ref, query_ref, kv_ref, sums_ref, base_ref, got_ref,
    up_out, down_out, wo_out, query_out, key_out, value_out,
    low_gain, low_shift, query_bias, value_bias, out_bias, high_gain, high_shift, up_bias, down_bias, result_out,
):
    x = lax.axis_index("x")
    width = big_ref.shape[-1]
    half = width // 2
    result_out[...] = (base_ref[...] + got_ref[...].astype(f32)).astype(bf16)
    for core in range(2):
        down_out[core] = big_ref[core, 0, 0:96].astype(f32)
        wo_out[core] = big_ref[core, 0, 192:UNIT].astype(f32)
        for owner in range(2):
            lane = (2 * owner + core) * width
            up_out[:, lane : lane + width] = big_ref[core, 0, 96 + 48 * owner : 144 + 48 * owner].astype(f32)
        query_out[core] = jnp.concatenate(
            [query_ref[core, z].astype(f32)[:, :HW] for z in range(GROUPS)], axis=1
        )
        both = [unpack_kv(kv_ref[core, z].astype(f32)) for z in range(GROUPS)]
        key_out[core] = jnp.concatenate([item[0] for item in both], axis=1)
        value_out[core] = jnp.concatenate([item[1] for item in both], axis=1)

    @pl.when(pl.program_id(0) == 0)
    def _():
        def own_half(row):
            whole = sums_ref[row : row + 1]
            return jnp.where(x == 0, whole[:, :half], whole[:, half:]).reshape(half)

        for ref, row in (
            (low_gain, 0), (low_shift, 1), (out_bias, 2), (high_gain, 3), (high_shift, 4), (down_bias, 5),
        ):
            ref[...] = own_half(row)
        pair = [sums_ref[pl.ds(16 + 2 * x + i, 1)] for i in range(2)]
        query_bias[...] = jnp.concatenate([item[:, :HW] for item in pair], axis=1).reshape(half)
        value_bias[...] = jnp.concatenate(
            [unpack_kv(item[:, 2 * BLK : 2 * BLK + 2 * HW])[1] for item in pair], axis=1
        ).reshape(half)
        up_bias[...] = jnp.concatenate(
            [sums_ref[pl.ds(8 + 2 * x + i, 1)] for i in range(2)], axis=1
        ).reshape(2 * width)


def lay_out(big, query, kv, sums, base, got):
    width = big.shape[-1]
    half, fourth = width // 2, width // 4
    rows = fourth // PARTS

    def spec(shape, index):
        return pl.BlockSpec(shape, index)

    def fixed(wide):
        return pl.BlockSpec((wide,), lambda p: (0,))

    narrow = spec((2, rows, width), lambda p: (0, p, 0))
    vector = jax.ShapeDtypeStruct((half,), f32)
    return pl.pallas_call(
        layout_kernel,
        grid=(PARTS,),
        out_shape=(
            jax.ShapeDtypeStruct((half, 4 * width), f32),
            jax.ShapeDtypeStruct((2, width, width), f32),
            *[jax.ShapeDtypeStruct((2, fourth, width), f32)] * 4,
            *[vector] * 7,
            jax.ShapeDtypeStruct((2 * width,), f32),
            vector,
            jax.ShapeDtypeStruct(base.shape, bf16),
        ),
        in_specs=[
            spec((2, 1, UNIT, width), lambda p: (0, p, 0, 0)),
            spec((2, GROUPS, rows, query.shape[-1]), lambda p: (0, 0, p, 0)),
            spec((2, GROUPS, rows, kv.shape[-1]), lambda p: (0, 0, p, 0)),
            spec(sums.shape, lambda p: (0, 0)),
            spec((base.shape[0] // PARTS, width), lambda p: (p, 0)),
            spec((base.shape[0] // PARTS, width), lambda p: (p, 0)),
        ],
        out_specs=(
            spec((48, 4 * width), lambda p: (p, 0)),
            spec((2, 96, width), lambda p: (0, p, 0)),
            *[narrow] * 4,
            *[fixed(half)] * 7,
            fixed(2 * width),
            fixed(half),
            spec((base.shape[0] // PARTS, width), lambda p: (p, 0)),
        ),
        compiler_params=pltpu.CompilerParams(
            vmem_limit_bytes=VMEM_LIMIT, dimension_semantics=("arbitrary",)
        ),
        name="lay_out",
    )(big, query, kv, sums, base, got)


ROWS = ("s", "r", "core", "x")
ALL = ("g", "s", "r", "core", "x")


def shards(
    tokens, cotangent, doc_lengths, deal, first_gain, first_shift, query_weight, query_bias,
    key_weight, value_weight, value_bias, output_weight, output_bias, second_gain, second_shift,
    up_weight, up_bias, down_weight, down_bias,
):
    rows, width = tokens.shape
    half = width // 2
    blocks = deal.shape[0]
    core, x = lax.axis_index("core"), lax.axis_index("x")
    swap = ((0, 1), (1, 0))

    def up_columns(owner):
        return lax.dynamic_slice_in_dim(up_weight, (2 * owner + core) * width, width, 1)

    def stay(*items):
        return tuple(pltpu.with_memory_space_constraint(item, pltpu.HBM) for item in items)

    kv, q, normed, small, wfull, wo = gather(
        *stay(
            tokens, query_weight, key_weight, value_weight, output_weight,
            first_gain, first_shift, output_bias, second_gain, second_shift, down_bias, query_bias, value_bias, up_bias,
        )
    )
    wide = blocks > 8 * 2 * GROUPS
    if wide:
        kv = lax.all_gather(kv, "s", axis=0, tiled=True)
    kv = kv.reshape(blocks, BLK, 2 * HW)
    q = q.reshape(2 * GROUPS, BLK, 2 * BLK)
    up_other, kv = lax.optimization_barrier((up_columns(1 - x), kv))
    up_other = lax.ppermute(up_other, "x", swap)
    out_t, kept, lse = attend_forward(deal, doc_lengths, q, kv)
    base, x_give, grad_middle, grad_t, kept_part, over, far, sums = dense(
        out_t, tokens, cotangent, small, wo, up_columns(x), up_other, down_weight
    )
    over = lax.ppermute(over, "r", swap)
    x_got = lax.ppermute(x_give, "x", swap)
    far = lax.ppermute(far, ("r", "x"), ((0, 3), (1, 2), (2, 1), (3, 0)))
    dq, dkv = attend_backward(deal, doc_lengths, q, kv, lse, grad_t, kept)
    dkv = dkv.reshape(-1, GROUPS, rows, 2 * HW)
    if wide:
        dkv = lax.psum_scatter(dkv, "s", scatter_dimension=0, tiled=True)
    dq = dq.reshape(GROUPS, rows, 2 * BLK)
    grad_tokens, big, query_own, kv_own, sums = scatter(
        *stay(dkv, dq, normed, wfull, tokens, grad_middle), small, *stay(kept_part, over, x_got, far), sums
    )
    if wide:
        big, query_own, kv_own, sums = (
            lax.psum(item, "s") for item in (big, query_own, kv_own, sums)
        )

    (
        up_own, down_own, wo_own, query_own, key_own, value_own,
        low_gain, low_shift, query_sum, value_sum, out_sum, high_gain, high_shift, up_sum, down_sum, result,
    ) = lay_out(big.reshape(2, PARTS, UNIT, width), query_own, kv_own, sums, *stay(base, x_got))

    def flat(item):
        return item.reshape(-1, width)

    return (
        result,
        grad_tokens,
        low_gain,
        low_shift,
        flat(query_own),
        query_sum,
        flat(key_own),
        flat(value_own),
        value_sum,
        flat(wo_own),
        out_sum,
        high_gain,
        high_shift,
        up_own,
        up_sum,
        flat(down_own),
        down_sum,
    )


def solution(mesh):
    devices = mesh.devices
    inner_mesh = Mesh(devices.reshape(GROUPS, devices.shape[0] // (4 * GROUPS), 2, 2, 2), ALL)
    row = P(ALL, None)
    mat = P("x", None)
    vec = P("x")
    in_specs = (
        row, row, P(), P(), vec, vec, mat, vec, mat, mat, vec, mat, vec, vec, vec, mat, vec, mat, vec,
    )
    out_specs = (
        row, row, vec, vec, mat, vec, mat, mat, vec, mat, vec, vec, vec, mat, vec, mat, vec,
    )
    return jax.shard_map(
        shards, mesh=inner_mesh, in_specs=in_specs, out_specs=out_specs, check_vma=False
    )
```

```python
import jax
import jax.numpy as jnp
from jax import lax
from jax.experimental import pallas as pl
from jax.experimental.pallas import tpu as pltpu
from jax.sharding import Mesh
from jax.sharding import PartitionSpec as P

HEADS = 12
DH = 64
NSUM = 50
SEG = 2048
BLK = 128
GROUPS = 4
PER = HEADS // GROUPS
HW = PER * DH
WIDE = PER * BLK
CHUNK = 2 * BLK
DEPTH = 8
EPS = 1e-05
SCALE = 0.125
MASKED = -1e30
ROOT_HALF = 0.7071067811865476
PDF_SCALE = 0.3989422804014327
VMEM_LIMIT = 56 << 20
bf16 = jnp.bfloat16
f32 = jnp.float32


def layer_norm(values, gain, shift):
    mean = jnp.mean(values, axis=-1, keepdims=True)
    centred = values - mean
    spread = jnp.mean(centred * centred, axis=-1, keepdims=True)
    return centred * lax.rsqrt(spread + EPS) * gain + shift


def outer(left, right):
    return lax.dot_general(left, right, (((0,), (0,)), ((), ())), preferred_element_type=f32)


def inner(left, right):
    return lax.dot_general(left, right, (((1,), (1,)), ((), ())), preferred_element_type=f32)


def dot(left, right):
    return jnp.dot(left, right, preferred_element_type=f32)


def survey(deal_ref, lengths_ref, where_ref, text_ref, low_ref, high_ref, first_ref):
    blocks = deal_ref.shape[0]
    per_group = blocks // (2 * GROUPS)
    rest = lax.axis_index(ROWS)

    def note(j, kept):
        pair = j // 2
        group = pair // per_group
        where_ref[deal_ref[j]] = ((pair - group * per_group) * GROUPS + group) * 2 + j % 2
        return kept

    lax.fori_loop(0, blocks, note, 0)
    starts = [jnp.int32(0)]
    for doc in range(lengths_ref.shape[0] - 1):
        starts.append(starts[-1] + lengths_ref[doc])

    def first_of(at):
        begin = jnp.zeros_like(at)
        for start in starts:
            begin = jnp.where(start <= at, jnp.maximum(begin, start), begin)
        return jnp.where(at - begin >= SEG + NSUM, begin + SEG, begin)

    for slot in range(2 * GROUPS):
        text = deal_ref[2 * ((slot // 2) * per_group + rest) + slot % 2]
        text_ref[slot] = text
        low_ref[slot] = first_of(text * BLK) // CHUNK
        high_ref[slot] = text // 2
        first_ref[slot] = first_of(text * BLK + lax.broadcasted_iota(jnp.int32, (1, BLK), 1))


def survey_scratch(blocks):
    slots = 2 * GROUPS
    return [
        pltpu.SMEM((blocks,), jnp.int32),
        pltpu.SMEM((slots,), jnp.int32),
        pltpu.SMEM((slots,), jnp.int32),
        pltpu.SMEM((slots,), jnp.int32),
        pltpu.VMEM((slots, 1, BLK), jnp.int32),
    ]


def spread_heads_t(part_t, order):
    rows = []
    zero = jnp.zeros((DH, BLK), part_t.dtype)
    for head in order:
        if head is None:
            rows.append(jnp.zeros((DH, WIDE), part_t.dtype))
        else:
            piece = part_t[DH * head : DH * head + DH]
            rows.append(
                jnp.concatenate([piece if h == head else zero for h in range(PER)], axis=1)
            )
    return jnp.concatenate(rows, axis=0)


K_ORDER = (0, 1, 2, None)
V_ORDER = (None, 2, 0, 1)


def visible(chunk, first, own):
    at = chunk * CHUNK + lax.broadcasted_iota(jnp.int32, (CHUNK, BLK), 0)
    allowed = (at >= first) & (at <= own)
    return jnp.concatenate([allowed] * PER, axis=1)


def load_chunk(kv_ref, where_ref, chunk):
    return jnp.concatenate(
        [kv_ref[where_ref[2 * chunk]], kv_ref[where_ref[2 * chunk + 1]]], axis=0
    )


def forward_kernel(
    deal_ref, lengths_ref, q_ref, kv_ref,
    out_ref, wide_ref, lse_ref,
    where_ref, text_ref, low_ref, high_ref, first_ref, acc_ref,
):
    survey(deal_ref, lengths_ref, where_ref, text_ref, low_ref, high_ref, first_ref)

    def one_slot(slot, kept):
        wide_q = spread_heads_t(q_ref[slot].T[:HW], K_ORDER)
        first = first_ref[slot]
        own = text_ref[slot] * BLK + lax.broadcasted_iota(jnp.int32, (1, BLK), 1)
        last_first = jnp.max(first)
        acc_ref[...] = jnp.zeros_like(acc_ref)

        def step(double, carry):
            top, total = carry
            scores = []
            for part in range(2):
                keys = load_chunk(kv_ref, where_ref, 2 * double + part)[:, : 2 * BLK]
                scores.append(jnp.where(visible(2 * double + part, first, own), dot(keys, wide_q), MASKED))
            scores = jnp.concatenate(scores, axis=0)
            fresh = jnp.maximum(top, jnp.max(scores, axis=0, keepdims=True))
            expo = jnp.exp(scores - fresh)
            shrink = jnp.exp(top - fresh)
            total = total * shrink + jnp.sum(expo, axis=0, keepdims=True)
            vals = jnp.concatenate([load_chunk(kv_ref, where_ref, 2 * double + part)[:, BLK:] for part in range(2)], axis=0)
            acc_ref[...] = acc_ref[...] * shrink + outer(vals, expo.astype(bf16))
            return fresh, total

        top, total = lax.fori_loop(
            low_ref[slot] // 2,
            high_ref[slot] // 2 + 1,
            step,
            (jnp.full((1, WIDE), MASKED, f32), jnp.zeros((1, WIDE), f32)),
        )
        lse_ref[slot] = top + jnp.log(total)
        scaled = acc_ref[...] / total
        pieces = []
        for head in range(PER):
            row = DH * V_ORDER.index(head)
            pieces.append(scaled[row : row + DH, BLK * head : BLK * head + BLK])
        whole = jnp.concatenate(pieces, axis=0)
        wide_ref[slot] = whole
        out_ref[slot] = whole.astype(bf16)
        return kept

    lax.fori_loop(0, q_ref.shape[0], one_slot, 0)


def whole_vmem():
    return pl.BlockSpec(memory_space=pltpu.VMEM)


def whole_smem():
    return pl.BlockSpec(memory_space=pltpu.SMEM)


def attend_forward(deal, lengths, q, kv):
    slots = q.shape[0]
    blocks = kv.shape[0]
    return pl.pallas_call(
        forward_kernel,
        out_shape=(
            jax.ShapeDtypeStruct((slots, HW, BLK), bf16),
            jax.ShapeDtypeStruct((slots, HW, BLK), f32),
            jax.ShapeDtypeStruct((slots, 1, WIDE), f32),
        ),
        in_specs=[whole_smem()] * 2 + [whole_vmem()] * 2,
        out_specs=(whole_vmem(),) * 3,
        scratch_shapes=[
            *survey_scratch(blocks),
            pltpu.VMEM((2 * BLK, WIDE), f32),
        ],
        compiler_params=pltpu.CompilerParams(vmem_limit_bytes=(6 << 20) + kv.size // 5 * 16),
        name="attend_forward",
    )(deal, lengths, q, kv)


def backward_kernel(
    deal_ref, lengths_ref, q_ref, kv_ref, lse_ref, do_ref, wide_ref,
    dq_ref, dkv_ref, where_ref, text_ref, low_ref, high_ref, first_ref, qt_ref, qm_ref, dot_ref, dom_ref, delta_ref, acc_ref, dk_acc, dv_acc,
    packed_ref, count_ref, list_ref, out_sem,
):
    survey(deal_ref, lengths_ref, where_ref, text_ref, low_ref, high_ref, first_ref)
    slots = q_ref.shape[0]
    chunks = kv_ref.shape[0] // 2

    def ready(slot, _):
        q = q_ref[slot]
        qt_ref[slot] = spread_heads_t(q.T[:HW], K_ORDER)
        lane = lax.broadcasted_iota(jnp.int32, (BLK, 2 * BLK), 1) // DH
        zero = jnp.zeros_like(q)
        qm_ref[slot] = jnp.concatenate(
            [jnp.where(lane == K_ORDER.index(h), q, zero) for h in range(PER)], axis=0
        )
        grad_t = do_ref[slot]
        dot_ref[slot] = spread_heads_t(grad_t, V_ORDER)
        ordered = jnp.concatenate(
            [
                jnp.zeros((DH, BLK), bf16) if h is None else grad_t[DH * h : DH * h + DH]
                for h in V_ORDER
            ],
            axis=0,
        ).T
        dom_ref[slot] = jnp.concatenate(
            [jnp.where(lane == V_ORDER.index(h), ordered, zero) for h in range(PER)], axis=0
        )
        both = grad_t.astype(f32) * wide_ref[slot]
        delta_ref[slot] = jnp.concatenate(
            [jnp.sum(both[DH * h : DH * h + DH], axis=0, keepdims=True) for h in range(PER)],
            axis=1,
        )
        acc_ref[slot] = jnp.zeros((HW, WIDE), f32)
        return _

    lax.fori_loop(0, slots, ready, 0)

    def clear(chunk, kept):
        count_ref[chunk] = 0
        return kept

    lax.fori_loop(0, chunks, clear, 0)

    def enlist(slot, kept):
        def seen(chunk, kept):
            count = count_ref[chunk]
            list_ref[chunk * slots + count] = slot
            count_ref[chunk] = count + 1
            return kept

        lax.fori_loop(low_ref[slot], high_ref[slot] + 1, seen, 0)
        return kept

    lax.fori_loop(0, slots, enlist, 0)

    def written(chunk, i):
        return pltpu.make_async_copy(
            packed_ref.at[chunk % DEPTH, i], dkv_ref.at[where_ref[2 * chunk + i]], out_sem.at[chunk % DEPTH, i]
        )

    def one_chunk(chunk, kept):
        part = load_chunk(kv_ref, where_ref, chunk)
        keys = part[:, : 2 * BLK]
        vals = part[:, BLK:]
        keys_t = keys.T[:HW]
        dk_acc[...] = jnp.zeros_like(dk_acc)
        dv_acc[...] = jnp.zeros_like(dv_acc)

        def one_slot(i, kept):
            for half in range(2):
                attend(list_ref[chunk * slots + 2 * i + half])
            return kept

        def attend(slot):
            own = text_ref[slot] * BLK + lax.broadcasted_iota(jnp.int32, (1, BLK), 1)
            scores = dot(keys, qt_ref[slot])
            dprobs = dot(vals, dot_ref[slot])
            probs = jnp.where(visible(chunk, first_ref[slot], own), jnp.exp(scores - lse_ref[slot]), 0.0)
            dscores = (probs * (dprobs - delta_ref[slot])).astype(bf16)
            dv_acc[...] += dot(probs.astype(bf16), dom_ref[slot])
            dk_acc[...] += dot(dscores, qm_ref[slot])
            acc_ref[slot] += dot(keys_t, dscores)

        lax.fori_loop(0, count_ref[chunk] // 2, one_slot, 0)
        pl.when(count_ref[chunk] % 2 == 1)(lambda: attend(list_ref[chunk * slots + count_ref[chunk] - 1]))
        packed = jnp.concatenate(
            [
                dk_acc[:, :BLK],
                dk_acc[:, BLK:] + dv_acc[:, :BLK],
                dv_acc[:, BLK:],
            ],
            axis=1,
        ).astype(bf16)

        @pl.when(chunk >= DEPTH)
        def _():
            for i in range(2):
                written(chunk - DEPTH, i).wait()

        for i in range(2):
            packed_ref[chunk % DEPTH, i] = packed[BLK * i : BLK * i + BLK]
            written(chunk, i).start()
        return kept

    lax.fori_loop(0, chunks, one_chunk, 0)
    for last in range(DEPTH):
        for i in range(2):
            written(chunks - DEPTH + last, i).wait()

    def finish(slot, _):
        total = acc_ref[slot]
        kept = jnp.concatenate(
            [total[DH * h : DH * h + DH, BLK * h : BLK * h + BLK] for h in range(PER)]
            + [jnp.zeros((DH, BLK), f32)],
            axis=0,
        )
        dq_ref[slot] = kept.T.astype(bf16)
        return _

    lax.fori_loop(0, slots, finish, 0)


def attend_backward(deal, lengths, q, kv, lse, grad_t, wide):
    slots = q.shape[0]
    return pl.pallas_call(
        backward_kernel,
        out_shape=(
            jax.ShapeDtypeStruct((slots, BLK, 2 * BLK), bf16),
            jax.ShapeDtypeStruct(kv.shape, bf16),
        ),
        in_specs=[whole_smem()] * 2 + [whole_vmem()] * 5,
        out_specs=(whole_vmem(), in_hbm()),
        scratch_shapes=[
            *survey_scratch(kv.shape[0]),
            pltpu.VMEM((slots, 2 * BLK, WIDE), bf16),
            pltpu.VMEM((slots, WIDE, 2 * BLK), bf16),
            pltpu.VMEM((slots, 2 * BLK, WIDE), bf16),
            pltpu.VMEM((slots, WIDE, 2 * BLK), bf16),
            pltpu.VMEM((slots, 1, WIDE), f32),
            pltpu.VMEM((slots, HW, WIDE), f32),
            pltpu.VMEM((CHUNK, 2 * BLK), f32),
            pltpu.VMEM((CHUNK, 2 * BLK), f32),
            pltpu.VMEM((DEPTH, 2, BLK, 2 * HW), bf16),
            pltpu.SMEM((kv.shape[0] // 2,), jnp.int32),
            pltpu.SMEM((kv.shape[0] // 2 * slots,), jnp.int32),
            pltpu.SemaphoreType.DMA((DEPTH, 2)),
        ],
        compiler_params=pltpu.CompilerParams(
            vmem_limit_bytes=max(46 << 20, (17 << 20) + kv.size * 2)
        ),
        name="attend_backward",
    )(deal, lengths, q, kv, lse, grad_t, wide)


MESH = pl.DeviceIdType.MESH


def send(src, dst, out_sem, in_sem, **device):
    return pltpu.make_async_remote_copy(
        src_ref=src, dst_ref=dst, send_sem=out_sem, recv_sem=in_sem, device_id=device, device_id_type=MESH
    )


def place():
    return tuple(lax.axis_index(name) for name in ("g", "r", "core", "x"))


def seat(r, core, x):
    return (r * 2 + core) * 2 + x


AROUND = ((0, 0, 1), (0, 1, 0), (0, 1, 1), (1, 0, 0), (1, 0, 1), (1, 1, 0), (1, 1, 1))


def neighbour(r, core, x, step):
    dr, dc, dx = AROUND[step]
    return {"r": 1 - r if dr else r, "core": 1 - core if dc else core, "x": 1 - x if dx else x}


def greet(g, r, core, x, line, around=False):
    barrier = pltpu.get_barrier_semaphore()

    def hello(**device):
        pl.semaphore_signal(barrier, inc=1, device_id=device, device_id_type=MESH)

    if around:
        for step in range(len(AROUND)):
            hello(**neighbour(r, core, x, step))
    else:
        hello(core=1 - core)
        hello(x=1 - x)
        hello(r=1 - r)
    near = len(AROUND) if around else 3
    if line:
        for away in range(1, GROUPS):
            hello(g=lax.rem(g + away, GROUPS))
        pl.semaphore_wait(barrier, near + GROUPS - 1)
    else:
        pl.when(g > 0)(lambda: hello(g=g - 1))
        pl.when(g < GROUPS - 1)(lambda: hello(g=g + 1))
        pl.semaphore_wait(barrier, near + 2 - jnp.where(g == 0, 1, 0) - jnp.where(g == GROUPS - 1, 1, 0))


NEAREST = ((0, 1, 2, 3), (1, 2, 0, 3), (2, 1, 3, 0), (3, 2, 1, 0))


def nearest(g, step):
    picked = NEAREST[0][step]
    for z in range(1, GROUPS):
        picked = jnp.where(g == z, NEAREST[z][step], picked)
    return picked


def prepare(g, x, weights, lines, narrow_ref, small_ref):
    half = weights.shape[1]
    odd = lax.rem(g, 2) == 1

    def columns(i):
        low = pl.multiple_of(3 * g // 2 * BLK, BLK)
        window = weights[i, :, pl.ds(low, 2 * BLK)]
        moved = jnp.concatenate([window[:, DH:], window[:, :DH]], axis=1)
        return jnp.where(odd, moved, window)

    lane = lax.broadcasted_iota(jnp.int32, (half, 2 * BLK), 1)
    query = columns(0)
    narrow_ref[:, : 2 * BLK] = jnp.where(lane < HW, query, jnp.zeros_like(query))
    narrow_ref[:, 2 * BLK :] = pack_kv(columns(1)[:, :HW], columns(2)[:, :HW])

    def line(i):
        return lines[i][...].astype(f32).reshape(1, -1)

    zero = jnp.zeros((1, half), f32)
    small_ref[...] = jnp.zeros_like(small_ref)
    for row in range(6):
        small_ref[row : row + 1] = jnp.where(
            x == 0, jnp.concatenate([line(row), zero], axis=1), jnp.concatenate([zero, line(row)], axis=1)
        )
    ups = line(8)
    for i in range(2):
        small_ref[pl.ds(8 + 2 * x + i, 1)] = ups[:, 2 * half * i : 2 * half * i + 2 * half]

    def part(i):
        mine = jnp.where(odd, line(i)[:, HW:], line(i)[:, :HW])
        return jnp.where(g // 2 == x, mine, jnp.zeros_like(mine))

    value = part(7)
    small_ref[12:13] = jnp.concatenate(
        [part(6), jnp.zeros((1, 2 * BLK), f32), value[:, 2 * DH :], value[:, : 2 * DH], jnp.zeros((1, BLK), f32)], axis=1
    )


def gather_kernel(
    tokens_ref, query_any, key_any, value_any, wo_ref, l0, l1, l2, l3, l4, l5, l6, l7, l8,
    kv_ref, q_ref, normed_ref, small_out, wfull, wo_out,
    lined, attn_w, narrow_ref, small_ref, small_in, kvs,
    z_own, z_send, z_recv, s_sem, n_send, n_recv, kv_send, kv_recv, kv_local, w_send, w_recv, w_local, a_sem,
):
    g, r, core, x = place()
    other = 1 - x
    rows, width = tokens_ref.shape
    half = width // 2
    fourth = half // 2
    eighth = half // 4
    loads = [
        pltpu.make_async_copy(ref, attn_w.at[i], a_sem.at[i]) for i, ref in enumerate((query_any, key_any, value_any))
    ]
    for load in loads:
        load.start()
    greet(g, r, core, x, False)

    def half_of(source, part):
        return lined.at[source, pl.ds(BLK * part, BLK)]

    def along(source, part, away, sem):
        return send(half_of(source, part), half_of(source, part), sem, z_recv.at[source, part], g=g + away)

    lined[g] = tokens_ref[...]
    for part in range(2):
        pl.when(g > 0)(lambda: along(g, part, -1, z_own.at[0, part]).start())
        pl.when(g < GROUPS - 1)(lambda: along(g, part, 1, z_own.at[1, part]).start())

    for load in loads:
        load.wait()
    prepare(g, x, attn_w, (l0, l1, l2, l3, l4, l5, l6, l7, l8), narrow_ref, small_ref)
    small_move = send(small_ref, small_in, s_sem.at[0], s_sem.at[1], x=other)
    small_move.start()
    mine = pl.ds(x * half + core * fourth, fourth)
    narrow_x = send(narrow_ref.at[pl.ds(core * fourth, fourth)], wfull.at[mine], n_send.at[0], n_recv.at[0], x=other)
    narrow_x.start()

    def wo_rows(owner, part):
        return wo_out.at[pl.ds(owner * half + core * fourth + part * eighth, eighth)]

    wo_x = send(wo_ref.at[pl.ds(core * fourth + r * eighth, eighth)], wo_rows(x, r), w_send.at[0], w_recv.at[0], x=other)
    wo_y = send(wo_rows(other, r), wo_rows(other, r), w_send.at[3], w_recv.at[3], r=1 - r)
    wo_s = [
        send(wo_rows(other, part), wo_rows(other, part), w_send.at[6 + i], w_recv.at[6 + i], core=1 - core)
        for i, part in enumerate((r, 1 - r))
    ]
    wo_x.start()
    locals_ = [pltpu.make_async_copy(wo_ref, wo_out.at[pl.ds(x * half, half)], w_local.at[0])]
    for item in locals_:
        item.start()

    wfull[pl.ds(x * half, half)] = narrow_ref[...]
    narrow_x.wait_recv()
    theirs = wfull.at[pl.ds(other * half + core * fourth, fourth)]
    narrow_s = send(theirs, theirs, n_send.at[1], n_recv.at[1], core=1 - core)
    narrow_s.start()
    small_move.wait_recv()
    small_out[...] = small_ref[...] + small_in[...]
    narrow_s.wait_recv()

    own = seat(r, core, x)

    def span(step):
        return (step, 0, rows) if step < GROUPS - 1 else (GROUPS - 1, BLK * (step - GROUPS + 1), BLK)

    def block(owner, step):
        nth, low, count = span(step)
        return kv_ref.at[owner, nearest(g, nth), pl.ds(low, count)]

    def made(step):
        nth, low, count = span(step)
        return kvs.at[nth, pl.ds(low, count)]

    def push(step, kind, src, dst, **device):
        send(src, dst, kv_send.at[kind, step], kv_recv.at[kind, step], **device).start()

    def settle(step, kind, owner):
        arrived(block(owner, step), kv_send.at[kind, step], kv_recv.at[kind, step], x)

    def forward(step):
        by_x = block(seat(r, core, other), step)
        settle(step, 0, seat(r, core, other))
        if step % 2 == 0:
            push(step, 3, by_x, by_x, r=1 - r)
        push(step, 4, by_x, by_x, core=1 - core)
        by_y = block(seat(1 - r, core, x), step)
        settle(step, 1, seat(1 - r, core, x))
        if step % 2 == 1:
            push(step, 3, by_y, by_y, x=other)
        push(step, 5, by_y, by_y, core=1 - core)

    def forward_far(step):
        far = block(seat(1 - r, core, other), step)
        settle(step, 3, seat(1 - r, core, other))
        push(step, 6, far, far, core=1 - core)

    def take(nth, part):
        source = nearest(g, nth)
        arrived(half_of(source, part), z_send.at[source, part], z_recv.at[source, part], x)
        pl.when((source < g) & (g < GROUPS - 1))(lambda: along(source, part, 1, z_send.at[source, part]).start())
        pl.when((source > g) & (g > 0))(lambda: along(source, part, -1, z_send.at[source, part]).start())

    def project(step):
        nth, low, count = span(step)
        source = nearest(g, nth)
        taken = pl.ds(low, count)
        values = lined[source, taken].astype(f32)
        normed = layer_norm(values, small_out[0:1], small_out[1:2]).astype(bf16)
        normed_ref[source, taken] = normed
        both = dot(normed, wfull[...]) + small_out[12:13, : wfull.shape[1]]
        kvs[nth, taken] = both[:, 2 * BLK :].astype(bf16)
        push(step, 0, made(step), block(own, step), x=other)
        push(step, 1, made(step), block(own, step), r=1 - r)
        push(step, 2, made(step), block(own, step), core=1 - core)
        q_ref[source, taken] = (both[:, : 2 * BLK] * SCALE).astype(bf16)
        pltpu.make_async_copy(made(step), block(own, step), kv_local.at[step]).start()

    at_end = (g == 0) | (g == GROUPS - 1)
    between = jnp.logical_not(at_end)
    project(0)
    take(1, 0)
    take(1, 1)

    @pl.when(between)
    def _():
        take(2, 0)
        take(2, 1)

    project(1)
    forward(0)

    @pl.when(at_end)
    def _():
        take(2, 0)
        take(2, 1)

    project(2)

    @pl.when(at_end)
    def _():
        forward(1)
        forward_far(0)

    take(3, 0)
    pl.when(between)(lambda: take(3, 1))
    project(3)
    pl.when(at_end)(lambda: take(3, 1))
    project(4)

    @pl.when(between)
    def _():
        forward(1)
        forward_far(0)

    wo_x.wait_recv()
    wo_y.start()
    wo_s[0].start()
    forward(2)
    forward_far(1)
    forward(3)
    forward_far(2)
    forward(4)
    forward_far(3)
    arrived(wo_rows(other, 1 - r), w_send.at[3], w_recv.at[3], x)
    wo_s[1].start()
    forward_far(4)

    for step in range(GROUPS + 1):
        pltpu.make_async_copy(made(step), block(own, step), kv_local.at[step]).wait()
        settle(step, 2, seat(r, 1 - core, x))
        settle(step, 4, seat(r, 1 - core, other))
        settle(step, 5, seat(1 - r, 1 - core, x))
        settle(step, 6, seat(1 - r, 1 - core, other))
        for kind in range(7):
            left(made(step), kv_send.at[kind, step], kv_recv.at[kind, step], x)
    for part in range(2):
        pl.when(g > 0)(lambda: left(half_of(g, part), z_own.at[0, part], z_recv.at[g, part], x))
        pl.when(g < GROUPS - 1)(lambda: left(half_of(g, part), z_own.at[1, part], z_recv.at[g, part], x))
        for nth in range(1, GROUPS):
            source = nearest(g, nth)
            passed = ((source < g) & (g < GROUPS - 1)) | ((source > g) & (g > 0))
            pl.when(passed)(
                lambda: left(half_of(source, part), z_send.at[source, part], z_recv.at[source, part], x)
            )
    small_move.wait_send()
    narrow_x.wait_send()
    narrow_s.wait_send()
    for item in locals_:
        item.wait()
    for item in (wo_x, wo_y, *wo_s):
        item.wait_send()
    for i, part in enumerate((r, 1 - r)):
        there = wo_out.at[pl.ds(other * half + (1 - core) * fourth + part * eighth, eighth)]
        send(there, there, w_send.at[6 + i], w_recv.at[6 + i], core=1 - core).wait_recv()


def anywhere():
    return pl.BlockSpec(memory_space=pl.ANY)


def in_hbm():
    return pl.BlockSpec(memory_space=pltpu.HBM)


def gather(tokens, query, key, value, wo, *lines):
    rows, width = tokens.shape
    wide = 2 * BLK + 2 * HW
    small = (16, width)
    dma = pltpu.SemaphoreType.DMA
    return pl.pallas_call(
        gather_kernel,
        out_shape=(
            jax.ShapeDtypeStruct((8, GROUPS, rows, 2 * HW), bf16),
            jax.ShapeDtypeStruct((GROUPS, rows, 2 * BLK), bf16),
            jax.ShapeDtypeStruct((GROUPS, rows, width), bf16),
            jax.ShapeDtypeStruct(small, f32),
            jax.ShapeDtypeStruct((width, wide), bf16),
            jax.ShapeDtypeStruct((width, width), bf16),
        ),
        in_specs=[whole_vmem(), *[in_hbm()] * 4, *[whole_vmem()] * len(lines)],
        out_specs=(anywhere(), *(whole_vmem(),) * 5),
        scratch_shapes=[
            pltpu.VMEM((GROUPS, rows, width), bf16),
            pltpu.VMEM((3, width // 2, width), bf16),
            pltpu.VMEM((width // 2, wide), bf16),
            pltpu.VMEM(small, f32),
            pltpu.VMEM(small, f32),
            pltpu.VMEM((GROUPS, rows, 2 * HW), bf16),
            dma((2, 2)), dma((GROUPS, 2)), dma((GROUPS, 2)), dma((2,)), dma((2,)), dma((2,)),
            dma((7, GROUPS + 1)), dma((7, GROUPS + 1)), dma((GROUPS + 1,)), dma((8,)), dma((8,)), dma((2,)), dma((3,)),
        ],
        compiler_params=pltpu.CompilerParams(
            collective_id=0, has_side_effects=True, vmem_limit_bytes=16 << 20
        ),
        name="gather",
    )(tokens, query, key, value, wo, *lines)


def erf_parts(values):
    below = 0.5 * (1.0 + lax.erf(values * ROOT_HALF))
    return below, PDF_SCALE * jnp.exp(-0.5 * values * values)


PARTS = 8
UNIT = 216
KEPT = 168


def dense_kernel(
    out_t_ref, tokens_ref, cot_ref, small_ref, wo_ref, up_mine, up_other, down_any,
    base_ref, x_give_ref, middle_grad_ref, grad_t_ref, keep_ref, give_ref, far_ref, sums_ref,
    down_ref, up_ref, attn_in, attn_t, cots, h2s, mid_ref, n2_ref, scales, part_y, part_d, in_y, in_d, pass_y, pass_d,
    x_y, x_d, hids, dus, branch_ref, grad_out, wo_keep, wo_give, wo_in, wo_pass, wo_x,
    l_sem, a_send, a_recv, c_send, c_recv, h_send, h_recv, y_send, y_recv, d_send, d_recv, o_send, o_recv,
    w_send, w_recv,
):
    g, r, core, x = place()
    other, sib = 1 - x, 1 - core
    rows, width = tokens_ref.shape
    half = width // 2
    fourth = half // 2
    loads = [
        pltpu.make_async_copy(
            down_any.at[pl.ds(pl.multiple_of(core * width, width), width)], down_ref, l_sem.at[0]
        ),
        pltpu.make_async_copy(up_mine, up_ref.at[pl.ds(x * half, half)], l_sem.at[1]),
        pltpu.make_async_copy(up_other, up_ref.at[pl.ds(other * half, half)], l_sem.at[2]),
    ]
    for load in loads:
        load.start()
    greet(g, r, core, x, True)
    pending = []

    def begin(src, dst, out_sem, in_sem, **device):
        move = send(src, dst, out_sem, in_sem, **device)
        move.start()
        pending.append(move)
        return move

    def other_group(away):
        return lax.rem(g + away, GROUPS)

    def rows_of(b):
        return pl.ds(BLK * b, BLK)

    for b in range(2):
        for away in range(1, GROUPS):
            to = other_group(away)
            begin(out_t_ref.at[2 * to + b], attn_in.at[g, b], a_send.at[b, away], a_recv.at[b, g], g=to)
        attn_in[g, b] = out_t_ref[2 * g + b]
        cots[b, 0] = cot_ref[rows_of(b)]
    cot_x = begin(cots.at[:, 0], cots.at[:, 2], c_send.at[2], c_recv.at[2], x=other)
    cot_moves = [begin(cots.at[:, 0], cots.at[:, 1], c_send.at[0], c_recv.at[0], core=sib)]
    sums_ref[...] = jnp.zeros_like(sums_ref)
    sums_ref[5:6] = jnp.sum(cot_ref[...].astype(f32), axis=0, keepdims=True)
    h2_moves = []

    def norm(b):
        for away in range(1, GROUPS):
            source = other_group(away)
            arrived(attn_in.at[source, b], a_send.at[b, away], a_recv.at[b, source], x)
        for source in range(GROUPS):
            attn_t[HW * source : HW * source + HW, BLK * b : BLK * b + BLK] = attn_in[source, b]
        middle = (
            tokens_ref[rows_of(b)].astype(f32)
            + outer(attn_t[:, BLK * b : BLK * b + BLK], wo_ref[...])
            + small_ref[2:3]
        )
        mid_ref[b] = middle
        mean = jnp.mean(middle, axis=-1, keepdims=True)
        centred = middle - mean
        scale = lax.rsqrt(jnp.mean(centred * centred, axis=-1, keepdims=True) + EPS)
        scales[b] = scale
        n2_ref[b] = centred * scale
        h2s[b, 0] = (n2_ref[b] * small_ref[3:4] + small_ref[4:5]).astype(bf16)
        h2_moves.append(
            (
                begin(h2s.at[b, 0], h2s.at[b, 2], h_send.at[b, 1], h_recv.at[b, 1], x=other),
                begin(h2s.at[b, 0], h2s.at[b, 1], h_send.at[b, 0], h_recv.at[b, 0], core=sib),
            )
        )

    def pass_on(b):
        h2_moves[b][0].wait_recv()
        return begin(h2s.at[b, 2], h2s.at[b, 3], h_send.at[b, 2], h_recv.at[b, 2], core=sib)

    bias_row = 8 + 2 * x + core

    def pair_of(ref, b, pair):
        return ref[b, 2 * pair : 2 * pair + 2].reshape(2 * BLK, width)

    def forward_backward(b, pair):
        cot = pair_of(cots, b, pair)
        expanded = dot(pair_of(h2s, b, pair), up_ref[...]) + small_ref[pl.ds(bias_row, 1)]
        below, density = erf_parts(expanded)
        hidden = (expanded * below).astype(bf16)
        hids[b, pair] = hidden
        slope = below + expanded * density
        grad_hidden = inner(cot, down_ref[...]).astype(bf16).astype(f32)
        grad_expand = (grad_hidden * slope).astype(bf16)
        dus[b, pair] = grad_expand
        part_d[b, pair] = inner(grad_expand, up_ref[...])
        part_y[b, pair] = dot(hidden, down_ref[...])
        sums_ref[pl.ds(bias_row, 1)] += jnp.sum(grad_expand.astype(f32), axis=0, keepdims=True)

    d_moves, y_passes = [None, None], [None, None]

    def near_pair(b):
        if b == 0:
            cot_moves[0].wait_recv()
        h2_moves[b][1].wait_recv()
        forward_backward(b, 0)
        return begin(part_d.at[b, 0, pl.ds(BLK, BLK)], in_d.at[b], d_send.at[b, 0], d_recv.at[b, 0], core=sib)

    def far_pair(b, passed):
        if b == 0:
            cot_moves[1].wait_recv()
        passed.wait_recv()
        forward_backward(b, 1)
        x_d[b, 0] = part_d[b, 1, BLK:].astype(bf16)
        across = begin(x_d.at[b, 0], pass_d.at[b], d_send.at[b, 1], d_recv.at[b, 1], core=sib)
        x_y[b] = part_y[b, 1, BLK:].astype(bf16)
        y_passes[b] = begin(x_y.at[b], pass_y.at[b], y_send.at[b, 1], y_recv.at[b, 1], core=sib)
        across.wait_recv()
        x_d[b, 1] = (part_d[b, 1, :BLK] + pass_d[b].astype(f32)).astype(bf16)
        return begin(x_d.at[b, 1], x_d.at[b, 2], d_send.at[b, 2], d_recv.at[b, 2], x=other)

    def back(b, near, far):
        near.wait_recv()
        far.wait_recv()
        grad_second = part_d[b, 0, :BLK] + in_d[b] + x_d[b, 2].astype(f32)
        n2 = n2_ref[b]
        sums_ref[3:4] += jnp.sum(grad_second * n2, axis=0, keepdims=True)
        sums_ref[4:5] += jnp.sum(grad_second, axis=0, keepdims=True)
        pulled = grad_second * small_ref[3:4]
        inward = (
            pulled - jnp.mean(pulled, axis=-1, keepdims=True) - n2 * jnp.mean(pulled * n2, axis=-1, keepdims=True)
        )
        grad_middle = cot_ref[rows_of(b)].astype(f32) + inward * scales[b]
        middle_grad_ref[rows_of(b)] = grad_middle
        branch = grad_middle.astype(bf16)
        branch_ref[rows_of(b)] = branch
        sums_ref[2:3] += jnp.sum(branch.astype(f32), axis=0, keepdims=True)
        grad_out_t = inner(wo_ref[...], branch).astype(bf16)
        for group in range(GROUPS):
            grad_out[group, b] = grad_out_t[HW * group : HW * group + HW]
        for away in range(1, GROUPS):
            to = other_group(away)
            begin(grad_out.at[to, b], grad_t_ref.at[2 * g + b], o_send.at[b, away], o_recv.at[b, g], g=to)
        grad_t_ref[2 * g + b] = grad_out[g, b]

    norm(0)
    norm(1)
    for load in loads:
        load.wait()
    near = [near_pair(0), None]
    cot_x.wait_recv()
    cot_moves.append(begin(cots.at[:, 2], cots.at[:, 3], c_send.at[1], c_recv.at[1], core=sib))
    passed = [pass_on(0), None]
    near[1] = near_pair(1)
    far = [far_pair(0, passed[0]), None]
    passed[1] = pass_on(1)
    far[1] = far_pair(1, passed[1])

    def over_rows(left, right):
        total = None
        for b in range(2):
            for pair in range(2):
                term = outer(left(b, pair), right(b, pair))
                total = term if total is None else total + term
        return total.astype(bf16)

    def parts(write):
        for y in range(2):
            pl.when(r == y)(lambda: write(keep_ref, y))
            pl.when(r != y)(lambda: write(give_ref, y))

    down_grad = over_rows(lambda b, pair: hids[b, pair], lambda b, pair: pair_of(cots, b, pair))

    def write_down(ref, y):
        for z in range(GROUPS):
            p = y * GROUPS + z
            ref[z, 0:96] = down_grad[96 * p : 96 * p + 96]

    parts(write_down)
    back(0, near[0], far[0])
    up_grad = over_rows(lambda b, pair: pair_of(h2s, b, pair), lambda b, pair: dus[b, pair])

    def up_part(p, h):
        return up_grad[half * h + 48 * p : half * h + 48 * p + 48]

    def write_up(y, h):
        @pl.when((r == y) & (x == h))
        def _():
            for z in range(GROUPS):
                keep_ref[z, 96:144] = up_part(y * GROUPS + z, h)

        @pl.when((r != y) & (x == h))
        def _():
            for z in range(GROUPS):
                give_ref[z, 96:144] = up_part(y * GROUPS + z, h)

        @pl.when((r == y) & (x != h))
        def _():
            for z in range(GROUPS):
                x_give_ref[rows + 48 * z : rows + 48 * z + 48] = up_part(y * GROUPS + z, h)

        @pl.when((r != y) & (x != h))
        def _():
            for z in range(GROUPS):
                far_ref[z] = up_part(y * GROUPS + z, h)

    for y in range(2):
        for h in range(2):
            write_up(y, h)
    back(1, near[1], far[1])

    for owner in range(2):
        for c in range(2):
            piece = dot(attn_t[half * owner + fourth * c : half * owner + fourth * c + fourth], branch_ref[...])

            @pl.when(core == c)
            def _():
                wo_keep[owner] = piece

            @pl.when(core != c)
            def _():
                wo_give[owner] = piece.astype(bf16)

    w_sib = begin(wo_give, wo_in, w_send.at[0], w_recv.at[0], core=sib)
    y_sibs = [
        begin(part_y.at[b, 0, pl.ds(BLK, BLK)], in_y.at[b], y_send.at[b, 0], y_recv.at[b, 0], core=sib)
        for b in range(2)
    ]
    w_sib.wait_recv()
    wo_pass[...] = (wo_keep[other] + wo_in[other].astype(f32)).astype(bf16)
    w_x = begin(wo_pass, wo_x, w_send.at[1], w_recv.at[1], x=other)
    for b in range(2):
        y_passes[b].wait_recv()
        x_give_ref[rows_of(b)] = (part_y[b, 1, :BLK] + pass_y[b].astype(f32)).astype(bf16)
        y_sibs[b].wait_recv()
        base_ref[rows_of(b)] = mid_ref[b] + part_y[b, 0, :BLK] + in_y[b] + small_ref[5:6]
    mine = wo_keep[x] + wo_in[x].astype(f32)
    for b in range(2):
        for away in range(1, GROUPS):
            source = other_group(away)
            arrived(grad_t_ref.at[2 * source + b], o_send.at[b, away], o_recv.at[b, source], x)
    w_x.wait_recv()
    wo_sum = (mine + wo_x[...].astype(f32)).astype(bf16)

    def write_wo(ref, y):
        for z in range(GROUPS):
            p = y * GROUPS + z
            ref[z, 144:KEPT] = wo_sum[24 * p : 24 * p + 24]

    parts(write_wo)
    for move in pending:
        move.wait_send()


def dense(out_t, tokens, cot, small, wo, up_mine, up_other, down):
    rows, width = tokens.shape
    dma = pltpu.SemaphoreType.DMA
    full = (rows, width)
    part = (BLK, width)
    pair = (2 * BLK, width)
    fourth = (width // 4, width)
    return pl.pallas_call(
        dense_kernel,
        out_shape=(
            jax.ShapeDtypeStruct(full, f32),
            jax.ShapeDtypeStruct((rows + 48 * GROUPS, width), bf16),
            jax.ShapeDtypeStruct(full, f32),
            jax.ShapeDtypeStruct(out_t.shape, bf16),
            jax.ShapeDtypeStruct((GROUPS, KEPT, width), bf16),
            jax.ShapeDtypeStruct((GROUPS, KEPT, width), bf16),
            jax.ShapeDtypeStruct((GROUPS, 48, width), bf16),
            jax.ShapeDtypeStruct(small.shape, f32),
        ),
        in_specs=[whole_vmem()] * 5 + [anywhere()] * 3,
        out_specs=(whole_vmem(),) * 8,
        scratch_shapes=[
            pltpu.VMEM((width, width), bf16),
            pltpu.VMEM((width, width), bf16),
            pltpu.VMEM((GROUPS, 2, HW, BLK), bf16),
            pltpu.VMEM((width, rows), bf16),
            pltpu.VMEM((2, 4, *part), bf16),
            pltpu.VMEM((2, 4, *part), bf16),
            pltpu.VMEM((2, *part), f32),
            pltpu.VMEM((2, *part), f32),
            pltpu.VMEM((2, BLK, 1), f32),
            pltpu.VMEM((2, 2, *pair), f32),
            pltpu.VMEM((2, 2, *pair), f32),
            pltpu.VMEM((2, *part), f32),
            pltpu.VMEM((2, *part), f32),
            pltpu.VMEM((2, *part), bf16),
            pltpu.VMEM((2, *part), bf16),
            pltpu.VMEM((2, *part), bf16),
            pltpu.VMEM((2, 3, *part), bf16),
            pltpu.VMEM((2, 2, *pair), bf16),
            pltpu.VMEM((2, 2, *pair), bf16),
            pltpu.VMEM(full, bf16),
            pltpu.VMEM((GROUPS, 2, HW, BLK), bf16),
            pltpu.VMEM((2, *fourth), f32),
            pltpu.VMEM((2, *fourth), bf16),
            pltpu.VMEM((2, *fourth), bf16),
            pltpu.VMEM(fourth, bf16),
            pltpu.VMEM(fourth, bf16),
            dma((3,)), dma((2, GROUPS)), dma((2, GROUPS)), dma((3,)), dma((3,)), dma((2, 3)), dma((2, 3)),
            dma((2, 2)), dma((2, 2)), dma((2, 3)), dma((2, 3)), dma((2, GROUPS)), dma((2, GROUPS)), dma((2,)), dma((2,)),
        ],
        compiler_params=pltpu.CompilerParams(
            collective_id=1, has_side_effects=True, vmem_limit_bytes=40 << 20
        ),
        name="dense",
    )(out_t, tokens, cot, small, wo, up_mine, up_other, down)


FARTHEST = ((3, 2, 1, 0), (3, 0, 2, 1), (0, 3, 1, 2), (0, 1, 2, 3))


def farthest(g, step):
    picked = FARTHEST[0][step]
    for z in range(1, GROUPS):
        picked = jnp.where(g == z, FARTHEST[z][step], picked)
    return picked


class Chain:
    def __init__(self, g, x, total, parts, inward, outward, out_sem, in_sem):
        self.g, self.x, self.total, self.parts = g, x, total, parts
        self.inward, self.outward, self.out_sem, self.in_sem = inward, outward, out_sem, in_sem

    def move(self, to, way):
        return send(
            self.outward.at[to], self.inward.at[way, to], self.out_sem.at[to], self.in_sem.at[way, to],
            g=jnp.clip(self.g + (1 if way == 0 else -1), 0, GROUPS - 1),
        )

    def step(self, to):
        g = self.g
        self.total[...] = self.parts[to].astype(f32)

        def take(way):
            arrived(self.inward.at[way, to], self.out_sem.at[to], self.in_sem.at[way, to], self.x)
            self.total[...] += self.inward[way, to].astype(f32)

        pl.when((to >= g) & (g > 0))(lambda: take(0))
        pl.when((to <= g) & (g < GROUPS - 1))(lambda: take(1))

        @pl.when(to != g)
        def _():
            self.outward[to] = self.total[...].astype(bf16)

        pl.when(to > g)(lambda: self.move(to, 0).start())
        pl.when(to < g)(lambda: self.move(to, 1).start())

    def finish(self):
        for step in range(GROUPS - 1):
            to = farthest(self.g, step)
            left(self.outward.at[to], self.out_sem.at[to], self.in_sem.at[0, to], self.x)


class Ring:
    def __init__(self, g, x, slot, own_sem, out_sem, in_sem):
        self.g, self.x, self.slot = g, x, slot
        self.own_sem, self.out_sem, self.in_sem = own_sem, out_sem, in_sem

    def move(self, source, way, sem):
        return send(
            self.slot(source), self.slot(source), sem, self.in_sem.at[source],
            g=jnp.clip(self.g + way, 0, GROUPS - 1),
        )

    def start(self):
        g = self.g
        pl.when(g > 0)(lambda: self.move(g, -1, self.own_sem.at[0]).start())
        pl.when(g < GROUPS - 1)(lambda: self.move(g, 1, self.own_sem.at[1]).start())

    def step(self, step):
        g, source = self.g, nearest(self.g, step)
        arrived(self.slot(source), self.out_sem.at[source], self.in_sem.at[source], self.x)
        pl.when((source < g) & (g < GROUPS - 1))(lambda: self.move(source, 1, self.out_sem.at[source]).start())
        pl.when((source > g) & (g > 0))(lambda: self.move(source, -1, self.out_sem.at[source]).start())
        return source

    def finish(self):
        g = self.g
        for i, there in enumerate((g > 0, g < GROUPS - 1)):
            pl.when(there)(lambda: left(self.slot(g), self.own_sem.at[i], self.in_sem.at[g], self.x))
        for step in range(1, GROUPS):
            source = nearest(g, step)
            passed = ((source < g) & (g < GROUPS - 1)) | ((source > g) & (g > 0))
            pl.when(passed)(
                lambda: left(self.slot(source), self.out_sem.at[source], self.in_sem.at[source], self.x)
            )


def arrived(what, out_sem, in_sem, x):
    send(what, what, out_sem, in_sem, x=1 - x).wait_recv()


def left(what, out_sem, in_sem, x):
    send(what, what, out_sem, in_sem, x=1 - x).wait_send()


def scatter_kernel(
    dkv_ref, dq_any, normed_any, wfull_any, tokens_any, mgrad_any, keep_any, over_any, near_any, far_any, small_ref, sums_in,
    tokens_grad_ref, big_ref, qout_ref, kvout_ref, sums_ref,
    dq_ref, normed_ref, wfull_ref, tokens_ref, mgrad_ref, kept, over, near, far,
    own_kv, sib_kv, keep_x, give_x, in_x, give_y, in_y, part_a, total_a, inward_a, outward_a, wg_kv,
    by_sum, total_b, inward_b, outward_b, unit,
    q_keep, q_give, q_in, q_pass, q_x, q_y, q_sum, v_keep, v_give, v_in, v_pass, v_x, v_y, v_sum,
    sums_got, late, late_sum, late_got,
    load_sem, own_sem, k_send, k_recv, x_send, x_recv, y_send, y_recv, ca_send, ca_recv,
    cb_send, cb_recv, rb_own, rb_send, rb_recv,
    fy_send, fy_recv, fs_send, fs_recv,
    q_send, q_recv, rq_own, rq_send, rq_recv, qs_send, qs_recv,
    v_send, v_recv, rv_own, rv_send, rv_recv, vs_send, vs_recv,
    s_send, s_recv, t_send, t_recv, l_sem,
):
    g, r, core, x = place()
    other, sib, far_r = 1 - x, 1 - core, 1 - r
    rows, width = tokens_ref.shape
    half = width // 2
    fourth = half // 2
    wide_q = 2 * BLK
    loads = [
        pltpu.make_async_copy(what, where, load_sem.at[i])
        for i, (what, where) in enumerate(
            (
                (keep_any, kept), (over_any, over), (near_any.at[pl.ds(rows, 48 * GROUPS)], near), (far_any, far),
                (dq_any, dq_ref), (normed_any, normed_ref), (wfull_any, wfull_ref), (tokens_any, tokens_ref),
                (mgrad_any, mgrad_ref),
            )
        )
    ]
    for load in loads:
        load.start()
    greet(g, r, core, x, True, True)
    pending = []

    def begin(src, dst, out_sem, in_sem, **device):
        move = send(src, dst, out_sem, in_sem, **device)
        move.start()
        pending.append(move)
        return move

    def settled(move):
        move.wait_recv()
        move.wait_send()
        pending[:] = [item for item in pending if item is not move]

    kv_moves = []

    def start_kv():
        for i in range(GROUPS):
            c = farthest(g, i)
            own = pltpu.make_async_copy(dkv_ref.at[:, core, :, c], own_kv.at[i], own_sem.at[i])
            own.start()
            kv_moves.append(
                (own, begin(dkv_ref.at[:, sib, :, c], sib_kv.at[i], k_send.at[i], k_recv.at[i], core=sib))
            )

    def split(total, keep, give):
        for owner in range(2):
            for c in range(2):
                low = half * owner + fourth * c
                chunk = total[low : low + fourth]

                @pl.when(core == c)
                def _():
                    keep[owner] = chunk

                @pl.when(core != c)
                def _():
                    give[owner] = chunk.astype(bf16)

    def scaled(c):
        return dq_ref[c] * bf16(SCALE)

    q_move = send(q_give, q_in, q_send.at[0], q_recv.at[0], core=sib)

    def query_grad():
        loads[4].wait()
        loads[5].wait()
        query_total = outer(normed_ref[0], scaled(0))
        for c in range(1, GROUPS):
            query_total += outer(normed_ref[c], scaled(c))
        split(query_total, q_keep, q_give)
        q_move.start()
        line_q = scaled(0).astype(f32)
        for c in range(1, GROUPS):
            line_q += scaled(c).astype(f32)
        sums_ref[pl.ds(16 + g, 1), 0:wide_q] = jnp.sum(line_q, axis=0, keepdims=True)

    start_kv()
    sums_ref[...] = jnp.zeros_like(sums_ref)
    sums_ref[0:16] = sums_in[...]
    wg_kv[...] = jnp.zeros_like(wg_kv)

    def q_slot(z):
        return qout_ref.at[core, z]

    def v_slot(z):
        return kvout_ref.at[core, z]

    def b_slot(z):
        return big_ref.at[core, r, z]

    ring_q = Ring(g, x, q_slot, rq_own, rq_send, rq_recv)
    ring_v = Ring(g, x, v_slot, rv_own, rv_send, rv_recv)
    ring_b = Ring(g, x, b_slot, rb_own, rb_send, rb_recv)

    def store(value_ref, slot, sem):
        copy = pltpu.make_async_copy(value_ref, slot, sem)
        copy.start()
        copy.wait()

    def spread_b(z, step):
        begin(b_slot(z), b_slot(z), fy_send.at[step], fy_recv.at[step], r=far_r)
        begin(b_slot(z), b_slot(z), fs_send.at[0, step], fs_recv.at[0, step], core=sib)

    def spread_far(step):
        what = big_ref.at[core, far_r, nearest(g, step)]
        arrived(what, fy_send.at[step], fy_recv.at[step], x)
        begin(what, what, fs_send.at[1, step], fs_recv.at[1, step], core=sib)

    def on_ring_b(step):
        spread_b(ring_b.step(step), step)

    def on_ring_q(step):
        z = ring_q.step(step)
        begin(q_slot(z), q_slot(z), qs_send.at[step], qs_recv.at[step], core=sib)

    def on_ring_v(step):
        z = ring_v.step(step)
        begin(v_slot(z), v_slot(z), vs_send.at[step], vs_recv.at[step], core=sib)

    chain_a = Chain(g, x, total_a, part_a, inward_a, outward_a, ca_send, ca_recv)
    chain_b = Chain(g, x, total_b, by_sum, inward_b, outward_b, cb_send, cb_recv)
    at_end = (g == 0) | (g == GROUPS - 1)
    between = jnp.logical_not(at_end)

    def steps(chain, *which):
        for i in which:
            chain.step(farthest(g, i))

    def on_sibling(i):
        own, across = kv_moves[i]
        own.wait()
        across.wait_recv()

        def total(row, column):
            return own_kv[i, row, column].astype(f32) + sib_kv[i, row, column].astype(f32)

        for k in range(2):
            give_x[i, k] = (total(k, other) if i % 2 == 0 else total(far_r, k)).astype(bf16)
            keep_x[i, k] = total(k, x) if i % 2 == 0 else total(r, k)

    def go_first(i):
        along = {"x": other} if i % 2 == 0 else {"r": far_r}
        begin(give_x.at[i], in_x.at[i], x_send.at[i], x_recv.at[i], **along)

    def on_first(i):
        arrived(in_x.at[i], x_send.at[i], x_recv.at[i], x)
        away, stay, along = (far_r, r, {"r": far_r}) if i % 2 == 0 else (other, x, {"x": other})
        give_y[i] = (keep_x[i, away] + in_x[i, away].astype(f32)).astype(bf16)
        begin(give_y.at[i], in_y.at[i], y_send.at[i], y_recv.at[i], **along)
        keep_x[i, stay] += in_x[i, stay].astype(f32)

    def on_second(i):
        c = farthest(g, i)
        arrived(in_y.at[i], y_send.at[i], y_recv.at[i], x)
        both = (keep_x[i, r if i % 2 == 0 else x] + in_y[i].astype(f32)).astype(bf16)
        part_a[c] = inner(scaled(c), wfull_ref[:, :wide_q]) + inner(both, wfull_ref[:, wide_q:])
        wg_kv[...] += outer(normed_ref[c], both)
        sums_ref[pl.ds(16 + g, 1), wide_q : wide_q + 2 * HW] += jnp.sum(both.astype(f32), axis=0, keepdims=True)

    for load in loads[:4]:
        load.wait()
    own_up = pl.ds(pl.multiple_of(96 + 48 * x, 48), 48)
    their_up = pl.ds(pl.multiple_of(96 + 48 * other, 48), 48)
    for z in range(GROUPS):
        pair = kept[z].astype(f32) + over[z].astype(f32)
        by_sum[z, 0:96] = pair[0:96]
        by_sum[z, own_up] = pair[96:144]
        by_sum[z, 192:UNIT] = pair[144:KEPT]
        by_sum[z, their_up] = near[48 * z : 48 * z + 48].astype(f32) + far[z].astype(f32)
    pl.when(at_end)(lambda: steps(chain_b, 0, 1, 2))
    on_sibling(0)
    go_first(0)
    on_sibling(1)
    go_first(1)
    on_sibling(2)
    on_sibling(3)
    pl.when(between)(lambda: steps(chain_b, 0))
    query_grad()
    on_first(0)
    on_first(1)
    go_first(2)
    go_first(3)
    pl.when(between)(lambda: steps(chain_b, 1, 2))
    settled(q_move)
    q_pass[...] = (q_keep[other] + q_in[other].astype(f32)).astype(bf16)
    q_across = begin(q_pass, q_x, q_send.at[1], q_recv.at[1], x=other)
    loads[6].wait()
    on_second(0)
    on_second(1)
    pl.when(at_end)(lambda: steps(chain_a, 0))
    chain_b.step(g)
    unit[...] = total_b[...].astype(bf16)
    store(unit, b_slot(g), l_sem.at[0])
    ring_b.start()
    spread_b(g, 0)
    pl.when(at_end)(lambda: steps(chain_a, 1))
    on_first(2)
    on_first(3)
    q_across.wait_recv()
    q_sum[...] = (q_keep[x] + q_in[x].astype(f32) + q_x[...].astype(f32)).astype(bf16)
    q_over = begin(q_sum, q_y, q_send.at[2], q_recv.at[2], r=far_r)
    pl.when(between)(lambda: steps(chain_a, 0))
    on_ring_b(1)
    on_second(2)
    on_second(3)
    pl.when(at_end)(lambda: steps(chain_a, 2))
    split(wg_kv, v_keep, v_give)
    v_move = begin(v_give, v_in, v_send.at[0], v_recv.at[0], core=sib)
    s_sib = begin(sums_ref, sums_got.at[0], s_send.at[0], s_recv.at[0], core=sib)
    on_ring_b(2)
    spread_far(0)
    settled(q_over)
    q_sum[...] = (q_sum[...].astype(f32) + q_y[...].astype(f32)).astype(bf16)
    store(q_sum, q_slot(g), l_sem.at[0])
    ring_q.start()
    begin(q_slot(g), q_slot(g), qs_send.at[0], qs_recv.at[0], core=sib)
    v_move.wait_recv()
    v_pass[...] = (v_keep[other] + v_in[other].astype(f32)).astype(bf16)
    v_across = begin(v_pass, v_x, v_send.at[1], v_recv.at[1], x=other)
    settled(s_sib)
    sums_ref[...] += sums_got[0]
    s_x = begin(sums_ref, sums_got.at[1], s_send.at[1], s_recv.at[1], x=other)
    pl.when(between)(lambda: steps(chain_a, 1))
    v_across.wait_recv()
    v_sum[...] = (v_keep[x] + v_in[x].astype(f32) + v_x[...].astype(f32)).astype(bf16)
    v_over = begin(v_sum, v_y, v_send.at[2], v_recv.at[2], r=far_r)
    settled(s_x)
    sums_ref[...] += sums_got[1]
    s_y = begin(sums_ref, sums_got.at[2], s_send.at[2], s_recv.at[2], r=far_r)
    pl.when(between)(lambda: steps(chain_a, 2))
    settled(v_over)
    v_sum[...] = (v_sum[...].astype(f32) + v_y[...].astype(f32)).astype(bf16)
    store(v_sum, v_slot(g), l_sem.at[0])
    ring_v.start()
    begin(v_slot(g), v_slot(g), vs_send.at[0], vs_recv.at[0], core=sib)
    on_ring_b(3)
    settled(s_y)
    sums_ref[...] += sums_got[2]
    for away in range(1, GROUPS):
        begin(
            sums_ref, sums_got.at[2 + away], s_send.at[2 + away], s_recv.at[2 + away],
            g=lax.rem(g + away, GROUPS),
        )
    spread_far(1)
    on_ring_q(1)
    chain_a.step(g)

    loads[7].wait()
    loads[8].wait()
    grad_first = total_a[...]
    values = tokens_ref[...].astype(f32)
    mean = jnp.mean(values, axis=-1, keepdims=True)
    centred = values - mean
    scale = lax.rsqrt(jnp.mean(centred * centred, axis=-1, keepdims=True) + EPS)
    n1 = centred * scale
    pulled = grad_first * small_ref[0:1]
    inward = pulled - jnp.mean(pulled, axis=-1, keepdims=True) - n1 * jnp.mean(pulled * n1, axis=-1, keepdims=True)
    tokens_grad_ref[...] = mgrad_ref[...] + inward * scale
    late[...] = jnp.zeros_like(late)
    late[0:1] = jnp.sum(grad_first * n1, axis=0, keepdims=True)
    late[1:2] = jnp.sum(grad_first, axis=0, keepdims=True)
    for step in range(len(AROUND)):
        begin(late, late_got.at[step], t_send.at[step], t_recv.at[step], **neighbour(r, core, x, step))
    on_ring_v(1)
    on_ring_q(2)
    on_ring_q(3)
    spread_far(2)
    on_ring_v(2)
    late_sum[...] = late[...]
    for step in range(len(AROUND)):
        arrived(late_got.at[step], t_send.at[step], t_recv.at[step], x)
        late_sum[...] += late_got[step]
    first_z = len(AROUND) - 1
    for away in range(1, GROUPS):
        begin(
            late_sum, late_got.at[first_z + away], t_send.at[first_z + away], t_recv.at[first_z + away],
            g=lax.rem(g + away, GROUPS),
        )
    on_ring_v(3)
    spread_far(3)

    for away in range(1, GROUPS):
        arrived(sums_got.at[2 + away], s_send.at[2 + away], s_recv.at[2 + away], x)
        arrived(late_got.at[first_z + away], t_send.at[first_z + away], t_recv.at[first_z + away], x)
    for step in range(GROUPS):
        z = nearest(g, step)
        arrived(qout_ref.at[sib, z], qs_send.at[step], qs_recv.at[step], x)
        arrived(kvout_ref.at[sib, z], vs_send.at[step], vs_recv.at[step], x)
        arrived(big_ref.at[sib, r, z], fs_send.at[0, step], fs_recv.at[0, step], x)
        arrived(big_ref.at[sib, far_r, z], fs_send.at[1, step], fs_recv.at[1, step], x)
    for move in pending:
        move.wait_send()
    for item in (chain_a, chain_b, ring_q, ring_v, ring_b):
        item.finish()
    sums_ref[...] += sums_got[3] + sums_got[4] + sums_got[5]
    total = late_sum[...] + late_got[first_z + 1] + late_got[first_z + 2] + late_got[first_z + 3]
    sums_ref[0:2] = total[0:2]


def scatter(dkv, dq, normed, wfull, tokens, mgrad, small, keep, over, near, far, sums):
    rows, width = tokens.shape
    fourth = width // 4
    dma = pltpu.SemaphoreType.DMA
    wide_q, wide_v = 2 * BLK, 2 * HW
    kv_block = (rows, wide_v)
    full = (rows, width)
    unit = (UNIT, width)

    def weight_scratch(wide):
        return [
            pltpu.VMEM((2, fourth, wide), f32),
            pltpu.VMEM((2, fourth, wide), bf16),
            pltpu.VMEM((2, fourth, wide), bf16),
            *[pltpu.VMEM((fourth, wide), bf16)] * 4,
        ]

    return pl.pallas_call(
        scatter_kernel,
        out_shape=(
            jax.ShapeDtypeStruct(full, f32),
            jax.ShapeDtypeStruct((2, 2, GROUPS, *unit), bf16),
            jax.ShapeDtypeStruct((2, GROUPS, fourth, wide_q), bf16),
            jax.ShapeDtypeStruct((2, GROUPS, fourth, wide_v), bf16),
            jax.ShapeDtypeStruct((24, width), f32),
        ),
        in_specs=[anywhere()] * 10 + [whole_vmem()] * 2,
        out_specs=(whole_vmem(), anywhere(), anywhere(), anywhere(), whole_vmem()),
        scratch_shapes=[
            *[
                pltpu.VMEM(item.shape, item.dtype)
                for item in (dq, normed, wfull, tokens, mgrad, keep, over)
            ],
            pltpu.VMEM((48 * GROUPS, width), bf16),
            pltpu.VMEM(far.shape, bf16),
            pltpu.VMEM((GROUPS, 2, 2, *kv_block), bf16),
            pltpu.VMEM((GROUPS, 2, 2, *kv_block), bf16),
            pltpu.VMEM((GROUPS, 2, *kv_block), f32),
            pltpu.VMEM((GROUPS, 2, *kv_block), bf16),
            pltpu.VMEM((GROUPS, 2, *kv_block), bf16),
            pltpu.VMEM((GROUPS, *kv_block), bf16),
            pltpu.VMEM((GROUPS, *kv_block), bf16),
            pltpu.VMEM((GROUPS, *full), f32),
            pltpu.VMEM(full, f32),
            pltpu.VMEM((2, GROUPS, *full), bf16),
            pltpu.VMEM((GROUPS, *full), bf16),
            pltpu.VMEM((width, wide_v), f32),
            pltpu.VMEM((GROUPS, *unit), f32),
            pltpu.VMEM(unit, f32),
            pltpu.VMEM((2, GROUPS, *unit), bf16),
            pltpu.VMEM((GROUPS, *unit), bf16),
            pltpu.VMEM(unit, bf16),
            *weight_scratch(wide_q),
            *weight_scratch(wide_v),
            pltpu.VMEM((6, 24, width), f32),
            pltpu.VMEM((8, width), f32),
            pltpu.VMEM((8, width), f32),
            pltpu.VMEM((len(AROUND) + GROUPS - 1, 8, width), f32),
            dma((9,)),
            dma((GROUPS,)), dma((GROUPS,)), dma((GROUPS,)), dma((GROUPS,)), dma((GROUPS,)), dma((GROUPS,)), dma((GROUPS,)),
            dma((GROUPS,)), dma((2, GROUPS)),
            dma((GROUPS,)), dma((2, GROUPS)), dma((2,)), dma((GROUPS,)), dma((GROUPS,)),
            dma((GROUPS,)), dma((GROUPS,)), dma((2, GROUPS)), dma((2, GROUPS)),
            dma((3,)), dma((3,)), dma((2,)), dma((GROUPS,)), dma((GROUPS,)), dma((GROUPS,)), dma((GROUPS,)),
            dma((3,)), dma((3,)), dma((2,)), dma((GROUPS,)), dma((GROUPS,)), dma((GROUPS,)), dma((GROUPS,)),
            dma((6,)), dma((6,)), dma((10,)), dma((10,)), dma((1,)),
        ],
        compiler_params=pltpu.CompilerParams(
            collective_id=2, has_side_effects=True, vmem_limit_bytes=54 << 20
        ),
        name="scatter",
    )(dkv, dq, normed, wfull, tokens, mgrad, keep, over, near, far, small, sums)


def pack_kv(key_part, value_part):
    return jnp.concatenate(
        [key_part, value_part[..., 2 * DH :], value_part[..., : 2 * DH]], axis=-1
    )


def unpack_kv(both):
    return both[..., :HW], jnp.concatenate([both[..., HW + DH :], both[..., HW : HW + DH]], axis=-1)


def layout_kernel(
    big_ref, query_ref, kv_ref, sums_ref, base_ref, got_ref,
    up_out, down_out, wo_out, query_out, key_out, value_out,
    low_gain, low_shift, query_bias, value_bias, out_bias, high_gain, high_shift, up_bias, down_bias, result_out,
):
    x = lax.axis_index("x")
    width = big_ref.shape[-1]
    half = width // 2
    result_out[...] = (base_ref[...] + got_ref[...].astype(f32)).astype(bf16)
    for core in range(2):
        down_out[core] = big_ref[core, 0, 0:96].astype(f32)
        wo_out[core] = big_ref[core, 0, 192:UNIT].astype(f32)
        for owner in range(2):
            lane = (2 * owner + core) * width
            up_out[:, lane : lane + width] = big_ref[core, 0, 96 + 48 * owner : 144 + 48 * owner].astype(f32)
        query_out[core] = jnp.concatenate(
            [query_ref[core, z].astype(f32)[:, :HW] for z in range(GROUPS)], axis=1
        )
        both = [unpack_kv(kv_ref[core, z].astype(f32)) for z in range(GROUPS)]
        key_out[core] = jnp.concatenate([item[0] for item in both], axis=1)
        value_out[core] = jnp.concatenate([item[1] for item in both], axis=1)

    @pl.when(pl.program_id(0) == 0)
    def _():
        def own_half(row):
            whole = sums_ref[row : row + 1]
            return jnp.where(x == 0, whole[:, :half], whole[:, half:]).reshape(half)

        for ref, row in (
            (low_gain, 0), (low_shift, 1), (out_bias, 2), (high_gain, 3), (high_shift, 4), (down_bias, 5),
        ):
            ref[...] = own_half(row)
        pair = [sums_ref[pl.ds(16 + 2 * x + i, 1)] for i in range(2)]
        query_bias[...] = jnp.concatenate([item[:, :HW] for item in pair], axis=1).reshape(half)
        value_bias[...] = jnp.concatenate(
            [unpack_kv(item[:, 2 * BLK : 2 * BLK + 2 * HW])[1] for item in pair], axis=1
        ).reshape(half)
        up_bias[...] = jnp.concatenate(
            [sums_ref[pl.ds(8 + 2 * x + i, 1)] for i in range(2)], axis=1
        ).reshape(2 * width)


def lay_out(big, query, kv, sums, base, got):
    width = big.shape[-1]
    half, fourth = width // 2, width // 4
    rows = fourth // PARTS

    def spec(shape, index):
        return pl.BlockSpec(shape, index)

    def fixed(wide):
        return pl.BlockSpec((wide,), lambda p: (0,))

    narrow = spec((2, rows, width), lambda p: (0, p, 0))
    vector = jax.ShapeDtypeStruct((half,), f32)
    return pl.pallas_call(
        layout_kernel,
        grid=(PARTS,),
        out_shape=(
            jax.ShapeDtypeStruct((half, 4 * width), f32),
            jax.ShapeDtypeStruct((2, width, width), f32),
            *[jax.ShapeDtypeStruct((2, fourth, width), f32)] * 4,
            *[vector] * 7,
            jax.ShapeDtypeStruct((2 * width,), f32),
            vector,
            jax.ShapeDtypeStruct(base.shape, bf16),
        ),
        in_specs=[
            spec((2, 1, UNIT, width), lambda p: (0, p, 0, 0)),
            spec((2, GROUPS, rows, query.shape[-1]), lambda p: (0, 0, p, 0)),
            spec((2, GROUPS, rows, kv.shape[-1]), lambda p: (0, 0, p, 0)),
            spec(sums.shape, lambda p: (0, 0)),
            spec((base.shape[0] // PARTS, width), lambda p: (p, 0)),
            spec((base.shape[0] // PARTS, width), lambda p: (p, 0)),
        ],
        out_specs=(
            spec((48, 4 * width), lambda p: (p, 0)),
            spec((2, 96, width), lambda p: (0, p, 0)),
            *[narrow] * 4,
            *[fixed(half)] * 7,
            fixed(2 * width),
            fixed(half),
            spec((base.shape[0] // PARTS, width), lambda p: (p, 0)),
        ),
        compiler_params=pltpu.CompilerParams(
            vmem_limit_bytes=VMEM_LIMIT, dimension_semantics=("arbitrary",)
        ),
        name="lay_out",
    )(big, query, kv, sums, base, got)


ROWS = ("s", "r", "core", "x")
ALL = ("g", "s", "r", "core", "x")


def shards(
    tokens, cotangent, doc_lengths, deal, first_gain, first_shift, query_weight, query_bias,
    key_weight, value_weight, value_bias, output_weight, output_bias, second_gain, second_shift,
    up_weight, up_bias, down_weight, down_bias,
):
    rows, width = tokens.shape
    half = width // 2
    blocks = deal.shape[0]
    core, x = lax.axis_index("core"), lax.axis_index("x")
    swap = ((0, 1), (1, 0))

    def up_columns(owner):
        return lax.dynamic_slice_in_dim(up_weight, (2 * owner + core) * width, width, 1)

    def stay(*items):
        return tuple(pltpu.with_memory_space_constraint(item, pltpu.HBM) for item in items)

    kv, q, normed, small, wfull, wo = gather(
        *stay(
            tokens, query_weight, key_weight, value_weight, output_weight,
            first_gain, first_shift, output_bias, second_gain, second_shift, down_bias, query_bias, value_bias, up_bias,
        )
    )
    wide = blocks > 8 * 2 * GROUPS
    if wide:
        kv = lax.all_gather(kv, "s", axis=0, tiled=True)
    kv = kv.reshape(blocks, BLK, 2 * HW)
    q = q.reshape(2 * GROUPS, BLK, 2 * BLK)
    up_other, kv = lax.optimization_barrier((up_columns(1 - x), kv))
    up_other = lax.ppermute(up_other, "x", swap)
    out_t, kept, lse = attend_forward(deal, doc_lengths, q, kv)
    base, x_give, grad_middle, grad_t, kept_part, over, far, sums = dense(
        out_t, tokens, cotangent, small, wo, up_columns(x), up_other, down_weight
    )
    over = lax.ppermute(over, "r", swap)
    x_got = lax.ppermute(x_give, "x", swap)
    far = lax.ppermute(far, ("r", "x"), ((0, 3), (1, 2), (2, 1), (3, 0)))
    dq, dkv = attend_backward(deal, doc_lengths, q, kv, lse, grad_t, kept)
    dkv = dkv.reshape(-1, GROUPS, rows, 2 * HW)
    if wide:
        dkv = lax.psum_scatter(dkv, "s", scatter_dimension=0, tiled=True)
    dkv = dkv.reshape(2, 2, 2, GROUPS, rows, 2 * HW)
    dq = dq.reshape(GROUPS, rows, 2 * BLK)
    grad_tokens, big, query_own, kv_own, sums = scatter(
        *stay(dkv, dq, normed, wfull, tokens, grad_middle), small, *stay(kept_part, over, x_got, far), sums
    )
    if wide:
        big, query_own, kv_own, sums = (
            lax.psum(item, "s") for item in (big, query_own, kv_own, sums)
        )

    (
        up_own, down_own, wo_own, query_own, key_own, value_own,
        low_gain, low_shift, query_sum, value_sum, out_sum, high_gain, high_shift, up_sum, down_sum, result,
    ) = lay_out(big.reshape(2, PARTS, UNIT, width), query_own, kv_own, sums, *stay(base, x_got))

    def flat(item):
        return item.reshape(-1, width)

    return (
        result,
        grad_tokens,
        low_gain,
        low_shift,
        flat(query_own),
        query_sum,
        flat(key_own),
        flat(value_own),
        value_sum,
        flat(wo_own),
        out_sum,
        high_gain,
        high_shift,
        up_own,
        up_sum,
        flat(down_own),
        down_sum,
    )


def solution(mesh):
    devices = mesh.devices
    inner_mesh = Mesh(devices.reshape(GROUPS, devices.shape[0] // (4 * GROUPS), 2, 2, 2), ALL)
    row = P(ALL, None)
    mat = P("x", None)
    vec = P("x")
    in_specs = (
        row, row, P(), P(), vec, vec, mat, vec, mat, mat, vec, mat, vec, vec, vec, mat, vec, mat, vec,
    )
    out_specs = (
        row, row, vec, vec, mat, vec, mat, mat, vec, mat, vec, vec, vec, mat, vec, mat, vec,
    )
    return jax.shard_map(
        shards, mesh=inner_mesh, in_specs=in_specs, out_specs=out_specs, check_vma=False
    )
```

```python
import jax
import jax.numpy as jnp
from jax import lax
from jax.experimental import pallas as pl
from jax.experimental.pallas import tpu as pltpu
from jax.sharding import Mesh
from jax.sharding import PartitionSpec as P

HEADS = 12
DH = 64
NSUM = 50
SEG = 2048
BLK = 128
GROUPS = 4
PER = HEADS // GROUPS
HW = PER * DH
WIDE = PER * BLK
CHUNK = 2 * BLK
DEPTH = 8
EPS = 1e-05
SCALE = 0.125
MASKED = -1e30
ROOT_HALF = 0.7071067811865476
PDF_SCALE = 0.3989422804014327
VMEM_LIMIT = 56 << 20
bf16 = jnp.bfloat16
f32 = jnp.float32


def layer_norm(values, gain, shift):
    mean = jnp.mean(values, axis=-1, keepdims=True)
    centred = values - mean
    spread = jnp.mean(centred * centred, axis=-1, keepdims=True)
    return centred * lax.rsqrt(spread + EPS) * gain + shift


def outer(left, right):
    return lax.dot_general(left, right, (((0,), (0,)), ((), ())), preferred_element_type=f32)


def inner(left, right):
    return lax.dot_general(left, right, (((1,), (1,)), ((), ())), preferred_element_type=f32)


def dot(left, right):
    return jnp.dot(left, right, preferred_element_type=f32)


def survey(deal_ref, lengths_ref, where_ref, text_ref, low_ref, high_ref, first_ref):
    blocks = deal_ref.shape[0]
    per_group = blocks // (2 * GROUPS)
    rest = lax.axis_index(ROWS)

    def note(j, kept):
        pair = j // 2
        group = pair // per_group
        where_ref[deal_ref[j]] = ((pair - group * per_group) * GROUPS + group) * 2 + j % 2
        return kept

    lax.fori_loop(0, blocks, note, 0)
    starts = [jnp.int32(0)]
    for doc in range(lengths_ref.shape[0] - 1):
        starts.append(starts[-1] + lengths_ref[doc])

    def first_of(at):
        begin = jnp.zeros_like(at)
        for start in starts:
            begin = jnp.where(start <= at, jnp.maximum(begin, start), begin)
        return jnp.where(at - begin >= SEG + NSUM, begin + SEG, begin)

    for slot in range(2 * GROUPS):
        text = deal_ref[2 * ((slot // 2) * per_group + rest) + slot % 2]
        text_ref[slot] = text
        low_ref[slot] = first_of(text * BLK) // CHUNK
        high_ref[slot] = text // 2
        first_ref[slot] = first_of(text * BLK + lax.broadcasted_iota(jnp.int32, (1, BLK), 1))


def survey_scratch(blocks):
    slots = 2 * GROUPS
    return [
        pltpu.SMEM((blocks,), jnp.int32),
        pltpu.SMEM((slots,), jnp.int32),
        pltpu.SMEM((slots,), jnp.int32),
        pltpu.SMEM((slots,), jnp.int32),
        pltpu.VMEM((slots, 1, BLK), jnp.int32),
    ]


def spread_heads_t(part_t, order):
    rows = []
    zero = jnp.zeros((DH, BLK), part_t.dtype)
    for head in order:
        if head is None:
            rows.append(jnp.zeros((DH, WIDE), part_t.dtype))
        else:
            piece = part_t[DH * head : DH * head + DH]
            rows.append(
                jnp.concatenate([piece if h == head else zero for h in range(PER)], axis=1)
            )
    return jnp.concatenate(rows, axis=0)


K_ORDER = (0, 1, 2, None)
V_ORDER = (None, 2, 0, 1)


def visible(chunk, first, own):
    at = chunk * CHUNK + lax.broadcasted_iota(jnp.int32, (CHUNK, BLK), 0)
    allowed = (at >= first) & (at <= own)
    return jnp.concatenate([allowed] * PER, axis=1)


def load_chunk(kv_ref, where_ref, chunk):
    return jnp.concatenate(
        [kv_ref[where_ref[2 * chunk]], kv_ref[where_ref[2 * chunk + 1]]], axis=0
    )


def forward_kernel(
    deal_ref, lengths_ref, q_ref, kv_ref,
    out_ref, wide_ref, lse_ref,
    where_ref, text_ref, low_ref, high_ref, first_ref, acc_ref,
):
    survey(deal_ref, lengths_ref, where_ref, text_ref, low_ref, high_ref, first_ref)

    def one_slot(slot, kept):
        wide_q = spread_heads_t(q_ref[slot].T[:HW], K_ORDER)
        first = first_ref[slot]
        own = text_ref[slot] * BLK + lax.broadcasted_iota(jnp.int32, (1, BLK), 1)
        last_first = jnp.max(first)
        acc_ref[...] = jnp.zeros_like(acc_ref)

        def step(double, carry):
            top, total = carry
            scores = []
            for part in range(2):
                keys = load_chunk(kv_ref, where_ref, 2 * double + part)[:, : 2 * BLK]
                scores.append(jnp.where(visible(2 * double + part, first, own), dot(keys, wide_q), MASKED))
            scores = jnp.concatenate(scores, axis=0)
            fresh = jnp.maximum(top, jnp.max(scores, axis=0, keepdims=True))
            expo = jnp.exp(scores - fresh)
            shrink = jnp.exp(top - fresh)
            total = total * shrink + jnp.sum(expo, axis=0, keepdims=True)
            vals = jnp.concatenate([load_chunk(kv_ref, where_ref, 2 * double + part)[:, BLK:] for part in range(2)], axis=0)
            acc_ref[...] = acc_ref[...] * shrink + outer(vals, expo.astype(bf16))
            return fresh, total

        top, total = lax.fori_loop(
            low_ref[slot] // 2,
            high_ref[slot] // 2 + 1,
            step,
            (jnp.full((1, WIDE), MASKED, f32), jnp.zeros((1, WIDE), f32)),
        )
        lse_ref[slot] = top + jnp.log(total)
        scaled = acc_ref[...] / total
        pieces = []
        for head in range(PER):
            row = DH * V_ORDER.index(head)
            pieces.append(scaled[row : row + DH, BLK * head : BLK * head + BLK])
        whole = jnp.concatenate(pieces, axis=0)
        wide_ref[slot] = whole
        out_ref[slot] = whole.astype(bf16)
        return kept

    lax.fori_loop(0, q_ref.shape[0], one_slot, 0)


def whole_vmem():
    return pl.BlockSpec(memory_space=pltpu.VMEM)


def whole_smem():
    return pl.BlockSpec(memory_space=pltpu.SMEM)


def attend_forward(deal, lengths, q, kv):
    slots = q.shape[0]
    blocks = kv.shape[0]
    return pl.pallas_call(
        forward_kernel,
        out_shape=(
            jax.ShapeDtypeStruct((slots, HW, BLK), bf16),
            jax.ShapeDtypeStruct((slots, HW, BLK), f32),
            jax.ShapeDtypeStruct((slots, 1, WIDE), f32),
        ),
        in_specs=[whole_smem()] * 2 + [whole_vmem()] * 2,
        out_specs=(whole_vmem(),) * 3,
        scratch_shapes=[
            *survey_scratch(blocks),
            pltpu.VMEM((2 * BLK, WIDE), f32),
        ],
        compiler_params=pltpu.CompilerParams(vmem_limit_bytes=(6 << 20) + kv.size // 5 * 16),
        name="attend_forward",
    )(deal, lengths, q, kv)


def backward_kernel(
    deal_ref, lengths_ref, q_ref, kv_ref, lse_ref, do_ref, wide_ref,
    dq_ref, dkv_ref, where_ref, text_ref, low_ref, high_ref, first_ref, qt_ref, qm_ref, dot_ref, dom_ref, delta_ref, acc_ref, dk_acc, dv_acc,
    packed_ref, count_ref, list_ref, out_sem,
):
    survey(deal_ref, lengths_ref, where_ref, text_ref, low_ref, high_ref, first_ref)
    slots = q_ref.shape[0]
    chunks = kv_ref.shape[0] // 2

    def ready(slot, _):
        q = q_ref[slot]
        qt_ref[slot] = spread_heads_t(q.T[:HW], K_ORDER)
        lane = lax.broadcasted_iota(jnp.int32, (BLK, 2 * BLK), 1) // DH
        zero = jnp.zeros_like(q)
        qm_ref[slot] = jnp.concatenate(
            [jnp.where(lane == K_ORDER.index(h), q, zero) for h in range(PER)], axis=0
        )
        grad_t = do_ref[slot]
        dot_ref[slot] = spread_heads_t(grad_t, V_ORDER)
        ordered = jnp.concatenate(
            [
                jnp.zeros((DH, BLK), bf16) if h is None else grad_t[DH * h : DH * h + DH]
                for h in V_ORDER
            ],
            axis=0,
        ).T
        dom_ref[slot] = jnp.concatenate(
            [jnp.where(lane == V_ORDER.index(h), ordered, zero) for h in range(PER)], axis=0
        )
        both = grad_t.astype(f32) * wide_ref[slot]
        delta_ref[slot] = jnp.concatenate(
            [jnp.sum(both[DH * h : DH * h + DH], axis=0, keepdims=True) for h in range(PER)],
            axis=1,
        )
        acc_ref[slot] = jnp.zeros((HW, WIDE), f32)
        return _

    lax.fori_loop(0, slots, ready, 0)

    def clear(chunk, kept):
        count_ref[chunk] = 0
        return kept

    lax.fori_loop(0, chunks, clear, 0)

    def enlist(slot, kept):
        def seen(chunk, kept):
            count = count_ref[chunk]
            list_ref[chunk * slots + count] = slot
            count_ref[chunk] = count + 1
            return kept

        lax.fori_loop(low_ref[slot], high_ref[slot] + 1, seen, 0)
        return kept

    lax.fori_loop(0, slots, enlist, 0)

    def written(chunk, i):
        return pltpu.make_async_copy(
            packed_ref.at[chunk % DEPTH, i], dkv_ref.at[where_ref[2 * chunk + i]], out_sem.at[chunk % DEPTH, i]
        )

    def one_chunk(chunk, kept):
        part = load_chunk(kv_ref, where_ref, chunk)
        keys = part[:, : 2 * BLK]
        vals = part[:, BLK:]
        keys_t = keys.T[:HW]
        dk_acc[...] = jnp.zeros_like(dk_acc)
        dv_acc[...] = jnp.zeros_like(dv_acc)

        def one_slot(i, kept):
            for half in range(2):
                attend(list_ref[chunk * slots + 2 * i + half])
            return kept

        def attend(slot):
            own = text_ref[slot] * BLK + lax.broadcasted_iota(jnp.int32, (1, BLK), 1)
            scores = dot(keys, qt_ref[slot])
            dprobs = dot(vals, dot_ref[slot])
            probs = jnp.where(visible(chunk, first_ref[slot], own), jnp.exp(scores - lse_ref[slot]), 0.0)
            dscores = (probs * (dprobs - delta_ref[slot])).astype(bf16)
            dv_acc[...] += dot(probs.astype(bf16), dom_ref[slot])
            dk_acc[...] += dot(dscores, qm_ref[slot])
            acc_ref[slot] += dot(keys_t, dscores)

        lax.fori_loop(0, count_ref[chunk] // 2, one_slot, 0)
        pl.when(count_ref[chunk] % 2 == 1)(lambda: attend(list_ref[chunk * slots + count_ref[chunk] - 1]))
        packed = jnp.concatenate(
            [
                dk_acc[:, :BLK],
                dk_acc[:, BLK:] + dv_acc[:, :BLK],
                dv_acc[:, BLK:],
            ],
            axis=1,
        ).astype(bf16)

        @pl.when(chunk >= DEPTH)
        def _():
            for i in range(2):
                written(chunk - DEPTH, i).wait()

        for i in range(2):
            packed_ref[chunk % DEPTH, i] = packed[BLK * i : BLK * i + BLK]
            written(chunk, i).start()
        return kept

    lax.fori_loop(0, chunks, one_chunk, 0)
    for last in range(DEPTH):
        for i in range(2):
            written(chunks - DEPTH + last, i).wait()

    def finish(slot, _):
        total = acc_ref[slot]
        kept = jnp.concatenate(
            [total[DH * h : DH * h + DH, BLK * h : BLK * h + BLK] for h in range(PER)]
            + [jnp.zeros((DH, BLK), f32)],
            axis=0,
        )
        dq_ref[slot] = kept.T.astype(bf16)
        return _

    lax.fori_loop(0, slots, finish, 0)


def attend_backward(deal, lengths, q, kv, lse, grad_t, wide):
    slots = q.shape[0]
    return pl.pallas_call(
        backward_kernel,
        out_shape=(
            jax.ShapeDtypeStruct((slots, BLK, 2 * BLK), bf16),
            jax.ShapeDtypeStruct(kv.shape, bf16),
        ),
        in_specs=[whole_smem()] * 2 + [whole_vmem()] * 5,
        out_specs=(whole_vmem(), in_hbm()),
        scratch_shapes=[
            *survey_scratch(kv.shape[0]),
            pltpu.VMEM((slots, 2 * BLK, WIDE), bf16),
            pltpu.VMEM((slots, WIDE, 2 * BLK), bf16),
            pltpu.VMEM((slots, 2 * BLK, WIDE), bf16),
            pltpu.VMEM((slots, WIDE, 2 * BLK), bf16),
            pltpu.VMEM((slots, 1, WIDE), f32),
            pltpu.VMEM((slots, HW, WIDE), f32),
            pltpu.VMEM((CHUNK, 2 * BLK), f32),
            pltpu.VMEM((CHUNK, 2 * BLK), f32),
            pltpu.VMEM((DEPTH, 2, BLK, 2 * HW), bf16),
            pltpu.SMEM((kv.shape[0] // 2,), jnp.int32),
            pltpu.SMEM((kv.shape[0] // 2 * slots,), jnp.int32),
            pltpu.SemaphoreType.DMA((DEPTH, 2)),
        ],
        compiler_params=pltpu.CompilerParams(
            vmem_limit_bytes=max(46 << 20, (17 << 20) + kv.size * 2)
        ),
        name="attend_backward",
    )(deal, lengths, q, kv, lse, grad_t, wide)


MESH = pl.DeviceIdType.MESH


def send(src, dst, out_sem, in_sem, **device):
    return pltpu.make_async_remote_copy(
        src_ref=src, dst_ref=dst, send_sem=out_sem, recv_sem=in_sem, device_id=device, device_id_type=MESH
    )


def place():
    return tuple(lax.axis_index(name) for name in ("g", "r", "core", "x"))


def seat(r, core, x):
    return (r * 2 + core) * 2 + x


AROUND = ((0, 0, 1), (0, 1, 0), (0, 1, 1), (1, 0, 0), (1, 0, 1), (1, 1, 0), (1, 1, 1))


def neighbour(r, core, x, step):
    dr, dc, dx = AROUND[step]
    return {"r": 1 - r if dr else r, "core": 1 - core if dc else core, "x": 1 - x if dx else x}


def greet(g, r, core, x, line, around=False):
    barrier = pltpu.get_barrier_semaphore()

    def hello(**device):
        pl.semaphore_signal(barrier, inc=1, device_id=device, device_id_type=MESH)

    if around:
        for step in range(len(AROUND)):
            hello(**neighbour(r, core, x, step))
    else:
        hello(core=1 - core)
        hello(x=1 - x)
        hello(r=1 - r)
    near = len(AROUND) if around else 3
    if line:
        for away in range(1, GROUPS):
            hello(g=lax.rem(g + away, GROUPS))
        pl.semaphore_wait(barrier, near + GROUPS - 1)
    else:
        pl.when(g > 0)(lambda: hello(g=g - 1))
        pl.when(g < GROUPS - 1)(lambda: hello(g=g + 1))
        pl.semaphore_wait(barrier, near + 2 - jnp.where(g == 0, 1, 0) - jnp.where(g == GROUPS - 1, 1, 0))


NEAREST = ((0, 1, 2, 3), (1, 2, 0, 3), (2, 1, 3, 0), (3, 2, 1, 0))


def nearest(g, step):
    picked = NEAREST[0][step]
    for z in range(1, GROUPS):
        picked = jnp.where(g == z, NEAREST[z][step], picked)
    return picked


def prepare(g, x, weights, lines, narrow_ref, small_ref):
    half = weights.shape[1]
    odd = lax.rem(g, 2) == 1

    def columns(i):
        low = pl.multiple_of(3 * g // 2 * BLK, BLK)
        window = weights[i, :, pl.ds(low, 2 * BLK)]
        moved = jnp.concatenate([window[:, DH:], window[:, :DH]], axis=1)
        return jnp.where(odd, moved, window)

    lane = lax.broadcasted_iota(jnp.int32, (half, 2 * BLK), 1)
    query = columns(0)
    narrow_ref[:, : 2 * BLK] = jnp.where(lane < HW, query, jnp.zeros_like(query))
    narrow_ref[:, 2 * BLK :] = pack_kv(columns(1)[:, :HW], columns(2)[:, :HW])

    def line(i):
        return lines[i][...].astype(f32).reshape(1, -1)

    zero = jnp.zeros((1, half), f32)
    small_ref[...] = jnp.zeros_like(small_ref)
    for row in range(6):
        small_ref[row : row + 1] = jnp.where(
            x == 0, jnp.concatenate([line(row), zero], axis=1), jnp.concatenate([zero, line(row)], axis=1)
        )
    ups = line(8)
    for i in range(2):
        small_ref[pl.ds(8 + 2 * x + i, 1)] = ups[:, 2 * half * i : 2 * half * i + 2 * half]

    def part(i):
        mine = jnp.where(odd, line(i)[:, HW:], line(i)[:, :HW])
        return jnp.where(g // 2 == x, mine, jnp.zeros_like(mine))

    value = part(7)
    small_ref[12:13] = jnp.concatenate(
        [part(6), jnp.zeros((1, 2 * BLK), f32), value[:, 2 * DH :], value[:, : 2 * DH], jnp.zeros((1, BLK), f32)], axis=1
    )


def gather_kernel(
    tokens_ref, query_any, key_any, value_any, wo_ref, l0, l1, l2, l3, l4, l5, l6, l7, l8,
    kv_ref, q_ref, normed_ref, small_out, wfull, wo_out,
    lined, attn_w, narrow_ref, small_ref, small_in, kvs,
    z_own, z_send, z_recv, s_sem, n_send, n_recv, kv_send, kv_recv, kv_local, w_send, w_recv, w_local, a_sem,
):
    g, r, core, x = place()
    other = 1 - x
    rows, width = tokens_ref.shape
    half = width // 2
    fourth = half // 2
    eighth = half // 4
    loads = [
        pltpu.make_async_copy(ref, attn_w.at[i], a_sem.at[i]) for i, ref in enumerate((query_any, key_any, value_any))
    ]
    for load in loads:
        load.start()
    greet(g, r, core, x, False)

    def half_of(source, part):
        return lined.at[source, pl.ds(BLK * part, BLK)]

    def along(source, part, away, sem):
        return send(half_of(source, part), half_of(source, part), sem, z_recv.at[source, part], g=g + away)

    lined[g] = tokens_ref[...]
    for part in range(2):
        pl.when(g > 0)(lambda: along(g, part, -1, z_own.at[0, part]).start())
        pl.when(g < GROUPS - 1)(lambda: along(g, part, 1, z_own.at[1, part]).start())

    for load in loads:
        load.wait()
    prepare(g, x, attn_w, (l0, l1, l2, l3, l4, l5, l6, l7, l8), narrow_ref, small_ref)
    small_move = send(small_ref, small_in, s_sem.at[0], s_sem.at[1], x=other)
    small_move.start()
    mine = pl.ds(x * half + core * fourth, fourth)
    narrow_x = send(narrow_ref.at[pl.ds(core * fourth, fourth)], wfull.at[mine], n_send.at[0], n_recv.at[0], x=other)
    narrow_x.start()

    def wo_rows(owner, part):
        return wo_out.at[pl.ds(owner * half + core * fourth + part * eighth, eighth)]

    wo_x = send(wo_ref.at[pl.ds(core * fourth + r * eighth, eighth)], wo_rows(x, r), w_send.at[0], w_recv.at[0], x=other)
    wo_y = send(wo_rows(other, r), wo_rows(other, r), w_send.at[3], w_recv.at[3], r=1 - r)
    wo_s = [
        send(wo_rows(other, part), wo_rows(other, part), w_send.at[6 + i], w_recv.at[6 + i], core=1 - core)
        for i, part in enumerate((r, 1 - r))
    ]
    wo_x.start()
    locals_ = [pltpu.make_async_copy(wo_ref, wo_out.at[pl.ds(x * half, half)], w_local.at[0])]
    for item in locals_:
        item.start()

    wfull[pl.ds(x * half, half)] = narrow_ref[...]
    narrow_x.wait_recv()
    theirs = wfull.at[pl.ds(other * half + core * fourth, fourth)]
    narrow_s = send(theirs, theirs, n_send.at[1], n_recv.at[1], core=1 - core)
    narrow_s.start()
    small_move.wait_recv()
    small_out[...] = small_ref[...] + small_in[...]
    narrow_s.wait_recv()

    own = seat(r, core, x)

    def span(step):
        return (step, 0, rows) if step < GROUPS - 1 else (GROUPS - 1, BLK * (step - GROUPS + 1), BLK)

    def block(owner, step):
        nth, low, count = span(step)
        return kv_ref.at[owner, nearest(g, nth), pl.ds(low, count)]

    def made(step):
        nth, low, count = span(step)
        return kvs.at[nth, pl.ds(low, count)]

    def push(step, kind, src, dst, **device):
        send(src, dst, kv_send.at[kind, step], kv_recv.at[kind, step], **device).start()

    def settle(step, kind, owner):
        arrived(block(owner, step), kv_send.at[kind, step], kv_recv.at[kind, step], x)

    def forward(step):
        by_x = block(seat(r, core, other), step)
        settle(step, 0, seat(r, core, other))
        if step % 2 == 0:
            push(step, 3, by_x, by_x, r=1 - r)
        push(step, 4, by_x, by_x, core=1 - core)
        by_y = block(seat(1 - r, core, x), step)
        settle(step, 1, seat(1 - r, core, x))
        if step % 2 == 1:
            push(step, 3, by_y, by_y, x=other)
        push(step, 5, by_y, by_y, core=1 - core)

    def forward_far(step):
        far = block(seat(1 - r, core, other), step)
        settle(step, 3, seat(1 - r, core, other))
        push(step, 6, far, far, core=1 - core)

    def take(nth, part):
        source = nearest(g, nth)
        arrived(half_of(source, part), z_send.at[source, part], z_recv.at[source, part], x)
        pl.when((source < g) & (g < GROUPS - 1))(lambda: along(source, part, 1, z_send.at[source, part]).start())
        pl.when((source > g) & (g > 0))(lambda: along(source, part, -1, z_send.at[source, part]).start())

    def project(step):
        nth, low, count = span(step)
        source = nearest(g, nth)
        taken = pl.ds(low, count)
        values = lined[source, taken].astype(f32)
        normed = layer_norm(values, small_out[0:1], small_out[1:2]).astype(bf16)
        normed_ref[source, taken] = normed
        both = dot(normed, wfull[...]) + small_out[12:13, : wfull.shape[1]]
        kvs[nth, taken] = both[:, 2 * BLK :].astype(bf16)
        push(step, 0, made(step), block(own, step), x=other)
        push(step, 1, made(step), block(own, step), r=1 - r)
        push(step, 2, made(step), block(own, step), core=1 - core)
        q_ref[source, taken] = (both[:, : 2 * BLK] * SCALE).astype(bf16)
        pltpu.make_async_copy(made(step), block(own, step), kv_local.at[step]).start()

    at_end = (g == 0) | (g == GROUPS - 1)
    between = jnp.logical_not(at_end)
    project(0)
    take(1, 0)
    take(1, 1)

    @pl.when(between)
    def _():
        take(2, 0)
        take(2, 1)

    project(1)
    forward(0)

    @pl.when(at_end)
    def _():
        take(2, 0)
        take(2, 1)

    project(2)

    @pl.when(at_end)
    def _():
        forward(1)
        forward_far(0)

    take(3, 0)
    pl.when(between)(lambda: take(3, 1))
    project(3)
    pl.when(at_end)(lambda: take(3, 1))
    project(4)

    @pl.when(between)
    def _():
        forward(1)
        forward_far(0)

    wo_x.wait_recv()
    wo_y.start()
    wo_s[0].start()
    forward(2)
    forward_far(1)
    forward(3)
    forward_far(2)
    forward(4)
    forward_far(3)
    arrived(wo_rows(other, 1 - r), w_send.at[3], w_recv.at[3], x)
    wo_s[1].start()
    forward_far(4)

    for step in range(GROUPS + 1):
        pltpu.make_async_copy(made(step), block(own, step), kv_local.at[step]).wait()
        settle(step, 2, seat(r, 1 - core, x))
        settle(step, 4, seat(r, 1 - core, other))
        settle(step, 5, seat(1 - r, 1 - core, x))
        settle(step, 6, seat(1 - r, 1 - core, other))
        for kind in range(7):
            left(made(step), kv_send.at[kind, step], kv_recv.at[kind, step], x)
    for part in range(2):
        pl.when(g > 0)(lambda: left(half_of(g, part), z_own.at[0, part], z_recv.at[g, part], x))
        pl.when(g < GROUPS - 1)(lambda: left(half_of(g, part), z_own.at[1, part], z_recv.at[g, part], x))
        for nth in range(1, GROUPS):
            source = nearest(g, nth)
            passed = ((source < g) & (g < GROUPS - 1)) | ((source > g) & (g > 0))
            pl.when(passed)(
                lambda: left(half_of(source, part), z_send.at[source, part], z_recv.at[source, part], x)
            )
    small_move.wait_send()
    narrow_x.wait_send()
    narrow_s.wait_send()
    for item in locals_:
        item.wait()
    for item in (wo_x, wo_y, *wo_s):
        item.wait_send()
    for i, part in enumerate((r, 1 - r)):
        there = wo_out.at[pl.ds(other * half + (1 - core) * fourth + part * eighth, eighth)]
        send(there, there, w_send.at[6 + i], w_recv.at[6 + i], core=1 - core).wait_recv()


def anywhere():
    return pl.BlockSpec(memory_space=pl.ANY)


def in_hbm():
    return pl.BlockSpec(memory_space=pltpu.HBM)


def gather(tokens, query, key, value, wo, *lines):
    rows, width = tokens.shape
    wide = 2 * BLK + 2 * HW
    small = (16, width)
    dma = pltpu.SemaphoreType.DMA
    return pl.pallas_call(
        gather_kernel,
        out_shape=(
            jax.ShapeDtypeStruct((8, GROUPS, rows, 2 * HW), bf16),
            jax.ShapeDtypeStruct((GROUPS, rows, 2 * BLK), bf16),
            jax.ShapeDtypeStruct((GROUPS, rows, width), bf16),
            jax.ShapeDtypeStruct(small, f32),
            jax.ShapeDtypeStruct((width, wide), bf16),
            jax.ShapeDtypeStruct((width, width), bf16),
        ),
        in_specs=[whole_vmem(), *[in_hbm()] * 4, *[whole_vmem()] * len(lines)],
        out_specs=(anywhere(), *(whole_vmem(),) * 5),
        scratch_shapes=[
            pltpu.VMEM((GROUPS, rows, width), bf16),
            pltpu.VMEM((3, width // 2, width), bf16),
            pltpu.VMEM((width // 2, wide), bf16),
            pltpu.VMEM(small, f32),
            pltpu.VMEM(small, f32),
            pltpu.VMEM((GROUPS, rows, 2 * HW), bf16),
            dma((2, 2)), dma((GROUPS, 2)), dma((GROUPS, 2)), dma((2,)), dma((2,)), dma((2,)),
            dma((7, GROUPS + 1)), dma((7, GROUPS + 1)), dma((GROUPS + 1,)), dma((8,)), dma((8,)), dma((2,)), dma((3,)),
        ],
        compiler_params=pltpu.CompilerParams(
            collective_id=0, has_side_effects=True, vmem_limit_bytes=16 << 20
        ),
        name="gather",
    )(tokens, query, key, value, wo, *lines)


def erf_parts(values):
    below = 0.5 * (1.0 + lax.erf(values * ROOT_HALF))
    return below, PDF_SCALE * jnp.exp(-0.5 * values * values)


PARTS = 8
UNIT = 216
KEPT = 168


def dense_kernel(
    out_t_ref, tokens_ref, cot_ref, small_ref, wo_ref, up_mine, up_other, down_any,
    base_ref, x_give_ref, middle_grad_ref, grad_t_ref, keep_ref, give_ref, far_ref, sums_ref,
    down_ref, up_ref, attn_in, attn_t, cots, h2s, mid_ref, n2_ref, scales, part_y, part_d, in_y, in_d, pass_y, pass_d,
    x_y, x_d, hids, dus, branch_ref, grad_out, wo_keep, wo_give, wo_in, wo_pass, wo_x,
    l_sem, a_send, a_recv, c_send, c_recv, h_send, h_recv, y_send, y_recv, d_send, d_recv, o_send, o_recv,
    w_send, w_recv,
):
    g, r, core, x = place()
    other, sib = 1 - x, 1 - core
    rows, width = tokens_ref.shape
    half = width // 2
    fourth = half // 2
    loads = [
        pltpu.make_async_copy(
            down_any.at[pl.ds(pl.multiple_of(core * width, width), width)], down_ref, l_sem.at[0]
        ),
        pltpu.make_async_copy(up_mine, up_ref.at[pl.ds(x * half, half)], l_sem.at[1]),
        pltpu.make_async_copy(up_other, up_ref.at[pl.ds(other * half, half)], l_sem.at[2]),
    ]
    for load in loads:
        load.start()
    greet(g, r, core, x, True)
    pending = []

    def begin(src, dst, out_sem, in_sem, **device):
        move = send(src, dst, out_sem, in_sem, **device)
        move.start()
        pending.append(move)
        return move

    def other_group(away):
        return lax.rem(g + away, GROUPS)

    def rows_of(b):
        return pl.ds(BLK * b, BLK)

    for b in range(2):
        for away in range(1, GROUPS):
            to = other_group(away)
            begin(out_t_ref.at[2 * to + b], attn_in.at[g, b], a_send.at[b, away], a_recv.at[b, g], g=to)
        attn_in[g, b] = out_t_ref[2 * g + b]
        cots[b, 0] = cot_ref[rows_of(b)]
    cot_x = begin(cots.at[:, 0], cots.at[:, 2], c_send.at[2], c_recv.at[2], x=other)
    cot_moves = [begin(cots.at[:, 0], cots.at[:, 1], c_send.at[0], c_recv.at[0], core=sib)]
    sums_ref[...] = jnp.zeros_like(sums_ref)
    sums_ref[5:6] = jnp.sum(cot_ref[...].astype(f32), axis=0, keepdims=True)
    h2_moves = []

    def norm(b):
        for away in range(1, GROUPS):
            source = other_group(away)
            arrived(attn_in.at[source, b], a_send.at[b, away], a_recv.at[b, source], x)
        for source in range(GROUPS):
            attn_t[HW * source : HW * source + HW, BLK * b : BLK * b + BLK] = attn_in[source, b]
        middle = (
            tokens_ref[rows_of(b)].astype(f32)
            + outer(attn_t[:, BLK * b : BLK * b + BLK], wo_ref[...])
            + small_ref[2:3]
        )
        mid_ref[b] = middle
        mean = jnp.mean(middle, axis=-1, keepdims=True)
        centred = middle - mean
        scale = lax.rsqrt(jnp.mean(centred * centred, axis=-1, keepdims=True) + EPS)
        scales[b] = scale
        n2_ref[b] = centred * scale
        h2s[b, 0] = (n2_ref[b] * small_ref[3:4] + small_ref[4:5]).astype(bf16)
        h2_moves.append(
            (
                begin(h2s.at[b, 0], h2s.at[b, 2], h_send.at[b, 1], h_recv.at[b, 1], x=other),
                begin(h2s.at[b, 0], h2s.at[b, 1], h_send.at[b, 0], h_recv.at[b, 0], core=sib),
            )
        )

    def pass_on(b):
        h2_moves[b][0].wait_recv()
        return begin(h2s.at[b, 2], h2s.at[b, 3], h_send.at[b, 2], h_recv.at[b, 2], core=sib)

    bias_row = 8 + 2 * x + core

    def pair_of(ref, b, pair):
        return ref[b, 2 * pair : 2 * pair + 2].reshape(2 * BLK, width)

    def forward_backward(b, pair):
        cot = pair_of(cots, b, pair)
        expanded = dot(pair_of(h2s, b, pair), up_ref[...]) + small_ref[pl.ds(bias_row, 1)]
        below, density = erf_parts(expanded)
        hidden = (expanded * below).astype(bf16)
        hids[b, pair] = hidden
        slope = below + expanded * density
        grad_hidden = inner(cot, down_ref[...]).astype(bf16).astype(f32)
        grad_expand = (grad_hidden * slope).astype(bf16)
        dus[b, pair] = grad_expand
        part_d[b, pair] = inner(grad_expand, up_ref[...])
        part_y[b, pair] = dot(hidden, down_ref[...])
        sums_ref[pl.ds(bias_row, 1)] += jnp.sum(grad_expand.astype(f32), axis=0, keepdims=True)

    d_moves, y_passes = [None, None], [None, None]

    def near_pair(b):
        if b == 0:
            cot_moves[0].wait_recv()
        h2_moves[b][1].wait_recv()
        forward_backward(b, 0)
        return begin(part_d.at[b, 0, pl.ds(BLK, BLK)], in_d.at[b], d_send.at[b, 0], d_recv.at[b, 0], core=sib)

    def far_pair(b, passed):
        if b == 0:
            cot_moves[1].wait_recv()
        passed.wait_recv()
        forward_backward(b, 1)
        x_d[b, 0] = part_d[b, 1, BLK:].astype(bf16)
        across = begin(x_d.at[b, 0], pass_d.at[b], d_send.at[b, 1], d_recv.at[b, 1], core=sib)
        x_y[b] = part_y[b, 1, BLK:].astype(bf16)
        y_passes[b] = begin(x_y.at[b], pass_y.at[b], y_send.at[b, 1], y_recv.at[b, 1], core=sib)
        across.wait_recv()
        x_d[b, 1] = (part_d[b, 1, :BLK] + pass_d[b].astype(f32)).astype(bf16)
        return begin(x_d.at[b, 1], x_d.at[b, 2], d_send.at[b, 2], d_recv.at[b, 2], x=other)

    def back(b, near, far):
        near.wait_recv()
        far.wait_recv()
        grad_second = part_d[b, 0, :BLK] + in_d[b] + x_d[b, 2].astype(f32)
        n2 = n2_ref[b]
        sums_ref[3:4] += jnp.sum(grad_second * n2, axis=0, keepdims=True)
        sums_ref[4:5] += jnp.sum(grad_second, axis=0, keepdims=True)
        pulled = grad_second * small_ref[3:4]
        inward = (
            pulled - jnp.mean(pulled, axis=-1, keepdims=True) - n2 * jnp.mean(pulled * n2, axis=-1, keepdims=True)
        )
        grad_middle = cot_ref[rows_of(b)].astype(f32) + inward * scales[b]
        middle_grad_ref[rows_of(b)] = grad_middle
        branch = grad_middle.astype(bf16)
        branch_ref[rows_of(b)] = branch
        sums_ref[2:3] += jnp.sum(branch.astype(f32), axis=0, keepdims=True)
        grad_out_t = inner(wo_ref[...], branch).astype(bf16)
        for group in range(GROUPS):
            grad_out[group, b] = grad_out_t[HW * group : HW * group + HW]
        for away in range(1, GROUPS):
            to = other_group(away)
            begin(grad_out.at[to, b], grad_t_ref.at[2 * g + b], o_send.at[b, away], o_recv.at[b, g], g=to)
        grad_t_ref[2 * g + b] = grad_out[g, b]

    norm(0)
    norm(1)
    for load in loads:
        load.wait()
    near = [near_pair(0), None]
    cot_x.wait_recv()
    cot_moves.append(begin(cots.at[:, 2], cots.at[:, 3], c_send.at[1], c_recv.at[1], core=sib))
    passed = [pass_on(0), None]
    near[1] = near_pair(1)
    far = [far_pair(0, passed[0]), None]
    passed[1] = pass_on(1)
    far[1] = far_pair(1, passed[1])

    def over_rows(left, right):
        total = None
        for b in range(2):
            for pair in range(2):
                term = outer(left(b, pair), right(b, pair))
                total = term if total is None else total + term
        return total.astype(bf16)

    def parts(write):
        for y in range(2):
            pl.when(r == y)(lambda: write(keep_ref, y))
            pl.when(r != y)(lambda: write(give_ref, y))

    down_grad = over_rows(lambda b, pair: hids[b, pair], lambda b, pair: pair_of(cots, b, pair))

    def write_down(ref, y):
        for z in range(GROUPS):
            p = y * GROUPS + z
            ref[z, 0:96] = down_grad[96 * p : 96 * p + 96]

    parts(write_down)
    back(0, near[0], far[0])
    up_grad = over_rows(lambda b, pair: pair_of(h2s, b, pair), lambda b, pair: dus[b, pair])

    def up_part(p, h):
        return up_grad[half * h + 48 * p : half * h + 48 * p + 48]

    def write_up(y, h):
        @pl.when((r == y) & (x == h))
        def _():
            for z in range(GROUPS):
                keep_ref[z, 96:144] = up_part(y * GROUPS + z, h)

        @pl.when((r != y) & (x == h))
        def _():
            for z in range(GROUPS):
                give_ref[z, 96:144] = up_part(y * GROUPS + z, h)

        @pl.when((r == y) & (x != h))
        def _():
            for z in range(GROUPS):
                x_give_ref[rows + 48 * z : rows + 48 * z + 48] = up_part(y * GROUPS + z, h)

        @pl.when((r != y) & (x != h))
        def _():
            for z in range(GROUPS):
                far_ref[z] = up_part(y * GROUPS + z, h)

    for y in range(2):
        for h in range(2):
            write_up(y, h)
    back(1, near[1], far[1])

    for owner in range(2):
        for c in range(2):
            piece = dot(attn_t[half * owner + fourth * c : half * owner + fourth * c + fourth], branch_ref[...])

            @pl.when(core == c)
            def _():
                wo_keep[owner] = piece

            @pl.when(core != c)
            def _():
                wo_give[owner] = piece.astype(bf16)

    w_sib = begin(wo_give, wo_in, w_send.at[0], w_recv.at[0], core=sib)
    y_sibs = [
        begin(part_y.at[b, 0, pl.ds(BLK, BLK)], in_y.at[b], y_send.at[b, 0], y_recv.at[b, 0], core=sib)
        for b in range(2)
    ]
    w_sib.wait_recv()
    wo_pass[...] = (wo_keep[other] + wo_in[other].astype(f32)).astype(bf16)
    w_x = begin(wo_pass, wo_x, w_send.at[1], w_recv.at[1], x=other)
    for b in range(2):
        y_passes[b].wait_recv()
        x_give_ref[rows_of(b)] = (part_y[b, 1, :BLK] + pass_y[b].astype(f32)).astype(bf16)
        y_sibs[b].wait_recv()
        base_ref[rows_of(b)] = mid_ref[b] + part_y[b, 0, :BLK] + in_y[b] + small_ref[5:6]
    mine = wo_keep[x] + wo_in[x].astype(f32)
    for b in range(2):
        for away in range(1, GROUPS):
            source = other_group(away)
            arrived(grad_t_ref.at[2 * source + b], o_send.at[b, away], o_recv.at[b, source], x)
    w_x.wait_recv()
    wo_sum = (mine + wo_x[...].astype(f32)).astype(bf16)

    def write_wo(ref, y):
        for z in range(GROUPS):
            p = y * GROUPS + z
            ref[z, 144:KEPT] = wo_sum[24 * p : 24 * p + 24]

    parts(write_wo)
    for move in pending:
        move.wait_send()


def dense(out_t, tokens, cot, small, wo, up_mine, up_other, down):
    rows, width = tokens.shape
    dma = pltpu.SemaphoreType.DMA
    full = (rows, width)
    part = (BLK, width)
    pair = (2 * BLK, width)
    fourth = (width // 4, width)
    return pl.pallas_call(
        dense_kernel,
        out_shape=(
            jax.ShapeDtypeStruct(full, f32),
            jax.ShapeDtypeStruct((rows + 48 * GROUPS, width), bf16),
            jax.ShapeDtypeStruct(full, f32),
            jax.ShapeDtypeStruct(out_t.shape, bf16),
            jax.ShapeDtypeStruct((GROUPS, KEPT, width), bf16),
            jax.ShapeDtypeStruct((GROUPS, KEPT, width), bf16),
            jax.ShapeDtypeStruct((GROUPS, 48, width), bf16),
            jax.ShapeDtypeStruct(small.shape, f32),
        ),
        in_specs=[whole_vmem()] * 5 + [anywhere()] * 3,
        out_specs=(whole_vmem(),) * 8,
        scratch_shapes=[
            pltpu.VMEM((width, width), bf16),
            pltpu.VMEM((width, width), bf16),
            pltpu.VMEM((GROUPS, 2, HW, BLK), bf16),
            pltpu.VMEM((width, rows), bf16),
            pltpu.VMEM((2, 4, *part), bf16),
            pltpu.VMEM((2, 4, *part), bf16),
            pltpu.VMEM((2, *part), f32),
            pltpu.VMEM((2, *part), f32),
            pltpu.VMEM((2, BLK, 1), f32),
            pltpu.VMEM((2, 2, *pair), f32),
            pltpu.VMEM((2, 2, *pair), f32),
            pltpu.VMEM((2, *part), f32),
            pltpu.VMEM((2, *part), f32),
            pltpu.VMEM((2, *part), bf16),
            pltpu.VMEM((2, *part), bf16),
            pltpu.VMEM((2, *part), bf16),
            pltpu.VMEM((2, 3, *part), bf16),
            pltpu.VMEM((2, 2, *pair), bf16),
            pltpu.VMEM((2, 2, *pair), bf16),
            pltpu.VMEM(full, bf16),
            pltpu.VMEM((GROUPS, 2, HW, BLK), bf16),
            pltpu.VMEM((2, *fourth), f32),
            pltpu.VMEM((2, *fourth), bf16),
            pltpu.VMEM((2, *fourth), bf16),
            pltpu.VMEM(fourth, bf16),
            pltpu.VMEM(fourth, bf16),
            dma((3,)), dma((2, GROUPS)), dma((2, GROUPS)), dma((3,)), dma((3,)), dma((2, 3)), dma((2, 3)),
            dma((2, 2)), dma((2, 2)), dma((2, 3)), dma((2, 3)), dma((2, GROUPS)), dma((2, GROUPS)), dma((2,)), dma((2,)),
        ],
        compiler_params=pltpu.CompilerParams(
            collective_id=1, has_side_effects=True, vmem_limit_bytes=46 << 20
        ),
        name="dense",
    )(out_t, tokens, cot, small, wo, up_mine, up_other, down)


FARTHEST = ((3, 2, 1, 0), (3, 0, 2, 1), (0, 3, 1, 2), (0, 1, 2, 3))


def farthest(g, step):
    picked = FARTHEST[0][step]
    for z in range(1, GROUPS):
        picked = jnp.where(g == z, FARTHEST[z][step], picked)
    return picked


class Chain:
    def __init__(self, g, x, total, parts, inward, outward, out_sem, in_sem):
        self.g, self.x, self.total, self.parts = g, x, total, parts
        self.inward, self.outward, self.out_sem, self.in_sem = inward, outward, out_sem, in_sem

    def move(self, to, way):
        return send(
            self.outward.at[to], self.inward.at[way, to], self.out_sem.at[to], self.in_sem.at[way, to],
            g=jnp.clip(self.g + (1 if way == 0 else -1), 0, GROUPS - 1),
        )

    def step(self, to):
        g = self.g
        self.total[...] = self.parts[to].astype(f32)

        def take(way):
            arrived(self.inward.at[way, to], self.out_sem.at[to], self.in_sem.at[way, to], self.x)
            self.total[...] += self.inward[way, to].astype(f32)

        pl.when((to >= g) & (g > 0))(lambda: take(0))
        pl.when((to <= g) & (g < GROUPS - 1))(lambda: take(1))

        @pl.when(to != g)
        def _():
            self.outward[to] = self.total[...].astype(bf16)

        pl.when(to > g)(lambda: self.move(to, 0).start())
        pl.when(to < g)(lambda: self.move(to, 1).start())

    def finish(self):
        for step in range(GROUPS - 1):
            to = farthest(self.g, step)
            left(self.outward.at[to], self.out_sem.at[to], self.in_sem.at[0, to], self.x)


class Ring:
    def __init__(self, g, x, slot, own_sem, out_sem, in_sem):
        self.g, self.x, self.slot = g, x, slot
        self.own_sem, self.out_sem, self.in_sem = own_sem, out_sem, in_sem

    def move(self, source, way, sem):
        return send(
            self.slot(source), self.slot(source), sem, self.in_sem.at[source],
            g=jnp.clip(self.g + way, 0, GROUPS - 1),
        )

    def start(self):
        g = self.g
        pl.when(g > 0)(lambda: self.move(g, -1, self.own_sem.at[0]).start())
        pl.when(g < GROUPS - 1)(lambda: self.move(g, 1, self.own_sem.at[1]).start())

    def step(self, step):
        g, source = self.g, nearest(self.g, step)
        arrived(self.slot(source), self.out_sem.at[source], self.in_sem.at[source], self.x)
        pl.when((source < g) & (g < GROUPS - 1))(lambda: self.move(source, 1, self.out_sem.at[source]).start())
        pl.when((source > g) & (g > 0))(lambda: self.move(source, -1, self.out_sem.at[source]).start())
        return source

    def finish(self):
        g = self.g
        for i, there in enumerate((g > 0, g < GROUPS - 1)):
            pl.when(there)(lambda: left(self.slot(g), self.own_sem.at[i], self.in_sem.at[g], self.x))
        for step in range(1, GROUPS):
            source = nearest(g, step)
            passed = ((source < g) & (g < GROUPS - 1)) | ((source > g) & (g > 0))
            pl.when(passed)(
                lambda: left(self.slot(source), self.out_sem.at[source], self.in_sem.at[source], self.x)
            )


def arrived(what, out_sem, in_sem, x):
    send(what, what, out_sem, in_sem, x=1 - x).wait_recv()


def left(what, out_sem, in_sem, x):
    send(what, what, out_sem, in_sem, x=1 - x).wait_send()


def scatter_kernel(
    dkv_ref, dq_any, normed_any, wfull_any, tokens_any, mgrad_any, keep_any, over_any, near_any, far_any, small_ref, sums_in,
    tokens_grad_ref, big_ref, qout_ref, kvout_ref, sums_ref,
    dq_ref, normed_ref, wfull_ref, tokens_ref, mgrad_ref, kept, over, near, far,
    own_kv, sib_kv, keep_x, give_x, in_x, give_y, in_y, part_a, total_a, inward_a, outward_a, wg_kv,
    by_sum, total_b, inward_b, outward_b, unit,
    q_keep, q_give, q_in, q_pass, q_x, q_y, q_sum, v_keep, v_give, v_in, v_pass, v_x, v_y, v_sum,
    sums_got, late, late_sum, late_got,
    load_sem, own_sem, k_send, k_recv, x_send, x_recv, y_send, y_recv, ca_send, ca_recv,
    cb_send, cb_recv, rb_own, rb_send, rb_recv,
    fy_send, fy_recv, fs_send, fs_recv,
    q_send, q_recv, rq_own, rq_send, rq_recv, qs_send, qs_recv,
    v_send, v_recv, rv_own, rv_send, rv_recv, vs_send, vs_recv,
    s_send, s_recv, t_send, t_recv, l_sem,
):
    g, r, core, x = place()
    other, sib, far_r = 1 - x, 1 - core, 1 - r
    rows, width = tokens_ref.shape
    half = width // 2
    fourth = half // 2
    wide_q = 2 * BLK
    loads = [
        pltpu.make_async_copy(what, where, load_sem.at[i])
        for i, (what, where) in enumerate(
            (
                (keep_any, kept), (over_any, over), (near_any.at[pl.ds(rows, 48 * GROUPS)], near), (far_any, far),
                (dq_any, dq_ref), (normed_any, normed_ref), (wfull_any, wfull_ref), (tokens_any, tokens_ref),
                (mgrad_any, mgrad_ref),
            )
        )
    ]
    for load in loads:
        load.start()
    greet(g, r, core, x, True, True)
    pending = []

    def begin(src, dst, out_sem, in_sem, **device):
        move = send(src, dst, out_sem, in_sem, **device)
        move.start()
        pending.append(move)
        return move

    def settled(move):
        move.wait_recv()
        move.wait_send()
        pending[:] = [item for item in pending if item is not move]

    kv_moves = []

    def start_kv():
        for i in range(GROUPS):
            c = farthest(g, i)
            own = pltpu.make_async_copy(dkv_ref.at[:, core, :, c], own_kv.at[i], own_sem.at[i])
            own.start()
            kv_moves.append(
                (own, begin(dkv_ref.at[:, sib, :, c], sib_kv.at[i], k_send.at[i], k_recv.at[i], core=sib))
            )

    def split(total, keep, give):
        for owner in range(2):
            for c in range(2):
                low = half * owner + fourth * c
                chunk = total[low : low + fourth]

                @pl.when(core == c)
                def _():
                    keep[owner] = chunk

                @pl.when(core != c)
                def _():
                    give[owner] = chunk.astype(bf16)

    def scaled(c):
        return dq_ref[c] * bf16(SCALE)

    q_move = send(q_give, q_in, q_send.at[0], q_recv.at[0], core=sib)

    def query_grad():
        loads[4].wait()
        loads[5].wait()
        query_total = outer(normed_ref[0], scaled(0))
        for c in range(1, GROUPS):
            query_total += outer(normed_ref[c], scaled(c))
        split(query_total, q_keep, q_give)
        q_move.start()
        line_q = scaled(0).astype(f32)
        for c in range(1, GROUPS):
            line_q += scaled(c).astype(f32)
        sums_ref[pl.ds(16 + g, 1), 0:wide_q] = jnp.sum(line_q, axis=0, keepdims=True)

    start_kv()
    sums_ref[...] = jnp.zeros_like(sums_ref)
    sums_ref[0:16] = sums_in[...]
    wg_kv[...] = jnp.zeros_like(wg_kv)

    def q_slot(z):
        return qout_ref.at[core, z]

    def v_slot(z):
        return kvout_ref.at[core, z]

    def b_slot(z):
        return big_ref.at[core, r, z]

    ring_q = Ring(g, x, q_slot, rq_own, rq_send, rq_recv)
    ring_v = Ring(g, x, v_slot, rv_own, rv_send, rv_recv)
    ring_b = Ring(g, x, b_slot, rb_own, rb_send, rb_recv)

    def store(value_ref, slot, sem):
        copy = pltpu.make_async_copy(value_ref, slot, sem)
        copy.start()
        copy.wait()

    def spread_b(z, step):
        begin(b_slot(z), b_slot(z), fy_send.at[step], fy_recv.at[step], r=far_r)
        begin(b_slot(z), b_slot(z), fs_send.at[0, step], fs_recv.at[0, step], core=sib)

    def spread_far(step):
        what = big_ref.at[core, far_r, nearest(g, step)]
        arrived(what, fy_send.at[step], fy_recv.at[step], x)
        begin(what, what, fs_send.at[1, step], fs_recv.at[1, step], core=sib)

    def on_ring_b(step):
        spread_b(ring_b.step(step), step)

    def on_ring_q(step):
        z = ring_q.step(step)
        begin(q_slot(z), q_slot(z), qs_send.at[step], qs_recv.at[step], core=sib)

    def on_ring_v(step):
        z = ring_v.step(step)
        begin(v_slot(z), v_slot(z), vs_send.at[step], vs_recv.at[step], core=sib)

    chain_a = Chain(g, x, total_a, part_a, inward_a, outward_a, ca_send, ca_recv)
    chain_b = Chain(g, x, total_b, by_sum, inward_b, outward_b, cb_send, cb_recv)
    at_end = (g == 0) | (g == GROUPS - 1)
    between = jnp.logical_not(at_end)

    def steps(chain, *which):
        for i in which:
            chain.step(farthest(g, i))

    def on_sibling(i):
        own, across = kv_moves[i]
        own.wait()
        across.wait_recv()

        def total(row, column):
            return own_kv[i, row, column].astype(f32) + sib_kv[i, row, column].astype(f32)

        for k in range(2):
            give_x[i, k] = (total(k, other) if i % 2 == 0 else total(far_r, k)).astype(bf16)
            keep_x[i, k] = total(k, x) if i % 2 == 0 else total(r, k)

    def go_first(i):
        along = {"x": other} if i % 2 == 0 else {"r": far_r}
        begin(give_x.at[i], in_x.at[i], x_send.at[i], x_recv.at[i], **along)

    def on_first(i):
        arrived(in_x.at[i], x_send.at[i], x_recv.at[i], x)
        away, stay, along = (far_r, r, {"r": far_r}) if i % 2 == 0 else (other, x, {"x": other})
        give_y[i] = (keep_x[i, away] + in_x[i, away].astype(f32)).astype(bf16)
        begin(give_y.at[i], in_y.at[i], y_send.at[i], y_recv.at[i], **along)
        keep_x[i, stay] += in_x[i, stay].astype(f32)

    def on_second(i):
        c = farthest(g, i)
        arrived(in_y.at[i], y_send.at[i], y_recv.at[i], x)
        both = (keep_x[i, r if i % 2 == 0 else x] + in_y[i].astype(f32)).astype(bf16)
        part_a[c] = inner(scaled(c), wfull_ref[:, :wide_q]) + inner(both, wfull_ref[:, wide_q:])
        wg_kv[...] += outer(normed_ref[c], both)
        sums_ref[pl.ds(16 + g, 1), wide_q : wide_q + 2 * HW] += jnp.sum(both.astype(f32), axis=0, keepdims=True)

    for load in loads[:4]:
        load.wait()
    own_up = pl.ds(pl.multiple_of(96 + 48 * x, 48), 48)
    their_up = pl.ds(pl.multiple_of(96 + 48 * other, 48), 48)
    for z in range(GROUPS):
        pair = kept[z].astype(f32) + over[z].astype(f32)
        by_sum[z, 0:96] = pair[0:96]
        by_sum[z, own_up] = pair[96:144]
        by_sum[z, 192:UNIT] = pair[144:KEPT]
        by_sum[z, their_up] = near[48 * z : 48 * z + 48].astype(f32) + far[z].astype(f32)
    pl.when(at_end)(lambda: steps(chain_b, 0, 1, 2))
    on_sibling(0)
    go_first(0)
    on_sibling(1)
    go_first(1)
    on_sibling(2)
    on_sibling(3)
    pl.when(between)(lambda: steps(chain_b, 0))
    query_grad()
    on_first(0)
    on_first(1)
    go_first(2)
    go_first(3)
    pl.when(between)(lambda: steps(chain_b, 1, 2))
    settled(q_move)
    q_pass[...] = (q_keep[other] + q_in[other].astype(f32)).astype(bf16)
    q_across = begin(q_pass, q_x, q_send.at[1], q_recv.at[1], x=other)
    loads[6].wait()
    on_second(0)
    on_second(1)
    pl.when(at_end)(lambda: steps(chain_a, 0))
    chain_b.step(g)
    unit[...] = total_b[...].astype(bf16)
    store(unit, b_slot(g), l_sem.at[0])
    ring_b.start()
    spread_b(g, 0)
    pl.when(at_end)(lambda: steps(chain_a, 1))
    on_first(2)
    on_first(3)
    q_across.wait_recv()
    q_sum[...] = (q_keep[x] + q_in[x].astype(f32) + q_x[...].astype(f32)).astype(bf16)
    q_over = begin(q_sum, q_y, q_send.at[2], q_recv.at[2], r=far_r)
    pl.when(between)(lambda: steps(chain_a, 0))
    on_ring_b(1)
    on_second(2)
    on_second(3)
    pl.when(at_end)(lambda: steps(chain_a, 2))
    split(wg_kv, v_keep, v_give)
    v_move = begin(v_give, v_in, v_send.at[0], v_recv.at[0], core=sib)
    s_sib = begin(sums_ref, sums_got.at[0], s_send.at[0], s_recv.at[0], core=sib)
    on_ring_b(2)
    spread_far(0)
    settled(q_over)
    q_sum[...] = (q_sum[...].astype(f32) + q_y[...].astype(f32)).astype(bf16)
    store(q_sum, q_slot(g), l_sem.at[0])
    ring_q.start()
    begin(q_slot(g), q_slot(g), qs_send.at[0], qs_recv.at[0], core=sib)
    v_move.wait_recv()
    v_pass[...] = (v_keep[other] + v_in[other].astype(f32)).astype(bf16)
    v_across = begin(v_pass, v_x, v_send.at[1], v_recv.at[1], x=other)
    settled(s_sib)
    sums_ref[...] += sums_got[0]
    s_x = begin(sums_ref, sums_got.at[1], s_send.at[1], s_recv.at[1], x=other)
    pl.when(between)(lambda: steps(chain_a, 1))
    v_across.wait_recv()
    v_sum[...] = (v_keep[x] + v_in[x].astype(f32) + v_x[...].astype(f32)).astype(bf16)
    v_over = begin(v_sum, v_y, v_send.at[2], v_recv.at[2], r=far_r)
    settled(s_x)
    sums_ref[...] += sums_got[1]
    s_y = begin(sums_ref, sums_got.at[2], s_send.at[2], s_recv.at[2], r=far_r)
    pl.when(between)(lambda: steps(chain_a, 2))
    settled(v_over)
    v_sum[...] = (v_sum[...].astype(f32) + v_y[...].astype(f32)).astype(bf16)
    store(v_sum, v_slot(g), l_sem.at[0])
    ring_v.start()
    begin(v_slot(g), v_slot(g), vs_send.at[0], vs_recv.at[0], core=sib)
    on_ring_b(3)
    settled(s_y)
    sums_ref[...] += sums_got[2]
    for away in range(1, GROUPS):
        begin(
            sums_ref, sums_got.at[2 + away], s_send.at[2 + away], s_recv.at[2 + away],
            g=lax.rem(g + away, GROUPS),
        )
    spread_far(1)
    on_ring_q(1)
    chain_a.step(g)

    loads[7].wait()
    loads[8].wait()
    grad_first = total_a[...]
    values = tokens_ref[...].astype(f32)
    mean = jnp.mean(values, axis=-1, keepdims=True)
    centred = values - mean
    scale = lax.rsqrt(jnp.mean(centred * centred, axis=-1, keepdims=True) + EPS)
    n1 = centred * scale
    pulled = grad_first * small_ref[0:1]
    inward = pulled - jnp.mean(pulled, axis=-1, keepdims=True) - n1 * jnp.mean(pulled * n1, axis=-1, keepdims=True)
    tokens_grad_ref[...] = mgrad_ref[...] + inward * scale
    late[...] = jnp.zeros_like(late)
    late[0:1] = jnp.sum(grad_first * n1, axis=0, keepdims=True)
    late[1:2] = jnp.sum(grad_first, axis=0, keepdims=True)
    for step in range(len(AROUND)):
        begin(late, late_got.at[step], t_send.at[step], t_recv.at[step], **neighbour(r, core, x, step))
    on_ring_v(1)
    on_ring_q(2)
    on_ring_q(3)
    spread_far(2)
    on_ring_v(2)
    late_sum[...] = late[...]
    for step in range(len(AROUND)):
        arrived(late_got.at[step], t_send.at[step], t_recv.at[step], x)
        late_sum[...] += late_got[step]
    first_z = len(AROUND) - 1
    for away in range(1, GROUPS):
        begin(
            late_sum, late_got.at[first_z + away], t_send.at[first_z + away], t_recv.at[first_z + away],
            g=lax.rem(g + away, GROUPS),
        )
    on_ring_v(3)
    spread_far(3)

    for away in range(1, GROUPS):
        arrived(sums_got.at[2 + away], s_send.at[2 + away], s_recv.at[2 + away], x)
        arrived(late_got.at[first_z + away], t_send.at[first_z + away], t_recv.at[first_z + away], x)
    for step in range(GROUPS):
        z = nearest(g, step)
        arrived(qout_ref.at[sib, z], qs_send.at[step], qs_recv.at[step], x)
        arrived(kvout_ref.at[sib, z], vs_send.at[step], vs_recv.at[step], x)
        arrived(big_ref.at[sib, r, z], fs_send.at[0, step], fs_recv.at[0, step], x)
        arrived(big_ref.at[sib, far_r, z], fs_send.at[1, step], fs_recv.at[1, step], x)
    for move in pending:
        move.wait_send()
    for item in (chain_a, chain_b, ring_q, ring_v, ring_b):
        item.finish()
    sums_ref[...] += sums_got[3] + sums_got[4] + sums_got[5]
    total = late_sum[...] + late_got[first_z + 1] + late_got[first_z + 2] + late_got[first_z + 3]
    sums_ref[0:2] = total[0:2]


def scatter(dkv, dq, normed, wfull, tokens, mgrad, small, keep, over, near, far, sums):
    rows, width = tokens.shape
    fourth = width // 4
    dma = pltpu.SemaphoreType.DMA
    wide_q, wide_v = 2 * BLK, 2 * HW
    kv_block = (rows, wide_v)
    full = (rows, width)
    unit = (UNIT, width)

    def weight_scratch(wide):
        return [
            pltpu.VMEM((2, fourth, wide), f32),
            pltpu.VMEM((2, fourth, wide), bf16),
            pltpu.VMEM((2, fourth, wide), bf16),
            *[pltpu.VMEM((fourth, wide), bf16)] * 4,
        ]

    return pl.pallas_call(
        scatter_kernel,
        out_shape=(
            jax.ShapeDtypeStruct(full, f32),
            jax.ShapeDtypeStruct((2, 2, GROUPS, *unit), bf16),
            jax.ShapeDtypeStruct((2, GROUPS, fourth, wide_q), bf16),
            jax.ShapeDtypeStruct((2, GROUPS, fourth, wide_v), bf16),
            jax.ShapeDtypeStruct((24, width), f32),
        ),
        in_specs=[anywhere()] * 10 + [whole_vmem()] * 2,
        out_specs=(whole_vmem(), anywhere(), anywhere(), anywhere(), whole_vmem()),
        scratch_shapes=[
            *[
                pltpu.VMEM(item.shape, item.dtype)
                for item in (dq, normed, wfull, tokens, mgrad, keep, over)
            ],
            pltpu.VMEM((48 * GROUPS, width), bf16),
            pltpu.VMEM(far.shape, bf16),
            pltpu.VMEM((GROUPS, 2, 2, *kv_block), bf16),
            pltpu.VMEM((GROUPS, 2, 2, *kv_block), bf16),
            pltpu.VMEM((GROUPS, 2, *kv_block), f32),
            pltpu.VMEM((GROUPS, 2, *kv_block), bf16),
            pltpu.VMEM((GROUPS, 2, *kv_block), bf16),
            pltpu.VMEM((GROUPS, *kv_block), bf16),
            pltpu.VMEM((GROUPS, *kv_block), bf16),
            pltpu.VMEM((GROUPS, *full), f32),
            pltpu.VMEM(full, f32),
            pltpu.VMEM((2, GROUPS, *full), bf16),
            pltpu.VMEM((GROUPS, *full), bf16),
            pltpu.VMEM((width, wide_v), f32),
            pltpu.VMEM((GROUPS, *unit), f32),
            pltpu.VMEM(unit, f32),
            pltpu.VMEM((2, GROUPS, *unit), bf16),
            pltpu.VMEM((GROUPS, *unit), bf16),
            pltpu.VMEM(unit, bf16),
            *weight_scratch(wide_q),
            *weight_scratch(wide_v),
            pltpu.VMEM((6, 24, width), f32),
            pltpu.VMEM((8, width), f32),
            pltpu.VMEM((8, width), f32),
            pltpu.VMEM((len(AROUND) + GROUPS - 1, 8, width), f32),
            dma((9,)),
            dma((GROUPS,)), dma((GROUPS,)), dma((GROUPS,)), dma((GROUPS,)), dma((GROUPS,)), dma((GROUPS,)), dma((GROUPS,)),
            dma((GROUPS,)), dma((2, GROUPS)),
            dma((GROUPS,)), dma((2, GROUPS)), dma((2,)), dma((GROUPS,)), dma((GROUPS,)),
            dma((GROUPS,)), dma((GROUPS,)), dma((2, GROUPS)), dma((2, GROUPS)),
            dma((3,)), dma((3,)), dma((2,)), dma((GROUPS,)), dma((GROUPS,)), dma((GROUPS,)), dma((GROUPS,)),
            dma((3,)), dma((3,)), dma((2,)), dma((GROUPS,)), dma((GROUPS,)), dma((GROUPS,)), dma((GROUPS,)),
            dma((6,)), dma((6,)), dma((10,)), dma((10,)), dma((1,)),
        ],
        compiler_params=pltpu.CompilerParams(
            collective_id=2, has_side_effects=True, vmem_limit_bytes=54 << 20
        ),
        name="scatter",
    )(dkv, dq, normed, wfull, tokens, mgrad, keep, over, near, far, small, sums)


def pack_kv(key_part, value_part):
    return jnp.concatenate(
        [key_part, value_part[..., 2 * DH :], value_part[..., : 2 * DH]], axis=-1
    )


def unpack_kv(both):
    return both[..., :HW], jnp.concatenate([both[..., HW + DH :], both[..., HW : HW + DH]], axis=-1)


def layout_kernel(
    big_ref, query_ref, kv_ref, sums_ref, base_ref, got_ref,
    up_out, down_out, wo_out, query_out, key_out, value_out,
    low_gain, low_shift, query_bias, value_bias, out_bias, high_gain, high_shift, up_bias, down_bias, result_out,
):
    x = lax.axis_index("x")
    width = big_ref.shape[-1]
    half = width // 2
    result_out[...] = (base_ref[...] + got_ref[...].astype(f32)).astype(bf16)
    for core in range(2):
        down_out[core] = big_ref[core, 0, 0:96].astype(f32)
        wo_out[core] = big_ref[core, 0, 192:UNIT].astype(f32)
        for owner in range(2):
            lane = (2 * owner + core) * width
            up_out[:, lane : lane + width] = big_ref[core, 0, 96 + 48 * owner : 144 + 48 * owner].astype(f32)
        query_out[core] = jnp.concatenate(
            [query_ref[core, z].astype(f32)[:, :HW] for z in range(GROUPS)], axis=1
        )
        both = [unpack_kv(kv_ref[core, z].astype(f32)) for z in range(GROUPS)]
        key_out[core] = jnp.concatenate([item[0] for item in both], axis=1)
        value_out[core] = jnp.concatenate([item[1] for item in both], axis=1)

    @pl.when(pl.program_id(0) == 0)
    def _():
        def own_half(row):
            whole = sums_ref[row : row + 1]
            return jnp.where(x == 0, whole[:, :half], whole[:, half:]).reshape(half)

        for ref, row in (
            (low_gain, 0), (low_shift, 1), (out_bias, 2), (high_gain, 3), (high_shift, 4), (down_bias, 5),
        ):
            ref[...] = own_half(row)
        pair = [sums_ref[pl.ds(16 + 2 * x + i, 1)] for i in range(2)]
        query_bias[...] = jnp.concatenate([item[:, :HW] for item in pair], axis=1).reshape(half)
        value_bias[...] = jnp.concatenate(
            [unpack_kv(item[:, 2 * BLK : 2 * BLK + 2 * HW])[1] for item in pair], axis=1
        ).reshape(half)
        up_bias[...] = jnp.concatenate(
            [sums_ref[pl.ds(8 + 2 * x + i, 1)] for i in range(2)], axis=1
        ).reshape(2 * width)


def lay_out(big, query, kv, sums, base, got):
    width = big.shape[-1]
    half, fourth = width // 2, width // 4
    rows = fourth // PARTS

    def spec(shape, index):
        return pl.BlockSpec(shape, index)

    def fixed(wide):
        return pl.BlockSpec((wide,), lambda p: (0,))

    narrow = spec((2, rows, width), lambda p: (0, p, 0))
    vector = jax.ShapeDtypeStruct((half,), f32)
    return pl.pallas_call(
        layout_kernel,
        grid=(PARTS,),
        out_shape=(
            jax.ShapeDtypeStruct((half, 4 * width), f32),
            jax.ShapeDtypeStruct((2, width, width), f32),
            *[jax.ShapeDtypeStruct((2, fourth, width), f32)] * 4,
            *[vector] * 7,
            jax.ShapeDtypeStruct((2 * width,), f32),
            vector,
            jax.ShapeDtypeStruct(base.shape, bf16),
        ),
        in_specs=[
            spec((2, 1, UNIT, width), lambda p: (0, p, 0, 0)),
            spec((2, GROUPS, rows, query.shape[-1]), lambda p: (0, 0, p, 0)),
            spec((2, GROUPS, rows, kv.shape[-1]), lambda p: (0, 0, p, 0)),
            spec(sums.shape, lambda p: (0, 0)),
            spec((base.shape[0] // PARTS, width), lambda p: (p, 0)),
            spec((base.shape[0] // PARTS, width), lambda p: (p, 0)),
        ],
        out_specs=(
            spec((48, 4 * width), lambda p: (p, 0)),
            spec((2, 96, width), lambda p: (0, p, 0)),
            *[narrow] * 4,
            *[fixed(half)] * 7,
            fixed(2 * width),
            fixed(half),
            spec((base.shape[0] // PARTS, width), lambda p: (p, 0)),
        ),
        compiler_params=pltpu.CompilerParams(
            vmem_limit_bytes=VMEM_LIMIT, dimension_semantics=("arbitrary",)
        ),
        name="lay_out",
    )(big, query, kv, sums, base, got)


ROWS = ("s", "r", "core", "x")
ALL = ("g", "s", "r", "core", "x")


def shards(
    tokens, cotangent, doc_lengths, deal, first_gain, first_shift, query_weight, query_bias,
    key_weight, value_weight, value_bias, output_weight, output_bias, second_gain, second_shift,
    up_weight, up_bias, down_weight, down_bias,
):
    rows, width = tokens.shape
    half = width // 2
    blocks = deal.shape[0]
    core, x = lax.axis_index("core"), lax.axis_index("x")
    swap = ((0, 1), (1, 0))

    def up_columns(owner):
        return lax.dynamic_slice_in_dim(up_weight, (2 * owner + core) * width, width, 1)

    def stay(*items):
        return tuple(pltpu.with_memory_space_constraint(item, pltpu.HBM) for item in items)

    kv, q, normed, small, wfull, wo = gather(
        *stay(
            tokens, query_weight, key_weight, value_weight, output_weight,
            first_gain, first_shift, output_bias, second_gain, second_shift, down_bias, query_bias, value_bias, up_bias,
        )
    )
    wide = blocks > 8 * 2 * GROUPS
    if wide:
        kv = lax.all_gather(kv, "s", axis=0, tiled=True)
    kv = kv.reshape(blocks, BLK, 2 * HW)
    q = q.reshape(2 * GROUPS, BLK, 2 * BLK)
    up_other, kv = lax.optimization_barrier((up_columns(1 - x), kv))
    up_other = lax.ppermute(up_other, "x", swap)
    out_t, kept, lse = attend_forward(deal, doc_lengths, q, kv)
    base, x_give, grad_middle, grad_t, kept_part, over, far, sums = dense(
        out_t, tokens, cotangent, small, wo, up_columns(x), up_other, down_weight
    )
    over = lax.ppermute(over, "r", swap)
    x_got = lax.ppermute(x_give, "x", swap)
    far = lax.ppermute(far, ("r", "x"), ((0, 3), (1, 2), (2, 1), (3, 0)))
    dq, dkv = attend_backward(deal, doc_lengths, q, kv, lse, grad_t, kept)
    dkv = dkv.reshape(-1, GROUPS, rows, 2 * HW)
    if wide:
        dkv = lax.psum_scatter(dkv, "s", scatter_dimension=0, tiled=True)
    dkv = dkv.reshape(2, 2, 2, GROUPS, rows, 2 * HW)
    dq = dq.reshape(GROUPS, rows, 2 * BLK)
    grad_tokens, big, query_own, kv_own, sums = scatter(
        *stay(dkv, dq, normed, wfull, tokens, grad_middle), small, *stay(kept_part, over, x_got, far), sums
    )
    if wide:
        big, query_own, kv_own, sums = (
            lax.psum(item, "s") for item in (big, query_own, kv_own, sums)
        )

    (
        up_own, down_own, wo_own, query_own, key_own, value_own,
        low_gain, low_shift, query_sum, value_sum, out_sum, high_gain, high_shift, up_sum, down_sum, result,
    ) = lay_out(big.reshape(2, PARTS, UNIT, width), query_own, kv_own, sums, *stay(base, x_got))

    def flat(item):
        return item.reshape(-1, width)

    return (
        result,
        grad_tokens,
        low_gain,
        low_shift,
        flat(query_own),
        query_sum,
        flat(key_own),
        flat(value_own),
        value_sum,
        flat(wo_own),
        out_sum,
        high_gain,
        high_shift,
        up_own,
        up_sum,
        flat(down_own),
        down_sum,
    )


def solution(mesh):
    devices = mesh.devices
    inner_mesh = Mesh(devices.reshape(GROUPS, devices.shape[0] // (4 * GROUPS), 2, 2, 2), ALL)
    row = P(ALL, None)
    mat = P("x", None)
    vec = P("x")
    in_specs = (
        row, row, P(), P(), vec, vec, mat, vec, mat, mat, vec, mat, vec, vec, vec, mat, vec, mat, vec,
    )
    out_specs = (
        row, row, vec, vec, mat, vec, mat, mat, vec, mat, vec, vec, vec, mat, vec, mat, vec,
    )
    return jax.shard_map(
        shards, mesh=inner_mesh, in_specs=in_specs, out_specs=out_specs, check_vma=False
    )
```

```python
import jax
import jax.numpy as jnp
from jax import lax
from jax.experimental import pallas as pl
from jax.experimental.pallas import tpu as pltpu
from jax.sharding import Mesh
from jax.sharding import PartitionSpec as P

HEADS = 12
DH = 64
NSUM = 50
SEG = 2048
BLK = 128
GROUPS = 4
PER = HEADS // GROUPS
HW = PER * DH
WIDE = PER * BLK
CHUNK = 2 * BLK
DEPTH = 8
EPS = 1e-05
SCALE = 0.125
MASKED = -1e30
ROOT_HALF = 0.7071067811865476
PDF_SCALE = 0.3989422804014327
VMEM_LIMIT = 56 << 20
bf16 = jnp.bfloat16
f32 = jnp.float32


def layer_norm(values, gain, shift):
    mean = jnp.mean(values, axis=-1, keepdims=True)
    centred = values - mean
    spread = jnp.mean(centred * centred, axis=-1, keepdims=True)
    return centred * lax.rsqrt(spread + EPS) * gain + shift


def outer(left, right):
    return lax.dot_general(left, right, (((0,), (0,)), ((), ())), preferred_element_type=f32)


def inner(left, right):
    return lax.dot_general(left, right, (((1,), (1,)), ((), ())), preferred_element_type=f32)


def dot(left, right):
    return jnp.dot(left, right, preferred_element_type=f32)


def survey(deal_ref, lengths_ref, where_ref, text_ref, low_ref, high_ref, first_ref):
    blocks = deal_ref.shape[0]
    per_group = blocks // (2 * GROUPS)
    rest = lax.axis_index(ROWS)

    def note(j, kept):
        pair = j // 2
        group = pair // per_group
        where_ref[deal_ref[j]] = ((pair - group * per_group) * GROUPS + group) * 2 + j % 2
        return kept

    lax.fori_loop(0, blocks, note, 0)
    starts = [jnp.int32(0)]
    for doc in range(lengths_ref.shape[0] - 1):
        starts.append(starts[-1] + lengths_ref[doc])

    def first_of(at):
        begin = jnp.zeros_like(at)
        for start in starts:
            begin = jnp.where(start <= at, jnp.maximum(begin, start), begin)
        return jnp.where(at - begin >= SEG + NSUM, begin + SEG, begin)

    for slot in range(2 * GROUPS):
        text = deal_ref[2 * ((slot // 2) * per_group + rest) + slot % 2]
        text_ref[slot] = text
        low_ref[slot] = first_of(text * BLK) // CHUNK
        high_ref[slot] = text // 2
        first_ref[slot] = first_of(text * BLK + lax.broadcasted_iota(jnp.int32, (1, BLK), 1))


def survey_scratch(blocks):
    slots = 2 * GROUPS
    return [
        pltpu.SMEM((blocks,), jnp.int32),
        pltpu.SMEM((slots,), jnp.int32),
        pltpu.SMEM((slots,), jnp.int32),
        pltpu.SMEM((slots,), jnp.int32),
        pltpu.VMEM((slots, 1, BLK), jnp.int32),
    ]


def spread_heads_t(part_t, order):
    rows = []
    zero = jnp.zeros((DH, BLK), part_t.dtype)
    for head in order:
        if head is None:
            rows.append(jnp.zeros((DH, WIDE), part_t.dtype))
        else:
            piece = part_t[DH * head : DH * head + DH]
            rows.append(
                jnp.concatenate([piece if h == head else zero for h in range(PER)], axis=1)
            )
    return jnp.concatenate(rows, axis=0)


K_ORDER = (0, 1, 2, None)
V_ORDER = (None, 2, 0, 1)


def visible(chunk, first, own):
    at = chunk * CHUNK + lax.broadcasted_iota(jnp.int32, (CHUNK, BLK), 0)
    allowed = (at >= first) & (at <= own)
    return jnp.concatenate([allowed] * PER, axis=1)


def load_chunk(kv_ref, where_ref, chunk):
    return jnp.concatenate(
        [kv_ref[where_ref[2 * chunk]], kv_ref[where_ref[2 * chunk + 1]]], axis=0
    )


def forward_kernel(
    deal_ref, lengths_ref, q_ref, kv_ref,
    out_ref, wide_ref, lse_ref,
    where_ref, text_ref, low_ref, high_ref, first_ref, acc_ref,
):
    survey(deal_ref, lengths_ref, where_ref, text_ref, low_ref, high_ref, first_ref)

    def one_slot(slot, kept):
        wide_q = spread_heads_t(q_ref[slot].T[:HW], K_ORDER)
        first = first_ref[slot]
        own = text_ref[slot] * BLK + lax.broadcasted_iota(jnp.int32, (1, BLK), 1)
        last_first = jnp.max(first)
        acc_ref[...] = jnp.zeros_like(acc_ref)

        def step(double, carry):
            top, total = carry
            scores = []
            for part in range(2):
                keys = load_chunk(kv_ref, where_ref, 2 * double + part)[:, : 2 * BLK]
                scores.append(jnp.where(visible(2 * double + part, first, own), dot(keys, wide_q), MASKED))
            scores = jnp.concatenate(scores, axis=0)
            fresh = jnp.maximum(top, jnp.max(scores, axis=0, keepdims=True))
            expo = jnp.exp(scores - fresh)
            shrink = jnp.exp(top - fresh)
            total = total * shrink + jnp.sum(expo, axis=0, keepdims=True)
            vals = jnp.concatenate([load_chunk(kv_ref, where_ref, 2 * double + part)[:, BLK:] for part in range(2)], axis=0)
            acc_ref[...] = acc_ref[...] * shrink + outer(vals, expo.astype(bf16))
            return fresh, total

        top, total = lax.fori_loop(
            low_ref[slot] // 2,
            high_ref[slot] // 2 + 1,
            step,
            (jnp.full((1, WIDE), MASKED, f32), jnp.zeros((1, WIDE), f32)),
        )
        lse_ref[slot] = top + jnp.log(total)
        scaled = acc_ref[...] / total
        pieces = []
        for head in range(PER):
            row = DH * V_ORDER.index(head)
            pieces.append(scaled[row : row + DH, BLK * head : BLK * head + BLK])
        whole = jnp.concatenate(pieces, axis=0)
        wide_ref[slot] = whole
        out_ref[slot] = whole.astype(bf16)
        return kept

    lax.fori_loop(0, q_ref.shape[0], one_slot, 0)


def whole_vmem():
    return pl.BlockSpec(memory_space=pltpu.VMEM)


def whole_smem():
    return pl.BlockSpec(memory_space=pltpu.SMEM)


def attend_forward(deal, lengths, q, kv):
    slots = q.shape[0]
    blocks = kv.shape[0]
    return pl.pallas_call(
        forward_kernel,
        out_shape=(
            jax.ShapeDtypeStruct((slots, HW, BLK), bf16),
            jax.ShapeDtypeStruct((slots, HW, BLK), f32),
            jax.ShapeDtypeStruct((slots, 1, WIDE), f32),
        ),
        in_specs=[whole_smem()] * 2 + [whole_vmem()] * 2,
        out_specs=(whole_vmem(),) * 3,
        scratch_shapes=[
            *survey_scratch(blocks),
            pltpu.VMEM((2 * BLK, WIDE), f32),
        ],
        compiler_params=pltpu.CompilerParams(vmem_limit_bytes=(6 << 20) + kv.size // 5 * 16),
        name="attend_forward",
    )(deal, lengths, q, kv)


def backward_kernel(
    deal_ref, lengths_ref, q_ref, kv_ref, lse_ref, do_ref, wide_ref,
    dq_ref, dkv_ref, where_ref, text_ref, low_ref, high_ref, first_ref, qt_ref, qm_ref, dot_ref, dom_ref, delta_ref, acc_ref, dk_acc, dv_acc,
    packed_ref, count_ref, list_ref, out_sem,
):
    survey(deal_ref, lengths_ref, where_ref, text_ref, low_ref, high_ref, first_ref)
    slots = q_ref.shape[0]
    chunks = kv_ref.shape[0] // 2

    def ready(slot, _):
        q = q_ref[slot]
        qt_ref[slot] = spread_heads_t(q.T[:HW], K_ORDER)
        lane = lax.broadcasted_iota(jnp.int32, (BLK, 2 * BLK), 1) // DH
        zero = jnp.zeros_like(q)
        qm_ref[slot] = jnp.concatenate(
            [jnp.where(lane == K_ORDER.index(h), q, zero) for h in range(PER)], axis=0
        )
        grad_t = do_ref[slot]
        dot_ref[slot] = spread_heads_t(grad_t, V_ORDER)
        ordered = jnp.concatenate(
            [
                jnp.zeros((DH, BLK), bf16) if h is None else grad_t[DH * h : DH * h + DH]
                for h in V_ORDER
            ],
            axis=0,
        ).T
        dom_ref[slot] = jnp.concatenate(
            [jnp.where(lane == V_ORDER.index(h), ordered, zero) for h in range(PER)], axis=0
        )
        both = grad_t.astype(f32) * wide_ref[slot]
        delta_ref[slot] = jnp.concatenate(
            [jnp.sum(both[DH * h : DH * h + DH], axis=0, keepdims=True) for h in range(PER)],
            axis=1,
        )
        acc_ref[slot] = jnp.zeros((HW, WIDE), f32)
        return _

    lax.fori_loop(0, slots, ready, 0)

    def clear(chunk, kept):
        count_ref[chunk] = 0
        return kept

    lax.fori_loop(0, chunks, clear, 0)

    def enlist(slot, kept):
        def seen(chunk, kept):
            count = count_ref[chunk]
            list_ref[chunk * slots + count] = slot
            count_ref[chunk] = count + 1
            return kept

        lax.fori_loop(low_ref[slot], high_ref[slot] + 1, seen, 0)
        return kept

    lax.fori_loop(0, slots, enlist, 0)

    def written(chunk, i):
        return pltpu.make_async_copy(
            packed_ref.at[chunk % DEPTH, i], dkv_ref.at[where_ref[2 * chunk + i]], out_sem.at[chunk % DEPTH, i]
        )

    def one_chunk(chunk, kept):
        part = load_chunk(kv_ref, where_ref, chunk)
        keys = part[:, : 2 * BLK]
        vals = part[:, BLK:]
        keys_t = keys.T[:HW]
        dk_acc[...] = jnp.zeros_like(dk_acc)
        dv_acc[...] = jnp.zeros_like(dv_acc)

        def one_slot(i, kept):
            for half in range(2):
                attend(list_ref[chunk * slots + 2 * i + half])
            return kept

        def attend(slot):
            own = text_ref[slot] * BLK + lax.broadcasted_iota(jnp.int32, (1, BLK), 1)
            scores = dot(keys, qt_ref[slot])
            dprobs = dot(vals, dot_ref[slot])
            probs = jnp.where(visible(chunk, first_ref[slot], own), jnp.exp(scores - lse_ref[slot]), 0.0)
            dscores = (probs * (dprobs - delta_ref[slot])).astype(bf16)
            dv_acc[...] += dot(probs.astype(bf16), dom_ref[slot])
            dk_acc[...] += dot(dscores, qm_ref[slot])
            acc_ref[slot] += dot(keys_t, dscores)

        lax.fori_loop(0, count_ref[chunk] // 2, one_slot, 0)
        pl.when(count_ref[chunk] % 2 == 1)(lambda: attend(list_ref[chunk * slots + count_ref[chunk] - 1]))
        packed = jnp.concatenate(
            [
                dk_acc[:, :BLK],
                dk_acc[:, BLK:] + dv_acc[:, :BLK],
                dv_acc[:, BLK:],
            ],
            axis=1,
        ).astype(bf16)

        @pl.when(chunk >= DEPTH)
        def _():
            for i in range(2):
                written(chunk - DEPTH, i).wait()

        for i in range(2):
            packed_ref[chunk % DEPTH, i] = packed[BLK * i : BLK * i + BLK]
            written(chunk, i).start()
        return kept

    lax.fori_loop(0, chunks, one_chunk, 0)
    for last in range(DEPTH):
        for i in range(2):
            written(chunks - DEPTH + last, i).wait()

    def finish(slot, _):
        total = acc_ref[slot]
        kept = jnp.concatenate(
            [total[DH * h : DH * h + DH, BLK * h : BLK * h + BLK] for h in range(PER)]
            + [jnp.zeros((DH, BLK), f32)],
            axis=0,
        )
        dq_ref[slot] = kept.T.astype(bf16)
        return _

    lax.fori_loop(0, slots, finish, 0)


def attend_backward(deal, lengths, q, kv, lse, grad_t, wide):
    slots = q.shape[0]
    return pl.pallas_call(
        backward_kernel,
        out_shape=(
            jax.ShapeDtypeStruct((slots, BLK, 2 * BLK), bf16),
            jax.ShapeDtypeStruct(kv.shape, bf16),
        ),
        in_specs=[whole_smem()] * 2 + [whole_vmem()] * 5,
        out_specs=(whole_vmem(), in_hbm()),
        scratch_shapes=[
            *survey_scratch(kv.shape[0]),
            pltpu.VMEM((slots, 2 * BLK, WIDE), bf16),
            pltpu.VMEM((slots, WIDE, 2 * BLK), bf16),
            pltpu.VMEM((slots, 2 * BLK, WIDE), bf16),
            pltpu.VMEM((slots, WIDE, 2 * BLK), bf16),
            pltpu.VMEM((slots, 1, WIDE), f32),
            pltpu.VMEM((slots, HW, WIDE), f32),
            pltpu.VMEM((CHUNK, 2 * BLK), f32),
            pltpu.VMEM((CHUNK, 2 * BLK), f32),
            pltpu.VMEM((DEPTH, 2, BLK, 2 * HW), bf16),
            pltpu.SMEM((kv.shape[0] // 2,), jnp.int32),
            pltpu.SMEM((kv.shape[0] // 2 * slots,), jnp.int32),
            pltpu.SemaphoreType.DMA((DEPTH, 2)),
        ],
        compiler_params=pltpu.CompilerParams(
            vmem_limit_bytes=max(46 << 20, (17 << 20) + kv.size * 2)
        ),
        name="attend_backward",
    )(deal, lengths, q, kv, lse, grad_t, wide)


MESH = pl.DeviceIdType.MESH


def send(src, dst, out_sem, in_sem, **device):
    return pltpu.make_async_remote_copy(
        src_ref=src, dst_ref=dst, send_sem=out_sem, recv_sem=in_sem, device_id=device, device_id_type=MESH
    )


def place():
    return tuple(lax.axis_index(name) for name in ("g", "r", "core", "x"))


def seat(r, core, x):
    return (r * 2 + core) * 2 + x


AROUND = ((0, 0, 1), (0, 1, 0), (0, 1, 1), (1, 0, 0), (1, 0, 1), (1, 1, 0), (1, 1, 1))


def neighbour(r, core, x, step):
    dr, dc, dx = AROUND[step]
    return {"r": 1 - r if dr else r, "core": 1 - core if dc else core, "x": 1 - x if dx else x}


def greet(g, r, core, x, line, around=False):
    barrier = pltpu.get_barrier_semaphore()

    def hello(**device):
        pl.semaphore_signal(barrier, inc=1, device_id=device, device_id_type=MESH)

    if around:
        for step in range(len(AROUND)):
            hello(**neighbour(r, core, x, step))
    else:
        hello(core=1 - core)
        hello(x=1 - x)
        hello(r=1 - r)
    near = len(AROUND) if around else 3
    if line:
        for away in range(1, GROUPS):
            hello(g=lax.rem(g + away, GROUPS))
        pl.semaphore_wait(barrier, near + GROUPS - 1)
    else:
        pl.when(g > 0)(lambda: hello(g=g - 1))
        pl.when(g < GROUPS - 1)(lambda: hello(g=g + 1))
        pl.semaphore_wait(barrier, near + 2 - jnp.where(g == 0, 1, 0) - jnp.where(g == GROUPS - 1, 1, 0))


NEAREST = ((0, 1, 2, 3), (1, 2, 0, 3), (2, 1, 3, 0), (3, 2, 1, 0))


def nearest(g, step):
    picked = NEAREST[0][step]
    for z in range(1, GROUPS):
        picked = jnp.where(g == z, NEAREST[z][step], picked)
    return picked


def prepare(g, x, weights, lines, narrow_ref, small_ref):
    half = weights.shape[1]
    odd = lax.rem(g, 2) == 1

    def columns(i):
        low = pl.multiple_of(3 * g // 2 * BLK, BLK)
        window = weights[i, :, pl.ds(low, 2 * BLK)]
        moved = jnp.concatenate([window[:, DH:], window[:, :DH]], axis=1)
        return jnp.where(odd, moved, window)

    lane = lax.broadcasted_iota(jnp.int32, (half, 2 * BLK), 1)
    query = columns(0)
    narrow_ref[:, : 2 * BLK] = jnp.where(lane < HW, query, jnp.zeros_like(query))
    narrow_ref[:, 2 * BLK :] = pack_kv(columns(1)[:, :HW], columns(2)[:, :HW])

    def line(i):
        return lines[i][...].astype(f32).reshape(1, -1)

    zero = jnp.zeros((1, half), f32)
    small_ref[...] = jnp.zeros_like(small_ref)
    for row in range(6):
        small_ref[row : row + 1] = jnp.where(
            x == 0, jnp.concatenate([line(row), zero], axis=1), jnp.concatenate([zero, line(row)], axis=1)
        )
    ups = line(8)
    for i in range(2):
        small_ref[pl.ds(8 + 2 * x + i, 1)] = ups[:, 2 * half * i : 2 * half * i + 2 * half]

    def part(i):
        mine = jnp.where(odd, line(i)[:, HW:], line(i)[:, :HW])
        return jnp.where(g // 2 == x, mine, jnp.zeros_like(mine))

    value = part(7)
    small_ref[12:13] = jnp.concatenate(
        [part(6), jnp.zeros((1, 2 * BLK), f32), value[:, 2 * DH :], value[:, : 2 * DH], jnp.zeros((1, BLK), f32)], axis=1
    )


def gather_kernel(
    tokens_ref, query_any, key_any, value_any, wo_ref, l0, l1, l2, l3, l4, l5, l6, l7, l8,
    kv_ref, q_ref, normed_ref, small_out, wfull, wo_out,
    lined, attn_w, narrow_ref, small_ref, small_in, kvs,
    z_own, z_send, z_recv, s_sem, n_send, n_recv, kv_send, kv_recv, kv_local, w_send, w_recv, w_local, a_sem,
):
    g, r, core, x = place()
    other = 1 - x
    rows, width = tokens_ref.shape
    half = width // 2
    fourth = half // 2
    eighth = half // 4
    loads = [
        pltpu.make_async_copy(ref, attn_w.at[i], a_sem.at[i]) for i, ref in enumerate((query_any, key_any, value_any))
    ]
    for load in loads:
        load.start()
    greet(g, r, core, x, False)

    def half_of(source, part):
        return lined.at[source, pl.ds(BLK * part, BLK)]

    def along(source, part, away, sem):
        return send(half_of(source, part), half_of(source, part), sem, z_recv.at[source, part], g=g + away)

    lined[g] = tokens_ref[...]
    for part in range(2):
        pl.when(g > 0)(lambda: along(g, part, -1, z_own.at[0, part]).start())
        pl.when(g < GROUPS - 1)(lambda: along(g, part, 1, z_own.at[1, part]).start())

    for load in loads:
        load.wait()
    prepare(g, x, attn_w, (l0, l1, l2, l3, l4, l5, l6, l7, l8), narrow_ref, small_ref)
    small_move = send(small_ref, small_in, s_sem.at[0], s_sem.at[1], x=other)
    small_move.start()
    mine = pl.ds(x * half + core * fourth, fourth)
    narrow_x = send(narrow_ref.at[pl.ds(core * fourth, fourth)], wfull.at[mine], n_send.at[0], n_recv.at[0], x=other)
    narrow_x.start()

    def wo_rows(owner, part):
        return wo_out.at[pl.ds(owner * half + core * fourth + part * eighth, eighth)]

    wo_x = send(wo_ref.at[pl.ds(core * fourth + r * eighth, eighth)], wo_rows(x, r), w_send.at[0], w_recv.at[0], x=other)
    wo_y = send(wo_rows(other, r), wo_rows(other, r), w_send.at[3], w_recv.at[3], r=1 - r)
    wo_s = [
        send(wo_rows(other, part), wo_rows(other, part), w_send.at[6 + i], w_recv.at[6 + i], core=1 - core)
        for i, part in enumerate((r, 1 - r))
    ]
    wo_x.start()
    locals_ = [pltpu.make_async_copy(wo_ref, wo_out.at[pl.ds(x * half, half)], w_local.at[0])]
    for item in locals_:
        item.start()

    wfull[pl.ds(x * half, half)] = narrow_ref[...]
    narrow_x.wait_recv()
    theirs = wfull.at[pl.ds(other * half + core * fourth, fourth)]
    narrow_s = send(theirs, theirs, n_send.at[1], n_recv.at[1], core=1 - core)
    narrow_s.start()
    small_move.wait_recv()
    small_out[...] = small_ref[...] + small_in[...]
    narrow_s.wait_recv()

    own = seat(r, core, x)

    def span(step):
        return (step, 0, rows) if step < GROUPS - 1 else (GROUPS - 1, BLK * (step - GROUPS + 1), BLK)

    def block(owner, step):
        nth, low, count = span(step)
        return kv_ref.at[owner, nearest(g, nth), pl.ds(low, count)]

    def made(step):
        nth, low, count = span(step)
        return kvs.at[nth, pl.ds(low, count)]

    def push(step, kind, src, dst, **device):
        send(src, dst, kv_send.at[kind, step], kv_recv.at[kind, step], **device).start()

    def settle(step, kind, owner):
        arrived(block(owner, step), kv_send.at[kind, step], kv_recv.at[kind, step], x)

    def forward(step):
        by_x = block(seat(r, core, other), step)
        settle(step, 0, seat(r, core, other))
        if step % 2 == 0:
            push(step, 3, by_x, by_x, r=1 - r)
        push(step, 4, by_x, by_x, core=1 - core)
        by_y = block(seat(1 - r, core, x), step)
        settle(step, 1, seat(1 - r, core, x))
        if step % 2 == 1:
            push(step, 3, by_y, by_y, x=other)
        push(step, 5, by_y, by_y, core=1 - core)

    def forward_far(step):
        far = block(seat(1 - r, core, other), step)
        settle(step, 3, seat(1 - r, core, other))
        push(step, 6, far, far, core=1 - core)

    def take(nth, part):
        source = nearest(g, nth)
        arrived(half_of(source, part), z_send.at[source, part], z_recv.at[source, part], x)
        pl.when((source < g) & (g < GROUPS - 1))(lambda: along(source, part, 1, z_send.at[source, part]).start())
        pl.when((source > g) & (g > 0))(lambda: along(source, part, -1, z_send.at[source, part]).start())

    def project(step):
        nth, low, count = span(step)
        source = nearest(g, nth)
        taken = pl.ds(low, count)
        values = lined[source, taken].astype(f32)
        normed = layer_norm(values, small_out[0:1], small_out[1:2]).astype(bf16)
        normed_ref[source, taken] = normed
        both = dot(normed, wfull[...]) + small_out[12:13, : wfull.shape[1]]
        kvs[nth, taken] = both[:, 2 * BLK :].astype(bf16)
        push(step, 0, made(step), block(own, step), x=other)
        push(step, 1, made(step), block(own, step), r=1 - r)
        push(step, 2, made(step), block(own, step), core=1 - core)
        q_ref[source, taken] = (both[:, : 2 * BLK] * SCALE).astype(bf16)
        pltpu.make_async_copy(made(step), block(own, step), kv_local.at[step]).start()

    at_end = (g == 0) | (g == GROUPS - 1)
    between = jnp.logical_not(at_end)
    project(0)
    take(1, 0)
    take(1, 1)

    @pl.when(between)
    def _():
        take(2, 0)
        take(2, 1)

    project(1)
    forward(0)

    @pl.when(at_end)
    def _():
        take(2, 0)
        take(2, 1)

    project(2)

    @pl.when(at_end)
    def _():
        forward(1)
        forward_far(0)

    take(3, 0)
    pl.when(between)(lambda: take(3, 1))
    project(3)
    pl.when(at_end)(lambda: take(3, 1))
    project(4)

    @pl.when(between)
    def _():
        forward(1)
        forward_far(0)

    wo_x.wait_recv()
    wo_y.start()
    wo_s[0].start()
    forward(2)
    forward_far(1)
    forward(3)
    forward_far(2)
    forward(4)
    forward_far(3)
    arrived(wo_rows(other, 1 - r), w_send.at[3], w_recv.at[3], x)
    wo_s[1].start()
    forward_far(4)

    for step in range(GROUPS + 1):
        pltpu.make_async_copy(made(step), block(own, step), kv_local.at[step]).wait()
        settle(step, 2, seat(r, 1 - core, x))
        settle(step, 4, seat(r, 1 - core, other))
        settle(step, 5, seat(1 - r, 1 - core, x))
        settle(step, 6, seat(1 - r, 1 - core, other))
        for kind in range(7):
            left(made(step), kv_send.at[kind, step], kv_recv.at[kind, step], x)
    for part in range(2):
        pl.when(g > 0)(lambda: left(half_of(g, part), z_own.at[0, part], z_recv.at[g, part], x))
        pl.when(g < GROUPS - 1)(lambda: left(half_of(g, part), z_own.at[1, part], z_recv.at[g, part], x))
        for nth in range(1, GROUPS):
            source = nearest(g, nth)
            passed = ((source < g) & (g < GROUPS - 1)) | ((source > g) & (g > 0))
            pl.when(passed)(
                lambda: left(half_of(source, part), z_send.at[source, part], z_recv.at[source, part], x)
            )
    small_move.wait_send()
    narrow_x.wait_send()
    narrow_s.wait_send()
    for item in locals_:
        item.wait()
    for item in (wo_x, wo_y, *wo_s):
        item.wait_send()
    for i, part in enumerate((r, 1 - r)):
        there = wo_out.at[pl.ds(other * half + (1 - core) * fourth + part * eighth, eighth)]
        send(there, there, w_send.at[6 + i], w_recv.at[6 + i], core=1 - core).wait_recv()


def anywhere():
    return pl.BlockSpec(memory_space=pl.ANY)


def in_hbm():
    return pl.BlockSpec(memory_space=pltpu.HBM)


def gather(tokens, query, key, value, wo, *lines):
    rows, width = tokens.shape
    wide = 2 * BLK + 2 * HW
    small = (16, width)
    dma = pltpu.SemaphoreType.DMA
    return pl.pallas_call(
        gather_kernel,
        out_shape=(
            jax.ShapeDtypeStruct((8, GROUPS, rows, 2 * HW), bf16),
            jax.ShapeDtypeStruct((GROUPS, rows, 2 * BLK), bf16),
            jax.ShapeDtypeStruct((GROUPS, rows, width), bf16),
            jax.ShapeDtypeStruct(small, f32),
            jax.ShapeDtypeStruct((width, wide), bf16),
            jax.ShapeDtypeStruct((width, width), bf16),
        ),
        in_specs=[whole_vmem(), *[in_hbm()] * 4, *[whole_vmem()] * len(lines)],
        out_specs=(anywhere(), *(whole_vmem(),) * 5),
        scratch_shapes=[
            pltpu.VMEM((GROUPS, rows, width), bf16),
            pltpu.VMEM((3, width // 2, width), bf16),
            pltpu.VMEM((width // 2, wide), bf16),
            pltpu.VMEM(small, f32),
            pltpu.VMEM(small, f32),
            pltpu.VMEM((GROUPS, rows, 2 * HW), bf16),
            dma((2, 2)), dma((GROUPS, 2)), dma((GROUPS, 2)), dma((2,)), dma((2,)), dma((2,)),
            dma((7, GROUPS + 1)), dma((7, GROUPS + 1)), dma((GROUPS + 1,)), dma((8,)), dma((8,)), dma((2,)), dma((3,)),
        ],
        compiler_params=pltpu.CompilerParams(
            collective_id=0, has_side_effects=True, vmem_limit_bytes=16 << 20
        ),
        name="gather",
    )(tokens, query, key, value, wo, *lines)


def erf_parts(values):
    below = 0.5 * (1.0 + lax.erf(values * ROOT_HALF))
    return below, PDF_SCALE * jnp.exp(-0.5 * values * values)


PARTS = 8
UNIT = 216
KEPT = 168


def dense_kernel(
    out_t_ref, tokens_ref, cot_ref, small_ref, wo_ref, up_mine, up_other, down_any,
    base_ref, x_give_ref, middle_grad_ref, grad_t_ref, keep_ref, give_ref, far_ref, sums_ref,
    down_ref, up_ref, attn_in, attn_t, cots, h2s, mid_ref, n2_ref, scales, part_y, part_d, in_y, in_d, pass_y, pass_d,
    x_y, x_d, hids, dus, branch_ref, grad_out, wo_keep, wo_give, wo_in, wo_pass, wo_x,
    l_sem, a_send, a_recv, c_send, c_recv, h_send, h_recv, y_send, y_recv, d_send, d_recv, o_send, o_recv,
    w_send, w_recv,
):
    g, r, core, x = place()
    other, sib = 1 - x, 1 - core
    rows, width = tokens_ref.shape
    half = width // 2
    fourth = half // 2
    loads = [
        pltpu.make_async_copy(
            down_any.at[pl.ds(pl.multiple_of(core * width, width), width)], down_ref, l_sem.at[0]
        ),
        pltpu.make_async_copy(up_mine, up_ref.at[pl.ds(x * half, half)], l_sem.at[1]),
        pltpu.make_async_copy(up_other, up_ref.at[pl.ds(other * half, half)], l_sem.at[2]),
    ]
    for load in loads:
        load.start()
    greet(g, r, core, x, True)
    pending = []

    def begin(src, dst, out_sem, in_sem, **device):
        move = send(src, dst, out_sem, in_sem, **device)
        move.start()
        pending.append(move)
        return move

    def other_group(away):
        return lax.rem(g + away, GROUPS)

    def rows_of(b):
        return pl.ds(BLK * b, BLK)

    for b in range(2):
        for away in range(1, GROUPS):
            to = other_group(away)
            begin(out_t_ref.at[2 * to + b], attn_in.at[g, b], a_send.at[b, away], a_recv.at[b, g], g=to)
        attn_in[g, b] = out_t_ref[2 * g + b]
        cots[b, 0] = cot_ref[rows_of(b)]
    cot_x = begin(cots.at[:, 0], cots.at[:, 2], c_send.at[2], c_recv.at[2], x=other)
    cot_moves = [begin(cots.at[:, 0], cots.at[:, 1], c_send.at[0], c_recv.at[0], core=sib)]
    sums_ref[...] = jnp.zeros_like(sums_ref)
    sums_ref[5:6] = jnp.sum(cot_ref[...].astype(f32), axis=0, keepdims=True)
    h2_moves = []

    def norm(b):
        for away in range(1, GROUPS):
            source = other_group(away)
            arrived(attn_in.at[source, b], a_send.at[b, away], a_recv.at[b, source], x)
        for source in range(GROUPS):
            attn_t[HW * source : HW * source + HW, BLK * b : BLK * b + BLK] = attn_in[source, b]
        middle = (
            tokens_ref[rows_of(b)].astype(f32)
            + outer(attn_t[:, BLK * b : BLK * b + BLK], wo_ref[...])
            + small_ref[2:3]
        )
        mid_ref[b] = middle
        mean = jnp.mean(middle, axis=-1, keepdims=True)
        centred = middle - mean
        scale = lax.rsqrt(jnp.mean(centred * centred, axis=-1, keepdims=True) + EPS)
        scales[b] = scale
        n2_ref[b] = centred * scale
        h2s[b, 0] = (n2_ref[b] * small_ref[3:4] + small_ref[4:5]).astype(bf16)
        h2_moves.append(
            (
                begin(h2s.at[b, 0], h2s.at[b, 2], h_send.at[b, 1], h_recv.at[b, 1], x=other),
                begin(h2s.at[b, 0], h2s.at[b, 1], h_send.at[b, 0], h_recv.at[b, 0], core=sib),
            )
        )

    def pass_on(b):
        h2_moves[b][0].wait_recv()
        return begin(h2s.at[b, 2], h2s.at[b, 3], h_send.at[b, 2], h_recv.at[b, 2], core=sib)

    bias_row = 8 + 2 * x + core

    def pair_of(ref, b, pair):
        return ref[b, 2 * pair : 2 * pair + 2].reshape(2 * BLK, width)

    def forward_backward(b, pair):
        cot = pair_of(cots, b, pair)
        expanded = dot(pair_of(h2s, b, pair), up_ref[...]) + small_ref[pl.ds(bias_row, 1)]
        below, density = erf_parts(expanded)
        hidden = (expanded * below).astype(bf16)
        hids[b, pair] = hidden
        slope = below + expanded * density
        grad_hidden = inner(cot, down_ref[...]).astype(bf16).astype(f32)
        grad_expand = (grad_hidden * slope).astype(bf16)
        dus[b, pair] = grad_expand
        part_d[b, pair] = inner(grad_expand, up_ref[...])
        part_y[b, pair] = dot(hidden, down_ref[...])
        sums_ref[pl.ds(bias_row, 1)] += jnp.sum(grad_expand.astype(f32), axis=0, keepdims=True)

    d_moves, y_passes = [None, None], [None, None]

    def near_pair(b):
        if b == 0:
            cot_moves[0].wait_recv()
        h2_moves[b][1].wait_recv()
        forward_backward(b, 0)
        return begin(part_d.at[b, 0, pl.ds(BLK, BLK)], in_d.at[b], d_send.at[b, 0], d_recv.at[b, 0], core=sib)

    def far_pair(b, passed):
        if b == 0:
            cot_moves[1].wait_recv()
        passed.wait_recv()
        forward_backward(b, 1)
        x_d[b, 0] = part_d[b, 1, BLK:].astype(bf16)
        across = begin(x_d.at[b, 0], pass_d.at[b], d_send.at[b, 1], d_recv.at[b, 1], core=sib)
        x_y[b] = part_y[b, 1, BLK:].astype(bf16)
        y_passes[b] = begin(x_y.at[b], pass_y.at[b], y_send.at[b, 1], y_recv.at[b, 1], core=sib)
        across.wait_recv()
        x_d[b, 1] = (part_d[b, 1, :BLK] + pass_d[b].astype(f32)).astype(bf16)
        return begin(x_d.at[b, 1], x_d.at[b, 2], d_send.at[b, 2], d_recv.at[b, 2], x=other)

    def back(b, near, far):
        near.wait_recv()
        far.wait_recv()
        grad_second = part_d[b, 0, :BLK] + in_d[b] + x_d[b, 2].astype(f32)
        n2 = n2_ref[b]
        sums_ref[3:4] += jnp.sum(grad_second * n2, axis=0, keepdims=True)
        sums_ref[4:5] += jnp.sum(grad_second, axis=0, keepdims=True)
        pulled = grad_second * small_ref[3:4]
        inward = (
            pulled - jnp.mean(pulled, axis=-1, keepdims=True) - n2 * jnp.mean(pulled * n2, axis=-1, keepdims=True)
        )
        grad_middle = cot_ref[rows_of(b)].astype(f32) + inward * scales[b]
        middle_grad_ref[rows_of(b)] = grad_middle
        branch = grad_middle.astype(bf16)
        branch_ref[rows_of(b)] = branch
        sums_ref[2:3] += jnp.sum(branch.astype(f32), axis=0, keepdims=True)
        grad_out_t = inner(wo_ref[...], branch).astype(bf16)
        for group in range(GROUPS):
            grad_out[group, b] = grad_out_t[HW * group : HW * group + HW]
        for away in range(1, GROUPS):
            to = other_group(away)
            begin(grad_out.at[to, b], grad_t_ref.at[2 * g + b], o_send.at[b, away], o_recv.at[b, g], g=to)
        grad_t_ref[2 * g + b] = grad_out[g, b]

    norm(0)
    norm(1)
    for load in loads:
        load.wait()
    near = [near_pair(0), None]
    cot_x.wait_recv()
    cot_moves.append(begin(cots.at[:, 2], cots.at[:, 3], c_send.at[1], c_recv.at[1], core=sib))
    passed = [pass_on(0), None]
    near[1] = near_pair(1)
    far = [far_pair(0, passed[0]), None]
    passed[1] = pass_on(1)
    far[1] = far_pair(1, passed[1])

    def over_rows(left, right):
        total = None
        for b in range(2):
            for pair in range(2):
                term = outer(left(b, pair), right(b, pair))
                total = term if total is None else total + term
        return total.astype(bf16)

    def parts(write):
        for y in range(2):
            pl.when(r == y)(lambda: write(keep_ref, y))
            pl.when(r != y)(lambda: write(give_ref, y))

    down_grad = over_rows(lambda b, pair: hids[b, pair], lambda b, pair: pair_of(cots, b, pair))

    def write_down(ref, y):
        for z in range(GROUPS):
            p = y * GROUPS + z
            ref[z, 0:96] = down_grad[96 * p : 96 * p + 96]

    parts(write_down)
    back(0, near[0], far[0])
    up_grad = over_rows(lambda b, pair: pair_of(h2s, b, pair), lambda b, pair: dus[b, pair])

    def up_part(p, h):
        return up_grad[half * h + 48 * p : half * h + 48 * p + 48]

    def write_up(y, h):
        @pl.when((r == y) & (x == h))
        def _():
            for z in range(GROUPS):
                keep_ref[z, 96:144] = up_part(y * GROUPS + z, h)

        @pl.when((r != y) & (x == h))
        def _():
            for z in range(GROUPS):
                give_ref[z, 96:144] = up_part(y * GROUPS + z, h)

        @pl.when((r == y) & (x != h))
        def _():
            for z in range(GROUPS):
                x_give_ref[rows + 48 * z : rows + 48 * z + 48] = up_part(y * GROUPS + z, h)

        @pl.when((r != y) & (x != h))
        def _():
            for z in range(GROUPS):
                far_ref[z] = up_part(y * GROUPS + z, h)

    for y in range(2):
        for h in range(2):
            write_up(y, h)
    back(1, near[1], far[1])

    for owner in range(2):
        for c in range(2):
            piece = dot(attn_t[half * owner + fourth * c : half * owner + fourth * c + fourth], branch_ref[...])

            @pl.when(core == c)
            def _():
                wo_keep[owner] = piece

            @pl.when(core != c)
            def _():
                wo_give[owner] = piece.astype(bf16)

    w_sib = begin(wo_give, wo_in, w_send.at[0], w_recv.at[0], core=sib)
    y_sibs = [
        begin(part_y.at[b, 0, pl.ds(BLK, BLK)], in_y.at[b], y_send.at[b, 0], y_recv.at[b, 0], core=sib)
        for b in range(2)
    ]
    w_sib.wait_recv()
    wo_pass[...] = (wo_keep[other] + wo_in[other].astype(f32)).astype(bf16)
    w_x = begin(wo_pass, wo_x, w_send.at[1], w_recv.at[1], x=other)
    for b in range(2):
        y_passes[b].wait_recv()
        x_give_ref[rows_of(b)] = (part_y[b, 1, :BLK] + pass_y[b].astype(f32)).astype(bf16)
        y_sibs[b].wait_recv()
        base_ref[rows_of(b)] = mid_ref[b] + part_y[b, 0, :BLK] + in_y[b] + small_ref[5:6]
    mine = wo_keep[x] + wo_in[x].astype(f32)
    for b in range(2):
        for away in range(1, GROUPS):
            source = other_group(away)
            arrived(grad_t_ref.at[2 * source + b], o_send.at[b, away], o_recv.at[b, source], x)
    w_x.wait_recv()
    wo_sum = (mine + wo_x[...].astype(f32)).astype(bf16)

    def write_wo(ref, y):
        for z in range(GROUPS):
            p = y * GROUPS + z
            ref[z, 144:KEPT] = wo_sum[24 * p : 24 * p + 24]

    parts(write_wo)
    for move in pending:
        move.wait_send()


def dense(out_t, tokens, cot, small, wo, up_mine, up_other, down):
    rows, width = tokens.shape
    dma = pltpu.SemaphoreType.DMA
    full = (rows, width)
    part = (BLK, width)
    pair = (2 * BLK, width)
    fourth = (width // 4, width)
    return pl.pallas_call(
        dense_kernel,
        out_shape=(
            jax.ShapeDtypeStruct(full, f32),
            jax.ShapeDtypeStruct((rows + 48 * GROUPS, width), bf16),
            jax.ShapeDtypeStruct(full, f32),
            jax.ShapeDtypeStruct(out_t.shape, bf16),
            jax.ShapeDtypeStruct((GROUPS, KEPT, width), bf16),
            jax.ShapeDtypeStruct((GROUPS, KEPT, width), bf16),
            jax.ShapeDtypeStruct((GROUPS, 48, width), bf16),
            jax.ShapeDtypeStruct(small.shape, f32),
        ),
        in_specs=[whole_vmem()] * 5 + [anywhere()] * 3,
        out_specs=(whole_vmem(),) * 8,
        scratch_shapes=[
            pltpu.VMEM((width, width), bf16),
            pltpu.VMEM((width, width), bf16),
            pltpu.VMEM((GROUPS, 2, HW, BLK), bf16),
            pltpu.VMEM((width, rows), bf16),
            pltpu.VMEM((2, 4, *part), bf16),
            pltpu.VMEM((2, 4, *part), bf16),
            pltpu.VMEM((2, *part), f32),
            pltpu.VMEM((2, *part), f32),
            pltpu.VMEM((2, BLK, 1), f32),
            pltpu.VMEM((2, 2, *pair), f32),
            pltpu.VMEM((2, 2, *pair), f32),
            pltpu.VMEM((2, *part), f32),
            pltpu.VMEM((2, *part), f32),
            pltpu.VMEM((2, *part), bf16),
            pltpu.VMEM((2, *part), bf16),
            pltpu.VMEM((2, *part), bf16),
            pltpu.VMEM((2, 3, *part), bf16),
            pltpu.VMEM((2, 2, *pair), bf16),
            pltpu.VMEM((2, 2, *pair), bf16),
            pltpu.VMEM(full, bf16),
            pltpu.VMEM((GROUPS, 2, HW, BLK), bf16),
            pltpu.VMEM((2, *fourth), f32),
            pltpu.VMEM((2, *fourth), bf16),
            pltpu.VMEM((2, *fourth), bf16),
            pltpu.VMEM(fourth, bf16),
            pltpu.VMEM(fourth, bf16),
            dma((3,)), dma((2, GROUPS)), dma((2, GROUPS)), dma((3,)), dma((3,)), dma((2, 3)), dma((2, 3)),
            dma((2, 2)), dma((2, 2)), dma((2, 3)), dma((2, 3)), dma((2, GROUPS)), dma((2, GROUPS)), dma((2,)), dma((2,)),
        ],
        compiler_params=pltpu.CompilerParams(
            collective_id=1, has_side_effects=True, vmem_limit_bytes=46 << 20
        ),
        name="dense",
    )(out_t, tokens, cot, small, wo, up_mine, up_other, down)


FARTHEST = ((3, 2, 1, 0), (3, 0, 2, 1), (0, 3, 1, 2), (0, 1, 2, 3))


def farthest(g, step):
    picked = FARTHEST[0][step]
    for z in range(1, GROUPS):
        picked = jnp.where(g == z, FARTHEST[z][step], picked)
    return picked


class Chain:
    def __init__(self, g, x, total, parts, inward, outward, out_sem, in_sem):
        self.g, self.x, self.total, self.parts = g, x, total, parts
        self.inward, self.outward, self.out_sem, self.in_sem = inward, outward, out_sem, in_sem

    def move(self, to, way):
        return send(
            self.outward.at[to], self.inward.at[way, to], self.out_sem.at[to], self.in_sem.at[way, to],
            g=jnp.clip(self.g + (1 if way == 0 else -1), 0, GROUPS - 1),
        )

    def step(self, to):
        g = self.g
        self.total[...] = self.parts[to].astype(f32)

        def take(way):
            arrived(self.inward.at[way, to], self.out_sem.at[to], self.in_sem.at[way, to], self.x)
            self.total[...] += self.inward[way, to].astype(f32)

        pl.when((to >= g) & (g > 0))(lambda: take(0))
        pl.when((to <= g) & (g < GROUPS - 1))(lambda: take(1))

        @pl.when(to != g)
        def _():
            self.outward[to] = self.total[...].astype(bf16)

        pl.when(to > g)(lambda: self.move(to, 0).start())
        pl.when(to < g)(lambda: self.move(to, 1).start())

    def finish(self):
        for step in range(GROUPS - 1):
            to = farthest(self.g, step)
            left(self.outward.at[to], self.out_sem.at[to], self.in_sem.at[0, to], self.x)


class Ring:
    def __init__(self, g, x, slot, own_sem, out_sem, in_sem):
        self.g, self.x, self.slot = g, x, slot
        self.own_sem, self.out_sem, self.in_sem = own_sem, out_sem, in_sem

    def move(self, source, way, sem):
        return send(
            self.slot(source), self.slot(source), sem, self.in_sem.at[source],
            g=jnp.clip(self.g + way, 0, GROUPS - 1),
        )

    def start(self):
        g = self.g
        pl.when(g > 0)(lambda: self.move(g, -1, self.own_sem.at[0]).start())
        pl.when(g < GROUPS - 1)(lambda: self.move(g, 1, self.own_sem.at[1]).start())

    def step(self, step):
        g, source = self.g, nearest(self.g, step)
        arrived(self.slot(source), self.out_sem.at[source], self.in_sem.at[source], self.x)
        pl.when((source < g) & (g < GROUPS - 1))(lambda: self.move(source, 1, self.out_sem.at[source]).start())
        pl.when((source > g) & (g > 0))(lambda: self.move(source, -1, self.out_sem.at[source]).start())
        return source

    def finish(self):
        g = self.g
        for i, there in enumerate((g > 0, g < GROUPS - 1)):
            pl.when(there)(lambda: left(self.slot(g), self.own_sem.at[i], self.in_sem.at[g], self.x))
        for step in range(1, GROUPS):
            source = nearest(g, step)
            passed = ((source < g) & (g < GROUPS - 1)) | ((source > g) & (g > 0))
            pl.when(passed)(
                lambda: left(self.slot(source), self.out_sem.at[source], self.in_sem.at[source], self.x)
            )


def arrived(what, out_sem, in_sem, x):
    send(what, what, out_sem, in_sem, x=1 - x).wait_recv()


def left(what, out_sem, in_sem, x):
    send(what, what, out_sem, in_sem, x=1 - x).wait_send()


def scatter_kernel(
    dkv_ref, dq_any, normed_any, wfull_any, tokens_any, mgrad_any, keep_any, over_any, near_any, far_any, small_ref, sums_in,
    tokens_grad_ref, big_ref, qout_ref, kvout_ref, sums_ref,
    dq_ref, normed_ref, wfull_ref, tokens_ref, mgrad_ref, kept, over, near, far,
    own_kv, sib_kv, keep_x, give_x, in_x, give_y, in_y, part_a, total_a, inward_a, outward_a, wg_kv,
    by_sum, total_b, inward_b, outward_b, unit,
    q_keep, q_give, q_in, q_pass, q_x, q_y, q_sum, v_keep, v_give, v_in, v_pass, v_x, v_y, v_sum,
    sums_got, late, late_sum, late_got,
    load_sem, own_sem, k_send, k_recv, x_send, x_recv, y_send, y_recv, ca_send, ca_recv,
    cb_send, cb_recv, rb_own, rb_send, rb_recv,
    fy_send, fy_recv, fs_send, fs_recv,
    q_send, q_recv, rq_own, rq_send, rq_recv, qs_send, qs_recv,
    v_send, v_recv, rv_own, rv_send, rv_recv, vs_send, vs_recv,
    s_send, s_recv, t_send, t_recv, l_sem,
):
    g, r, core, x = place()
    other, sib, far_r = 1 - x, 1 - core, 1 - r
    rows, width = tokens_ref.shape
    half = width // 2
    fourth = half // 2
    wide_q = 2 * BLK
    loads = [
        pltpu.make_async_copy(what, where, load_sem.at[i])
        for i, (what, where) in enumerate(
            (
                (keep_any, kept), (over_any, over), (near_any.at[pl.ds(rows, 48 * GROUPS)], near), (far_any, far),
                (dq_any, dq_ref), (normed_any, normed_ref), (wfull_any, wfull_ref), (tokens_any, tokens_ref),
                (mgrad_any, mgrad_ref),
            )
        )
    ]
    for load in loads:
        load.start()
    greet(g, r, core, x, True, True)
    pending = []

    def begin(src, dst, out_sem, in_sem, **device):
        move = send(src, dst, out_sem, in_sem, **device)
        move.start()
        pending.append(move)
        return move

    def settled(move):
        move.wait_recv()
        move.wait_send()
        pending[:] = [item for item in pending if item is not move]

    kv_moves = []

    def start_kv():
        for i in range(GROUPS):
            c = farthest(g, i)
            own = pltpu.make_async_copy(dkv_ref.at[:, core, :, c], own_kv.at[i], own_sem.at[i])
            own.start()
            kv_moves.append(
                (own, begin(dkv_ref.at[:, sib, :, c], sib_kv.at[i], k_send.at[i], k_recv.at[i], core=sib))
            )

    def split(total, keep, give):
        for owner in range(2):
            for c in range(2):
                low = half * owner + fourth * c
                chunk = total[low : low + fourth]

                @pl.when(core == c)
                def _():
                    keep[owner] = chunk

                @pl.when(core != c)
                def _():
                    give[owner] = chunk.astype(bf16)

    def scaled(c):
        return dq_ref[c] * bf16(SCALE)

    q_move = send(q_give, q_in, q_send.at[0], q_recv.at[0], core=sib)

    def query_grad():
        loads[4].wait()
        loads[5].wait()
        query_total = outer(normed_ref[0], scaled(0))
        for c in range(1, GROUPS):
            query_total += outer(normed_ref[c], scaled(c))
        split(query_total, q_keep, q_give)
        q_move.start()
        line_q = scaled(0).astype(f32)
        for c in range(1, GROUPS):
            line_q += scaled(c).astype(f32)
        sums_ref[pl.ds(16 + g, 1), 0:wide_q] = jnp.sum(line_q, axis=0, keepdims=True)

    start_kv()
    sums_ref[...] = jnp.zeros_like(sums_ref)
    sums_ref[0:16] = sums_in[...]
    wg_kv[...] = jnp.zeros_like(wg_kv)

    def q_slot(z):
        return qout_ref.at[core, z]

    def v_slot(z):
        return kvout_ref.at[core, z]

    def b_slot(z):
        return big_ref.at[core, r, z]

    ring_q = Ring(g, x, q_slot, rq_own, rq_send, rq_recv)
    ring_v = Ring(g, x, v_slot, rv_own, rv_send, rv_recv)
    ring_b = Ring(g, x, b_slot, rb_own, rb_send, rb_recv)

    def store(value_ref, slot, sem):
        copy = pltpu.make_async_copy(value_ref, slot, sem)
        copy.start()
        copy.wait()

    def spread_b(z, step):
        begin(b_slot(z), b_slot(z), fy_send.at[step], fy_recv.at[step], r=far_r)
        begin(b_slot(z), b_slot(z), fs_send.at[0, step], fs_recv.at[0, step], core=sib)

    def spread_far(step):
        what = big_ref.at[core, far_r, nearest(g, step)]
        arrived(what, fy_send.at[step], fy_recv.at[step], x)
        begin(what, what, fs_send.at[1, step], fs_recv.at[1, step], core=sib)

    def on_ring_b(step):
        spread_b(ring_b.step(step), step)

    def on_ring_q(step):
        z = ring_q.step(step)
        begin(q_slot(z), q_slot(z), qs_send.at[step], qs_recv.at[step], core=sib)

    def on_ring_v(step):
        z = ring_v.step(step)
        begin(v_slot(z), v_slot(z), vs_send.at[step], vs_recv.at[step], core=sib)

    chain_a = Chain(g, x, total_a, part_a, inward_a, outward_a, ca_send, ca_recv)
    chain_b = Chain(g, x, total_b, by_sum, inward_b, outward_b, cb_send, cb_recv)
    at_end = (g == 0) | (g == GROUPS - 1)
    between = jnp.logical_not(at_end)

    def steps(chain, *which):
        for i in which:
            chain.step(farthest(g, i))

    def on_sibling(i):
        own, across = kv_moves[i]
        own.wait()
        across.wait_recv()

        def total(row, column):
            return own_kv[i, row, column].astype(f32) + sib_kv[i, row, column].astype(f32)

        for k in range(2):
            give_x[i, k] = (total(k, other) if i % 2 == 0 else total(far_r, k)).astype(bf16)
            keep_x[i, k] = total(k, x) if i % 2 == 0 else total(r, k)

    def go_first(i):
        along = {"x": other} if i % 2 == 0 else {"r": far_r}
        begin(give_x.at[i], in_x.at[i], x_send.at[i], x_recv.at[i], **along)

    def on_first(i):
        arrived(in_x.at[i], x_send.at[i], x_recv.at[i], x)
        away, stay, along = (far_r, r, {"r": far_r}) if i % 2 == 0 else (other, x, {"x": other})
        give_y[i] = (keep_x[i, away] + in_x[i, away].astype(f32)).astype(bf16)
        begin(give_y.at[i], in_y.at[i], y_send.at[i], y_recv.at[i], **along)
        keep_x[i, stay] += in_x[i, stay].astype(f32)

    def on_second(i):
        c = farthest(g, i)
        arrived(in_y.at[i], y_send.at[i], y_recv.at[i], x)
        both = (keep_x[i, r if i % 2 == 0 else x] + in_y[i].astype(f32)).astype(bf16)
        part_a[c] = inner(scaled(c), wfull_ref[:, :wide_q]) + inner(both, wfull_ref[:, wide_q:])
        wg_kv[...] += outer(normed_ref[c], both)
        sums_ref[pl.ds(16 + g, 1), wide_q : wide_q + 2 * HW] += jnp.sum(both.astype(f32), axis=0, keepdims=True)

    for load in loads[:4]:
        load.wait()
    own_up = pl.ds(pl.multiple_of(96 + 48 * x, 48), 48)
    their_up = pl.ds(pl.multiple_of(96 + 48 * other, 48), 48)
    for z in range(GROUPS):
        pair = kept[z].astype(f32) + over[z].astype(f32)
        by_sum[z, 0:96] = pair[0:96]
        by_sum[z, own_up] = pair[96:144]
        by_sum[z, 192:UNIT] = pair[144:KEPT]
        by_sum[z, their_up] = near[48 * z : 48 * z + 48].astype(f32) + far[z].astype(f32)
    pl.when(at_end)(lambda: steps(chain_b, 0, 1, 2))
    on_sibling(0)
    go_first(0)
    on_sibling(1)
    go_first(1)
    on_sibling(2)
    on_sibling(3)
    pl.when(between)(lambda: steps(chain_b, 0))
    query_grad()
    on_first(0)
    on_first(1)
    go_first(2)
    go_first(3)
    pl.when(between)(lambda: steps(chain_b, 1, 2))
    settled(q_move)
    q_pass[...] = (q_keep[other] + q_in[other].astype(f32)).astype(bf16)
    q_across = begin(q_pass, q_x, q_send.at[1], q_recv.at[1], x=other)
    loads[6].wait()
    on_second(0)
    on_second(1)
    pl.when(at_end)(lambda: steps(chain_a, 0))
    chain_b.step(g)
    unit[...] = total_b[...].astype(bf16)
    store(unit, b_slot(g), l_sem.at[0])
    ring_b.start()
    spread_b(g, 0)
    pl.when(at_end)(lambda: steps(chain_a, 1))
    on_first(2)
    on_first(3)
    q_across.wait_recv()
    q_sum[...] = (q_keep[x] + q_in[x].astype(f32) + q_x[...].astype(f32)).astype(bf16)
    q_over = begin(q_sum, q_y, q_send.at[2], q_recv.at[2], r=far_r)
    pl.when(between)(lambda: steps(chain_a, 0))
    on_ring_b(1)
    on_second(2)
    on_second(3)
    pl.when(at_end)(lambda: steps(chain_a, 2))
    split(wg_kv, v_keep, v_give)
    v_move = begin(v_give, v_in, v_send.at[0], v_recv.at[0], core=sib)
    s_sib = begin(sums_ref, sums_got.at[0], s_send.at[0], s_recv.at[0], core=sib)
    on_ring_b(2)
    spread_far(0)
    settled(q_over)
    q_sum[...] = (q_sum[...].astype(f32) + q_y[...].astype(f32)).astype(bf16)
    store(q_sum, q_slot(g), l_sem.at[0])
    ring_q.start()
    begin(q_slot(g), q_slot(g), qs_send.at[0], qs_recv.at[0], core=sib)
    v_move.wait_recv()
    v_pass[...] = (v_keep[other] + v_in[other].astype(f32)).astype(bf16)
    v_across = begin(v_pass, v_x, v_send.at[1], v_recv.at[1], x=other)
    settled(s_sib)
    sums_ref[...] += sums_got[0]
    s_x = begin(sums_ref, sums_got.at[1], s_send.at[1], s_recv.at[1], x=other)
    pl.when(between)(lambda: steps(chain_a, 1))
    v_across.wait_recv()
    v_sum[...] = (v_keep[x] + v_in[x].astype(f32) + v_x[...].astype(f32)).astype(bf16)
    v_over = begin(v_sum, v_y, v_send.at[2], v_recv.at[2], r=far_r)
    settled(s_x)
    sums_ref[...] += sums_got[1]
    s_y = begin(sums_ref, sums_got.at[2], s_send.at[2], s_recv.at[2], r=far_r)
    pl.when(between)(lambda: steps(chain_a, 2))
    settled(v_over)
    v_sum[...] = (v_sum[...].astype(f32) + v_y[...].astype(f32)).astype(bf16)
    store(v_sum, v_slot(g), l_sem.at[0])
    ring_v.start()
    begin(v_slot(g), v_slot(g), vs_send.at[0], vs_recv.at[0], core=sib)
    on_ring_b(3)
    settled(s_y)
    sums_ref[...] += sums_got[2]
    for away in range(1, GROUPS):
        begin(
            sums_ref, sums_got.at[2 + away], s_send.at[2 + away], s_recv.at[2 + away],
            g=lax.rem(g + away, GROUPS),
        )
    spread_far(1)
    on_ring_q(1)
    chain_a.step(g)

    loads[7].wait()
    loads[8].wait()
    grad_first = total_a[...]
    values = tokens_ref[...].astype(f32)
    mean = jnp.mean(values, axis=-1, keepdims=True)
    centred = values - mean
    scale = lax.rsqrt(jnp.mean(centred * centred, axis=-1, keepdims=True) + EPS)
    n1 = centred * scale
    pulled = grad_first * small_ref[0:1]
    inward = pulled - jnp.mean(pulled, axis=-1, keepdims=True) - n1 * jnp.mean(pulled * n1, axis=-1, keepdims=True)
    tokens_grad_ref[...] = mgrad_ref[...] + inward * scale
    late[...] = jnp.zeros_like(late)
    late[0:1] = jnp.sum(grad_first * n1, axis=0, keepdims=True)
    late[1:2] = jnp.sum(grad_first, axis=0, keepdims=True)
    for step in range(len(AROUND)):
        begin(late, late_got.at[step], t_send.at[step], t_recv.at[step], **neighbour(r, core, x, step))
    on_ring_v(1)
    on_ring_q(2)
    on_ring_q(3)
    spread_far(2)
    on_ring_v(2)
    late_sum[...] = late[...]
    for step in range(len(AROUND)):
        arrived(late_got.at[step], t_send.at[step], t_recv.at[step], x)
        late_sum[...] += late_got[step]
    first_z = len(AROUND) - 1
    for away in range(1, GROUPS):
        begin(
            late_sum, late_got.at[first_z + away], t_send.at[first_z + away], t_recv.at[first_z + away],
            g=lax.rem(g + away, GROUPS),
        )
    on_ring_v(3)
    spread_far(3)

    for away in range(1, GROUPS):
        arrived(sums_got.at[2 + away], s_send.at[2 + away], s_recv.at[2 + away], x)
        arrived(late_got.at[first_z + away], t_send.at[first_z + away], t_recv.at[first_z + away], x)
    for step in range(GROUPS):
        z = nearest(g, step)
        arrived(qout_ref.at[sib, z], qs_send.at[step], qs_recv.at[step], x)
        arrived(kvout_ref.at[sib, z], vs_send.at[step], vs_recv.at[step], x)
        arrived(big_ref.at[sib, r, z], fs_send.at[0, step], fs_recv.at[0, step], x)
        arrived(big_ref.at[sib, far_r, z], fs_send.at[1, step], fs_recv.at[1, step], x)
    for move in pending:
        move.wait_send()
    for item in (chain_a, chain_b, ring_q, ring_v, ring_b):
        item.finish()
    sums_ref[...] += sums_got[3] + sums_got[4] + sums_got[5]
    total = late_sum[...] + late_got[first_z + 1] + late_got[first_z + 2] + late_got[first_z + 3]
    sums_ref[0:2] = total[0:2]


def scatter(dkv, dq, normed, wfull, tokens, mgrad, small, keep, over, near, far, sums):
    rows, width = tokens.shape
    fourth = width // 4
    dma = pltpu.SemaphoreType.DMA
    wide_q, wide_v = 2 * BLK, 2 * HW
    kv_block = (rows, wide_v)
    full = (rows, width)
    unit = (UNIT, width)

    def weight_scratch(wide):
        return [
            pltpu.VMEM((2, fourth, wide), f32),
            pltpu.VMEM((2, fourth, wide), bf16),
            pltpu.VMEM((2, fourth, wide), bf16),
            *[pltpu.VMEM((fourth, wide), bf16)] * 4,
        ]

    return pl.pallas_call(
        scatter_kernel,
        out_shape=(
            jax.ShapeDtypeStruct(full, f32),
            jax.ShapeDtypeStruct((2, 2, GROUPS, *unit), bf16),
            jax.ShapeDtypeStruct((2, GROUPS, fourth, wide_q), bf16),
            jax.ShapeDtypeStruct((2, GROUPS, fourth, wide_v), bf16),
            jax.ShapeDtypeStruct((24, width), f32),
        ),
        in_specs=[anywhere()] * 10 + [whole_vmem()] * 2,
        out_specs=(whole_vmem(), anywhere(), anywhere(), anywhere(), whole_vmem()),
        scratch_shapes=[
            *[
                pltpu.VMEM(item.shape, item.dtype)
                for item in (dq, normed, wfull, tokens, mgrad, keep, over)
            ],
            pltpu.VMEM((48 * GROUPS, width), bf16),
            pltpu.VMEM(far.shape, bf16),
            pltpu.VMEM((GROUPS, 2, 2, *kv_block), bf16),
            pltpu.VMEM((GROUPS, 2, 2, *kv_block), bf16),
            pltpu.VMEM((GROUPS, 2, *kv_block), f32),
            pltpu.VMEM((GROUPS, 2, *kv_block), bf16),
            pltpu.VMEM((GROUPS, 2, *kv_block), bf16),
            pltpu.VMEM((GROUPS, *kv_block), bf16),
            pltpu.VMEM((GROUPS, *kv_block), bf16),
            pltpu.VMEM((GROUPS, *full), f32),
            pltpu.VMEM(full, f32),
            pltpu.VMEM((2, GROUPS, *full), bf16),
            pltpu.VMEM((GROUPS, *full), bf16),
            pltpu.VMEM((width, wide_v), f32),
            pltpu.VMEM((GROUPS, *unit), f32),
            pltpu.VMEM(unit, f32),
            pltpu.VMEM((2, GROUPS, *unit), bf16),
            pltpu.VMEM((GROUPS, *unit), bf16),
            pltpu.VMEM(unit, bf16),
            *weight_scratch(wide_q),
            *weight_scratch(wide_v),
            pltpu.VMEM((6, 24, width), f32),
            pltpu.VMEM((8, width), f32),
            pltpu.VMEM((8, width), f32),
            pltpu.VMEM((len(AROUND) + GROUPS - 1, 8, width), f32),
            dma((9,)),
            dma((GROUPS,)), dma((GROUPS,)), dma((GROUPS,)), dma((GROUPS,)), dma((GROUPS,)), dma((GROUPS,)), dma((GROUPS,)),
            dma((GROUPS,)), dma((2, GROUPS)),
            dma((GROUPS,)), dma((2, GROUPS)), dma((2,)), dma((GROUPS,)), dma((GROUPS,)),
            dma((GROUPS,)), dma((GROUPS,)), dma((2, GROUPS)), dma((2, GROUPS)),
            dma((3,)), dma((3,)), dma((2,)), dma((GROUPS,)), dma((GROUPS,)), dma((GROUPS,)), dma((GROUPS,)),
            dma((3,)), dma((3,)), dma((2,)), dma((GROUPS,)), dma((GROUPS,)), dma((GROUPS,)), dma((GROUPS,)),
            dma((6,)), dma((6,)), dma((10,)), dma((10,)), dma((1,)),
        ],
        compiler_params=pltpu.CompilerParams(
            collective_id=2, has_side_effects=True, vmem_limit_bytes=47 << 20
        ),
        name="scatter",
    )(dkv, dq, normed, wfull, tokens, mgrad, keep, over, near, far, small, sums)


def pack_kv(key_part, value_part):
    return jnp.concatenate(
        [key_part, value_part[..., 2 * DH :], value_part[..., : 2 * DH]], axis=-1
    )


def unpack_kv(both):
    return both[..., :HW], jnp.concatenate([both[..., HW + DH :], both[..., HW : HW + DH]], axis=-1)


def layout_kernel(
    big_ref, query_ref, kv_ref, sums_ref, base_ref, got_ref,
    up_out, down_out, wo_out, query_out, key_out, value_out,
    low_gain, low_shift, query_bias, value_bias, out_bias, high_gain, high_shift, up_bias, down_bias, result_out,
):
    x = lax.axis_index("x")
    width = big_ref.shape[-1]
    half = width // 2
    result_out[...] = (base_ref[...] + got_ref[...].astype(f32)).astype(bf16)
    for core in range(2):
        down_out[core] = big_ref[core, 0, 0:96].astype(f32)
        wo_out[core] = big_ref[core, 0, 192:UNIT].astype(f32)
        for owner in range(2):
            lane = (2 * owner + core) * width
            up_out[:, lane : lane + width] = big_ref[core, 0, 96 + 48 * owner : 144 + 48 * owner].astype(f32)
        query_out[core] = jnp.concatenate(
            [query_ref[core, z].astype(f32)[:, :HW] for z in range(GROUPS)], axis=1
        )
        both = [unpack_kv(kv_ref[core, z].astype(f32)) for z in range(GROUPS)]
        key_out[core] = jnp.concatenate([item[0] for item in both], axis=1)
        value_out[core] = jnp.concatenate([item[1] for item in both], axis=1)

    @pl.when(pl.program_id(0) == 0)
    def _():
        def own_half(row):
            whole = sums_ref[row : row + 1]
            return jnp.where(x == 0, whole[:, :half], whole[:, half:]).reshape(half)

        for ref, row in (
            (low_gain, 0), (low_shift, 1), (out_bias, 2), (high_gain, 3), (high_shift, 4), (down_bias, 5),
        ):
            ref[...] = own_half(row)
        pair = [sums_ref[pl.ds(16 + 2 * x + i, 1)] for i in range(2)]
        query_bias[...] = jnp.concatenate([item[:, :HW] for item in pair], axis=1).reshape(half)
        value_bias[...] = jnp.concatenate(
            [unpack_kv(item[:, 2 * BLK : 2 * BLK + 2 * HW])[1] for item in pair], axis=1
        ).reshape(half)
        up_bias[...] = jnp.concatenate(
            [sums_ref[pl.ds(8 + 2 * x + i, 1)] for i in range(2)], axis=1
        ).reshape(2 * width)


def lay_out(big, query, kv, sums, base, got):
    width = big.shape[-1]
    half, fourth = width // 2, width // 4
    rows = fourth // PARTS

    def spec(shape, index):
        return pl.BlockSpec(shape, index)

    def fixed(wide):
        return pl.BlockSpec((wide,), lambda p: (0,))

    narrow = spec((2, rows, width), lambda p: (0, p, 0))
    vector = jax.ShapeDtypeStruct((half,), f32)
    return pl.pallas_call(
        layout_kernel,
        grid=(PARTS,),
        out_shape=(
            jax.ShapeDtypeStruct((half, 4 * width), f32),
            jax.ShapeDtypeStruct((2, width, width), f32),
            *[jax.ShapeDtypeStruct((2, fourth, width), f32)] * 4,
            *[vector] * 7,
            jax.ShapeDtypeStruct((2 * width,), f32),
            vector,
            jax.ShapeDtypeStruct(base.shape, bf16),
        ),
        in_specs=[
            spec((2, 1, UNIT, width), lambda p: (0, p, 0, 0)),
            spec((2, GROUPS, rows, query.shape[-1]), lambda p: (0, 0, p, 0)),
            spec((2, GROUPS, rows, kv.shape[-1]), lambda p: (0, 0, p, 0)),
            spec(sums.shape, lambda p: (0, 0)),
            spec((base.shape[0] // PARTS, width), lambda p: (p, 0)),
            spec((base.shape[0] // PARTS, width), lambda p: (p, 0)),
        ],
        out_specs=(
            spec((48, 4 * width), lambda p: (p, 0)),
            spec((2, 96, width), lambda p: (0, p, 0)),
            *[narrow] * 4,
            *[fixed(half)] * 7,
            fixed(2 * width),
            fixed(half),
            spec((base.shape[0] // PARTS, width), lambda p: (p, 0)),
        ),
        compiler_params=pltpu.CompilerParams(
            vmem_limit_bytes=50 << 20, dimension_semantics=("arbitrary",)
        ),
        name="lay_out",
    )(big, query, kv, sums, base, got)


ROWS = ("s", "r", "core", "x")
ALL = ("g", "s", "r", "core", "x")


def shards(
    tokens, cotangent, doc_lengths, deal, first_gain, first_shift, query_weight, query_bias,
    key_weight, value_weight, value_bias, output_weight, output_bias, second_gain, second_shift,
    up_weight, up_bias, down_weight, down_bias,
):
    rows, width = tokens.shape
    half = width // 2
    blocks = deal.shape[0]
    core, x = lax.axis_index("core"), lax.axis_index("x")
    swap = ((0, 1), (1, 0))

    def up_columns(owner):
        return lax.dynamic_slice_in_dim(up_weight, (2 * owner + core) * width, width, 1)

    def stay(*items):
        return tuple(pltpu.with_memory_space_constraint(item, pltpu.HBM) for item in items)

    kv, q, normed, small, wfull, wo = gather(
        *stay(
            tokens, query_weight, key_weight, value_weight, output_weight,
            first_gain, first_shift, output_bias, second_gain, second_shift, down_bias, query_bias, value_bias, up_bias,
        )
    )
    wide = blocks > 8 * 2 * GROUPS
    if wide:
        kv = lax.all_gather(kv, "s", axis=0, tiled=True)
    kv = kv.reshape(blocks, BLK, 2 * HW)
    q = q.reshape(2 * GROUPS, BLK, 2 * BLK)
    up_other, kv = lax.optimization_barrier((up_columns(1 - x), kv))
    up_other = lax.ppermute(up_other, "x", swap)
    out_t, kept, lse = attend_forward(deal, doc_lengths, q, kv)
    base, x_give, grad_middle, grad_t, kept_part, over, far, sums = dense(
        out_t, tokens, cotangent, small, wo, up_columns(x), up_other, down_weight
    )
    over = lax.ppermute(over, "r", swap)
    x_got = lax.ppermute(x_give, "x", swap)
    far = lax.ppermute(far, ("r", "x"), ((0, 3), (1, 2), (2, 1), (3, 0)))
    dq, dkv = attend_backward(deal, doc_lengths, q, kv, lse, grad_t, kept)
    dkv = dkv.reshape(-1, GROUPS, rows, 2 * HW)
    if wide:
        dkv = lax.psum_scatter(dkv, "s", scatter_dimension=0, tiled=True)
    dkv = dkv.reshape(2, 2, 2, GROUPS, rows, 2 * HW)
    dq = dq.reshape(GROUPS, rows, 2 * BLK)
    grad_tokens, big, query_own, kv_own, sums = scatter(
        *stay(dkv), dq, *stay(normed, wfull, tokens, grad_middle), small, *stay(kept_part), over, x_got, far, sums
    )
    if wide:
        big, query_own, kv_own, sums = (
            lax.psum(item, "s") for item in (big, query_own, kv_own, sums)
        )

    (
        up_own, down_own, wo_own, query_own, key_own, value_own,
        low_gain, low_shift, query_sum, value_sum, out_sum, high_gain, high_shift, up_sum, down_sum, result,
    ) = lay_out(big.reshape(2, PARTS, UNIT, width), query_own, kv_own, sums, *stay(base, x_got))

    def flat(item):
        return item.reshape(-1, width)

    return (
        result,
        grad_tokens,
        low_gain,
        low_shift,
        flat(query_own),
        query_sum,
        flat(key_own),
        flat(value_own),
        value_sum,
        flat(wo_own),
        out_sum,
        high_gain,
        high_shift,
        up_own,
        up_sum,
        flat(down_own),
        down_sum,
    )


def solution(mesh):
    devices = mesh.devices
    inner_mesh = Mesh(devices.reshape(GROUPS, devices.shape[0] // (4 * GROUPS), 2, 2, 2), ALL)
    row = P(ALL, None)
    mat = P("x", None)
    vec = P("x")
    in_specs = (
        row, row, P(), P(), vec, vec, mat, vec, mat, mat, vec, mat, vec, vec, vec, mat, vec, mat, vec,
    )
    out_specs = (
        row, row, vec, vec, mat, vec, mat, mat, vec, mat, vec, vec, vec, mat, vec, mat, vec,
    )
    return jax.shard_map(
        shards, mesh=inner_mesh, in_specs=in_specs, out_specs=out_specs, check_vma=False
    )
```
